32 devices in a mesh: fsdp: 16 (over z, y, core), ctx: 2 (over x).
Axes of the slice: x: 2, y: 2, z: 4, core: 2. Of those that a mesh axis runs over, the one named last changes fastest.
Arguments:
- tokens: bfloat16 [8192, 2048], P(('fsdp', 'ctx')), may hold values from -6 to 6
- qkv_weight: bfloat16 [2048, 5120], P('fsdp'), may hold values from -0.125 to 0.125
- out_weight: bfloat16 [4096, 2048], P('fsdp'), may hold values from -1.5 to 1.5
- router_weight: bfloat16 [2048, 32], P('fsdp'), may hold values from -0.125 to 0.125
- attn_gain: bfloat16 [2048], P('fsdp'), may hold values from 0.5 to 1.5
- moe_gain: bfloat16 [2048], P('fsdp'), may hold values from 0.5 to 1.5
- query_gain: bfloat16 [128], replicated, may hold values from 0.5 to 1.5
- key_gain: bfloat16 [128], replicated, may hold values from 0.5 to 1.5
- expert_gate_up: bfloat16 [32, 2048, 1536], P(('fsdp', 'ctx')), may hold values from -0.125 to 0.125
- expert_down: bfloat16 [32, 768, 2048], P(('fsdp', 'ctx')), may hold values from -0.21875 to 0.21875
- routes: int32 [8192, 8], P(('fsdp', 'ctx')), may hold values from 0 to 31, all different within a row; in each aligned block of 256 rows (0 to 255, 256 to 511, ...) at most 128 rows name the same one
- cotangent: bfloat16 [8192, 2048], P(('fsdp', 'ctx')), may hold values from -6 to 6
Outputs:
- output: bfloat16 [8192, 2048], P(('fsdp', 'ctx'))
- grad_tokens: float32 [8192, 2048], P(('fsdp', 'ctx'))
- grad_qkv: float32 [2048, 5120], P('fsdp')
- grad_out: float32 [4096, 2048], P('fsdp')
- grad_router: float32 [2048, 32], P('fsdp')
- grad_attn_gain: float32 [2048], P('fsdp')
- grad_moe_gain: float32 [2048], P('fsdp')
- grad_query_gain: float32 [128], replicated
- grad_key_gain: float32 [128], replicated
- grad_gate_up: float32 [32, 2048, 1536], P(('fsdp', 'ctx'))
- grad_down: float32 [32, 768, 2048], P(('fsdp', 'ctx'))
The draws below stay inside these ranges and needn't reach their ends.
Inputs may be any that keep to these rules, and one draw needn't show every extreme that they name: `routes`: each row names 8 different experts. In each aligned block of 256 rows (the rows of one device) no expert is named by more than 128 rows, a bound that some block reaches.
All inputs are finite; a program needn't handle non-finite values.
Results may differ from the reference program's by a relative error of at most 0.019.
Values may be sent and summed in bfloat16 or wider, within the bound.
No kernel may reach another device: no remote copies, remote signals or barrier semaphores. Data moves between devices by JAX's collectives and lax.ppermute only.
A program may use at most 448 MiB of HBM per device.

```python
import math
import jax
import jax.numpy as jnp
import numpy as np
from jax import lax

D = 2048
HEADS = 32
KV_HEADS = 4
HEAD_DIM = 128
FF = 768
TOP = 8
TOK_DEV = 256
EXPERTS = 32
SEQ_LEN = 512
TOKENS = 8192
CAP = 128
N_FSDP = 16
N_CTX = 2


def level_of(rng, dims, cuts, low, high):
    level, own = 1.0, jax.random.fold_in(rng, 6)
    for axis_at, parts in cuts:
        heights = jnp.exp(jax.random.uniform(jax.random.fold_in(own, axis_at), (parts,), jnp.float32, low / len(cuts), high / len(cuts)))
        level = level * jnp.repeat(heights, dims[axis_at] // parts).reshape([-1 if axis == axis_at else 1 for axis in range(len(dims))])
    return level


def assign_block(rng, own, number, rows, number_of, top, most, lean):
    order = jax.random.permutation(rng, number_of)
    heavy_load, ordinary = portions_of(number_of, rows * top, most, lean, True), portions_of(number_of, rows * top, most, lean, False)
    places = jnp.arange(number_of)

    def named(sizes, rotation):
        used = int((sizes > 0).sum())
        fixed = max(1, used // 4)
        passed = fixed + (places - fixed + rotation * (used - fixed)) % max(1, number_of - fixed)
        return jnp.zeros((number_of,), jnp.int32).at[order[jnp.where(places < fixed, places, passed)]].set(jnp.asarray(sizes, jnp.int32))

    sizes = jnp.where(number % 4 == 0, named(heavy_load, number // 4), named(ordinary, number - number // 4 - 1))
    mixed = jax.random.permutation(jax.random.fold_in(own, 3), number_of)
    source_of, receiver = mixed[0:number_of // 2 * 2:2], mixed[1:number_of // 2 * 2:2]
    room = jnp.minimum(sizes[source_of] - 1, most - sizes[receiver]) // 2
    room = jnp.where((source_of == order[0]) | (receiver == order[0]) | (sizes[receiver] == 0), 0, jnp.maximum(room, 0))
    passed = jax.random.randint(jax.random.fold_in(own, 4), (number_of // 2,), 0, 1 << 20) % (room + 1)
    sizes = sizes.at[source_of].add(-passed).at[receiver].add(passed)
    labels = jnp.searchsorted(jnp.cumsum(sizes), jnp.arange(rows * top), side="right").astype(jnp.int32)
    listing = labels.reshape(top, rows).T
    listing = listing[jax.random.permutation(jax.random.fold_in(own, 1), rows)]
    rotation = jax.random.randint(jax.random.fold_in(own, 2), (rows, 1), 0, top)
    return jnp.take_along_axis(listing, (jnp.arange(top)[None, :] + rotation) % top, axis=1)


def portions_of(amount, total, limit, skew, full):
    portions = [(1 << 20) // math.isqrt(standing ** skew) + 1 for standing in range(1, amount + 1)]
    largest = limit if full else min(limit, max(-(-total // amount), total * portions[0] // sum(portions)))
    least = 1 if total - largest >= amount - 1 else 0
    given, surplus = [largest] + [least] * (amount - 1), total - largest - least * (amount - 1)
    while surplus > 0:
        movable = [i for i in range(1, amount) if given[i] < largest] or [i for i in range(1, amount) if given[i] < limit]
        mass, left = sum([portions[i] for i in movable]), surplus
        for i in movable:
            addition = min(limit - given[i], max(1, left * portions[i] // mass), surplus)
            given[i] = given[i] + addition
            surplus = surplus - addition
    return np.array(given)


def normal_values(own_key, dims, deviation, limit, cuts=(), kind=jnp.bfloat16):
    level = level_of(own_key, dims, cuts, -0.22, 0.18) if cuts else 1.0
    entries = jax.random.normal(own_key, dims, jnp.float32) * deviation * level
    return jnp.minimum(jnp.maximum(entries, -limit), limit).astype(kind)


def setup_inputs(seed: int = 0) -> dict:
    key_list = jax.random.split(jax.random.key(seed), 13)
    tokens = normal_values(key_list[0], (TOKENS, D), 1.0, 6.0, ((0, 32),))
    qkv_weight = normal_values(key_list[1], (D, (HEADS + 2 * KV_HEADS) * HEAD_DIM), D ** -0.5, 0.125, ((0, 16),))
    out_weight = normal_values(key_list[2], (HEADS * HEAD_DIM, D), (max(1, HEADS * HEAD_DIM // TOK_DEV)) ** -0.5, 1.5, ((0, 16),))
    router_weight = normal_values(key_list[3], (D, EXPERTS), D ** -0.5, 0.125, ((0, 16),))
    attn_gain = jnp.clip(1.0 + 0.1 * jax.random.normal(key_list[4], (D,), jnp.float32), 0.5, 1.5).astype(jnp.bfloat16)
    moe_gain = jnp.clip(1.0 + 0.1 * jax.random.normal(key_list[5], (D,), jnp.float32), 0.5, 1.5).astype(jnp.bfloat16)
    query_gain = jnp.clip(1.0 + 0.1 * jax.random.normal(key_list[6], (HEAD_DIM,), jnp.float32), 0.5, 1.5).astype(jnp.bfloat16)
    key_gain = jnp.clip(1.0 + 0.1 * jax.random.normal(key_list[7], (HEAD_DIM,), jnp.float32), 0.5, 1.5).astype(jnp.bfloat16)
    expert_gate_up = normal_values(key_list[8], (EXPERTS, D, 2 * FF), D ** -0.5, 0.125, ((0, 32),))
    expert_down = normal_values(key_list[9], (EXPERTS, FF, D), FF ** -0.5, 0.21875, ((0, 32),))
    routes_keys = jax.random.split(jax.random.fold_in(key_list[10], 1), TOKENS // TOK_DEV)
    routes_turns = jax.random.permutation(jax.random.fold_in(key_list[10], 3), TOKENS // TOK_DEV)
    routes = jax.vmap(lambda own, number: assign_block(jax.random.fold_in(key_list[10], 2), own, number, TOK_DEV, EXPERTS, TOP, CAP, 1))(routes_keys, routes_turns).reshape((TOKENS, TOP))
    cotangent = normal_values(key_list[11], (TOKENS, D), 1.0, 6.0, ((0, 32),))
    return {"tokens": tokens, "qkv_weight": qkv_weight, "out_weight": out_weight, "router_weight": router_weight, "attn_gain": attn_gain, "moe_gain": moe_gain, "query_gain": query_gain, "key_gain": key_gain, "expert_gate_up": expert_gate_up, "expert_down": expert_down, "routes": routes, "cotangent": cotangent}


@jax.custom_vjp
def low(v):
    return lax.optimization_barrier(v.astype(jnp.bfloat16)).astype(jnp.float32)

@jax.custom_vjp
def low_back(v):
    return v

def low_keep(v):
    return (low(v), None)

def low_pass(kept, grad):
    return (grad,)

def back_keep(v):
    return (v, None)

def back_low(kept, grad):
    return (low(grad),)
low.defvjp(low_keep, low_pass)
low_back.defvjp(back_keep, back_low)
eps_norm = 1e-06
theta_base = 1000000.0
highest = lax.Precision.HIGHEST

def rms_scale(values, gain):
    return values * lax.rsqrt(lax.optimization_barrier(jnp.mean(values * values, axis=-1, keepdims=True)) + eps_norm) * gain

def rotate(values, cosine, sine):
    half_width = values.shape[-1] // 2
    turned = jnp.concatenate([-values[..., half_width:], values[..., :half_width]], axis=-1)
    return values * cosine + turned * sine

def angles(positions, width):
    freqs = theta_base ** (-(jnp.arange(width // 2, dtype=jnp.float32) * 2.0) / width)
    phase = positions.astype(jnp.float32)[:, None] * freqs[None, :]
    phase = jnp.concatenate([phase, phase], axis=-1)
    return (jnp.cos(phase)[:, None, :], jnp.sin(phase)[:, None, :])

def stored_positions(ctx_count, tok_dev):
    half_rows = tok_dev // 2
    indices = jnp.arange(ctx_count * tok_dev, dtype=jnp.int32)
    block_rank = indices // tok_dev
    within = indices % tok_dev
    span_id = jnp.where(within < half_rows, block_rank, 2 * ctx_count - 1 - block_rank)
    return (span_id * half_rows + within % half_rows).astype(jnp.int32)

def layer(params, tokens_in, routes_in):
    qkv_w, out_w, router_w, attn_g, moe_g, query_g, key_g, gate_up, down_w = params
    seq_count = tokens_in.shape[0] // SEQ_LEN
    group_size = HEADS // KV_HEADS
    width_q = HEADS * HEAD_DIM
    width_k = KV_HEADS * HEAD_DIM
    normed_in = low(rms_scale(tokens_in, attn_g))
    projected = jnp.dot(normed_in, qkv_w, precision=highest)
    query = low_back(projected[:, :width_q]).reshape(-1, HEADS, HEAD_DIM)
    key_raw = low_back(projected[:, width_q:width_q + width_k]).reshape(-1, KV_HEADS, HEAD_DIM)
    value_raw = low_back(low(projected[:, width_q + width_k:])).reshape(-1, KV_HEADS, HEAD_DIM)
    seq_pos = stored_positions(N_CTX, TOK_DEV)
    cosine, sine = angles(jnp.tile(seq_pos, seq_count), HEAD_DIM)
    query = low_back(low(rotate(rms_scale(query, query_g), cosine, sine)))
    key_raw = low_back(low(rotate(rms_scale(key_raw, key_g), cosine, sine)))
    query_seq = query.reshape(seq_count, SEQ_LEN, KV_HEADS, group_size, HEAD_DIM)
    key_seq = key_raw.reshape(seq_count, SEQ_LEN, KV_HEADS, HEAD_DIM)
    value_seq = value_raw.reshape(seq_count, SEQ_LEN, KV_HEADS, HEAD_DIM)
    scores = low_back(jnp.einsum('bqkgd,bskd->bkgqs', query_seq, key_seq, precision=highest) / math.sqrt(HEAD_DIM))
    causal = seq_pos[None, :] <= seq_pos[:, None]
    expo = jnp.where(causal, jnp.exp(scores), 0.0)
    probs = low(expo / lax.optimization_barrier(jnp.sum(expo, axis=-1, keepdims=True)))
    attended = jnp.einsum('bkgqs,bskd->bqkgd', probs, value_seq, precision=highest)
    attended = low_back(low(attended.reshape(-1, HEADS * HEAD_DIM)))
    mixed = tokens_in + low_back(jnp.dot(attended, out_w, precision=highest))
    normed_mid = low(rms_scale(mixed, moe_g))
    logits = low_back(jnp.dot(normed_mid, router_w, precision=highest))
    chosen = jnp.exp(jnp.take_along_axis(logits, routes_in, axis=1))
    gates = chosen / lax.optimization_barrier(jnp.sum(chosen, axis=1, keepdims=True))
    blocks = tokens_in.shape[0] // TOK_DEV
    flat_routes = routes_in.reshape(blocks, TOK_DEV * TOP)
    expert_ids = jnp.arange(EXPERTS, dtype=jnp.int32)
    hit_table = (flat_routes[:, :, None] == expert_ids[None, None, :]).astype(jnp.int32)
    slot_index = (lax.optimization_barrier(jnp.sum(jnp.cumsum(hit_table, axis=1) * hit_table, axis=2)) - 1).astype(jnp.int32)
    block_ids = jnp.arange(blocks, dtype=jnp.int32)
    target = (flat_routes * (blocks * CAP) + block_ids[:, None] * CAP + slot_index).reshape(-1).astype(jnp.int32)
    pair_ids = jnp.arange(target.shape[0], dtype=jnp.int32)
    source_row = jnp.full((EXPERTS * blocks * CAP,), tokens_in.shape[0], jnp.int32).at[target].set(pair_ids // TOP)
    padded = jnp.concatenate([normed_mid, jnp.zeros((1, D), jnp.float32)], axis=0)
    expert_rows = low_back(padded[source_row].reshape(EXPERTS, blocks * CAP, D))
    gate_and_up = low_back(jnp.einsum('esd,edf->esf', expert_rows, gate_up, precision=highest))
    hidden = low(jax.nn.silu(gate_and_up[..., :FF]) * gate_and_up[..., FF:])
    result = low_back(low(jnp.einsum('esf,efd->esd', hidden, down_w, precision=highest)))
    picked = result.reshape(-1, D)[target].reshape(-1, TOP, D)
    return mixed + lax.optimization_barrier(jnp.sum(gates[:, :, None] * picked, axis=1))

def reference(tokens, qkv_weight, out_weight, router_weight, attn_gain, moe_gain, query_gain, key_gain, expert_gate_up, expert_down, routes, cotangent):
    params = tuple((item.astype(jnp.float32) for item in (qkv_weight, out_weight, router_weight, attn_gain, moe_gain, query_gain, key_gain, expert_gate_up, expert_down)))
    per_step = math.gcd(N_FSDP, max(1, 4096 // SEQ_LEN))
    step_count = N_FSDP // per_step
    rows_step = per_step * SEQ_LEN
    inputs = tokens.astype(jnp.float32).reshape(step_count, rows_step, D)
    route_steps = routes.reshape(step_count, rows_step, TOP)
    checked = jax.checkpoint(layer)

    def forward(params_in, inputs_in):
        return lax.map(lambda member: checked(params_in, member[0], member[1]), (inputs_in, route_steps))
    outputs, pullback = jax.vjp(forward, params, inputs)
    grads, grad_inputs = pullback(cotangent.astype(jnp.float32).reshape(step_count, rows_step, D))
    return (outputs.reshape(TOKENS, D).astype(jnp.bfloat16), grad_inputs.reshape(TOKENS, D), grads[0], grads[1], grads[2], grads[3], grads[4], grads[5], grads[6], grads[7], grads[8])
```

```python
import functools
import math

import jax
import jax.numpy as jnp
from jax import lax
from jax.experimental import pallas as pl
from jax.experimental.pallas import tpu as pltpu
from jax.sharding import PartitionSpec as P

eps_norm = 1e-06
theta_base = 1000000.0


def rms_scale(values, gain):
    return values * lax.rsqrt(jnp.mean(values * values, axis=-1, keepdims=True) + eps_norm) * gain


def rotate(values, cosine, sine):
    half_width = values.shape[-1] // 2
    turned = jnp.concatenate([-values[..., half_width:], values[..., :half_width]], axis=-1)
    return values * cosine + turned * sine


def angles(positions, width):
    freqs = theta_base ** (-(jnp.arange(width // 2, dtype=jnp.float32) * 2.0) / width)
    phase = positions.astype(jnp.float32)[:, None] * freqs[None, :]
    phase = jnp.concatenate([phase, phase], axis=-1)
    return (jnp.cos(phase)[:, None, :], jnp.sin(phase)[:, None, :])


def device_positions(block_rank, ctx_count, tok_rows):
    half_rows = tok_rows // 2
    within = jnp.arange(tok_rows, dtype=jnp.int32)
    span_id = jnp.where(within < half_rows, block_rank, 2 * ctx_count - 1 - block_rank)
    return span_id * half_rows + within % half_rows


def attend_head(query, keys_in, values_in, causal, scale_root):
    scores = (
        jnp.einsum("tgd,sd->gts", query, keys_in, preferred_element_type=jnp.float32) / scale_root
    )
    expo = jnp.where(causal[None], jnp.exp(scores), 0.0)
    totals = jnp.sum(expo, axis=-1, keepdims=True)
    probs = (expo / totals).astype(jnp.bfloat16)
    attended = jnp.einsum("gts,sd->tgd", probs, values_in, preferred_element_type=jnp.float32)
    return (attended, jnp.log(totals[..., 0]))


def attend_back(query, keys_in, values_in, causal, log_total, grad_attended, scale_root):
    scores = (
        jnp.einsum("tgd,sd->gts", query, keys_in, preferred_element_type=jnp.float32) / scale_root
    )
    probs = jnp.where(causal[None], jnp.exp(scores - log_total[..., None]), 0.0)
    low_probs = probs.astype(jnp.bfloat16)
    grad_values = jnp.einsum(
        "gts,tgd->sd", low_probs, grad_attended, preferred_element_type=jnp.float32
    )
    grad_probs = jnp.einsum(
        "tgd,sd->gts", grad_attended, values_in, preferred_element_type=jnp.float32
    )
    delta_rows = jnp.sum(grad_probs * probs, axis=-1, keepdims=True)
    grad_scores = (probs * (grad_probs - delta_rows)).astype(jnp.bfloat16)
    grad_query = (
        jnp.einsum("gts,sd->tgd", grad_scores, keys_in, preferred_element_type=jnp.float32)
        / scale_root
    )
    grad_keys = (
        jnp.einsum("gts,tgd->sd", grad_scores, query, preferred_element_type=jnp.float32)
        / scale_root
    )
    return (grad_query, grad_keys, grad_values)


def swiglu(paired):
    half_width = paired.shape[-1] // 2
    return jax.nn.silu(paired[..., :half_width]) * paired[..., half_width:]


def gating(selected):
    expo = jnp.exp(selected)
    return expo / jnp.sum(expo, axis=1, keepdims=True)


def body_routed(
    tokens,
    qkv_weight,
    out_weight,
    router_weight,
    attn_gain,
    moe_gain,
    query_gain,
    key_gain,
    expert_gate_up,
    expert_down,
    routes,
    cotangent,
):
    rows_dev, width = tokens.shape
    head_dim = query_gain.shape[0]
    top_k = routes.shape[1]
    ctx_count = lax.axis_size("ctx")
    ctx_rank = lax.axis_index("ctx")
    qkv_all, out_all, router_all, attn_all, moe_all = (
        lax.all_gather(qkv_weight, "fsdp", axis=0, tiled=True),
        lax.all_gather(out_weight, "fsdp", axis=0, tiled=True),
        lax.all_gather(router_weight, "fsdp", axis=0, tiled=True),
        lax.all_gather(attn_gain, "fsdp", axis=0, tiled=True),
        lax.all_gather(moe_gain, "fsdp", axis=0, tiled=True),
    )
    experts_all = router_all.shape[1]
    heads = out_all.shape[0] // head_dim
    kv_heads = (qkv_all.shape[1] // head_dim - heads) // 2
    group_size = heads // kv_heads
    capacity = 2 * rows_dev * top_k // experts_all
    width_q = heads * head_dim
    width_k = kv_heads * head_dim
    scale_root = math.sqrt(head_dim)
    inputs = tokens.astype(jnp.float32)
    normed_in = rms_scale(inputs, attn_all.astype(jnp.float32))
    low_in = normed_in.astype(jnp.bfloat16)
    projected = jnp.dot(low_in, qkv_all, preferred_element_type=jnp.float32)
    query_raw = projected[:, :width_q].reshape(rows_dev, heads, head_dim)
    key_raw = projected[:, width_q : width_q + width_k].reshape(rows_dev, kv_heads, head_dim)
    value_low = (
        projected[:, width_q + width_k :].astype(jnp.bfloat16).reshape(rows_dev, kv_heads, head_dim)
    )
    positions = device_positions(ctx_rank, ctx_count, rows_dev)
    cosine, sine = angles(positions, head_dim)
    query_gain_f = query_gain.astype(jnp.float32)
    key_gain_f = key_gain.astype(jnp.float32)

    def query_rope(values_in, gain):
        return rotate(rms_scale(values_in, gain), cosine, sine)

    query_low = query_rope(query_raw, query_gain_f).astype(jnp.bfloat16)
    key_low = query_rope(key_raw, key_gain_f).astype(jnp.bfloat16)
    keys_all, values_all = (
        lax.all_gather(key_low, "ctx", axis=0, tiled=True),
        lax.all_gather(value_low, "ctx", axis=0, tiled=True),
    )
    key_pos = jnp.concatenate(
        [device_positions(other, ctx_count, rows_dev) for other in range(ctx_count)]
    )
    causal = key_pos[None, :] <= positions[:, None]
    query_heads = query_low.reshape(rows_dev, kv_heads, group_size, head_dim).transpose(1, 0, 2, 3)
    key_heads = keys_all.transpose(1, 0, 2)
    value_heads = values_all.transpose(1, 0, 2)
    attended, log_total = lax.map(
        lambda member: attend_head(member[0], member[1], member[2], causal, scale_root),
        (query_heads, key_heads, value_heads),
    )
    attended_low = attended.transpose(1, 0, 2, 3).reshape(rows_dev, width_q).astype(jnp.bfloat16)
    mixed = inputs + jnp.dot(attended_low, out_all, preferred_element_type=jnp.float32)
    normed_mid = rms_scale(mixed, moe_all.astype(jnp.float32))
    low_mid = normed_mid.astype(jnp.bfloat16)
    logits = jnp.dot(low_mid, router_all, preferred_element_type=jnp.float32)
    selected = jnp.take_along_axis(logits, routes, axis=1)
    gates, gate_back = jax.vjp(gating, selected)
    flat_routes = routes.reshape(-1)
    expert_ids = jnp.arange(experts_all, dtype=jnp.int32)
    hit_table = (flat_routes[:, None] == expert_ids[None, :]).astype(jnp.int32)
    slot_index = jnp.sum(jnp.cumsum(hit_table, axis=0) * hit_table, axis=1) - 1
    target = flat_routes * capacity + slot_index
    pair_count = rows_dev * top_k
    source_pair = (
        jnp.full((experts_all * capacity,), pair_count, jnp.int32)
        .at[target]
        .set(jnp.arange(pair_count, dtype=jnp.int32))
    )
    padded = jnp.concatenate([low_mid, jnp.zeros((1, width), jnp.bfloat16)], axis=0)
    outgoing = padded[source_pair // top_k].reshape(experts_all, capacity, width)
    received = lax.all_to_all(outgoing, ("fsdp", "ctx"), split_axis=0, concat_axis=1, tiled=True)
    gate_and_up = jnp.einsum(
        "esd,edf->esf", received, expert_gate_up, preferred_element_type=jnp.float32
    )
    hidden_val, swiglu_back = jax.vjp(swiglu, gate_and_up)
    hidden_low = hidden_val.astype(jnp.bfloat16)
    result_low = jnp.einsum(
        "esf,efd->esd", hidden_low, expert_down, preferred_element_type=jnp.float32
    ).astype(jnp.bfloat16)
    returned = lax.all_to_all(
        result_low, ("fsdp", "ctx"), split_axis=1, concat_axis=0, tiled=True
    ).reshape(experts_all * capacity, width)
    picked = returned[target].reshape(rows_dev, top_k, width).astype(jnp.float32)
    output = (mixed + jnp.sum(gates[:, :, None] * picked, axis=1)).astype(jnp.bfloat16)
    qkv_back, out_back, router_back, attn_back_g, moe_back_g = (
        qkv_all,
        out_all,
        router_all,
        attn_all,
        moe_all,
    )
    grad_final = cotangent.astype(jnp.float32)
    grad_gates = jnp.sum(grad_final[:, None, :] * picked, axis=2)
    grad_result = (
        (gates[:, :, None] * grad_final[:, None, :]).astype(jnp.bfloat16).reshape(pair_count, width)
    )
    grad_padded = jnp.concatenate([grad_result, jnp.zeros((1, width), jnp.bfloat16)], axis=0)
    grad_outgoing = grad_padded[source_pair].reshape(experts_all, capacity, width)
    grad_received = lax.all_to_all(
        grad_outgoing, ("fsdp", "ctx"), split_axis=0, concat_axis=1, tiled=True
    )
    grad_down = jnp.einsum(
        "esf,esd->efd", hidden_low, grad_received, preferred_element_type=jnp.float32
    )
    grad_hidden = jnp.einsum(
        "esd,efd->esf", grad_received, expert_down, preferred_element_type=jnp.float32
    )
    grad_paired = swiglu_back(grad_hidden)[0].astype(jnp.bfloat16)
    grad_gate_up = jnp.einsum(
        "esd,esf->edf", received, grad_paired, preferred_element_type=jnp.float32
    )
    grad_rows = jnp.einsum(
        "esf,edf->esd", grad_paired, expert_gate_up, preferred_element_type=jnp.float32
    ).astype(jnp.bfloat16)
    grad_returned = lax.all_to_all(
        grad_rows, ("fsdp", "ctx"), split_axis=1, concat_axis=0, tiled=True
    ).reshape(experts_all * capacity, width)
    grad_mid = jnp.sum(
        grad_returned[target].reshape(rows_dev, top_k, width).astype(jnp.float32), axis=1
    )
    grad_selected = gate_back(grad_gates)[0]
    route_table = (routes[:, :, None] == expert_ids[None, None, :]).astype(jnp.float32)
    grad_logits = jnp.sum(route_table * grad_selected[:, :, None], axis=1).astype(jnp.bfloat16)
    grad_router = jnp.dot(low_mid.T, grad_logits, preferred_element_type=jnp.float32)
    grad_mid = grad_mid + jnp.dot(grad_logits, router_back.T, preferred_element_type=jnp.float32)
    unused_mid, mid_back = jax.vjp(rms_scale, mixed, moe_back_g.astype(jnp.float32))
    grad_mixed_part, grad_moe_gain = mid_back(grad_mid)
    grad_mixed = grad_final + grad_mixed_part
    grad_branch = grad_mixed.astype(jnp.bfloat16)
    grad_out = jnp.dot(attended_low.T, grad_branch, preferred_element_type=jnp.float32)
    grad_attended = jnp.dot(grad_branch, out_back.T, preferred_element_type=jnp.float32).astype(
        jnp.bfloat16
    )
    grad_heads = grad_attended.reshape(rows_dev, kv_heads, group_size, head_dim).transpose(
        1, 0, 2, 3
    )
    grad_query_h, grad_key_h, grad_value_h = lax.map(
        lambda member: attend_back(
            member[0], member[1], member[2], causal, member[3], member[4], scale_root
        ),
        (query_heads, key_heads, value_heads, log_total, grad_heads),
    )
    grad_keys, grad_values = (
        lax.psum_scatter(
            grad_key_h.transpose(1, 0, 2).astype(jnp.bfloat16),
            "ctx",
            scatter_dimension=0,
            tiled=True,
        ).astype(jnp.float32),
        lax.psum_scatter(
            grad_value_h.transpose(1, 0, 2).astype(jnp.bfloat16),
            "ctx",
            scatter_dimension=0,
            tiled=True,
        ).astype(jnp.float32),
    )
    grad_query_rot = (
        grad_query_h.transpose(1, 0, 2, 3).reshape(rows_dev, heads, head_dim).astype(jnp.bfloat16)
    )
    grad_query_rot = lax.optimization_barrier(grad_query_rot).astype(jnp.float32)
    grad_key_rot = lax.optimization_barrier(grad_keys.astype(jnp.bfloat16)).astype(jnp.float32)
    unused_query, query_back = jax.vjp(query_rope, query_raw, query_gain_f)
    grad_query_raw, grad_query_gain = query_back(grad_query_rot)
    unused_key, key_back = jax.vjp(query_rope, key_raw, key_gain_f)
    grad_key_raw, grad_key_gain = key_back(grad_key_rot)
    grad_projected = jnp.concatenate(
        [
            grad_query_raw.reshape(rows_dev, width_q).astype(jnp.bfloat16),
            grad_key_raw.reshape(rows_dev, width_k).astype(jnp.bfloat16),
            grad_values.reshape(rows_dev, width_k).astype(jnp.bfloat16),
        ],
        axis=1,
    )
    grad_qkv = jnp.dot(low_in.T, grad_projected, preferred_element_type=jnp.float32)
    grad_normed = jnp.dot(grad_projected, qkv_back.T, preferred_element_type=jnp.float32)
    unused_in, in_back = jax.vjp(rms_scale, inputs, attn_back_g.astype(jnp.float32))
    grad_in_part, grad_attn_gain = in_back(grad_normed)
    grad_tokens = grad_mixed + grad_in_part
    gradients = (grad_qkv, grad_out, grad_router, grad_attn_gain, grad_moe_gain)
    pieces = (
        lax.psum_scatter(gradients[0], "fsdp", scatter_dimension=0, tiled=True),
        lax.psum_scatter(gradients[1], "fsdp", scatter_dimension=0, tiled=True),
        lax.psum_scatter(gradients[2], "fsdp", scatter_dimension=0, tiled=True),
        lax.psum_scatter(gradients[3], "fsdp", scatter_dimension=0, tiled=True),
        lax.psum_scatter(gradients[4], "fsdp", scatter_dimension=0, tiled=True),
    )
    reduced = (
        lax.psum(pieces[0].astype(jnp.bfloat16), "ctx").astype(jnp.float32),
        lax.psum(pieces[1].astype(jnp.bfloat16), "ctx").astype(jnp.float32),
        lax.psum(pieces[2].astype(jnp.bfloat16), "ctx").astype(jnp.float32),
        lax.psum(pieces[3].astype(jnp.bfloat16), "ctx").astype(jnp.float32),
        lax.psum(pieces[4].astype(jnp.bfloat16), "ctx").astype(jnp.float32),
    )
    gain_sums = lax.psum((grad_query_gain, grad_key_gain), ("fsdp", "ctx"))
    return (
        output,
        grad_tokens,
        reduced[0],
        reduced[1],
        reduced[2],
        reduced[3],
        reduced[4],
        gain_sums[0],
        gain_sums[1],
        grad_gate_up,
        grad_down,
    )


low = jnp.bfloat16
full = jnp.float32
plain = (((1,), (0,)), ((), ()))
rhs_turned = (((1,), (1,)), ((), ()))
lhs_turned = (((0,), (0,)), ((), ()))
vmem_bytes = 58 << 20


def mul(left, right, dims=plain):
    return lax.dot_general(left, right, dims, preferred_element_type=full)


def core_pairs(fsdp):
    return [(i, i ^ 1) for i in range(fsdp)]


def side_pairs(fsdp):
    return [(i, i ^ 2) for i in range(fsdp)]


def swap_core(values):
    return lax.ppermute(values, "fsdp", core_pairs(lax.axis_size("fsdp")))


def swap_side(values):
    return lax.ppermute(values, "fsdp", side_pairs(lax.axis_size("fsdp")))


def swap_ctx(values):
    return lax.ppermute(values, "ctx", [(0, 1), (1, 0)])


def add_low(one, two):
    return (one.astype(full) + two.astype(full)).astype(low)


def take(values, index):
    return lax.dynamic_index_in_dim(values, index, 0, keepdims=False)


def halve(values, index, swap):
    return add_low(take(values, index), swap(take(values, 1 - index)))


def line_sum(values, place):
    count = values.shape[0]
    fsdp = lax.axis_size("fsdp")
    up = down = None
    for step in range(1, count):
        pairs_up = [
            (i, i + 4) for i in range(fsdp - 4) if i // 4 < step
        ]
        pairs_down = [
            (i, i - 4) for i in range(4, fsdp) if count - 1 - i // 4 < step
        ]
        send_up = take(values, jnp.clip(count - step + place, 0, count - 1))
        send_down = take(values, jnp.clip(place + step - count, 0, count - 1))
        if up is not None:
            send_up = add_low(send_up, up)
            send_down = add_low(send_down, down)
        up = lax.ppermute(send_up, "fsdp", pairs_up)
        down = lax.ppermute(send_down, "fsdp", pairs_down)
    return take(values, place).astype(full) + up.astype(full) + down.astype(full)


def sum_rows(keep, send, place):
    mine = add_low(keep, swap_core(send))
    half = keep.shape[-1] // 2
    one, two = mine[..., :half], mine[..., half:]
    one = add_low(one[:, 0], swap_ctx(one[:, 1]))
    two = add_low(two[0], swap_side(two[1]))
    one = add_low(one[0], swap_side(one[1]))
    two = add_low(two[0], swap_ctx(two[1]))
    return jnp.concatenate([line_sum(one, place), line_sum(two, place)], axis=-1)


def sum_fsdp(values, place, side, core):
    fsdp = lax.axis_size("fsdp")
    rows, width = values.shape[0] // fsdp, values.shape[1]
    parts = values.reshape(fsdp // 2, 2, rows, width).swapaxes(0, 1)
    mine = halve(parts, core, swap_core).reshape(fsdp // 4, 2, rows, width)
    half = width // 2
    one, two = mine[..., :half], mine[..., half:]
    one = line_sum(halve(one.swapaxes(0, 1), side, swap_side), place)
    two = line_sum(two, place).astype(low)
    two = take(two, side).astype(full) + swap_side(take(two, 1 - side)).astype(full)
    return jnp.concatenate([one, two], axis=-1)


def sum_all(values, fsdp):
    values = values + lax.ppermute(values, "fsdp", core_pairs(fsdp))
    values = values + swap_ctx(values)
    step = 2
    while step < fsdp:
        values = values + lax.ppermute(values, "fsdp", [(i, i ^ step) for i in range(fsdp)])
        step *= 2
    return values


def turn(values):
    return pltpu.roll(values, values.shape[-1] // 2, 1)


def norm_rope(raw, gain, cosine, sine):
    scale = lax.rsqrt(jnp.mean(raw * raw, axis=-1, keepdims=True) + eps_norm)
    scaled = raw * scale * gain
    return scaled * cosine + turn(scaled) * sine


def norm_rope_back(raw, gain, cosine, sine, grad):
    scale = lax.rsqrt(jnp.mean(raw * raw, axis=-1, keepdims=True) + eps_norm)
    unit = raw * scale
    grad_scaled = grad * cosine - turn(grad) * sine
    grad_gain = jnp.sum(grad_scaled * unit, axis=0, keepdims=True)
    grad_unit = grad_scaled * gain
    grad_raw = scale * (grad_unit - unit * jnp.mean(grad_unit * unit, axis=-1, keepdims=True))
    return grad_raw, grad_gain


def tiles_of(rows):
    step = rows // 2
    return [(start, start + step) for start in range(0, rows, step)]


def allowed(start, stop):
    shape = (stop - start, stop)
    return lax.broadcasted_iota(jnp.int32, shape, 1) <= (
        lax.broadcasted_iota(jnp.int32, shape, 0) + start
    )


def attend_kernel(q_ref, k_ref, v_ref, cos_ref, sin_ref, qg_ref, kg_ref, o_ref, qr_ref, kr_ref, vl_ref):
    head_dim = k_ref.shape[1]
    rows = k_ref.shape[0]
    cosine, sine = cos_ref[...], sin_ref[...]
    keys = norm_rope(k_ref[...], kg_ref[...], cosine, sine).astype(low)
    values = v_ref[...].astype(low)
    kr_ref[...] = keys
    vl_ref[...] = values
    for head in range(q_ref.shape[1] // head_dim):
        cols = slice(head * head_dim, (head + 1) * head_dim)
        query = norm_rope(q_ref[:, cols], qg_ref[...], cosine, sine).astype(low)
        qr_ref[:, cols] = query
        for start, stop in tiles_of(rows):
            scores = mul(query[start:stop], keys[:stop], rhs_turned) * (1.0 / math.sqrt(head_dim))
            expo = jnp.where(allowed(start, stop), jnp.exp(scores), 0.0)
            probs = (expo / jnp.sum(expo, axis=-1, keepdims=True)).astype(low)
            o_ref[start:stop, cols] = mul(probs, values[:stop]).astype(low)


def attend_grad_kernel(
    q_ref, k_ref, qr_ref, kr_ref, vl_ref, go_ref, cos_ref, sin_ref, qg_ref, kg_ref,
    dq_ref, dk_ref, dv_ref, dqg_ref, dkg_ref, dk_sum, dv_sum, dq_sum,
):
    head_dim = k_ref.shape[1]
    rows = k_ref.shape[0]
    root = 1.0 / math.sqrt(head_dim)
    cosine, sine = cos_ref[...], sin_ref[...]
    keys, values = kr_ref[...], vl_ref[...]
    gain_sum = jnp.zeros((1, head_dim), full)
    dk_sum[...] = jnp.zeros_like(dk_sum)
    dv_sum[...] = jnp.zeros_like(dv_sum)
    for head in range(q_ref.shape[1] // head_dim):
        cols = slice(head * head_dim, (head + 1) * head_dim)
        for start, stop in tiles_of(rows):
            query = qr_ref[start:stop, cols]
            grad = go_ref[start:stop, cols]
            scores = mul(query, keys[:stop], rhs_turned) * root
            expo = jnp.where(allowed(start, stop), jnp.exp(scores), 0.0)
            probs = expo / jnp.sum(expo, axis=-1, keepdims=True)
            grad_probs = mul(grad, values[:stop], rhs_turned)
            delta = jnp.sum(grad_probs * probs, axis=-1, keepdims=True)
            grad_scores = (probs * (grad_probs - delta)).astype(low)
            dv_sum[:stop] += mul(probs.astype(low), grad, lhs_turned)
            dk_sum[:stop] += mul(grad_scores, query, lhs_turned)
            dq_sum[start:stop] = mul(grad_scores, keys[:stop])
        grad_query = (dq_sum[...] * root).astype(low).astype(full)
        grad_raw, grad_gain = norm_rope_back(q_ref[:, cols], qg_ref[...], cosine, sine, grad_query)
        dq_ref[:, cols] = grad_raw.astype(low)
        gain_sum = gain_sum + grad_gain
    dqg_ref[0] = gain_sum
    grad_key = (dk_sum[...] * root).astype(low).astype(full)
    grad_raw, grad_gain = norm_rope_back(k_ref[...], kg_ref[...], cosine, sine, grad_key)
    dk_ref[...] = grad_raw.astype(low)
    dkg_ref[0] = grad_gain
    dv_ref[...] = dv_sum[...].astype(low)


def attention_specs(rows, head_dim, kv_heads, group):
    wide, narrow = group * head_dim, head_dim
    heads_end = kv_heads * group
    return dict(
        q=pl.BlockSpec((rows, wide), lambda i: (0, i)),
        k=pl.BlockSpec((rows, narrow), lambda i: (0, heads_end + i)),
        v=pl.BlockSpec((rows, narrow), lambda i: (0, heads_end + kv_heads + i)),
        own=pl.BlockSpec((rows, narrow), lambda i: (0, i)),
        table=pl.BlockSpec((rows, head_dim), lambda i: (0, 0)),
        gain=pl.BlockSpec((1, head_dim), lambda i: (0, 0)),
        gain_out=pl.BlockSpec((1, 1, head_dim), lambda i: (i, 0, 0)),
    )


def attend(projected, cosine, sine, query_gain, key_gain, kv_heads, group):
    rows, head_dim = cosine.shape
    s = attention_specs(rows, head_dim, kv_heads, group)
    shape = jax.ShapeDtypeStruct
    work = rows * rows * head_dim * kv_heads * group
    return pl.pallas_call(
        attend_kernel,
        grid=(kv_heads,),
        in_specs=[s["q"], s["k"], s["v"], s["table"], s["table"], s["gain"], s["gain"]],
        out_specs=[s["q"], s["q"], s["own"], s["own"]],
        out_shape=[
            shape((rows, kv_heads * group * head_dim), low),
            shape((rows, kv_heads * group * head_dim), low),
            shape((rows, kv_heads * head_dim), low),
            shape((rows, kv_heads * head_dim), low),
        ],
        compiler_params=pltpu.CompilerParams(vmem_limit_bytes=48 << 20),
        cost_estimate=pl.CostEstimate(
            flops=4 * work, bytes_accessed=projected.size * 6, transcendentals=work // head_dim
        ),
        name="attend",
    )(projected, projected, projected, cosine, sine, query_gain, key_gain)


def attend_grad(projected, roped_q, roped_k, values_low, grad, cosine, sine, query_gain, key_gain, kv_heads, group):
    rows, head_dim = cosine.shape
    s = attention_specs(rows, head_dim, kv_heads, group)
    shape = jax.ShapeDtypeStruct
    work = rows * rows * head_dim * kv_heads * group
    return pl.pallas_call(
        attend_grad_kernel,
        grid=(kv_heads,),
        in_specs=[
            s["q"], s["k"], s["q"], s["own"], s["own"], s["q"],
            s["table"], s["table"], s["gain"], s["gain"],
        ],
        out_specs=[s["q"], s["own"], s["own"], s["gain_out"], s["gain_out"]],
        out_shape=[
            shape((rows, kv_heads * group * head_dim), low),
            shape((rows, kv_heads * head_dim), low),
            shape((rows, kv_heads * head_dim), low),
            shape((kv_heads, 1, head_dim), full),
            shape((kv_heads, 1, head_dim), full),
        ],
        scratch_shapes=[pltpu.VMEM((rows, head_dim), full)] * 3,
        compiler_params=pltpu.CompilerParams(vmem_limit_bytes=48 << 20),
        cost_estimate=pl.CostEstimate(
            flops=10 * work, bytes_accessed=projected.size * 10, transcendentals=work // head_dim
        ),
        name="attend_grad",
    )(projected, projected, roped_q, roped_k, values_low, grad, cosine, sine, query_gain, key_gain)


def expert_kernel(
    who, order, m_ref, g_ref, r_ref, w_ref, gu_ref, dn_ref,
    keep_out, send_out, keep_back, send_back, gate_back, rows_ref, dy_ref, z_ref, pair_ref,
):
    expert, core = who[0], who[1]
    block = m_ref.shape[3]
    hidden = dn_ref.shape[0]
    slots = z_ref.shape[0] // 2
    shape = (block, block)
    earlier = (
        lax.broadcasted_iota(jnp.int32, shape, 0) < lax.broadcasted_iota(jnp.int32, shape, 1)
    ).astype(low)
    slot_ids = lax.broadcasted_iota(jnp.int32, (slots, block), 0)
    places, picks, weights, rows, grads = [], [], [], [], []
    for part in range(2):
        at = lax.rem(core + part, 2)
        named = r_ref[0, at, 0] == expert
        ones = jnp.where(named, 1.0, 0.0)
        hit = jnp.sum(ones, axis=0, keepdims=True)
        gate = jnp.sum(jnp.where(named, w_ref[0, at, 0], 0.0), axis=0, keepdims=True)
        count = jnp.sum(mul(ones.astype(low), earlier), axis=0, keepdims=True).astype(jnp.int32)
        place = (slot_ids == count) & (hit > 0.5)
        pick = place.astype(full).astype(low)
        places.append(place)
        picks.append(pick)
        weights.append(jnp.sum(jnp.where(place, gate, 0.0), axis=1, keepdims=True))
        rows.append(mul(pick, m_ref[0, at, 0]).astype(low))
        grads.append(mul(pick, g_ref[0, at, 0]))
    row, grad, weight = (jnp.concatenate(items, axis=0) for items in (rows, grads, weights))
    rows_ref[...] = row
    paired = mul(row, gu_ref[...])
    gate_in, up = paired[:, :hidden], paired[:, hidden:]
    sig = jax.nn.sigmoid(gate_in)
    act = gate_in * sig
    z = (act * up).astype(low)
    z_ref[...] = z
    y = mul(z, dn_ref[...]).astype(low).astype(full)
    grad_gate = jnp.sum(grad * y, axis=1, keepdims=True)
    y_scaled = (weight * y).astype(low)
    dy = (weight * grad).astype(low)
    dy_ref[...] = dy
    for part, out in enumerate((keep_out, send_out)):
        mine = slice(part * slots, (part + 1) * slots)
        out[0] = mul(picks[part], y_scaled[mine], lhs_turned).astype(low)
        gate_back[0, lax.rem(core + part, 2), 0] = jnp.sum(
            jnp.where(places[part], grad_gate[mine], 0.0), axis=0, keepdims=True
        )
    dz = mul(dy, dn_ref[...], rhs_turned)
    grad_in = dz * up * (sig * (1.0 + gate_in * (1.0 - sig)))
    pair = jnp.concatenate([grad_in, dz * act], axis=1).astype(low)
    pair_ref[...] = pair
    back = mul(pair, gu_ref[...], rhs_turned).astype(low)
    for part, out in enumerate((keep_back, send_back)):
        mine = slice(part * slots, (part + 1) * slots)
        out[0] = mul(picks[part], back[mine], lhs_turned).astype(low)


def run_expert(who, order, m_all, g_all, routes_all, gates_all, gate_up, down, slots):
    places, _, _, block, width = m_all.shape
    top = routes_all.shape[3]
    paired = gate_up.shape[1]
    steps = places * 2
    total = steps * 2 * slots
    hidden = paired // 2
    shape = jax.ShapeDtypeStruct

    def token_at(i, who, order):
        return (order[2 * i], 0, order[2 * i + 1], 0, 0)

    def fixed(i, who, order):
        return (0, 0)

    def flat(i, who, order):
        return (i, 0)

    def stacked(i, who, order):
        return (i, 0, 0)

    tokens = pl.BlockSpec((1, 2, 1, block, width), token_at)
    small = pl.BlockSpec((1, 2, 1, top, block), token_at)
    out_rows = pl.BlockSpec((1, block, width), stacked)
    slot_rows = [pl.BlockSpec((2 * slots, n), flat) for n in (width, width, hidden, paired)]
    grid_spec = pltpu.PrefetchScalarGridSpec(
        num_scalar_prefetch=2,
        grid=(steps,),
        in_specs=[
            tokens, tokens, small, small,
            pl.BlockSpec(gate_up.shape, fixed, pipeline_mode=pl.Buffered(1)),
            pl.BlockSpec(down.shape, fixed, pipeline_mode=pl.Buffered(1)),
        ],
        out_specs=[out_rows] * 4 + [pl.BlockSpec((1, 2, 1, 1, block), token_at)] + slot_rows,
    )
    return pl.pallas_call(
        expert_kernel,
        grid_spec=grid_spec,
        out_shape=[shape((steps, block, width), low)] * 4
        + [shape((places, 2, 2, 1, block), full)]
        + [shape((total, n), low) for n in (width, width, hidden, paired)],
        compiler_params=pltpu.CompilerParams(vmem_limit_bytes=vmem_bytes),
        cost_estimate=pl.CostEstimate(
            flops=total * width * (4 * paired + 4 * hidden + 8 * block),
            bytes_accessed=steps * block * width * 16 + total * (width * 4 + paired * 3),
            transcendentals=total * hidden,
        ),
        name="experts",
    )(who, order, m_all, g_all, routes_all, gates_all, gate_up, down)


def rms_back(values, gain, grad):
    scale = lax.rsqrt(jnp.mean(values * values, axis=-1, keepdims=True) + eps_norm)
    unit = values * scale
    grad_gain = jnp.sum(grad * unit, axis=0)
    grad_unit = grad * gain
    back = scale * (grad_unit - unit * jnp.mean(grad_unit * unit, axis=-1, keepdims=True))
    return back, grad_gain


def in_order(first, second):
    half = first.shape[0] // 2
    return jnp.concatenate([first[:half], second, first[half:]], axis=0)


def of_block(values, rank):
    quarter = values.shape[0] // 4
    outer = jnp.concatenate([values[:quarter], values[3 * quarter :]], axis=0)
    return jnp.where(rank == 0, outer, values[quarter : 3 * quarter])


def body_gathered(
    tokens, qkv_weight, out_weight, router_weight, attn_gain, moe_gain, query_gain, key_gain,
    expert_gate_up, expert_down, routes, cotangent,
):
    rows_dev, width = tokens.shape
    head_dim = query_gain.shape[0]
    top_k = routes.shape[1]
    fsdp = lax.axis_size("fsdp")
    spot = lax.axis_index("fsdp")
    rank = lax.axis_index("ctx")
    place, side, core = spot // 4, (spot // 2) % 2, spot % 2
    shard = qkv_weight.shape[0]
    heads = out_weight.shape[0] * fsdp // head_dim
    kv_heads = (qkv_weight.shape[1] // head_dim - heads) // 2
    group = heads // kv_heads // 2
    my_heads = heads // 2
    width_q, width_k = my_heads * head_dim, kv_heads * head_dim
    experts_all = router_weight.shape[1]
    capacity = 2 * rows_dev * top_k // experts_all
    both = ("fsdp", "ctx")

    def sequence(values):
        other = swap_ctx(values)
        first = jnp.where(rank == 0, values, other)
        second = jnp.where(rank == 0, other, values)
        return in_order(first, second)

    by_parity = qkv_weight[:, : 2 * width_q].reshape(shard, my_heads, 2, head_dim)
    q_local = jnp.where(rank == 0, by_parity[:, :, 0], by_parity[:, :, 1]).reshape(shard, width_q)
    qkv_local = jnp.concatenate([q_local, qkv_weight[:, 2 * width_q :]], axis=1)
    out_local = lax.dynamic_slice_in_dim(out_weight, rank * head_dim, head_dim, 0)
    small_local = jnp.concatenate([router_weight, attn_gain[:, None], moe_gain[:, None]], axis=1)
    small_all = lax.all_gather(small_local, "fsdp", axis=0, tiled=True)
    qkv_all = lax.all_gather(qkv_local, "fsdp", axis=0, tiled=True)
    out_all = lax.all_gather(out_local, "fsdp", axis=0, tiled=True)
    router_all = small_all[:, :experts_all]
    attn_all = small_all[:, experts_all].astype(full)
    moe_all = small_all[:, experts_all + 1].astype(full)
    routes_all = lax.all_gather(routes.T, both, axis=0)
    g_all = lax.all_gather(cotangent, both, axis=0)

    sequence_in = sequence(tokens).astype(full)
    low_in = rms_scale(sequence_in, attn_all).astype(low)
    projected = mul(low_in, qkv_all)
    cosine, sine = (t[:, 0] for t in angles(jnp.arange(2 * rows_dev, dtype=jnp.int32), head_dim))
    sine = jnp.concatenate([-sine[:, : head_dim // 2], sine[:, head_dim // 2 :]], axis=1)
    gain_q, gain_k = query_gain.astype(full)[None], key_gain.astype(full)[None]
    attended, roped_q, roped_k, values_low = attend(
        projected, cosine, sine, gain_q, gain_k, kv_heads, group
    )
    branch = mul(attended, out_all)
    inputs = tokens.astype(full)
    mixed = (
        inputs
        + of_block(branch, rank)
        + swap_ctx(of_block(branch, 1 - rank).astype(low)).astype(full)
    )
    low_mid = rms_scale(mixed, moe_all).astype(low)
    m_all = lax.all_gather(low_mid, both, axis=0)

    logits = mul(low_mid, router_all)
    named = routes[:, :, None] == jnp.arange(experts_all, dtype=jnp.int32)[None, None, :]
    selected = jnp.sum(jnp.where(named, logits[:, None, :], 0.0), axis=2)
    gates = gating(selected)
    gates_all = lax.all_gather(gates.T, both, axis=0)

    steps = jnp.arange(fsdp, dtype=jnp.int32)
    lines = fsdp // 4
    order = jnp.stack(
        [
            (steps % lines) * 2 + (side + steps // (2 * lines)) % 2,
            (rank + steps // lines) % 2,
        ],
        axis=1,
    ).reshape(-1)
    who = jnp.stack([spot * 2 + rank, core]).astype(jnp.int32)
    grid_of = (fsdp // 2, 2, 2)
    keep_out, send_out, keep_back, send_back, gate_back, rows, grad_rows, hidden, grad_pair = run_expert(
        who,
        order.astype(jnp.int32),
        m_all.reshape(*grid_of, rows_dev, width),
        g_all.reshape(*grid_of, rows_dev, width),
        routes_all.reshape(*grid_of, top_k, rows_dev),
        gates_all.reshape(*grid_of, top_k, rows_dev),
        expert_gate_up[0],
        expert_down[0],
        capacity,
    )
    parts = (2, 2, lines, rows_dev, width)
    grad_gates = lax.all_to_all(
        gate_back.reshape(fsdp * 2, rows_dev), both, split_axis=0, concat_axis=0, tiled=True
    ).T
    grad_mid = sum_rows(keep_back.reshape(parts), send_back.reshape(parts), place)
    grad_down = mul(hidden, grad_rows, lhs_turned)[None]
    grad_gate_up = mul(rows, grad_pair, lhs_turned)[None]
    output = (mixed + sum_rows(keep_out.reshape(parts), send_out.reshape(parts), place)).astype(low)

    gates_wide = jnp.sum(jnp.where(named, gates[:, :, None], 0.0), axis=1)
    chosen = jnp.any(named, axis=1)
    grad_wide = jnp.where(chosen, grad_gates, 0.0)
    grad_logits = (
        gates_wide * (grad_wide - jnp.sum(gates_wide * grad_wide, axis=1, keepdims=True))
    ).astype(low)
    grad_router = mul(low_mid, grad_logits, lhs_turned)
    grad_mid = grad_mid + mul(grad_logits, router_all, rhs_turned)
    grad_mixed_part, grad_moe_gain = rms_back(mixed, moe_all, grad_mid)
    grad_mixed = cotangent.astype(full) + grad_mixed_part

    grad_branch = sequence(grad_mixed.astype(low))
    grad_attended = mul(grad_branch, out_all, rhs_turned).astype(low)
    grad_out_part = mul(attended, grad_branch, lhs_turned).astype(low)
    grad_q, grad_k, grad_v, gain_q_part, gain_k_part = attend_grad(
        projected, roped_q, roped_k, values_low, grad_attended, cosine, sine, gain_q, gain_k, kv_heads, group
    )
    grad_projected = jnp.concatenate([grad_q, grad_k, grad_v], axis=1)
    grad_qkv_part = mul(low_in, grad_projected, lhs_turned).astype(low)
    grad_normed_part = mul(grad_projected, qkv_all, rhs_turned)
    grad_normed = of_block(grad_normed_part, rank) + swap_ctx(
        of_block(grad_normed_part, 1 - rank).astype(low)
    ).astype(full)
    grad_in_part, grad_attn_gain = rms_back(inputs, attn_all, grad_normed)
    grad_tokens = grad_mixed + grad_in_part

    out_mine = sum_fsdp(grad_out_part, place, side, core)
    out_other = swap_ctx(out_mine.astype(low)).astype(full)
    grad_out = jnp.where(
        rank == 0,
        jnp.concatenate([out_mine, out_other], axis=0),
        jnp.concatenate([out_other, out_mine], axis=0),
    )
    qkv_mine = sum_fsdp(grad_qkv_part, place, side, core)
    qkv_other = swap_ctx(qkv_mine.astype(low)).astype(full)
    q_mine = qkv_mine[:, :width_q].reshape(shard, my_heads, 1, head_dim)
    q_other = qkv_other[:, :width_q].reshape(shard, my_heads, 1, head_dim)
    grad_q_all = jnp.where(
        rank == 0,
        jnp.concatenate([q_mine, q_other], axis=2),
        jnp.concatenate([q_other, q_mine], axis=2),
    ).reshape(shard, 2 * width_q)
    grad_qkv = jnp.concatenate(
        [grad_q_all, qkv_mine[:, width_q:] + qkv_other[:, width_q:]], axis=1
    )
    total = sum_all(
        jnp.concatenate(
            [
                grad_router,
                grad_attn_gain[:, None],
                grad_moe_gain[:, None],
            ],
            axis=1,
        ),
        fsdp,
    )
    gains = sum_all(
        jnp.concatenate([jnp.sum(gain_q_part, axis=0), jnp.sum(gain_k_part, axis=0)], axis=0), fsdp
    )
    owned = lax.dynamic_slice_in_dim(total, spot * shard, shard, 0)
    return (
        output,
        grad_tokens,
        grad_qkv,
        grad_out,
        owned[:, :experts_all],
        owned[:, experts_all],
        owned[:, experts_all + 1],
        gains[0],
        gains[1],
        grad_gate_up,
        grad_down,
    )


gathered_bytes = 1 << 26


def choose_body(*args):
    tokens, gate_up = args[0], args[8]
    fsdp, ctx = lax.axis_size("fsdp"), lax.axis_size("ctx")
    fits = tokens.size * tokens.dtype.itemsize * fsdp * ctx <= gathered_bytes
    if fits and fsdp % 4 == 0 and ctx == 2 and gate_up.shape[0] == 1:
        return body_gathered(*args)
    return body_routed(*args)


def solution(mesh):
    in_specs = (
        P(("fsdp", "ctx"), None),
        P("fsdp", None),
        P("fsdp", None),
        P("fsdp", None),
        P("fsdp"),
        P("fsdp"),
        P(),
        P(),
        P(("fsdp", "ctx"), None, None),
        P(("fsdp", "ctx"), None, None),
        P(("fsdp", "ctx"), None),
        P(("fsdp", "ctx"), None),
    )
    out_specs = (
        P(("fsdp", "ctx"), None),
        P(("fsdp", "ctx"), None),
        P("fsdp", None),
        P("fsdp", None),
        P("fsdp", None),
        P("fsdp"),
        P("fsdp"),
        P(),
        P(),
        P(("fsdp", "ctx"), None, None),
        P(("fsdp", "ctx"), None, None),
    )
    return jax.shard_map(choose_body, mesh=mesh, in_specs=in_specs, out_specs=out_specs, check_vma=False)
```

```python
import functools
import math

import jax
import jax.numpy as jnp
from jax import lax
from jax.experimental import pallas as pl
from jax.experimental.pallas import tpu as pltpu
from jax.sharding import PartitionSpec as P

eps_norm = 1e-06
theta_base = 1000000.0


def rms_scale(values, gain):
    return values * lax.rsqrt(jnp.mean(values * values, axis=-1, keepdims=True) + eps_norm) * gain


def rotate(values, cosine, sine):
    half_width = values.shape[-1] // 2
    turned = jnp.concatenate([-values[..., half_width:], values[..., :half_width]], axis=-1)
    return values * cosine + turned * sine


def angles(positions, width):
    freqs = theta_base ** (-(jnp.arange(width // 2, dtype=jnp.float32) * 2.0) / width)
    phase = positions.astype(jnp.float32)[:, None] * freqs[None, :]
    phase = jnp.concatenate([phase, phase], axis=-1)
    return (jnp.cos(phase)[:, None, :], jnp.sin(phase)[:, None, :])


def device_positions(block_rank, ctx_count, tok_rows):
    half_rows = tok_rows // 2
    within = jnp.arange(tok_rows, dtype=jnp.int32)
    span_id = jnp.where(within < half_rows, block_rank, 2 * ctx_count - 1 - block_rank)
    return span_id * half_rows + within % half_rows


def attend_head(query, keys_in, values_in, causal, scale_root):
    scores = (
        jnp.einsum("tgd,sd->gts", query, keys_in, preferred_element_type=jnp.float32) / scale_root
    )
    expo = jnp.where(causal[None], jnp.exp(scores), 0.0)
    totals = jnp.sum(expo, axis=-1, keepdims=True)
    probs = (expo / totals).astype(jnp.bfloat16)
    attended = jnp.einsum("gts,sd->tgd", probs, values_in, preferred_element_type=jnp.float32)
    return (attended, jnp.log(totals[..., 0]))


def attend_back(query, keys_in, values_in, causal, log_total, grad_attended, scale_root):
    scores = (
        jnp.einsum("tgd,sd->gts", query, keys_in, preferred_element_type=jnp.float32) / scale_root
    )
    probs = jnp.where(causal[None], jnp.exp(scores - log_total[..., None]), 0.0)
    low_probs = probs.astype(jnp.bfloat16)
    grad_values = jnp.einsum(
        "gts,tgd->sd", low_probs, grad_attended, preferred_element_type=jnp.float32
    )
    grad_probs = jnp.einsum(
        "tgd,sd->gts", grad_attended, values_in, preferred_element_type=jnp.float32
    )
    delta_rows = jnp.sum(grad_probs * probs, axis=-1, keepdims=True)
    grad_scores = (probs * (grad_probs - delta_rows)).astype(jnp.bfloat16)
    grad_query = (
        jnp.einsum("gts,sd->tgd", grad_scores, keys_in, preferred_element_type=jnp.float32)
        / scale_root
    )
    grad_keys = (
        jnp.einsum("gts,tgd->sd", grad_scores, query, preferred_element_type=jnp.float32)
        / scale_root
    )
    return (grad_query, grad_keys, grad_values)


def swiglu(paired):
    half_width = paired.shape[-1] // 2
    return jax.nn.silu(paired[..., :half_width]) * paired[..., half_width:]


def gating(selected):
    expo = jnp.exp(selected)
    return expo / jnp.sum(expo, axis=1, keepdims=True)


def body_routed(
    tokens,
    qkv_weight,
    out_weight,
    router_weight,
    attn_gain,
    moe_gain,
    query_gain,
    key_gain,
    expert_gate_up,
    expert_down,
    routes,
    cotangent,
):
    rows_dev, width = tokens.shape
    head_dim = query_gain.shape[0]
    top_k = routes.shape[1]
    ctx_count = lax.axis_size("ctx")
    ctx_rank = lax.axis_index("ctx")
    qkv_all, out_all, router_all, attn_all, moe_all = (
        lax.all_gather(qkv_weight, "fsdp", axis=0, tiled=True),
        lax.all_gather(out_weight, "fsdp", axis=0, tiled=True),
        lax.all_gather(router_weight, "fsdp", axis=0, tiled=True),
        lax.all_gather(attn_gain, "fsdp", axis=0, tiled=True),
        lax.all_gather(moe_gain, "fsdp", axis=0, tiled=True),
    )
    experts_all = router_all.shape[1]
    heads = out_all.shape[0] // head_dim
    kv_heads = (qkv_all.shape[1] // head_dim - heads) // 2
    group_size = heads // kv_heads
    capacity = 2 * rows_dev * top_k // experts_all
    width_q = heads * head_dim
    width_k = kv_heads * head_dim
    scale_root = math.sqrt(head_dim)
    inputs = tokens.astype(jnp.float32)
    normed_in = rms_scale(inputs, attn_all.astype(jnp.float32))
    low_in = normed_in.astype(jnp.bfloat16)
    projected = jnp.dot(low_in, qkv_all, preferred_element_type=jnp.float32)
    query_raw = projected[:, :width_q].reshape(rows_dev, heads, head_dim)
    key_raw = projected[:, width_q : width_q + width_k].reshape(rows_dev, kv_heads, head_dim)
    value_low = (
        projected[:, width_q + width_k :].astype(jnp.bfloat16).reshape(rows_dev, kv_heads, head_dim)
    )
    positions = device_positions(ctx_rank, ctx_count, rows_dev)
    cosine, sine = angles(positions, head_dim)
    query_gain_f = query_gain.astype(jnp.float32)
    key_gain_f = key_gain.astype(jnp.float32)

    def query_rope(values_in, gain):
        return rotate(rms_scale(values_in, gain), cosine, sine)

    query_low = query_rope(query_raw, query_gain_f).astype(jnp.bfloat16)
    key_low = query_rope(key_raw, key_gain_f).astype(jnp.bfloat16)
    keys_all, values_all = (
        lax.all_gather(key_low, "ctx", axis=0, tiled=True),
        lax.all_gather(value_low, "ctx", axis=0, tiled=True),
    )
    key_pos = jnp.concatenate(
        [device_positions(other, ctx_count, rows_dev) for other in range(ctx_count)]
    )
    causal = key_pos[None, :] <= positions[:, None]
    query_heads = query_low.reshape(rows_dev, kv_heads, group_size, head_dim).transpose(1, 0, 2, 3)
    key_heads = keys_all.transpose(1, 0, 2)
    value_heads = values_all.transpose(1, 0, 2)
    attended, log_total = lax.map(
        lambda member: attend_head(member[0], member[1], member[2], causal, scale_root),
        (query_heads, key_heads, value_heads),
    )
    attended_low = attended.transpose(1, 0, 2, 3).reshape(rows_dev, width_q).astype(jnp.bfloat16)
    mixed = inputs + jnp.dot(attended_low, out_all, preferred_element_type=jnp.float32)
    normed_mid = rms_scale(mixed, moe_all.astype(jnp.float32))
    low_mid = normed_mid.astype(jnp.bfloat16)
    logits = jnp.dot(low_mid, router_all, preferred_element_type=jnp.float32)
    selected = jnp.take_along_axis(logits, routes, axis=1)
    gates, gate_back = jax.vjp(gating, selected)
    flat_routes = routes.reshape(-1)
    expert_ids = jnp.arange(experts_all, dtype=jnp.int32)
    hit_table = (flat_routes[:, None] == expert_ids[None, :]).astype(jnp.int32)
    slot_index = jnp.sum(jnp.cumsum(hit_table, axis=0) * hit_table, axis=1) - 1
    target = flat_routes * capacity + slot_index
    pair_count = rows_dev * top_k
    source_pair = (
        jnp.full((experts_all * capacity,), pair_count, jnp.int32)
        .at[target]
        .set(jnp.arange(pair_count, dtype=jnp.int32))
    )
    padded = jnp.concatenate([low_mid, jnp.zeros((1, width), jnp.bfloat16)], axis=0)
    outgoing = padded[source_pair // top_k].reshape(experts_all, capacity, width)
    received = lax.all_to_all(outgoing, ("fsdp", "ctx"), split_axis=0, concat_axis=1, tiled=True)
    gate_and_up = jnp.einsum(
        "esd,edf->esf", received, expert_gate_up, preferred_element_type=jnp.float32
    )
    hidden_val, swiglu_back = jax.vjp(swiglu, gate_and_up)
    hidden_low = hidden_val.astype(jnp.bfloat16)
    result_low = jnp.einsum(
        "esf,efd->esd", hidden_low, expert_down, preferred_element_type=jnp.float32
    ).astype(jnp.bfloat16)
    returned = lax.all_to_all(
        result_low, ("fsdp", "ctx"), split_axis=1, concat_axis=0, tiled=True
    ).reshape(experts_all * capacity, width)
    picked = returned[target].reshape(rows_dev, top_k, width).astype(jnp.float32)
    output = (mixed + jnp.sum(gates[:, :, None] * picked, axis=1)).astype(jnp.bfloat16)
    qkv_back, out_back, router_back, attn_back_g, moe_back_g = (
        qkv_all,
        out_all,
        router_all,
        attn_all,
        moe_all,
    )
    grad_final = cotangent.astype(jnp.float32)
    grad_gates = jnp.sum(grad_final[:, None, :] * picked, axis=2)
    grad_result = (
        (gates[:, :, None] * grad_final[:, None, :]).astype(jnp.bfloat16).reshape(pair_count, width)
    )
    grad_padded = jnp.concatenate([grad_result, jnp.zeros((1, width), jnp.bfloat16)], axis=0)
    grad_outgoing = grad_padded[source_pair].reshape(experts_all, capacity, width)
    grad_received = lax.all_to_all(
        grad_outgoing, ("fsdp", "ctx"), split_axis=0, concat_axis=1, tiled=True
    )
    grad_down = jnp.einsum(
        "esf,esd->efd", hidden_low, grad_received, preferred_element_type=jnp.float32
    )
    grad_hidden = jnp.einsum(
        "esd,efd->esf", grad_received, expert_down, preferred_element_type=jnp.float32
    )
    grad_paired = swiglu_back(grad_hidden)[0].astype(jnp.bfloat16)
    grad_gate_up = jnp.einsum(
        "esd,esf->edf", received, grad_paired, preferred_element_type=jnp.float32
    )
    grad_rows = jnp.einsum(
        "esf,edf->esd", grad_paired, expert_gate_up, preferred_element_type=jnp.float32
    ).astype(jnp.bfloat16)
    grad_returned = lax.all_to_all(
        grad_rows, ("fsdp", "ctx"), split_axis=1, concat_axis=0, tiled=True
    ).reshape(experts_all * capacity, width)
    grad_mid = jnp.sum(
        grad_returned[target].reshape(rows_dev, top_k, width).astype(jnp.float32), axis=1
    )
    grad_selected = gate_back(grad_gates)[0]
    route_table = (routes[:, :, None] == expert_ids[None, None, :]).astype(jnp.float32)
    grad_logits = jnp.sum(route_table * grad_selected[:, :, None], axis=1).astype(jnp.bfloat16)
    grad_router = jnp.dot(low_mid.T, grad_logits, preferred_element_type=jnp.float32)
    grad_mid = grad_mid + jnp.dot(grad_logits, router_back.T, preferred_element_type=jnp.float32)
    unused_mid, mid_back = jax.vjp(rms_scale, mixed, moe_back_g.astype(jnp.float32))
    grad_mixed_part, grad_moe_gain = mid_back(grad_mid)
    grad_mixed = grad_final + grad_mixed_part
    grad_branch = grad_mixed.astype(jnp.bfloat16)
    grad_out = jnp.dot(attended_low.T, grad_branch, preferred_element_type=jnp.float32)
    grad_attended = jnp.dot(grad_branch, out_back.T, preferred_element_type=jnp.float32).astype(
        jnp.bfloat16
    )
    grad_heads = grad_attended.reshape(rows_dev, kv_heads, group_size, head_dim).transpose(
        1, 0, 2, 3
    )
    grad_query_h, grad_key_h, grad_value_h = lax.map(
        lambda member: attend_back(
            member[0], member[1], member[2], causal, member[3], member[4], scale_root
        ),
        (query_heads, key_heads, value_heads, log_total, grad_heads),
    )
    grad_keys, grad_values = (
        lax.psum_scatter(
            grad_key_h.transpose(1, 0, 2).astype(jnp.bfloat16),
            "ctx",
            scatter_dimension=0,
            tiled=True,
        ).astype(jnp.float32),
        lax.psum_scatter(
            grad_value_h.transpose(1, 0, 2).astype(jnp.bfloat16),
            "ctx",
            scatter_dimension=0,
            tiled=True,
        ).astype(jnp.float32),
    )
    grad_query_rot = (
        grad_query_h.transpose(1, 0, 2, 3).reshape(rows_dev, heads, head_dim).astype(jnp.bfloat16)
    )
    grad_query_rot = lax.optimization_barrier(grad_query_rot).astype(jnp.float32)
    grad_key_rot = lax.optimization_barrier(grad_keys.astype(jnp.bfloat16)).astype(jnp.float32)
    unused_query, query_back = jax.vjp(query_rope, query_raw, query_gain_f)
    grad_query_raw, grad_query_gain = query_back(grad_query_rot)
    unused_key, key_back = jax.vjp(query_rope, key_raw, key_gain_f)
    grad_key_raw, grad_key_gain = key_back(grad_key_rot)
    grad_projected = jnp.concatenate(
        [
            grad_query_raw.reshape(rows_dev, width_q).astype(jnp.bfloat16),
            grad_key_raw.reshape(rows_dev, width_k).astype(jnp.bfloat16),
            grad_values.reshape(rows_dev, width_k).astype(jnp.bfloat16),
        ],
        axis=1,
    )
    grad_qkv = jnp.dot(low_in.T, grad_projected, preferred_element_type=jnp.float32)
    grad_normed = jnp.dot(grad_projected, qkv_back.T, preferred_element_type=jnp.float32)
    unused_in, in_back = jax.vjp(rms_scale, inputs, attn_back_g.astype(jnp.float32))
    grad_in_part, grad_attn_gain = in_back(grad_normed)
    grad_tokens = grad_mixed + grad_in_part
    gradients = (grad_qkv, grad_out, grad_router, grad_attn_gain, grad_moe_gain)
    pieces = (
        lax.psum_scatter(gradients[0], "fsdp", scatter_dimension=0, tiled=True),
        lax.psum_scatter(gradients[1], "fsdp", scatter_dimension=0, tiled=True),
        lax.psum_scatter(gradients[2], "fsdp", scatter_dimension=0, tiled=True),
        lax.psum_scatter(gradients[3], "fsdp", scatter_dimension=0, tiled=True),
        lax.psum_scatter(gradients[4], "fsdp", scatter_dimension=0, tiled=True),
    )
    reduced = (
        lax.psum(pieces[0].astype(jnp.bfloat16), "ctx").astype(jnp.float32),
        lax.psum(pieces[1].astype(jnp.bfloat16), "ctx").astype(jnp.float32),
        lax.psum(pieces[2].astype(jnp.bfloat16), "ctx").astype(jnp.float32),
        lax.psum(pieces[3].astype(jnp.bfloat16), "ctx").astype(jnp.float32),
        lax.psum(pieces[4].astype(jnp.bfloat16), "ctx").astype(jnp.float32),
    )
    gain_sums = lax.psum((grad_query_gain, grad_key_gain), ("fsdp", "ctx"))
    return (
        output,
        grad_tokens,
        reduced[0],
        reduced[1],
        reduced[2],
        reduced[3],
        reduced[4],
        gain_sums[0],
        gain_sums[1],
        grad_gate_up,
        grad_down,
    )


low = jnp.bfloat16
full = jnp.float32
plain = (((1,), (0,)), ((), ()))
rhs_turned = (((1,), (1,)), ((), ()))
lhs_turned = (((0,), (0,)), ((), ()))
vmem_bytes = 58 << 20


def mul(left, right, dims=plain):
    return lax.dot_general(left, right, dims, preferred_element_type=full)


def core_pairs(fsdp):
    return [(i, i ^ 1) for i in range(fsdp)]


def side_pairs(fsdp):
    return [(i, i ^ 2) for i in range(fsdp)]


def swap_core(values):
    return lax.ppermute(values, "fsdp", core_pairs(lax.axis_size("fsdp")))


def swap_side(values):
    return lax.ppermute(values, "fsdp", side_pairs(lax.axis_size("fsdp")))


def swap_ctx(values):
    return lax.ppermute(values, "ctx", [(0, 1), (1, 0)])


def add_low(one, two):
    return (one.astype(full) + two.astype(full)).astype(low)


def take(values, index):
    return lax.dynamic_index_in_dim(values, index, 0, keepdims=False)


def halve(values, index, swap):
    return add_low(take(values, index), swap(take(values, 1 - index)))


def line_sum(values, place, relative=False):
    count = values.shape[0]
    fsdp = lax.axis_size("fsdp")
    up = down = None

    def part(at):
        at = jnp.clip(at, 0, count - 1)
        return take(values, (place - at) % count if relative else at)

    for step in range(1, count):
        pairs_up = [
            (i, i + 4) for i in range(fsdp - 4) if i // 4 < step
        ]
        pairs_down = [
            (i, i - 4) for i in range(4, fsdp) if count - 1 - i // 4 < step
        ]
        send_up = part(count - step + place)
        send_down = part(place + step - count)
        if up is not None:
            send_up = add_low(send_up, up)
            send_down = add_low(send_down, down)
        up = lax.ppermute(send_up, "fsdp", pairs_up)
        down = lax.ppermute(send_down, "fsdp", pairs_down)
    return part(place).astype(full) + up.astype(full) + down.astype(full)


def sum_quarters(quarters, place):
    half = quarters[0, 0][0].shape[-1] // 2
    one, two = {}, {}
    for at in ((1, 1), (0, 1), (1, 0), (0, 0)):
        keep, send = quarters[at]
        other = swap_core(send)
        one[at] = add_low(keep[..., :half], other[..., :half])
        two[at] = add_low(keep[..., half:], other[..., half:])
    one_side = add_low(one[1, 0], swap_ctx(one[1, 1]))
    two_ctx = add_low(two[0, 1], swap_side(two[1, 1]))
    one_ctx = swap_ctx(one[0, 1])
    two_side = swap_side(two[1, 0])
    one_mine = add_low(add_low(one[0, 0], one_ctx), swap_side(one_side))
    two_mine = add_low(add_low(two[0, 0], two_side), swap_ctx(two_ctx))
    sums = [line_sum(item, place, relative=True) for item in (two_mine, one_mine)]
    return jnp.concatenate([sums[1], sums[0]], axis=-1)


def gather_line(values):
    fsdp = lax.axis_size("fsdp")
    count = fsdp // 4
    ups, downs = [values], [values]
    for _ in range(count - 1):
        ups.append(lax.ppermute(ups[-1], "fsdp", [(i, i + 4) for i in range(fsdp - 4)]))
        downs.append(lax.ppermute(downs[-1], "fsdp", [(i, i - 4) for i in range(4, fsdp)]))
    return jnp.stack([values] + [ups[s] + downs[count - s] for s in range(1, count)])


def gather_quarters(values):
    got = {(0, 0, 0): gather_line(values)}
    got[1, 0, 0] = swap_side(got[0, 0, 0])
    for side in range(2):
        got[side, 1, 0] = swap_ctx(got[side, 0, 0])
    for side in range(2):
        for ctx in range(2):
            got[side, ctx, 1] = swap_core(got[side, ctx, 0])
    return got


def sum_fsdp(values, place, side, core):
    fsdp = lax.axis_size("fsdp")
    rows, width = values.shape[0] // fsdp, values.shape[1]
    parts = values.reshape(fsdp // 2, 2, rows, width).swapaxes(0, 1)
    mine = halve(parts, core, swap_core).reshape(fsdp // 4, 2, rows, width)
    half = width // 2
    one, two = mine[..., :half], mine[..., half:]
    one = line_sum(halve(one.swapaxes(0, 1), side, swap_side), place)
    two = line_sum(two, place).astype(low)
    two = take(two, side).astype(full) + swap_side(take(two, 1 - side)).astype(full)
    return jnp.concatenate([one, two], axis=-1)


def sum_all(values, fsdp):
    values = values + lax.ppermute(values, "fsdp", core_pairs(fsdp))
    values = values + swap_ctx(values)
    step = 2
    while step < fsdp:
        values = values + lax.ppermute(values, "fsdp", [(i, i ^ step) for i in range(fsdp)])
        step *= 2
    return values


def turn(values):
    return pltpu.roll(values, values.shape[-1] // 2, 1)


def norm_rope(raw, gain, cosine, sine):
    scale = lax.rsqrt(jnp.mean(raw * raw, axis=-1, keepdims=True) + eps_norm)
    scaled = raw * scale * gain
    return scaled * cosine + turn(scaled) * sine


def norm_rope_back(raw, gain, cosine, sine, grad):
    scale = lax.rsqrt(jnp.mean(raw * raw, axis=-1, keepdims=True) + eps_norm)
    unit = raw * scale
    grad_scaled = grad * cosine - turn(grad) * sine
    grad_gain = jnp.sum(grad_scaled * unit, axis=0, keepdims=True)
    grad_unit = grad_scaled * gain
    grad_raw = scale * (grad_unit - unit * jnp.mean(grad_unit * unit, axis=-1, keepdims=True))
    return grad_raw, grad_gain


def tiles_of(rows):
    step = rows // 2
    return [(start, start + step) for start in range(0, rows, step)]


def allowed(start, stop):
    shape = (stop - start, stop)
    return lax.broadcasted_iota(jnp.int32, shape, 1) <= (
        lax.broadcasted_iota(jnp.int32, shape, 0) + start
    )


def attend_kernel(q_ref, k_ref, v_ref, cos_ref, sin_ref, qg_ref, kg_ref, o_ref, qr_ref, kr_ref, vl_ref):
    head_dim = k_ref.shape[1]
    rows = k_ref.shape[0]
    cosine, sine = cos_ref[...], sin_ref[...]
    keys = norm_rope(k_ref[...], kg_ref[...], cosine, sine).astype(low)
    values = v_ref[...].astype(low)
    kr_ref[...] = keys
    vl_ref[...] = values
    for head in range(q_ref.shape[1] // head_dim):
        cols = slice(head * head_dim, (head + 1) * head_dim)
        query = norm_rope(q_ref[:, cols], qg_ref[...], cosine, sine).astype(low)
        qr_ref[:, cols] = query
        for start, stop in tiles_of(rows):
            scores = mul(query[start:stop], keys[:stop], rhs_turned) * (1.0 / math.sqrt(head_dim))
            expo = jnp.where(allowed(start, stop), jnp.exp(scores), 0.0)
            probs = (expo / jnp.sum(expo, axis=-1, keepdims=True)).astype(low)
            o_ref[start:stop, cols] = mul(probs, values[:stop]).astype(low)


def attend_grad_kernel(
    q_ref, k_ref, qr_ref, kr_ref, vl_ref, go_ref, cos_ref, sin_ref, qg_ref, kg_ref,
    dq_ref, dk_ref, dv_ref, dqg_ref, dkg_ref, dk_sum, dv_sum, dq_sum,
):
    head_dim = k_ref.shape[1]
    rows = k_ref.shape[0]
    root = 1.0 / math.sqrt(head_dim)
    cosine, sine = cos_ref[...], sin_ref[...]
    keys, values = kr_ref[...], vl_ref[...]
    gain_sum = jnp.zeros((1, head_dim), full)
    dk_sum[...] = jnp.zeros_like(dk_sum)
    dv_sum[...] = jnp.zeros_like(dv_sum)
    for head in range(q_ref.shape[1] // head_dim):
        cols = slice(head * head_dim, (head + 1) * head_dim)
        for start, stop in tiles_of(rows):
            query = qr_ref[start:stop, cols]
            grad = go_ref[start:stop, cols]
            scores = mul(query, keys[:stop], rhs_turned) * root
            expo = jnp.where(allowed(start, stop), jnp.exp(scores), 0.0)
            probs = expo / jnp.sum(expo, axis=-1, keepdims=True)
            grad_probs = mul(grad, values[:stop], rhs_turned)
            delta = jnp.sum(grad_probs * probs, axis=-1, keepdims=True)
            grad_scores = (probs * (grad_probs - delta)).astype(low)
            dv_sum[:stop] += mul(probs.astype(low), grad, lhs_turned)
            dk_sum[:stop] += mul(grad_scores, query, lhs_turned)
            dq_sum[start:stop] = mul(grad_scores, keys[:stop])
        grad_query = (dq_sum[...] * root).astype(low).astype(full)
        grad_raw, grad_gain = norm_rope_back(q_ref[:, cols], qg_ref[...], cosine, sine, grad_query)
        dq_ref[:, cols] = grad_raw.astype(low)
        gain_sum = gain_sum + grad_gain
    dqg_ref[0] = gain_sum
    grad_key = (dk_sum[...] * root).astype(low).astype(full)
    grad_raw, grad_gain = norm_rope_back(k_ref[...], kg_ref[...], cosine, sine, grad_key)
    dk_ref[...] = grad_raw.astype(low)
    dkg_ref[0] = grad_gain
    dv_ref[...] = dv_sum[...].astype(low)


def attention_specs(rows, head_dim, kv_heads, group):
    wide, narrow = group * head_dim, head_dim
    heads_end = kv_heads * group
    return dict(
        q=pl.BlockSpec((rows, wide), lambda i: (0, i)),
        k=pl.BlockSpec((rows, narrow), lambda i: (0, heads_end + i)),
        v=pl.BlockSpec((rows, narrow), lambda i: (0, heads_end + kv_heads + i)),
        own=pl.BlockSpec((rows, narrow), lambda i: (0, i)),
        table=pl.BlockSpec((rows, head_dim), lambda i: (0, 0)),
        gain=pl.BlockSpec((1, head_dim), lambda i: (0, 0)),
        gain_out=pl.BlockSpec((1, 1, head_dim), lambda i: (i, 0, 0)),
    )


def attend(projected, cosine, sine, query_gain, key_gain, kv_heads, group):
    rows, head_dim = cosine.shape
    s = attention_specs(rows, head_dim, kv_heads, group)
    shape = jax.ShapeDtypeStruct
    work = rows * rows * head_dim * kv_heads * group
    return pl.pallas_call(
        attend_kernel,
        grid=(kv_heads,),
        in_specs=[s["q"], s["k"], s["v"], s["table"], s["table"], s["gain"], s["gain"]],
        out_specs=[s["q"], s["q"], s["own"], s["own"]],
        out_shape=[
            shape((rows, kv_heads * group * head_dim), low),
            shape((rows, kv_heads * group * head_dim), low),
            shape((rows, kv_heads * head_dim), low),
            shape((rows, kv_heads * head_dim), low),
        ],
        compiler_params=pltpu.CompilerParams(vmem_limit_bytes=48 << 20),
        cost_estimate=pl.CostEstimate(
            flops=4 * work, bytes_accessed=projected.size * 6, transcendentals=work // head_dim
        ),
        name="attend",
    )(projected, projected, projected, cosine, sine, query_gain, key_gain)


def attend_grad(projected, roped_q, roped_k, values_low, grad, cosine, sine, query_gain, key_gain, kv_heads, group):
    rows, head_dim = cosine.shape
    s = attention_specs(rows, head_dim, kv_heads, group)
    shape = jax.ShapeDtypeStruct
    work = rows * rows * head_dim * kv_heads * group
    return pl.pallas_call(
        attend_grad_kernel,
        grid=(kv_heads,),
        in_specs=[
            s["q"], s["k"], s["q"], s["own"], s["own"], s["q"],
            s["table"], s["table"], s["gain"], s["gain"],
        ],
        out_specs=[s["q"], s["own"], s["own"], s["gain_out"], s["gain_out"]],
        out_shape=[
            shape((rows, kv_heads * group * head_dim), low),
            shape((rows, kv_heads * head_dim), low),
            shape((rows, kv_heads * head_dim), low),
            shape((kv_heads, 1, head_dim), full),
            shape((kv_heads, 1, head_dim), full),
        ],
        scratch_shapes=[pltpu.VMEM((rows, head_dim), full)] * 3,
        compiler_params=pltpu.CompilerParams(vmem_limit_bytes=48 << 20),
        cost_estimate=pl.CostEstimate(
            flops=10 * work, bytes_accessed=projected.size * 10, transcendentals=work // head_dim
        ),
        name="attend_grad",
    )(projected, projected, roped_q, roped_k, values_low, grad, cosine, sine, query_gain, key_gain)


def expert_kernel(core_ref, order, m_ref, g_keep, g_send, w_ref, gu_ref, dn_ref, *refs):
    (keep_out, send_out, keep_back, send_back, gate_back, rows_ref, dy_ref, z_ref, pair_ref) = refs[-9:]
    core = core_ref[0]
    block = m_ref.shape[3]
    hidden = dn_ref.shape[0]
    slots = z_ref.shape[0] // 2
    shape = (block, block)
    earlier = (
        lax.broadcasted_iota(jnp.int32, shape, 0) < lax.broadcasted_iota(jnp.int32, shape, 1)
    ).astype(low)
    slot_ids = lax.broadcasted_iota(jnp.int32, (slots, block), 0)
    places, picks, weights, rows, grads = [], [], [], [], []
    for part, g_ref in enumerate((g_keep, g_send)):
        at = lax.rem(core + part, 2)
        gate = w_ref[0, at, 0]
        hit = jnp.where(gate >= 0.0, 1.0, 0.0)
        ones = jnp.broadcast_to(hit, (8, block)).astype(low)
        count = mul(ones, earlier)[:1].astype(jnp.int32)
        place = (slot_ids == count) & (hit > 0.5)
        pick = place.astype(full).astype(low)
        places.append(place)
        picks.append(pick)
        weights.append(jnp.sum(jnp.where(place, gate, 0.0), axis=1, keepdims=True))
        rows.append(mul(pick, m_ref[0, at, 0]).astype(low))
        grads.append(mul(pick, g_ref[0]))
    row, grad, weight = (jnp.concatenate(items, axis=0) for items in (rows, grads, weights))
    rows_ref[...] = row
    paired = mul(row, gu_ref[...])
    gate_in, up = paired[:, :hidden], paired[:, hidden:]
    sig = jax.nn.sigmoid(gate_in)
    act = gate_in * sig
    z = (act * up).astype(low)
    z_ref[...] = z
    y = mul(z, dn_ref[...]).astype(low).astype(full)
    grad_gate = jnp.sum(grad * y, axis=1, keepdims=True)
    y_scaled = (weight * y).astype(low)
    dy = (weight * grad).astype(low)
    dy_ref[...] = dy
    for part, out in enumerate((keep_out, send_out)):
        mine = slice(part * slots, (part + 1) * slots)
        out[0] = mul(picks[part], y_scaled[mine], lhs_turned).astype(low)
        gate_back[0, lax.rem(core + part, 2), 0] = jnp.sum(
            jnp.where(places[part], grad_gate[mine], 0.0), axis=0, keepdims=True
        )
    dz = mul(dy, dn_ref[...], rhs_turned)
    grad_in = dz * up * (sig * (1.0 + gate_in * (1.0 - sig)))
    pair = jnp.concatenate([grad_in, dz * act], axis=1).astype(low)
    pair_ref[...] = pair
    back = mul(pair, gu_ref[...], rhs_turned).astype(low)
    for part, out in enumerate((keep_back, send_back)):
        mine = slice(part * slots, (part + 1) * slots)
        out[0] = mul(picks[part], back[mine], lhs_turned).astype(low)


def run_expert(core, order, number, parts, m_all, g_keep, g_send, gates_all, gate_up, down, slots, kept):
    places, _, _, block, width = m_all.shape
    paired = gate_up.shape[1]
    steps = g_keep.shape[0]
    part_rows = steps * 2 * slots
    hidden = paired // 2
    shape = jax.ShapeDtypeStruct

    def token_at(i, core, order):
        return (order[2 * i], 0, order[2 * i + 1], 0, 0)

    def fixed(i, core, order):
        return (0, 0)

    def flat(i, core, order):
        return (number * steps + i, 0)

    def stacked(i, core, order):
        return (i, 0, 0)

    small = pl.BlockSpec((1, 2, 1, 1, block), token_at)
    one_block = pl.BlockSpec((1, block, width), stacked)
    widths = (width, width, hidden, paired)
    grid_spec = pltpu.PrefetchScalarGridSpec(
        num_scalar_prefetch=2,
        grid=(steps,),
        in_specs=[
            pl.BlockSpec((1, 2, 1, block, width), token_at), one_block, one_block, small,
            pl.BlockSpec(gate_up.shape, fixed, pipeline_mode=pl.Buffered(1)),
            pl.BlockSpec(down.shape, fixed, pipeline_mode=pl.Buffered(1)),
        ]
        + [pl.BlockSpec(memory_space=pl.ANY)] * (0 if kept is None else 5),
        out_specs=[one_block] * 4 + [small] + [pl.BlockSpec((2 * slots, n), flat) for n in widths],
    )
    return pl.pallas_call(
        expert_kernel,
        grid_spec=grid_spec,
        out_shape=[shape((steps, block, width), low)] * 4
        + [shape((places, 2, 2, 1, block), full)]
        + [shape((parts * part_rows, n), low) for n in widths],
        input_output_aliases={} if kept is None else {8 + i: 4 + i for i in range(5)},
        compiler_params=pltpu.CompilerParams(vmem_limit_bytes=vmem_bytes),
        cost_estimate=pl.CostEstimate(
            flops=part_rows * width * (4 * paired + 4 * hidden + 8 * block),
            bytes_accessed=steps * block * width * 16 + part_rows * (width * 4 + paired * 3),
            transcendentals=part_rows * hidden,
        ),
        name="experts",
    )(core, order, m_all, g_keep, g_send, gates_all, gate_up, down, *(() if kept is None else kept))


def rms_back(values, gain, grad):
    scale = lax.rsqrt(jnp.mean(values * values, axis=-1, keepdims=True) + eps_norm)
    unit = values * scale
    grad_gain = jnp.sum(grad * unit, axis=0)
    grad_unit = grad * gain
    back = scale * (grad_unit - unit * jnp.mean(grad_unit * unit, axis=-1, keepdims=True))
    return back, grad_gain


def in_order(first, second):
    half = first.shape[0] // 2
    return jnp.concatenate([first[:half], second, first[half:]], axis=0)


def of_block(values, rank):
    quarter = values.shape[0] // 4
    outer = jnp.concatenate([values[:quarter], values[3 * quarter :]], axis=0)
    return jnp.where(rank == 0, outer, values[quarter : 3 * quarter])


def body_gathered(
    tokens, qkv_weight, out_weight, router_weight, attn_gain, moe_gain, query_gain, key_gain,
    expert_gate_up, expert_down, routes, cotangent,
):
    rows_dev, width = tokens.shape
    head_dim = query_gain.shape[0]
    top_k = routes.shape[1]
    fsdp = lax.axis_size("fsdp")
    spot = lax.axis_index("fsdp")
    rank = lax.axis_index("ctx")
    place, side, core = spot // 4, (spot // 2) % 2, spot % 2
    shard = qkv_weight.shape[0]
    heads = out_weight.shape[0] * fsdp // head_dim
    kv_heads = (qkv_weight.shape[1] // head_dim - heads) // 2
    group = heads // kv_heads // 2
    my_heads = heads // 2
    width_q, width_k = my_heads * head_dim, kv_heads * head_dim
    experts_all = router_weight.shape[1]
    capacity = 2 * rows_dev * top_k // experts_all
    both = ("fsdp", "ctx")

    def sequence(values):
        other = swap_ctx(values)
        first = jnp.where(rank == 0, values, other)
        second = jnp.where(rank == 0, other, values)
        return in_order(first, second)

    by_parity = qkv_weight[:, : 2 * width_q].reshape(shard, my_heads, 2, head_dim)
    q_local = jnp.where(rank == 0, by_parity[:, :, 0], by_parity[:, :, 1]).reshape(shard, width_q)
    out_local = lax.dynamic_slice_in_dim(out_weight, rank * head_dim, head_dim, 0)
    weights_local = jnp.concatenate([q_local, qkv_weight[:, 2 * width_q :], out_local], axis=1)
    small_local = jnp.concatenate([router_weight, attn_gain[:, None], moe_gain[:, None]], axis=1)
    small_all = lax.all_gather(small_local, "fsdp", axis=0, tiled=True)
    weights_all = lax.all_gather(weights_local, "fsdp", axis=0, tiled=True)
    qkv_all = weights_all[:, : width_q + 2 * width_k]
    out_all = weights_all[:, width_q + 2 * width_k :]
    router_all = small_all[:, :experts_all]
    attn_all = small_all[:, experts_all].astype(full)
    moe_all = small_all[:, experts_all + 1].astype(full)
    g_parts = gather_quarters(cotangent)

    sequence_in = sequence(tokens).astype(full)
    low_in = rms_scale(sequence_in, attn_all).astype(low)
    projected = mul(low_in, qkv_all)
    cosine, sine = (t[:, 0] for t in angles(jnp.arange(2 * rows_dev, dtype=jnp.int32), head_dim))
    sine = jnp.concatenate([-sine[:, : head_dim // 2], sine[:, head_dim // 2 :]], axis=1)
    gain_q, gain_k = query_gain.astype(full)[None], key_gain.astype(full)[None]
    attended, roped_q, roped_k, values_low = attend(
        projected, cosine, sine, gain_q, gain_k, kv_heads, group
    )
    branch = mul(attended, out_all)
    inputs = tokens.astype(full)
    mixed = (
        inputs
        + of_block(branch, rank)
        + swap_ctx(of_block(branch, 1 - rank).astype(low)).astype(full)
    )
    low_mid = rms_scale(mixed, moe_all).astype(low)
    m_all = lax.all_gather(low_mid, both, axis=0)

    logits = mul(low_mid, router_all)
    named = routes[:, :, None] == jnp.arange(experts_all, dtype=jnp.int32)[None, None, :]
    selected = jnp.sum(jnp.where(named, logits[:, None, :], 0.0), axis=2)
    gates = gating(selected)
    chosen = jnp.any(named, axis=1)
    gates_wide = jnp.sum(jnp.where(named, gates[:, :, None], 0.0), axis=1)
    gates_sent = jnp.where(chosen, gates_wide, -1.0).T
    gates_all = lax.all_to_all(gates_sent, both, split_axis=0, concat_axis=0, tiled=True)

    lines = fsdp // 4
    grid_of = (fsdp // 2, 2, 2)
    lines_at = (place - jnp.arange(lines, dtype=jnp.int32)) % lines
    kept, summed_back, summed_out = None, {}, {}
    for number, (d_side, d_ctx) in enumerate(((1, 1), (0, 1), (1, 0), (0, 0))):
        order = jnp.stack(
            [lines_at * 2 + (side + d_side) % 2, jnp.broadcast_to((rank + d_ctx) % 2, (lines,))], axis=1
        ).reshape(-1)
        keep_out, send_out, keep_back, send_back, *kept = run_expert(
            core[None].astype(jnp.int32),
            order.astype(jnp.int32),
            number,
            4,
            m_all.reshape(*grid_of, rows_dev, width),
            g_parts[d_side, d_ctx, 0],
            g_parts[d_side, d_ctx, 1],
            gates_all.reshape(*grid_of, 1, rows_dev),
            expert_gate_up[0],
            expert_down[0],
            capacity,
            kept,
        )
        summed_back[d_side, d_ctx] = (keep_back, send_back)
        summed_out[d_side, d_ctx] = (keep_out, send_out)
    gate_back, rows, grad_rows, hidden, grad_pair = kept
    grad_gates = lax.all_to_all(
        gate_back.reshape(fsdp * 2, rows_dev), both, split_axis=0, concat_axis=0, tiled=True
    ).T
    grad_mid = sum_quarters(summed_back, place)
    grad_down = mul(hidden, grad_rows, lhs_turned)[None]
    grad_gate_up = mul(rows, grad_pair, lhs_turned)[None]
    summed_out, grad_mid = lax.optimization_barrier((summed_out, grad_mid))
    output = (mixed + sum_quarters(summed_out, place)).astype(low)

    grad_wide = jnp.where(chosen, grad_gates, 0.0)
    grad_logits = (
        gates_wide * (grad_wide - jnp.sum(gates_wide * grad_wide, axis=1, keepdims=True))
    ).astype(low)
    grad_router = mul(low_mid, grad_logits, lhs_turned)
    grad_mid = grad_mid + mul(grad_logits, router_all, rhs_turned)
    grad_mixed_part, grad_moe_gain = rms_back(mixed, moe_all, grad_mid)
    grad_mixed = cotangent.astype(full) + grad_mixed_part

    grad_branch = sequence(grad_mixed.astype(low))
    grad_attended = mul(grad_branch, out_all, rhs_turned).astype(low)
    grad_out_part = mul(attended, grad_branch, lhs_turned).astype(low)
    grad_q, grad_k, grad_v, gain_q_part, gain_k_part = attend_grad(
        projected, roped_q, roped_k, values_low, grad_attended, cosine, sine, gain_q, gain_k, kv_heads, group
    )
    grad_projected = jnp.concatenate([grad_q, grad_k, grad_v], axis=1)
    grad_qkv_part = mul(low_in, grad_projected, lhs_turned).astype(low)
    grad_normed_part = mul(grad_projected, qkv_all, rhs_turned)
    grad_normed = of_block(grad_normed_part, rank) + swap_ctx(
        of_block(grad_normed_part, 1 - rank).astype(low)
    ).astype(full)
    grad_in_part, grad_attn_gain = rms_back(inputs, attn_all, grad_normed)
    grad_tokens = grad_mixed + grad_in_part

    out_mine = sum_fsdp(grad_out_part, place, side, core)
    out_other = swap_ctx(out_mine.astype(low)).astype(full)
    grad_out = jnp.where(
        rank == 0,
        jnp.concatenate([out_mine, out_other], axis=0),
        jnp.concatenate([out_other, out_mine], axis=0),
    )
    qkv_mine = sum_fsdp(grad_qkv_part, place, side, core)
    qkv_other = swap_ctx(qkv_mine.astype(low)).astype(full)
    q_mine = qkv_mine[:, :width_q].reshape(shard, my_heads, 1, head_dim)
    q_other = qkv_other[:, :width_q].reshape(shard, my_heads, 1, head_dim)
    grad_q_all = jnp.where(
        rank == 0,
        jnp.concatenate([q_mine, q_other], axis=2),
        jnp.concatenate([q_other, q_mine], axis=2),
    ).reshape(shard, 2 * width_q)
    grad_qkv = jnp.concatenate(
        [grad_q_all, qkv_mine[:, width_q:] + qkv_other[:, width_q:]], axis=1
    )
    total = sum_all(
        jnp.concatenate(
            [
                grad_router,
                grad_attn_gain[:, None],
                grad_moe_gain[:, None],
            ],
            axis=1,
        ),
        fsdp,
    )
    gains = sum_all(
        jnp.concatenate([jnp.sum(gain_q_part, axis=0), jnp.sum(gain_k_part, axis=0)], axis=0), fsdp
    )
    owned = lax.dynamic_slice_in_dim(total, spot * shard, shard, 0)
    return (
        output,
        grad_tokens,
        grad_qkv,
        grad_out,
        owned[:, :experts_all],
        owned[:, experts_all],
        owned[:, experts_all + 1],
        gains[0],
        gains[1],
        grad_gate_up,
        grad_down,
    )


gathered_bytes = 1 << 26


def choose_body(*args):
    tokens, gate_up = args[0], args[8]
    fsdp, ctx = lax.axis_size("fsdp"), lax.axis_size("ctx")
    fits = tokens.size * tokens.dtype.itemsize * fsdp * ctx <= gathered_bytes
    if fits and fsdp % 4 == 0 and ctx == 2 and gate_up.shape[0] == 1:
        return body_gathered(*args)
    return body_routed(*args)


def solution(mesh):
    in_specs = (
        P(("fsdp", "ctx"), None),
        P("fsdp", None),
        P("fsdp", None),
        P("fsdp", None),
        P("fsdp"),
        P("fsdp"),
        P(),
        P(),
        P(("fsdp", "ctx"), None, None),
        P(("fsdp", "ctx"), None, None),
        P(("fsdp", "ctx"), None),
        P(("fsdp", "ctx"), None),
    )
    out_specs = (
        P(("fsdp", "ctx"), None),
        P(("fsdp", "ctx"), None),
        P("fsdp", None),
        P("fsdp", None),
        P("fsdp", None),
        P("fsdp"),
        P("fsdp"),
        P(),
        P(),
        P(("fsdp", "ctx"), None, None),
        P(("fsdp", "ctx"), None, None),
    )
    return jax.shard_map(choose_body, mesh=mesh, in_specs=in_specs, out_specs=out_specs, check_vma=False)
```

```python
import functools
import math

import jax
import jax.numpy as jnp
from jax import lax
from jax.experimental import pallas as pl
from jax.experimental.pallas import tpu as pltpu
from jax.sharding import PartitionSpec as P

eps_norm = 1e-06
theta_base = 1000000.0


def rms_scale(values, gain):
    return values * lax.rsqrt(jnp.mean(values * values, axis=-1, keepdims=True) + eps_norm) * gain


def rotate(values, cosine, sine):
    half_width = values.shape[-1] // 2
    turned = jnp.concatenate([-values[..., half_width:], values[..., :half_width]], axis=-1)
    return values * cosine + turned * sine


def angles(positions, width):
    freqs = theta_base ** (-(jnp.arange(width // 2, dtype=jnp.float32) * 2.0) / width)
    phase = positions.astype(jnp.float32)[:, None] * freqs[None, :]
    phase = jnp.concatenate([phase, phase], axis=-1)
    return (jnp.cos(phase)[:, None, :], jnp.sin(phase)[:, None, :])


def device_positions(block_rank, ctx_count, tok_rows):
    half_rows = tok_rows // 2
    within = jnp.arange(tok_rows, dtype=jnp.int32)
    span_id = jnp.where(within < half_rows, block_rank, 2 * ctx_count - 1 - block_rank)
    return span_id * half_rows + within % half_rows


def attend_head(query, keys_in, values_in, causal, scale_root):
    scores = (
        jnp.einsum("tgd,sd->gts", query, keys_in, preferred_element_type=jnp.float32) / scale_root
    )
    expo = jnp.where(causal[None], jnp.exp(scores), 0.0)
    totals = jnp.sum(expo, axis=-1, keepdims=True)
    probs = (expo / totals).astype(jnp.bfloat16)
    attended = jnp.einsum("gts,sd->tgd", probs, values_in, preferred_element_type=jnp.float32)
    return (attended, jnp.log(totals[..., 0]))


def attend_back(query, keys_in, values_in, causal, log_total, grad_attended, scale_root):
    scores = (
        jnp.einsum("tgd,sd->gts", query, keys_in, preferred_element_type=jnp.float32) / scale_root
    )
    probs = jnp.where(causal[None], jnp.exp(scores - log_total[..., None]), 0.0)
    low_probs = probs.astype(jnp.bfloat16)
    grad_values = jnp.einsum(
        "gts,tgd->sd", low_probs, grad_attended, preferred_element_type=jnp.float32
    )
    grad_probs = jnp.einsum(
        "tgd,sd->gts", grad_attended, values_in, preferred_element_type=jnp.float32
    )
    delta_rows = jnp.sum(grad_probs * probs, axis=-1, keepdims=True)
    grad_scores = (probs * (grad_probs - delta_rows)).astype(jnp.bfloat16)
    grad_query = (
        jnp.einsum("gts,sd->tgd", grad_scores, keys_in, preferred_element_type=jnp.float32)
        / scale_root
    )
    grad_keys = (
        jnp.einsum("gts,tgd->sd", grad_scores, query, preferred_element_type=jnp.float32)
        / scale_root
    )
    return (grad_query, grad_keys, grad_values)


def swiglu(paired):
    half_width = paired.shape[-1] // 2
    return jax.nn.silu(paired[..., :half_width]) * paired[..., half_width:]


def gating(selected):
    expo = jnp.exp(selected)
    return expo / jnp.sum(expo, axis=1, keepdims=True)


def body_routed(
    tokens,
    qkv_weight,
    out_weight,
    router_weight,
    attn_gain,
    moe_gain,
    query_gain,
    key_gain,
    expert_gate_up,
    expert_down,
    routes,
    cotangent,
):
    rows_dev, width = tokens.shape
    head_dim = query_gain.shape[0]
    top_k = routes.shape[1]
    ctx_count = lax.axis_size("ctx")
    ctx_rank = lax.axis_index("ctx")
    qkv_all, out_all, router_all, attn_all, moe_all = (
        lax.all_gather(qkv_weight, "fsdp", axis=0, tiled=True),
        lax.all_gather(out_weight, "fsdp", axis=0, tiled=True),
        lax.all_gather(router_weight, "fsdp", axis=0, tiled=True),
        lax.all_gather(attn_gain, "fsdp", axis=0, tiled=True),
        lax.all_gather(moe_gain, "fsdp", axis=0, tiled=True),
    )
    experts_all = router_all.shape[1]
    heads = out_all.shape[0] // head_dim
    kv_heads = (qkv_all.shape[1] // head_dim - heads) // 2
    group_size = heads // kv_heads
    capacity = 2 * rows_dev * top_k // experts_all
    width_q = heads * head_dim
    width_k = kv_heads * head_dim
    scale_root = math.sqrt(head_dim)
    inputs = tokens.astype(jnp.float32)
    normed_in = rms_scale(inputs, attn_all.astype(jnp.float32))
    low_in = normed_in.astype(jnp.bfloat16)
    projected = jnp.dot(low_in, qkv_all, preferred_element_type=jnp.float32)
    query_raw = projected[:, :width_q].reshape(rows_dev, heads, head_dim)
    key_raw = projected[:, width_q : width_q + width_k].reshape(rows_dev, kv_heads, head_dim)
    value_low = (
        projected[:, width_q + width_k :].astype(jnp.bfloat16).reshape(rows_dev, kv_heads, head_dim)
    )
    positions = device_positions(ctx_rank, ctx_count, rows_dev)
    cosine, sine = angles(positions, head_dim)
    query_gain_f = query_gain.astype(jnp.float32)
    key_gain_f = key_gain.astype(jnp.float32)

    def query_rope(values_in, gain):
        return rotate(rms_scale(values_in, gain), cosine, sine)

    query_low = query_rope(query_raw, query_gain_f).astype(jnp.bfloat16)
    key_low = query_rope(key_raw, key_gain_f).astype(jnp.bfloat16)
    keys_all, values_all = (
        lax.all_gather(key_low, "ctx", axis=0, tiled=True),
        lax.all_gather(value_low, "ctx", axis=0, tiled=True),
    )
    key_pos = jnp.concatenate(
        [device_positions(other, ctx_count, rows_dev) for other in range(ctx_count)]
    )
    causal = key_pos[None, :] <= positions[:, None]
    query_heads = query_low.reshape(rows_dev, kv_heads, group_size, head_dim).transpose(1, 0, 2, 3)
    key_heads = keys_all.transpose(1, 0, 2)
    value_heads = values_all.transpose(1, 0, 2)
    attended, log_total = lax.map(
        lambda member: attend_head(member[0], member[1], member[2], causal, scale_root),
        (query_heads, key_heads, value_heads),
    )
    attended_low = attended.transpose(1, 0, 2, 3).reshape(rows_dev, width_q).astype(jnp.bfloat16)
    mixed = inputs + jnp.dot(attended_low, out_all, preferred_element_type=jnp.float32)
    normed_mid = rms_scale(mixed, moe_all.astype(jnp.float32))
    low_mid = normed_mid.astype(jnp.bfloat16)
    logits = jnp.dot(low_mid, router_all, preferred_element_type=jnp.float32)
    selected = jnp.take_along_axis(logits, routes, axis=1)
    gates, gate_back = jax.vjp(gating, selected)
    flat_routes = routes.reshape(-1)
    expert_ids = jnp.arange(experts_all, dtype=jnp.int32)
    hit_table = (flat_routes[:, None] == expert_ids[None, :]).astype(jnp.int32)
    slot_index = jnp.sum(jnp.cumsum(hit_table, axis=0) * hit_table, axis=1) - 1
    target = flat_routes * capacity + slot_index
    pair_count = rows_dev * top_k
    source_pair = (
        jnp.full((experts_all * capacity,), pair_count, jnp.int32)
        .at[target]
        .set(jnp.arange(pair_count, dtype=jnp.int32))
    )
    padded = jnp.concatenate([low_mid, jnp.zeros((1, width), jnp.bfloat16)], axis=0)
    outgoing = padded[source_pair // top_k].reshape(experts_all, capacity, width)
    received = lax.all_to_all(outgoing, ("fsdp", "ctx"), split_axis=0, concat_axis=1, tiled=True)
    gate_and_up = jnp.einsum(
        "esd,edf->esf", received, expert_gate_up, preferred_element_type=jnp.float32
    )
    hidden_val, swiglu_back = jax.vjp(swiglu, gate_and_up)
    hidden_low = hidden_val.astype(jnp.bfloat16)
    result_low = jnp.einsum(
        "esf,efd->esd", hidden_low, expert_down, preferred_element_type=jnp.float32
    ).astype(jnp.bfloat16)
    returned = lax.all_to_all(
        result_low, ("fsdp", "ctx"), split_axis=1, concat_axis=0, tiled=True
    ).reshape(experts_all * capacity, width)
    picked = returned[target].reshape(rows_dev, top_k, width).astype(jnp.float32)
    output = (mixed + jnp.sum(gates[:, :, None] * picked, axis=1)).astype(jnp.bfloat16)
    qkv_back, out_back, router_back, attn_back_g, moe_back_g = (
        qkv_all,
        out_all,
        router_all,
        attn_all,
        moe_all,
    )
    grad_final = cotangent.astype(jnp.float32)
    grad_gates = jnp.sum(grad_final[:, None, :] * picked, axis=2)
    grad_result = (
        (gates[:, :, None] * grad_final[:, None, :]).astype(jnp.bfloat16).reshape(pair_count, width)
    )
    grad_padded = jnp.concatenate([grad_result, jnp.zeros((1, width), jnp.bfloat16)], axis=0)
    grad_outgoing = grad_padded[source_pair].reshape(experts_all, capacity, width)
    grad_received = lax.all_to_all(
        grad_outgoing, ("fsdp", "ctx"), split_axis=0, concat_axis=1, tiled=True
    )
    grad_down = jnp.einsum(
        "esf,esd->efd", hidden_low, grad_received, preferred_element_type=jnp.float32
    )
    grad_hidden = jnp.einsum(
        "esd,efd->esf", grad_received, expert_down, preferred_element_type=jnp.float32
    )
    grad_paired = swiglu_back(grad_hidden)[0].astype(jnp.bfloat16)
    grad_gate_up = jnp.einsum(
        "esd,esf->edf", received, grad_paired, preferred_element_type=jnp.float32
    )
    grad_rows = jnp.einsum(
        "esf,edf->esd", grad_paired, expert_gate_up, preferred_element_type=jnp.float32
    ).astype(jnp.bfloat16)
    grad_returned = lax.all_to_all(
        grad_rows, ("fsdp", "ctx"), split_axis=1, concat_axis=0, tiled=True
    ).reshape(experts_all * capacity, width)
    grad_mid = jnp.sum(
        grad_returned[target].reshape(rows_dev, top_k, width).astype(jnp.float32), axis=1
    )
    grad_selected = gate_back(grad_gates)[0]
    route_table = (routes[:, :, None] == expert_ids[None, None, :]).astype(jnp.float32)
    grad_logits = jnp.sum(route_table * grad_selected[:, :, None], axis=1).astype(jnp.bfloat16)
    grad_router = jnp.dot(low_mid.T, grad_logits, preferred_element_type=jnp.float32)
    grad_mid = grad_mid + jnp.dot(grad_logits, router_back.T, preferred_element_type=jnp.float32)
    unused_mid, mid_back = jax.vjp(rms_scale, mixed, moe_back_g.astype(jnp.float32))
    grad_mixed_part, grad_moe_gain = mid_back(grad_mid)
    grad_mixed = grad_final + grad_mixed_part
    grad_branch = grad_mixed.astype(jnp.bfloat16)
    grad_out = jnp.dot(attended_low.T, grad_branch, preferred_element_type=jnp.float32)
    grad_attended = jnp.dot(grad_branch, out_back.T, preferred_element_type=jnp.float32).astype(
        jnp.bfloat16
    )
    grad_heads = grad_attended.reshape(rows_dev, kv_heads, group_size, head_dim).transpose(
        1, 0, 2, 3
    )
    grad_query_h, grad_key_h, grad_value_h = lax.map(
        lambda member: attend_back(
            member[0], member[1], member[2], causal, member[3], member[4], scale_root
        ),
        (query_heads, key_heads, value_heads, log_total, grad_heads),
    )
    grad_keys, grad_values = (
        lax.psum_scatter(
            grad_key_h.transpose(1, 0, 2).astype(jnp.bfloat16),
            "ctx",
            scatter_dimension=0,
            tiled=True,
        ).astype(jnp.float32),
        lax.psum_scatter(
            grad_value_h.transpose(1, 0, 2).astype(jnp.bfloat16),
            "ctx",
            scatter_dimension=0,
            tiled=True,
        ).astype(jnp.float32),
    )
    grad_query_rot = (
        grad_query_h.transpose(1, 0, 2, 3).reshape(rows_dev, heads, head_dim).astype(jnp.bfloat16)
    )
    grad_query_rot = lax.optimization_barrier(grad_query_rot).astype(jnp.float32)
    grad_key_rot = lax.optimization_barrier(grad_keys.astype(jnp.bfloat16)).astype(jnp.float32)
    unused_query, query_back = jax.vjp(query_rope, query_raw, query_gain_f)
    grad_query_raw, grad_query_gain = query_back(grad_query_rot)
    unused_key, key_back = jax.vjp(query_rope, key_raw, key_gain_f)
    grad_key_raw, grad_key_gain = key_back(grad_key_rot)
    grad_projected = jnp.concatenate(
        [
            grad_query_raw.reshape(rows_dev, width_q).astype(jnp.bfloat16),
            grad_key_raw.reshape(rows_dev, width_k).astype(jnp.bfloat16),
            grad_values.reshape(rows_dev, width_k).astype(jnp.bfloat16),
        ],
        axis=1,
    )
    grad_qkv = jnp.dot(low_in.T, grad_projected, preferred_element_type=jnp.float32)
    grad_normed = jnp.dot(grad_projected, qkv_back.T, preferred_element_type=jnp.float32)
    unused_in, in_back = jax.vjp(rms_scale, inputs, attn_back_g.astype(jnp.float32))
    grad_in_part, grad_attn_gain = in_back(grad_normed)
    grad_tokens = grad_mixed + grad_in_part
    gradients = (grad_qkv, grad_out, grad_router, grad_attn_gain, grad_moe_gain)
    pieces = (
        lax.psum_scatter(gradients[0], "fsdp", scatter_dimension=0, tiled=True),
        lax.psum_scatter(gradients[1], "fsdp", scatter_dimension=0, tiled=True),
        lax.psum_scatter(gradients[2], "fsdp", scatter_dimension=0, tiled=True),
        lax.psum_scatter(gradients[3], "fsdp", scatter_dimension=0, tiled=True),
        lax.psum_scatter(gradients[4], "fsdp", scatter_dimension=0, tiled=True),
    )
    reduced = (
        lax.psum(pieces[0].astype(jnp.bfloat16), "ctx").astype(jnp.float32),
        lax.psum(pieces[1].astype(jnp.bfloat16), "ctx").astype(jnp.float32),
        lax.psum(pieces[2].astype(jnp.bfloat16), "ctx").astype(jnp.float32),
        lax.psum(pieces[3].astype(jnp.bfloat16), "ctx").astype(jnp.float32),
        lax.psum(pieces[4].astype(jnp.bfloat16), "ctx").astype(jnp.float32),
    )
    gain_sums = lax.psum((grad_query_gain, grad_key_gain), ("fsdp", "ctx"))
    return (
        output,
        grad_tokens,
        reduced[0],
        reduced[1],
        reduced[2],
        reduced[3],
        reduced[4],
        gain_sums[0],
        gain_sums[1],
        grad_gate_up,
        grad_down,
    )


low = jnp.bfloat16
full = jnp.float32
plain = (((1,), (0,)), ((), ()))
rhs_turned = (((1,), (1,)), ((), ()))
lhs_turned = (((0,), (0,)), ((), ()))
vmem_bytes = 58 << 20


def mul(left, right, dims=plain):
    return lax.dot_general(left, right, dims, preferred_element_type=full)


def core_pairs(fsdp):
    return [(i, i ^ 1) for i in range(fsdp)]


def side_pairs(fsdp):
    return [(i, i ^ 2) for i in range(fsdp)]


def swap_core(values):
    return lax.ppermute(values, "fsdp", core_pairs(lax.axis_size("fsdp")))


def swap_side(values):
    return lax.ppermute(values, "fsdp", side_pairs(lax.axis_size("fsdp")))


def swap_ctx(values):
    return lax.ppermute(values, "ctx", [(0, 1), (1, 0)])


def add_low(one, two):
    return (one.astype(full) + two.astype(full)).astype(low)


def hold(values, first):
    return lax.optimization_barrier((values, first))


def take(values, index):
    return lax.dynamic_index_in_dim(values, index, 0, keepdims=False)


def halve(values, index, swap):
    return add_low(take(values, index), swap(take(values, 1 - index)))


def line_sum(values, place, relative=False):
    count = values.shape[0]
    fsdp = lax.axis_size("fsdp")
    up = down = None

    def part(at):
        at = jnp.clip(at, 0, count - 1)
        return take(values, (place - at) % count if relative else at)

    for step in range(1, count):
        pairs_up = [
            (i, i + 4) for i in range(fsdp - 4) if i // 4 < step
        ]
        pairs_down = [
            (i, i - 4) for i in range(4, fsdp) if count - 1 - i // 4 < step
        ]
        send_up = part(count - step + place)
        send_down = part(place + step - count)
        if up is not None:
            send_up = add_low(send_up, up)
            send_down = add_low(send_down, down)
        up = lax.ppermute(send_up, "fsdp", pairs_up)
        down = lax.ppermute(send_down, "fsdp", pairs_down)
    return part(place).astype(full) + up.astype(full) + down.astype(full)


def over_core(keep, send):
    half = keep.shape[-1] // 2
    other = swap_core(send)
    return add_low(keep[..., :half], other[..., :half]), add_low(keep[..., half:], other[..., half:])


def gather_line(values):
    fsdp = lax.axis_size("fsdp")
    count = fsdp // 4
    ups, downs = [values], [values]
    for _ in range(count - 1):
        ups.append(lax.ppermute(ups[-1], "fsdp", [(i, i + 4) for i in range(fsdp - 4)]))
        downs.append(lax.ppermute(downs[-1], "fsdp", [(i, i - 4) for i in range(4, fsdp)]))
    return jnp.stack([values] + [ups[s] + downs[count - s] for s in range(1, count)])


def gather_quarters(values):
    got = {(0, 0, 0): gather_line(values)}
    got[1, 0, 0] = swap_side(got[0, 0, 0])
    for side in range(2):
        got[side, 1, 0] = swap_ctx(got[side, 0, 0])
    for side in range(2):
        for ctx in range(2):
            got[side, ctx, 1] = swap_core(got[side, ctx, 0])
    return got


def sum_fsdp(values, place, side, core):
    fsdp = lax.axis_size("fsdp")
    rows, width = values.shape[0] // fsdp, values.shape[1]
    parts = values.reshape(fsdp // 2, 2, rows, width).swapaxes(0, 1)
    mine = halve(parts, core, swap_core).reshape(fsdp // 4, 2, rows, width)
    half = width // 2
    one, two = mine[..., :half], mine[..., half:]
    one = line_sum(halve(one.swapaxes(0, 1), side, swap_side), place)
    two = line_sum(two, place).astype(low)
    two = take(two, side).astype(full) + swap_side(take(two, 1 - side)).astype(full)
    return jnp.concatenate([one, two], axis=-1)


def sum_all(values, fsdp):
    values = values + lax.ppermute(values, "fsdp", core_pairs(fsdp))
    values = values + swap_ctx(values)
    step = 2
    while step < fsdp:
        values = values + lax.ppermute(values, "fsdp", [(i, i ^ step) for i in range(fsdp)])
        step *= 2
    return values


def sum_owned(values, fsdp, spot):
    items, shard = values.shape[0], values.shape[1] // fsdp
    values = values.reshape(items, fsdp, shard).swapaxes(0, 1)
    step = fsdp // 2
    while step:
        bit = (spot // step) % 2
        values = values.reshape(2, step, items, shard)
        other = lax.ppermute(take(values, 1 - bit), "fsdp", [(i, i ^ step) for i in range(fsdp)])
        values = take(values, bit) + other
        step //= 2
    values = values[0]
    return values + swap_ctx(values)


def turn(values):
    return pltpu.roll(values, values.shape[-1] // 2, 1)


def norm_rope(raw, gain, cosine, sine):
    scale = lax.rsqrt(jnp.mean(raw * raw, axis=-1, keepdims=True) + eps_norm)
    scaled = raw * scale * gain
    return scaled * cosine + turn(scaled) * sine


def norm_rope_back(raw, gain, cosine, sine, grad):
    scale = lax.rsqrt(jnp.mean(raw * raw, axis=-1, keepdims=True) + eps_norm)
    unit = raw * scale
    grad_scaled = grad * cosine - turn(grad) * sine
    grad_gain = jnp.sum(grad_scaled * unit, axis=0, keepdims=True)
    grad_unit = grad_scaled * gain
    grad_raw = scale * (grad_unit - unit * jnp.mean(grad_unit * unit, axis=-1, keepdims=True))
    return grad_raw, grad_gain


def tiles_of(rows):
    step = rows // 2
    return [(start, start + step) for start in range(0, rows, step)]


def allowed(start, stop):
    shape = (stop - start, stop)
    return lax.broadcasted_iota(jnp.int32, shape, 1) <= (
        lax.broadcasted_iota(jnp.int32, shape, 0) + start
    )


def attend_kernel(q_ref, k_ref, v_ref, cos_ref, sin_ref, qg_ref, kg_ref, o_ref, qr_ref, kr_ref, vl_ref):
    head_dim = k_ref.shape[1]
    rows = k_ref.shape[0]
    cosine, sine = cos_ref[...], sin_ref[...]
    keys = norm_rope(k_ref[...], kg_ref[...], cosine, sine).astype(low)
    values = v_ref[...].astype(low)
    kr_ref[...] = keys
    vl_ref[...] = values
    for head in range(q_ref.shape[1] // head_dim):
        cols = slice(head * head_dim, (head + 1) * head_dim)
        query = norm_rope(q_ref[:, cols], qg_ref[...], cosine, sine).astype(low)
        qr_ref[:, cols] = query
        for start, stop in tiles_of(rows):
            scores = mul(query[start:stop], keys[:stop], rhs_turned) * (1.0 / math.sqrt(head_dim))
            expo = jnp.where(allowed(start, stop), jnp.exp(scores), 0.0)
            probs = (expo / jnp.sum(expo, axis=-1, keepdims=True)).astype(low)
            o_ref[start:stop, cols] = mul(probs, values[:stop]).astype(low)


def attend_grad_kernel(
    q_ref, k_ref, qr_ref, kr_ref, vl_ref, go_ref, cos_ref, sin_ref, qg_ref, kg_ref,
    dq_ref, dk_ref, dv_ref, dqg_ref, dkg_ref, dk_sum, dv_sum, dq_sum,
):
    head_dim = k_ref.shape[1]
    rows = k_ref.shape[0]
    root = 1.0 / math.sqrt(head_dim)
    cosine, sine = cos_ref[...], sin_ref[...]
    keys, values = kr_ref[...], vl_ref[...]
    gain_sum = jnp.zeros((1, head_dim), full)
    dk_sum[...] = jnp.zeros_like(dk_sum)
    dv_sum[...] = jnp.zeros_like(dv_sum)
    for head in range(q_ref.shape[1] // head_dim):
        cols = slice(head * head_dim, (head + 1) * head_dim)
        for start, stop in tiles_of(rows):
            query = qr_ref[start:stop, cols]
            grad = go_ref[start:stop, cols]
            scores = mul(query, keys[:stop], rhs_turned) * root
            expo = jnp.where(allowed(start, stop), jnp.exp(scores), 0.0)
            probs = expo / jnp.sum(expo, axis=-1, keepdims=True)
            grad_probs = mul(grad, values[:stop], rhs_turned)
            delta = jnp.sum(grad_probs * probs, axis=-1, keepdims=True)
            grad_scores = (probs * (grad_probs - delta)).astype(low)
            dv_sum[:stop] += mul(probs.astype(low), grad, lhs_turned)
            dk_sum[:stop] += mul(grad_scores, query, lhs_turned)
            dq_sum[start:stop] = mul(grad_scores, keys[:stop])
        grad_query = (dq_sum[...] * root).astype(low).astype(full)
        grad_raw, grad_gain = norm_rope_back(q_ref[:, cols], qg_ref[...], cosine, sine, grad_query)
        dq_ref[:, cols] = grad_raw.astype(low)
        gain_sum = gain_sum + grad_gain
    dqg_ref[0] = gain_sum
    grad_key = (dk_sum[...] * root).astype(low).astype(full)
    grad_raw, grad_gain = norm_rope_back(k_ref[...], kg_ref[...], cosine, sine, grad_key)
    dk_ref[...] = grad_raw.astype(low)
    dkg_ref[0] = grad_gain
    dv_ref[...] = dv_sum[...].astype(low)


def attention_specs(rows, head_dim, kv_heads, group):
    wide, narrow = group * head_dim, head_dim
    heads_end = kv_heads * group
    return dict(
        q=pl.BlockSpec((rows, wide), lambda i: (0, i)),
        k=pl.BlockSpec((rows, narrow), lambda i: (0, heads_end + i)),
        v=pl.BlockSpec((rows, narrow), lambda i: (0, heads_end + kv_heads + i)),
        own=pl.BlockSpec((rows, narrow), lambda i: (0, i)),
        table=pl.BlockSpec((rows, head_dim), lambda i: (0, 0)),
        gain=pl.BlockSpec((1, head_dim), lambda i: (0, 0)),
        gain_out=pl.BlockSpec((1, 1, head_dim), lambda i: (i, 0, 0)),
    )


def attend(projected, cosine, sine, query_gain, key_gain, kv_heads, group):
    rows, head_dim = cosine.shape
    s = attention_specs(rows, head_dim, kv_heads, group)
    shape = jax.ShapeDtypeStruct
    work = rows * rows * head_dim * kv_heads * group
    return pl.pallas_call(
        attend_kernel,
        grid=(kv_heads,),
        in_specs=[s["q"], s["k"], s["v"], s["table"], s["table"], s["gain"], s["gain"]],
        out_specs=[s["q"], s["q"], s["own"], s["own"]],
        out_shape=[
            shape((rows, kv_heads * group * head_dim), low),
            shape((rows, kv_heads * group * head_dim), low),
            shape((rows, kv_heads * head_dim), low),
            shape((rows, kv_heads * head_dim), low),
        ],
        compiler_params=pltpu.CompilerParams(vmem_limit_bytes=48 << 20),
        cost_estimate=pl.CostEstimate(
            flops=4 * work, bytes_accessed=projected.size * 6, transcendentals=work // head_dim
        ),
        name="attend",
    )(projected, projected, projected, cosine, sine, query_gain, key_gain)


def attend_grad(projected, roped_q, roped_k, values_low, grad, cosine, sine, query_gain, key_gain, kv_heads, group):
    rows, head_dim = cosine.shape
    s = attention_specs(rows, head_dim, kv_heads, group)
    shape = jax.ShapeDtypeStruct
    work = rows * rows * head_dim * kv_heads * group
    return pl.pallas_call(
        attend_grad_kernel,
        grid=(kv_heads,),
        in_specs=[
            s["q"], s["k"], s["q"], s["own"], s["own"], s["q"],
            s["table"], s["table"], s["gain"], s["gain"],
        ],
        out_specs=[s["q"], s["own"], s["own"], s["gain_out"], s["gain_out"]],
        out_shape=[
            shape((rows, kv_heads * group * head_dim), low),
            shape((rows, kv_heads * head_dim), low),
            shape((rows, kv_heads * head_dim), low),
            shape((kv_heads, 1, head_dim), full),
            shape((kv_heads, 1, head_dim), full),
        ],
        scratch_shapes=[pltpu.VMEM((rows, head_dim), full)] * 3,
        compiler_params=pltpu.CompilerParams(vmem_limit_bytes=48 << 20),
        cost_estimate=pl.CostEstimate(
            flops=10 * work, bytes_accessed=projected.size * 10, transcendentals=work // head_dim
        ),
        name="attend_grad",
    )(projected, projected, roped_q, roped_k, values_low, grad, cosine, sine, query_gain, key_gain)


def expert_kernel(core_ref, order, m_ref, g_ref, g_keep, g_send, w_ref, gu_ref, dn_ref, *refs):
    (keep_out, send_out, keep_back, send_back, gate_back, rows_ref, dy_ref, z_ref, pair_ref) = refs[-9:]
    core = core_ref[0]
    block = m_ref.shape[3]
    hidden = dn_ref.shape[0]
    slots = z_ref.shape[0] // 2
    shape = (block, block)
    earlier = (
        lax.broadcasted_iota(jnp.int32, shape, 0) < lax.broadcasted_iota(jnp.int32, shape, 1)
    ).astype(low)
    slot_ids = lax.broadcasted_iota(jnp.int32, (slots, block), 0)
    places, picks, weights, rows, grads = [], [], [], [], []
    for part, g_more in enumerate((g_keep, g_send)):
        at = lax.rem(core + part, 2)
        gate = w_ref[0, at, 0]
        hit = jnp.where(gate >= 0.0, 1.0, 0.0)
        ones = jnp.broadcast_to(hit, (8, block)).astype(low)
        count = mul(ones, earlier)[:1].astype(jnp.int32)
        place = (slot_ids == count) & (hit > 0.5)
        pick = place.astype(full).astype(low)
        places.append(place)
        picks.append(pick)
        weights.append(jnp.sum(jnp.where(place, gate, 0.0), axis=1, keepdims=True))
        rows.append(mul(pick, m_ref[0, at, 0]).astype(low))
        grads.append(
            jnp.concatenate([mul(pick, g_ref[0, at, 0]), mul(pick, g_more[0])], axis=1)
        )
    row, grad, weight = (jnp.concatenate(items, axis=0) for items in (rows, grads, weights))
    rows_ref[...] = row
    paired = mul(row, gu_ref[...])
    gate_in, up = paired[:, :hidden], paired[:, hidden:]
    sig = jax.nn.sigmoid(gate_in)
    act = gate_in * sig
    z = (act * up).astype(low)
    z_ref[...] = z
    y = mul(z, dn_ref[...]).astype(low).astype(full)
    grad_gate = jnp.sum(grad * y, axis=1, keepdims=True)
    y_scaled = (weight * y).astype(low)
    dy = (weight * grad).astype(low)
    dy_ref[...] = dy
    for part, out in enumerate((keep_out, send_out)):
        mine = slice(part * slots, (part + 1) * slots)
        out[0] = mul(picks[part], y_scaled[mine], lhs_turned).astype(low)
        gate_back[0, lax.rem(core + part, 2), 0] = jnp.sum(
            jnp.where(places[part], grad_gate[mine], 0.0), axis=0, keepdims=True
        )
    dz = mul(dy, dn_ref[...], rhs_turned)
    grad_in = dz * up * (sig * (1.0 + gate_in * (1.0 - sig)))
    pair = jnp.concatenate([grad_in, dz * act], axis=1).astype(low)
    pair_ref[...] = pair
    back = mul(pair, gu_ref[...], rhs_turned).astype(low)
    for part, out in enumerate((keep_back, send_back)):
        mine = slice(part * slots, (part + 1) * slots)
        out[0] = mul(picks[part], back[mine], lhs_turned).astype(low)


def run_expert(core, order, number, parts, m_all, g_all, g_keep, g_send, gates_all, gate_up, down, slots, kept):
    places, _, _, block, width = m_all.shape
    paired = gate_up.shape[1]
    steps = g_keep.shape[0]
    part_rows = steps * 2 * slots
    hidden = paired // 2
    shape = jax.ShapeDtypeStruct

    def token_at(i, core, order):
        return (order[2 * i], 0, order[2 * i + 1], 0, 0)

    def fixed(i, core, order):
        return (0, 0)

    def flat(i, core, order):
        return (number * steps + i, 0)

    def stacked(i, core, order):
        return (i, 0, 0)

    small = pl.BlockSpec((1, 2, 1, 1, block), token_at)
    one_block = pl.BlockSpec((1, block, width), stacked)
    widths = (width, width, hidden, paired)
    grid_spec = pltpu.PrefetchScalarGridSpec(
        num_scalar_prefetch=2,
        grid=(steps,),
        in_specs=[
            pl.BlockSpec((1, 2, 1, block, width), token_at),
            pl.BlockSpec((1, 2, 1, block, g_all.shape[4]), token_at),
            pl.BlockSpec((1, block, g_keep.shape[2]), stacked),
            pl.BlockSpec((1, block, g_keep.shape[2]), stacked),
            small,
            pl.BlockSpec(gate_up.shape, fixed, pipeline_mode=pl.Buffered(1)),
            pl.BlockSpec(down.shape, fixed, pipeline_mode=pl.Buffered(1)),
        ]
        + [pl.BlockSpec(memory_space=pl.ANY)] * (0 if kept is None else 5),
        out_specs=[one_block] * 4 + [small] + [pl.BlockSpec((2 * slots, n), flat) for n in widths],
    )
    return pl.pallas_call(
        expert_kernel,
        grid_spec=grid_spec,
        out_shape=[shape((steps, block, width), low)] * 4
        + [shape((places, 2, 2, 1, block), full)]
        + [shape((parts * part_rows, n), low) for n in widths],
        input_output_aliases={} if kept is None else {9 + i: 4 + i for i in range(5)},
        compiler_params=pltpu.CompilerParams(vmem_limit_bytes=vmem_bytes),
        cost_estimate=pl.CostEstimate(
            flops=part_rows * width * (4 * paired + 4 * hidden + 8 * block),
            bytes_accessed=steps * block * width * 16 + part_rows * (width * 4 + paired * 3),
            transcendentals=part_rows * hidden,
        ),
        name="experts",
    )(core, order, m_all, g_all, g_keep, g_send, gates_all, gate_up, down, *(() if kept is None else kept))


def rms_back(values, gain, grad):
    scale = lax.rsqrt(jnp.mean(values * values, axis=-1, keepdims=True) + eps_norm)
    unit = values * scale
    grad_gain = jnp.sum(grad * unit, axis=0)
    grad_unit = grad * gain
    back = scale * (grad_unit - unit * jnp.mean(grad_unit * unit, axis=-1, keepdims=True))
    return back, grad_gain


def in_order(first, second):
    half = first.shape[0] // 2
    return jnp.concatenate([first[:half], second, first[half:]], axis=0)


def of_block(values, rank):
    quarter = values.shape[0] // 4
    outer = jnp.concatenate([values[:quarter], values[3 * quarter :]], axis=0)
    return jnp.where(rank == 0, outer, values[quarter : 3 * quarter])


def body_gathered(
    tokens, qkv_weight, out_weight, router_weight, attn_gain, moe_gain, query_gain, key_gain,
    expert_gate_up, expert_down, routes, cotangent,
):
    rows_dev, width = tokens.shape
    head_dim = query_gain.shape[0]
    top_k = routes.shape[1]
    fsdp = lax.axis_size("fsdp")
    spot = lax.axis_index("fsdp")
    rank = lax.axis_index("ctx")
    place, side, core = spot // 4, (spot // 2) % 2, spot % 2
    shard = qkv_weight.shape[0]
    heads = out_weight.shape[0] * fsdp // head_dim
    kv_heads = (qkv_weight.shape[1] // head_dim - heads) // 2
    group = heads // kv_heads // 2
    my_heads = heads // 2
    width_q, width_k = my_heads * head_dim, kv_heads * head_dim
    experts_all = router_weight.shape[1]
    capacity = 2 * rows_dev * top_k // experts_all
    both = ("fsdp", "ctx")

    def sequence(values):
        other = swap_ctx(values)
        first = jnp.where(rank == 0, values, other)
        second = jnp.where(rank == 0, other, values)
        return in_order(first, second)

    by_parity = qkv_weight[:, : 2 * width_q].reshape(shard, my_heads, 2, head_dim)
    q_local = jnp.where(rank == 0, by_parity[:, :, 0], by_parity[:, :, 1]).reshape(shard, width_q)
    out_local = lax.dynamic_slice_in_dim(out_weight, rank * head_dim, head_dim, 0)
    weights_local = jnp.concatenate([q_local, qkv_weight[:, 2 * width_q :], out_local], axis=1)
    small_local = jnp.concatenate([router_weight, attn_gain[:, None], moe_gain[:, None]], axis=1)
    small_all = lax.all_gather(small_local, "fsdp", axis=0, tiled=True)
    weights_all = lax.all_gather(weights_local, "fsdp", axis=0, tiled=True)
    qkv_all = weights_all[:, : width_q + 2 * width_k]
    out_all = weights_all[:, width_q + 2 * width_k :]
    router_all = small_all[:, :experts_all]
    attn_all = small_all[:, experts_all].astype(full)
    moe_all = small_all[:, experts_all + 1].astype(full)
    g_half = width // 2
    g_all = lax.all_gather(cotangent[:, :g_half], both, axis=0)
    g_parts = gather_quarters(cotangent[:, g_half:])

    sequence_in = sequence(tokens).astype(full)
    low_in = rms_scale(sequence_in, attn_all).astype(low)
    projected = mul(low_in, qkv_all)
    cosine, sine = (t[:, 0] for t in angles(jnp.arange(2 * rows_dev, dtype=jnp.int32), head_dim))
    sine = jnp.concatenate([-sine[:, : head_dim // 2], sine[:, head_dim // 2 :]], axis=1)
    gain_q, gain_k = query_gain.astype(full)[None], key_gain.astype(full)[None]
    attended, roped_q, roped_k, values_low = attend(
        projected, cosine, sine, gain_q, gain_k, kv_heads, group
    )
    branch = mul(attended, out_all)
    inputs = tokens.astype(full)
    mixed = (
        inputs
        + of_block(branch, rank)
        + swap_ctx(of_block(branch, 1 - rank).astype(low)).astype(full)
    )
    low_mid = rms_scale(mixed, moe_all).astype(low)
    m_all = lax.all_gather(low_mid, both, axis=0)

    logits = mul(low_mid, router_all)
    named = routes[:, :, None] == jnp.arange(experts_all, dtype=jnp.int32)[None, None, :]
    selected = jnp.sum(jnp.where(named, logits[:, None, :], 0.0), axis=2)
    gates = gating(selected)
    chosen = jnp.any(named, axis=1)
    gates_wide = jnp.sum(jnp.where(named, gates[:, :, None], 0.0), axis=1)
    gates_sent = jnp.where(chosen, gates_wide, -1.0).T
    gates_all = lax.all_to_all(gates_sent, both, split_axis=0, concat_axis=0, tiled=True)

    lines = fsdp // 4
    grid_of = (fsdp // 2, 2, 2)
    lines_at = (place - jnp.arange(lines, dtype=jnp.int32)) % lines
    kept, back, out, wait = None, {}, {}, None
    core_at = core[None].astype(jnp.int32)
    for number, at in enumerate(((1, 1), (0, 1), (1, 0), (0, 0))):
        d_side, d_ctx = at
        order = jnp.stack(
            [lines_at * 2 + (side + d_side) % 2, jnp.broadcast_to((rank + d_ctx) % 2, (lines,))], axis=1
        ).reshape(-1)
        if number == 2:
            core_at, back[1, 1] = hold(core_at, back[1, 1])
        if number == 3:
            far_ctx, far_side = swap_ctx(back[1, 1][0]), swap_side(back[1, 1][1])
            core_at, (back[0, 1], far_ctx, far_side) = hold(core_at, (back[0, 1], far_ctx, far_side))
        keep_out, send_out, keep_back, send_back, *kept = run_expert(
            core_at,
            order.astype(jnp.int32),
            number,
            4,
            m_all.reshape(*grid_of, rows_dev, width),
            g_all.reshape(*grid_of, rows_dev, g_half),
            g_parts[d_side, d_ctx, 0],
            g_parts[d_side, d_ctx, 1],
            gates_all.reshape(*grid_of, 1, rows_dev),
            expert_gate_up[0],
            expert_down[0],
            capacity,
            kept,
        )
        back[at] = over_core(keep_back, send_back)
        out[at] = (keep_out, send_out)
    gate_back, rows, grad_rows, hidden, grad_pair = kept
    grad_gates = lax.all_to_all(
        gate_back.reshape(fsdp * 2, rows_dev), both, split_axis=0, concat_axis=0, tiled=True
    ).T
    one_ctx, two_side = swap_ctx(back[0, 1][0]), swap_side(back[1, 0][1])
    one_side = swap_side(add_low(back[1, 0][0], far_ctx))
    two_ctx = swap_ctx(add_low(back[0, 1][1], far_side))
    one_mine = add_low(add_low(back[0, 0][0], one_ctx), one_side)
    two_mine = add_low(add_low(back[0, 0][1], two_side), two_ctx)
    two_sum = line_sum(two_mine, place, relative=True)
    one_sum = line_sum(one_mine, place, relative=True)
    grad_mid = jnp.concatenate([one_sum, two_sum], axis=-1)
    out = {at: over_core(*out[at]) for at in out}
    out_far_ctx, out_far_side = swap_ctx(out[1, 1][0]), swap_side(out[1, 1][1])
    grad_mid, (out_far_ctx, out_far_side) = hold(grad_mid, (out_far_ctx, out_far_side))
    grad_down = mul(hidden, grad_rows, lhs_turned)[None]
    grad_gate_up = mul(rows, grad_pair, lhs_turned)[None]

    grad_wide = jnp.where(chosen, grad_gates, 0.0)
    grad_logits = (
        gates_wide * (grad_wide - jnp.sum(gates_wide * grad_wide, axis=1, keepdims=True))
    ).astype(low)
    grad_router = mul(low_mid, grad_logits, lhs_turned)
    grad_mid = grad_mid + mul(grad_logits, router_all, rhs_turned)
    grad_mixed_part, grad_moe_gain = rms_back(mixed, moe_all, grad_mid)
    grad_mixed = cotangent.astype(full) + grad_mixed_part

    grad_branch = sequence(grad_mixed.astype(low))
    grad_attended = mul(grad_branch, out_all, rhs_turned).astype(low)
    grad_out_part = mul(attended, grad_branch, lhs_turned).astype(low)
    out_ctx, out_side = swap_ctx(out[0, 1][0]), swap_side(out[1, 0][1])
    grad_attended, (out_ctx, out_side) = hold(grad_attended, (out_ctx, out_side))
    grad_q, grad_k, grad_v, gain_q_part, gain_k_part = attend_grad(
        projected, roped_q, roped_k, values_low, grad_attended, cosine, sine, gain_q, gain_k, kv_heads, group
    )
    grad_projected = jnp.concatenate([grad_q, grad_k, grad_v], axis=1)
    out_one = swap_side(add_low(out[1, 0][0], out_far_ctx))
    out_two = swap_ctx(add_low(out[0, 1][1], out_far_side))
    grad_projected, (out_one, out_two) = hold(grad_projected, (out_one, out_two))
    one_mine = add_low(add_low(out[0, 0][0], out_ctx), out_one)
    two_mine = add_low(add_low(out[0, 0][1], out_side), out_two)
    output = (
        mixed
        + jnp.concatenate(
            [line_sum(one_mine, place, relative=True), line_sum(two_mine, place, relative=True)], axis=-1
        )
    ).astype(low)
    grad_qkv_part = mul(low_in, grad_projected, lhs_turned).astype(low)
    grad_normed_part = mul(grad_projected, qkv_all, rhs_turned)
    grad_normed = of_block(grad_normed_part, rank) + swap_ctx(
        of_block(grad_normed_part, 1 - rank).astype(low)
    ).astype(full)
    grad_in_part, grad_attn_gain = rms_back(inputs, attn_all, grad_normed)
    grad_tokens = grad_mixed + grad_in_part

    out_mine = sum_fsdp(grad_out_part, place, side, core)
    out_other = swap_ctx(out_mine.astype(low)).astype(full)
    grad_out = jnp.where(
        rank == 0,
        jnp.concatenate([out_mine, out_other], axis=0),
        jnp.concatenate([out_other, out_mine], axis=0),
    )
    qkv_mine = sum_fsdp(grad_qkv_part, place, side, core)
    qkv_other = swap_ctx(qkv_mine.astype(low)).astype(full)
    q_mine = qkv_mine[:, :width_q].reshape(shard, my_heads, 1, head_dim)
    q_other = qkv_other[:, :width_q].reshape(shard, my_heads, 1, head_dim)
    grad_q_all = jnp.where(
        rank == 0,
        jnp.concatenate([q_mine, q_other], axis=2),
        jnp.concatenate([q_other, q_mine], axis=2),
    ).reshape(shard, 2 * width_q)
    grad_qkv = jnp.concatenate(
        [grad_q_all, qkv_mine[:, width_q:] + qkv_other[:, width_q:]], axis=1
    )
    early = sum_owned(jnp.concatenate([grad_router.T, grad_moe_gain[None]], axis=0), fsdp, spot)
    late = sum_all(
        jnp.concatenate(
            [
                grad_attn_gain.reshape(-1, head_dim),
                jnp.sum(gain_q_part, axis=0),
                jnp.sum(gain_k_part, axis=0),
            ],
            axis=0,
        ),
        fsdp,
    )
    gain_rows = width // head_dim
    return (
        output,
        grad_tokens,
        grad_qkv,
        grad_out,
        early[:experts_all].T,
        lax.dynamic_slice_in_dim(late[:gain_rows].reshape(-1), spot * shard, shard, 0),
        early[experts_all],
        late[gain_rows],
        late[gain_rows + 1],
        grad_gate_up,
        grad_down,
    )


gathered_bytes = 1 << 26


def choose_body(*args):
    tokens, gate_up = args[0], args[8]
    fsdp, ctx = lax.axis_size("fsdp"), lax.axis_size("ctx")
    fits = tokens.size * tokens.dtype.itemsize * fsdp * ctx <= gathered_bytes
    if fits and fsdp % 4 == 0 and ctx == 2 and fsdp & (fsdp - 1) == 0 and gate_up.shape[0] == 1:
        return body_gathered(*args)
    return body_routed(*args)


def solution(mesh):
    in_specs = (
        P(("fsdp", "ctx"), None),
        P("fsdp", None),
        P("fsdp", None),
        P("fsdp", None),
        P("fsdp"),
        P("fsdp"),
        P(),
        P(),
        P(("fsdp", "ctx"), None, None),
        P(("fsdp", "ctx"), None, None),
        P(("fsdp", "ctx"), None),
        P(("fsdp", "ctx"), None),
    )
    out_specs = (
        P(("fsdp", "ctx"), None),
        P(("fsdp", "ctx"), None),
        P("fsdp", None),
        P("fsdp", None),
        P("fsdp", None),
        P("fsdp"),
        P("fsdp"),
        P(),
        P(),
        P(("fsdp", "ctx"), None, None),
        P(("fsdp", "ctx"), None, None),
    )
    return jax.shard_map(choose_body, mesh=mesh, in_specs=in_specs, out_specs=out_specs, check_vma=False)
```

```python
import functools
import math

import jax
import jax.numpy as jnp
from jax import lax
from jax.experimental import pallas as pl
from jax.experimental.pallas import tpu as pltpu
from jax.sharding import PartitionSpec as P

eps_norm = 1e-06
theta_base = 1000000.0


def rms_scale(values, gain):
    return values * lax.rsqrt(jnp.mean(values * values, axis=-1, keepdims=True) + eps_norm) * gain


def rotate(values, cosine, sine):
    half_width = values.shape[-1] // 2
    turned = jnp.concatenate([-values[..., half_width:], values[..., :half_width]], axis=-1)
    return values * cosine + turned * sine


def angles(positions, width):
    freqs = theta_base ** (-(jnp.arange(width // 2, dtype=jnp.float32) * 2.0) / width)
    phase = positions.astype(jnp.float32)[:, None] * freqs[None, :]
    phase = jnp.concatenate([phase, phase], axis=-1)
    return (jnp.cos(phase)[:, None, :], jnp.sin(phase)[:, None, :])


def device_positions(block_rank, ctx_count, tok_rows):
    half_rows = tok_rows // 2
    within = jnp.arange(tok_rows, dtype=jnp.int32)
    span_id = jnp.where(within < half_rows, block_rank, 2 * ctx_count - 1 - block_rank)
    return span_id * half_rows + within % half_rows


def attend_head(query, keys_in, values_in, causal, scale_root):
    scores = (
        jnp.einsum("tgd,sd->gts", query, keys_in, preferred_element_type=jnp.float32) / scale_root
    )
    expo = jnp.where(causal[None], jnp.exp(scores), 0.0)
    totals = jnp.sum(expo, axis=-1, keepdims=True)
    probs = (expo / totals).astype(jnp.bfloat16)
    attended = jnp.einsum("gts,sd->tgd", probs, values_in, preferred_element_type=jnp.float32)
    return (attended, jnp.log(totals[..., 0]))


def attend_back(query, keys_in, values_in, causal, log_total, grad_attended, scale_root):
    scores = (
        jnp.einsum("tgd,sd->gts", query, keys_in, preferred_element_type=jnp.float32) / scale_root
    )
    probs = jnp.where(causal[None], jnp.exp(scores - log_total[..., None]), 0.0)
    low_probs = probs.astype(jnp.bfloat16)
    grad_values = jnp.einsum(
        "gts,tgd->sd", low_probs, grad_attended, preferred_element_type=jnp.float32
    )
    grad_probs = jnp.einsum(
        "tgd,sd->gts", grad_attended, values_in, preferred_element_type=jnp.float32
    )
    delta_rows = jnp.sum(grad_probs * probs, axis=-1, keepdims=True)
    grad_scores = (probs * (grad_probs - delta_rows)).astype(jnp.bfloat16)
    grad_query = (
        jnp.einsum("gts,sd->tgd", grad_scores, keys_in, preferred_element_type=jnp.float32)
        / scale_root
    )
    grad_keys = (
        jnp.einsum("gts,tgd->sd", grad_scores, query, preferred_element_type=jnp.float32)
        / scale_root
    )
    return (grad_query, grad_keys, grad_values)


def swiglu(paired):
    half_width = paired.shape[-1] // 2
    return jax.nn.silu(paired[..., :half_width]) * paired[..., half_width:]


def gating(selected):
    expo = jnp.exp(selected)
    return expo / jnp.sum(expo, axis=1, keepdims=True)


def body_routed(
    tokens,
    qkv_weight,
    out_weight,
    router_weight,
    attn_gain,
    moe_gain,
    query_gain,
    key_gain,
    expert_gate_up,
    expert_down,
    routes,
    cotangent,
):
    rows_dev, width = tokens.shape
    head_dim = query_gain.shape[0]
    top_k = routes.shape[1]
    ctx_count = lax.axis_size("ctx")
    ctx_rank = lax.axis_index("ctx")
    qkv_all, out_all, router_all, attn_all, moe_all = (
        lax.all_gather(qkv_weight, "fsdp", axis=0, tiled=True),
        lax.all_gather(out_weight, "fsdp", axis=0, tiled=True),
        lax.all_gather(router_weight, "fsdp", axis=0, tiled=True),
        lax.all_gather(attn_gain, "fsdp", axis=0, tiled=True),
        lax.all_gather(moe_gain, "fsdp", axis=0, tiled=True),
    )
    experts_all = router_all.shape[1]
    heads = out_all.shape[0] // head_dim
    kv_heads = (qkv_all.shape[1] // head_dim - heads) // 2
    group_size = heads // kv_heads
    capacity = 2 * rows_dev * top_k // experts_all
    width_q = heads * head_dim
    width_k = kv_heads * head_dim
    scale_root = math.sqrt(head_dim)
    inputs = tokens.astype(jnp.float32)
    normed_in = rms_scale(inputs, attn_all.astype(jnp.float32))
    low_in = normed_in.astype(jnp.bfloat16)
    projected = jnp.dot(low_in, qkv_all, preferred_element_type=jnp.float32)
    query_raw = projected[:, :width_q].reshape(rows_dev, heads, head_dim)
    key_raw = projected[:, width_q : width_q + width_k].reshape(rows_dev, kv_heads, head_dim)
    value_low = (
        projected[:, width_q + width_k :].astype(jnp.bfloat16).reshape(rows_dev, kv_heads, head_dim)
    )
    positions = device_positions(ctx_rank, ctx_count, rows_dev)
    cosine, sine = angles(positions, head_dim)
    query_gain_f = query_gain.astype(jnp.float32)
    key_gain_f = key_gain.astype(jnp.float32)

    def query_rope(values_in, gain):
        return rotate(rms_scale(values_in, gain), cosine, sine)

    query_low = query_rope(query_raw, query_gain_f).astype(jnp.bfloat16)
    key_low = query_rope(key_raw, key_gain_f).astype(jnp.bfloat16)
    keys_all, values_all = (
        lax.all_gather(key_low, "ctx", axis=0, tiled=True),
        lax.all_gather(value_low, "ctx", axis=0, tiled=True),
    )
    key_pos = jnp.concatenate(
        [device_positions(other, ctx_count, rows_dev) for other in range(ctx_count)]
    )
    causal = key_pos[None, :] <= positions[:, None]
    query_heads = query_low.reshape(rows_dev, kv_heads, group_size, head_dim).transpose(1, 0, 2, 3)
    key_heads = keys_all.transpose(1, 0, 2)
    value_heads = values_all.transpose(1, 0, 2)
    attended, log_total = lax.map(
        lambda member: attend_head(member[0], member[1], member[2], causal, scale_root),
        (query_heads, key_heads, value_heads),
    )
    attended_low = attended.transpose(1, 0, 2, 3).reshape(rows_dev, width_q).astype(jnp.bfloat16)
    mixed = inputs + jnp.dot(attended_low, out_all, preferred_element_type=jnp.float32)
    normed_mid = rms_scale(mixed, moe_all.astype(jnp.float32))
    low_mid = normed_mid.astype(jnp.bfloat16)
    logits = jnp.dot(low_mid, router_all, preferred_element_type=jnp.float32)
    selected = jnp.take_along_axis(logits, routes, axis=1)
    gates, gate_back = jax.vjp(gating, selected)
    flat_routes = routes.reshape(-1)
    expert_ids = jnp.arange(experts_all, dtype=jnp.int32)
    hit_table = (flat_routes[:, None] == expert_ids[None, :]).astype(jnp.int32)
    slot_index = jnp.sum(jnp.cumsum(hit_table, axis=0) * hit_table, axis=1) - 1
    target = flat_routes * capacity + slot_index
    pair_count = rows_dev * top_k
    source_pair = (
        jnp.full((experts_all * capacity,), pair_count, jnp.int32)
        .at[target]
        .set(jnp.arange(pair_count, dtype=jnp.int32))
    )
    padded = jnp.concatenate([low_mid, jnp.zeros((1, width), jnp.bfloat16)], axis=0)
    outgoing = padded[source_pair // top_k].reshape(experts_all, capacity, width)
    received = lax.all_to_all(outgoing, ("fsdp", "ctx"), split_axis=0, concat_axis=1, tiled=True)
    gate_and_up = jnp.einsum(
        "esd,edf->esf", received, expert_gate_up, preferred_element_type=jnp.float32
    )
    hidden_val, swiglu_back = jax.vjp(swiglu, gate_and_up)
    hidden_low = hidden_val.astype(jnp.bfloat16)
    result_low = jnp.einsum(
        "esf,efd->esd", hidden_low, expert_down, preferred_element_type=jnp.float32
    ).astype(jnp.bfloat16)
    returned = lax.all_to_all(
        result_low, ("fsdp", "ctx"), split_axis=1, concat_axis=0, tiled=True
    ).reshape(experts_all * capacity, width)
    picked = returned[target].reshape(rows_dev, top_k, width).astype(jnp.float32)
    output = (mixed + jnp.sum(gates[:, :, None] * picked, axis=1)).astype(jnp.bfloat16)
    qkv_back, out_back, router_back, attn_back_g, moe_back_g = (
        qkv_all,
        out_all,
        router_all,
        attn_all,
        moe_all,
    )
    grad_final = cotangent.astype(jnp.float32)
    grad_gates = jnp.sum(grad_final[:, None, :] * picked, axis=2)
    grad_result = (
        (gates[:, :, None] * grad_final[:, None, :]).astype(jnp.bfloat16).reshape(pair_count, width)
    )
    grad_padded = jnp.concatenate([grad_result, jnp.zeros((1, width), jnp.bfloat16)], axis=0)
    grad_outgoing = grad_padded[source_pair].reshape(experts_all, capacity, width)
    grad_received = lax.all_to_all(
        grad_outgoing, ("fsdp", "ctx"), split_axis=0, concat_axis=1, tiled=True
    )
    grad_down = jnp.einsum(
        "esf,esd->efd", hidden_low, grad_received, preferred_element_type=jnp.float32
    )
    grad_hidden = jnp.einsum(
        "esd,efd->esf", grad_received, expert_down, preferred_element_type=jnp.float32
    )
    grad_paired = swiglu_back(grad_hidden)[0].astype(jnp.bfloat16)
    grad_gate_up = jnp.einsum(
        "esd,esf->edf", received, grad_paired, preferred_element_type=jnp.float32
    )
    grad_rows = jnp.einsum(
        "esf,edf->esd", grad_paired, expert_gate_up, preferred_element_type=jnp.float32
    ).astype(jnp.bfloat16)
    grad_returned = lax.all_to_all(
        grad_rows, ("fsdp", "ctx"), split_axis=1, concat_axis=0, tiled=True
    ).reshape(experts_all * capacity, width)
    grad_mid = jnp.sum(
        grad_returned[target].reshape(rows_dev, top_k, width).astype(jnp.float32), axis=1
    )
    grad_selected = gate_back(grad_gates)[0]
    route_table = (routes[:, :, None] == expert_ids[None, None, :]).astype(jnp.float32)
    grad_logits = jnp.sum(route_table * grad_selected[:, :, None], axis=1).astype(jnp.bfloat16)
    grad_router = jnp.dot(low_mid.T, grad_logits, preferred_element_type=jnp.float32)
    grad_mid = grad_mid + jnp.dot(grad_logits, router_back.T, preferred_element_type=jnp.float32)
    unused_mid, mid_back = jax.vjp(rms_scale, mixed, moe_back_g.astype(jnp.float32))
    grad_mixed_part, grad_moe_gain = mid_back(grad_mid)
    grad_mixed = grad_final + grad_mixed_part
    grad_branch = grad_mixed.astype(jnp.bfloat16)
    grad_out = jnp.dot(attended_low.T, grad_branch, preferred_element_type=jnp.float32)
    grad_attended = jnp.dot(grad_branch, out_back.T, preferred_element_type=jnp.float32).astype(
        jnp.bfloat16
    )
    grad_heads = grad_attended.reshape(rows_dev, kv_heads, group_size, head_dim).transpose(
        1, 0, 2, 3
    )
    grad_query_h, grad_key_h, grad_value_h = lax.map(
        lambda member: attend_back(
            member[0], member[1], member[2], causal, member[3], member[4], scale_root
        ),
        (query_heads, key_heads, value_heads, log_total, grad_heads),
    )
    grad_keys, grad_values = (
        lax.psum_scatter(
            grad_key_h.transpose(1, 0, 2).astype(jnp.bfloat16),
            "ctx",
            scatter_dimension=0,
            tiled=True,
        ).astype(jnp.float32),
        lax.psum_scatter(
            grad_value_h.transpose(1, 0, 2).astype(jnp.bfloat16),
            "ctx",
            scatter_dimension=0,
            tiled=True,
        ).astype(jnp.float32),
    )
    grad_query_rot = (
        grad_query_h.transpose(1, 0, 2, 3).reshape(rows_dev, heads, head_dim).astype(jnp.bfloat16)
    )
    grad_query_rot = lax.optimization_barrier(grad_query_rot).astype(jnp.float32)
    grad_key_rot = lax.optimization_barrier(grad_keys.astype(jnp.bfloat16)).astype(jnp.float32)
    unused_query, query_back = jax.vjp(query_rope, query_raw, query_gain_f)
    grad_query_raw, grad_query_gain = query_back(grad_query_rot)
    unused_key, key_back = jax.vjp(query_rope, key_raw, key_gain_f)
    grad_key_raw, grad_key_gain = key_back(grad_key_rot)
    grad_projected = jnp.concatenate(
        [
            grad_query_raw.reshape(rows_dev, width_q).astype(jnp.bfloat16),
            grad_key_raw.reshape(rows_dev, width_k).astype(jnp.bfloat16),
            grad_values.reshape(rows_dev, width_k).astype(jnp.bfloat16),
        ],
        axis=1,
    )
    grad_qkv = jnp.dot(low_in.T, grad_projected, preferred_element_type=jnp.float32)
    grad_normed = jnp.dot(grad_projected, qkv_back.T, preferred_element_type=jnp.float32)
    unused_in, in_back = jax.vjp(rms_scale, inputs, attn_back_g.astype(jnp.float32))
    grad_in_part, grad_attn_gain = in_back(grad_normed)
    grad_tokens = grad_mixed + grad_in_part
    gradients = (grad_qkv, grad_out, grad_router, grad_attn_gain, grad_moe_gain)
    pieces = (
        lax.psum_scatter(gradients[0], "fsdp", scatter_dimension=0, tiled=True),
        lax.psum_scatter(gradients[1], "fsdp", scatter_dimension=0, tiled=True),
        lax.psum_scatter(gradients[2], "fsdp", scatter_dimension=0, tiled=True),
        lax.psum_scatter(gradients[3], "fsdp", scatter_dimension=0, tiled=True),
        lax.psum_scatter(gradients[4], "fsdp", scatter_dimension=0, tiled=True),
    )
    reduced = (
        lax.psum(pieces[0].astype(jnp.bfloat16), "ctx").astype(jnp.float32),
        lax.psum(pieces[1].astype(jnp.bfloat16), "ctx").astype(jnp.float32),
        lax.psum(pieces[2].astype(jnp.bfloat16), "ctx").astype(jnp.float32),
        lax.psum(pieces[3].astype(jnp.bfloat16), "ctx").astype(jnp.float32),
        lax.psum(pieces[4].astype(jnp.bfloat16), "ctx").astype(jnp.float32),
    )
    gain_sums = lax.psum((grad_query_gain, grad_key_gain), ("fsdp", "ctx"))
    return (
        output,
        grad_tokens,
        reduced[0],
        reduced[1],
        reduced[2],
        reduced[3],
        reduced[4],
        gain_sums[0],
        gain_sums[1],
        grad_gate_up,
        grad_down,
    )


low = jnp.bfloat16
full = jnp.float32
plain = (((1,), (0,)), ((), ()))
rhs_turned = (((1,), (1,)), ((), ()))
lhs_turned = (((0,), (0,)), ((), ()))
vmem_bytes = 58 << 20


def mul(left, right, dims=plain):
    return lax.dot_general(left, right, dims, preferred_element_type=full)


def core_pairs(fsdp):
    return [(i, i ^ 1) for i in range(fsdp)]


def side_pairs(fsdp):
    return [(i, i ^ 2) for i in range(fsdp)]


def swap_core(values):
    return lax.ppermute(values, "fsdp", core_pairs(lax.axis_size("fsdp")))


def swap_side(values):
    return lax.ppermute(values, "fsdp", side_pairs(lax.axis_size("fsdp")))


def swap_ctx(values):
    return lax.ppermute(values, "ctx", [(0, 1), (1, 0)])


def add_low(one, two):
    return (one.astype(full) + two.astype(full)).astype(low)


def hold(values, first):
    return lax.optimization_barrier((values, first))


def take(values, index):
    return lax.dynamic_index_in_dim(values, index, 0, keepdims=False)


def line_shift(values, step):
    fsdp = lax.axis_size("fsdp")
    return lax.ppermute(values, "fsdp", [(i, (i + 4 * step) % fsdp) for i in range(fsdp)])


def line_sum(values):
    count = values.shape[0]
    total = values[0].astype(full)
    for step in range(1, count):
        total = total + line_shift(values[count - step], step).astype(full)
    return total


def over_core(keep, send, pieces):
    step = keep.shape[-1] // pieces
    other = swap_core(send)
    return [
        add_low(keep[..., i * step : (i + 1) * step], other[..., i * step : (i + 1) * step])
        for i in range(pieces)
    ]


def sum_all(values, fsdp):
    values = values + lax.ppermute(values, "fsdp", core_pairs(fsdp))
    values = values + swap_ctx(values)
    step = 2
    while step < fsdp:
        values = values + lax.ppermute(values, "fsdp", [(i, i ^ step) for i in range(fsdp)])
        step *= 2
    return values


def sum_owned(values, fsdp, spot):
    items, shard = values.shape[0], values.shape[1] // fsdp
    values = values.reshape(items, fsdp, shard).swapaxes(0, 1)
    step = fsdp // 2
    while step:
        bit = (spot // step) % 2
        values = values.reshape(2, step, items, shard)
        other = lax.ppermute(take(values, 1 - bit), "fsdp", [(i, i ^ step) for i in range(fsdp)])
        values = take(values, bit) + other
        step //= 2
    values = values[0]
    return values + swap_ctx(values)


def turn(values):
    return pltpu.roll(values, values.shape[-1] // 2, 1)


def norm_rope(raw, gain, cosine, sine):
    scale = lax.rsqrt(jnp.mean(raw * raw, axis=-1, keepdims=True) + eps_norm)
    scaled = raw * scale * gain
    return scaled * cosine + turn(scaled) * sine


def norm_rope_back(raw, gain, cosine, sine, grad):
    scale = lax.rsqrt(jnp.mean(raw * raw, axis=-1, keepdims=True) + eps_norm)
    unit = raw * scale
    grad_scaled = grad * cosine - turn(grad) * sine
    grad_gain = jnp.sum(grad_scaled * unit, axis=0, keepdims=True)
    grad_unit = grad_scaled * gain
    grad_raw = scale * (grad_unit - unit * jnp.mean(grad_unit * unit, axis=-1, keepdims=True))
    return grad_raw, grad_gain


def tiles_of(rows):
    step = rows // 2
    return [(start, start + step) for start in range(0, rows, step)]


def allowed(start, stop):
    shape = (stop - start, stop)
    return lax.broadcasted_iota(jnp.int32, shape, 1) <= (
        lax.broadcasted_iota(jnp.int32, shape, 0) + start
    )


def attend_kernel(q_ref, k_ref, v_ref, cos_ref, sin_ref, qg_ref, kg_ref, o_ref, qr_ref, kr_ref, vl_ref):
    head_dim = k_ref.shape[1]
    rows = k_ref.shape[0]
    cosine, sine = cos_ref[...], sin_ref[...]
    keys = norm_rope(k_ref[...], kg_ref[...], cosine, sine).astype(low)
    values = v_ref[...].astype(low)
    kr_ref[...] = keys
    vl_ref[...] = values
    for head in range(q_ref.shape[1] // head_dim):
        cols = slice(head * head_dim, (head + 1) * head_dim)
        query = norm_rope(q_ref[:, cols], qg_ref[...], cosine, sine).astype(low)
        qr_ref[:, cols] = query
        for start, stop in tiles_of(rows):
            scores = mul(query[start:stop], keys[:stop], rhs_turned) * (1.0 / math.sqrt(head_dim))
            expo = jnp.where(allowed(start, stop), jnp.exp(scores), 0.0)
            probs = (expo / jnp.sum(expo, axis=-1, keepdims=True)).astype(low)
            o_ref[start:stop, cols] = mul(probs, values[:stop]).astype(low)


def attend_grad_kernel(
    q_ref, k_ref, qr_ref, kr_ref, vl_ref, go_ref, cos_ref, sin_ref, qg_ref, kg_ref,
    dq_ref, dk_ref, dv_ref, dqg_ref, dkg_ref, dk_sum, dv_sum, dq_sum,
):
    head_dim = k_ref.shape[1]
    rows = k_ref.shape[0]
    root = 1.0 / math.sqrt(head_dim)
    cosine, sine = cos_ref[...], sin_ref[...]
    keys, values = kr_ref[...], vl_ref[...]
    gain_sum = jnp.zeros((1, head_dim), full)
    dk_sum[...] = jnp.zeros_like(dk_sum)
    dv_sum[...] = jnp.zeros_like(dv_sum)
    for head in range(q_ref.shape[1] // head_dim):
        cols = slice(head * head_dim, (head + 1) * head_dim)
        for start, stop in tiles_of(rows):
            query = qr_ref[start:stop, cols]
            grad = go_ref[start:stop, cols]
            scores = mul(query, keys[:stop], rhs_turned) * root
            expo = jnp.where(allowed(start, stop), jnp.exp(scores), 0.0)
            probs = expo / jnp.sum(expo, axis=-1, keepdims=True)
            grad_probs = mul(grad, values[:stop], rhs_turned)
            delta = jnp.sum(grad_probs * probs, axis=-1, keepdims=True)
            grad_scores = (probs * (grad_probs - delta)).astype(low)
            dv_sum[:stop] += mul(probs.astype(low), grad, lhs_turned)
            dk_sum[:stop] += mul(grad_scores, query, lhs_turned)
            dq_sum[start:stop] = mul(grad_scores, keys[:stop])
        grad_query = (dq_sum[...] * root).astype(low).astype(full)
        grad_raw, grad_gain = norm_rope_back(q_ref[:, cols], qg_ref[...], cosine, sine, grad_query)
        dq_ref[:, cols] = grad_raw.astype(low)
        gain_sum = gain_sum + grad_gain
    dqg_ref[0] = gain_sum
    grad_key = (dk_sum[...] * root).astype(low).astype(full)
    grad_raw, grad_gain = norm_rope_back(k_ref[...], kg_ref[...], cosine, sine, grad_key)
    dk_ref[...] = grad_raw.astype(low)
    dkg_ref[0] = grad_gain
    dv_ref[...] = dv_sum[...].astype(low)


def attention_specs(rows, head_dim, kv_heads, group):
    wide, narrow = group * head_dim, head_dim
    heads_end = kv_heads * group
    return dict(
        q=pl.BlockSpec((rows, wide), lambda i: (0, i)),
        k=pl.BlockSpec((rows, narrow), lambda i: (0, heads_end + i)),
        v=pl.BlockSpec((rows, narrow), lambda i: (0, heads_end + kv_heads + i)),
        own=pl.BlockSpec((rows, narrow), lambda i: (0, i)),
        table=pl.BlockSpec((rows, head_dim), lambda i: (0, 0)),
        gain=pl.BlockSpec((1, head_dim), lambda i: (0, 0)),
        gain_out=pl.BlockSpec((1, 1, head_dim), lambda i: (i, 0, 0)),
    )


def attend(projected, cosine, sine, query_gain, key_gain, kv_heads, group):
    rows, head_dim = cosine.shape
    s = attention_specs(rows, head_dim, kv_heads, group)
    shape = jax.ShapeDtypeStruct
    work = rows * rows * head_dim * kv_heads * group
    return pl.pallas_call(
        attend_kernel,
        grid=(kv_heads,),
        in_specs=[s["q"], s["k"], s["v"], s["table"], s["table"], s["gain"], s["gain"]],
        out_specs=[s["q"], s["q"], s["own"], s["own"]],
        out_shape=[
            shape((rows, kv_heads * group * head_dim), low),
            shape((rows, kv_heads * group * head_dim), low),
            shape((rows, kv_heads * head_dim), low),
            shape((rows, kv_heads * head_dim), low),
        ],
        compiler_params=pltpu.CompilerParams(vmem_limit_bytes=48 << 20),
        cost_estimate=pl.CostEstimate(
            flops=4 * work, bytes_accessed=projected.size * 6, transcendentals=work // head_dim
        ),
        name="attend",
    )(projected, projected, projected, cosine, sine, query_gain, key_gain)


def attend_grad(projected, roped_q, roped_k, values_low, grad, cosine, sine, query_gain, key_gain, kv_heads, group):
    rows, head_dim = cosine.shape
    s = attention_specs(rows, head_dim, kv_heads, group)
    shape = jax.ShapeDtypeStruct
    work = rows * rows * head_dim * kv_heads * group
    return pl.pallas_call(
        attend_grad_kernel,
        grid=(kv_heads,),
        in_specs=[
            s["q"], s["k"], s["q"], s["own"], s["own"], s["q"],
            s["table"], s["table"], s["gain"], s["gain"],
        ],
        out_specs=[s["q"], s["own"], s["own"], s["gain_out"], s["gain_out"]],
        out_shape=[
            shape((rows, kv_heads * group * head_dim), low),
            shape((rows, kv_heads * head_dim), low),
            shape((rows, kv_heads * head_dim), low),
            shape((kv_heads, 1, head_dim), full),
            shape((kv_heads, 1, head_dim), full),
        ],
        scratch_shapes=[pltpu.VMEM((rows, head_dim), full)] * 3,
        compiler_params=pltpu.CompilerParams(vmem_limit_bytes=48 << 20),
        cost_estimate=pl.CostEstimate(
            flops=10 * work, bytes_accessed=projected.size * 10, transcendentals=work // head_dim
        ),
        name="attend_grad",
    )(projected, projected, roped_q, roped_k, values_low, grad, cosine, sine, query_gain, key_gain)


def expert_kernel(core_ref, order, m_ref, g_ref, g_more, w_ref, gu_ref, dn_ref, *refs):
    (keep_out, send_out, keep_back, send_back, gate_back, rows_ref, dy_ref, z_ref, pair_ref) = refs[-9:]
    core = core_ref[0]
    block = m_ref.shape[3]
    hidden = dn_ref.shape[0]
    slots = z_ref.shape[0] // 2
    shape = (block, block)
    earlier = (
        lax.broadcasted_iota(jnp.int32, shape, 0) < lax.broadcasted_iota(jnp.int32, shape, 1)
    ).astype(low)
    slot_ids = lax.broadcasted_iota(jnp.int32, (slots, block), 0)
    places, picks, weights, rows, grads = [], [], [], [], []
    for part in range(2):
        at = lax.rem(core + part, 2)
        gate = w_ref[0, at, 0]
        hit = jnp.where(gate >= 0.0, 1.0, 0.0)
        ones = jnp.broadcast_to(hit, (8, block)).astype(low)
        count = mul(ones, earlier)[:1].astype(jnp.int32)
        place = (slot_ids == count) & (hit > 0.5)
        pick = place.astype(full).astype(low)
        places.append(place)
        picks.append(pick)
        weights.append(jnp.sum(jnp.where(place, gate, 0.0), axis=1, keepdims=True))
        rows.append(mul(pick, m_ref[0, at, 0]).astype(low))
        grads.append(
            jnp.concatenate([mul(pick, g_ref[0, at, 0]), mul(pick, g_more[0, at, 0])], axis=1)
        )
    row, grad, weight = (jnp.concatenate(items, axis=0) for items in (rows, grads, weights))
    rows_ref[...] = row
    paired = mul(row, gu_ref[...])
    gate_in, up = paired[:, :hidden], paired[:, hidden:]
    sig = jax.nn.sigmoid(gate_in)
    act = gate_in * sig
    z = (act * up).astype(low)
    z_ref[...] = z
    y = mul(z, dn_ref[...]).astype(low).astype(full)
    grad_gate = jnp.sum(grad * y, axis=1, keepdims=True)
    y_scaled = (weight * y).astype(low)
    dy = (weight * grad).astype(low)
    dy_ref[...] = dy
    for part, out in enumerate((keep_out, send_out)):
        mine = slice(part * slots, (part + 1) * slots)
        out[0] = mul(picks[part], y_scaled[mine], lhs_turned).astype(low)
        gate_back[0, lax.rem(core + part, 2), 0] = jnp.sum(
            jnp.where(places[part], grad_gate[mine], 0.0), axis=0, keepdims=True
        )
    dz = mul(dy, dn_ref[...], rhs_turned)
    grad_in = dz * up * (sig * (1.0 + gate_in * (1.0 - sig)))
    pair = jnp.concatenate([grad_in, dz * act], axis=1).astype(low)
    pair_ref[...] = pair
    back = mul(pair, gu_ref[...], rhs_turned).astype(low)
    for part, out in enumerate((keep_back, send_back)):
        mine = slice(part * slots, (part + 1) * slots)
        out[0] = mul(picks[part], back[mine], lhs_turned).astype(low)


def run_expert(core, order, number, parts, m_all, g_one, g_two, gates_all, gate_up, down, slots, kept):
    places, _, _, block, width = m_all.shape
    paired = gate_up.shape[1]
    steps = order.shape[0] // 3
    part_rows = steps * 2 * slots
    hidden = paired // 2
    shape = jax.ShapeDtypeStruct

    def gates_at(i, core, order):
        return (order[3 * i], 0, order[3 * i + 1], 0, 0)

    def token_at(i, core, order):
        return (order[3 * i], 0, order[3 * i + 2], 0, 0)

    def half_spec(index):
        return pl.BlockSpec((1, 2, 1, block, width // 2), lambda i, core, order: (order[3 * i], 0, index, 0, 0))

    def fixed(i, core, order):
        return (0, 0)

    def flat(i, core, order):
        return (number * steps + i, 0)

    def stacked(i, core, order):
        return (i, 0, 0)

    small = pl.BlockSpec((1, 2, 1, 1, block), gates_at)
    one_block = pl.BlockSpec((1, block, width), stacked)
    widths = (width, width, hidden, paired)
    grid_spec = pltpu.PrefetchScalarGridSpec(
        num_scalar_prefetch=2,
        grid=(steps,),
        in_specs=[
            pl.BlockSpec((1, 2, 1, block, width), token_at),
            half_spec(g_one[1]), half_spec(g_two[1]), small,
            pl.BlockSpec(gate_up.shape, fixed, pipeline_mode=pl.Buffered(1)),
            pl.BlockSpec(down.shape, fixed, pipeline_mode=pl.Buffered(1)),
        ]
        + [pl.BlockSpec(memory_space=pl.ANY)] * (0 if kept is None else 5),
        out_specs=[one_block] * 4 + [small] + [pl.BlockSpec((2 * slots, n), flat) for n in widths],
    )
    return pl.pallas_call(
        expert_kernel,
        grid_spec=grid_spec,
        out_shape=[shape((steps, block, width), low)] * 4
        + [shape((places, 2, 2, 1, block), full)]
        + [shape((parts * part_rows, n), low) for n in widths],
        input_output_aliases={} if kept is None else {8 + i: 4 + i for i in range(5)},
        compiler_params=pltpu.CompilerParams(vmem_limit_bytes=vmem_bytes),
        cost_estimate=pl.CostEstimate(
            flops=part_rows * width * (4 * paired + 4 * hidden + 8 * block),
            bytes_accessed=steps * block * width * 16 + part_rows * (width * 4 + paired * 3),
            transcendentals=part_rows * hidden,
        ),
        name="experts",
    )(core, order, m_all, g_one[0], g_two[0], gates_all, gate_up, down, *(() if kept is None else kept))


def rms_back(values, gain, grad):
    scale = lax.rsqrt(jnp.mean(values * values, axis=-1, keepdims=True) + eps_norm)
    unit = values * scale
    grad_gain = jnp.sum(grad * unit, axis=0)
    grad_unit = grad * gain
    back = scale * (grad_unit - unit * jnp.mean(grad_unit * unit, axis=-1, keepdims=True))
    return back, grad_gain


def in_order(first, second):
    half = first.shape[0] // 2
    return jnp.concatenate([first[:half], second, first[half:]], axis=0)


def of_block(values, rank):
    quarter = values.shape[0] // 4
    outer = jnp.concatenate([values[:quarter], values[3 * quarter :]], axis=0)
    return jnp.where(rank == 0, outer, values[quarter : 3 * quarter])


def body_gathered(
    tokens, qkv_weight, out_weight, router_weight, attn_gain, moe_gain, query_gain, key_gain,
    expert_gate_up, expert_down, routes, cotangent,
):
    rows_dev, width = tokens.shape
    head_dim = query_gain.shape[0]
    top_k = routes.shape[1]
    fsdp = lax.axis_size("fsdp")
    spot = lax.axis_index("fsdp")
    rank = lax.axis_index("ctx")
    place, side, core = spot // 4, (spot // 2) % 2, spot % 2
    shard = qkv_weight.shape[0]
    heads = out_weight.shape[0] * fsdp // head_dim
    kv_heads = (qkv_weight.shape[1] // head_dim - heads) // 2
    group = heads // kv_heads // 2
    my_heads = heads // 2
    width_q, width_k = my_heads * head_dim, kv_heads * head_dim
    experts_all = router_weight.shape[1]
    capacity = 2 * rows_dev * top_k // experts_all
    both = ("fsdp", "ctx")

    def sequence(values):
        other = swap_ctx(values)
        first = jnp.where(rank == 0, values, other)
        second = jnp.where(rank == 0, other, values)
        return in_order(first, second)

    by_parity = qkv_weight[:, : 2 * width_q].reshape(shard, my_heads, 2, head_dim)
    q_local = jnp.where(rank == 0, by_parity[:, :, 0], by_parity[:, :, 1]).reshape(shard, width_q)
    out_local = lax.dynamic_slice_in_dim(out_weight, rank * head_dim, head_dim, 0)
    weights_local = jnp.concatenate([q_local, qkv_weight[:, 2 * width_q :], out_local], axis=1)
    small_local = jnp.concatenate([router_weight, attn_gain[:, None], moe_gain[:, None]], axis=1)
    small_all = lax.all_gather(small_local, "fsdp", axis=0, tiled=True)
    weights_all = lax.all_gather(weights_local, "fsdp", axis=0, tiled=True)
    qkv_all = weights_all[:, : width_q + 2 * width_k]
    out_all = weights_all[:, width_q + 2 * width_k :]
    router_all = small_all[:, :experts_all]
    attn_all = small_all[:, experts_all].astype(full)
    moe_all = small_all[:, experts_all + 1].astype(full)
    g_half = width // 2
    g_local = jnp.stack(
        [cotangent[:, :g_half], cotangent[:, g_half:], swap_ctx(cotangent[:, g_half:])]
    )
    g_all = lax.all_gather(
        g_local.reshape(3 * rows_dev, g_half), "fsdp", axis=0, tiled=True
    ).reshape(fsdp // 2, 2, 3, rows_dev, g_half)
    g_far = swap_ctx(g_all[:, :, :1])

    sequence_in = sequence(tokens).astype(full)
    low_in = rms_scale(sequence_in, attn_all).astype(low)
    projected = mul(low_in, qkv_all)
    cosine, sine = (t[:, 0] for t in angles(jnp.arange(2 * rows_dev, dtype=jnp.int32), head_dim))
    sine = jnp.concatenate([-sine[:, : head_dim // 2], sine[:, head_dim // 2 :]], axis=1)
    gain_q, gain_k = query_gain.astype(full)[None], key_gain.astype(full)[None]
    attended, roped_q, roped_k, values_low = attend(
        projected, cosine, sine, gain_q, gain_k, kv_heads, group
    )
    branch = mul(attended, out_all)
    inputs = tokens.astype(full)
    mixed = (
        inputs
        + of_block(branch, rank)
        + swap_ctx(of_block(branch, 1 - rank).astype(low)).astype(full)
    )
    low_mid = rms_scale(mixed, moe_all).astype(low)
    m_all = lax.all_gather(jnp.concatenate([low_mid, swap_ctx(low_mid)]), "fsdp", axis=0, tiled=True)

    logits = mul(low_mid, router_all)
    named = routes[:, :, None] == jnp.arange(experts_all, dtype=jnp.int32)[None, None, :]
    selected = jnp.sum(jnp.where(named, logits[:, None, :], 0.0), axis=2)
    gates = gating(selected)
    chosen = jnp.any(named, axis=1)
    gates_wide = jnp.sum(jnp.where(named, gates[:, :, None], 0.0), axis=1)
    gates_sent = jnp.where(chosen, gates_wide, -1.0).T
    gates_all = lax.all_to_all(gates_sent, both, split_axis=0, concat_axis=0, tiled=True)

    lines = fsdp // 4
    grid_of = (fsdp // 2, 2, 2)
    lines_at = (place - jnp.arange(lines, dtype=jnp.int32)) % lines
    kept, back, out = None, {}, {}
    core_at = core[None].astype(jnp.int32)
    for number, at in enumerate(((1, 1), (0, 1), (1, 0), (0, 0))):
        d_side, d_ctx = at
        order = jnp.stack(
            [
                lines_at * 2 + (side + d_side) % 2,
                jnp.broadcast_to((rank + d_ctx) % 2, (lines,)),
                jnp.full((lines,), d_ctx),
            ],
            axis=1,
        ).reshape(-1)
        if number == 1:
            core_at, back[1, 1] = hold(core_at, back[1, 1])
        if number == 2:
            far_ctx = swap_ctx(jnp.concatenate(back[1, 1][:2], axis=-1))
            far_side = swap_side(jnp.concatenate(back[1, 1][2:], axis=-1))
            core_at, (far_ctx, far_side) = hold(core_at, (far_ctx, far_side))
        if number == 3:
            core_at, (back[0, 1], back[1, 0]) = hold(core_at, (back[0, 1], back[1, 0]))
        keep_out, send_out, keep_back, send_back, *kept = run_expert(
            core_at,
            order.astype(jnp.int32),
            number,
            4,
            m_all.reshape(*grid_of, rows_dev, width),
            (g_far, 0) if d_ctx else (g_all, 0),
            (g_all, 1 + d_ctx),
            gates_all.reshape(*grid_of, 1, rows_dev),
            expert_gate_up[0],
            expert_down[0],
            capacity,
            kept,
        )
        back[at] = over_core(keep_back, send_back, 4)
        out[at] = (keep_out, send_out)
    gate_back, rows, grad_rows, hidden, grad_pair = kept
    grad_gates = lax.all_to_all(
        gate_back.reshape(fsdp * 2, rows_dev), both, split_axis=0, concat_axis=0, tiled=True
    ).T
    cut = far_ctx.shape[-1] // 2
    grad_down = mul(hidden, grad_rows, lhs_turned)[None]
    grad_gate_up = mul(rows, grad_pair, lhs_turned)[None]
    sums = []
    for k in range(2):
        cols = slice(k * cut, (k + 1) * cut)
        from_ctx, from_side = swap_ctx(back[0, 1][k]), swap_side(back[1, 0][2 + k])
        one_side = swap_side(add_low(back[1, 0][k], far_ctx[..., cols]))
        two_ctx = swap_ctx(add_low(back[0, 1][2 + k], far_side[..., cols]))
        both_mine = jnp.concatenate(
            [
                add_low(add_low(back[0, 0][k], from_ctx), one_side),
                add_low(add_low(back[0, 0][2 + k], from_side), two_ctx),
            ],
            axis=-1,
        )
        if k == 1:
            both_mine, (grad_down, grad_gate_up) = hold(both_mine, (grad_down, grad_gate_up))
        sums.append(line_sum(both_mine))
    out, last_round = hold(out, (one_side, two_ctx))
    out = {at: over_core(*out[at], 2) for at in out}
    out_far_ctx, out_far_side = swap_ctx(out[1, 1][0]), swap_side(out[1, 1][1])
    sums, (out_far_ctx, out_far_side) = hold(sums, (out_far_ctx, out_far_side))
    grad_mid = jnp.concatenate(
        [sums[0][:, :cut], sums[1][:, :cut], sums[0][:, cut:], sums[1][:, cut:]], axis=-1
    )

    grad_wide = jnp.where(chosen, grad_gates, 0.0)
    grad_logits = (
        gates_wide * (grad_wide - jnp.sum(gates_wide * grad_wide, axis=1, keepdims=True))
    ).astype(low)
    grad_router = mul(low_mid, grad_logits, lhs_turned)
    grad_mid = grad_mid + mul(grad_logits, router_all, rhs_turned)
    grad_mixed_part, grad_moe_gain = rms_back(mixed, moe_all, grad_mid)
    grad_mixed = cotangent.astype(full) + grad_mixed_part

    grad_branch = sequence(grad_mixed.astype(low))
    grad_attended = mul(grad_branch, out_all, rhs_turned).astype(low)
    grad_out_part = mul(attended, grad_branch, lhs_turned).astype(low)
    out, grad_branch = hold(out, grad_branch)
    out_ctx, out_side = swap_ctx(out[0, 1][0]), swap_side(out[1, 0][1])
    grad_attended, (out_ctx, out_side) = hold(grad_attended, (out_ctx, out_side))
    grad_q, grad_k, grad_v, gain_q_part, gain_k_part = attend_grad(
        projected, roped_q, roped_k, values_low, grad_attended, cosine, sine, gain_q, gain_k, kv_heads, group
    )
    grad_projected = jnp.concatenate([grad_q, grad_k, grad_v], axis=1)
    out_one = swap_side(add_low(out[1, 0][0], out_far_ctx))
    out_two = swap_ctx(add_low(out[0, 1][1], out_far_side))
    grad_projected, (out_one, out_two) = hold(grad_projected, (out_one, out_two))
    one_mine = add_low(add_low(out[0, 0][0], out_ctx), out_one)
    two_mine = add_low(add_low(out[0, 0][1], out_side), out_two)
    output = (
        mixed
        + jnp.concatenate(
            [line_sum(one_mine), line_sum(two_mine)], axis=-1
        )
    ).astype(low)
    grad_qkv_part = mul(low_in, grad_projected, lhs_turned).astype(low)
    grad_normed_part = mul(grad_projected, qkv_all, rhs_turned)
    grad_normed = of_block(grad_normed_part, rank) + swap_ctx(
        of_block(grad_normed_part, 1 - rank).astype(low)
    ).astype(full)
    grad_in_part, grad_attn_gain = rms_back(inputs, attn_all, grad_normed)
    grad_tokens = grad_mixed + grad_in_part

    out_mine = lax.psum_scatter(grad_out_part, "fsdp", scatter_dimension=0, tiled=True).astype(full)
    out_other = swap_ctx(out_mine.astype(low)).astype(full)
    grad_out = jnp.where(
        rank == 0,
        jnp.concatenate([out_mine, out_other], axis=0),
        jnp.concatenate([out_other, out_mine], axis=0),
    )
    qkv_mine = lax.psum_scatter(grad_qkv_part, "fsdp", scatter_dimension=0, tiled=True).astype(full)
    qkv_other = swap_ctx(qkv_mine.astype(low)).astype(full)
    q_mine = qkv_mine[:, :width_q].reshape(shard, my_heads, 1, head_dim)
    q_other = qkv_other[:, :width_q].reshape(shard, my_heads, 1, head_dim)
    grad_q_all = jnp.where(
        rank == 0,
        jnp.concatenate([q_mine, q_other], axis=2),
        jnp.concatenate([q_other, q_mine], axis=2),
    ).reshape(shard, 2 * width_q)
    grad_qkv = jnp.concatenate(
        [grad_q_all, qkv_mine[:, width_q:] + qkv_other[:, width_q:]], axis=1
    )
    early = sum_owned(jnp.concatenate([grad_router.T, grad_moe_gain[None]], axis=0), fsdp, spot)
    late = sum_all(
        jnp.concatenate(
            [
                grad_attn_gain.reshape(-1, head_dim),
                jnp.sum(gain_q_part, axis=0),
                jnp.sum(gain_k_part, axis=0),
            ],
            axis=0,
        ),
        fsdp,
    )
    gain_rows = width // head_dim
    return (
        output,
        grad_tokens,
        grad_qkv,
        grad_out,
        early[:experts_all].T,
        lax.dynamic_slice_in_dim(late[:gain_rows].reshape(-1), spot * shard, shard, 0),
        early[experts_all],
        late[gain_rows],
        late[gain_rows + 1],
        grad_gate_up,
        grad_down,
    )


gathered_bytes = 1 << 26


def choose_body(*args):
    tokens, gate_up = args[0], args[8]
    fsdp, ctx = lax.axis_size("fsdp"), lax.axis_size("ctx")
    fits = tokens.size * tokens.dtype.itemsize * fsdp * ctx <= gathered_bytes
    if fits and fsdp % 4 == 0 and ctx == 2 and fsdp & (fsdp - 1) == 0 and gate_up.shape[0] == 1:
        return body_gathered(*args)
    return body_routed(*args)


def solution(mesh):
    in_specs = (
        P(("fsdp", "ctx"), None),
        P("fsdp", None),
        P("fsdp", None),
        P("fsdp", None),
        P("fsdp"),
        P("fsdp"),
        P(),
        P(),
        P(("fsdp", "ctx"), None, None),
        P(("fsdp", "ctx"), None, None),
        P(("fsdp", "ctx"), None),
        P(("fsdp", "ctx"), None),
    )
    out_specs = (
        P(("fsdp", "ctx"), None),
        P(("fsdp", "ctx"), None),
        P("fsdp", None),
        P("fsdp", None),
        P("fsdp", None),
        P("fsdp"),
        P("fsdp"),
        P(),
        P(),
        P(("fsdp", "ctx"), None, None),
        P(("fsdp", "ctx"), None, None),
    )
    return jax.shard_map(choose_body, mesh=mesh, in_specs=in_specs, out_specs=out_specs, check_vma=False)
```

```python
import functools
import math

import jax
import jax.numpy as jnp
from jax import lax
from jax.experimental import pallas as pl
from jax.experimental.pallas import tpu as pltpu
from jax.sharding import PartitionSpec as P

eps_norm = 1e-06
theta_base = 1000000.0


def rms_scale(values, gain):
    return values * lax.rsqrt(jnp.mean(values * values, axis=-1, keepdims=True) + eps_norm) * gain


def rotate(values, cosine, sine):
    half_width = values.shape[-1] // 2
    turned = jnp.concatenate([-values[..., half_width:], values[..., :half_width]], axis=-1)
    return values * cosine + turned * sine


def angles(positions, width):
    freqs = theta_base ** (-(jnp.arange(width // 2, dtype=jnp.float32) * 2.0) / width)
    phase = positions.astype(jnp.float32)[:, None] * freqs[None, :]
    phase = jnp.concatenate([phase, phase], axis=-1)
    return (jnp.cos(phase)[:, None, :], jnp.sin(phase)[:, None, :])


def device_positions(block_rank, ctx_count, tok_rows):
    half_rows = tok_rows // 2
    within = jnp.arange(tok_rows, dtype=jnp.int32)
    span_id = jnp.where(within < half_rows, block_rank, 2 * ctx_count - 1 - block_rank)
    return span_id * half_rows + within % half_rows


def attend_head(query, keys_in, values_in, causal, scale_root):
    scores = (
        jnp.einsum("tgd,sd->gts", query, keys_in, preferred_element_type=jnp.float32) / scale_root
    )
    expo = jnp.where(causal[None], jnp.exp(scores), 0.0)
    totals = jnp.sum(expo, axis=-1, keepdims=True)
    probs = (expo / totals).astype(jnp.bfloat16)
    attended = jnp.einsum("gts,sd->tgd", probs, values_in, preferred_element_type=jnp.float32)
    return (attended, jnp.log(totals[..., 0]))


def attend_back(query, keys_in, values_in, causal, log_total, grad_attended, scale_root):
    scores = (
        jnp.einsum("tgd,sd->gts", query, keys_in, preferred_element_type=jnp.float32) / scale_root
    )
    probs = jnp.where(causal[None], jnp.exp(scores - log_total[..., None]), 0.0)
    low_probs = probs.astype(jnp.bfloat16)
    grad_values = jnp.einsum(
        "gts,tgd->sd", low_probs, grad_attended, preferred_element_type=jnp.float32
    )
    grad_probs = jnp.einsum(
        "tgd,sd->gts", grad_attended, values_in, preferred_element_type=jnp.float32
    )
    delta_rows = jnp.sum(grad_probs * probs, axis=-1, keepdims=True)
    grad_scores = (probs * (grad_probs - delta_rows)).astype(jnp.bfloat16)
    grad_query = (
        jnp.einsum("gts,sd->tgd", grad_scores, keys_in, preferred_element_type=jnp.float32)
        / scale_root
    )
    grad_keys = (
        jnp.einsum("gts,tgd->sd", grad_scores, query, preferred_element_type=jnp.float32)
        / scale_root
    )
    return (grad_query, grad_keys, grad_values)


def swiglu(paired):
    half_width = paired.shape[-1] // 2
    return jax.nn.silu(paired[..., :half_width]) * paired[..., half_width:]


def gating(selected):
    expo = jnp.exp(selected)
    return expo / jnp.sum(expo, axis=1, keepdims=True)


def body_routed(
    tokens,
    qkv_weight,
    out_weight,
    router_weight,
    attn_gain,
    moe_gain,
    query_gain,
    key_gain,
    expert_gate_up,
    expert_down,
    routes,
    cotangent,
):
    rows_dev, width = tokens.shape
    head_dim = query_gain.shape[0]
    top_k = routes.shape[1]
    ctx_count = lax.axis_size("ctx")
    ctx_rank = lax.axis_index("ctx")
    qkv_all, out_all, router_all, attn_all, moe_all = (
        lax.all_gather(qkv_weight, "fsdp", axis=0, tiled=True),
        lax.all_gather(out_weight, "fsdp", axis=0, tiled=True),
        lax.all_gather(router_weight, "fsdp", axis=0, tiled=True),
        lax.all_gather(attn_gain, "fsdp", axis=0, tiled=True),
        lax.all_gather(moe_gain, "fsdp", axis=0, tiled=True),
    )
    experts_all = router_all.shape[1]
    heads = out_all.shape[0] // head_dim
    kv_heads = (qkv_all.shape[1] // head_dim - heads) // 2
    group_size = heads // kv_heads
    capacity = 2 * rows_dev * top_k // experts_all
    width_q = heads * head_dim
    width_k = kv_heads * head_dim
    scale_root = math.sqrt(head_dim)
    inputs = tokens.astype(jnp.float32)
    normed_in = rms_scale(inputs, attn_all.astype(jnp.float32))
    low_in = normed_in.astype(jnp.bfloat16)
    projected = jnp.dot(low_in, qkv_all, preferred_element_type=jnp.float32)
    query_raw = projected[:, :width_q].reshape(rows_dev, heads, head_dim)
    key_raw = projected[:, width_q : width_q + width_k].reshape(rows_dev, kv_heads, head_dim)
    value_low = (
        projected[:, width_q + width_k :].astype(jnp.bfloat16).reshape(rows_dev, kv_heads, head_dim)
    )
    positions = device_positions(ctx_rank, ctx_count, rows_dev)
    cosine, sine = angles(positions, head_dim)
    query_gain_f = query_gain.astype(jnp.float32)
    key_gain_f = key_gain.astype(jnp.float32)

    def query_rope(values_in, gain):
        return rotate(rms_scale(values_in, gain), cosine, sine)

    query_low = query_rope(query_raw, query_gain_f).astype(jnp.bfloat16)
    key_low = query_rope(key_raw, key_gain_f).astype(jnp.bfloat16)
    keys_all, values_all = (
        lax.all_gather(key_low, "ctx", axis=0, tiled=True),
        lax.all_gather(value_low, "ctx", axis=0, tiled=True),
    )
    key_pos = jnp.concatenate(
        [device_positions(other, ctx_count, rows_dev) for other in range(ctx_count)]
    )
    causal = key_pos[None, :] <= positions[:, None]
    query_heads = query_low.reshape(rows_dev, kv_heads, group_size, head_dim).transpose(1, 0, 2, 3)
    key_heads = keys_all.transpose(1, 0, 2)
    value_heads = values_all.transpose(1, 0, 2)
    attended, log_total = lax.map(
        lambda member: attend_head(member[0], member[1], member[2], causal, scale_root),
        (query_heads, key_heads, value_heads),
    )
    attended_low = attended.transpose(1, 0, 2, 3).reshape(rows_dev, width_q).astype(jnp.bfloat16)
    mixed = inputs + jnp.dot(attended_low, out_all, preferred_element_type=jnp.float32)
    normed_mid = rms_scale(mixed, moe_all.astype(jnp.float32))
    low_mid = normed_mid.astype(jnp.bfloat16)
    logits = jnp.dot(low_mid, router_all, preferred_element_type=jnp.float32)
    selected = jnp.take_along_axis(logits, routes, axis=1)
    gates, gate_back = jax.vjp(gating, selected)
    flat_routes = routes.reshape(-1)
    expert_ids = jnp.arange(experts_all, dtype=jnp.int32)
    hit_table = (flat_routes[:, None] == expert_ids[None, :]).astype(jnp.int32)
    slot_index = jnp.sum(jnp.cumsum(hit_table, axis=0) * hit_table, axis=1) - 1
    target = flat_routes * capacity + slot_index
    pair_count = rows_dev * top_k
    source_pair = (
        jnp.full((experts_all * capacity,), pair_count, jnp.int32)
        .at[target]
        .set(jnp.arange(pair_count, dtype=jnp.int32))
    )
    padded = jnp.concatenate([low_mid, jnp.zeros((1, width), jnp.bfloat16)], axis=0)
    outgoing = padded[source_pair // top_k].reshape(experts_all, capacity, width)
    received = lax.all_to_all(outgoing, ("fsdp", "ctx"), split_axis=0, concat_axis=1, tiled=True)
    gate_and_up = jnp.einsum(
        "esd,edf->esf", received, expert_gate_up, preferred_element_type=jnp.float32
    )
    hidden_val, swiglu_back = jax.vjp(swiglu, gate_and_up)
    hidden_low = hidden_val.astype(jnp.bfloat16)
    result_low = jnp.einsum(
        "esf,efd->esd", hidden_low, expert_down, preferred_element_type=jnp.float32
    ).astype(jnp.bfloat16)
    returned = lax.all_to_all(
        result_low, ("fsdp", "ctx"), split_axis=1, concat_axis=0, tiled=True
    ).reshape(experts_all * capacity, width)
    picked = returned[target].reshape(rows_dev, top_k, width).astype(jnp.float32)
    output = (mixed + jnp.sum(gates[:, :, None] * picked, axis=1)).astype(jnp.bfloat16)
    qkv_back, out_back, router_back, attn_back_g, moe_back_g = (
        qkv_all,
        out_all,
        router_all,
        attn_all,
        moe_all,
    )
    grad_final = cotangent.astype(jnp.float32)
    grad_gates = jnp.sum(grad_final[:, None, :] * picked, axis=2)
    grad_result = (
        (gates[:, :, None] * grad_final[:, None, :]).astype(jnp.bfloat16).reshape(pair_count, width)
    )
    grad_padded = jnp.concatenate([grad_result, jnp.zeros((1, width), jnp.bfloat16)], axis=0)
    grad_outgoing = grad_padded[source_pair].reshape(experts_all, capacity, width)
    grad_received = lax.all_to_all(
        grad_outgoing, ("fsdp", "ctx"), split_axis=0, concat_axis=1, tiled=True
    )
    grad_down = jnp.einsum(
        "esf,esd->efd", hidden_low, grad_received, preferred_element_type=jnp.float32
    )
    grad_hidden = jnp.einsum(
        "esd,efd->esf", grad_received, expert_down, preferred_element_type=jnp.float32
    )
    grad_paired = swiglu_back(grad_hidden)[0].astype(jnp.bfloat16)
    grad_gate_up = jnp.einsum(
        "esd,esf->edf", received, grad_paired, preferred_element_type=jnp.float32
    )
    grad_rows = jnp.einsum(
        "esf,edf->esd", grad_paired, expert_gate_up, preferred_element_type=jnp.float32
    ).astype(jnp.bfloat16)
    grad_returned = lax.all_to_all(
        grad_rows, ("fsdp", "ctx"), split_axis=1, concat_axis=0, tiled=True
    ).reshape(experts_all * capacity, width)
    grad_mid = jnp.sum(
        grad_returned[target].reshape(rows_dev, top_k, width).astype(jnp.float32), axis=1
    )
    grad_selected = gate_back(grad_gates)[0]
    route_table = (routes[:, :, None] == expert_ids[None, None, :]).astype(jnp.float32)
    grad_logits = jnp.sum(route_table * grad_selected[:, :, None], axis=1).astype(jnp.bfloat16)
    grad_router = jnp.dot(low_mid.T, grad_logits, preferred_element_type=jnp.float32)
    grad_mid = grad_mid + jnp.dot(grad_logits, router_back.T, preferred_element_type=jnp.float32)
    unused_mid, mid_back = jax.vjp(rms_scale, mixed, moe_back_g.astype(jnp.float32))
    grad_mixed_part, grad_moe_gain = mid_back(grad_mid)
    grad_mixed = grad_final + grad_mixed_part
    grad_branch = grad_mixed.astype(jnp.bfloat16)
    grad_out = jnp.dot(attended_low.T, grad_branch, preferred_element_type=jnp.float32)
    grad_attended = jnp.dot(grad_branch, out_back.T, preferred_element_type=jnp.float32).astype(
        jnp.bfloat16
    )
    grad_heads = grad_attended.reshape(rows_dev, kv_heads, group_size, head_dim).transpose(
        1, 0, 2, 3
    )
    grad_query_h, grad_key_h, grad_value_h = lax.map(
        lambda member: attend_back(
            member[0], member[1], member[2], causal, member[3], member[4], scale_root
        ),
        (query_heads, key_heads, value_heads, log_total, grad_heads),
    )
    grad_keys, grad_values = (
        lax.psum_scatter(
            grad_key_h.transpose(1, 0, 2).astype(jnp.bfloat16),
            "ctx",
            scatter_dimension=0,
            tiled=True,
        ).astype(jnp.float32),
        lax.psum_scatter(
            grad_value_h.transpose(1, 0, 2).astype(jnp.bfloat16),
            "ctx",
            scatter_dimension=0,
            tiled=True,
        ).astype(jnp.float32),
    )
    grad_query_rot = (
        grad_query_h.transpose(1, 0, 2, 3).reshape(rows_dev, heads, head_dim).astype(jnp.bfloat16)
    )
    grad_query_rot = lax.optimization_barrier(grad_query_rot).astype(jnp.float32)
    grad_key_rot = lax.optimization_barrier(grad_keys.astype(jnp.bfloat16)).astype(jnp.float32)
    unused_query, query_back = jax.vjp(query_rope, query_raw, query_gain_f)
    grad_query_raw, grad_query_gain = query_back(grad_query_rot)
    unused_key, key_back = jax.vjp(query_rope, key_raw, key_gain_f)
    grad_key_raw, grad_key_gain = key_back(grad_key_rot)
    grad_projected = jnp.concatenate(
        [
            grad_query_raw.reshape(rows_dev, width_q).astype(jnp.bfloat16),
            grad_key_raw.reshape(rows_dev, width_k).astype(jnp.bfloat16),
            grad_values.reshape(rows_dev, width_k).astype(jnp.bfloat16),
        ],
        axis=1,
    )
    grad_qkv = jnp.dot(low_in.T, grad_projected, preferred_element_type=jnp.float32)
    grad_normed = jnp.dot(grad_projected, qkv_back.T, preferred_element_type=jnp.float32)
    unused_in, in_back = jax.vjp(rms_scale, inputs, attn_back_g.astype(jnp.float32))
    grad_in_part, grad_attn_gain = in_back(grad_normed)
    grad_tokens = grad_mixed + grad_in_part
    gradients = (grad_qkv, grad_out, grad_router, grad_attn_gain, grad_moe_gain)
    pieces = (
        lax.psum_scatter(gradients[0], "fsdp", scatter_dimension=0, tiled=True),
        lax.psum_scatter(gradients[1], "fsdp", scatter_dimension=0, tiled=True),
        lax.psum_scatter(gradients[2], "fsdp", scatter_dimension=0, tiled=True),
        lax.psum_scatter(gradients[3], "fsdp", scatter_dimension=0, tiled=True),
        lax.psum_scatter(gradients[4], "fsdp", scatter_dimension=0, tiled=True),
    )
    reduced = (
        lax.psum(pieces[0].astype(jnp.bfloat16), "ctx").astype(jnp.float32),
        lax.psum(pieces[1].astype(jnp.bfloat16), "ctx").astype(jnp.float32),
        lax.psum(pieces[2].astype(jnp.bfloat16), "ctx").astype(jnp.float32),
        lax.psum(pieces[3].astype(jnp.bfloat16), "ctx").astype(jnp.float32),
        lax.psum(pieces[4].astype(jnp.bfloat16), "ctx").astype(jnp.float32),
    )
    gain_sums = lax.psum((grad_query_gain, grad_key_gain), ("fsdp", "ctx"))
    return (
        output,
        grad_tokens,
        reduced[0],
        reduced[1],
        reduced[2],
        reduced[3],
        reduced[4],
        gain_sums[0],
        gain_sums[1],
        grad_gate_up,
        grad_down,
    )


low = jnp.bfloat16
full = jnp.float32
plain = (((1,), (0,)), ((), ()))
rhs_turned = (((1,), (1,)), ((), ()))
lhs_turned = (((0,), (0,)), ((), ()))
vmem_bytes = 58 << 20


def mul(left, right, dims=plain):
    return lax.dot_general(left, right, dims, preferred_element_type=full)


def core_pairs(fsdp):
    return [(i, i ^ 1) for i in range(fsdp)]


def side_pairs(fsdp):
    return [(i, i ^ 2) for i in range(fsdp)]


def swap_core(values):
    return lax.ppermute(values, "fsdp", core_pairs(lax.axis_size("fsdp")))


def swap_side(values):
    return lax.ppermute(values, "fsdp", side_pairs(lax.axis_size("fsdp")))


def swap_ctx(values):
    return lax.ppermute(values, "ctx", [(0, 1), (1, 0)])


def add_low(one, two):
    return (one.astype(full) + two.astype(full)).astype(low)


def hold(values, first):
    return lax.optimization_barrier((values, first))


def take(values, index):
    return lax.dynamic_index_in_dim(values, index, 0, keepdims=False)


def line_shift(values, step):
    fsdp = lax.axis_size("fsdp")
    return lax.ppermute(values, "fsdp", [(i, (i + 4 * step) % fsdp) for i in range(fsdp)])


def line_total(own, arrived):
    total = own.astype(full)
    for item in arrived.values():
        total = total + item.astype(full)
    return total


def line_sum(entries, count):
    return line_total(entries[0], {s: line_shift(entries[s], count - s) for s in range(1, count)})


def joined(places, own, got):
    from_ctx, from_side, one_side, two_ctx = got
    entries = {}
    for at, p in enumerate(places):
        one = add_low(add_low(own[0][at], from_ctx[at]), one_side[at])
        two = add_low(add_low(own[1][at], from_side[at]), two_ctx[at])
        entries[p] = jnp.concatenate([one, two], axis=-1)
    return entries


def over_core(keep, send):
    return keep, swap_core(send)


def pick_sum(parts, start, stop, column):
    keep, other = parts
    half = keep.shape[-1] // 2
    cut = (slice(start, stop), slice(None), slice(column * half, (column + 1) * half))
    return add_low(keep[cut], other[cut])


def sum_all(values, fsdp):
    values = values + lax.ppermute(values, "fsdp", core_pairs(fsdp))
    values = values + swap_ctx(values)
    step = 2
    while step < fsdp:
        values = values + lax.ppermute(values, "fsdp", [(i, i ^ step) for i in range(fsdp)])
        step *= 2
    return values


def sum_owned(values, fsdp, spot):
    items, shard = values.shape[0], values.shape[1] // fsdp
    values = values.reshape(items, fsdp, shard).swapaxes(0, 1)
    step = fsdp // 2
    while step:
        bit = (spot // step) % 2
        values = values.reshape(2, step, items, shard)
        other = lax.ppermute(take(values, 1 - bit), "fsdp", [(i, i ^ step) for i in range(fsdp)])
        values = take(values, bit) + other
        step //= 2
    values = values[0]
    return values + swap_ctx(values)


def turn(values):
    return pltpu.roll(values, values.shape[-1] // 2, 1)


def norm_rope(raw, gain, cosine, sine):
    scale = lax.rsqrt(jnp.mean(raw * raw, axis=-1, keepdims=True) + eps_norm)
    scaled = raw * scale * gain
    return scaled * cosine + turn(scaled) * sine


def norm_rope_back(raw, gain, cosine, sine, grad):
    scale = lax.rsqrt(jnp.mean(raw * raw, axis=-1, keepdims=True) + eps_norm)
    unit = raw * scale
    grad_scaled = grad * cosine - turn(grad) * sine
    grad_gain = jnp.sum(grad_scaled * unit, axis=0, keepdims=True)
    grad_unit = grad_scaled * gain
    grad_raw = scale * (grad_unit - unit * jnp.mean(grad_unit * unit, axis=-1, keepdims=True))
    return grad_raw, grad_gain


def tiles_of(rows):
    step = rows // 2
    return [(start, start + step) for start in range(0, rows, step)]


def allowed(start, stop):
    shape = (stop - start, stop)
    return lax.broadcasted_iota(jnp.int32, shape, 1) <= (
        lax.broadcasted_iota(jnp.int32, shape, 0) + start
    )


def attend_kernel(q_ref, k_ref, v_ref, cos_ref, sin_ref, qg_ref, kg_ref, o_ref, qr_ref, kr_ref, vl_ref):
    head_dim = k_ref.shape[1]
    rows = k_ref.shape[0]
    cosine, sine = cos_ref[...], sin_ref[...]
    keys = norm_rope(k_ref[...], kg_ref[...], cosine, sine).astype(low)
    values = v_ref[...].astype(low)
    kr_ref[...] = keys
    vl_ref[...] = values
    for head in range(q_ref.shape[1] // head_dim):
        cols = slice(head * head_dim, (head + 1) * head_dim)
        query = norm_rope(q_ref[:, cols], qg_ref[...], cosine, sine).astype(low)
        qr_ref[:, cols] = query
        for start, stop in tiles_of(rows):
            scores = mul(query[start:stop], keys[:stop], rhs_turned) * (1.0 / math.sqrt(head_dim))
            expo = jnp.where(allowed(start, stop), jnp.exp(scores), 0.0)
            probs = (expo / jnp.sum(expo, axis=-1, keepdims=True)).astype(low)
            o_ref[start:stop, cols] = mul(probs, values[:stop]).astype(low)


def attend_grad_kernel(
    q_ref, k_ref, qr_ref, kr_ref, vl_ref, go_ref, cos_ref, sin_ref, qg_ref, kg_ref,
    dq_ref, dk_ref, dv_ref, dqg_ref, dkg_ref, dk_sum, dv_sum, dq_sum,
):
    head_dim = k_ref.shape[1]
    rows = k_ref.shape[0]
    root = 1.0 / math.sqrt(head_dim)
    cosine, sine = cos_ref[...], sin_ref[...]
    keys, values = kr_ref[...], vl_ref[...]
    gain_sum = jnp.zeros((1, head_dim), full)
    dk_sum[...] = jnp.zeros_like(dk_sum)
    dv_sum[...] = jnp.zeros_like(dv_sum)
    for head in range(q_ref.shape[1] // head_dim):
        cols = slice(head * head_dim, (head + 1) * head_dim)
        for start, stop in tiles_of(rows):
            query = qr_ref[start:stop, cols]
            grad = go_ref[start:stop, cols]
            scores = mul(query, keys[:stop], rhs_turned) * root
            expo = jnp.where(allowed(start, stop), jnp.exp(scores), 0.0)
            probs = expo / jnp.sum(expo, axis=-1, keepdims=True)
            grad_probs = mul(grad, values[:stop], rhs_turned)
            delta = jnp.sum(grad_probs * probs, axis=-1, keepdims=True)
            grad_scores = (probs * (grad_probs - delta)).astype(low)
            dv_sum[:stop] += mul(probs.astype(low), grad, lhs_turned)
            dk_sum[:stop] += mul(grad_scores, query, lhs_turned)
            dq_sum[start:stop] = mul(grad_scores, keys[:stop])
        grad_query = (dq_sum[...] * root).astype(low).astype(full)
        grad_raw, grad_gain = norm_rope_back(q_ref[:, cols], qg_ref[...], cosine, sine, grad_query)
        dq_ref[:, cols] = grad_raw.astype(low)
        gain_sum = gain_sum + grad_gain
    dqg_ref[0] = gain_sum
    grad_key = (dk_sum[...] * root).astype(low).astype(full)
    grad_raw, grad_gain = norm_rope_back(k_ref[...], kg_ref[...], cosine, sine, grad_key)
    dk_ref[...] = grad_raw.astype(low)
    dkg_ref[0] = grad_gain
    dv_ref[...] = dv_sum[...].astype(low)


def attention_specs(rows, head_dim, kv_heads, group):
    wide, narrow = group * head_dim, head_dim
    heads_end = kv_heads * group
    return dict(
        q=pl.BlockSpec((rows, wide), lambda i: (0, i)),
        k=pl.BlockSpec((rows, narrow), lambda i: (0, heads_end + i)),
        v=pl.BlockSpec((rows, narrow), lambda i: (0, heads_end + kv_heads + i)),
        own=pl.BlockSpec((rows, narrow), lambda i: (0, i)),
        table=pl.BlockSpec((rows, head_dim), lambda i: (0, 0)),
        gain=pl.BlockSpec((1, head_dim), lambda i: (0, 0)),
        gain_out=pl.BlockSpec((1, 1, head_dim), lambda i: (i, 0, 0)),
    )


def attend(projected, cosine, sine, query_gain, key_gain, kv_heads, group):
    rows, head_dim = cosine.shape
    s = attention_specs(rows, head_dim, kv_heads, group)
    shape = jax.ShapeDtypeStruct
    work = rows * rows * head_dim * kv_heads * group
    return pl.pallas_call(
        attend_kernel,
        grid=(kv_heads,),
        in_specs=[s["q"], s["k"], s["v"], s["table"], s["table"], s["gain"], s["gain"]],
        out_specs=[s["q"], s["q"], s["own"], s["own"]],
        out_shape=[
            shape((rows, kv_heads * group * head_dim), low),
            shape((rows, kv_heads * group * head_dim), low),
            shape((rows, kv_heads * head_dim), low),
            shape((rows, kv_heads * head_dim), low),
        ],
        compiler_params=pltpu.CompilerParams(vmem_limit_bytes=48 << 20),
        cost_estimate=pl.CostEstimate(
            flops=4 * work, bytes_accessed=projected.size * 6, transcendentals=work // head_dim
        ),
        name="attend",
    )(projected, projected, projected, cosine, sine, query_gain, key_gain)


def attend_grad(projected, roped_q, roped_k, values_low, grad, cosine, sine, query_gain, key_gain, kv_heads, group):
    rows, head_dim = cosine.shape
    s = attention_specs(rows, head_dim, kv_heads, group)
    shape = jax.ShapeDtypeStruct
    work = rows * rows * head_dim * kv_heads * group
    return pl.pallas_call(
        attend_grad_kernel,
        grid=(kv_heads,),
        in_specs=[
            s["q"], s["k"], s["q"], s["own"], s["own"], s["q"],
            s["table"], s["table"], s["gain"], s["gain"],
        ],
        out_specs=[s["q"], s["own"], s["own"], s["gain_out"], s["gain_out"]],
        out_shape=[
            shape((rows, kv_heads * group * head_dim), low),
            shape((rows, kv_heads * head_dim), low),
            shape((rows, kv_heads * head_dim), low),
            shape((kv_heads, 1, head_dim), full),
            shape((kv_heads, 1, head_dim), full),
        ],
        scratch_shapes=[pltpu.VMEM((rows, head_dim), full)] * 3,
        compiler_params=pltpu.CompilerParams(vmem_limit_bytes=48 << 20),
        cost_estimate=pl.CostEstimate(
            flops=10 * work, bytes_accessed=projected.size * 10, transcendentals=work // head_dim
        ),
        name="attend_grad",
    )(projected, projected, roped_q, roped_k, values_low, grad, cosine, sine, query_gain, key_gain)


def expert_kernel(core_ref, order, m_ref, near_ref, far_ref, g_ref, w_ref, gu_ref, dn_ref, *refs):
    (keep_out, send_out, keep_back, send_back, gate_back, rows_ref, dy_ref, z_ref, pair_ref) = refs[-9:]
    core = core_ref[0]
    far = order[5 * pl.program_id(0) + 2] == 1
    block = m_ref.shape[3]
    hidden = dn_ref.shape[0]
    slots = z_ref.shape[0] // 2
    shape = (block, block)
    earlier = (
        lax.broadcasted_iota(jnp.int32, shape, 0) < lax.broadcasted_iota(jnp.int32, shape, 1)
    ).astype(low)
    slot_ids = lax.broadcasted_iota(jnp.int32, (slots, block), 0)
    places, picks, weights, rows, grads = [], [], [], [], []
    for part in range(2):
        at = lax.rem(core + part, 2)
        gate = w_ref[0, at, 0]
        hit = jnp.where(gate >= 0.0, 1.0, 0.0)
        ones = jnp.broadcast_to(hit, (8, block)).astype(low)
        count = mul(ones, earlier)[:1].astype(jnp.int32)
        place = (slot_ids == count) & (hit > 0.5)
        pick = place.astype(full).astype(low)
        places.append(place)
        picks.append(pick)
        weights.append(jnp.sum(jnp.where(place, gate, 0.0), axis=1, keepdims=True))
        rows.append(mul(pick, m_ref[0, at, 0]).astype(low))
        grads.append(
            jnp.concatenate(
                [
                    mul(pick, jnp.where(far, far_ref[0, at, 0], near_ref[0, at, 0])),
                    mul(pick, g_ref[0, at, 0]),
                ],
                axis=1,
            )
        )
    row, grad, weight = (jnp.concatenate(items, axis=0) for items in (rows, grads, weights))
    rows_ref[...] = row
    paired = mul(row, gu_ref[...])
    gate_in, up = paired[:, :hidden], paired[:, hidden:]
    sig = jax.nn.sigmoid(gate_in)
    act = gate_in * sig
    z = (act * up).astype(low)
    z_ref[...] = z
    y = mul(z, dn_ref[...]).astype(low).astype(full)
    grad_gate = jnp.sum(grad * y, axis=1, keepdims=True)
    y_scaled = (weight * y).astype(low)
    dy = (weight * grad).astype(low)
    dy_ref[...] = dy
    for part, out in enumerate((keep_out, send_out)):
        mine = slice(part * slots, (part + 1) * slots)
        out[0] = mul(picks[part], y_scaled[mine], lhs_turned).astype(low)
        gate_back[0, lax.rem(core + part, 2), 0] = jnp.sum(
            jnp.where(places[part], grad_gate[mine], 0.0), axis=0, keepdims=True
        )
    dz = mul(dy, dn_ref[...], rhs_turned)
    grad_in = dz * up * (sig * (1.0 + gate_in * (1.0 - sig)))
    pair = jnp.concatenate([grad_in, dz * act], axis=1).astype(low)
    pair_ref[...] = pair
    back = mul(pair, gu_ref[...], rhs_turned).astype(low)
    for part, out in enumerate((keep_back, send_back)):
        mine = slice(part * slots, (part + 1) * slots)
        out[0] = mul(picks[part], back[mine], lhs_turned).astype(low)


def run_expert(core, order, first, total_steps, m_all, g_all, g_far, gates_all, gate_up, down, slots, kept):
    places, _, _, block, width = m_all.shape
    paired = gate_up.shape[1]
    steps = order.shape[0] // 5
    part_rows = steps * 2 * slots
    hidden = paired // 2
    shape = jax.ShapeDtypeStruct

    def gates_at(i, core, order):
        return (order[5 * i], 0, order[5 * i + 1], 0, 0)

    def token_at(i, core, order):
        return (order[5 * i], 0, order[5 * i + 2], 0, 0)

    def half_at(i, core, order):
        return (order[5 * i], 0, 1 + order[5 * i + 2], 0, 0)

    def near_at(i, core, order):
        return (order[5 * i + 3], 0, 0, 0, 0)

    def far_at(i, core, order):
        return (order[5 * i + 4], 0, 0, 0, 0)

    def fixed(i, core, order):
        return (0, 0)

    def flat(i, core, order):
        return (first + i, 0)

    def stacked(i, core, order):
        return (i, 0, 0)

    small = pl.BlockSpec((1, 2, 1, 1, block), gates_at)
    one_block = pl.BlockSpec((1, block, width), stacked)
    half_block = (1, 2, 1, block, width // 2)
    widths = (width, width, hidden, paired)
    grid_spec = pltpu.PrefetchScalarGridSpec(
        num_scalar_prefetch=2,
        grid=(steps,),
        in_specs=[
            pl.BlockSpec((1, 2, 1, block, width), token_at),
            pl.BlockSpec(half_block, near_at),
            pl.BlockSpec(half_block, far_at),
            pl.BlockSpec(half_block, half_at),
            small,
            pl.BlockSpec(gate_up.shape, fixed, pipeline_mode=pl.Buffered(1)),
            pl.BlockSpec(down.shape, fixed, pipeline_mode=pl.Buffered(1)),
        ]
        + [pl.BlockSpec(memory_space=pl.ANY)] * (0 if kept is None else 5),
        out_specs=[one_block] * 4 + [small] + [pl.BlockSpec((2 * slots, n), flat) for n in widths],
    )
    return pl.pallas_call(
        expert_kernel,
        grid_spec=grid_spec,
        out_shape=[shape((steps, block, width), low)] * 4
        + [shape((places, 2, 2, 1, block), full)]
        + [shape((total_steps * 2 * slots, n), low) for n in widths],
        input_output_aliases={} if kept is None else {9 + i: 4 + i for i in range(5)},
        compiler_params=pltpu.CompilerParams(vmem_limit_bytes=vmem_bytes),
        cost_estimate=pl.CostEstimate(
            flops=part_rows * width * (4 * paired + 4 * hidden + 8 * block),
            bytes_accessed=steps * block * width * 16 + part_rows * (width * 4 + paired * 3),
            transcendentals=part_rows * hidden,
        ),
        name="experts",
    )(core, order, m_all, g_all, g_far, g_all, gates_all, gate_up, down, *(() if kept is None else kept))


def rms_back(values, gain, grad):
    scale = lax.rsqrt(jnp.mean(values * values, axis=-1, keepdims=True) + eps_norm)
    unit = values * scale
    grad_gain = jnp.sum(grad * unit, axis=0)
    grad_unit = grad * gain
    back = scale * (grad_unit - unit * jnp.mean(grad_unit * unit, axis=-1, keepdims=True))
    return back, grad_gain


def in_order(first, second):
    half = first.shape[0] // 2
    return jnp.concatenate([first[:half], second, first[half:]], axis=0)


def of_block(values, rank):
    quarter = values.shape[0] // 4
    outer = jnp.concatenate([values[:quarter], values[3 * quarter :]], axis=0)
    return jnp.where(rank == 0, outer, values[quarter : 3 * quarter])


def body_gathered(
    tokens, qkv_weight, out_weight, router_weight, attn_gain, moe_gain, query_gain, key_gain,
    expert_gate_up, expert_down, routes, cotangent,
):
    rows_dev, width = tokens.shape
    head_dim = query_gain.shape[0]
    top_k = routes.shape[1]
    fsdp = lax.axis_size("fsdp")
    spot = lax.axis_index("fsdp")
    rank = lax.axis_index("ctx")
    place, side, core = spot // 4, (spot // 2) % 2, spot % 2
    shard = qkv_weight.shape[0]
    heads = out_weight.shape[0] * fsdp // head_dim
    kv_heads = (qkv_weight.shape[1] // head_dim - heads) // 2
    group = heads // kv_heads // 2
    my_heads = heads // 2
    width_q, width_k = my_heads * head_dim, kv_heads * head_dim
    experts_all = router_weight.shape[1]
    capacity = 2 * rows_dev * top_k // experts_all
    both = ("fsdp", "ctx")

    def sequence(values):
        other = swap_ctx(values)
        first = jnp.where(rank == 0, values, other)
        second = jnp.where(rank == 0, other, values)
        return in_order(first, second)

    by_parity = qkv_weight[:, : 2 * width_q].reshape(shard, my_heads, 2, head_dim)
    q_local = jnp.where(rank == 0, by_parity[:, :, 0], by_parity[:, :, 1]).reshape(shard, width_q)
    out_local = lax.dynamic_slice_in_dim(out_weight, rank * head_dim, head_dim, 0)
    weights_local = jnp.concatenate([q_local, qkv_weight[:, 2 * width_q :], out_local], axis=1)
    small_local = jnp.concatenate([router_weight, attn_gain[:, None], moe_gain[:, None]], axis=1)
    small_all = lax.all_gather(small_local, "fsdp", axis=0, tiled=True)
    weights_all = lax.all_gather(weights_local, "fsdp", axis=0, tiled=True)
    qkv_all = weights_all[:, : width_q + 2 * width_k]
    out_all = weights_all[:, width_q + 2 * width_k :]
    router_all = small_all[:, :experts_all]
    attn_all = small_all[:, experts_all].astype(full)
    moe_all = small_all[:, experts_all + 1].astype(full)
    g_half = width // 2
    g_local = jnp.stack(
        [cotangent[:, :g_half], cotangent[:, g_half:], swap_ctx(cotangent[:, g_half:])]
    )
    g_all = lax.all_gather(
        g_local.reshape(3 * rows_dev, g_half), "fsdp", axis=0, tiled=True
    ).reshape(fsdp // 2, 2, 3, rows_dev, g_half)

    sequence_in = sequence(tokens).astype(full)
    low_in = rms_scale(sequence_in, attn_all).astype(low)
    projected = mul(low_in, qkv_all)
    cosine, sine = (t[:, 0] for t in angles(jnp.arange(2 * rows_dev, dtype=jnp.int32), head_dim))
    sine = jnp.concatenate([-sine[:, : head_dim // 2], sine[:, head_dim // 2 :]], axis=1)
    gain_q, gain_k = query_gain.astype(full)[None], key_gain.astype(full)[None]
    attended, roped_q, roped_k, values_low = attend(
        projected, cosine, sine, gain_q, gain_k, kv_heads, group
    )
    branch = mul(attended, out_all)
    inputs = tokens.astype(full)
    mixed = (
        inputs
        + of_block(branch, rank)
        + swap_ctx(of_block(branch, 1 - rank).astype(low)).astype(full)
    )
    low_mid = rms_scale(mixed, moe_all).astype(low)
    m_all = lax.all_gather(jnp.concatenate([low_mid, swap_ctx(low_mid)]), "fsdp", axis=0, tiled=True)

    logits = mul(low_mid, router_all)
    named = routes[:, :, None] == jnp.arange(experts_all, dtype=jnp.int32)[None, None, :]
    selected = jnp.sum(jnp.where(named, logits[:, None, :], 0.0), axis=2)
    gates = gating(selected)
    chosen = jnp.any(named, axis=1)
    gates_wide = jnp.sum(jnp.where(named, gates[:, :, None], 0.0), axis=1)
    gates_sent = jnp.where(chosen, gates_wide, -1.0).T
    gates_all = lax.all_to_all(gates_sent, both, split_axis=0, concat_axis=0, tiled=True)

    g_all, gates_all = hold(g_all, gates_all)
    g_far = swap_ctx(g_all[:, :, :1])

    lines = fsdp // 4
    places = list(range(1, lines)) + [0]
    cut = lines // 2
    parts = [places[:cut], places[cut:]]
    m_all = m_all.reshape(fsdp // 2, 2, 2, rows_dev, width)
    gates_all = gates_all.reshape(fsdp // 2, 2, 2, 1, rows_dev)
    state = dict(kept=None, first=0, core=core[None].astype(jnp.int32))

    def call(steps, raw=False):
        spots = [((place - p) % lines) * 2 + (side + d) % 2 for d, _, p in steps]
        near = [i for i, step in enumerate(steps) if step[1] == 0] or [0]
        far = [i for i, step in enumerate(steps) if step[1] == 1] or [0]

        def nearest(i, among):
            return spots[min(among, key=lambda j: abs(j - i))]

        order = [
            item
            for i, step in enumerate(steps)
            for item in (spots[i], (rank + step[1]) % 2, step[1], nearest(i, near), nearest(i, far))
        ]
        keep_out, send_out, keep_back, send_back, *kept = run_expert(
            state["core"],
            jnp.stack([jnp.asarray(item, jnp.int32) for item in order]),
            state["first"],
            4 * lines,
            m_all,
            g_all,
            g_far,
            gates_all,
            expert_gate_up[0],
            expert_down[0],
            capacity,
            state["kept"],
        )
        state["kept"] = kept
        state["first"] += len(steps)
        back = (keep_back, send_back)
        return back if raw else over_core(*back), (keep_out, send_out)

    def wait(first):
        state["core"], first = hold(state["core"], first)
        return first

    back, out_far = call([(1, 1, p) for p in places])
    far_one, far_two = wait([pick_sum(back, 0, lines, column) for column in range(2)])
    far_one, far_two = swap_ctx(far_one), swap_side(far_two)

    def mixed_call(part, raw=False):
        return call([(1, 0, p) for p in parts[part]] + [(0, 1, p) for p in parts[part]], raw)

    def mixed_sums(back):
        return [pick_sum(back, start, start + cut, column) for start in (0, cut) for column in range(2)]

    def rounds(sums, part):
        side_one, side_two, ctx_one, ctx_two = sums
        span = slice(part * cut, (part + 1) * cut)
        return [
            swap_ctx(ctx_one),
            swap_side(side_two),
            swap_side(add_low(side_one, far_one[span])),
            swap_ctx(add_low(ctx_two, far_two[span])),
        ]

    (keep, send), out_first = mixed_call(0, raw=True)
    send, (far_one, far_two) = hold(send, (far_one, far_two))
    back = over_core(keep, send)
    back_own, out_own = call([(0, 0, p) for p in places])
    sums = wait(mixed_sums(back))
    back_own = [pick_sum(back_own, 0, lines, column) for column in range(2)]
    got = rounds(sums, 0)
    (keep, send), out_second = mixed_call(1, raw=True)
    send, got = hold(send, got)
    back = over_core(keep, send)
    entries = joined(parts[0], [item[:cut] for item in back_own], got)
    arrived = {p: line_shift(entries[p], lines - p) for p in parts[0]}
    got = rounds(mixed_sums(back), 1)
    gate_back, rows, grad_rows, hidden, grad_pair = state["kept"]
    grad_gates = lax.all_to_all(
        gate_back.reshape(fsdp * 2, rows_dev), both, split_axis=0, concat_axis=0, tiled=True
    ).T
    grad_gate_up = mul(rows, grad_pair, lhs_turned)[None]
    grad_down = mul(hidden, grad_rows, lhs_turned)[None]
    out_far = over_core(*out_far)
    out_far = [pick_sum(out_far, 0, lines, column) for column in range(2)]
    grad_gate_up, got, out_far, arrived = lax.optimization_barrier((grad_gate_up, got, out_far, arrived))
    entries.update(joined(parts[1], [item[cut:] for item in back_own], got))
    out_far = [swap_ctx(out_far[0]), swap_side(out_far[1])]
    outs, entries = hold((out_first, out_own, out_second), entries)
    out_first, out_own, out_second = (over_core(*item) for item in outs)
    for p in parts[1][:-1]:
        arrived[p] = line_shift(entries[p], lines - p)
    arrived, grad_down = hold(arrived, grad_down)
    grad_mid = line_total(entries[0], arrived)

    grad_wide = jnp.where(chosen, grad_gates, 0.0)
    grad_logits = (
        gates_wide * (grad_wide - jnp.sum(gates_wide * grad_wide, axis=1, keepdims=True))
    ).astype(low)
    grad_router = mul(low_mid, grad_logits, lhs_turned)
    grad_mid = grad_mid + mul(grad_logits, router_all, rhs_turned)
    grad_mixed_part, grad_moe_gain = rms_back(mixed, moe_all, grad_mid)
    grad_mixed = cotangent.astype(full) + grad_mixed_part

    low_mixed, (out_far, outs) = hold(
        grad_mixed.astype(low), (out_far, (out_first, out_own, out_second))
    )
    grad_branch = sequence(low_mixed)
    out_first, out_own, out_second = outs
    out_sums = [
        jnp.concatenate([one, two]) for one, two in zip(mixed_sums(out_first), mixed_sums(out_second))
    ]
    out_own = [pick_sum(out_own, 0, lines, column) for column in range(2)]
    (out_sums, out_own), grad_branch = hold((out_sums, out_own), grad_branch)
    side_one, side_two, ctx_one, ctx_two = out_sums
    got = [
        swap_ctx(ctx_one),
        swap_side(side_two),
        add_low(side_one, out_far[0]),
        add_low(ctx_two, out_far[1]),
    ]
    grad_attended = mul(grad_branch, out_all, rhs_turned).astype(low)
    grad_out_part = mul(attended, grad_branch, lhs_turned).astype(low)
    grad_q, grad_k, grad_v, gain_q_part, gain_k_part = attend_grad(
        projected, roped_q, roped_k, values_low, grad_attended, cosine, sine, gain_q, gain_k, kv_heads, group
    )
    grad_projected = jnp.concatenate([grad_q, grad_k, grad_v], axis=1)
    grad_projected, got = hold(grad_projected, got)
    got[2], got[3] = swap_side(got[2]), swap_ctx(got[3])
    grad_qkv_part = mul(low_in, grad_projected, lhs_turned).astype(low)
    grad_normed_part = mul(grad_projected, qkv_all, rhs_turned)
    grad_normed_part, got = hold(grad_normed_part, got)
    entries = joined(places, out_own, got)
    output = (mixed + line_sum(entries, lines)).astype(low)
    grad_normed = of_block(grad_normed_part, rank) + swap_ctx(
        of_block(grad_normed_part, 1 - rank).astype(low)
    ).astype(full)
    grad_in_part, grad_attn_gain = rms_back(inputs, attn_all, grad_normed)
    grad_tokens = grad_mixed + grad_in_part

    out_mine = lax.psum_scatter(grad_out_part, "fsdp", scatter_dimension=0, tiled=True).astype(full)
    out_other = swap_ctx(out_mine.astype(low)).astype(full)
    grad_out = jnp.where(
        rank == 0,
        jnp.concatenate([out_mine, out_other], axis=0),
        jnp.concatenate([out_other, out_mine], axis=0),
    )
    qkv_mine = lax.psum_scatter(grad_qkv_part, "fsdp", scatter_dimension=0, tiled=True).astype(full)
    qkv_other = swap_ctx(qkv_mine.astype(low)).astype(full)
    q_mine = qkv_mine[:, :width_q].reshape(shard, my_heads, 1, head_dim)
    q_other = qkv_other[:, :width_q].reshape(shard, my_heads, 1, head_dim)
    grad_q_all = jnp.where(
        rank == 0,
        jnp.concatenate([q_mine, q_other], axis=2),
        jnp.concatenate([q_other, q_mine], axis=2),
    ).reshape(shard, 2 * width_q)
    grad_qkv = jnp.concatenate(
        [grad_q_all, qkv_mine[:, width_q:] + qkv_other[:, width_q:]], axis=1
    )
    early = sum_owned(jnp.concatenate([grad_router.T, grad_moe_gain[None]], axis=0), fsdp, spot)
    late = sum_all(
        jnp.concatenate(
            [
                grad_attn_gain.reshape(-1, head_dim),
                jnp.sum(gain_q_part, axis=0),
                jnp.sum(gain_k_part, axis=0),
            ],
            axis=0,
        ),
        fsdp,
    )
    gain_rows = width // head_dim
    return (
        output,
        grad_tokens,
        grad_qkv,
        grad_out,
        early[:experts_all].T,
        lax.dynamic_slice_in_dim(late[:gain_rows].reshape(-1), spot * shard, shard, 0),
        early[experts_all],
        late[gain_rows],
        late[gain_rows + 1],
        grad_gate_up,
        grad_down,
    )


gathered_bytes = 1 << 26


def choose_body(*args):
    tokens, gate_up = args[0], args[8]
    fsdp, ctx = lax.axis_size("fsdp"), lax.axis_size("ctx")
    fits = tokens.size * tokens.dtype.itemsize * fsdp * ctx <= gathered_bytes
    if fits and fsdp % 4 == 0 and ctx == 2 and fsdp >= 8 and fsdp & (fsdp - 1) == 0 and gate_up.shape[0] == 1:
        return body_gathered(*args)
    return body_routed(*args)


def solution(mesh):
    in_specs = (
        P(("fsdp", "ctx"), None),
        P("fsdp", None),
        P("fsdp", None),
        P("fsdp", None),
        P("fsdp"),
        P("fsdp"),
        P(),
        P(),
        P(("fsdp", "ctx"), None, None),
        P(("fsdp", "ctx"), None, None),
        P(("fsdp", "ctx"), None),
        P(("fsdp", "ctx"), None),
    )
    out_specs = (
        P(("fsdp", "ctx"), None),
        P(("fsdp", "ctx"), None),
        P("fsdp", None),
        P("fsdp", None),
        P("fsdp", None),
        P("fsdp"),
        P("fsdp"),
        P(),
        P(),
        P(("fsdp", "ctx"), None, None),
        P(("fsdp", "ctx"), None, None),
    )
    return jax.shard_map(choose_body, mesh=mesh, in_specs=in_specs, out_specs=out_specs, check_vma=False)
```

```python
import functools
import math

import jax
import jax.numpy as jnp
from jax import lax
from jax.experimental import pallas as pl
from jax.experimental.pallas import tpu as pltpu
from jax.sharding import PartitionSpec as P

eps_norm = 1e-06
theta_base = 1000000.0


def rms_scale(values, gain):
    return values * lax.rsqrt(jnp.mean(values * values, axis=-1, keepdims=True) + eps_norm) * gain


def rotate(values, cosine, sine):
    half_width = values.shape[-1] // 2
    turned = jnp.concatenate([-values[..., half_width:], values[..., :half_width]], axis=-1)
    return values * cosine + turned * sine


def angles(positions, width):
    freqs = theta_base ** (-(jnp.arange(width // 2, dtype=jnp.float32) * 2.0) / width)
    phase = positions.astype(jnp.float32)[:, None] * freqs[None, :]
    phase = jnp.concatenate([phase, phase], axis=-1)
    return (jnp.cos(phase)[:, None, :], jnp.sin(phase)[:, None, :])


def device_positions(block_rank, ctx_count, tok_rows):
    half_rows = tok_rows // 2
    within = jnp.arange(tok_rows, dtype=jnp.int32)
    span_id = jnp.where(within < half_rows, block_rank, 2 * ctx_count - 1 - block_rank)
    return span_id * half_rows + within % half_rows


def attend_head(query, keys_in, values_in, causal, scale_root):
    scores = (
        jnp.einsum("tgd,sd->gts", query, keys_in, preferred_element_type=jnp.float32) / scale_root
    )
    expo = jnp.where(causal[None], jnp.exp(scores), 0.0)
    totals = jnp.sum(expo, axis=-1, keepdims=True)
    probs = (expo / totals).astype(jnp.bfloat16)
    attended = jnp.einsum("gts,sd->tgd", probs, values_in, preferred_element_type=jnp.float32)
    return (attended, jnp.log(totals[..., 0]))


def attend_back(query, keys_in, values_in, causal, log_total, grad_attended, scale_root):
    scores = (
        jnp.einsum("tgd,sd->gts", query, keys_in, preferred_element_type=jnp.float32) / scale_root
    )
    probs = jnp.where(causal[None], jnp.exp(scores - log_total[..., None]), 0.0)
    low_probs = probs.astype(jnp.bfloat16)
    grad_values = jnp.einsum(
        "gts,tgd->sd", low_probs, grad_attended, preferred_element_type=jnp.float32
    )
    grad_probs = jnp.einsum(
        "tgd,sd->gts", grad_attended, values_in, preferred_element_type=jnp.float32
    )
    delta_rows = jnp.sum(grad_probs * probs, axis=-1, keepdims=True)
    grad_scores = (probs * (grad_probs - delta_rows)).astype(jnp.bfloat16)
    grad_query = (
        jnp.einsum("gts,sd->tgd", grad_scores, keys_in, preferred_element_type=jnp.float32)
        / scale_root
    )
    grad_keys = (
        jnp.einsum("gts,tgd->sd", grad_scores, query, preferred_element_type=jnp.float32)
        / scale_root
    )
    return (grad_query, grad_keys, grad_values)


def swiglu(paired):
    half_width = paired.shape[-1] // 2
    return jax.nn.silu(paired[..., :half_width]) * paired[..., half_width:]


def gating(selected):
    expo = jnp.exp(selected)
    return expo / jnp.sum(expo, axis=1, keepdims=True)


def body_routed(
    tokens,
    qkv_weight,
    out_weight,
    router_weight,
    attn_gain,
    moe_gain,
    query_gain,
    key_gain,
    expert_gate_up,
    expert_down,
    routes,
    cotangent,
):
    rows_dev, width = tokens.shape
    head_dim = query_gain.shape[0]
    top_k = routes.shape[1]
    ctx_count = lax.axis_size("ctx")
    ctx_rank = lax.axis_index("ctx")
    qkv_all, out_all, router_all, attn_all, moe_all = (
        lax.all_gather(qkv_weight, "fsdp", axis=0, tiled=True),
        lax.all_gather(out_weight, "fsdp", axis=0, tiled=True),
        lax.all_gather(router_weight, "fsdp", axis=0, tiled=True),
        lax.all_gather(attn_gain, "fsdp", axis=0, tiled=True),
        lax.all_gather(moe_gain, "fsdp", axis=0, tiled=True),
    )
    experts_all = router_all.shape[1]
    heads = out_all.shape[0] // head_dim
    kv_heads = (qkv_all.shape[1] // head_dim - heads) // 2
    group_size = heads // kv_heads
    capacity = 2 * rows_dev * top_k // experts_all
    width_q = heads * head_dim
    width_k = kv_heads * head_dim
    scale_root = math.sqrt(head_dim)
    inputs = tokens.astype(jnp.float32)
    normed_in = rms_scale(inputs, attn_all.astype(jnp.float32))
    low_in = normed_in.astype(jnp.bfloat16)
    projected = jnp.dot(low_in, qkv_all, preferred_element_type=jnp.float32)
    query_raw = projected[:, :width_q].reshape(rows_dev, heads, head_dim)
    key_raw = projected[:, width_q : width_q + width_k].reshape(rows_dev, kv_heads, head_dim)
    value_low = (
        projected[:, width_q + width_k :].astype(jnp.bfloat16).reshape(rows_dev, kv_heads, head_dim)
    )
    positions = device_positions(ctx_rank, ctx_count, rows_dev)
    cosine, sine = angles(positions, head_dim)
    query_gain_f = query_gain.astype(jnp.float32)
    key_gain_f = key_gain.astype(jnp.float32)

    def query_rope(values_in, gain):
        return rotate(rms_scale(values_in, gain), cosine, sine)

    query_low = query_rope(query_raw, query_gain_f).astype(jnp.bfloat16)
    key_low = query_rope(key_raw, key_gain_f).astype(jnp.bfloat16)
    keys_all, values_all = (
        lax.all_gather(key_low, "ctx", axis=0, tiled=True),
        lax.all_gather(value_low, "ctx", axis=0, tiled=True),
    )
    key_pos = jnp.concatenate(
        [device_positions(other, ctx_count, rows_dev) for other in range(ctx_count)]
    )
    causal = key_pos[None, :] <= positions[:, None]
    query_heads = query_low.reshape(rows_dev, kv_heads, group_size, head_dim).transpose(1, 0, 2, 3)
    key_heads = keys_all.transpose(1, 0, 2)
    value_heads = values_all.transpose(1, 0, 2)
    attended, log_total = lax.map(
        lambda member: attend_head(member[0], member[1], member[2], causal, scale_root),
        (query_heads, key_heads, value_heads),
    )
    attended_low = attended.transpose(1, 0, 2, 3).reshape(rows_dev, width_q).astype(jnp.bfloat16)
    mixed = inputs + jnp.dot(attended_low, out_all, preferred_element_type=jnp.float32)
    normed_mid = rms_scale(mixed, moe_all.astype(jnp.float32))
    low_mid = normed_mid.astype(jnp.bfloat16)
    logits = jnp.dot(low_mid, router_all, preferred_element_type=jnp.float32)
    selected = jnp.take_along_axis(logits, routes, axis=1)
    gates, gate_back = jax.vjp(gating, selected)
    flat_routes = routes.reshape(-1)
    expert_ids = jnp.arange(experts_all, dtype=jnp.int32)
    hit_table = (flat_routes[:, None] == expert_ids[None, :]).astype(jnp.int32)
    slot_index = jnp.sum(jnp.cumsum(hit_table, axis=0) * hit_table, axis=1) - 1
    target = flat_routes * capacity + slot_index
    pair_count = rows_dev * top_k
    source_pair = (
        jnp.full((experts_all * capacity,), pair_count, jnp.int32)
        .at[target]
        .set(jnp.arange(pair_count, dtype=jnp.int32))
    )
    padded = jnp.concatenate([low_mid, jnp.zeros((1, width), jnp.bfloat16)], axis=0)
    outgoing = padded[source_pair // top_k].reshape(experts_all, capacity, width)
    received = lax.all_to_all(outgoing, ("fsdp", "ctx"), split_axis=0, concat_axis=1, tiled=True)
    gate_and_up = jnp.einsum(
        "esd,edf->esf", received, expert_gate_up, preferred_element_type=jnp.float32
    )
    hidden_val, swiglu_back = jax.vjp(swiglu, gate_and_up)
    hidden_low = hidden_val.astype(jnp.bfloat16)
    result_low = jnp.einsum(
        "esf,efd->esd", hidden_low, expert_down, preferred_element_type=jnp.float32
    ).astype(jnp.bfloat16)
    returned = lax.all_to_all(
        result_low, ("fsdp", "ctx"), split_axis=1, concat_axis=0, tiled=True
    ).reshape(experts_all * capacity, width)
    picked = returned[target].reshape(rows_dev, top_k, width).astype(jnp.float32)
    output = (mixed + jnp.sum(gates[:, :, None] * picked, axis=1)).astype(jnp.bfloat16)
    qkv_back, out_back, router_back, attn_back_g, moe_back_g = (
        qkv_all,
        out_all,
        router_all,
        attn_all,
        moe_all,
    )
    grad_final = cotangent.astype(jnp.float32)
    grad_gates = jnp.sum(grad_final[:, None, :] * picked, axis=2)
    grad_result = (
        (gates[:, :, None] * grad_final[:, None, :]).astype(jnp.bfloat16).reshape(pair_count, width)
    )
    grad_padded = jnp.concatenate([grad_result, jnp.zeros((1, width), jnp.bfloat16)], axis=0)
    grad_outgoing = grad_padded[source_pair].reshape(experts_all, capacity, width)
    grad_received = lax.all_to_all(
        grad_outgoing, ("fsdp", "ctx"), split_axis=0, concat_axis=1, tiled=True
    )
    grad_down = jnp.einsum(
        "esf,esd->efd", hidden_low, grad_received, preferred_element_type=jnp.float32
    )
    grad_hidden = jnp.einsum(
        "esd,efd->esf", grad_received, expert_down, preferred_element_type=jnp.float32
    )
    grad_paired = swiglu_back(grad_hidden)[0].astype(jnp.bfloat16)
    grad_gate_up = jnp.einsum(
        "esd,esf->edf", received, grad_paired, preferred_element_type=jnp.float32
    )
    grad_rows = jnp.einsum(
        "esf,edf->esd", grad_paired, expert_gate_up, preferred_element_type=jnp.float32
    ).astype(jnp.bfloat16)
    grad_returned = lax.all_to_all(
        grad_rows, ("fsdp", "ctx"), split_axis=1, concat_axis=0, tiled=True
    ).reshape(experts_all * capacity, width)
    grad_mid = jnp.sum(
        grad_returned[target].reshape(rows_dev, top_k, width).astype(jnp.float32), axis=1
    )
    grad_selected = gate_back(grad_gates)[0]
    route_table = (routes[:, :, None] == expert_ids[None, None, :]).astype(jnp.float32)
    grad_logits = jnp.sum(route_table * grad_selected[:, :, None], axis=1).astype(jnp.bfloat16)
    grad_router = jnp.dot(low_mid.T, grad_logits, preferred_element_type=jnp.float32)
    grad_mid = grad_mid + jnp.dot(grad_logits, router_back.T, preferred_element_type=jnp.float32)
    unused_mid, mid_back = jax.vjp(rms_scale, mixed, moe_back_g.astype(jnp.float32))
    grad_mixed_part, grad_moe_gain = mid_back(grad_mid)
    grad_mixed = grad_final + grad_mixed_part
    grad_branch = grad_mixed.astype(jnp.bfloat16)
    grad_out = jnp.dot(attended_low.T, grad_branch, preferred_element_type=jnp.float32)
    grad_attended = jnp.dot(grad_branch, out_back.T, preferred_element_type=jnp.float32).astype(
        jnp.bfloat16
    )
    grad_heads = grad_attended.reshape(rows_dev, kv_heads, group_size, head_dim).transpose(
        1, 0, 2, 3
    )
    grad_query_h, grad_key_h, grad_value_h = lax.map(
        lambda member: attend_back(
            member[0], member[1], member[2], causal, member[3], member[4], scale_root
        ),
        (query_heads, key_heads, value_heads, log_total, grad_heads),
    )
    grad_keys, grad_values = (
        lax.psum_scatter(
            grad_key_h.transpose(1, 0, 2).astype(jnp.bfloat16),
            "ctx",
            scatter_dimension=0,
            tiled=True,
        ).astype(jnp.float32),
        lax.psum_scatter(
            grad_value_h.transpose(1, 0, 2).astype(jnp.bfloat16),
            "ctx",
            scatter_dimension=0,
            tiled=True,
        ).astype(jnp.float32),
    )
    grad_query_rot = (
        grad_query_h.transpose(1, 0, 2, 3).reshape(rows_dev, heads, head_dim).astype(jnp.bfloat16)
    )
    grad_query_rot = lax.optimization_barrier(grad_query_rot).astype(jnp.float32)
    grad_key_rot = lax.optimization_barrier(grad_keys.astype(jnp.bfloat16)).astype(jnp.float32)
    unused_query, query_back = jax.vjp(query_rope, query_raw, query_gain_f)
    grad_query_raw, grad_query_gain = query_back(grad_query_rot)
    unused_key, key_back = jax.vjp(query_rope, key_raw, key_gain_f)
    grad_key_raw, grad_key_gain = key_back(grad_key_rot)
    grad_projected = jnp.concatenate(
        [
            grad_query_raw.reshape(rows_dev, width_q).astype(jnp.bfloat16),
            grad_key_raw.reshape(rows_dev, width_k).astype(jnp.bfloat16),
            grad_values.reshape(rows_dev, width_k).astype(jnp.bfloat16),
        ],
        axis=1,
    )
    grad_qkv = jnp.dot(low_in.T, grad_projected, preferred_element_type=jnp.float32)
    grad_normed = jnp.dot(grad_projected, qkv_back.T, preferred_element_type=jnp.float32)
    unused_in, in_back = jax.vjp(rms_scale, inputs, attn_back_g.astype(jnp.float32))
    grad_in_part, grad_attn_gain = in_back(grad_normed)
    grad_tokens = grad_mixed + grad_in_part
    gradients = (grad_qkv, grad_out, grad_router, grad_attn_gain, grad_moe_gain)
    pieces = (
        lax.psum_scatter(gradients[0], "fsdp", scatter_dimension=0, tiled=True),
        lax.psum_scatter(gradients[1], "fsdp", scatter_dimension=0, tiled=True),
        lax.psum_scatter(gradients[2], "fsdp", scatter_dimension=0, tiled=True),
        lax.psum_scatter(gradients[3], "fsdp", scatter_dimension=0, tiled=True),
        lax.psum_scatter(gradients[4], "fsdp", scatter_dimension=0, tiled=True),
    )
    reduced = (
        lax.psum(pieces[0].astype(jnp.bfloat16), "ctx").astype(jnp.float32),
        lax.psum(pieces[1].astype(jnp.bfloat16), "ctx").astype(jnp.float32),
        lax.psum(pieces[2].astype(jnp.bfloat16), "ctx").astype(jnp.float32),
        lax.psum(pieces[3].astype(jnp.bfloat16), "ctx").astype(jnp.float32),
        lax.psum(pieces[4].astype(jnp.bfloat16), "ctx").astype(jnp.float32),
    )
    gain_sums = lax.psum((grad_query_gain, grad_key_gain), ("fsdp", "ctx"))
    return (
        output,
        grad_tokens,
        reduced[0],
        reduced[1],
        reduced[2],
        reduced[3],
        reduced[4],
        gain_sums[0],
        gain_sums[1],
        grad_gate_up,
        grad_down,
    )


low = jnp.bfloat16
full = jnp.float32
plain = (((1,), (0,)), ((), ()))
rhs_turned = (((1,), (1,)), ((), ()))
lhs_turned = (((0,), (0,)), ((), ()))
vmem_bytes = 58 << 20


def mul(left, right, dims=plain):
    return lax.dot_general(left, right, dims, preferred_element_type=full)


def core_pairs(fsdp):
    return [(i, i ^ 1) for i in range(fsdp)]


def side_pairs(fsdp):
    return [(i, i ^ 2) for i in range(fsdp)]


def swap_core(values):
    return lax.ppermute(values, "fsdp", core_pairs(lax.axis_size("fsdp")))


def swap_side(values):
    return lax.ppermute(values, "fsdp", side_pairs(lax.axis_size("fsdp")))


def swap_ctx(values):
    return lax.ppermute(values, "ctx", [(0, 1), (1, 0)])


def add_low(one, two):
    return (one.astype(full) + two.astype(full)).astype(low)


def hold(values, first):
    return lax.optimization_barrier((values, first))


def take(values, index):
    return lax.dynamic_index_in_dim(values, index, 0, keepdims=False)


def line_shift(values, step):
    fsdp = lax.axis_size("fsdp")
    return lax.ppermute(values, "fsdp", [(i, (i + 4 * step) % fsdp) for i in range(fsdp)])


def line_total(own, arrived):
    total = own.astype(full)
    for item in arrived.values():
        total = total + item.astype(full)
    return total


def line_sum(entries, count):
    return line_total(entries[0], {s: line_shift(entries[s], count - s) for s in range(1, count)})


def joined(places, own, got):
    from_ctx, from_side, one_side, two_ctx = got
    entries = {}
    for at, p in enumerate(places):
        one = add_low(add_low(own[0][at], from_ctx[at]), one_side[at])
        two = add_low(add_low(own[1][at], from_side[at]), two_ctx[at])
        entries[p] = jnp.concatenate([one, two], axis=-1)
    return entries


def over_core(keep, send):
    return keep, swap_core(send)


def pick_sum(parts, start, stop, column):
    keep, other = parts
    half = keep.shape[-1] // 2
    cut = (slice(start, stop), slice(None), slice(column * half, (column + 1) * half))
    return add_low(keep[cut], other[cut])


def sum_all(values, fsdp):
    values = values + lax.ppermute(values, "fsdp", core_pairs(fsdp))
    values = values + swap_ctx(values)
    step = 2
    while step < fsdp:
        values = values + lax.ppermute(values, "fsdp", [(i, i ^ step) for i in range(fsdp)])
        step *= 2
    return values


def sum_owned(values, fsdp, spot):
    items, shard = values.shape[0], values.shape[1] // fsdp
    values = values.reshape(items, fsdp, shard).swapaxes(0, 1)
    step = fsdp // 2
    while step:
        bit = (spot // step) % 2
        values = values.reshape(2, step, items, shard)
        other = lax.ppermute(take(values, 1 - bit), "fsdp", [(i, i ^ step) for i in range(fsdp)])
        values = take(values, bit) + other
        step //= 2
    values = values[0]
    return values + swap_ctx(values)


def turn(values):
    return pltpu.roll(values, values.shape[-1] // 2, 1)


def norm_rope(raw, gain, cosine, sine):
    scale = lax.rsqrt(jnp.mean(raw * raw, axis=-1, keepdims=True) + eps_norm)
    scaled = raw * scale * gain
    return scaled * cosine + turn(scaled) * sine


def norm_rope_back(raw, gain, cosine, sine, grad):
    scale = lax.rsqrt(jnp.mean(raw * raw, axis=-1, keepdims=True) + eps_norm)
    unit = raw * scale
    grad_scaled = grad * cosine - turn(grad) * sine
    grad_gain = jnp.sum(grad_scaled * unit, axis=0, keepdims=True)
    grad_unit = grad_scaled * gain
    grad_raw = scale * (grad_unit - unit * jnp.mean(grad_unit * unit, axis=-1, keepdims=True))
    return grad_raw, grad_gain


def tiles_of(rows):
    step = rows // 2
    return [(start, start + step) for start in range(0, rows, step)]


def allowed(start, stop):
    shape = (stop - start, stop)
    return lax.broadcasted_iota(jnp.int32, shape, 1) <= (
        lax.broadcasted_iota(jnp.int32, shape, 0) + start
    )


def attend_kernel(q_ref, k_ref, v_ref, cos_ref, sin_ref, qg_ref, kg_ref, o_ref, qr_ref, kr_ref, vl_ref):
    head_dim = k_ref.shape[1]
    rows = k_ref.shape[0]
    cosine, sine = cos_ref[...], sin_ref[...]
    keys = norm_rope(k_ref[...], kg_ref[...], cosine, sine).astype(low)
    values = v_ref[...].astype(low)
    kr_ref[...] = keys
    vl_ref[...] = values
    for head in range(q_ref.shape[1] // head_dim):
        cols = slice(head * head_dim, (head + 1) * head_dim)
        query = norm_rope(q_ref[:, cols], qg_ref[...], cosine, sine).astype(low)
        qr_ref[:, cols] = query
        for start, stop in tiles_of(rows):
            scores = mul(query[start:stop], keys[:stop], rhs_turned) * (1.0 / math.sqrt(head_dim))
            expo = jnp.where(allowed(start, stop), jnp.exp(scores), 0.0)
            probs = (expo / jnp.sum(expo, axis=-1, keepdims=True)).astype(low)
            o_ref[start:stop, cols] = mul(probs, values[:stop]).astype(low)


def attend_grad_kernel(
    q_ref, k_ref, qr_ref, kr_ref, vl_ref, go_ref, cos_ref, sin_ref, qg_ref, kg_ref,
    dq_ref, dk_ref, dv_ref, dqg_ref, dkg_ref, dk_sum, dv_sum, dq_sum,
):
    head_dim = k_ref.shape[1]
    rows = k_ref.shape[0]
    root = 1.0 / math.sqrt(head_dim)
    cosine, sine = cos_ref[...], sin_ref[...]
    keys, values = kr_ref[...], vl_ref[...]
    gain_sum = jnp.zeros((1, head_dim), full)
    dk_sum[...] = jnp.zeros_like(dk_sum)
    dv_sum[...] = jnp.zeros_like(dv_sum)
    for head in range(q_ref.shape[1] // head_dim):
        cols = slice(head * head_dim, (head + 1) * head_dim)
        for start, stop in tiles_of(rows):
            query = qr_ref[start:stop, cols]
            grad = go_ref[start:stop, cols]
            scores = mul(query, keys[:stop], rhs_turned) * root
            expo = jnp.where(allowed(start, stop), jnp.exp(scores), 0.0)
            probs = expo / jnp.sum(expo, axis=-1, keepdims=True)
            grad_probs = mul(grad, values[:stop], rhs_turned)
            delta = jnp.sum(grad_probs * probs, axis=-1, keepdims=True)
            grad_scores = (probs * (grad_probs - delta)).astype(low)
            dv_sum[:stop] += mul(probs.astype(low), grad, lhs_turned)
            dk_sum[:stop] += mul(grad_scores, query, lhs_turned)
            dq_sum[start:stop] = mul(grad_scores, keys[:stop])
        grad_query = (dq_sum[...] * root).astype(low).astype(full)
        grad_raw, grad_gain = norm_rope_back(q_ref[:, cols], qg_ref[...], cosine, sine, grad_query)
        dq_ref[:, cols] = grad_raw.astype(low)
        gain_sum = gain_sum + grad_gain
    dqg_ref[0] = gain_sum
    grad_key = (dk_sum[...] * root).astype(low).astype(full)
    grad_raw, grad_gain = norm_rope_back(k_ref[...], kg_ref[...], cosine, sine, grad_key)
    dk_ref[...] = grad_raw.astype(low)
    dkg_ref[0] = grad_gain
    dv_ref[...] = dv_sum[...].astype(low)


def attention_specs(rows, head_dim, kv_heads, group):
    wide, narrow = group * head_dim, head_dim
    heads_end = kv_heads * group
    return dict(
        q=pl.BlockSpec((rows, wide), lambda i: (0, i)),
        k=pl.BlockSpec((rows, narrow), lambda i: (0, heads_end + i)),
        v=pl.BlockSpec((rows, narrow), lambda i: (0, heads_end + kv_heads + i)),
        own=pl.BlockSpec((rows, narrow), lambda i: (0, i)),
        table=pl.BlockSpec((rows, head_dim), lambda i: (0, 0)),
        gain=pl.BlockSpec((1, head_dim), lambda i: (0, 0)),
        gain_out=pl.BlockSpec((1, 1, head_dim), lambda i: (i, 0, 0)),
    )


def attend(projected, cosine, sine, query_gain, key_gain, kv_heads, group):
    rows, head_dim = cosine.shape
    s = attention_specs(rows, head_dim, kv_heads, group)
    shape = jax.ShapeDtypeStruct
    work = rows * rows * head_dim * kv_heads * group
    return pl.pallas_call(
        attend_kernel,
        grid=(kv_heads,),
        in_specs=[s["q"], s["k"], s["v"], s["table"], s["table"], s["gain"], s["gain"]],
        out_specs=[s["q"], s["q"], s["own"], s["own"]],
        out_shape=[
            shape((rows, kv_heads * group * head_dim), low),
            shape((rows, kv_heads * group * head_dim), low),
            shape((rows, kv_heads * head_dim), low),
            shape((rows, kv_heads * head_dim), low),
        ],
        compiler_params=pltpu.CompilerParams(vmem_limit_bytes=48 << 20),
        cost_estimate=pl.CostEstimate(
            flops=4 * work, bytes_accessed=projected.size * 6, transcendentals=work // head_dim
        ),
        name="attend",
    )(projected, projected, projected, cosine, sine, query_gain, key_gain)


def attend_grad(projected, roped_q, roped_k, values_low, grad, cosine, sine, query_gain, key_gain, kv_heads, group):
    rows, head_dim = cosine.shape
    s = attention_specs(rows, head_dim, kv_heads, group)
    shape = jax.ShapeDtypeStruct
    work = rows * rows * head_dim * kv_heads * group
    return pl.pallas_call(
        attend_grad_kernel,
        grid=(kv_heads,),
        in_specs=[
            s["q"], s["k"], s["q"], s["own"], s["own"], s["q"],
            s["table"], s["table"], s["gain"], s["gain"],
        ],
        out_specs=[s["q"], s["own"], s["own"], s["gain_out"], s["gain_out"]],
        out_shape=[
            shape((rows, kv_heads * group * head_dim), low),
            shape((rows, kv_heads * head_dim), low),
            shape((rows, kv_heads * head_dim), low),
            shape((kv_heads, 1, head_dim), full),
            shape((kv_heads, 1, head_dim), full),
        ],
        scratch_shapes=[pltpu.VMEM((rows, head_dim), full)] * 3,
        compiler_params=pltpu.CompilerParams(vmem_limit_bytes=48 << 20),
        cost_estimate=pl.CostEstimate(
            flops=10 * work, bytes_accessed=projected.size * 10, transcendentals=work // head_dim
        ),
        name="attend_grad",
    )(projected, projected, roped_q, roped_k, values_low, grad, cosine, sine, query_gain, key_gain)


def placed(gate, slots):
    block = gate.shape[1]
    shape = (block, block)
    earlier = (
        lax.broadcasted_iota(jnp.int32, shape, 0) < lax.broadcasted_iota(jnp.int32, shape, 1)
    ).astype(low)
    hit = jnp.where(gate >= 0.0, 1.0, 0.0)
    count = mul(jnp.broadcast_to(hit, (8, block)).astype(low), earlier)[:1].astype(jnp.int32)
    place = (lax.broadcasted_iota(jnp.int32, (slots, block), 0) == count) & (hit > 0.5)
    weight = jnp.sum(jnp.where(place, gate, 0.0), axis=1, keepdims=True)
    return place, place.astype(full).astype(low), weight


def expert_kernel(core_ref, order, m_ref, g_ref, far_ref, w_ref, gu_ref, dn_ref, *refs):
    keep_back, send_back, gate_back, rows_ref, dy_ref, z_ref, pair_ref = refs[-7:]
    core = core_ref[0]
    far = order[4 * pl.program_id(0) + 2] == 1
    width = m_ref.shape[4]
    hidden = dn_ref.shape[0]
    slots = z_ref.shape[0] // 2
    places, picks, weights, rows, grads = [], [], [], [], []
    for part in range(2):
        at = lax.rem(core + part, 2)
        place, pick, weight = placed(w_ref[0, at, 0], slots)
        places.append(place)
        picks.append(pick)
        weights.append(weight)
        rows.append(mul(pick, m_ref[0, at, 0]).astype(low))
        near_rows = g_ref[0, at, :, :width]
        far_rows = jnp.concatenate([far_ref[0, at], g_ref[0, at, :, width:]], axis=1)
        grads.append(mul(pick, jnp.where(far, far_rows, near_rows)).astype(low))
    row, grad, weight = (jnp.concatenate(items, axis=0) for items in (rows, grads, weights))
    rows_ref[...] = row
    paired = mul(row, gu_ref[...])
    gate_in, up = paired[:, :hidden], paired[:, hidden:]
    sig = jax.nn.sigmoid(gate_in)
    act = gate_in * sig
    z = (act * up).astype(low)
    z_ref[...] = z
    dy_ref[...] = (weight * grad.astype(full)).astype(low)
    unweighted = mul(grad, dn_ref[...], rhs_turned)
    grad_gate = jnp.sum(unweighted * z.astype(full), axis=1, keepdims=True)
    dz = weight * unweighted
    grad_in = dz * up * (sig * (1.0 + gate_in * (1.0 - sig)))
    pair = jnp.concatenate([grad_in, dz * act], axis=1).astype(low)
    pair_ref[...] = pair
    back = mul(pair, gu_ref[...], rhs_turned).astype(low)
    for part, out in enumerate((keep_back, send_back)):
        mine = slice(part * slots, (part + 1) * slots)
        out[0] = mul(picks[part], back[mine], lhs_turned).astype(low)
        gate_back[0, lax.rem(core + part, 2), 0] = jnp.sum(
            jnp.where(places[part], grad_gate[mine], 0.0), axis=0, keepdims=True
        )


def run_expert(core, order, first, total_steps, m_all, g_all, g_far, gates_all, gate_up, down, slots, kept):
    places, _, _, block, width = m_all.shape
    paired = gate_up.shape[1]
    steps = order.shape[0] // 4
    part_rows = steps * 2 * slots
    hidden = paired // 2
    shape = jax.ShapeDtypeStruct

    def gates_at(i, core, order):
        return (order[4 * i], 0, order[4 * i + 1], 0, 0)

    def token_at(i, core, order):
        return (order[4 * i], 0, order[4 * i + 2], 0, 0)

    def near_at(i, core, order):
        return (order[4 * i], 0, 0, 0)

    def far_at(i, core, order):
        return (order[4 * i + 3], 0, 0, 0)

    def fixed(i, core, order):
        return (0, 0)

    def flat(i, core, order):
        return (first + i, 0)

    def stacked(i, core, order):
        return (i, 0, 0)

    small = pl.BlockSpec((1, 2, 1, 1, block), gates_at)
    one_block = pl.BlockSpec((1, block, width), stacked)
    widths = (width, width, hidden, paired)
    grid_spec = pltpu.PrefetchScalarGridSpec(
        num_scalar_prefetch=2,
        grid=(steps,),
        in_specs=[
            pl.BlockSpec((1, 2, 1, block, width), token_at),
            pl.BlockSpec((1, 2, block, g_all.shape[3]), near_at),
            pl.BlockSpec((1, 2, block, g_far.shape[3]), far_at),
            small,
            pl.BlockSpec(gate_up.shape, fixed, pipeline_mode=pl.Buffered(1)),
            pl.BlockSpec(down.shape, fixed, pipeline_mode=pl.Buffered(1)),
        ]
        + [pl.BlockSpec(memory_space=pl.ANY)] * (0 if kept is None else 5),
        out_specs=[one_block] * 2 + [small] + [pl.BlockSpec((2 * slots, n), flat) for n in widths],
    )
    return pl.pallas_call(
        expert_kernel,
        grid_spec=grid_spec,
        out_shape=[shape((steps, block, width), low)] * 2
        + [shape((places, 2, 2, 1, block), full)]
        + [shape((total_steps * 2 * slots, n), low) for n in widths],
        input_output_aliases={} if kept is None else {8 + i: 2 + i for i in range(5)},
        compiler_params=pltpu.CompilerParams(vmem_limit_bytes=vmem_bytes),
        cost_estimate=pl.CostEstimate(
            flops=part_rows * width * (4 * paired + 2 * hidden + 6 * block),
            bytes_accessed=steps * block * width * 12 + part_rows * (width * 4 + paired * 3),
            transcendentals=part_rows * hidden,
        ),
        name="experts",
    )(core, order, m_all, g_all, g_far, gates_all, gate_up, down, *(() if kept is None else kept))


def result_kernel(core_ref, order, z_ref, w_ref, dn_ref, keep_out, send_out):
    core = core_ref[0]
    slots = z_ref.shape[0] // 2
    y = mul(z_ref[...], dn_ref[...]).astype(low).astype(full)
    for part, out in enumerate((keep_out, send_out)):
        _, pick, weight = placed(w_ref[0, lax.rem(core + part, 2), 0], slots)
        scaled = (weight * y[part * slots : (part + 1) * slots]).astype(low)
        out[0] = mul(pick, scaled, lhs_turned).astype(low)


def run_result(core, order, first, hidden, gates_all, down, slots):
    block, width, inner = gates_all.shape[4], down.shape[1], down.shape[0]
    steps = order.shape[0] // 4
    one_block = pl.BlockSpec((1, block, width), lambda i, core, order: (i, 0, 0))
    return pl.pallas_call(
        result_kernel,
        grid_spec=pltpu.PrefetchScalarGridSpec(
            num_scalar_prefetch=2,
            grid=(steps,),
            in_specs=[
                pl.BlockSpec((2 * slots, inner), lambda i, core, order: (first + i, 0)),
                pl.BlockSpec(
                    (1, 2, 1, 1, block), lambda i, core, order: (order[4 * i], 0, order[4 * i + 1], 0, 0)
                ),
                pl.BlockSpec(down.shape, lambda i, core, order: (0, 0), pipeline_mode=pl.Buffered(1)),
            ],
            out_specs=[one_block] * 2,
        ),
        out_shape=[jax.ShapeDtypeStruct((steps, block, width), low)] * 2,
        compiler_params=pltpu.CompilerParams(vmem_limit_bytes=vmem_bytes),
        cost_estimate=pl.CostEstimate(
            flops=steps * 2 * slots * width * (2 * inner + 2 * block),
            bytes_accessed=steps * (4 * block * width + 4 * slots * inner) + 2 * inner * width,
            transcendentals=0,
        ),
        name="results",
    )(core, order, hidden, gates_all, down)


def own_heads_kernel(rank, qkv_ref, out_ref, o_ref, *, head_dim, heads):
    first = rank[0] == 0
    for head in range(heads):
        pair = [qkv_ref[:, (2 * head + i) * head_dim : (2 * head + i + 1) * head_dim] for i in range(2)]
        o_ref[:, head * head_dim : (head + 1) * head_dim] = jnp.where(first, pair[0], pair[1])
    kv = qkv_ref.shape[1] - 2 * heads * head_dim
    o_ref[:, heads * head_dim : heads * head_dim + kv] = qkv_ref[:, 2 * heads * head_dim :]
    o_ref[:, heads * head_dim + kv :] = jnp.where(first, out_ref[:head_dim], out_ref[head_dim:])


def own_heads(rank, qkv_weight, out_weight, head_dim, heads):
    kv = qkv_weight.shape[1] - 2 * heads * head_dim
    return pl.pallas_call(
        functools.partial(own_heads_kernel, head_dim=head_dim, heads=heads),
        grid_spec=pltpu.PrefetchScalarGridSpec(
            num_scalar_prefetch=1,
            grid=(1,),
            in_specs=[
                pl.BlockSpec(qkv_weight.shape, lambda i, rank: (0, 0)),
                pl.BlockSpec(out_weight.shape, lambda i, rank: (0, 0)),
            ],
            out_specs=pl.BlockSpec(
                (qkv_weight.shape[0], heads * head_dim + kv + out_weight.shape[1]), lambda i, rank: (0, 0)
            ),
        ),
        out_shape=jax.ShapeDtypeStruct(
            (qkv_weight.shape[0], heads * head_dim + kv + out_weight.shape[1]), qkv_weight.dtype
        ),
        name="own_heads",
    )(rank, qkv_weight, out_weight)


def all_heads_kernel(rank, mine_ref, other_ref, o_ref, *, head_dim, heads):
    first = rank[0] == 0
    for head in range(heads):
        cols = slice(head * head_dim, (head + 1) * head_dim)
        mine, other = mine_ref[:, cols].astype(full), other_ref[:, cols].astype(full)
        o_ref[:, 2 * head * head_dim : (2 * head + 1) * head_dim] = jnp.where(first, mine, other)
        o_ref[:, (2 * head + 1) * head_dim : (2 * head + 2) * head_dim] = jnp.where(first, other, mine)
    o_ref[:, 2 * heads * head_dim :] = mine_ref[:, heads * head_dim :].astype(full) + other_ref[
        :, heads * head_dim :
    ].astype(full)


def all_heads(rank, mine, other, head_dim, heads):
    rows, width = mine.shape
    return pl.pallas_call(
        functools.partial(all_heads_kernel, head_dim=head_dim, heads=heads),
        grid_spec=pltpu.PrefetchScalarGridSpec(
            num_scalar_prefetch=1,
            grid=(1,),
            in_specs=[pl.BlockSpec((rows, width), lambda i, rank: (0, 0))] * 2,
            out_specs=pl.BlockSpec((rows, width + heads * head_dim), lambda i, rank: (0, 0)),
        ),
        out_shape=jax.ShapeDtypeStruct((rows, width + heads * head_dim), full),
        name="all_heads",
    )(rank, mine, other)


def rms_back(values, gain, grad):
    scale = lax.rsqrt(jnp.mean(values * values, axis=-1, keepdims=True) + eps_norm)
    unit = values * scale
    grad_gain = jnp.sum(grad * unit, axis=0)
    grad_unit = grad * gain
    back = scale * (grad_unit - unit * jnp.mean(grad_unit * unit, axis=-1, keepdims=True))
    return back, grad_gain


def in_order(first, second):
    half = first.shape[0] // 2
    return jnp.concatenate([first[:half], second, first[half:]], axis=0)


def of_block(values, rank):
    quarter = values.shape[0] // 4
    outer = jnp.concatenate([values[:quarter], values[3 * quarter :]], axis=0)
    return jnp.where(rank == 0, outer, values[quarter : 3 * quarter])


def body_gathered(
    tokens, qkv_weight, out_weight, router_weight, attn_gain, moe_gain, query_gain, key_gain,
    expert_gate_up, expert_down, routes, cotangent,
):
    rows_dev, width = tokens.shape
    head_dim = query_gain.shape[0]
    top_k = routes.shape[1]
    fsdp = lax.axis_size("fsdp")
    spot = lax.axis_index("fsdp")
    rank = lax.axis_index("ctx")
    place, side, core = spot // 4, (spot // 2) % 2, spot % 2
    shard = qkv_weight.shape[0]
    heads = out_weight.shape[0] * fsdp // head_dim
    kv_heads = (qkv_weight.shape[1] // head_dim - heads) // 2
    group = heads // kv_heads // 2
    my_heads = heads // 2
    width_q, width_k = my_heads * head_dim, kv_heads * head_dim
    experts_all = router_weight.shape[1]
    capacity = 2 * rows_dev * top_k // experts_all
    both = ("fsdp", "ctx")

    def sequence(values):
        other = swap_ctx(values)
        first = jnp.where(rank == 0, values, other)
        second = jnp.where(rank == 0, other, values)
        return in_order(first, second)

    rank_at = rank[None].astype(jnp.int32)
    weights_local = own_heads(rank_at, qkv_weight, out_weight, head_dim, my_heads)
    small_local = jnp.concatenate([router_weight, attn_gain[:, None], moe_gain[:, None]], axis=1)
    small_all = lax.all_gather(small_local, "fsdp", axis=0, tiled=True)
    weights_all = lax.all_gather(weights_local, "fsdp", axis=0, tiled=True)
    qkv_all = weights_all[:, : width_q + 2 * width_k]
    out_all = weights_all[:, width_q + 2 * width_k :]
    router_all = small_all[:, :experts_all]
    attn_all = small_all[:, experts_all].astype(full)
    moe_all = small_all[:, experts_all + 1].astype(full)
    late_cols = width * 7 // 16
    g_all = lax.all_gather(
        jnp.concatenate([cotangent, swap_ctx(cotangent[:, late_cols:])], axis=1), "fsdp", axis=0, tiled=True
    ).reshape(fsdp // 2, 2, rows_dev, 2 * width - late_cols)

    sequence_in = sequence(tokens).astype(full)
    low_in = rms_scale(sequence_in, attn_all).astype(low)
    projected = mul(low_in, qkv_all)
    cosine, sine = (t[:, 0] for t in angles(jnp.arange(2 * rows_dev, dtype=jnp.int32), head_dim))
    sine = jnp.concatenate([-sine[:, : head_dim // 2], sine[:, head_dim // 2 :]], axis=1)
    gain_q, gain_k = query_gain.astype(full)[None], key_gain.astype(full)[None]
    attended, roped_q, roped_k, values_low = attend(
        projected, cosine, sine, gain_q, gain_k, kv_heads, group
    )
    branch = mul(attended, out_all)
    inputs = tokens.astype(full)
    mixed = (
        inputs
        + of_block(branch, rank)
        + swap_ctx(of_block(branch, 1 - rank).astype(low)).astype(full)
    )
    low_mid = rms_scale(mixed, moe_all).astype(low)
    m_all = lax.all_gather(jnp.concatenate([low_mid, swap_ctx(low_mid)]), "fsdp", axis=0, tiled=True)

    logits = mul(low_mid, router_all)
    named = routes[:, :, None] == jnp.arange(experts_all, dtype=jnp.int32)[None, None, :]
    selected = jnp.sum(jnp.where(named, logits[:, None, :], 0.0), axis=2)
    gates = gating(selected)
    chosen = jnp.any(named, axis=1)
    gates_wide = jnp.sum(jnp.where(named, gates[:, :, None], 0.0), axis=1)
    gates_sent = jnp.where(chosen, gates_wide, -1.0).T
    gates_all = lax.all_to_all(gates_sent, both, split_axis=0, concat_axis=0, tiled=True)

    g_all, gates_all = hold(g_all, gates_all)
    g_far = swap_ctx(g_all[..., :late_cols])

    lines = fsdp // 4
    places = list(range(1, lines)) + [0]
    cut = lines // 2
    parts = [places[:cut], places[cut:]]
    m_all = m_all.reshape(fsdp // 2, 2, 2, rows_dev, width)
    gates_all = gates_all.reshape(fsdp // 2, 2, 2, 1, rows_dev)
    state = dict(kept=None, first=0, core=core[None].astype(jnp.int32))

    def order_of(steps):
        spots = [((place - p) % lines) * 2 + (side + d) % 2 for d, _, p in steps]
        far = [i for i, step in enumerate(steps) if step[1] == 1] or [0]
        return jnp.stack(
            [
                jnp.asarray(item, jnp.int32)
                for i, step in enumerate(steps)
                for item in (
                    spots[i],
                    (rank + step[1]) % 2,
                    step[1],
                    spots[min(far, key=lambda j, i=i: abs(j - i))],
                )
            ]
        )

    def call(steps, raw=False):
        keep_back, send_back, *kept = run_expert(
            state["core"],
            order_of(steps),
            state["first"],
            4 * lines,
            m_all,
            g_all,
            g_far,
            gates_all,
            expert_gate_up[0],
            expert_down[0],
            capacity,
            state["kept"],
        )
        state["kept"] = kept
        state["first"] += len(steps)
        return (keep_back, send_back) if raw else over_core(keep_back, send_back)

    def wait(first):
        state["core"], first = hold(state["core"], first)
        return first

    steps_far, steps_own = ([(d, d, p) for p in places] for d in (1, 0))
    steps_mixed = [[(1, 0, p) for p in part] + [(0, 1, p) for p in part] for part in parts]
    back = call(steps_far)
    far_one, far_two = wait([pick_sum(back, 0, lines, column) for column in range(2)])
    far_one, far_two = swap_ctx(far_one), swap_side(far_two)

    def mixed_sums(back, at=0):
        return [
            pick_sum(back, start, start + cut, column) for start in (at, at + cut) for column in range(2)
        ]

    def rounds(sums, part):
        side_one, side_two, ctx_one, ctx_two = sums
        span = slice(part * cut, (part + 1) * cut)
        return [
            swap_ctx(ctx_one),
            swap_side(side_two),
            swap_side(add_low(side_one, far_one[span])),
            swap_ctx(add_low(ctx_two, far_two[span])),
        ]

    keep, send = call(steps_mixed[0], raw=True)
    send, (far_one, far_two) = hold(send, (far_one, far_two))
    back = over_core(keep, send)
    back_own = call(steps_own)
    sums = wait(mixed_sums(back))
    back_own = [pick_sum(back_own, 0, lines, column) for column in range(2)]
    got = rounds(sums, 0)
    keep, send = call(steps_mixed[1], raw=True)
    send, got = hold(send, got)
    back = over_core(keep, send)
    entries = joined(parts[0], [item[:cut] for item in back_own], got)
    arrived = {p: line_shift(entries[p], lines - p) for p in parts[0]}
    gate_back, rows, grad_rows, hidden, grad_pair = state["kept"]
    hidden, sums = hold(hidden, mixed_sums(back))
    got = rounds(sums, 1)
    grad_gates = lax.all_to_all(
        gate_back.reshape(fsdp * 2, rows_dev), both, split_axis=0, concat_axis=0, tiled=True
    ).T
    out_far = run_result(state["core"], order_of(steps_far), 0, hidden, gates_all, expert_down[0], capacity)
    out_rest = run_result(
        state["core"],
        order_of(steps_mixed[0] + steps_own + steps_mixed[1]),
        lines,
        hidden,
        gates_all,
        expert_down[0],
        capacity,
    )
    got, out_far, out_rest, arrived = lax.optimization_barrier((got, out_far, out_rest, arrived))
    entries.update(joined(parts[1], [item[cut:] for item in back_own], got))
    out_far = over_core(*out_far)
    out_far = [
        swap_ctx(pick_sum(out_far, 0, lines, 0)),
        swap_side(pick_sum(out_far, 0, lines, 1)),
    ]
    out_rest = over_core(*out_rest)
    for p in parts[1][:-1]:
        arrived[p] = line_shift(entries[p], lines - p)
    grad_mid = line_total(entries[0], arrived)

    grad_wide = jnp.where(chosen, grad_gates, 0.0)
    grad_logits = (
        gates_wide * (grad_wide - jnp.sum(gates_wide * grad_wide, axis=1, keepdims=True))
    ).astype(low)
    grad_router = mul(low_mid, grad_logits, lhs_turned)
    grad_mid = grad_mid + mul(grad_logits, router_all, rhs_turned)
    grad_mixed_part, grad_moe_gain = rms_back(mixed, moe_all, grad_mid)
    grad_mixed = cotangent.astype(full) + grad_mixed_part

    low_mixed, (out_far, out_rest) = hold(grad_mixed.astype(low), (out_far, out_rest))
    grad_branch = sequence(low_mixed)
    out_sums = [
        jnp.concatenate([one, two])
        for one, two in zip(mixed_sums(out_rest), mixed_sums(out_rest, 2 * cut + lines))
    ]
    out_own = [pick_sum(out_rest, 2 * cut, 2 * cut + lines, column) for column in range(2)]
    (out_sums, out_own), grad_branch = hold((out_sums, out_own), grad_branch)
    side_one, side_two, ctx_one, ctx_two = out_sums
    got = [
        swap_ctx(ctx_one),
        swap_side(side_two),
        add_low(side_one, out_far[0]),
        add_low(ctx_two, out_far[1]),
    ]
    grad_attended = mul(grad_branch, out_all, rhs_turned).astype(low)
    grad_out_part = mul(attended, grad_branch, lhs_turned).astype(low)
    grad_q, grad_k, grad_v, gain_q_part, gain_k_part = attend_grad(
        projected, roped_q, roped_k, values_low, grad_attended, cosine, sine, gain_q, gain_k, kv_heads, group
    )
    grad_projected = jnp.concatenate([grad_q, grad_k, grad_v], axis=1)
    grad_projected, got = hold(grad_projected, got)
    got[2], got[3] = swap_side(got[2]), swap_ctx(got[3])
    grad_qkv_part = mul(low_in, grad_projected, lhs_turned).astype(low)
    grad_normed_part = mul(grad_projected, qkv_all, rhs_turned)
    grad_normed_part, got = hold(grad_normed_part, got)
    entries = joined(places, out_own, got)
    (rows, grad_pair, hidden, grad_rows), entries = hold((rows, grad_pair, hidden, grad_rows), entries)
    grad_gate_up = mul(rows, grad_pair, lhs_turned)[None]
    grad_down = mul(hidden, grad_rows, lhs_turned)[None]
    output = (mixed + line_sum(entries, lines)).astype(low)
    grad_normed = of_block(grad_normed_part, rank) + swap_ctx(
        of_block(grad_normed_part, 1 - rank).astype(low)
    ).astype(full)
    grad_in_part, grad_attn_gain = rms_back(inputs, attn_all, grad_normed)
    grad_tokens = grad_mixed + grad_in_part

    out_mine = lax.psum_scatter(grad_out_part, "fsdp", scatter_dimension=0, tiled=True).astype(full)
    out_other = swap_ctx(out_mine.astype(low)).astype(full)
    grad_out = jnp.where(
        rank == 0,
        jnp.concatenate([out_mine, out_other], axis=0),
        jnp.concatenate([out_other, out_mine], axis=0),
    )
    qkv_mine = lax.psum_scatter(grad_qkv_part, "fsdp", scatter_dimension=0, tiled=True)
    grad_qkv = all_heads(rank_at, qkv_mine, swap_ctx(qkv_mine), head_dim, my_heads)
    early = sum_owned(jnp.concatenate([grad_router.T, grad_moe_gain[None]], axis=0), fsdp, spot)
    late = sum_all(
        jnp.concatenate(
            [
                grad_attn_gain.reshape(-1, head_dim),
                jnp.sum(gain_q_part, axis=0),
                jnp.sum(gain_k_part, axis=0),
            ],
            axis=0,
        ),
        fsdp,
    )
    gain_rows = width // head_dim
    return (
        output,
        grad_tokens,
        grad_qkv,
        grad_out,
        early[:experts_all].T,
        lax.dynamic_slice_in_dim(late[:gain_rows].reshape(-1), spot * shard, shard, 0),
        early[experts_all],
        late[gain_rows],
        late[gain_rows + 1],
        grad_gate_up,
        grad_down,
    )


gathered_bytes = 1 << 26


def choose_body(*args):
    tokens, gate_up = args[0], args[8]
    fsdp, ctx = lax.axis_size("fsdp"), lax.axis_size("ctx")
    fits = tokens.size * tokens.dtype.itemsize * fsdp * ctx <= gathered_bytes
    if fits and fsdp % 4 == 0 and ctx == 2 and fsdp >= 8 and fsdp & (fsdp - 1) == 0 and gate_up.shape[0] == 1:
        return body_gathered(*args)
    return body_routed(*args)


def solution(mesh):
    in_specs = (
        P(("fsdp", "ctx"), None),
        P("fsdp", None),
        P("fsdp", None),
        P("fsdp", None),
        P("fsdp"),
        P("fsdp"),
        P(),
        P(),
        P(("fsdp", "ctx"), None, None),
        P(("fsdp", "ctx"), None, None),
        P(("fsdp", "ctx"), None),
        P(("fsdp", "ctx"), None),
    )
    out_specs = (
        P(("fsdp", "ctx"), None),
        P(("fsdp", "ctx"), None),
        P("fsdp", None),
        P("fsdp", None),
        P("fsdp", None),
        P("fsdp"),
        P("fsdp"),
        P(),
        P(),
        P(("fsdp", "ctx"), None, None),
        P(("fsdp", "ctx"), None, None),
    )
    return jax.shard_map(choose_body, mesh=mesh, in_specs=in_specs, out_specs=out_specs, check_vma=False)
```

```python
import functools
import math

import jax
import jax.numpy as jnp
from jax import lax
from jax.experimental import pallas as pl
from jax.experimental.pallas import tpu as pltpu
from jax.sharding import PartitionSpec as P

eps_norm = 1e-06
theta_base = 1000000.0


def rms_scale(values, gain):
    return values * lax.rsqrt(jnp.mean(values * values, axis=-1, keepdims=True) + eps_norm) * gain


def rotate(values, cosine, sine):
    half_width = values.shape[-1] // 2
    turned = jnp.concatenate([-values[..., half_width:], values[..., :half_width]], axis=-1)
    return values * cosine + turned * sine


def angles(positions, width):
    freqs = theta_base ** (-(jnp.arange(width // 2, dtype=jnp.float32) * 2.0) / width)
    phase = positions.astype(jnp.float32)[:, None] * freqs[None, :]
    phase = jnp.concatenate([phase, phase], axis=-1)
    return (jnp.cos(phase)[:, None, :], jnp.sin(phase)[:, None, :])


def device_positions(block_rank, ctx_count, tok_rows):
    half_rows = tok_rows // 2
    within = jnp.arange(tok_rows, dtype=jnp.int32)
    span_id = jnp.where(within < half_rows, block_rank, 2 * ctx_count - 1 - block_rank)
    return span_id * half_rows + within % half_rows


def attend_head(query, keys_in, values_in, causal, scale_root):
    scores = (
        jnp.einsum("tgd,sd->gts", query, keys_in, preferred_element_type=jnp.float32) / scale_root
    )
    expo = jnp.where(causal[None], jnp.exp(scores), 0.0)
    totals = jnp.sum(expo, axis=-1, keepdims=True)
    probs = (expo / totals).astype(jnp.bfloat16)
    attended = jnp.einsum("gts,sd->tgd", probs, values_in, preferred_element_type=jnp.float32)
    return (attended, jnp.log(totals[..., 0]))


def attend_back(query, keys_in, values_in, causal, log_total, grad_attended, scale_root):
    scores = (
        jnp.einsum("tgd,sd->gts", query, keys_in, preferred_element_type=jnp.float32) / scale_root
    )
    probs = jnp.where(causal[None], jnp.exp(scores - log_total[..., None]), 0.0)
    low_probs = probs.astype(jnp.bfloat16)
    grad_values = jnp.einsum(
        "gts,tgd->sd", low_probs, grad_attended, preferred_element_type=jnp.float32
    )
    grad_probs = jnp.einsum(
        "tgd,sd->gts", grad_attended, values_in, preferred_element_type=jnp.float32
    )
    delta_rows = jnp.sum(grad_probs * probs, axis=-1, keepdims=True)
    grad_scores = (probs * (grad_probs - delta_rows)).astype(jnp.bfloat16)
    grad_query = (
        jnp.einsum("gts,sd->tgd", grad_scores, keys_in, preferred_element_type=jnp.float32)
        / scale_root
    )
    grad_keys = (
        jnp.einsum("gts,tgd->sd", grad_scores, query, preferred_element_type=jnp.float32)
        / scale_root
    )
    return (grad_query, grad_keys, grad_values)


def swiglu(paired):
    half_width = paired.shape[-1] // 2
    return jax.nn.silu(paired[..., :half_width]) * paired[..., half_width:]


def gating(selected):
    expo = jnp.exp(selected)
    return expo / jnp.sum(expo, axis=1, keepdims=True)


def body_routed(
    tokens,
    qkv_weight,
    out_weight,
    router_weight,
    attn_gain,
    moe_gain,
    query_gain,
    key_gain,
    expert_gate_up,
    expert_down,
    routes,
    cotangent,
):
    rows_dev, width = tokens.shape
    head_dim = query_gain.shape[0]
    top_k = routes.shape[1]
    ctx_count = lax.axis_size("ctx")
    ctx_rank = lax.axis_index("ctx")
    qkv_all, out_all, router_all, attn_all, moe_all = (
        lax.all_gather(qkv_weight, "fsdp", axis=0, tiled=True),
        lax.all_gather(out_weight, "fsdp", axis=0, tiled=True),
        lax.all_gather(router_weight, "fsdp", axis=0, tiled=True),
        lax.all_gather(attn_gain, "fsdp", axis=0, tiled=True),
        lax.all_gather(moe_gain, "fsdp", axis=0, tiled=True),
    )
    experts_all = router_all.shape[1]
    heads = out_all.shape[0] // head_dim
    kv_heads = (qkv_all.shape[1] // head_dim - heads) // 2
    group_size = heads // kv_heads
    capacity = 2 * rows_dev * top_k // experts_all
    width_q = heads * head_dim
    width_k = kv_heads * head_dim
    scale_root = math.sqrt(head_dim)
    inputs = tokens.astype(jnp.float32)
    normed_in = rms_scale(inputs, attn_all.astype(jnp.float32))
    low_in = normed_in.astype(jnp.bfloat16)
    projected = jnp.dot(low_in, qkv_all, preferred_element_type=jnp.float32)
    query_raw = projected[:, :width_q].reshape(rows_dev, heads, head_dim)
    key_raw = projected[:, width_q : width_q + width_k].reshape(rows_dev, kv_heads, head_dim)
    value_low = (
        projected[:, width_q + width_k :].astype(jnp.bfloat16).reshape(rows_dev, kv_heads, head_dim)
    )
    positions = device_positions(ctx_rank, ctx_count, rows_dev)
    cosine, sine = angles(positions, head_dim)
    query_gain_f = query_gain.astype(jnp.float32)
    key_gain_f = key_gain.astype(jnp.float32)

    def query_rope(values_in, gain):
        return rotate(rms_scale(values_in, gain), cosine, sine)

    query_low = query_rope(query_raw, query_gain_f).astype(jnp.bfloat16)
    key_low = query_rope(key_raw, key_gain_f).astype(jnp.bfloat16)
    keys_all, values_all = (
        lax.all_gather(key_low, "ctx", axis=0, tiled=True),
        lax.all_gather(value_low, "ctx", axis=0, tiled=True),
    )
    key_pos = jnp.concatenate(
        [device_positions(other, ctx_count, rows_dev) for other in range(ctx_count)]
    )
    causal = key_pos[None, :] <= positions[:, None]
    query_heads = query_low.reshape(rows_dev, kv_heads, group_size, head_dim).transpose(1, 0, 2, 3)
    key_heads = keys_all.transpose(1, 0, 2)
    value_heads = values_all.transpose(1, 0, 2)
    attended, log_total = lax.map(
        lambda member: attend_head(member[0], member[1], member[2], causal, scale_root),
        (query_heads, key_heads, value_heads),
    )
    attended_low = attended.transpose(1, 0, 2, 3).reshape(rows_dev, width_q).astype(jnp.bfloat16)
    mixed = inputs + jnp.dot(attended_low, out_all, preferred_element_type=jnp.float32)
    normed_mid = rms_scale(mixed, moe_all.astype(jnp.float32))
    low_mid = normed_mid.astype(jnp.bfloat16)
    logits = jnp.dot(low_mid, router_all, preferred_element_type=jnp.float32)
    selected = jnp.take_along_axis(logits, routes, axis=1)
    gates, gate_back = jax.vjp(gating, selected)
    flat_routes = routes.reshape(-1)
    expert_ids = jnp.arange(experts_all, dtype=jnp.int32)
    hit_table = (flat_routes[:, None] == expert_ids[None, :]).astype(jnp.int32)
    slot_index = jnp.sum(jnp.cumsum(hit_table, axis=0) * hit_table, axis=1) - 1
    target = flat_routes * capacity + slot_index
    pair_count = rows_dev * top_k
    source_pair = (
        jnp.full((experts_all * capacity,), pair_count, jnp.int32)
        .at[target]
        .set(jnp.arange(pair_count, dtype=jnp.int32))
    )
    padded = jnp.concatenate([low_mid, jnp.zeros((1, width), jnp.bfloat16)], axis=0)
    outgoing = padded[source_pair // top_k].reshape(experts_all, capacity, width)
    received = lax.all_to_all(outgoing, ("fsdp", "ctx"), split_axis=0, concat_axis=1, tiled=True)
    gate_and_up = jnp.einsum(
        "esd,edf->esf", received, expert_gate_up, preferred_element_type=jnp.float32
    )
    hidden_val, swiglu_back = jax.vjp(swiglu, gate_and_up)
    hidden_low = hidden_val.astype(jnp.bfloat16)
    result_low = jnp.einsum(
        "esf,efd->esd", hidden_low, expert_down, preferred_element_type=jnp.float32
    ).astype(jnp.bfloat16)
    returned = lax.all_to_all(
        result_low, ("fsdp", "ctx"), split_axis=1, concat_axis=0, tiled=True
    ).reshape(experts_all * capacity, width)
    picked = returned[target].reshape(rows_dev, top_k, width).astype(jnp.float32)
    output = (mixed + jnp.sum(gates[:, :, None] * picked, axis=1)).astype(jnp.bfloat16)
    qkv_back, out_back, router_back, attn_back_g, moe_back_g = (
        qkv_all,
        out_all,
        router_all,
        attn_all,
        moe_all,
    )
    grad_final = cotangent.astype(jnp.float32)
    grad_gates = jnp.sum(grad_final[:, None, :] * picked, axis=2)
    grad_result = (
        (gates[:, :, None] * grad_final[:, None, :]).astype(jnp.bfloat16).reshape(pair_count, width)
    )
    grad_padded = jnp.concatenate([grad_result, jnp.zeros((1, width), jnp.bfloat16)], axis=0)
    grad_outgoing = grad_padded[source_pair].reshape(experts_all, capacity, width)
    grad_received = lax.all_to_all(
        grad_outgoing, ("fsdp", "ctx"), split_axis=0, concat_axis=1, tiled=True
    )
    grad_down = jnp.einsum(
        "esf,esd->efd", hidden_low, grad_received, preferred_element_type=jnp.float32
    )
    grad_hidden = jnp.einsum(
        "esd,efd->esf", grad_received, expert_down, preferred_element_type=jnp.float32
    )
    grad_paired = swiglu_back(grad_hidden)[0].astype(jnp.bfloat16)
    grad_gate_up = jnp.einsum(
        "esd,esf->edf", received, grad_paired, preferred_element_type=jnp.float32
    )
    grad_rows = jnp.einsum(
        "esf,edf->esd", grad_paired, expert_gate_up, preferred_element_type=jnp.float32
    ).astype(jnp.bfloat16)
    grad_returned = lax.all_to_all(
        grad_rows, ("fsdp", "ctx"), split_axis=1, concat_axis=0, tiled=True
    ).reshape(experts_all * capacity, width)
    grad_mid = jnp.sum(
        grad_returned[target].reshape(rows_dev, top_k, width).astype(jnp.float32), axis=1
    )
    grad_selected = gate_back(grad_gates)[0]
    route_table = (routes[:, :, None] == expert_ids[None, None, :]).astype(jnp.float32)
    grad_logits = jnp.sum(route_table * grad_selected[:, :, None], axis=1).astype(jnp.bfloat16)
    grad_router = jnp.dot(low_mid.T, grad_logits, preferred_element_type=jnp.float32)
    grad_mid = grad_mid + jnp.dot(grad_logits, router_back.T, preferred_element_type=jnp.float32)
    unused_mid, mid_back = jax.vjp(rms_scale, mixed, moe_back_g.astype(jnp.float32))
    grad_mixed_part, grad_moe_gain = mid_back(grad_mid)
    grad_mixed = grad_final + grad_mixed_part
    grad_branch = grad_mixed.astype(jnp.bfloat16)
    grad_out = jnp.dot(attended_low.T, grad_branch, preferred_element_type=jnp.float32)
    grad_attended = jnp.dot(grad_branch, out_back.T, preferred_element_type=jnp.float32).astype(
        jnp.bfloat16
    )
    grad_heads = grad_attended.reshape(rows_dev, kv_heads, group_size, head_dim).transpose(
        1, 0, 2, 3
    )
    grad_query_h, grad_key_h, grad_value_h = lax.map(
        lambda member: attend_back(
            member[0], member[1], member[2], causal, member[3], member[4], scale_root
        ),
        (query_heads, key_heads, value_heads, log_total, grad_heads),
    )
    grad_keys, grad_values = (
        lax.psum_scatter(
            grad_key_h.transpose(1, 0, 2).astype(jnp.bfloat16),
            "ctx",
            scatter_dimension=0,
            tiled=True,
        ).astype(jnp.float32),
        lax.psum_scatter(
            grad_value_h.transpose(1, 0, 2).astype(jnp.bfloat16),
            "ctx",
            scatter_dimension=0,
            tiled=True,
        ).astype(jnp.float32),
    )
    grad_query_rot = (
        grad_query_h.transpose(1, 0, 2, 3).reshape(rows_dev, heads, head_dim).astype(jnp.bfloat16)
    )
    grad_query_rot = lax.optimization_barrier(grad_query_rot).astype(jnp.float32)
    grad_key_rot = lax.optimization_barrier(grad_keys.astype(jnp.bfloat16)).astype(jnp.float32)
    unused_query, query_back = jax.vjp(query_rope, query_raw, query_gain_f)
    grad_query_raw, grad_query_gain = query_back(grad_query_rot)
    unused_key, key_back = jax.vjp(query_rope, key_raw, key_gain_f)
    grad_key_raw, grad_key_gain = key_back(grad_key_rot)
    grad_projected = jnp.concatenate(
        [
            grad_query_raw.reshape(rows_dev, width_q).astype(jnp.bfloat16),
            grad_key_raw.reshape(rows_dev, width_k).astype(jnp.bfloat16),
            grad_values.reshape(rows_dev, width_k).astype(jnp.bfloat16),
        ],
        axis=1,
    )
    grad_qkv = jnp.dot(low_in.T, grad_projected, preferred_element_type=jnp.float32)
    grad_normed = jnp.dot(grad_projected, qkv_back.T, preferred_element_type=jnp.float32)
    unused_in, in_back = jax.vjp(rms_scale, inputs, attn_back_g.astype(jnp.float32))
    grad_in_part, grad_attn_gain = in_back(grad_normed)
    grad_tokens = grad_mixed + grad_in_part
    gradients = (grad_qkv, grad_out, grad_router, grad_attn_gain, grad_moe_gain)
    pieces = (
        lax.psum_scatter(gradients[0], "fsdp", scatter_dimension=0, tiled=True),
        lax.psum_scatter(gradients[1], "fsdp", scatter_dimension=0, tiled=True),
        lax.psum_scatter(gradients[2], "fsdp", scatter_dimension=0, tiled=True),
        lax.psum_scatter(gradients[3], "fsdp", scatter_dimension=0, tiled=True),
        lax.psum_scatter(gradients[4], "fsdp", scatter_dimension=0, tiled=True),
    )
    reduced = (
        lax.psum(pieces[0].astype(jnp.bfloat16), "ctx").astype(jnp.float32),
        lax.psum(pieces[1].astype(jnp.bfloat16), "ctx").astype(jnp.float32),
        lax.psum(pieces[2].astype(jnp.bfloat16), "ctx").astype(jnp.float32),
        lax.psum(pieces[3].astype(jnp.bfloat16), "ctx").astype(jnp.float32),
        lax.psum(pieces[4].astype(jnp.bfloat16), "ctx").astype(jnp.float32),
    )
    gain_sums = lax.psum((grad_query_gain, grad_key_gain), ("fsdp", "ctx"))
    return (
        output,
        grad_tokens,
        reduced[0],
        reduced[1],
        reduced[2],
        reduced[3],
        reduced[4],
        gain_sums[0],
        gain_sums[1],
        grad_gate_up,
        grad_down,
    )


low = jnp.bfloat16
full = jnp.float32
plain = (((1,), (0,)), ((), ()))
rhs_turned = (((1,), (1,)), ((), ()))
lhs_turned = (((0,), (0,)), ((), ()))
vmem_bytes = 58 << 20


def mul(left, right, dims=plain):
    return lax.dot_general(left, right, dims, preferred_element_type=full)


def core_pairs(fsdp):
    return [(i, i ^ 1) for i in range(fsdp)]


def side_pairs(fsdp):
    return [(i, i ^ 2) for i in range(fsdp)]


def swap_core(values):
    return lax.ppermute(values, "fsdp", core_pairs(lax.axis_size("fsdp")))


def swap_side(values):
    return lax.ppermute(values, "fsdp", side_pairs(lax.axis_size("fsdp")))


def swap_ctx(values):
    return lax.ppermute(values, "ctx", [(0, 1), (1, 0)])


def add_low(one, two):
    return (one.astype(full) + two.astype(full)).astype(low)


def hold(values, first):
    return lax.optimization_barrier((values, first))


def take(values, index):
    return lax.dynamic_index_in_dim(values, index, 0, keepdims=False)


def line_shift(values, step):
    fsdp = lax.axis_size("fsdp")
    return lax.ppermute(values, "fsdp", [(i, (i + 4 * step) % fsdp) for i in range(fsdp)])


def line_total(own, arrived):
    total = own.astype(full)
    for item in arrived.values():
        total = total + item.astype(full)
    return total


def joined(places, own, got):
    from_ctx, from_side, one_side, two_ctx = got
    entries = {}
    for at, p in enumerate(places):
        one = add_low(add_low(own[0][at], from_ctx[at]), one_side[at])
        two = add_low(add_low(own[1][at], from_side[at]), two_ctx[at])
        entries[p] = jnp.concatenate([one, two], axis=-1)
    return entries


def over_core(keep, send):
    return keep, swap_core(send)


def pick_sum(parts, start, stop, column):
    keep, other = parts
    half = keep.shape[-1] // 2
    cut = (slice(start, stop), slice(None), slice(column * half, (column + 1) * half))
    return add_low(keep[cut], other[cut])


def sum_all(values, fsdp):
    values = values + lax.ppermute(values, "fsdp", core_pairs(fsdp))
    values = values + swap_ctx(values)
    step = 2
    while step < fsdp:
        values = values + lax.ppermute(values, "fsdp", [(i, i ^ step) for i in range(fsdp)])
        step *= 2
    return values


def sum_owned(values, fsdp, spot):
    items, shard = values.shape[0], values.shape[1] // fsdp
    values = values.reshape(items, fsdp, shard).swapaxes(0, 1)
    step = fsdp // 2
    while step:
        bit = (spot // step) % 2
        values = values.reshape(2, step, items, shard)
        other = lax.ppermute(take(values, 1 - bit), "fsdp", [(i, i ^ step) for i in range(fsdp)])
        values = take(values, bit) + other
        step //= 2
    values = values[0]
    return values + swap_ctx(values)


def turn(values):
    return pltpu.roll(values, values.shape[-1] // 2, 1)


def norm_rope(raw, gain, cosine, sine):
    scale = lax.rsqrt(jnp.mean(raw * raw, axis=-1, keepdims=True) + eps_norm)
    scaled = raw * scale * gain
    return scaled * cosine + turn(scaled) * sine


def norm_rope_back(raw, gain, cosine, sine, grad):
    scale = lax.rsqrt(jnp.mean(raw * raw, axis=-1, keepdims=True) + eps_norm)
    unit = raw * scale
    grad_scaled = grad * cosine - turn(grad) * sine
    grad_gain = jnp.sum(grad_scaled * unit, axis=0, keepdims=True)
    grad_unit = grad_scaled * gain
    grad_raw = scale * (grad_unit - unit * jnp.mean(grad_unit * unit, axis=-1, keepdims=True))
    return grad_raw, grad_gain


def tiles_of(rows):
    step = rows // 2
    return [(start, start + step) for start in range(0, rows, step)]


def allowed(start, stop):
    shape = (stop - start, stop)
    return lax.broadcasted_iota(jnp.int32, shape, 1) <= (
        lax.broadcasted_iota(jnp.int32, shape, 0) + start
    )


def attend_kernel(q_ref, k_ref, v_ref, cos_ref, sin_ref, qg_ref, kg_ref, o_ref, qr_ref, kr_ref, vl_ref):
    head_dim = k_ref.shape[1]
    rows = k_ref.shape[0]
    cosine, sine = cos_ref[...], sin_ref[...]
    keys = norm_rope(k_ref[...], kg_ref[...], cosine, sine).astype(low)
    values = v_ref[...].astype(low)
    kr_ref[...] = keys
    vl_ref[...] = values
    for head in range(q_ref.shape[1] // head_dim):
        cols = slice(head * head_dim, (head + 1) * head_dim)
        query = norm_rope(q_ref[:, cols], qg_ref[...], cosine, sine).astype(low)
        qr_ref[:, cols] = query
        for start, stop in tiles_of(rows):
            scores = mul(query[start:stop], keys[:stop], rhs_turned) * (1.0 / math.sqrt(head_dim))
            expo = jnp.where(allowed(start, stop), jnp.exp(scores), 0.0)
            probs = (expo / jnp.sum(expo, axis=-1, keepdims=True)).astype(low)
            o_ref[start:stop, cols] = mul(probs, values[:stop]).astype(low)


def attend_grad_kernel(
    q_ref, k_ref, qr_ref, kr_ref, vl_ref, go_ref, cos_ref, sin_ref, qg_ref, kg_ref,
    dq_ref, dk_ref, dv_ref, dqg_ref, dkg_ref, dk_sum, dv_sum, dq_sum,
):
    head_dim = k_ref.shape[1]
    rows = k_ref.shape[0]
    root = 1.0 / math.sqrt(head_dim)
    cosine, sine = cos_ref[...], sin_ref[...]
    keys, values = kr_ref[...], vl_ref[...]
    gain_sum = jnp.zeros((1, head_dim), full)
    dk_sum[...] = jnp.zeros_like(dk_sum)
    dv_sum[...] = jnp.zeros_like(dv_sum)
    for head in range(q_ref.shape[1] // head_dim):
        cols = slice(head * head_dim, (head + 1) * head_dim)
        for start, stop in tiles_of(rows):
            query = qr_ref[start:stop, cols]
            grad = go_ref[start:stop, cols]
            scores = mul(query, keys[:stop], rhs_turned) * root
            expo = jnp.where(allowed(start, stop), jnp.exp(scores), 0.0)
            probs = expo / jnp.sum(expo, axis=-1, keepdims=True)
            grad_probs = mul(grad, values[:stop], rhs_turned)
            delta = jnp.sum(grad_probs * probs, axis=-1, keepdims=True)
            grad_scores = (probs * (grad_probs - delta)).astype(low)
            dv_sum[:stop] += mul(probs.astype(low), grad, lhs_turned)
            dk_sum[:stop] += mul(grad_scores, query, lhs_turned)
            dq_sum[start:stop] = mul(grad_scores, keys[:stop])
        grad_query = (dq_sum[...] * root).astype(low).astype(full)
        grad_raw, grad_gain = norm_rope_back(q_ref[:, cols], qg_ref[...], cosine, sine, grad_query)
        dq_ref[:, cols] = grad_raw.astype(low)
        gain_sum = gain_sum + grad_gain
    dqg_ref[0] = gain_sum
    grad_key = (dk_sum[...] * root).astype(low).astype(full)
    grad_raw, grad_gain = norm_rope_back(k_ref[...], kg_ref[...], cosine, sine, grad_key)
    dk_ref[...] = grad_raw.astype(low)
    dkg_ref[0] = grad_gain
    dv_ref[...] = dv_sum[...].astype(low)


def attention_specs(rows, head_dim, kv_heads, group):
    wide, narrow = group * head_dim, head_dim
    heads_end = kv_heads * group
    return dict(
        q=pl.BlockSpec((rows, wide), lambda i: (0, i)),
        k=pl.BlockSpec((rows, narrow), lambda i: (0, heads_end + i)),
        v=pl.BlockSpec((rows, narrow), lambda i: (0, heads_end + kv_heads + i)),
        own=pl.BlockSpec((rows, narrow), lambda i: (0, i)),
        table=pl.BlockSpec((rows, head_dim), lambda i: (0, 0)),
        gain=pl.BlockSpec((1, head_dim), lambda i: (0, 0)),
        gain_out=pl.BlockSpec((1, 1, head_dim), lambda i: (i, 0, 0)),
    )


def attend(projected, cosine, sine, query_gain, key_gain, kv_heads, group):
    rows, head_dim = cosine.shape
    s = attention_specs(rows, head_dim, kv_heads, group)
    shape = jax.ShapeDtypeStruct
    work = rows * rows * head_dim * kv_heads * group
    return pl.pallas_call(
        attend_kernel,
        grid=(kv_heads,),
        in_specs=[s["q"], s["k"], s["v"], s["table"], s["table"], s["gain"], s["gain"]],
        out_specs=[s["q"], s["q"], s["own"], s["own"]],
        out_shape=[
            shape((rows, kv_heads * group * head_dim), low),
            shape((rows, kv_heads * group * head_dim), low),
            shape((rows, kv_heads * head_dim), low),
            shape((rows, kv_heads * head_dim), low),
        ],
        compiler_params=pltpu.CompilerParams(vmem_limit_bytes=48 << 20),
        cost_estimate=pl.CostEstimate(
            flops=4 * work, bytes_accessed=projected.size * 6, transcendentals=work // head_dim
        ),
        name="attend",
    )(projected, projected, projected, cosine, sine, query_gain, key_gain)


def attend_grad(projected, roped_q, roped_k, values_low, grad, cosine, sine, query_gain, key_gain, kv_heads, group):
    rows, head_dim = cosine.shape
    s = attention_specs(rows, head_dim, kv_heads, group)
    shape = jax.ShapeDtypeStruct
    work = rows * rows * head_dim * kv_heads * group
    return pl.pallas_call(
        attend_grad_kernel,
        grid=(kv_heads,),
        in_specs=[
            s["q"], s["k"], s["q"], s["own"], s["own"], s["q"],
            s["table"], s["table"], s["gain"], s["gain"],
        ],
        out_specs=[s["q"], s["own"], s["own"], s["gain_out"], s["gain_out"]],
        out_shape=[
            shape((rows, kv_heads * group * head_dim), low),
            shape((rows, kv_heads * head_dim), low),
            shape((rows, kv_heads * head_dim), low),
            shape((kv_heads, 1, head_dim), full),
            shape((kv_heads, 1, head_dim), full),
        ],
        scratch_shapes=[pltpu.VMEM((rows, head_dim), full)] * 3,
        compiler_params=pltpu.CompilerParams(vmem_limit_bytes=48 << 20),
        cost_estimate=pl.CostEstimate(
            flops=10 * work, bytes_accessed=projected.size * 10, transcendentals=work // head_dim
        ),
        name="attend_grad",
    )(projected, projected, roped_q, roped_k, values_low, grad, cosine, sine, query_gain, key_gain)


def placed(gate, slots):
    block = gate.shape[1]
    shape = (block, block)
    earlier = (
        lax.broadcasted_iota(jnp.int32, shape, 0) < lax.broadcasted_iota(jnp.int32, shape, 1)
    ).astype(low)
    hit = jnp.where(gate >= 0.0, 1.0, 0.0)
    count = mul(jnp.broadcast_to(hit, (8, block)).astype(low), earlier)[:1].astype(jnp.int32)
    place = (lax.broadcasted_iota(jnp.int32, (slots, block), 0) == count) & (hit > 0.5)
    weight = jnp.sum(jnp.where(place, gate, 0.0), axis=1, keepdims=True)
    return place, place.astype(full).astype(low), weight


def expert_kernel(core_ref, order, m_ref, g_ref, far_ref, w_ref, gu_ref, dn_ref, *refs):
    keep_back, send_back, gate_back, rows_ref, dy_ref, z_ref, pair_ref = refs[-7:]
    core = core_ref[0]
    far = order[4 * pl.program_id(0) + 2] == 1
    width = m_ref.shape[4]
    hidden = dn_ref.shape[0]
    slots = z_ref.shape[0] // 2
    places, picks, weights, rows, grads = [], [], [], [], []
    for part in range(2):
        at = lax.rem(core + part, 2)
        place, pick, weight = placed(w_ref[0, at, 0], slots)
        places.append(place)
        picks.append(pick)
        weights.append(weight)
        rows.append(mul(pick, m_ref[0, at, 0]).astype(low))
        near_rows = g_ref[0, at, :, :width]
        far_rows = jnp.concatenate([far_ref[0, at], g_ref[0, at, :, width:]], axis=1)
        grads.append(mul(pick, jnp.where(far, far_rows, near_rows)).astype(low))
    row, grad, weight = (jnp.concatenate(items, axis=0) for items in (rows, grads, weights))
    rows_ref[...] = row
    paired = mul(row, gu_ref[...])
    gate_in, up = paired[:, :hidden], paired[:, hidden:]
    sig = jax.nn.sigmoid(gate_in)
    act = gate_in * sig
    z = (act * up).astype(low)
    z_ref[...] = z
    dy_ref[...] = (weight * grad.astype(full)).astype(low)
    unweighted = mul(grad, dn_ref[...], rhs_turned)
    grad_gate = jnp.sum(unweighted * z.astype(full), axis=1, keepdims=True)
    dz = weight * unweighted
    grad_in = dz * up * (sig * (1.0 + gate_in * (1.0 - sig)))
    pair = jnp.concatenate([grad_in, dz * act], axis=1).astype(low)
    pair_ref[...] = pair
    back = mul(pair, gu_ref[...], rhs_turned).astype(low)
    for part, out in enumerate((keep_back, send_back)):
        mine = slice(part * slots, (part + 1) * slots)
        out[0] = mul(picks[part], back[mine], lhs_turned).astype(low)
        gate_back[0, lax.rem(core + part, 2), 0] = jnp.sum(
            jnp.where(places[part], grad_gate[mine], 0.0), axis=0, keepdims=True
        )


def run_expert(core, order, first, total_steps, m_all, g_all, g_far, gates_all, gate_up, down, slots, kept):
    places, _, _, block, width = m_all.shape
    paired = gate_up.shape[1]
    steps = order.shape[0] // 4
    part_rows = steps * 2 * slots
    hidden = paired // 2
    shape = jax.ShapeDtypeStruct

    def gates_at(i, core, order):
        return (order[4 * i], 0, order[4 * i + 1], 0, 0)

    def token_at(i, core, order):
        return (order[4 * i], 0, order[4 * i + 2], 0, 0)

    def near_at(i, core, order):
        return (order[4 * i], 0, 0, 0)

    def far_at(i, core, order):
        return (order[4 * i + 3], 0, 0, 0)

    def fixed(i, core, order):
        return (0, 0)

    def flat(i, core, order):
        return (first + i, 0)

    def stacked(i, core, order):
        return (i, 0, 0)

    small = pl.BlockSpec((1, 2, 1, 1, block), gates_at)
    one_block = pl.BlockSpec((1, block, width), stacked)
    widths = (width, width, hidden, paired)
    grid_spec = pltpu.PrefetchScalarGridSpec(
        num_scalar_prefetch=2,
        grid=(steps,),
        in_specs=[
            pl.BlockSpec((1, 2, 1, block, width), token_at),
            pl.BlockSpec((1, 2, block, g_all.shape[3]), near_at),
            pl.BlockSpec((1, 2, block, g_far.shape[3]), far_at),
            small,
            pl.BlockSpec(gate_up.shape, fixed, pipeline_mode=pl.Buffered(1)),
            pl.BlockSpec(down.shape, fixed, pipeline_mode=pl.Buffered(1)),
        ]
        + [pl.BlockSpec(memory_space=pl.ANY)] * (0 if kept is None else 5),
        out_specs=[one_block] * 2 + [small] + [pl.BlockSpec((2 * slots, n), flat) for n in widths],
    )
    return pl.pallas_call(
        expert_kernel,
        grid_spec=grid_spec,
        out_shape=[shape((steps, block, width), low)] * 2
        + [shape((places, 2, 2, 1, block), full)]
        + [shape((total_steps * 2 * slots, n), low) for n in widths],
        input_output_aliases={} if kept is None else {8 + i: 2 + i for i in range(5)},
        compiler_params=pltpu.CompilerParams(vmem_limit_bytes=vmem_bytes),
        cost_estimate=pl.CostEstimate(
            flops=part_rows * width * (4 * paired + 2 * hidden + 6 * block),
            bytes_accessed=steps * block * width * 12 + part_rows * (width * 4 + paired * 3),
            transcendentals=part_rows * hidden,
        ),
        name="experts",
    )(core, order, m_all, g_all, g_far, gates_all, gate_up, down, *(() if kept is None else kept))


def result_kernel(core_ref, order, z_ref, w_ref, dn_ref, keep_out, send_out):
    core = core_ref[0]
    slots = z_ref.shape[0] // 2
    y = mul(z_ref[...], dn_ref[...]).astype(low).astype(full)
    for part, out in enumerate((keep_out, send_out)):
        _, pick, weight = placed(w_ref[0, lax.rem(core + part, 2), 0], slots)
        scaled = (weight * y[part * slots : (part + 1) * slots]).astype(low)
        out[0] = mul(pick, scaled, lhs_turned).astype(low)


def run_result(core, order, first, hidden, gates_all, down, slots):
    block, width, inner = gates_all.shape[4], down.shape[1], down.shape[0]
    steps = order.shape[0] // 4
    one_block = pl.BlockSpec((1, block, width), lambda i, core, order: (i, 0, 0))
    return pl.pallas_call(
        result_kernel,
        grid_spec=pltpu.PrefetchScalarGridSpec(
            num_scalar_prefetch=2,
            grid=(steps,),
            in_specs=[
                pl.BlockSpec((2 * slots, inner), lambda i, core, order: (first + i, 0)),
                pl.BlockSpec(
                    (1, 2, 1, 1, block), lambda i, core, order: (order[4 * i], 0, order[4 * i + 1], 0, 0)
                ),
                pl.BlockSpec(down.shape, lambda i, core, order: (0, 0), pipeline_mode=pl.Buffered(1)),
            ],
            out_specs=[one_block] * 2,
        ),
        out_shape=[jax.ShapeDtypeStruct((steps, block, width), low)] * 2,
        compiler_params=pltpu.CompilerParams(vmem_limit_bytes=vmem_bytes),
        cost_estimate=pl.CostEstimate(
            flops=steps * 2 * slots * width * (2 * inner + 2 * block),
            bytes_accessed=steps * (4 * block * width + 4 * slots * inner) + 2 * inner * width,
            transcendentals=0,
        ),
        name="results",
    )(core, order, hidden, gates_all, down)


def own_heads_kernel(rank, qkv_ref, out_ref, o_ref, *, head_dim, heads):
    first = rank[0] == 0
    for head in range(heads):
        pair = [qkv_ref[:, (2 * head + i) * head_dim : (2 * head + i + 1) * head_dim] for i in range(2)]
        o_ref[:, head * head_dim : (head + 1) * head_dim] = jnp.where(first, pair[0], pair[1])
    kv = qkv_ref.shape[1] - 2 * heads * head_dim
    o_ref[:, heads * head_dim : heads * head_dim + kv] = qkv_ref[:, 2 * heads * head_dim :]
    o_ref[:, heads * head_dim + kv :] = jnp.where(first, out_ref[:head_dim], out_ref[head_dim:])


def own_heads(rank, qkv_weight, out_weight, head_dim, heads):
    kv = qkv_weight.shape[1] - 2 * heads * head_dim
    return pl.pallas_call(
        functools.partial(own_heads_kernel, head_dim=head_dim, heads=heads),
        grid_spec=pltpu.PrefetchScalarGridSpec(
            num_scalar_prefetch=1,
            grid=(1,),
            in_specs=[
                pl.BlockSpec(qkv_weight.shape, lambda i, rank: (0, 0)),
                pl.BlockSpec(out_weight.shape, lambda i, rank: (0, 0)),
            ],
            out_specs=pl.BlockSpec(
                (qkv_weight.shape[0], heads * head_dim + kv + out_weight.shape[1]), lambda i, rank: (0, 0)
            ),
        ),
        out_shape=jax.ShapeDtypeStruct(
            (qkv_weight.shape[0], heads * head_dim + kv + out_weight.shape[1]), qkv_weight.dtype
        ),
        name="own_heads",
    )(rank, qkv_weight, out_weight)


def all_heads_kernel(rank, mine_ref, other_ref, o_ref, *, head_dim, heads):
    first = rank[0] == 0
    for head in range(heads):
        cols = slice(head * head_dim, (head + 1) * head_dim)
        mine, other = mine_ref[:, cols].astype(full), other_ref[:, cols].astype(full)
        o_ref[:, 2 * head * head_dim : (2 * head + 1) * head_dim] = jnp.where(first, mine, other)
        o_ref[:, (2 * head + 1) * head_dim : (2 * head + 2) * head_dim] = jnp.where(first, other, mine)
    o_ref[:, 2 * heads * head_dim :] = mine_ref[:, heads * head_dim :].astype(full) + other_ref[
        :, heads * head_dim :
    ].astype(full)


def all_heads(rank, mine, other, head_dim, heads):
    rows, width = mine.shape
    return pl.pallas_call(
        functools.partial(all_heads_kernel, head_dim=head_dim, heads=heads),
        grid_spec=pltpu.PrefetchScalarGridSpec(
            num_scalar_prefetch=1,
            grid=(1,),
            in_specs=[pl.BlockSpec((rows, width), lambda i, rank: (0, 0))] * 2,
            out_specs=pl.BlockSpec((rows, width + heads * head_dim), lambda i, rank: (0, 0)),
        ),
        out_shape=jax.ShapeDtypeStruct((rows, width + heads * head_dim), full),
        name="all_heads",
    )(rank, mine, other)


def rms_back(values, gain, grad):
    scale = lax.rsqrt(jnp.mean(values * values, axis=-1, keepdims=True) + eps_norm)
    unit = values * scale
    grad_gain = jnp.sum(grad * unit, axis=0)
    grad_unit = grad * gain
    back = scale * (grad_unit - unit * jnp.mean(grad_unit * unit, axis=-1, keepdims=True))
    return back, grad_gain


def in_order(first, second):
    half = first.shape[0] // 2
    return jnp.concatenate([first[:half], second, first[half:]], axis=0)


def of_block(values, rank):
    quarter = values.shape[0] // 4
    outer = jnp.concatenate([values[:quarter], values[3 * quarter :]], axis=0)
    return jnp.where(rank == 0, outer, values[quarter : 3 * quarter])


def body_gathered(
    tokens, qkv_weight, out_weight, router_weight, attn_gain, moe_gain, query_gain, key_gain,
    expert_gate_up, expert_down, routes, cotangent,
):
    rows_dev, width = tokens.shape
    head_dim = query_gain.shape[0]
    top_k = routes.shape[1]
    fsdp = lax.axis_size("fsdp")
    spot = lax.axis_index("fsdp")
    rank = lax.axis_index("ctx")
    place, side, core = spot // 4, (spot // 2) % 2, spot % 2
    shard = qkv_weight.shape[0]
    heads = out_weight.shape[0] * fsdp // head_dim
    kv_heads = (qkv_weight.shape[1] // head_dim - heads) // 2
    group = heads // kv_heads // 2
    my_heads = heads // 2
    width_q, width_k = my_heads * head_dim, kv_heads * head_dim
    experts_all = router_weight.shape[1]
    capacity = 2 * rows_dev * top_k // experts_all
    both = ("fsdp", "ctx")

    def sequence(values):
        other = swap_ctx(values)
        first = jnp.where(rank == 0, values, other)
        second = jnp.where(rank == 0, other, values)
        return in_order(first, second)

    rank_at = rank[None].astype(jnp.int32)
    weights_local = own_heads(rank_at, qkv_weight, out_weight, head_dim, my_heads)
    small_local = jnp.concatenate([router_weight, attn_gain[:, None], moe_gain[:, None]], axis=1)
    small_all = lax.all_gather(small_local, "fsdp", axis=0, tiled=True)
    weights_all = lax.all_gather(weights_local, "fsdp", axis=0, tiled=True)
    qkv_all = weights_all[:, : width_q + 2 * width_k]
    out_all = weights_all[:, width_q + 2 * width_k :]
    router_all = small_all[:, :experts_all]
    attn_all = small_all[:, experts_all].astype(full)
    moe_all = small_all[:, experts_all + 1].astype(full)
    late_cols = width * 7 // 16
    g_all = lax.all_gather(
        jnp.concatenate([cotangent, swap_ctx(cotangent[:, late_cols:])], axis=1), "fsdp", axis=0, tiled=True
    ).reshape(fsdp // 2, 2, rows_dev, 2 * width - late_cols)

    sequence_in = sequence(tokens).astype(full)
    low_in = rms_scale(sequence_in, attn_all).astype(low)
    projected = mul(low_in, qkv_all)
    cosine, sine = (t[:, 0] for t in angles(jnp.arange(2 * rows_dev, dtype=jnp.int32), head_dim))
    sine = jnp.concatenate([-sine[:, : head_dim // 2], sine[:, head_dim // 2 :]], axis=1)
    gain_q, gain_k = query_gain.astype(full)[None], key_gain.astype(full)[None]
    attended, roped_q, roped_k, values_low = attend(
        projected, cosine, sine, gain_q, gain_k, kv_heads, group
    )
    branch = mul(attended, out_all)
    inputs = tokens.astype(full)
    mixed = (
        inputs
        + of_block(branch, rank)
        + swap_ctx(of_block(branch, 1 - rank).astype(low)).astype(full)
    )
    low_mid = rms_scale(mixed, moe_all).astype(low)
    m_all = lax.all_gather(jnp.concatenate([low_mid, swap_ctx(low_mid)]), "fsdp", axis=0, tiled=True)

    logits = mul(low_mid, router_all)
    named = routes[:, :, None] == jnp.arange(experts_all, dtype=jnp.int32)[None, None, :]
    selected = jnp.sum(jnp.where(named, logits[:, None, :], 0.0), axis=2)
    gates = gating(selected)
    chosen = jnp.any(named, axis=1)
    gates_wide = jnp.sum(jnp.where(named, gates[:, :, None], 0.0), axis=1)
    gates_sent = jnp.where(chosen, gates_wide, -1.0).T
    gates_all = lax.all_to_all(gates_sent, both, split_axis=0, concat_axis=0, tiled=True)

    g_all, gates_all = hold(g_all, gates_all)
    g_far = swap_ctx(g_all[..., :late_cols])

    lines = fsdp // 4
    places = list(range(1, lines)) + [0]
    cut = lines // 2
    parts = [places[:cut], places[cut:]]
    m_all = m_all.reshape(fsdp // 2, 2, 2, rows_dev, width)
    gates_all = gates_all.reshape(fsdp // 2, 2, 2, 1, rows_dev)
    state = dict(kept=None, first=0, core=core[None].astype(jnp.int32))

    def order_of(steps):
        spots = [((place - p) % lines) * 2 + (side + d) % 2 for d, _, p in steps]
        far = [i for i, step in enumerate(steps) if step[1] == 1] or [0]
        return jnp.stack(
            [
                jnp.asarray(item, jnp.int32)
                for i, step in enumerate(steps)
                for item in (
                    spots[i],
                    (rank + step[1]) % 2,
                    step[1],
                    spots[min(far, key=lambda j, i=i: abs(j - i))],
                )
            ]
        )

    def call(steps, raw=False):
        keep_back, send_back, *kept = run_expert(
            state["core"],
            order_of(steps),
            state["first"],
            4 * lines,
            m_all,
            g_all,
            g_far,
            gates_all,
            expert_gate_up[0],
            expert_down[0],
            capacity,
            state["kept"],
        )
        state["kept"] = kept
        state["first"] += len(steps)
        return (keep_back, send_back) if raw else over_core(keep_back, send_back)

    def wait(first):
        state["core"], first = hold(state["core"], first)
        return first

    steps_far, steps_own = ([(d, d, p) for p in places] for d in (1, 0))
    steps_mixed = [[(1, 0, p) for p in part] + [(0, 1, p) for p in part] for part in parts]
    back = call(steps_far)
    far_one, far_two = wait([pick_sum(back, 0, lines, column) for column in range(2)])
    far_one, far_two = swap_ctx(far_one), swap_side(far_two)

    def mixed_sums(back, at=0):
        return [
            pick_sum(back, start, start + cut, column) for start in (at, at + cut) for column in range(2)
        ]

    def rounds(sums, part):
        side_one, side_two, ctx_one, ctx_two = sums
        span = slice(part * cut, (part + 1) * cut)
        return [
            swap_ctx(ctx_one),
            swap_side(side_two),
            swap_side(add_low(side_one, far_one[span])),
            swap_ctx(add_low(ctx_two, far_two[span])),
        ]

    keep, send = call(steps_mixed[0], raw=True)
    send, (far_one, far_two) = hold(send, (far_one, far_two))
    back = over_core(keep, send)
    back_own = call(steps_own)
    sums = wait(mixed_sums(back))
    back_own = [pick_sum(back_own, 0, lines, column) for column in range(2)]
    got = rounds(sums, 0)
    keep, send = call(steps_mixed[1], raw=True)
    send, got = hold(send, got)
    back = over_core(keep, send)
    entries = joined(parts[0], [item[:cut] for item in back_own], got)
    arrived = {p: line_shift(entries[p], lines - p) for p in parts[0]}
    gate_back, rows, grad_rows, hidden, grad_pair = state["kept"]
    hidden, sums = hold(hidden, mixed_sums(back))
    got = rounds(sums, 1)
    grad_gates = lax.all_to_all(
        gate_back.reshape(fsdp * 2, rows_dev), both, split_axis=0, concat_axis=0, tiled=True
    ).T
    def results(first, steps, hidden):
        return run_result(
            state["core"], order_of(steps), first, hidden, gates_all, expert_down[0], capacity
        )

    out_far = results(0, steps_far, hidden)
    out_rest = results(lines, steps_mixed[0] + steps_own + steps_mixed[1], hidden)
    got, out_far, out_rest, arrived, grad_gates = lax.optimization_barrier(
        (got, out_far, out_rest, arrived, grad_gates)
    )
    entries.update(joined(parts[1], [item[cut:] for item in back_own], got))
    out_far = over_core(*out_far)
    out_far = [
        swap_ctx(pick_sum(out_far, 0, lines, 0)),
        swap_side(pick_sum(out_far, 0, lines, 1)),
    ]
    out_rest = over_core(*out_rest)
    for p in parts[1][:-1]:
        arrived[p] = line_shift(entries[p], lines - p)
    grad_mid = line_total(entries[0], arrived)

    grad_wide = jnp.where(chosen, grad_gates, 0.0)
    grad_logits = (
        gates_wide * (grad_wide - jnp.sum(gates_wide * grad_wide, axis=1, keepdims=True))
    ).astype(low)
    grad_router = mul(low_mid, grad_logits, lhs_turned)
    grad_mid = grad_mid + mul(grad_logits, router_all, rhs_turned)
    grad_mixed_part, grad_moe_gain = rms_back(mixed, moe_all, grad_mid)
    grad_mixed = cotangent.astype(full) + grad_mixed_part

    low_mixed, (out_far, out_rest) = hold(grad_mixed.astype(low), (out_far, out_rest))
    grad_branch = sequence(low_mixed)
    out_sums = [
        jnp.concatenate([one, two])
        for one, two in zip(mixed_sums(out_rest), mixed_sums(out_rest, 2 * cut + lines))
    ]
    out_own = [pick_sum(out_rest, 2 * cut, 2 * cut + lines, column) for column in range(2)]
    (out_sums, out_own), grad_branch = hold((out_sums, out_own), grad_branch)
    side_one, side_two, ctx_one, ctx_two = out_sums
    got = [
        swap_ctx(ctx_one),
        swap_side(side_two),
        add_low(side_one, out_far[0]),
        add_low(ctx_two, out_far[1]),
    ]
    grad_attended = mul(grad_branch, out_all, rhs_turned).astype(low)
    grad_attended, got = hold(grad_attended, got)
    got[2], got[3] = swap_side(got[2]), swap_ctx(got[3])
    grad_out_part = mul(attended, grad_branch, lhs_turned).astype(low)
    grad_q, grad_k, grad_v, gain_q_part, gain_k_part = attend_grad(
        projected, roped_q, roped_k, values_low, grad_attended, cosine, sine, gain_q, gain_k, kv_heads, group
    )
    grad_projected = jnp.concatenate([grad_q, grad_k, grad_v], axis=1)
    grad_qkv_part = mul(low_in, grad_projected, lhs_turned).astype(low)
    grad_projected, got = hold(grad_projected, got)
    entries = joined(places, out_own, got)
    grad_projected, entries = hold(grad_projected, entries)
    arrived = {p: line_shift(entries[p], lines - p) for p in places[:-1]}
    grad_normed_part = mul(grad_projected, qkv_all, rhs_turned)
    (rows, grad_pair, hidden, grad_rows), arrived = hold((rows, grad_pair, hidden, grad_rows), arrived)
    grad_gate_up = mul(rows, grad_pair, lhs_turned)[None]
    grad_down = mul(hidden, grad_rows, lhs_turned)[None]
    output = (mixed + line_total(entries[0], arrived)).astype(low)
    grad_normed = of_block(grad_normed_part, rank) + swap_ctx(
        of_block(grad_normed_part, 1 - rank).astype(low)
    ).astype(full)
    grad_in_part, grad_attn_gain = rms_back(inputs, attn_all, grad_normed)
    grad_tokens = grad_mixed + grad_in_part

    out_mine = lax.psum_scatter(grad_out_part, "fsdp", scatter_dimension=0, tiled=True).astype(full)
    out_other = swap_ctx(out_mine.astype(low)).astype(full)
    grad_out = jnp.where(
        rank == 0,
        jnp.concatenate([out_mine, out_other], axis=0),
        jnp.concatenate([out_other, out_mine], axis=0),
    )
    qkv_mine = lax.psum_scatter(grad_qkv_part, "fsdp", scatter_dimension=0, tiled=True)
    grad_qkv = all_heads(rank_at, qkv_mine, swap_ctx(qkv_mine), head_dim, my_heads)
    early = sum_owned(jnp.concatenate([grad_router.T, grad_moe_gain[None]], axis=0), fsdp, spot)
    late = sum_all(
        jnp.concatenate(
            [
                grad_attn_gain.reshape(-1, head_dim),
                jnp.sum(gain_q_part, axis=0),
                jnp.sum(gain_k_part, axis=0),
            ],
            axis=0,
        ),
        fsdp,
    )
    gain_rows = width // head_dim
    return (
        output,
        grad_tokens,
        grad_qkv,
        grad_out,
        early[:experts_all].T,
        lax.dynamic_slice_in_dim(late[:gain_rows].reshape(-1), spot * shard, shard, 0),
        early[experts_all],
        late[gain_rows],
        late[gain_rows + 1],
        grad_gate_up,
        grad_down,
    )


gathered_bytes = 1 << 26


def choose_body(*args):
    tokens, gate_up = args[0], args[8]
    fsdp, ctx = lax.axis_size("fsdp"), lax.axis_size("ctx")
    fits = tokens.size * tokens.dtype.itemsize * fsdp * ctx <= gathered_bytes
    if fits and fsdp % 4 == 0 and ctx == 2 and fsdp >= 8 and fsdp & (fsdp - 1) == 0 and gate_up.shape[0] == 1:
        return body_gathered(*args)
    return body_routed(*args)


def solution(mesh):
    in_specs = (
        P(("fsdp", "ctx"), None),
        P("fsdp", None),
        P("fsdp", None),
        P("fsdp", None),
        P("fsdp"),
        P("fsdp"),
        P(),
        P(),
        P(("fsdp", "ctx"), None, None),
        P(("fsdp", "ctx"), None, None),
        P(("fsdp", "ctx"), None),
        P(("fsdp", "ctx"), None),
    )
    out_specs = (
        P(("fsdp", "ctx"), None),
        P(("fsdp", "ctx"), None),
        P("fsdp", None),
        P("fsdp", None),
        P("fsdp", None),
        P("fsdp"),
        P("fsdp"),
        P(),
        P(),
        P(("fsdp", "ctx"), None, None),
        P(("fsdp", "ctx"), None, None),
    )
    return jax.shard_map(choose_body, mesh=mesh, in_specs=in_specs, out_specs=out_specs, check_vma=False)
```

```python
import functools
import math

import jax
import jax.numpy as jnp
from jax import lax
from jax.experimental import pallas as pl
from jax.experimental.pallas import tpu as pltpu
from jax.sharding import PartitionSpec as P

eps_norm = 1e-06
theta_base = 1000000.0


def rms_scale(values, gain):
    return values * lax.rsqrt(jnp.mean(values * values, axis=-1, keepdims=True) + eps_norm) * gain


def rotate(values, cosine, sine):
    half_width = values.shape[-1] // 2
    turned = jnp.concatenate([-values[..., half_width:], values[..., :half_width]], axis=-1)
    return values * cosine + turned * sine


def angles(positions, width):
    freqs = theta_base ** (-(jnp.arange(width // 2, dtype=jnp.float32) * 2.0) / width)
    phase = positions.astype(jnp.float32)[:, None] * freqs[None, :]
    phase = jnp.concatenate([phase, phase], axis=-1)
    return (jnp.cos(phase)[:, None, :], jnp.sin(phase)[:, None, :])


def device_positions(block_rank, ctx_count, tok_rows):
    half_rows = tok_rows // 2
    within = jnp.arange(tok_rows, dtype=jnp.int32)
    span_id = jnp.where(within < half_rows, block_rank, 2 * ctx_count - 1 - block_rank)
    return span_id * half_rows + within % half_rows


def attend_head(query, keys_in, values_in, causal, scale_root):
    scores = (
        jnp.einsum("tgd,sd->gts", query, keys_in, preferred_element_type=jnp.float32) / scale_root
    )
    expo = jnp.where(causal[None], jnp.exp(scores), 0.0)
    totals = jnp.sum(expo, axis=-1, keepdims=True)
    probs = (expo / totals).astype(jnp.bfloat16)
    attended = jnp.einsum("gts,sd->tgd", probs, values_in, preferred_element_type=jnp.float32)
    return (attended, jnp.log(totals[..., 0]))


def attend_back(query, keys_in, values_in, causal, log_total, grad_attended, scale_root):
    scores = (
        jnp.einsum("tgd,sd->gts", query, keys_in, preferred_element_type=jnp.float32) / scale_root
    )
    probs = jnp.where(causal[None], jnp.exp(scores - log_total[..., None]), 0.0)
    low_probs = probs.astype(jnp.bfloat16)
    grad_values = jnp.einsum(
        "gts,tgd->sd", low_probs, grad_attended, preferred_element_type=jnp.float32
    )
    grad_probs = jnp.einsum(
        "tgd,sd->gts", grad_attended, values_in, preferred_element_type=jnp.float32
    )
    delta_rows = jnp.sum(grad_probs * probs, axis=-1, keepdims=True)
    grad_scores = (probs * (grad_probs - delta_rows)).astype(jnp.bfloat16)
    grad_query = (
        jnp.einsum("gts,sd->tgd", grad_scores, keys_in, preferred_element_type=jnp.float32)
        / scale_root
    )
    grad_keys = (
        jnp.einsum("gts,tgd->sd", grad_scores, query, preferred_element_type=jnp.float32)
        / scale_root
    )
    return (grad_query, grad_keys, grad_values)


def swiglu(paired):
    half_width = paired.shape[-1] // 2
    return jax.nn.silu(paired[..., :half_width]) * paired[..., half_width:]


def gating(selected):
    expo = jnp.exp(selected)
    return expo / jnp.sum(expo, axis=1, keepdims=True)


def body_routed(
    tokens,
    qkv_weight,
    out_weight,
    router_weight,
    attn_gain,
    moe_gain,
    query_gain,
    key_gain,
    expert_gate_up,
    expert_down,
    routes,
    cotangent,
):
    rows_dev, width = tokens.shape
    head_dim = query_gain.shape[0]
    top_k = routes.shape[1]
    ctx_count = lax.axis_size("ctx")
    ctx_rank = lax.axis_index("ctx")
    qkv_all, out_all, router_all, attn_all, moe_all = (
        lax.all_gather(qkv_weight, "fsdp", axis=0, tiled=True),
        lax.all_gather(out_weight, "fsdp", axis=0, tiled=True),
        lax.all_gather(router_weight, "fsdp", axis=0, tiled=True),
        lax.all_gather(attn_gain, "fsdp", axis=0, tiled=True),
        lax.all_gather(moe_gain, "fsdp", axis=0, tiled=True),
    )
    experts_all = router_all.shape[1]
    heads = out_all.shape[0] // head_dim
    kv_heads = (qkv_all.shape[1] // head_dim - heads) // 2
    group_size = heads // kv_heads
    capacity = 2 * rows_dev * top_k // experts_all
    width_q = heads * head_dim
    width_k = kv_heads * head_dim
    scale_root = math.sqrt(head_dim)
    inputs = tokens.astype(jnp.float32)
    normed_in = rms_scale(inputs, attn_all.astype(jnp.float32))
    low_in = normed_in.astype(jnp.bfloat16)
    projected = jnp.dot(low_in, qkv_all, preferred_element_type=jnp.float32)
    query_raw = projected[:, :width_q].reshape(rows_dev, heads, head_dim)
    key_raw = projected[:, width_q : width_q + width_k].reshape(rows_dev, kv_heads, head_dim)
    value_low = (
        projected[:, width_q + width_k :].astype(jnp.bfloat16).reshape(rows_dev, kv_heads, head_dim)
    )
    positions = device_positions(ctx_rank, ctx_count, rows_dev)
    cosine, sine = angles(positions, head_dim)
    query_gain_f = query_gain.astype(jnp.float32)
    key_gain_f = key_gain.astype(jnp.float32)

    def query_rope(values_in, gain):
        return rotate(rms_scale(values_in, gain), cosine, sine)

    query_low = query_rope(query_raw, query_gain_f).astype(jnp.bfloat16)
    key_low = query_rope(key_raw, key_gain_f).astype(jnp.bfloat16)
    keys_all, values_all = (
        lax.all_gather(key_low, "ctx", axis=0, tiled=True),
        lax.all_gather(value_low, "ctx", axis=0, tiled=True),
    )
    key_pos = jnp.concatenate(
        [device_positions(other, ctx_count, rows_dev) for other in range(ctx_count)]
    )
    causal = key_pos[None, :] <= positions[:, None]
    query_heads = query_low.reshape(rows_dev, kv_heads, group_size, head_dim).transpose(1, 0, 2, 3)
    key_heads = keys_all.transpose(1, 0, 2)
    value_heads = values_all.transpose(1, 0, 2)
    attended, log_total = lax.map(
        lambda member: attend_head(member[0], member[1], member[2], causal, scale_root),
        (query_heads, key_heads, value_heads),
    )
    attended_low = attended.transpose(1, 0, 2, 3).reshape(rows_dev, width_q).astype(jnp.bfloat16)
    mixed = inputs + jnp.dot(attended_low, out_all, preferred_element_type=jnp.float32)
    normed_mid = rms_scale(mixed, moe_all.astype(jnp.float32))
    low_mid = normed_mid.astype(jnp.bfloat16)
    logits = jnp.dot(low_mid, router_all, preferred_element_type=jnp.float32)
    selected = jnp.take_along_axis(logits, routes, axis=1)
    gates, gate_back = jax.vjp(gating, selected)
    flat_routes = routes.reshape(-1)
    expert_ids = jnp.arange(experts_all, dtype=jnp.int32)
    hit_table = (flat_routes[:, None] == expert_ids[None, :]).astype(jnp.int32)
    slot_index = jnp.sum(jnp.cumsum(hit_table, axis=0) * hit_table, axis=1) - 1
    target = flat_routes * capacity + slot_index
    pair_count = rows_dev * top_k
    source_pair = (
        jnp.full((experts_all * capacity,), pair_count, jnp.int32)
        .at[target]
        .set(jnp.arange(pair_count, dtype=jnp.int32))
    )
    padded = jnp.concatenate([low_mid, jnp.zeros((1, width), jnp.bfloat16)], axis=0)
    outgoing = padded[source_pair // top_k].reshape(experts_all, capacity, width)
    received = lax.all_to_all(outgoing, ("fsdp", "ctx"), split_axis=0, concat_axis=1, tiled=True)
    gate_and_up = jnp.einsum(
        "esd,edf->esf", received, expert_gate_up, preferred_element_type=jnp.float32
    )
    hidden_val, swiglu_back = jax.vjp(swiglu, gate_and_up)
    hidden_low = hidden_val.astype(jnp.bfloat16)
    result_low = jnp.einsum(
        "esf,efd->esd", hidden_low, expert_down, preferred_element_type=jnp.float32
    ).astype(jnp.bfloat16)
    returned = lax.all_to_all(
        result_low, ("fsdp", "ctx"), split_axis=1, concat_axis=0, tiled=True
    ).reshape(experts_all * capacity, width)
    picked = returned[target].reshape(rows_dev, top_k, width).astype(jnp.float32)
    output = (mixed + jnp.sum(gates[:, :, None] * picked, axis=1)).astype(jnp.bfloat16)
    qkv_back, out_back, router_back, attn_back_g, moe_back_g = (
        qkv_all,
        out_all,
        router_all,
        attn_all,
        moe_all,
    )
    grad_final = cotangent.astype(jnp.float32)
    grad_gates = jnp.sum(grad_final[:, None, :] * picked, axis=2)
    grad_result = (
        (gates[:, :, None] * grad_final[:, None, :]).astype(jnp.bfloat16).reshape(pair_count, width)
    )
    grad_padded = jnp.concatenate([grad_result, jnp.zeros((1, width), jnp.bfloat16)], axis=0)
    grad_outgoing = grad_padded[source_pair].reshape(experts_all, capacity, width)
    grad_received = lax.all_to_all(
        grad_outgoing, ("fsdp", "ctx"), split_axis=0, concat_axis=1, tiled=True
    )
    grad_down = jnp.einsum(
        "esf,esd->efd", hidden_low, grad_received, preferred_element_type=jnp.float32
    )
    grad_hidden = jnp.einsum(
        "esd,efd->esf", grad_received, expert_down, preferred_element_type=jnp.float32
    )
    grad_paired = swiglu_back(grad_hidden)[0].astype(jnp.bfloat16)
    grad_gate_up = jnp.einsum(
        "esd,esf->edf", received, grad_paired, preferred_element_type=jnp.float32
    )
    grad_rows = jnp.einsum(
        "esf,edf->esd", grad_paired, expert_gate_up, preferred_element_type=jnp.float32
    ).astype(jnp.bfloat16)
    grad_returned = lax.all_to_all(
        grad_rows, ("fsdp", "ctx"), split_axis=1, concat_axis=0, tiled=True
    ).reshape(experts_all * capacity, width)
    grad_mid = jnp.sum(
        grad_returned[target].reshape(rows_dev, top_k, width).astype(jnp.float32), axis=1
    )
    grad_selected = gate_back(grad_gates)[0]
    route_table = (routes[:, :, None] == expert_ids[None, None, :]).astype(jnp.float32)
    grad_logits = jnp.sum(route_table * grad_selected[:, :, None], axis=1).astype(jnp.bfloat16)
    grad_router = jnp.dot(low_mid.T, grad_logits, preferred_element_type=jnp.float32)
    grad_mid = grad_mid + jnp.dot(grad_logits, router_back.T, preferred_element_type=jnp.float32)
    unused_mid, mid_back = jax.vjp(rms_scale, mixed, moe_back_g.astype(jnp.float32))
    grad_mixed_part, grad_moe_gain = mid_back(grad_mid)
    grad_mixed = grad_final + grad_mixed_part
    grad_branch = grad_mixed.astype(jnp.bfloat16)
    grad_out = jnp.dot(attended_low.T, grad_branch, preferred_element_type=jnp.float32)
    grad_attended = jnp.dot(grad_branch, out_back.T, preferred_element_type=jnp.float32).astype(
        jnp.bfloat16
    )
    grad_heads = grad_attended.reshape(rows_dev, kv_heads, group_size, head_dim).transpose(
        1, 0, 2, 3
    )
    grad_query_h, grad_key_h, grad_value_h = lax.map(
        lambda member: attend_back(
            member[0], member[1], member[2], causal, member[3], member[4], scale_root
        ),
        (query_heads, key_heads, value_heads, log_total, grad_heads),
    )
    grad_keys, grad_values = (
        lax.psum_scatter(
            grad_key_h.transpose(1, 0, 2).astype(jnp.bfloat16),
            "ctx",
            scatter_dimension=0,
            tiled=True,
        ).astype(jnp.float32),
        lax.psum_scatter(
            grad_value_h.transpose(1, 0, 2).astype(jnp.bfloat16),
            "ctx",
            scatter_dimension=0,
            tiled=True,
        ).astype(jnp.float32),
    )
    grad_query_rot = (
        grad_query_h.transpose(1, 0, 2, 3).reshape(rows_dev, heads, head_dim).astype(jnp.bfloat16)
    )
    grad_query_rot = lax.optimization_barrier(grad_query_rot).astype(jnp.float32)
    grad_key_rot = lax.optimization_barrier(grad_keys.astype(jnp.bfloat16)).astype(jnp.float32)
    unused_query, query_back = jax.vjp(query_rope, query_raw, query_gain_f)
    grad_query_raw, grad_query_gain = query_back(grad_query_rot)
    unused_key, key_back = jax.vjp(query_rope, key_raw, key_gain_f)
    grad_key_raw, grad_key_gain = key_back(grad_key_rot)
    grad_projected = jnp.concatenate(
        [
            grad_query_raw.reshape(rows_dev, width_q).astype(jnp.bfloat16),
            grad_key_raw.reshape(rows_dev, width_k).astype(jnp.bfloat16),
            grad_values.reshape(rows_dev, width_k).astype(jnp.bfloat16),
        ],
        axis=1,
    )
    grad_qkv = jnp.dot(low_in.T, grad_projected, preferred_element_type=jnp.float32)
    grad_normed = jnp.dot(grad_projected, qkv_back.T, preferred_element_type=jnp.float32)
    unused_in, in_back = jax.vjp(rms_scale, inputs, attn_back_g.astype(jnp.float32))
    grad_in_part, grad_attn_gain = in_back(grad_normed)
    grad_tokens = grad_mixed + grad_in_part
    gradients = (grad_qkv, grad_out, grad_router, grad_attn_gain, grad_moe_gain)
    pieces = (
        lax.psum_scatter(gradients[0], "fsdp", scatter_dimension=0, tiled=True),
        lax.psum_scatter(gradients[1], "fsdp", scatter_dimension=0, tiled=True),
        lax.psum_scatter(gradients[2], "fsdp", scatter_dimension=0, tiled=True),
        lax.psum_scatter(gradients[3], "fsdp", scatter_dimension=0, tiled=True),
        lax.psum_scatter(gradients[4], "fsdp", scatter_dimension=0, tiled=True),
    )
    reduced = (
        lax.psum(pieces[0].astype(jnp.bfloat16), "ctx").astype(jnp.float32),
        lax.psum(pieces[1].astype(jnp.bfloat16), "ctx").astype(jnp.float32),
        lax.psum(pieces[2].astype(jnp.bfloat16), "ctx").astype(jnp.float32),
        lax.psum(pieces[3].astype(jnp.bfloat16), "ctx").astype(jnp.float32),
        lax.psum(pieces[4].astype(jnp.bfloat16), "ctx").astype(jnp.float32),
    )
    gain_sums = lax.psum((grad_query_gain, grad_key_gain), ("fsdp", "ctx"))
    return (
        output,
        grad_tokens,
        reduced[0],
        reduced[1],
        reduced[2],
        reduced[3],
        reduced[4],
        gain_sums[0],
        gain_sums[1],
        grad_gate_up,
        grad_down,
    )


low = jnp.bfloat16
full = jnp.float32
plain = (((1,), (0,)), ((), ()))
rhs_turned = (((1,), (1,)), ((), ()))
lhs_turned = (((0,), (0,)), ((), ()))
vmem_bytes = 58 << 20


def mul(left, right, dims=plain):
    return lax.dot_general(left, right, dims, preferred_element_type=full)


def core_pairs(fsdp):
    return [(i, i ^ 1) for i in range(fsdp)]


def side_pairs(fsdp):
    return [(i, i ^ 2) for i in range(fsdp)]


def swap_core(values):
    return lax.ppermute(values, "fsdp", core_pairs(lax.axis_size("fsdp")))


def swap_side(values):
    return lax.ppermute(values, "fsdp", side_pairs(lax.axis_size("fsdp")))


def swap_ctx(values):
    return lax.ppermute(values, "ctx", [(0, 1), (1, 0)])


def add_low(one, two):
    return (one.astype(full) + two.astype(full)).astype(low)


def hold(values, first):
    return lax.optimization_barrier((values, first))


def take(values, index):
    return lax.dynamic_index_in_dim(values, index, 0, keepdims=False)


def line_shift(values, step):
    fsdp = lax.axis_size("fsdp")
    return lax.ppermute(values, "fsdp", [(i, (i + 4 * step) % fsdp) for i in range(fsdp)])


def line_total(own, arrived):
    total = own.astype(full)
    for item in arrived.values():
        total = total + item.astype(full)
    return total


def joined(places, own, got):
    from_ctx, from_side, one_side, two_ctx = got
    entries = {}
    for at, p in enumerate(places):
        one = add_low(add_low(own[0][at], from_ctx[at]), one_side[at])
        two = add_low(add_low(own[1][at], from_side[at]), two_ctx[at])
        entries[p] = jnp.concatenate([one, two], axis=-1)
    return entries


def over_core(keep, send):
    return keep, swap_core(send)


def pick_sum(parts, start, stop, column):
    keep, other = parts
    half = keep.shape[-1] // 2
    cut = (slice(start, stop), slice(None), slice(column * half, (column + 1) * half))
    return add_low(keep[cut], other[cut])


def sum_all(values, fsdp):
    values = values + lax.ppermute(values, "fsdp", core_pairs(fsdp))
    values = values + swap_ctx(values)
    step = 2
    while step < fsdp:
        values = values + lax.ppermute(values, "fsdp", [(i, i ^ step) for i in range(fsdp)])
        step *= 2
    return values


def sum_owned(values, fsdp, spot):
    items, shard = values.shape[0], values.shape[1] // fsdp
    values = values.reshape(items, fsdp, shard).swapaxes(0, 1)
    step = fsdp // 2
    while step:
        bit = (spot // step) % 2
        values = values.reshape(2, step, items, shard)
        other = lax.ppermute(take(values, 1 - bit), "fsdp", [(i, i ^ step) for i in range(fsdp)])
        values = take(values, bit) + other
        step //= 2
    values = values[0]
    return values + swap_ctx(values)


def turn(values):
    return pltpu.roll(values, values.shape[-1] // 2, 1)


def norm_rope(raw, gain, cosine, sine):
    scale = lax.rsqrt(jnp.mean(raw * raw, axis=-1, keepdims=True) + eps_norm)
    scaled = raw * scale * gain
    return scaled * cosine + turn(scaled) * sine


def norm_rope_back(raw, gain, cosine, sine, grad):
    scale = lax.rsqrt(jnp.mean(raw * raw, axis=-1, keepdims=True) + eps_norm)
    unit = raw * scale
    grad_scaled = grad * cosine - turn(grad) * sine
    grad_gain = jnp.sum(grad_scaled * unit, axis=0, keepdims=True)
    grad_unit = grad_scaled * gain
    grad_raw = scale * (grad_unit - unit * jnp.mean(grad_unit * unit, axis=-1, keepdims=True))
    return grad_raw, grad_gain


def tiles_of(rows):
    step = rows // 2
    return [(start, start + step) for start in range(0, rows, step)]


def allowed(start, stop):
    shape = (stop - start, stop)
    return lax.broadcasted_iota(jnp.int32, shape, 1) <= (
        lax.broadcasted_iota(jnp.int32, shape, 0) + start
    )


def attend_kernel(q_ref, k_ref, v_ref, cos_ref, sin_ref, qg_ref, kg_ref, o_ref, qr_ref, kr_ref, vl_ref):
    head_dim = k_ref.shape[1]
    rows = k_ref.shape[0]
    cosine, sine = cos_ref[...], sin_ref[...]
    keys = norm_rope(k_ref[...], kg_ref[...], cosine, sine).astype(low)
    values = v_ref[...].astype(low)
    kr_ref[...] = keys
    vl_ref[...] = values
    for head in range(q_ref.shape[1] // head_dim):
        cols = slice(head * head_dim, (head + 1) * head_dim)
        query = norm_rope(q_ref[:, cols], qg_ref[...], cosine, sine).astype(low)
        qr_ref[:, cols] = query
        for start, stop in tiles_of(rows):
            scores = mul(query[start:stop], keys[:stop], rhs_turned) * (1.0 / math.sqrt(head_dim))
            expo = jnp.where(allowed(start, stop), jnp.exp(scores), 0.0)
            probs = (expo / jnp.sum(expo, axis=-1, keepdims=True)).astype(low)
            o_ref[start:stop, cols] = mul(probs, values[:stop]).astype(low)


def attend_grad_kernel(
    q_ref, k_ref, qr_ref, kr_ref, vl_ref, go_ref, cos_ref, sin_ref, qg_ref, kg_ref,
    dq_ref, dk_ref, dv_ref, dqg_ref, dkg_ref, dk_sum, dv_sum, dq_sum,
):
    head_dim = k_ref.shape[1]
    rows = k_ref.shape[0]
    root = 1.0 / math.sqrt(head_dim)
    cosine, sine = cos_ref[...], sin_ref[...]
    keys, values = kr_ref[...], vl_ref[...]
    gain_sum = jnp.zeros((1, head_dim), full)
    dk_sum[...] = jnp.zeros_like(dk_sum)
    dv_sum[...] = jnp.zeros_like(dv_sum)
    for head in range(q_ref.shape[1] // head_dim):
        cols = slice(head * head_dim, (head + 1) * head_dim)
        for start, stop in tiles_of(rows):
            query = qr_ref[start:stop, cols]
            grad = go_ref[start:stop, cols]
            scores = mul(query, keys[:stop], rhs_turned) * root
            expo = jnp.where(allowed(start, stop), jnp.exp(scores), 0.0)
            probs = expo / jnp.sum(expo, axis=-1, keepdims=True)
            grad_probs = mul(grad, values[:stop], rhs_turned)
            delta = jnp.sum(grad_probs * probs, axis=-1, keepdims=True)
            grad_scores = (probs * (grad_probs - delta)).astype(low)
            dv_sum[:stop] += mul(probs.astype(low), grad, lhs_turned)
            dk_sum[:stop] += mul(grad_scores, query, lhs_turned)
            dq_sum[start:stop] = mul(grad_scores, keys[:stop])
        grad_query = (dq_sum[...] * root).astype(low).astype(full)
        grad_raw, grad_gain = norm_rope_back(q_ref[:, cols], qg_ref[...], cosine, sine, grad_query)
        dq_ref[:, cols] = grad_raw.astype(low)
        gain_sum = gain_sum + grad_gain
    dqg_ref[0] = gain_sum
    grad_key = (dk_sum[...] * root).astype(low).astype(full)
    grad_raw, grad_gain = norm_rope_back(k_ref[...], kg_ref[...], cosine, sine, grad_key)
    dk_ref[...] = grad_raw.astype(low)
    dkg_ref[0] = grad_gain
    dv_ref[...] = dv_sum[...].astype(low)


def attention_specs(rows, head_dim, kv_heads, group):
    wide, narrow = group * head_dim, head_dim
    heads_end = kv_heads * group
    return dict(
        q=pl.BlockSpec((rows, wide), lambda i: (0, i)),
        k=pl.BlockSpec((rows, narrow), lambda i: (0, heads_end + i)),
        v=pl.BlockSpec((rows, narrow), lambda i: (0, heads_end + kv_heads + i)),
        own=pl.BlockSpec((rows, narrow), lambda i: (0, i)),
        table=pl.BlockSpec((rows, head_dim), lambda i: (0, 0)),
        gain=pl.BlockSpec((1, head_dim), lambda i: (0, 0)),
        gain_out=pl.BlockSpec((1, 1, head_dim), lambda i: (i, 0, 0)),
    )


def attend(projected, cosine, sine, query_gain, key_gain, kv_heads, group):
    rows, head_dim = cosine.shape
    s = attention_specs(rows, head_dim, kv_heads, group)
    shape = jax.ShapeDtypeStruct
    work = rows * rows * head_dim * kv_heads * group
    return pl.pallas_call(
        attend_kernel,
        grid=(kv_heads,),
        in_specs=[s["q"], s["k"], s["v"], s["table"], s["table"], s["gain"], s["gain"]],
        out_specs=[s["q"], s["q"], s["own"], s["own"]],
        out_shape=[
            shape((rows, kv_heads * group * head_dim), low),
            shape((rows, kv_heads * group * head_dim), low),
            shape((rows, kv_heads * head_dim), low),
            shape((rows, kv_heads * head_dim), low),
        ],
        compiler_params=pltpu.CompilerParams(vmem_limit_bytes=48 << 20),
        cost_estimate=pl.CostEstimate(
            flops=4 * work, bytes_accessed=projected.size * 6, transcendentals=work // head_dim
        ),
        name="attend",
    )(projected, projected, projected, cosine, sine, query_gain, key_gain)


def attend_grad(projected, roped_q, roped_k, values_low, grad, cosine, sine, query_gain, key_gain, kv_heads, group):
    rows, head_dim = cosine.shape
    s = attention_specs(rows, head_dim, kv_heads, group)
    shape = jax.ShapeDtypeStruct
    work = rows * rows * head_dim * kv_heads * group
    return pl.pallas_call(
        attend_grad_kernel,
        grid=(kv_heads,),
        in_specs=[
            s["q"], s["k"], s["q"], s["own"], s["own"], s["q"],
            s["table"], s["table"], s["gain"], s["gain"],
        ],
        out_specs=[s["q"], s["own"], s["own"], s["gain_out"], s["gain_out"]],
        out_shape=[
            shape((rows, kv_heads * group * head_dim), low),
            shape((rows, kv_heads * head_dim), low),
            shape((rows, kv_heads * head_dim), low),
            shape((kv_heads, 1, head_dim), full),
            shape((kv_heads, 1, head_dim), full),
        ],
        scratch_shapes=[pltpu.VMEM((rows, head_dim), full)] * 3,
        compiler_params=pltpu.CompilerParams(vmem_limit_bytes=48 << 20),
        cost_estimate=pl.CostEstimate(
            flops=10 * work, bytes_accessed=projected.size * 10, transcendentals=work // head_dim
        ),
        name="attend_grad",
    )(projected, projected, roped_q, roped_k, values_low, grad, cosine, sine, query_gain, key_gain)


def placed(gate, slots):
    block = gate.shape[1]
    shape = (block, block)
    earlier = (
        lax.broadcasted_iota(jnp.int32, shape, 0) < lax.broadcasted_iota(jnp.int32, shape, 1)
    ).astype(low)
    hit = jnp.where(gate >= 0.0, 1.0, 0.0)
    count = mul(jnp.broadcast_to(hit, (8, block)).astype(low), earlier)[:1].astype(jnp.int32)
    place = (lax.broadcasted_iota(jnp.int32, (slots, block), 0) == count) & (hit > 0.5)
    weight = jnp.sum(jnp.where(place, gate, 0.0), axis=1, keepdims=True)
    return place, place.astype(full).astype(low), weight


def expert_kernel(core_ref, order, m_ref, g_ref, far_ref, w_ref, gu_ref, dn_ref, *refs):
    keep_back, send_back, gate_back, rows_ref, dy_ref, z_ref, pair_ref = refs[-7:]
    core = core_ref[0]
    far = order[4 * pl.program_id(0) + 2] == 1
    width = m_ref.shape[4]
    hidden = dn_ref.shape[0]
    slots = z_ref.shape[0] // 2
    places, picks, weights, rows, grads = [], [], [], [], []
    for part in range(2):
        at = lax.rem(core + part, 2)
        place, pick, weight = placed(w_ref[0, at, 0], slots)
        places.append(place)
        picks.append(pick)
        weights.append(weight)
        rows.append(mul(pick, m_ref[0, at, 0]).astype(low))
        near_rows = g_ref[0, at, :, :width]
        far_rows = jnp.concatenate([far_ref[0, at], g_ref[0, at, :, width:]], axis=1)
        grads.append(mul(pick, jnp.where(far, far_rows, near_rows)).astype(low))
    row, grad, weight = (jnp.concatenate(items, axis=0) for items in (rows, grads, weights))
    rows_ref[...] = row
    paired = mul(row, gu_ref[...])
    gate_in, up = paired[:, :hidden], paired[:, hidden:]
    sig = jax.nn.sigmoid(gate_in)
    act = gate_in * sig
    z = (act * up).astype(low)
    z_ref[...] = z
    dy_ref[...] = (weight * grad.astype(full)).astype(low)
    unweighted = mul(grad, dn_ref[...], rhs_turned)
    grad_gate = jnp.sum(unweighted * z.astype(full), axis=1, keepdims=True)
    dz = weight * unweighted
    grad_in = dz * up * (sig * (1.0 + gate_in * (1.0 - sig)))
    pair = jnp.concatenate([grad_in, dz * act], axis=1).astype(low)
    pair_ref[...] = pair
    back = mul(pair, gu_ref[...], rhs_turned).astype(low)
    for part, out in enumerate((keep_back, send_back)):
        mine = slice(part * slots, (part + 1) * slots)
        out[0] = mul(picks[part], back[mine], lhs_turned).astype(low)
        gate_back[0, lax.rem(core + part, 2), 0] = jnp.sum(
            jnp.where(places[part], grad_gate[mine], 0.0), axis=0, keepdims=True
        )


def run_expert(core, order, first, total_steps, m_all, g_all, g_far, gates_all, gate_up, down, slots, kept):
    places, _, _, block, width = m_all.shape
    paired = gate_up.shape[1]
    steps = order.shape[0] // 4
    part_rows = steps * 2 * slots
    hidden = paired // 2
    shape = jax.ShapeDtypeStruct

    def gates_at(i, core, order):
        return (order[4 * i], 0, order[4 * i + 1], 0, 0)

    def token_at(i, core, order):
        return (order[4 * i], 0, order[4 * i + 2], 0, 0)

    def near_at(i, core, order):
        return (order[4 * i], 0, 0, 0)

    def far_at(i, core, order):
        return (order[4 * i + 3], 0, 0, 0)

    def fixed(i, core, order):
        return (0, 0)

    def flat(i, core, order):
        return (first + i, 0)

    def stacked(i, core, order):
        return (i, 0, 0)

    small = pl.BlockSpec((1, 2, 1, 1, block), gates_at)
    one_block = pl.BlockSpec((1, block, width), stacked)
    widths = (width, width, hidden, paired)
    grid_spec = pltpu.PrefetchScalarGridSpec(
        num_scalar_prefetch=2,
        grid=(steps,),
        in_specs=[
            pl.BlockSpec((1, 2, 1, block, width), token_at),
            pl.BlockSpec((1, 2, block, g_all.shape[3]), near_at),
            pl.BlockSpec((1, 2, block, g_far.shape[3]), far_at),
            small,
            pl.BlockSpec(gate_up.shape, fixed, pipeline_mode=pl.Buffered(1)),
            pl.BlockSpec(down.shape, fixed, pipeline_mode=pl.Buffered(1)),
        ]
        + [pl.BlockSpec(memory_space=pl.ANY)] * (0 if kept is None else 5),
        out_specs=[one_block] * 2 + [small] + [pl.BlockSpec((2 * slots, n), flat) for n in widths],
    )
    return pl.pallas_call(
        expert_kernel,
        grid_spec=grid_spec,
        out_shape=[shape((steps, block, width), low)] * 2
        + [shape((places, 2, 2, 1, block), full)]
        + [shape((total_steps * 2 * slots, n), low) for n in widths],
        input_output_aliases={} if kept is None else {8 + i: 2 + i for i in range(5)},
        compiler_params=pltpu.CompilerParams(vmem_limit_bytes=vmem_bytes),
        cost_estimate=pl.CostEstimate(
            flops=part_rows * width * (4 * paired + 2 * hidden + 6 * block),
            bytes_accessed=steps * block * width * 12 + part_rows * (width * 4 + paired * 3),
            transcendentals=part_rows * hidden,
        ),
        name="experts",
    )(core, order, m_all, g_all, g_far, gates_all, gate_up, down, *(() if kept is None else kept))


def result_kernel(core_ref, order, z_ref, w_ref, dn_ref, keep_out, send_out):
    core = core_ref[0]
    slots = z_ref.shape[0] // 2
    y = mul(z_ref[...], dn_ref[...]).astype(low).astype(full)
    for part, out in enumerate((keep_out, send_out)):
        _, pick, weight = placed(w_ref[0, lax.rem(core + part, 2), 0], slots)
        scaled = (weight * y[part * slots : (part + 1) * slots]).astype(low)
        out[0] = mul(pick, scaled, lhs_turned).astype(low)


def run_result(core, order, first, hidden, gates_all, down, slots):
    block, width, inner = gates_all.shape[4], down.shape[1], down.shape[0]
    steps = order.shape[0] // 4
    one_block = pl.BlockSpec((1, block, width), lambda i, core, order: (i, 0, 0))
    return pl.pallas_call(
        result_kernel,
        grid_spec=pltpu.PrefetchScalarGridSpec(
            num_scalar_prefetch=2,
            grid=(steps,),
            in_specs=[
                pl.BlockSpec((2 * slots, inner), lambda i, core, order: (first + i, 0)),
                pl.BlockSpec(
                    (1, 2, 1, 1, block), lambda i, core, order: (order[4 * i], 0, order[4 * i + 1], 0, 0)
                ),
                pl.BlockSpec(down.shape, lambda i, core, order: (0, 0), pipeline_mode=pl.Buffered(1)),
            ],
            out_specs=[one_block] * 2,
        ),
        out_shape=[jax.ShapeDtypeStruct((steps, block, width), low)] * 2,
        compiler_params=pltpu.CompilerParams(vmem_limit_bytes=vmem_bytes),
        cost_estimate=pl.CostEstimate(
            flops=steps * 2 * slots * width * (2 * inner + 2 * block),
            bytes_accessed=steps * (4 * block * width + 4 * slots * inner) + 2 * inner * width,
            transcendentals=0,
        ),
        name="results",
    )(core, order, hidden, gates_all, down)


def own_heads_kernel(rank, qkv_ref, out_ref, o_ref, *, head_dim, heads):
    first = rank[0] == 0
    for head in range(heads):
        pair = [qkv_ref[:, (2 * head + i) * head_dim : (2 * head + i + 1) * head_dim] for i in range(2)]
        o_ref[:, head * head_dim : (head + 1) * head_dim] = jnp.where(first, pair[0], pair[1])
    kv = qkv_ref.shape[1] - 2 * heads * head_dim
    o_ref[:, heads * head_dim : heads * head_dim + kv] = qkv_ref[:, 2 * heads * head_dim :]
    o_ref[:, heads * head_dim + kv :] = jnp.where(first, out_ref[:head_dim], out_ref[head_dim:])


def own_heads(rank, qkv_weight, out_weight, head_dim, heads):
    kv = qkv_weight.shape[1] - 2 * heads * head_dim
    return pl.pallas_call(
        functools.partial(own_heads_kernel, head_dim=head_dim, heads=heads),
        grid_spec=pltpu.PrefetchScalarGridSpec(
            num_scalar_prefetch=1,
            grid=(1,),
            in_specs=[
                pl.BlockSpec(qkv_weight.shape, lambda i, rank: (0, 0)),
                pl.BlockSpec(out_weight.shape, lambda i, rank: (0, 0)),
            ],
            out_specs=pl.BlockSpec(
                (qkv_weight.shape[0], heads * head_dim + kv + out_weight.shape[1]), lambda i, rank: (0, 0)
            ),
        ),
        out_shape=jax.ShapeDtypeStruct(
            (qkv_weight.shape[0], heads * head_dim + kv + out_weight.shape[1]), qkv_weight.dtype
        ),
        name="own_heads",
    )(rank, qkv_weight, out_weight)


def all_heads_kernel(rank, mine_ref, other_ref, o_ref, *, head_dim, heads):
    first = rank[0] == 0
    for head in range(heads):
        cols = slice(head * head_dim, (head + 1) * head_dim)
        mine, other = mine_ref[:, cols].astype(full), other_ref[:, cols].astype(full)
        o_ref[:, 2 * head * head_dim : (2 * head + 1) * head_dim] = jnp.where(first, mine, other)
        o_ref[:, (2 * head + 1) * head_dim : (2 * head + 2) * head_dim] = jnp.where(first, other, mine)
    o_ref[:, 2 * heads * head_dim :] = mine_ref[:, heads * head_dim :].astype(full) + other_ref[
        :, heads * head_dim :
    ].astype(full)


def all_heads(rank, mine, other, head_dim, heads):
    rows, width = mine.shape
    return pl.pallas_call(
        functools.partial(all_heads_kernel, head_dim=head_dim, heads=heads),
        grid_spec=pltpu.PrefetchScalarGridSpec(
            num_scalar_prefetch=1,
            grid=(1,),
            in_specs=[pl.BlockSpec((rows, width), lambda i, rank: (0, 0))] * 2,
            out_specs=pl.BlockSpec((rows, width + heads * head_dim), lambda i, rank: (0, 0)),
        ),
        out_shape=jax.ShapeDtypeStruct((rows, width + heads * head_dim), full),
        name="all_heads",
    )(rank, mine, other)


def rms_back(values, gain, grad):
    scale = lax.rsqrt(jnp.mean(values * values, axis=-1, keepdims=True) + eps_norm)
    unit = values * scale
    grad_gain = jnp.sum(grad * unit, axis=0)
    grad_unit = grad * gain
    back = scale * (grad_unit - unit * jnp.mean(grad_unit * unit, axis=-1, keepdims=True))
    return back, grad_gain


def in_order(first, second):
    half = first.shape[0] // 2
    return jnp.concatenate([first[:half], second, first[half:]], axis=0)


def of_block(values, rank):
    quarter = values.shape[0] // 4
    outer = jnp.concatenate([values[:quarter], values[3 * quarter :]], axis=0)
    return jnp.where(rank == 0, outer, values[quarter : 3 * quarter])


def body_gathered(
    tokens, qkv_weight, out_weight, router_weight, attn_gain, moe_gain, query_gain, key_gain,
    expert_gate_up, expert_down, routes, cotangent,
):
    rows_dev, width = tokens.shape
    head_dim = query_gain.shape[0]
    top_k = routes.shape[1]
    fsdp = lax.axis_size("fsdp")
    spot = lax.axis_index("fsdp")
    rank = lax.axis_index("ctx")
    place, side, core = spot // 4, (spot // 2) % 2, spot % 2
    shard = qkv_weight.shape[0]
    heads = out_weight.shape[0] * fsdp // head_dim
    kv_heads = (qkv_weight.shape[1] // head_dim - heads) // 2
    group = heads // kv_heads // 2
    my_heads = heads // 2
    width_q, width_k = my_heads * head_dim, kv_heads * head_dim
    experts_all = router_weight.shape[1]
    capacity = 2 * rows_dev * top_k // experts_all
    both = ("fsdp", "ctx")

    def sequence(values):
        other = swap_ctx(values)
        first = jnp.where(rank == 0, values, other)
        second = jnp.where(rank == 0, other, values)
        return in_order(first, second)

    rank_at = rank[None].astype(jnp.int32)
    weights_local = own_heads(rank_at, qkv_weight, out_weight, head_dim, my_heads)
    small_local = jnp.concatenate([router_weight, attn_gain[:, None], moe_gain[:, None]], axis=1)
    small_all = lax.all_gather(small_local, "fsdp", axis=0, tiled=True)
    weights_all = lax.all_gather(weights_local, "fsdp", axis=0, tiled=True)
    qkv_all = weights_all[:, : width_q + 2 * width_k]
    out_all = weights_all[:, width_q + 2 * width_k :]
    router_all = small_all[:, :experts_all]
    attn_all = small_all[:, experts_all].astype(full)
    moe_all = small_all[:, experts_all + 1].astype(full)
    late_cols = width * 7 // 16
    g_all = lax.all_gather(
        jnp.concatenate([cotangent, swap_ctx(cotangent[:, late_cols:])], axis=1), "fsdp", axis=0, tiled=True
    ).reshape(fsdp // 2, 2, rows_dev, 2 * width - late_cols)

    sequence_in = sequence(tokens).astype(full)
    low_in = rms_scale(sequence_in, attn_all).astype(low)
    projected = mul(low_in, qkv_all)
    cosine, sine = (t[:, 0] for t in angles(jnp.arange(2 * rows_dev, dtype=jnp.int32), head_dim))
    sine = jnp.concatenate([-sine[:, : head_dim // 2], sine[:, head_dim // 2 :]], axis=1)
    gain_q, gain_k = query_gain.astype(full)[None], key_gain.astype(full)[None]
    attended, roped_q, roped_k, values_low = attend(
        projected, cosine, sine, gain_q, gain_k, kv_heads, group
    )
    branch = mul(attended, out_all)
    inputs = tokens.astype(full)
    mixed = (
        inputs
        + of_block(branch, rank)
        + swap_ctx(of_block(branch, 1 - rank).astype(low)).astype(full)
    )
    low_mid = rms_scale(mixed, moe_all).astype(low)
    m_all = lax.all_gather(jnp.concatenate([low_mid, swap_ctx(low_mid)]), "fsdp", axis=0, tiled=True)

    logits = mul(low_mid, router_all)
    named = routes[:, :, None] == jnp.arange(experts_all, dtype=jnp.int32)[None, None, :]
    selected = jnp.sum(jnp.where(named, logits[:, None, :], 0.0), axis=2)
    gates = gating(selected)
    chosen = jnp.any(named, axis=1)
    gates_wide = jnp.sum(jnp.where(named, gates[:, :, None], 0.0), axis=1)
    gates_sent = jnp.where(chosen, gates_wide, -1.0).T
    gates_all = lax.all_to_all(gates_sent, both, split_axis=0, concat_axis=0, tiled=True)

    g_all, gates_all = hold(g_all, gates_all)
    g_far = swap_ctx(g_all[..., :late_cols])

    lines = fsdp // 4
    places = list(range(1, lines)) + [0]
    cut = lines // 2
    parts = [places[:cut], places[cut:]]
    m_all = m_all.reshape(fsdp // 2, 2, 2, rows_dev, width)
    gates_all = gates_all.reshape(fsdp // 2, 2, 2, 1, rows_dev)
    state = dict(kept=None, first=0, core=core[None].astype(jnp.int32))

    def order_of(steps):
        spots = [((place - p) % lines) * 2 + (side + d) % 2 for d, _, p in steps]
        far = [i for i, step in enumerate(steps) if step[1] == 1] or [0]
        return jnp.stack(
            [
                jnp.asarray(item, jnp.int32)
                for i, step in enumerate(steps)
                for item in (
                    spots[i],
                    (rank + step[1]) % 2,
                    step[1],
                    spots[min(far, key=lambda j, i=i: abs(j - i))],
                )
            ]
        )

    def call(steps, raw=False):
        keep_back, send_back, *kept = run_expert(
            state["core"],
            order_of(steps),
            state["first"],
            4 * lines,
            m_all,
            g_all,
            g_far,
            gates_all,
            expert_gate_up[0],
            expert_down[0],
            capacity,
            state["kept"],
        )
        state["kept"] = kept
        state["first"] += len(steps)
        return (keep_back, send_back) if raw else over_core(keep_back, send_back)

    def wait(first):
        state["core"], first = hold(state["core"], first)
        return first

    steps_far, steps_own = ([(d, d, p) for p in places] for d in (1, 0))
    steps_mixed = [[(1, 0, p) for p in part] + [(0, 1, p) for p in part] for part in parts]
    back = call(steps_far)
    far_one, far_two = wait([pick_sum(back, 0, lines, column) for column in range(2)])
    far_one, far_two = swap_ctx(far_one), swap_side(far_two)

    def mixed_sums(back, at=0):
        return [
            pick_sum(back, start, start + cut, column) for start in (at, at + cut) for column in range(2)
        ]

    def rounds(sums, part):
        side_one, side_two, ctx_one, ctx_two = sums
        span = slice(part * cut, (part + 1) * cut)
        return [
            swap_ctx(ctx_one),
            swap_side(side_two),
            swap_side(add_low(side_one, far_one[span])),
            swap_ctx(add_low(ctx_two, far_two[span])),
        ]

    keep, send = call(steps_mixed[0], raw=True)
    send, (far_one, far_two) = hold(send, (far_one, far_two))
    back = over_core(keep, send)
    back_own = call(steps_own)
    sums = wait(mixed_sums(back))
    back_own = [pick_sum(back_own, 0, lines, column) for column in range(2)]
    got = rounds(sums, 0)
    keep, send = call(steps_mixed[1], raw=True)
    send, got = hold(send, got)
    back = over_core(keep, send)
    entries = joined(parts[0], [item[:cut] for item in back_own], got)
    arrived = {p: line_shift(entries[p], lines - p) for p in parts[0]}
    gate_back, rows, grad_rows, hidden, grad_pair = state["kept"]
    hidden, sums = hold(hidden, mixed_sums(back))
    got = rounds(sums, 1)
    grad_gates = lax.all_to_all(
        gate_back.reshape(fsdp * 2, rows_dev), both, split_axis=0, concat_axis=0, tiled=True
    ).T
    def results(first, steps, hidden):
        return run_result(
            state["core"], order_of(steps), first, hidden, gates_all, expert_down[0], capacity
        )

    out_far = results(0, steps_far, hidden)
    out_rest = results(lines, steps_mixed[0] + steps_own + steps_mixed[1], hidden)
    got, out_far, out_rest, arrived, grad_gates = lax.optimization_barrier(
        (got, out_far, out_rest, arrived, grad_gates)
    )
    entries.update(joined(parts[1], [item[cut:] for item in back_own], got))
    out_far = over_core(*out_far)
    out_far = [pick_sum(out_far, 0, lines, 0), swap_side(pick_sum(out_far, 0, lines, 1))]
    out_rest = over_core(*out_rest)
    for p in parts[1][:-1]:
        arrived[p] = line_shift(entries[p], lines - p)
    grad_mid = line_total(entries[0], arrived)

    grad_wide = jnp.where(chosen, grad_gates, 0.0)
    grad_logits = (
        gates_wide * (grad_wide - jnp.sum(gates_wide * grad_wide, axis=1, keepdims=True))
    ).astype(low)
    grad_router = mul(low_mid, grad_logits, lhs_turned)
    grad_mid = grad_mid + mul(grad_logits, router_all, rhs_turned)
    grad_mixed_part, grad_moe_gain = rms_back(mixed, moe_all, grad_mid)
    grad_mixed = cotangent.astype(full) + grad_mixed_part

    low_mixed, (out_far[0], out_rest) = hold(grad_mixed.astype(low), (out_far[0], out_rest))
    grad_branch = sequence(low_mixed)
    out_sums = [
        jnp.concatenate([one, two])
        for one, two in zip(mixed_sums(out_rest), mixed_sums(out_rest, 2 * cut + lines))
    ]
    out_own = [pick_sum(out_rest, 2 * cut, 2 * cut + lines, column) for column in range(2)]
    (out_far[0], out_sums, out_own), grad_branch = hold((out_far[0], out_sums, out_own), grad_branch)
    side_one, side_two, ctx_one, ctx_two = out_sums
    out_far[0] = swap_ctx(out_far[0])
    grad_attended = mul(grad_branch, out_all, rhs_turned).astype(low)
    grad_attended, out_far = hold(grad_attended, out_far)
    got = [
        swap_ctx(ctx_one),
        swap_side(side_two),
        swap_side(add_low(side_one, out_far[0])),
        swap_ctx(add_low(ctx_two, out_far[1])),
    ]
    grad_out_part = mul(attended, grad_branch, lhs_turned).astype(low)
    grad_q, grad_k, grad_v, gain_q_part, gain_k_part = attend_grad(
        projected, roped_q, roped_k, values_low, grad_attended, cosine, sine, gain_q, gain_k, kv_heads, group
    )
    grad_projected = jnp.concatenate([grad_q, grad_k, grad_v], axis=1)
    grad_projected, (got[0], got[1]) = hold(grad_projected, (got[0], got[1]))
    grad_qkv_part = mul(low_in, grad_projected, lhs_turned).astype(low)
    grad_projected, got = hold(grad_projected, got)
    entries = joined(places, out_own, got)
    grad_projected, entries, rows, grad_pair, hidden, grad_rows = lax.optimization_barrier(
        (grad_projected, entries, rows, grad_pair, hidden, grad_rows)
    )
    arrived = {p: line_shift(entries[p], lines - p) for p in places[:-1]}
    grad_normed_part = mul(grad_projected, qkv_all, rhs_turned)
    grad_gate_up = mul(rows, grad_pair, lhs_turned)[None]
    grad_down = mul(hidden, grad_rows, lhs_turned)[None]
    output = (mixed + line_total(entries[0], arrived)).astype(low)
    grad_normed = of_block(grad_normed_part, rank) + swap_ctx(
        of_block(grad_normed_part, 1 - rank).astype(low)
    ).astype(full)
    grad_in_part, grad_attn_gain = rms_back(inputs, attn_all, grad_normed)
    grad_tokens = grad_mixed + grad_in_part

    out_mine = lax.psum_scatter(grad_out_part, "fsdp", scatter_dimension=0, tiled=True).astype(full)
    out_other = swap_ctx(out_mine.astype(low)).astype(full)
    grad_out = jnp.where(
        rank == 0,
        jnp.concatenate([out_mine, out_other], axis=0),
        jnp.concatenate([out_other, out_mine], axis=0),
    )
    qkv_mine = lax.psum_scatter(grad_qkv_part, "fsdp", scatter_dimension=0, tiled=True)
    grad_qkv = all_heads(rank_at, qkv_mine, swap_ctx(qkv_mine), head_dim, my_heads)
    early = sum_owned(jnp.concatenate([grad_router.T, grad_moe_gain[None]], axis=0), fsdp, spot)
    late = sum_all(
        jnp.concatenate(
            [
                grad_attn_gain.reshape(-1, head_dim),
                jnp.sum(gain_q_part, axis=0),
                jnp.sum(gain_k_part, axis=0),
            ],
            axis=0,
        ),
        fsdp,
    )
    gain_rows = width // head_dim
    return (
        output,
        grad_tokens,
        grad_qkv,
        grad_out,
        early[:experts_all].T,
        lax.dynamic_slice_in_dim(late[:gain_rows].reshape(-1), spot * shard, shard, 0),
        early[experts_all],
        late[gain_rows],
        late[gain_rows + 1],
        grad_gate_up,
        grad_down,
    )


gathered_bytes = 1 << 26


def choose_body(*args):
    tokens, gate_up = args[0], args[8]
    fsdp, ctx = lax.axis_size("fsdp"), lax.axis_size("ctx")
    fits = tokens.size * tokens.dtype.itemsize * fsdp * ctx <= gathered_bytes
    if fits and fsdp % 4 == 0 and ctx == 2 and fsdp >= 8 and fsdp & (fsdp - 1) == 0 and gate_up.shape[0] == 1:
        return body_gathered(*args)
    return body_routed(*args)


def solution(mesh):
    in_specs = (
        P(("fsdp", "ctx"), None),
        P("fsdp", None),
        P("fsdp", None),
        P("fsdp", None),
        P("fsdp"),
        P("fsdp"),
        P(),
        P(),
        P(("fsdp", "ctx"), None, None),
        P(("fsdp", "ctx"), None, None),
        P(("fsdp", "ctx"), None),
        P(("fsdp", "ctx"), None),
    )
    out_specs = (
        P(("fsdp", "ctx"), None),
        P(("fsdp", "ctx"), None),
        P("fsdp", None),
        P("fsdp", None),
        P("fsdp", None),
        P("fsdp"),
        P("fsdp"),
        P(),
        P(),
        P(("fsdp", "ctx"), None, None),
        P(("fsdp", "ctx"), None, None),
    )
    return jax.shard_map(choose_body, mesh=mesh, in_specs=in_specs, out_specs=out_specs, check_vma=False)
```

```python
import functools
import math

import jax
import jax.numpy as jnp
from jax import lax
from jax.experimental import pallas as pl
from jax.experimental.pallas import tpu as pltpu
from jax.sharding import PartitionSpec as P

eps_norm = 1e-06
theta_base = 1000000.0


def rms_scale(values, gain):
    return values * lax.rsqrt(jnp.mean(values * values, axis=-1, keepdims=True) + eps_norm) * gain


def rotate(values, cosine, sine):
    half_width = values.shape[-1] // 2
    turned = jnp.concatenate([-values[..., half_width:], values[..., :half_width]], axis=-1)
    return values * cosine + turned * sine


def angles(positions, width):
    freqs = theta_base ** (-(jnp.arange(width // 2, dtype=jnp.float32) * 2.0) / width)
    phase = positions.astype(jnp.float32)[:, None] * freqs[None, :]
    phase = jnp.concatenate([phase, phase], axis=-1)
    return (jnp.cos(phase)[:, None, :], jnp.sin(phase)[:, None, :])


def device_positions(block_rank, ctx_count, tok_rows):
    half_rows = tok_rows // 2
    within = jnp.arange(tok_rows, dtype=jnp.int32)
    span_id = jnp.where(within < half_rows, block_rank, 2 * ctx_count - 1 - block_rank)
    return span_id * half_rows + within % half_rows


def attend_head(query, keys_in, values_in, causal, scale_root):
    scores = (
        jnp.einsum("tgd,sd->gts", query, keys_in, preferred_element_type=jnp.float32) / scale_root
    )
    expo = jnp.where(causal[None], jnp.exp(scores), 0.0)
    totals = jnp.sum(expo, axis=-1, keepdims=True)
    probs = (expo / totals).astype(jnp.bfloat16)
    attended = jnp.einsum("gts,sd->tgd", probs, values_in, preferred_element_type=jnp.float32)
    return (attended, jnp.log(totals[..., 0]))


def attend_back(query, keys_in, values_in, causal, log_total, grad_attended, scale_root):
    scores = (
        jnp.einsum("tgd,sd->gts", query, keys_in, preferred_element_type=jnp.float32) / scale_root
    )
    probs = jnp.where(causal[None], jnp.exp(scores - log_total[..., None]), 0.0)
    low_probs = probs.astype(jnp.bfloat16)
    grad_values = jnp.einsum(
        "gts,tgd->sd", low_probs, grad_attended, preferred_element_type=jnp.float32
    )
    grad_probs = jnp.einsum(
        "tgd,sd->gts", grad_attended, values_in, preferred_element_type=jnp.float32
    )
    delta_rows = jnp.sum(grad_probs * probs, axis=-1, keepdims=True)
    grad_scores = (probs * (grad_probs - delta_rows)).astype(jnp.bfloat16)
    grad_query = (
        jnp.einsum("gts,sd->tgd", grad_scores, keys_in, preferred_element_type=jnp.float32)
        / scale_root
    )
    grad_keys = (
        jnp.einsum("gts,tgd->sd", grad_scores, query, preferred_element_type=jnp.float32)
        / scale_root
    )
    return (grad_query, grad_keys, grad_values)


def swiglu(paired):
    half_width = paired.shape[-1] // 2
    return jax.nn.silu(paired[..., :half_width]) * paired[..., half_width:]


def gating(selected):
    expo = jnp.exp(selected)
    return expo / jnp.sum(expo, axis=1, keepdims=True)


def body_routed(
    tokens,
    qkv_weight,
    out_weight,
    router_weight,
    attn_gain,
    moe_gain,
    query_gain,
    key_gain,
    expert_gate_up,
    expert_down,
    routes,
    cotangent,
):
    rows_dev, width = tokens.shape
    head_dim = query_gain.shape[0]
    top_k = routes.shape[1]
    ctx_count = lax.axis_size("ctx")
    ctx_rank = lax.axis_index("ctx")
    qkv_all, out_all, router_all, attn_all, moe_all = (
        lax.all_gather(qkv_weight, "fsdp", axis=0, tiled=True),
        lax.all_gather(out_weight, "fsdp", axis=0, tiled=True),
        lax.all_gather(router_weight, "fsdp", axis=0, tiled=True),
        lax.all_gather(attn_gain, "fsdp", axis=0, tiled=True),
        lax.all_gather(moe_gain, "fsdp", axis=0, tiled=True),
    )
    experts_all = router_all.shape[1]
    heads = out_all.shape[0] // head_dim
    kv_heads = (qkv_all.shape[1] // head_dim - heads) // 2
    group_size = heads // kv_heads
    capacity = 2 * rows_dev * top_k // experts_all
    width_q = heads * head_dim
    width_k = kv_heads * head_dim
    scale_root = math.sqrt(head_dim)
    inputs = tokens.astype(jnp.float32)
    normed_in = rms_scale(inputs, attn_all.astype(jnp.float32))
    low_in = normed_in.astype(jnp.bfloat16)
    projected = jnp.dot(low_in, qkv_all, preferred_element_type=jnp.float32)
    query_raw = projected[:, :width_q].reshape(rows_dev, heads, head_dim)
    key_raw = projected[:, width_q : width_q + width_k].reshape(rows_dev, kv_heads, head_dim)
    value_low = (
        projected[:, width_q + width_k :].astype(jnp.bfloat16).reshape(rows_dev, kv_heads, head_dim)
    )
    positions = device_positions(ctx_rank, ctx_count, rows_dev)
    cosine, sine = angles(positions, head_dim)
    query_gain_f = query_gain.astype(jnp.float32)
    key_gain_f = key_gain.astype(jnp.float32)

    def query_rope(values_in, gain):
        return rotate(rms_scale(values_in, gain), cosine, sine)

    query_low = query_rope(query_raw, query_gain_f).astype(jnp.bfloat16)
    key_low = query_rope(key_raw, key_gain_f).astype(jnp.bfloat16)
    keys_all, values_all = (
        lax.all_gather(key_low, "ctx", axis=0, tiled=True),
        lax.all_gather(value_low, "ctx", axis=0, tiled=True),
    )
    key_pos = jnp.concatenate(
        [device_positions(other, ctx_count, rows_dev) for other in range(ctx_count)]
    )
    causal = key_pos[None, :] <= positions[:, None]
    query_heads = query_low.reshape(rows_dev, kv_heads, group_size, head_dim).transpose(1, 0, 2, 3)
    key_heads = keys_all.transpose(1, 0, 2)
    value_heads = values_all.transpose(1, 0, 2)
    attended, log_total = lax.map(
        lambda member: attend_head(member[0], member[1], member[2], causal, scale_root),
        (query_heads, key_heads, value_heads),
    )
    attended_low = attended.transpose(1, 0, 2, 3).reshape(rows_dev, width_q).astype(jnp.bfloat16)
    mixed = inputs + jnp.dot(attended_low, out_all, preferred_element_type=jnp.float32)
    normed_mid = rms_scale(mixed, moe_all.astype(jnp.float32))
    low_mid = normed_mid.astype(jnp.bfloat16)
    logits = jnp.dot(low_mid, router_all, preferred_element_type=jnp.float32)
    selected = jnp.take_along_axis(logits, routes, axis=1)
    gates, gate_back = jax.vjp(gating, selected)
    flat_routes = routes.reshape(-1)
    expert_ids = jnp.arange(experts_all, dtype=jnp.int32)
    hit_table = (flat_routes[:, None] == expert_ids[None, :]).astype(jnp.int32)
    slot_index = jnp.sum(jnp.cumsum(hit_table, axis=0) * hit_table, axis=1) - 1
    target = flat_routes * capacity + slot_index
    pair_count = rows_dev * top_k
    source_pair = (
        jnp.full((experts_all * capacity,), pair_count, jnp.int32)
        .at[target]
        .set(jnp.arange(pair_count, dtype=jnp.int32))
    )
    padded = jnp.concatenate([low_mid, jnp.zeros((1, width), jnp.bfloat16)], axis=0)
    outgoing = padded[source_pair // top_k].reshape(experts_all, capacity, width)
    received = lax.all_to_all(outgoing, ("fsdp", "ctx"), split_axis=0, concat_axis=1, tiled=True)
    gate_and_up = jnp.einsum(
        "esd,edf->esf", received, expert_gate_up, preferred_element_type=jnp.float32
    )
    hidden_val, swiglu_back = jax.vjp(swiglu, gate_and_up)
    hidden_low = hidden_val.astype(jnp.bfloat16)
    result_low = jnp.einsum(
        "esf,efd->esd", hidden_low, expert_down, preferred_element_type=jnp.float32
    ).astype(jnp.bfloat16)
    returned = lax.all_to_all(
        result_low, ("fsdp", "ctx"), split_axis=1, concat_axis=0, tiled=True
    ).reshape(experts_all * capacity, width)
    picked = returned[target].reshape(rows_dev, top_k, width).astype(jnp.float32)
    output = (mixed + jnp.sum(gates[:, :, None] * picked, axis=1)).astype(jnp.bfloat16)
    qkv_back, out_back, router_back, attn_back_g, moe_back_g = (
        qkv_all,
        out_all,
        router_all,
        attn_all,
        moe_all,
    )
    grad_final = cotangent.astype(jnp.float32)
    grad_gates = jnp.sum(grad_final[:, None, :] * picked, axis=2)
    grad_result = (
        (gates[:, :, None] * grad_final[:, None, :]).astype(jnp.bfloat16).reshape(pair_count, width)
    )
    grad_padded = jnp.concatenate([grad_result, jnp.zeros((1, width), jnp.bfloat16)], axis=0)
    grad_outgoing = grad_padded[source_pair].reshape(experts_all, capacity, width)
    grad_received = lax.all_to_all(
        grad_outgoing, ("fsdp", "ctx"), split_axis=0, concat_axis=1, tiled=True
    )
    grad_down = jnp.einsum(
        "esf,esd->efd", hidden_low, grad_received, preferred_element_type=jnp.float32
    )
    grad_hidden = jnp.einsum(
        "esd,efd->esf", grad_received, expert_down, preferred_element_type=jnp.float32
    )
    grad_paired = swiglu_back(grad_hidden)[0].astype(jnp.bfloat16)
    grad_gate_up = jnp.einsum(
        "esd,esf->edf", received, grad_paired, preferred_element_type=jnp.float32
    )
    grad_rows = jnp.einsum(
        "esf,edf->esd", grad_paired, expert_gate_up, preferred_element_type=jnp.float32
    ).astype(jnp.bfloat16)
    grad_returned = lax.all_to_all(
        grad_rows, ("fsdp", "ctx"), split_axis=1, concat_axis=0, tiled=True
    ).reshape(experts_all * capacity, width)
    grad_mid = jnp.sum(
        grad_returned[target].reshape(rows_dev, top_k, width).astype(jnp.float32), axis=1
    )
    grad_selected = gate_back(grad_gates)[0]
    route_table = (routes[:, :, None] == expert_ids[None, None, :]).astype(jnp.float32)
    grad_logits = jnp.sum(route_table * grad_selected[:, :, None], axis=1).astype(jnp.bfloat16)
    grad_router = jnp.dot(low_mid.T, grad_logits, preferred_element_type=jnp.float32)
    grad_mid = grad_mid + jnp.dot(grad_logits, router_back.T, preferred_element_type=jnp.float32)
    unused_mid, mid_back = jax.vjp(rms_scale, mixed, moe_back_g.astype(jnp.float32))
    grad_mixed_part, grad_moe_gain = mid_back(grad_mid)
    grad_mixed = grad_final + grad_mixed_part
    grad_branch = grad_mixed.astype(jnp.bfloat16)
    grad_out = jnp.dot(attended_low.T, grad_branch, preferred_element_type=jnp.float32)
    grad_attended = jnp.dot(grad_branch, out_back.T, preferred_element_type=jnp.float32).astype(
        jnp.bfloat16
    )
    grad_heads = grad_attended.reshape(rows_dev, kv_heads, group_size, head_dim).transpose(
        1, 0, 2, 3
    )
    grad_query_h, grad_key_h, grad_value_h = lax.map(
        lambda member: attend_back(
            member[0], member[1], member[2], causal, member[3], member[4], scale_root
        ),
        (query_heads, key_heads, value_heads, log_total, grad_heads),
    )
    grad_keys, grad_values = (
        lax.psum_scatter(
            grad_key_h.transpose(1, 0, 2).astype(jnp.bfloat16),
            "ctx",
            scatter_dimension=0,
            tiled=True,
        ).astype(jnp.float32),
        lax.psum_scatter(
            grad_value_h.transpose(1, 0, 2).astype(jnp.bfloat16),
            "ctx",
            scatter_dimension=0,
            tiled=True,
        ).astype(jnp.float32),
    )
    grad_query_rot = (
        grad_query_h.transpose(1, 0, 2, 3).reshape(rows_dev, heads, head_dim).astype(jnp.bfloat16)
    )
    grad_query_rot = lax.optimization_barrier(grad_query_rot).astype(jnp.float32)
    grad_key_rot = lax.optimization_barrier(grad_keys.astype(jnp.bfloat16)).astype(jnp.float32)
    unused_query, query_back = jax.vjp(query_rope, query_raw, query_gain_f)
    grad_query_raw, grad_query_gain = query_back(grad_query_rot)
    unused_key, key_back = jax.vjp(query_rope, key_raw, key_gain_f)
    grad_key_raw, grad_key_gain = key_back(grad_key_rot)
    grad_projected = jnp.concatenate(
        [
            grad_query_raw.reshape(rows_dev, width_q).astype(jnp.bfloat16),
            grad_key_raw.reshape(rows_dev, width_k).astype(jnp.bfloat16),
            grad_values.reshape(rows_dev, width_k).astype(jnp.bfloat16),
        ],
        axis=1,
    )
    grad_qkv = jnp.dot(low_in.T, grad_projected, preferred_element_type=jnp.float32)
    grad_normed = jnp.dot(grad_projected, qkv_back.T, preferred_element_type=jnp.float32)
    unused_in, in_back = jax.vjp(rms_scale, inputs, attn_back_g.astype(jnp.float32))
    grad_in_part, grad_attn_gain = in_back(grad_normed)
    grad_tokens = grad_mixed + grad_in_part
    gradients = (grad_qkv, grad_out, grad_router, grad_attn_gain, grad_moe_gain)
    pieces = (
        lax.psum_scatter(gradients[0], "fsdp", scatter_dimension=0, tiled=True),
        lax.psum_scatter(gradients[1], "fsdp", scatter_dimension=0, tiled=True),
        lax.psum_scatter(gradients[2], "fsdp", scatter_dimension=0, tiled=True),
        lax.psum_scatter(gradients[3], "fsdp", scatter_dimension=0, tiled=True),
        lax.psum_scatter(gradients[4], "fsdp", scatter_dimension=0, tiled=True),
    )
    reduced = (
        lax.psum(pieces[0].astype(jnp.bfloat16), "ctx").astype(jnp.float32),
        lax.psum(pieces[1].astype(jnp.bfloat16), "ctx").astype(jnp.float32),
        lax.psum(pieces[2].astype(jnp.bfloat16), "ctx").astype(jnp.float32),
        lax.psum(pieces[3].astype(jnp.bfloat16), "ctx").astype(jnp.float32),
        lax.psum(pieces[4].astype(jnp.bfloat16), "ctx").astype(jnp.float32),
    )
    gain_sums = lax.psum((grad_query_gain, grad_key_gain), ("fsdp", "ctx"))
    return (
        output,
        grad_tokens,
        reduced[0],
        reduced[1],
        reduced[2],
        reduced[3],
        reduced[4],
        gain_sums[0],
        gain_sums[1],
        grad_gate_up,
        grad_down,
    )


low = jnp.bfloat16
full = jnp.float32
plain = (((1,), (0,)), ((), ()))
rhs_turned = (((1,), (1,)), ((), ()))
lhs_turned = (((0,), (0,)), ((), ()))
vmem_bytes = 58 << 20


def mul(left, right, dims=plain):
    return lax.dot_general(left, right, dims, preferred_element_type=full)


def core_pairs(fsdp):
    return [(i, i ^ 1) for i in range(fsdp)]


def side_pairs(fsdp):
    return [(i, i ^ 2) for i in range(fsdp)]


def swap_core(values):
    return lax.ppermute(values, "fsdp", core_pairs(lax.axis_size("fsdp")))


def swap_side(values):
    return lax.ppermute(values, "fsdp", side_pairs(lax.axis_size("fsdp")))


def swap_ctx(values):
    return lax.ppermute(values, "ctx", [(0, 1), (1, 0)])


def add_low(one, two):
    return (one.astype(full) + two.astype(full)).astype(low)


def hold(values, first):
    return lax.optimization_barrier((values, first))


def take(values, index):
    return lax.dynamic_index_in_dim(values, index, 0, keepdims=False)


def line_shift(values, step):
    fsdp = lax.axis_size("fsdp")
    return lax.ppermute(values, "fsdp", [(i, (i + 4 * step) % fsdp) for i in range(fsdp)])


def line_total(own, arrived):
    total = own.astype(full)
    for item in arrived.values():
        total = total + item.astype(full)
    return total


def joined(places, own, got):
    from_ctx, from_side, one_side, two_ctx = got
    entries = {}
    for at, p in enumerate(places):
        one = add_low(add_low(own[0][at], from_ctx[at]), one_side[at])
        two = add_low(add_low(own[1][at], from_side[at]), two_ctx[at])
        entries[p] = jnp.concatenate([one, two], axis=-1)
    return entries


def over_core(keep, send):
    return keep, swap_core(send)


def pick_sum(parts, start, stop, column):
    keep, other = parts
    half = keep.shape[-1] // 2
    cut = (slice(start, stop), slice(None), slice(column * half, (column + 1) * half))
    return add_low(keep[cut], other[cut])


def sum_all(values, fsdp):
    values = values + lax.ppermute(values, "fsdp", core_pairs(fsdp))
    values = values + swap_ctx(values)
    step = 2
    while step < fsdp:
        values = values + lax.ppermute(values, "fsdp", [(i, i ^ step) for i in range(fsdp)])
        step *= 2
    return values


def sum_owned(values, fsdp, spot):
    items, shard = values.shape[0], values.shape[1] // fsdp
    values = values.reshape(items, fsdp, shard).swapaxes(0, 1)
    step = fsdp // 2
    while step:
        bit = (spot // step) % 2
        values = values.reshape(2, step, items, shard)
        other = lax.ppermute(take(values, 1 - bit), "fsdp", [(i, i ^ step) for i in range(fsdp)])
        values = take(values, bit) + other
        step //= 2
    values = values[0]
    return values + swap_ctx(values)


def turn(values):
    return pltpu.roll(values, values.shape[-1] // 2, 1)


def norm_rope(raw, gain, cosine, sine):
    scale = lax.rsqrt(jnp.mean(raw * raw, axis=-1, keepdims=True) + eps_norm)
    scaled = raw * scale * gain
    return scaled * cosine + turn(scaled) * sine


def norm_rope_back(raw, gain, cosine, sine, grad):
    scale = lax.rsqrt(jnp.mean(raw * raw, axis=-1, keepdims=True) + eps_norm)
    unit = raw * scale
    grad_scaled = grad * cosine - turn(grad) * sine
    grad_gain = jnp.sum(grad_scaled * unit, axis=0, keepdims=True)
    grad_unit = grad_scaled * gain
    grad_raw = scale * (grad_unit - unit * jnp.mean(grad_unit * unit, axis=-1, keepdims=True))
    return grad_raw, grad_gain


def tiles_of(rows):
    step = rows // 2
    return [(start, start + step) for start in range(0, rows, step)]


def allowed(start, stop):
    shape = (stop - start, stop)
    return lax.broadcasted_iota(jnp.int32, shape, 1) <= (
        lax.broadcasted_iota(jnp.int32, shape, 0) + start
    )


def attend_kernel(q_ref, k_ref, v_ref, cos_ref, sin_ref, qg_ref, kg_ref, o_ref, qr_ref, kr_ref, vl_ref):
    head_dim = k_ref.shape[1]
    rows = k_ref.shape[0]
    cosine, sine = cos_ref[...], sin_ref[...]
    keys = norm_rope(k_ref[...], kg_ref[...], cosine, sine).astype(low)
    values = v_ref[...].astype(low)
    kr_ref[...] = keys
    vl_ref[...] = values
    for head in range(q_ref.shape[1] // head_dim):
        cols = slice(head * head_dim, (head + 1) * head_dim)
        query = norm_rope(q_ref[:, cols], qg_ref[...], cosine, sine).astype(low)
        qr_ref[:, cols] = query
        for start, stop in tiles_of(rows):
            scores = mul(query[start:stop], keys[:stop], rhs_turned) * (1.0 / math.sqrt(head_dim))
            expo = jnp.where(allowed(start, stop), jnp.exp(scores), 0.0)
            probs = (expo / jnp.sum(expo, axis=-1, keepdims=True)).astype(low)
            o_ref[start:stop, cols] = mul(probs, values[:stop]).astype(low)


def attend_grad_kernel(
    q_ref, k_ref, qr_ref, kr_ref, vl_ref, go_ref, cos_ref, sin_ref, qg_ref, kg_ref,
    dq_ref, dk_ref, dv_ref, dqg_ref, dkg_ref, dk_sum, dv_sum, dq_sum,
):
    head_dim = k_ref.shape[1]
    rows = k_ref.shape[0]
    root = 1.0 / math.sqrt(head_dim)
    cosine, sine = cos_ref[...], sin_ref[...]
    keys, values = kr_ref[...], vl_ref[...]
    gain_sum = jnp.zeros((1, head_dim), full)
    dk_sum[...] = jnp.zeros_like(dk_sum)
    dv_sum[...] = jnp.zeros_like(dv_sum)
    for head in range(q_ref.shape[1] // head_dim):
        cols = slice(head * head_dim, (head + 1) * head_dim)
        for start, stop in tiles_of(rows):
            query = qr_ref[start:stop, cols]
            grad = go_ref[start:stop, cols]
            scores = mul(query, keys[:stop], rhs_turned) * root
            expo = jnp.where(allowed(start, stop), jnp.exp(scores), 0.0)
            probs = expo / jnp.sum(expo, axis=-1, keepdims=True)
            grad_probs = mul(grad, values[:stop], rhs_turned)
            delta = jnp.sum(grad_probs * probs, axis=-1, keepdims=True)
            grad_scores = (probs * (grad_probs - delta)).astype(low)
            dv_sum[:stop] += mul(probs.astype(low), grad, lhs_turned)
            dk_sum[:stop] += mul(grad_scores, query, lhs_turned)
            dq_sum[start:stop] = mul(grad_scores, keys[:stop])
        grad_query = (dq_sum[...] * root).astype(low).astype(full)
        grad_raw, grad_gain = norm_rope_back(q_ref[:, cols], qg_ref[...], cosine, sine, grad_query)
        dq_ref[:, cols] = grad_raw.astype(low)
        gain_sum = gain_sum + grad_gain
    dqg_ref[0] = gain_sum
    grad_key = (dk_sum[...] * root).astype(low).astype(full)
    grad_raw, grad_gain = norm_rope_back(k_ref[...], kg_ref[...], cosine, sine, grad_key)
    dk_ref[...] = grad_raw.astype(low)
    dkg_ref[0] = grad_gain
    dv_ref[...] = dv_sum[...].astype(low)


def attention_specs(rows, head_dim, kv_heads, group):
    wide, narrow = group * head_dim, head_dim
    heads_end = kv_heads * group
    return dict(
        q=pl.BlockSpec((rows, wide), lambda i: (0, i)),
        k=pl.BlockSpec((rows, narrow), lambda i: (0, heads_end + i)),
        v=pl.BlockSpec((rows, narrow), lambda i: (0, heads_end + kv_heads + i)),
        own=pl.BlockSpec((rows, narrow), lambda i: (0, i)),
        table=pl.BlockSpec((rows, head_dim), lambda i: (0, 0)),
        gain=pl.BlockSpec((1, head_dim), lambda i: (0, 0)),
        gain_out=pl.BlockSpec((1, 1, head_dim), lambda i: (i, 0, 0)),
    )


def attend(projected, cosine, sine, query_gain, key_gain, kv_heads, group):
    rows, head_dim = cosine.shape
    s = attention_specs(rows, head_dim, kv_heads, group)
    shape = jax.ShapeDtypeStruct
    work = rows * rows * head_dim * kv_heads * group
    return pl.pallas_call(
        attend_kernel,
        grid=(kv_heads,),
        in_specs=[s["q"], s["k"], s["v"], s["table"], s["table"], s["gain"], s["gain"]],
        out_specs=[s["q"], s["q"], s["own"], s["own"]],
        out_shape=[
            shape((rows, kv_heads * group * head_dim), low),
            shape((rows, kv_heads * group * head_dim), low),
            shape((rows, kv_heads * head_dim), low),
            shape((rows, kv_heads * head_dim), low),
        ],
        compiler_params=pltpu.CompilerParams(vmem_limit_bytes=48 << 20),
        cost_estimate=pl.CostEstimate(
            flops=4 * work, bytes_accessed=projected.size * 6, transcendentals=work // head_dim
        ),
        name="attend",
    )(projected, projected, projected, cosine, sine, query_gain, key_gain)


def attend_grad(projected, roped_q, roped_k, values_low, grad, cosine, sine, query_gain, key_gain, kv_heads, group):
    rows, head_dim = cosine.shape
    s = attention_specs(rows, head_dim, kv_heads, group)
    shape = jax.ShapeDtypeStruct
    work = rows * rows * head_dim * kv_heads * group
    return pl.pallas_call(
        attend_grad_kernel,
        grid=(kv_heads,),
        in_specs=[
            s["q"], s["k"], s["q"], s["own"], s["own"], s["q"],
            s["table"], s["table"], s["gain"], s["gain"],
        ],
        out_specs=[s["q"], s["own"], s["own"], s["gain_out"], s["gain_out"]],
        out_shape=[
            shape((rows, kv_heads * group * head_dim), low),
            shape((rows, kv_heads * head_dim), low),
            shape((rows, kv_heads * head_dim), low),
            shape((kv_heads, 1, head_dim), full),
            shape((kv_heads, 1, head_dim), full),
        ],
        scratch_shapes=[pltpu.VMEM((rows, head_dim), full)] * 3,
        compiler_params=pltpu.CompilerParams(vmem_limit_bytes=48 << 20),
        cost_estimate=pl.CostEstimate(
            flops=10 * work, bytes_accessed=projected.size * 10, transcendentals=work // head_dim
        ),
        name="attend_grad",
    )(projected, projected, roped_q, roped_k, values_low, grad, cosine, sine, query_gain, key_gain)


def placed(gate, slots):
    block = gate.shape[1]
    shape = (block, block)
    earlier = (
        lax.broadcasted_iota(jnp.int32, shape, 0) < lax.broadcasted_iota(jnp.int32, shape, 1)
    ).astype(low)
    hit = jnp.where(gate >= 0.0, 1.0, 0.0)
    count = mul(jnp.broadcast_to(hit, (8, block)).astype(low), earlier)[:1].astype(jnp.int32)
    place = (lax.broadcasted_iota(jnp.int32, (slots, block), 0) == count) & (hit > 0.5)
    weight = jnp.sum(jnp.where(place, gate, 0.0), axis=1, keepdims=True)
    return place, place.astype(full).astype(low), weight


def expert_kernel(core_ref, order, m_ref, g_ref, far_ref, w_ref, gu_ref, dn_ref, *refs):
    keep_back, send_back, gate_back, rows_ref, dy_ref, z_ref, pair_ref = refs[-7:]
    core = core_ref[0]
    far = order[4 * pl.program_id(0) + 2] == 1
    width = m_ref.shape[4]
    hidden = dn_ref.shape[0]
    slots = z_ref.shape[0] // 2
    places, picks, weights, rows, grads = [], [], [], [], []
    for part in range(2):
        at = lax.rem(core + part, 2)
        place, pick, weight = placed(w_ref[0, at, 0], slots)
        places.append(place)
        picks.append(pick)
        weights.append(weight)
        rows.append(mul(pick, m_ref[0, at, 0]).astype(low))
        near_rows = g_ref[0, at, :, :width]
        far_rows = jnp.concatenate([far_ref[0, at], g_ref[0, at, :, width:]], axis=1)
        grads.append(mul(pick, jnp.where(far, far_rows, near_rows)).astype(low))
    row, grad, weight = (jnp.concatenate(items, axis=0) for items in (rows, grads, weights))
    rows_ref[...] = row
    paired = mul(row, gu_ref[...])
    gate_in, up = paired[:, :hidden], paired[:, hidden:]
    sig = jax.nn.sigmoid(gate_in)
    act = gate_in * sig
    z = (act * up).astype(low)
    z_ref[...] = z
    dy_ref[...] = (weight * grad.astype(full)).astype(low)
    unweighted = mul(grad, dn_ref[...], rhs_turned)
    grad_gate = jnp.sum(unweighted * z.astype(full), axis=1, keepdims=True)
    dz = weight * unweighted
    grad_in = dz * up * (sig * (1.0 + gate_in * (1.0 - sig)))
    pair = jnp.concatenate([grad_in, dz * act], axis=1).astype(low)
    pair_ref[...] = pair
    back = mul(pair, gu_ref[...], rhs_turned).astype(low)
    for part, out in enumerate((keep_back, send_back)):
        mine = slice(part * slots, (part + 1) * slots)
        out[0] = mul(picks[part], back[mine], lhs_turned).astype(low)
        gate_back[0, lax.rem(core + part, 2), 0] = jnp.sum(
            jnp.where(places[part], grad_gate[mine], 0.0), axis=0, keepdims=True
        )


def run_expert(core, order, first, total_steps, m_all, g_all, g_far, gates_all, gate_up, down, slots, kept):
    places, _, _, block, width = m_all.shape
    paired = gate_up.shape[1]
    steps = order.shape[0] // 4
    part_rows = steps * 2 * slots
    hidden = paired // 2
    shape = jax.ShapeDtypeStruct

    def gates_at(i, core, order):
        return (order[4 * i], 0, order[4 * i + 1], 0, 0)

    def token_at(i, core, order):
        return (order[4 * i], 0, order[4 * i + 2], 0, 0)

    def near_at(i, core, order):
        return (order[4 * i], 0, 0, 0)

    def far_at(i, core, order):
        return (order[4 * i + 3], 0, 0, 0)

    def fixed(i, core, order):
        return (0, 0)

    def flat(i, core, order):
        return (first + i, 0)

    def stacked(i, core, order):
        return (i, 0, 0)

    small = pl.BlockSpec((1, 2, 1, 1, block), gates_at)
    one_block = pl.BlockSpec((1, block, width), stacked)
    widths = (width, width, hidden, paired)
    grid_spec = pltpu.PrefetchScalarGridSpec(
        num_scalar_prefetch=2,
        grid=(steps,),
        in_specs=[
            pl.BlockSpec((1, 2, 1, block, width), token_at),
            pl.BlockSpec((1, 2, block, g_all.shape[3]), near_at),
            pl.BlockSpec((1, 2, block, g_far.shape[3]), far_at),
            small,
            pl.BlockSpec(gate_up.shape, fixed, pipeline_mode=pl.Buffered(1)),
            pl.BlockSpec(down.shape, fixed, pipeline_mode=pl.Buffered(1)),
        ]
        + [pl.BlockSpec(memory_space=pl.ANY)] * (0 if kept is None else 5),
        out_specs=[one_block] * 2 + [small] + [pl.BlockSpec((2 * slots, n), flat) for n in widths],
    )
    return pl.pallas_call(
        expert_kernel,
        grid_spec=grid_spec,
        out_shape=[shape((steps, block, width), low)] * 2
        + [shape((places, 2, 2, 1, block), full)]
        + [shape((total_steps * 2 * slots, n), low) for n in widths],
        input_output_aliases={} if kept is None else {8 + i: 2 + i for i in range(5)},
        compiler_params=pltpu.CompilerParams(vmem_limit_bytes=vmem_bytes),
        cost_estimate=pl.CostEstimate(
            flops=part_rows * width * (4 * paired + 2 * hidden + 6 * block),
            bytes_accessed=steps * block * width * 12 + part_rows * (width * 4 + paired * 3),
            transcendentals=part_rows * hidden,
        ),
        name="experts",
    )(core, order, m_all, g_all, g_far, gates_all, gate_up, down, *(() if kept is None else kept))


def result_kernel(core_ref, order, z_ref, w_ref, dn_ref, keep_out, send_out):
    core = core_ref[0]
    slots = z_ref.shape[0] // 2
    y = mul(z_ref[...], dn_ref[...]).astype(low).astype(full)
    for part, out in enumerate((keep_out, send_out)):
        _, pick, weight = placed(w_ref[0, lax.rem(core + part, 2), 0], slots)
        scaled = (weight * y[part * slots : (part + 1) * slots]).astype(low)
        out[0] = mul(pick, scaled, lhs_turned).astype(low)


def run_result(core, order, first, hidden, gates_all, down, slots):
    block, width, inner = gates_all.shape[4], down.shape[1], down.shape[0]
    steps = order.shape[0] // 4
    one_block = pl.BlockSpec((1, block, width), lambda i, core, order: (i, 0, 0))
    return pl.pallas_call(
        result_kernel,
        grid_spec=pltpu.PrefetchScalarGridSpec(
            num_scalar_prefetch=2,
            grid=(steps,),
            in_specs=[
                pl.BlockSpec((2 * slots, inner), lambda i, core, order: (first + i, 0)),
                pl.BlockSpec(
                    (1, 2, 1, 1, block), lambda i, core, order: (order[4 * i], 0, order[4 * i + 1], 0, 0)
                ),
                pl.BlockSpec(down.shape, lambda i, core, order: (0, 0), pipeline_mode=pl.Buffered(1)),
            ],
            out_specs=[one_block] * 2,
        ),
        out_shape=[jax.ShapeDtypeStruct((steps, block, width), low)] * 2,
        compiler_params=pltpu.CompilerParams(vmem_limit_bytes=vmem_bytes),
        cost_estimate=pl.CostEstimate(
            flops=steps * 2 * slots * width * (2 * inner + 2 * block),
            bytes_accessed=steps * (4 * block * width + 4 * slots * inner) + 2 * inner * width,
            transcendentals=0,
        ),
        name="results",
    )(core, order, hidden, gates_all, down)


def own_heads_kernel(rank, qkv_ref, out_ref, o_ref, *, head_dim, heads):
    first = rank[0] == 0
    for head in range(heads):
        pair = [qkv_ref[:, (2 * head + i) * head_dim : (2 * head + i + 1) * head_dim] for i in range(2)]
        o_ref[:, head * head_dim : (head + 1) * head_dim] = jnp.where(first, pair[0], pair[1])
    kv = qkv_ref.shape[1] - 2 * heads * head_dim
    o_ref[:, heads * head_dim : heads * head_dim + kv] = qkv_ref[:, 2 * heads * head_dim :]
    o_ref[:, heads * head_dim + kv :] = jnp.where(first, out_ref[:head_dim], out_ref[head_dim:])


def own_heads(rank, qkv_weight, out_weight, head_dim, heads):
    kv = qkv_weight.shape[1] - 2 * heads * head_dim
    return pl.pallas_call(
        functools.partial(own_heads_kernel, head_dim=head_dim, heads=heads),
        grid_spec=pltpu.PrefetchScalarGridSpec(
            num_scalar_prefetch=1,
            grid=(1,),
            in_specs=[
                pl.BlockSpec(qkv_weight.shape, lambda i, rank: (0, 0)),
                pl.BlockSpec(out_weight.shape, lambda i, rank: (0, 0)),
            ],
            out_specs=pl.BlockSpec(
                (qkv_weight.shape[0], heads * head_dim + kv + out_weight.shape[1]), lambda i, rank: (0, 0)
            ),
        ),
        out_shape=jax.ShapeDtypeStruct(
            (qkv_weight.shape[0], heads * head_dim + kv + out_weight.shape[1]), qkv_weight.dtype
        ),
        name="own_heads",
    )(rank, qkv_weight, out_weight)


def all_heads_kernel(rank, mine_ref, other_ref, o_ref, *, head_dim, heads):
    first = rank[0] == 0
    for head in range(heads):
        cols = slice(head * head_dim, (head + 1) * head_dim)
        mine, other = mine_ref[:, cols].astype(full), other_ref[:, cols].astype(full)
        o_ref[:, 2 * head * head_dim : (2 * head + 1) * head_dim] = jnp.where(first, mine, other)
        o_ref[:, (2 * head + 1) * head_dim : (2 * head + 2) * head_dim] = jnp.where(first, other, mine)
    o_ref[:, 2 * heads * head_dim :] = mine_ref[:, heads * head_dim :].astype(full) + other_ref[
        :, heads * head_dim :
    ].astype(full)


def all_heads(rank, mine, other, head_dim, heads):
    rows, width = mine.shape
    return pl.pallas_call(
        functools.partial(all_heads_kernel, head_dim=head_dim, heads=heads),
        grid_spec=pltpu.PrefetchScalarGridSpec(
            num_scalar_prefetch=1,
            grid=(1,),
            in_specs=[pl.BlockSpec((rows, width), lambda i, rank: (0, 0))] * 2,
            out_specs=pl.BlockSpec((rows, width + heads * head_dim), lambda i, rank: (0, 0)),
        ),
        out_shape=jax.ShapeDtypeStruct((rows, width + heads * head_dim), full),
        name="all_heads",
    )(rank, mine, other)


def rms_back(values, gain, grad):
    scale = lax.rsqrt(jnp.mean(values * values, axis=-1, keepdims=True) + eps_norm)
    unit = values * scale
    grad_gain = jnp.sum(grad * unit, axis=0)
    grad_unit = grad * gain
    back = scale * (grad_unit - unit * jnp.mean(grad_unit * unit, axis=-1, keepdims=True))
    return back, grad_gain


def in_order(first, second):
    half = first.shape[0] // 2
    return jnp.concatenate([first[:half], second, first[half:]], axis=0)


def of_block(values, rank):
    quarter = values.shape[0] // 4
    outer = jnp.concatenate([values[:quarter], values[3 * quarter :]], axis=0)
    return jnp.where(rank == 0, outer, values[quarter : 3 * quarter])


def body_gathered(
    tokens, qkv_weight, out_weight, router_weight, attn_gain, moe_gain, query_gain, key_gain,
    expert_gate_up, expert_down, routes, cotangent,
):
    rows_dev, width = tokens.shape
    head_dim = query_gain.shape[0]
    top_k = routes.shape[1]
    fsdp = lax.axis_size("fsdp")
    spot = lax.axis_index("fsdp")
    rank = lax.axis_index("ctx")
    place, side, core = spot // 4, (spot // 2) % 2, spot % 2
    shard = qkv_weight.shape[0]
    heads = out_weight.shape[0] * fsdp // head_dim
    kv_heads = (qkv_weight.shape[1] // head_dim - heads) // 2
    group = heads // kv_heads // 2
    my_heads = heads // 2
    width_q, width_k = my_heads * head_dim, kv_heads * head_dim
    experts_all = router_weight.shape[1]
    capacity = 2 * rows_dev * top_k // experts_all
    both = ("fsdp", "ctx")

    def sequence(values):
        other = swap_ctx(values)
        first = jnp.where(rank == 0, values, other)
        second = jnp.where(rank == 0, other, values)
        return in_order(first, second)

    rank_at = rank[None].astype(jnp.int32)
    weights_local = own_heads(rank_at, qkv_weight, out_weight, head_dim, my_heads)
    small_local = jnp.concatenate([router_weight, attn_gain[:, None], moe_gain[:, None]], axis=1)
    small_all = lax.all_gather(small_local, "fsdp", axis=0, tiled=True)
    weights_all = lax.all_gather(weights_local, "fsdp", axis=0, tiled=True)
    qkv_all = weights_all[:, : width_q + 2 * width_k]
    out_all = weights_all[:, width_q + 2 * width_k :]
    router_all = small_all[:, :experts_all]
    attn_all = small_all[:, experts_all].astype(full)
    moe_all = small_all[:, experts_all + 1].astype(full)
    late_cols = width * 7 // 16
    g_all = lax.all_gather(
        jnp.concatenate([cotangent, swap_ctx(cotangent[:, late_cols:])], axis=1), "fsdp", axis=0, tiled=True
    ).reshape(fsdp // 2, 2, rows_dev, 2 * width - late_cols)

    sequence_in = sequence(tokens).astype(full)
    low_in = rms_scale(sequence_in, attn_all).astype(low)
    projected = mul(low_in, qkv_all)
    cosine, sine = (t[:, 0] for t in angles(jnp.arange(2 * rows_dev, dtype=jnp.int32), head_dim))
    sine = jnp.concatenate([-sine[:, : head_dim // 2], sine[:, head_dim // 2 :]], axis=1)
    gain_q, gain_k = query_gain.astype(full)[None], key_gain.astype(full)[None]
    attended, roped_q, roped_k, values_low = attend(
        projected, cosine, sine, gain_q, gain_k, kv_heads, group
    )
    branch = mul(attended, out_all)
    inputs = tokens.astype(full)
    mixed = (
        inputs
        + of_block(branch, rank)
        + swap_ctx(of_block(branch, 1 - rank).astype(low)).astype(full)
    )
    low_mid = rms_scale(mixed, moe_all).astype(low)
    m_all = lax.all_gather(jnp.concatenate([low_mid, swap_ctx(low_mid)]), "fsdp", axis=0, tiled=True)

    logits = mul(low_mid, router_all)
    named = routes[:, :, None] == jnp.arange(experts_all, dtype=jnp.int32)[None, None, :]
    selected = jnp.sum(jnp.where(named, logits[:, None, :], 0.0), axis=2)
    gates = gating(selected)
    chosen = jnp.any(named, axis=1)
    gates_wide = jnp.sum(jnp.where(named, gates[:, :, None], 0.0), axis=1)
    gates_sent = jnp.where(chosen, gates_wide, -1.0).T
    gates_all = lax.all_to_all(gates_sent, both, split_axis=0, concat_axis=0, tiled=True)

    g_all, gates_all = hold(g_all, gates_all)
    g_far = swap_ctx(g_all[..., :late_cols])

    lines = fsdp // 4
    places = list(range(1, lines)) + [0]
    cut = lines // 2
    parts = [places[:cut], places[cut:]]
    m_all = m_all.reshape(fsdp // 2, 2, 2, rows_dev, width)
    gates_all = gates_all.reshape(fsdp // 2, 2, 2, 1, rows_dev)
    state = dict(kept=None, first=0, core=core[None].astype(jnp.int32))

    def order_of(steps):
        spots = [((place - p) % lines) * 2 + (side + d) % 2 for d, _, p in steps]
        far = [i for i, step in enumerate(steps) if step[1] == 1] or [0]
        return jnp.stack(
            [
                jnp.asarray(item, jnp.int32)
                for i, step in enumerate(steps)
                for item in (
                    spots[i],
                    (rank + step[1]) % 2,
                    step[1],
                    spots[min(far, key=lambda j, i=i: abs(j - i))],
                )
            ]
        )

    def call(steps, raw=False):
        keep_back, send_back, *kept = run_expert(
            state["core"],
            order_of(steps),
            state["first"],
            4 * lines,
            m_all,
            g_all,
            g_far,
            gates_all,
            expert_gate_up[0],
            expert_down[0],
            capacity,
            state["kept"],
        )
        state["kept"] = kept
        state["first"] += len(steps)
        return (keep_back, send_back) if raw else over_core(keep_back, send_back)

    def wait(first):
        state["core"], first = hold(state["core"], first)
        return first

    steps_far, steps_own = ([(d, d, p) for p in places] for d in (1, 0))
    steps_mixed = [[(1, 0, p) for p in part] + [(0, 1, p) for p in part] for part in parts]
    back = call(steps_far)
    far_one, far_two = wait([pick_sum(back, 0, lines, column) for column in range(2)])
    far_one, far_two = swap_ctx(far_one), swap_side(far_two)

    def mixed_sums(back, at=0):
        return [
            pick_sum(back, start, start + cut, column) for start in (at, at + cut) for column in range(2)
        ]

    def rounds(sums, part):
        side_one, side_two, ctx_one, ctx_two = sums
        span = slice(part * cut, (part + 1) * cut)
        return [
            swap_ctx(ctx_one),
            swap_side(side_two),
            swap_side(add_low(side_one, far_one[span])),
            swap_ctx(add_low(ctx_two, far_two[span])),
        ]

    keep, send = call(steps_mixed[0], raw=True)
    send, (far_one, far_two) = hold(send, (far_one, far_two))
    back = over_core(keep, send)
    back_own = call(steps_own)
    sums = wait(mixed_sums(back))
    back_own = [pick_sum(back_own, 0, lines, column) for column in range(2)]
    got = rounds(sums, 0)
    keep, send = call(steps_mixed[1], raw=True)
    send, got = hold(send, got)
    back = over_core(keep, send)
    entries = joined(parts[0], [item[:cut] for item in back_own], got)
    arrived = {p: line_shift(entries[p], lines - p) for p in parts[0]}
    gate_back, rows, grad_rows, hidden, grad_pair = state["kept"]
    hidden, sums = hold(hidden, mixed_sums(back))
    got = rounds(sums, 1)
    grad_gates = lax.all_to_all(
        gate_back.reshape(fsdp * 2, rows_dev), both, split_axis=0, concat_axis=0, tiled=True
    ).T
    def results(first, steps, hidden):
        return run_result(
            state["core"], order_of(steps), first, hidden, gates_all, expert_down[0], capacity
        )

    out_far = results(0, steps_far, hidden)
    out_rest = results(lines, steps_mixed[0] + steps_own + steps_mixed[1], hidden)
    got, out_far, out_rest, arrived, grad_gates = lax.optimization_barrier(
        (got, out_far, out_rest, arrived, grad_gates)
    )
    entries.update(joined(parts[1], [item[cut:] for item in back_own], got))
    out_far = over_core(*out_far)
    out_far = [pick_sum(out_far, 0, lines, column) for column in range(2)]
    out_rest, out_far = hold(out_rest, out_far)
    out_far = [swap_ctx(out_far[0]), swap_side(out_far[1])]
    out_rest = over_core(*out_rest)
    for p in parts[1][:-1]:
        arrived[p] = line_shift(entries[p], lines - p)
    grad_mid = line_total(entries[0], arrived)

    grad_wide = jnp.where(chosen, grad_gates, 0.0)
    grad_logits = (
        gates_wide * (grad_wide - jnp.sum(gates_wide * grad_wide, axis=1, keepdims=True))
    ).astype(low)
    grad_router = mul(low_mid, grad_logits, lhs_turned)
    grad_mid = grad_mid + mul(grad_logits, router_all, rhs_turned)
    grad_mixed_part, grad_moe_gain = rms_back(mixed, moe_all, grad_mid)
    grad_mixed = cotangent.astype(full) + grad_mixed_part

    low_mixed, (out_far, out_rest) = hold(grad_mixed.astype(low), (out_far, out_rest))
    grad_branch = sequence(low_mixed)
    out_sums = [
        jnp.concatenate([one, two])
        for one, two in zip(mixed_sums(out_rest), mixed_sums(out_rest, 2 * cut + lines))
    ]
    out_own = [pick_sum(out_rest, 2 * cut, 2 * cut + lines, column) for column in range(2)]
    (out_sums, out_own), grad_branch = hold((out_sums, out_own), grad_branch)
    side_one, side_two, ctx_one, ctx_two = out_sums
    grad_attended = mul(grad_branch, out_all, rhs_turned).astype(low)
    got = [swap_ctx(ctx_one), swap_side(side_two)]
    grad_gate_up = mul(rows, grad_pair, lhs_turned)[None]
    grad_attended, got, grad_gate_up = lax.optimization_barrier((grad_attended, got, grad_gate_up))
    got += [swap_side(add_low(side_one, out_far[0])), swap_ctx(add_low(ctx_two, out_far[1]))]
    grad_out_part = mul(attended, grad_branch, lhs_turned).astype(low)
    grad_q, grad_k, grad_v, gain_q_part, gain_k_part = attend_grad(
        projected, roped_q, roped_k, values_low, grad_attended, cosine, sine, gain_q, gain_k, kv_heads, group
    )
    grad_projected = jnp.concatenate([grad_q, grad_k, grad_v], axis=1)
    grad_down = mul(hidden, grad_rows, lhs_turned)[None]
    grad_projected, (got[3], grad_down) = hold(grad_projected, (got[3], grad_down))
    grad_qkv_part = mul(low_in, grad_projected, lhs_turned).astype(low)
    grad_normed_part = mul(grad_projected, qkv_all, rhs_turned)
    entries = joined(places, out_own, got)
    grad_normed_part, entries = hold(grad_normed_part, entries)
    arrived = {p: line_shift(entries[p], lines - p) for p in places[:-1]}
    output = (mixed + line_total(entries[0], arrived)).astype(low)
    grad_normed = of_block(grad_normed_part, rank) + swap_ctx(
        of_block(grad_normed_part, 1 - rank).astype(low)
    ).astype(full)
    grad_in_part, grad_attn_gain = rms_back(inputs, attn_all, grad_normed)
    grad_tokens = grad_mixed + grad_in_part

    out_mine = lax.psum_scatter(grad_out_part, "fsdp", scatter_dimension=0, tiled=True).astype(full)
    out_other = swap_ctx(out_mine.astype(low)).astype(full)
    grad_out = jnp.where(
        rank == 0,
        jnp.concatenate([out_mine, out_other], axis=0),
        jnp.concatenate([out_other, out_mine], axis=0),
    )
    qkv_mine = lax.psum_scatter(grad_qkv_part, "fsdp", scatter_dimension=0, tiled=True)
    grad_qkv = all_heads(rank_at, qkv_mine, swap_ctx(qkv_mine), head_dim, my_heads)
    early = sum_owned(jnp.concatenate([grad_router.T, grad_moe_gain[None]], axis=0), fsdp, spot)
    late = sum_all(
        jnp.concatenate(
            [
                grad_attn_gain.reshape(-1, head_dim),
                jnp.sum(gain_q_part, axis=0),
                jnp.sum(gain_k_part, axis=0),
            ],
            axis=0,
        ),
        fsdp,
    )
    gain_rows = width // head_dim
    return (
        output,
        grad_tokens,
        grad_qkv,
        grad_out,
        early[:experts_all].T,
        lax.dynamic_slice_in_dim(late[:gain_rows].reshape(-1), spot * shard, shard, 0),
        early[experts_all],
        late[gain_rows],
        late[gain_rows + 1],
        grad_gate_up,
        grad_down,
    )


gathered_bytes = 1 << 26


def choose_body(*args):
    tokens, gate_up = args[0], args[8]
    fsdp, ctx = lax.axis_size("fsdp"), lax.axis_size("ctx")
    fits = tokens.size * tokens.dtype.itemsize * fsdp * ctx <= gathered_bytes
    if fits and fsdp % 4 == 0 and ctx == 2 and fsdp >= 8 and fsdp & (fsdp - 1) == 0 and gate_up.shape[0] == 1:
        return body_gathered(*args)
    return body_routed(*args)


def solution(mesh):
    in_specs = (
        P(("fsdp", "ctx"), None),
        P("fsdp", None),
        P("fsdp", None),
        P("fsdp", None),
        P("fsdp"),
        P("fsdp"),
        P(),
        P(),
        P(("fsdp", "ctx"), None, None),
        P(("fsdp", "ctx"), None, None),
        P(("fsdp", "ctx"), None),
        P(("fsdp", "ctx"), None),
    )
    out_specs = (
        P(("fsdp", "ctx"), None),
        P(("fsdp", "ctx"), None),
        P("fsdp", None),
        P("fsdp", None),
        P("fsdp", None),
        P("fsdp"),
        P("fsdp"),
        P(),
        P(),
        P(("fsdp", "ctx"), None, None),
        P(("fsdp", "ctx"), None, None),
    )
    return jax.shard_map(choose_body, mesh=mesh, in_specs=in_specs, out_specs=out_specs, check_vma=False)
```

```python
import functools
import math

import jax
import jax.numpy as jnp
from jax import lax
from jax.experimental import pallas as pl
from jax.experimental.pallas import tpu as pltpu
from jax.sharding import PartitionSpec as P

eps_norm = 1e-06
theta_base = 1000000.0


def rms_scale(values, gain):
    return values * lax.rsqrt(jnp.mean(values * values, axis=-1, keepdims=True) + eps_norm) * gain


def rotate(values, cosine, sine):
    half_width = values.shape[-1] // 2
    turned = jnp.concatenate([-values[..., half_width:], values[..., :half_width]], axis=-1)
    return values * cosine + turned * sine


def angles(positions, width):
    freqs = theta_base ** (-(jnp.arange(width // 2, dtype=jnp.float32) * 2.0) / width)
    phase = positions.astype(jnp.float32)[:, None] * freqs[None, :]
    phase = jnp.concatenate([phase, phase], axis=-1)
    return (jnp.cos(phase)[:, None, :], jnp.sin(phase)[:, None, :])


def device_positions(block_rank, ctx_count, tok_rows):
    half_rows = tok_rows // 2
    within = jnp.arange(tok_rows, dtype=jnp.int32)
    span_id = jnp.where(within < half_rows, block_rank, 2 * ctx_count - 1 - block_rank)
    return span_id * half_rows + within % half_rows


def attend_head(query, keys_in, values_in, causal, scale_root):
    scores = (
        jnp.einsum("tgd,sd->gts", query, keys_in, preferred_element_type=jnp.float32) / scale_root
    )
    expo = jnp.where(causal[None], jnp.exp(scores), 0.0)
    totals = jnp.sum(expo, axis=-1, keepdims=True)
    probs = (expo / totals).astype(jnp.bfloat16)
    attended = jnp.einsum("gts,sd->tgd", probs, values_in, preferred_element_type=jnp.float32)
    return (attended, jnp.log(totals[..., 0]))


def attend_back(query, keys_in, values_in, causal, log_total, grad_attended, scale_root):
    scores = (
        jnp.einsum("tgd,sd->gts", query, keys_in, preferred_element_type=jnp.float32) / scale_root
    )
    probs = jnp.where(causal[None], jnp.exp(scores - log_total[..., None]), 0.0)
    low_probs = probs.astype(jnp.bfloat16)
    grad_values = jnp.einsum(
        "gts,tgd->sd", low_probs, grad_attended, preferred_element_type=jnp.float32
    )
    grad_probs = jnp.einsum(
        "tgd,sd->gts", grad_attended, values_in, preferred_element_type=jnp.float32
    )
    delta_rows = jnp.sum(grad_probs * probs, axis=-1, keepdims=True)
    grad_scores = (probs * (grad_probs - delta_rows)).astype(jnp.bfloat16)
    grad_query = (
        jnp.einsum("gts,sd->tgd", grad_scores, keys_in, preferred_element_type=jnp.float32)
        / scale_root
    )
    grad_keys = (
        jnp.einsum("gts,tgd->sd", grad_scores, query, preferred_element_type=jnp.float32)
        / scale_root
    )
    return (grad_query, grad_keys, grad_values)


def swiglu(paired):
    half_width = paired.shape[-1] // 2
    return jax.nn.silu(paired[..., :half_width]) * paired[..., half_width:]


def gating(selected):
    expo = jnp.exp(selected)
    return expo / jnp.sum(expo, axis=1, keepdims=True)


def body_routed(
    tokens,
    qkv_weight,
    out_weight,
    router_weight,
    attn_gain,
    moe_gain,
    query_gain,
    key_gain,
    expert_gate_up,
    expert_down,
    routes,
    cotangent,
):
    rows_dev, width = tokens.shape
    head_dim = query_gain.shape[0]
    top_k = routes.shape[1]
    ctx_count = lax.axis_size("ctx")
    ctx_rank = lax.axis_index("ctx")
    qkv_all, out_all, router_all, attn_all, moe_all = (
        lax.all_gather(qkv_weight, "fsdp", axis=0, tiled=True),
        lax.all_gather(out_weight, "fsdp", axis=0, tiled=True),
        lax.all_gather(router_weight, "fsdp", axis=0, tiled=True),
        lax.all_gather(attn_gain, "fsdp", axis=0, tiled=True),
        lax.all_gather(moe_gain, "fsdp", axis=0, tiled=True),
    )
    experts_all = router_all.shape[1]
    heads = out_all.shape[0] // head_dim
    kv_heads = (qkv_all.shape[1] // head_dim - heads) // 2
    group_size = heads // kv_heads
    capacity = 2 * rows_dev * top_k // experts_all
    width_q = heads * head_dim
    width_k = kv_heads * head_dim
    scale_root = math.sqrt(head_dim)
    inputs = tokens.astype(jnp.float32)
    normed_in = rms_scale(inputs, attn_all.astype(jnp.float32))
    low_in = normed_in.astype(jnp.bfloat16)
    projected = jnp.dot(low_in, qkv_all, preferred_element_type=jnp.float32)
    query_raw = projected[:, :width_q].reshape(rows_dev, heads, head_dim)
    key_raw = projected[:, width_q : width_q + width_k].reshape(rows_dev, kv_heads, head_dim)
    value_low = (
        projected[:, width_q + width_k :].astype(jnp.bfloat16).reshape(rows_dev, kv_heads, head_dim)
    )
    positions = device_positions(ctx_rank, ctx_count, rows_dev)
    cosine, sine = angles(positions, head_dim)
    query_gain_f = query_gain.astype(jnp.float32)
    key_gain_f = key_gain.astype(jnp.float32)

    def query_rope(values_in, gain):
        return rotate(rms_scale(values_in, gain), cosine, sine)

    query_low = query_rope(query_raw, query_gain_f).astype(jnp.bfloat16)
    key_low = query_rope(key_raw, key_gain_f).astype(jnp.bfloat16)
    keys_all, values_all = (
        lax.all_gather(key_low, "ctx", axis=0, tiled=True),
        lax.all_gather(value_low, "ctx", axis=0, tiled=True),
    )
    key_pos = jnp.concatenate(
        [device_positions(other, ctx_count, rows_dev) for other in range(ctx_count)]
    )
    causal = key_pos[None, :] <= positions[:, None]
    query_heads = query_low.reshape(rows_dev, kv_heads, group_size, head_dim).transpose(1, 0, 2, 3)
    key_heads = keys_all.transpose(1, 0, 2)
    value_heads = values_all.transpose(1, 0, 2)
    attended, log_total = lax.map(
        lambda member: attend_head(member[0], member[1], member[2], causal, scale_root),
        (query_heads, key_heads, value_heads),
    )
    attended_low = attended.transpose(1, 0, 2, 3).reshape(rows_dev, width_q).astype(jnp.bfloat16)
    mixed = inputs + jnp.dot(attended_low, out_all, preferred_element_type=jnp.float32)
    normed_mid = rms_scale(mixed, moe_all.astype(jnp.float32))
    low_mid = normed_mid.astype(jnp.bfloat16)
    logits = jnp.dot(low_mid, router_all, preferred_element_type=jnp.float32)
    selected = jnp.take_along_axis(logits, routes, axis=1)
    gates, gate_back = jax.vjp(gating, selected)
    flat_routes = routes.reshape(-1)
    expert_ids = jnp.arange(experts_all, dtype=jnp.int32)
    hit_table = (flat_routes[:, None] == expert_ids[None, :]).astype(jnp.int32)
    slot_index = jnp.sum(jnp.cumsum(hit_table, axis=0) * hit_table, axis=1) - 1
    target = flat_routes * capacity + slot_index
    pair_count = rows_dev * top_k
    source_pair = (
        jnp.full((experts_all * capacity,), pair_count, jnp.int32)
        .at[target]
        .set(jnp.arange(pair_count, dtype=jnp.int32))
    )
    padded = jnp.concatenate([low_mid, jnp.zeros((1, width), jnp.bfloat16)], axis=0)
    outgoing = padded[source_pair // top_k].reshape(experts_all, capacity, width)
    received = lax.all_to_all(outgoing, ("fsdp", "ctx"), split_axis=0, concat_axis=1, tiled=True)
    gate_and_up = jnp.einsum(
        "esd,edf->esf", received, expert_gate_up, preferred_element_type=jnp.float32
    )
    hidden_val, swiglu_back = jax.vjp(swiglu, gate_and_up)
    hidden_low = hidden_val.astype(jnp.bfloat16)
    result_low = jnp.einsum(
        "esf,efd->esd", hidden_low, expert_down, preferred_element_type=jnp.float32
    ).astype(jnp.bfloat16)
    returned = lax.all_to_all(
        result_low, ("fsdp", "ctx"), split_axis=1, concat_axis=0, tiled=True
    ).reshape(experts_all * capacity, width)
    picked = returned[target].reshape(rows_dev, top_k, width).astype(jnp.float32)
    output = (mixed + jnp.sum(gates[:, :, None] * picked, axis=1)).astype(jnp.bfloat16)
    qkv_back, out_back, router_back, attn_back_g, moe_back_g = (
        qkv_all,
        out_all,
        router_all,
        attn_all,
        moe_all,
    )
    grad_final = cotangent.astype(jnp.float32)
    grad_gates = jnp.sum(grad_final[:, None, :] * picked, axis=2)
    grad_result = (
        (gates[:, :, None] * grad_final[:, None, :]).astype(jnp.bfloat16).reshape(pair_count, width)
    )
    grad_padded = jnp.concatenate([grad_result, jnp.zeros((1, width), jnp.bfloat16)], axis=0)
    grad_outgoing = grad_padded[source_pair].reshape(experts_all, capacity, width)
    grad_received = lax.all_to_all(
        grad_outgoing, ("fsdp", "ctx"), split_axis=0, concat_axis=1, tiled=True
    )
    grad_down = jnp.einsum(
        "esf,esd->efd", hidden_low, grad_received, preferred_element_type=jnp.float32
    )
    grad_hidden = jnp.einsum(
        "esd,efd->esf", grad_received, expert_down, preferred_element_type=jnp.float32
    )
    grad_paired = swiglu_back(grad_hidden)[0].astype(jnp.bfloat16)
    grad_gate_up = jnp.einsum(
        "esd,esf->edf", received, grad_paired, preferred_element_type=jnp.float32
    )
    grad_rows = jnp.einsum(
        "esf,edf->esd", grad_paired, expert_gate_up, preferred_element_type=jnp.float32
    ).astype(jnp.bfloat16)
    grad_returned = lax.all_to_all(
        grad_rows, ("fsdp", "ctx"), split_axis=1, concat_axis=0, tiled=True
    ).reshape(experts_all * capacity, width)
    grad_mid = jnp.sum(
        grad_returned[target].reshape(rows_dev, top_k, width).astype(jnp.float32), axis=1
    )
    grad_selected = gate_back(grad_gates)[0]
    route_table = (routes[:, :, None] == expert_ids[None, None, :]).astype(jnp.float32)
    grad_logits = jnp.sum(route_table * grad_selected[:, :, None], axis=1).astype(jnp.bfloat16)
    grad_router = jnp.dot(low_mid.T, grad_logits, preferred_element_type=jnp.float32)
    grad_mid = grad_mid + jnp.dot(grad_logits, router_back.T, preferred_element_type=jnp.float32)
    unused_mid, mid_back = jax.vjp(rms_scale, mixed, moe_back_g.astype(jnp.float32))
    grad_mixed_part, grad_moe_gain = mid_back(grad_mid)
    grad_mixed = grad_final + grad_mixed_part
    grad_branch = grad_mixed.astype(jnp.bfloat16)
    grad_out = jnp.dot(attended_low.T, grad_branch, preferred_element_type=jnp.float32)
    grad_attended = jnp.dot(grad_branch, out_back.T, preferred_element_type=jnp.float32).astype(
        jnp.bfloat16
    )
    grad_heads = grad_attended.reshape(rows_dev, kv_heads, group_size, head_dim).transpose(
        1, 0, 2, 3
    )
    grad_query_h, grad_key_h, grad_value_h = lax.map(
        lambda member: attend_back(
            member[0], member[1], member[2], causal, member[3], member[4], scale_root
        ),
        (query_heads, key_heads, value_heads, log_total, grad_heads),
    )
    grad_keys, grad_values = (
        lax.psum_scatter(
            grad_key_h.transpose(1, 0, 2).astype(jnp.bfloat16),
            "ctx",
            scatter_dimension=0,
            tiled=True,
        ).astype(jnp.float32),
        lax.psum_scatter(
            grad_value_h.transpose(1, 0, 2).astype(jnp.bfloat16),
            "ctx",
            scatter_dimension=0,
            tiled=True,
        ).astype(jnp.float32),
    )
    grad_query_rot = (
        grad_query_h.transpose(1, 0, 2, 3).reshape(rows_dev, heads, head_dim).astype(jnp.bfloat16)
    )
    grad_query_rot = lax.optimization_barrier(grad_query_rot).astype(jnp.float32)
    grad_key_rot = lax.optimization_barrier(grad_keys.astype(jnp.bfloat16)).astype(jnp.float32)
    unused_query, query_back = jax.vjp(query_rope, query_raw, query_gain_f)
    grad_query_raw, grad_query_gain = query_back(grad_query_rot)
    unused_key, key_back = jax.vjp(query_rope, key_raw, key_gain_f)
    grad_key_raw, grad_key_gain = key_back(grad_key_rot)
    grad_projected = jnp.concatenate(
        [
            grad_query_raw.reshape(rows_dev, width_q).astype(jnp.bfloat16),
            grad_key_raw.reshape(rows_dev, width_k).astype(jnp.bfloat16),
            grad_values.reshape(rows_dev, width_k).astype(jnp.bfloat16),
        ],
        axis=1,
    )
    grad_qkv = jnp.dot(low_in.T, grad_projected, preferred_element_type=jnp.float32)
    grad_normed = jnp.dot(grad_projected, qkv_back.T, preferred_element_type=jnp.float32)
    unused_in, in_back = jax.vjp(rms_scale, inputs, attn_back_g.astype(jnp.float32))
    grad_in_part, grad_attn_gain = in_back(grad_normed)
    grad_tokens = grad_mixed + grad_in_part
    gradients = (grad_qkv, grad_out, grad_router, grad_attn_gain, grad_moe_gain)
    pieces = (
        lax.psum_scatter(gradients[0], "fsdp", scatter_dimension=0, tiled=True),
        lax.psum_scatter(gradients[1], "fsdp", scatter_dimension=0, tiled=True),
        lax.psum_scatter(gradients[2], "fsdp", scatter_dimension=0, tiled=True),
        lax.psum_scatter(gradients[3], "fsdp", scatter_dimension=0, tiled=True),
        lax.psum_scatter(gradients[4], "fsdp", scatter_dimension=0, tiled=True),
    )
    reduced = (
        lax.psum(pieces[0].astype(jnp.bfloat16), "ctx").astype(jnp.float32),
        lax.psum(pieces[1].astype(jnp.bfloat16), "ctx").astype(jnp.float32),
        lax.psum(pieces[2].astype(jnp.bfloat16), "ctx").astype(jnp.float32),
        lax.psum(pieces[3].astype(jnp.bfloat16), "ctx").astype(jnp.float32),
        lax.psum(pieces[4].astype(jnp.bfloat16), "ctx").astype(jnp.float32),
    )
    gain_sums = lax.psum((grad_query_gain, grad_key_gain), ("fsdp", "ctx"))
    return (
        output,
        grad_tokens,
        reduced[0],
        reduced[1],
        reduced[2],
        reduced[3],
        reduced[4],
        gain_sums[0],
        gain_sums[1],
        grad_gate_up,
        grad_down,
    )


low = jnp.bfloat16
full = jnp.float32
plain = (((1,), (0,)), ((), ()))
rhs_turned = (((1,), (1,)), ((), ()))
lhs_turned = (((0,), (0,)), ((), ()))
vmem_bytes = 58 << 20


def mul(left, right, dims=plain):
    return lax.dot_general(left, right, dims, preferred_element_type=full)


def core_pairs(fsdp):
    return [(i, i ^ 1) for i in range(fsdp)]


def side_pairs(fsdp):
    return [(i, i ^ 2) for i in range(fsdp)]


def swap_core(values):
    return lax.ppermute(values, "fsdp", core_pairs(lax.axis_size("fsdp")))


def swap_side(values):
    return lax.ppermute(values, "fsdp", side_pairs(lax.axis_size("fsdp")))


def swap_ctx(values):
    return lax.ppermute(values, "ctx", [(0, 1), (1, 0)])


def add_low(one, two):
    return (one.astype(full) + two.astype(full)).astype(low)


def hold(values, first):
    return lax.optimization_barrier((values, first))


def take(values, index):
    return lax.dynamic_index_in_dim(values, index, 0, keepdims=False)


def line_shift(values, step):
    fsdp = lax.axis_size("fsdp")
    return lax.ppermute(values, "fsdp", [(i, (i + 4 * step) % fsdp) for i in range(fsdp)])


def line_total(own, arrived):
    total = own.astype(full)
    for item in arrived.values():
        total = total + item.astype(full)
    return total


def line_halving(entries, place):
    fsdp = lax.axis_size("fsdp")
    even = place % 2 == 0
    one, two = jnp.where(even, entries[3], entries[1]), jnp.where(even, entries[1], entries[3])
    one, two = (lax.ppermute(item, "fsdp", [(i, i ^ 4) for i in range(fsdp)]) for item in (one, two))
    far = lax.ppermute(add_low(entries[2], two), "fsdp", [(i, i ^ 8) for i in range(fsdp)])
    return entries[0].astype(full) + one.astype(full) + far.astype(full)


def joined(places, own, got):
    from_ctx, from_side, one_side, two_ctx = got
    entries = {}
    for at, p in enumerate(places):
        one = add_low(add_low(own[0][at], from_ctx[at]), one_side[at])
        two = add_low(add_low(own[1][at], from_side[at]), two_ctx[at])
        entries[p] = jnp.concatenate([one, two], axis=-1)
    return entries


def over_core(keep, send):
    return keep, swap_core(send)


def pick_sum(parts, start, stop, column):
    keep, other = parts
    half = keep.shape[-1] // 2
    cut = (slice(start, stop), slice(None), slice(column * half, (column + 1) * half))
    return add_low(keep[cut], other[cut])


def sum_all(values, fsdp):
    values = values + lax.ppermute(values, "fsdp", core_pairs(fsdp))
    values = values + swap_ctx(values)
    step = 2
    while step < fsdp:
        values = values + lax.ppermute(values, "fsdp", [(i, i ^ step) for i in range(fsdp)])
        step *= 2
    return values


def sum_owned(values, fsdp, spot):
    items, shard = values.shape[0], values.shape[1] // fsdp
    values = values.reshape(items, fsdp, shard).swapaxes(0, 1)
    step = fsdp // 2
    while step:
        bit = (spot // step) % 2
        values = values.reshape(2, step, items, shard)
        other = lax.ppermute(take(values, 1 - bit), "fsdp", [(i, i ^ step) for i in range(fsdp)])
        values = take(values, bit) + other
        step //= 2
    values = values[0]
    return values + swap_ctx(values)


def turn(values):
    return pltpu.roll(values, values.shape[-1] // 2, 1)


def norm_rope(raw, gain, cosine, sine):
    scale = lax.rsqrt(jnp.mean(raw * raw, axis=-1, keepdims=True) + eps_norm)
    scaled = raw * scale * gain
    return scaled * cosine + turn(scaled) * sine


def norm_rope_back(raw, gain, cosine, sine, grad):
    scale = lax.rsqrt(jnp.mean(raw * raw, axis=-1, keepdims=True) + eps_norm)
    unit = raw * scale
    grad_scaled = grad * cosine - turn(grad) * sine
    grad_gain = jnp.sum(grad_scaled * unit, axis=0, keepdims=True)
    grad_unit = grad_scaled * gain
    grad_raw = scale * (grad_unit - unit * jnp.mean(grad_unit * unit, axis=-1, keepdims=True))
    return grad_raw, grad_gain


def tiles_of(rows):
    step = rows // 2
    return [(start, start + step) for start in range(0, rows, step)]


def allowed(start, stop):
    shape = (stop - start, stop)
    return lax.broadcasted_iota(jnp.int32, shape, 1) <= (
        lax.broadcasted_iota(jnp.int32, shape, 0) + start
    )


def attend_kernel(q_ref, k_ref, v_ref, cos_ref, sin_ref, qg_ref, kg_ref, o_ref, qr_ref, kr_ref, vl_ref):
    head_dim = k_ref.shape[1]
    rows = k_ref.shape[0]
    cosine, sine = cos_ref[...], sin_ref[...]
    keys = norm_rope(k_ref[...], kg_ref[...], cosine, sine).astype(low)
    values = v_ref[...].astype(low)
    kr_ref[...] = keys
    vl_ref[...] = values
    for head in range(q_ref.shape[1] // head_dim):
        cols = slice(head * head_dim, (head + 1) * head_dim)
        query = norm_rope(q_ref[:, cols], qg_ref[...], cosine, sine).astype(low)
        qr_ref[:, cols] = query
        for start, stop in tiles_of(rows):
            scores = mul(query[start:stop], keys[:stop], rhs_turned) * (1.0 / math.sqrt(head_dim))
            expo = jnp.where(allowed(start, stop), jnp.exp(scores), 0.0)
            probs = (expo / jnp.sum(expo, axis=-1, keepdims=True)).astype(low)
            o_ref[start:stop, cols] = mul(probs, values[:stop]).astype(low)


def attend_grad_kernel(
    q_ref, k_ref, qr_ref, kr_ref, vl_ref, go_ref, cos_ref, sin_ref, qg_ref, kg_ref,
    dq_ref, dk_ref, dv_ref, dqg_ref, dkg_ref, dk_sum, dv_sum, dq_sum,
):
    head_dim = k_ref.shape[1]
    rows = k_ref.shape[0]
    root = 1.0 / math.sqrt(head_dim)
    cosine, sine = cos_ref[...], sin_ref[...]
    keys, values = kr_ref[...], vl_ref[...]
    gain_sum = jnp.zeros((1, head_dim), full)
    dk_sum[...] = jnp.zeros_like(dk_sum)
    dv_sum[...] = jnp.zeros_like(dv_sum)
    for head in range(q_ref.shape[1] // head_dim):
        cols = slice(head * head_dim, (head + 1) * head_dim)
        for start, stop in tiles_of(rows):
            query = qr_ref[start:stop, cols]
            grad = go_ref[start:stop, cols]
            scores = mul(query, keys[:stop], rhs_turned) * root
            expo = jnp.where(allowed(start, stop), jnp.exp(scores), 0.0)
            probs = expo / jnp.sum(expo, axis=-1, keepdims=True)
            grad_probs = mul(grad, values[:stop], rhs_turned)
            delta = jnp.sum(grad_probs * probs, axis=-1, keepdims=True)
            grad_scores = (probs * (grad_probs - delta)).astype(low)
            dv_sum[:stop] += mul(probs.astype(low), grad, lhs_turned)
            dk_sum[:stop] += mul(grad_scores, query, lhs_turned)
            dq_sum[start:stop] = mul(grad_scores, keys[:stop])
        grad_query = (dq_sum[...] * root).astype(low).astype(full)
        grad_raw, grad_gain = norm_rope_back(q_ref[:, cols], qg_ref[...], cosine, sine, grad_query)
        dq_ref[:, cols] = grad_raw.astype(low)
        gain_sum = gain_sum + grad_gain
    dqg_ref[0] = gain_sum
    grad_key = (dk_sum[...] * root).astype(low).astype(full)
    grad_raw, grad_gain = norm_rope_back(k_ref[...], kg_ref[...], cosine, sine, grad_key)
    dk_ref[...] = grad_raw.astype(low)
    dkg_ref[0] = grad_gain
    dv_ref[...] = dv_sum[...].astype(low)


def attention_specs(rows, head_dim, kv_heads, group):
    wide, narrow = group * head_dim, head_dim
    heads_end = kv_heads * group
    return dict(
        q=pl.BlockSpec((rows, wide), lambda i: (0, i)),
        k=pl.BlockSpec((rows, narrow), lambda i: (0, heads_end + i)),
        v=pl.BlockSpec((rows, narrow), lambda i: (0, heads_end + kv_heads + i)),
        own=pl.BlockSpec((rows, narrow), lambda i: (0, i)),
        table=pl.BlockSpec((rows, head_dim), lambda i: (0, 0)),
        gain=pl.BlockSpec((1, head_dim), lambda i: (0, 0)),
        gain_out=pl.BlockSpec((1, 1, head_dim), lambda i: (i, 0, 0)),
    )


def attend(projected, cosine, sine, query_gain, key_gain, kv_heads, group):
    rows, head_dim = cosine.shape
    s = attention_specs(rows, head_dim, kv_heads, group)
    shape = jax.ShapeDtypeStruct
    work = rows * rows * head_dim * kv_heads * group
    return pl.pallas_call(
        attend_kernel,
        grid=(kv_heads,),
        in_specs=[s["q"], s["k"], s["v"], s["table"], s["table"], s["gain"], s["gain"]],
        out_specs=[s["q"], s["q"], s["own"], s["own"]],
        out_shape=[
            shape((rows, kv_heads * group * head_dim), low),
            shape((rows, kv_heads * group * head_dim), low),
            shape((rows, kv_heads * head_dim), low),
            shape((rows, kv_heads * head_dim), low),
        ],
        compiler_params=pltpu.CompilerParams(vmem_limit_bytes=48 << 20),
        cost_estimate=pl.CostEstimate(
            flops=4 * work, bytes_accessed=projected.size * 6, transcendentals=work // head_dim
        ),
        name="attend",
    )(projected, projected, projected, cosine, sine, query_gain, key_gain)


def attend_grad(projected, roped_q, roped_k, values_low, grad, cosine, sine, query_gain, key_gain, kv_heads, group):
    rows, head_dim = cosine.shape
    s = attention_specs(rows, head_dim, kv_heads, group)
    shape = jax.ShapeDtypeStruct
    work = rows * rows * head_dim * kv_heads * group
    return pl.pallas_call(
        attend_grad_kernel,
        grid=(kv_heads,),
        in_specs=[
            s["q"], s["k"], s["q"], s["own"], s["own"], s["q"],
            s["table"], s["table"], s["gain"], s["gain"],
        ],
        out_specs=[s["q"], s["own"], s["own"], s["gain_out"], s["gain_out"]],
        out_shape=[
            shape((rows, kv_heads * group * head_dim), low),
            shape((rows, kv_heads * head_dim), low),
            shape((rows, kv_heads * head_dim), low),
            shape((kv_heads, 1, head_dim), full),
            shape((kv_heads, 1, head_dim), full),
        ],
        scratch_shapes=[pltpu.VMEM((rows, head_dim), full)] * 3,
        compiler_params=pltpu.CompilerParams(vmem_limit_bytes=48 << 20),
        cost_estimate=pl.CostEstimate(
            flops=10 * work, bytes_accessed=projected.size * 10, transcendentals=work // head_dim
        ),
        name="attend_grad",
    )(projected, projected, roped_q, roped_k, values_low, grad, cosine, sine, query_gain, key_gain)


def placed(gate, slots):
    block = gate.shape[1]
    shape = (block, block)
    earlier = (
        lax.broadcasted_iota(jnp.int32, shape, 0) < lax.broadcasted_iota(jnp.int32, shape, 1)
    ).astype(low)
    hit = jnp.where(gate >= 0.0, 1.0, 0.0)
    count = mul(jnp.broadcast_to(hit, (8, block)).astype(low), earlier)[:1].astype(jnp.int32)
    place = (lax.broadcasted_iota(jnp.int32, (slots, block), 0) == count) & (hit > 0.5)
    weight = jnp.sum(jnp.where(place, gate, 0.0), axis=1, keepdims=True)
    return place, place.astype(full).astype(low), weight


def expert_kernel(core_ref, order, m_ref, g_ref, far_ref, w_ref, gu_ref, dn_ref, *refs):
    keep_back, send_back, gate_back, rows_ref, dy_ref, z_ref, pair_ref = refs[-7:]
    core = core_ref[0]
    far = order[4 * pl.program_id(0) + 2] == 1
    width = m_ref.shape[4]
    hidden = dn_ref.shape[0]
    slots = z_ref.shape[0] // 2
    places, picks, weights, rows, grads = [], [], [], [], []
    for part in range(2):
        at = lax.rem(core + part, 2)
        place, pick, weight = placed(w_ref[0, at, 0], slots)
        places.append(place)
        picks.append(pick)
        weights.append(weight)
        rows.append(mul(pick, m_ref[0, at, 0]).astype(low))
        near_rows = g_ref[0, at, :, :width]
        far_rows = jnp.concatenate([far_ref[0, at], g_ref[0, at, :, width:]], axis=1)
        grads.append(mul(pick, jnp.where(far, far_rows, near_rows)).astype(low))
    row, grad, weight = (jnp.concatenate(items, axis=0) for items in (rows, grads, weights))
    rows_ref[...] = row
    paired = mul(row, gu_ref[...])
    gate_in, up = paired[:, :hidden], paired[:, hidden:]
    sig = jax.nn.sigmoid(gate_in)
    act = gate_in * sig
    z = (act * up).astype(low)
    z_ref[...] = z
    dy_ref[...] = (weight * grad.astype(full)).astype(low)
    unweighted = mul(grad, dn_ref[...], rhs_turned)
    grad_gate = jnp.sum(unweighted * z.astype(full), axis=1, keepdims=True)
    dz = weight * unweighted
    grad_in = dz * up * (sig * (1.0 + gate_in * (1.0 - sig)))
    pair = jnp.concatenate([grad_in, dz * act], axis=1).astype(low)
    pair_ref[...] = pair
    back = mul(pair, gu_ref[...], rhs_turned).astype(low)
    for part, out in enumerate((keep_back, send_back)):
        mine = slice(part * slots, (part + 1) * slots)
        out[0] = mul(picks[part], back[mine], lhs_turned).astype(low)
        gate_back[0, lax.rem(core + part, 2), 0] = jnp.sum(
            jnp.where(places[part], grad_gate[mine], 0.0), axis=0, keepdims=True
        )


def run_expert(core, order, first, total_steps, m_all, g_all, g_far, gates_all, gate_up, down, slots, kept):
    places, _, _, block, width = m_all.shape
    paired = gate_up.shape[1]
    steps = order.shape[0] // 4
    part_rows = steps * 2 * slots
    hidden = paired // 2
    shape = jax.ShapeDtypeStruct

    def gates_at(i, core, order):
        return (order[4 * i], 0, order[4 * i + 1], 0, 0)

    def token_at(i, core, order):
        return (order[4 * i], 0, order[4 * i + 2], 0, 0)

    def near_at(i, core, order):
        return (order[4 * i], 0, 0, 0)

    def far_at(i, core, order):
        return (order[4 * i + 3], 0, 0, 0)

    def fixed(i, core, order):
        return (0, 0)

    def flat(i, core, order):
        return (first + i, 0)

    def stacked(i, core, order):
        return (i, 0, 0)

    small = pl.BlockSpec((1, 2, 1, 1, block), gates_at)
    one_block = pl.BlockSpec((1, block, width), stacked)
    widths = (width, width, hidden, paired)
    grid_spec = pltpu.PrefetchScalarGridSpec(
        num_scalar_prefetch=2,
        grid=(steps,),
        in_specs=[
            pl.BlockSpec((1, 2, 1, block, width), token_at),
            pl.BlockSpec((1, 2, block, g_all.shape[3]), near_at),
            pl.BlockSpec((1, 2, block, g_far.shape[3]), far_at),
            small,
            pl.BlockSpec(gate_up.shape, fixed, pipeline_mode=pl.Buffered(1)),
            pl.BlockSpec(down.shape, fixed, pipeline_mode=pl.Buffered(1)),
        ]
        + [pl.BlockSpec(memory_space=pl.ANY)] * (0 if kept is None else 5),
        out_specs=[one_block] * 2 + [small] + [pl.BlockSpec((2 * slots, n), flat) for n in widths],
    )
    return pl.pallas_call(
        expert_kernel,
        grid_spec=grid_spec,
        out_shape=[shape((steps, block, width), low)] * 2
        + [shape((places, 2, 2, 1, block), full)]
        + [shape((total_steps * 2 * slots, n), low) for n in widths],
        input_output_aliases={} if kept is None else {8 + i: 2 + i for i in range(5)},
        compiler_params=pltpu.CompilerParams(vmem_limit_bytes=vmem_bytes),
        cost_estimate=pl.CostEstimate(
            flops=part_rows * width * (4 * paired + 2 * hidden + 6 * block),
            bytes_accessed=steps * block * width * 12 + part_rows * (width * 4 + paired * 3),
            transcendentals=part_rows * hidden,
        ),
        name="experts",
    )(core, order, m_all, g_all, g_far, gates_all, gate_up, down, *(() if kept is None else kept))


def result_kernel(core_ref, order, z_ref, w_ref, dn_ref, keep_out, send_out):
    core = core_ref[0]
    slots = z_ref.shape[0] // 2
    y = mul(z_ref[...], dn_ref[...]).astype(low).astype(full)
    for part, out in enumerate((keep_out, send_out)):
        _, pick, weight = placed(w_ref[0, lax.rem(core + part, 2), 0], slots)
        scaled = (weight * y[part * slots : (part + 1) * slots]).astype(low)
        out[0] = mul(pick, scaled, lhs_turned).astype(low)


def run_result(core, order, first, hidden, gates_all, down, slots):
    block, width, inner = gates_all.shape[4], down.shape[1], down.shape[0]
    steps = order.shape[0] // 4
    one_block = pl.BlockSpec((1, block, width), lambda i, core, order: (i, 0, 0))
    return pl.pallas_call(
        result_kernel,
        grid_spec=pltpu.PrefetchScalarGridSpec(
            num_scalar_prefetch=2,
            grid=(steps,),
            in_specs=[
                pl.BlockSpec((2 * slots, inner), lambda i, core, order: (first + i, 0)),
                pl.BlockSpec(
                    (1, 2, 1, 1, block), lambda i, core, order: (order[4 * i], 0, order[4 * i + 1], 0, 0)
                ),
                pl.BlockSpec(down.shape, lambda i, core, order: (0, 0), pipeline_mode=pl.Buffered(1)),
            ],
            out_specs=[one_block] * 2,
        ),
        out_shape=[jax.ShapeDtypeStruct((steps, block, width), low)] * 2,
        compiler_params=pltpu.CompilerParams(vmem_limit_bytes=vmem_bytes),
        cost_estimate=pl.CostEstimate(
            flops=steps * 2 * slots * width * (2 * inner + 2 * block),
            bytes_accessed=steps * (4 * block * width + 4 * slots * inner) + 2 * inner * width,
            transcendentals=0,
        ),
        name="results",
    )(core, order, hidden, gates_all, down)


def own_heads_kernel(rank, qkv_ref, out_ref, o_ref, *, head_dim, heads):
    first = rank[0] == 0
    for head in range(heads):
        pair = [qkv_ref[:, (2 * head + i) * head_dim : (2 * head + i + 1) * head_dim] for i in range(2)]
        o_ref[:, head * head_dim : (head + 1) * head_dim] = jnp.where(first, pair[0], pair[1])
    kv = qkv_ref.shape[1] - 2 * heads * head_dim
    o_ref[:, heads * head_dim : heads * head_dim + kv] = qkv_ref[:, 2 * heads * head_dim :]
    o_ref[:, heads * head_dim + kv :] = jnp.where(first, out_ref[:head_dim], out_ref[head_dim:])


def own_heads(rank, qkv_weight, out_weight, head_dim, heads):
    kv = qkv_weight.shape[1] - 2 * heads * head_dim
    return pl.pallas_call(
        functools.partial(own_heads_kernel, head_dim=head_dim, heads=heads),
        grid_spec=pltpu.PrefetchScalarGridSpec(
            num_scalar_prefetch=1,
            grid=(1,),
            in_specs=[
                pl.BlockSpec(qkv_weight.shape, lambda i, rank: (0, 0)),
                pl.BlockSpec(out_weight.shape, lambda i, rank: (0, 0)),
            ],
            out_specs=pl.BlockSpec(
                (qkv_weight.shape[0], heads * head_dim + kv + out_weight.shape[1]), lambda i, rank: (0, 0)
            ),
        ),
        out_shape=jax.ShapeDtypeStruct(
            (qkv_weight.shape[0], heads * head_dim + kv + out_weight.shape[1]), qkv_weight.dtype
        ),
        name="own_heads",
    )(rank, qkv_weight, out_weight)


def all_heads_kernel(rank, mine_ref, other_ref, o_ref, *, head_dim, heads):
    first = rank[0] == 0
    for head in range(heads):
        cols = slice(head * head_dim, (head + 1) * head_dim)
        mine, other = mine_ref[:, cols].astype(full), other_ref[:, cols].astype(full)
        o_ref[:, 2 * head * head_dim : (2 * head + 1) * head_dim] = jnp.where(first, mine, other)
        o_ref[:, (2 * head + 1) * head_dim : (2 * head + 2) * head_dim] = jnp.where(first, other, mine)
    o_ref[:, 2 * heads * head_dim :] = mine_ref[:, heads * head_dim :].astype(full) + other_ref[
        :, heads * head_dim :
    ].astype(full)


def all_heads(rank, mine, other, head_dim, heads):
    rows, width = mine.shape
    return pl.pallas_call(
        functools.partial(all_heads_kernel, head_dim=head_dim, heads=heads),
        grid_spec=pltpu.PrefetchScalarGridSpec(
            num_scalar_prefetch=1,
            grid=(1,),
            in_specs=[pl.BlockSpec((rows, width), lambda i, rank: (0, 0))] * 2,
            out_specs=pl.BlockSpec((rows, width + heads * head_dim), lambda i, rank: (0, 0)),
        ),
        out_shape=jax.ShapeDtypeStruct((rows, width + heads * head_dim), full),
        name="all_heads",
    )(rank, mine, other)


def rms_back(values, gain, grad):
    scale = lax.rsqrt(jnp.mean(values * values, axis=-1, keepdims=True) + eps_norm)
    unit = values * scale
    grad_gain = jnp.sum(grad * unit, axis=0)
    grad_unit = grad * gain
    back = scale * (grad_unit - unit * jnp.mean(grad_unit * unit, axis=-1, keepdims=True))
    return back, grad_gain


def in_order(first, second):
    half = first.shape[0] // 2
    return jnp.concatenate([first[:half], second, first[half:]], axis=0)


def of_block(values, rank):
    quarter = values.shape[0] // 4
    outer = jnp.concatenate([values[:quarter], values[3 * quarter :]], axis=0)
    return jnp.where(rank == 0, outer, values[quarter : 3 * quarter])


def body_gathered(
    tokens, qkv_weight, out_weight, router_weight, attn_gain, moe_gain, query_gain, key_gain,
    expert_gate_up, expert_down, routes, cotangent,
):
    rows_dev, width = tokens.shape
    head_dim = query_gain.shape[0]
    top_k = routes.shape[1]
    fsdp = lax.axis_size("fsdp")
    spot = lax.axis_index("fsdp")
    rank = lax.axis_index("ctx")
    place, side, core = spot // 4, (spot // 2) % 2, spot % 2
    shard = qkv_weight.shape[0]
    heads = out_weight.shape[0] * fsdp // head_dim
    kv_heads = (qkv_weight.shape[1] // head_dim - heads) // 2
    group = heads // kv_heads // 2
    my_heads = heads // 2
    width_q, width_k = my_heads * head_dim, kv_heads * head_dim
    experts_all = router_weight.shape[1]
    capacity = 2 * rows_dev * top_k // experts_all
    both = ("fsdp", "ctx")

    def sequence(values):
        other = swap_ctx(values)
        first = jnp.where(rank == 0, values, other)
        second = jnp.where(rank == 0, other, values)
        return in_order(first, second)

    rank_at = rank[None].astype(jnp.int32)
    weights_local = own_heads(rank_at, qkv_weight, out_weight, head_dim, my_heads)
    small_local = jnp.concatenate([router_weight, attn_gain[:, None], moe_gain[:, None]], axis=1)
    small_all = lax.all_gather(small_local, "fsdp", axis=0, tiled=True)
    weights_all = lax.all_gather(weights_local, "fsdp", axis=0, tiled=True)
    qkv_all = weights_all[:, : width_q + 2 * width_k]
    out_all = weights_all[:, width_q + 2 * width_k :]
    router_all = small_all[:, :experts_all]
    attn_all = small_all[:, experts_all].astype(full)
    moe_all = small_all[:, experts_all + 1].astype(full)
    late_cols = width * 7 // 16
    g_all = lax.all_gather(
        jnp.concatenate([cotangent, swap_ctx(cotangent[:, late_cols:])], axis=1), "fsdp", axis=0, tiled=True
    ).reshape(fsdp // 2, 2, rows_dev, 2 * width - late_cols)

    sequence_in = sequence(tokens).astype(full)
    low_in = rms_scale(sequence_in, attn_all).astype(low)
    projected = mul(low_in, qkv_all)
    cosine, sine = (t[:, 0] for t in angles(jnp.arange(2 * rows_dev, dtype=jnp.int32), head_dim))
    sine = jnp.concatenate([-sine[:, : head_dim // 2], sine[:, head_dim // 2 :]], axis=1)
    gain_q, gain_k = query_gain.astype(full)[None], key_gain.astype(full)[None]
    attended, roped_q, roped_k, values_low = attend(
        projected, cosine, sine, gain_q, gain_k, kv_heads, group
    )
    branch = mul(attended, out_all)
    inputs = tokens.astype(full)
    mixed = (
        inputs
        + of_block(branch, rank)
        + swap_ctx(of_block(branch, 1 - rank).astype(low)).astype(full)
    )
    low_mid = rms_scale(mixed, moe_all).astype(low)
    m_all = lax.all_gather(jnp.concatenate([low_mid, swap_ctx(low_mid)]), "fsdp", axis=0, tiled=True)

    logits = mul(low_mid, router_all)
    named = routes[:, :, None] == jnp.arange(experts_all, dtype=jnp.int32)[None, None, :]
    selected = jnp.sum(jnp.where(named, logits[:, None, :], 0.0), axis=2)
    gates = gating(selected)
    chosen = jnp.any(named, axis=1)
    gates_wide = jnp.sum(jnp.where(named, gates[:, :, None], 0.0), axis=1)
    gates_sent = jnp.where(chosen, gates_wide, -1.0).T
    gates_all = lax.all_to_all(gates_sent, both, split_axis=0, concat_axis=0, tiled=True)

    g_all, gates_all = hold(g_all, gates_all)
    g_far = swap_ctx(g_all[..., :late_cols])

    lines = fsdp // 4
    places = list(range(1, lines)) + [0]
    cut = lines // 2
    parts = [places[:cut], places[cut:]]
    m_all = m_all.reshape(fsdp // 2, 2, 2, rows_dev, width)
    gates_all = gates_all.reshape(fsdp // 2, 2, 2, 1, rows_dev)
    state = dict(kept=None, first=0, core=core[None].astype(jnp.int32))

    def order_of(steps):
        spots = [((place - p) % lines) * 2 + (side + d) % 2 for d, _, p in steps]
        far = [i for i, step in enumerate(steps) if step[1] == 1] or [0]
        return jnp.stack(
            [
                jnp.asarray(item, jnp.int32)
                for i, step in enumerate(steps)
                for item in (
                    spots[i],
                    (rank + step[1]) % 2,
                    step[1],
                    spots[min(far, key=lambda j, i=i: abs(j - i))],
                )
            ]
        )

    def call(steps, raw=False):
        keep_back, send_back, *kept = run_expert(
            state["core"],
            order_of(steps),
            state["first"],
            4 * lines,
            m_all,
            g_all,
            g_far,
            gates_all,
            expert_gate_up[0],
            expert_down[0],
            capacity,
            state["kept"],
        )
        state["kept"] = kept
        state["first"] += len(steps)
        return (keep_back, send_back) if raw else over_core(keep_back, send_back)

    def wait(first):
        state["core"], first = hold(state["core"], first)
        return first

    steps_far, steps_own = ([(d, d, p) for p in places] for d in (1, 0))
    steps_mixed = [[(1, 0, p) for p in part] + [(0, 1, p) for p in part] for part in parts]
    back = call(steps_far)
    far_one, far_two = wait([pick_sum(back, 0, lines, column) for column in range(2)])
    far_one, far_two = swap_ctx(far_one), swap_side(far_two)

    def mixed_sums(back, at=0):
        return [
            pick_sum(back, start, start + cut, column) for start in (at, at + cut) for column in range(2)
        ]

    def rounds(sums, part):
        side_one, side_two, ctx_one, ctx_two = sums
        span = slice(part * cut, (part + 1) * cut)
        return [
            swap_ctx(ctx_one),
            swap_side(side_two),
            swap_side(add_low(side_one, far_one[span])),
            swap_ctx(add_low(ctx_two, far_two[span])),
        ]

    keep, send = call(steps_mixed[0], raw=True)
    send, (far_one, far_two) = hold(send, (far_one, far_two))
    back = over_core(keep, send)
    back_own = call(steps_own)
    sums = wait(mixed_sums(back))
    back_own = [pick_sum(back_own, 0, lines, column) for column in range(2)]
    got = rounds(sums, 0)
    keep, send = call(steps_mixed[1], raw=True)
    send, got = hold(send, got)
    back = over_core(keep, send)
    entries = joined(parts[0], [item[:cut] for item in back_own], got)
    arrived = {p: line_shift(entries[p], lines - p) for p in parts[0]}
    gate_back, rows, grad_rows, hidden, grad_pair = state["kept"]
    hidden, sums = hold(hidden, mixed_sums(back))
    got = rounds(sums, 1)
    grad_gates = lax.all_to_all(
        gate_back.reshape(fsdp * 2, rows_dev), both, split_axis=0, concat_axis=0, tiled=True
    ).T
    def results(first, steps, hidden):
        return run_result(
            state["core"], order_of(steps), first, hidden, gates_all, expert_down[0], capacity
        )

    out_far = results(0, steps_far, hidden)
    out_rest = results(lines, steps_mixed[0] + steps_own + steps_mixed[1], hidden)
    got, out_far, out_rest, arrived, grad_gates = lax.optimization_barrier(
        (got, out_far, out_rest, arrived, grad_gates)
    )
    entries.update(joined(parts[1], [item[cut:] for item in back_own], got))
    out_far = over_core(*out_far)
    out_far = [pick_sum(out_far, 0, lines, 0), swap_side(pick_sum(out_far, 0, lines, 1))]
    out_rest = over_core(*out_rest)
    for p in parts[1][:-1]:
        arrived[p] = line_shift(entries[p], lines - p)
    grad_mid = line_total(entries[0], arrived)

    grad_wide = jnp.where(chosen, grad_gates, 0.0)
    grad_logits = (
        gates_wide * (grad_wide - jnp.sum(gates_wide * grad_wide, axis=1, keepdims=True))
    ).astype(low)
    grad_router = mul(low_mid, grad_logits, lhs_turned)
    grad_mid = grad_mid + mul(grad_logits, router_all, rhs_turned)
    grad_mixed_part, grad_moe_gain = rms_back(mixed, moe_all, grad_mid)
    grad_mixed = cotangent.astype(full) + grad_mixed_part

    low_mixed, (out_far[0], out_rest) = hold(grad_mixed.astype(low), (out_far[0], out_rest))
    grad_branch = sequence(low_mixed)
    out_sums = [
        jnp.concatenate([one, two])
        for one, two in zip(mixed_sums(out_rest), mixed_sums(out_rest, 2 * cut + lines))
    ]
    out_own = [pick_sum(out_rest, 2 * cut, 2 * cut + lines, column) for column in range(2)]
    (out_far[0], out_sums, out_own), grad_branch = hold((out_far[0], out_sums, out_own), grad_branch)
    side_one, side_two, ctx_one, ctx_two = out_sums
    out_far[0] = swap_ctx(out_far[0])
    grad_attended = mul(grad_branch, out_all, rhs_turned).astype(low)
    grad_attended, out_far = hold(grad_attended, out_far)
    got = [
        swap_ctx(ctx_one),
        swap_side(side_two),
        swap_side(add_low(side_one, out_far[0])),
        swap_ctx(add_low(ctx_two, out_far[1])),
    ]
    grad_out_part = mul(attended, grad_branch, lhs_turned).astype(low)
    grad_q, grad_k, grad_v, gain_q_part, gain_k_part = attend_grad(
        projected, roped_q, roped_k, values_low, grad_attended, cosine, sine, gain_q, gain_k, kv_heads, group
    )
    grad_projected = jnp.concatenate([grad_q, grad_k, grad_v], axis=1)
    grad_projected, (got[0], got[1]) = hold(grad_projected, (got[0], got[1]))
    grad_qkv_part = mul(low_in, grad_projected, lhs_turned).astype(low)
    grad_gate_up = mul(rows, grad_pair, lhs_turned)[None]
    got, grad_gate_up = hold(got, grad_gate_up)
    entries = joined(places, out_own, got)
    if lines == 4:
        output = (mixed + line_halving(entries, place)).astype(low)
    else:
        output = (
            mixed + line_total(entries[0], {p: line_shift(entries[p], lines - p) for p in places[:-1]})
        ).astype(low)
    grad_normed_part = mul(grad_projected, qkv_all, rhs_turned)
    grad_normed = of_block(grad_normed_part, rank) + swap_ctx(
        of_block(grad_normed_part, 1 - rank).astype(low)
    ).astype(full)
    grad_in_part, grad_attn_gain = rms_back(inputs, attn_all, grad_normed)
    grad_tokens = grad_mixed + grad_in_part

    out_mine = lax.psum_scatter(grad_out_part, "fsdp", scatter_dimension=0, tiled=True).astype(full)
    out_other = swap_ctx(out_mine.astype(low)).astype(full)
    grad_out = jnp.where(
        rank == 0,
        jnp.concatenate([out_mine, out_other], axis=0),
        jnp.concatenate([out_other, out_mine], axis=0),
    )
    qkv_mine = lax.psum_scatter(grad_qkv_part, "fsdp", scatter_dimension=0, tiled=True)
    grad_qkv = all_heads(rank_at, qkv_mine, swap_ctx(qkv_mine), head_dim, my_heads)
    early, got = hold(jnp.concatenate([grad_router.T, grad_moe_gain[None]], axis=0), got)
    early = sum_owned(early, fsdp, spot)
    late = sum_all(
        jnp.concatenate(
            [
                grad_attn_gain.reshape(-1, head_dim),
                jnp.sum(gain_q_part, axis=0),
                jnp.sum(gain_k_part, axis=0),
            ],
            axis=0,
        ),
        fsdp,
    )
    (hidden, grad_rows), late = hold((hidden, grad_rows), late)
    grad_down = mul(hidden, grad_rows, lhs_turned)[None]
    gain_rows = width // head_dim
    return (
        output,
        grad_tokens,
        grad_qkv,
        grad_out,
        early[:experts_all].T,
        lax.dynamic_slice_in_dim(late[:gain_rows].reshape(-1), spot * shard, shard, 0),
        early[experts_all],
        late[gain_rows],
        late[gain_rows + 1],
        grad_gate_up,
        grad_down,
    )


gathered_bytes = 1 << 26


def choose_body(*args):
    tokens, gate_up = args[0], args[8]
    fsdp, ctx = lax.axis_size("fsdp"), lax.axis_size("ctx")
    fits = tokens.size * tokens.dtype.itemsize * fsdp * ctx <= gathered_bytes
    if fits and fsdp % 4 == 0 and ctx == 2 and fsdp >= 8 and fsdp & (fsdp - 1) == 0 and gate_up.shape[0] == 1:
        return body_gathered(*args)
    return body_routed(*args)


def solution(mesh):
    in_specs = (
        P(("fsdp", "ctx"), None),
        P("fsdp", None),
        P("fsdp", None),
        P("fsdp", None),
        P("fsdp"),
        P("fsdp"),
        P(),
        P(),
        P(("fsdp", "ctx"), None, None),
        P(("fsdp", "ctx"), None, None),
        P(("fsdp", "ctx"), None),
        P(("fsdp", "ctx"), None),
    )
    out_specs = (
        P(("fsdp", "ctx"), None),
        P(("fsdp", "ctx"), None),
        P("fsdp", None),
        P("fsdp", None),
        P("fsdp", None),
        P("fsdp"),
        P("fsdp"),
        P(),
        P(),
        P(("fsdp", "ctx"), None, None),
        P(("fsdp", "ctx"), None, None),
    )
    return jax.shard_map(choose_body, mesh=mesh, in_specs=in_specs, out_specs=out_specs, check_vma=False)
```

```python
import functools
import math

import jax
import jax.numpy as jnp
from jax import lax
from jax.experimental import pallas as pl
from jax.experimental.pallas import tpu as pltpu
from jax.sharding import PartitionSpec as P

eps_norm = 1e-06
theta_base = 1000000.0


def rms_scale(values, gain):
    return values * lax.rsqrt(jnp.mean(values * values, axis=-1, keepdims=True) + eps_norm) * gain


def rotate(values, cosine, sine):
    half_width = values.shape[-1] // 2
    turned = jnp.concatenate([-values[..., half_width:], values[..., :half_width]], axis=-1)
    return values * cosine + turned * sine


def angles(positions, width):
    freqs = theta_base ** (-(jnp.arange(width // 2, dtype=jnp.float32) * 2.0) / width)
    phase = positions.astype(jnp.float32)[:, None] * freqs[None, :]
    phase = jnp.concatenate([phase, phase], axis=-1)
    return (jnp.cos(phase)[:, None, :], jnp.sin(phase)[:, None, :])


def device_positions(block_rank, ctx_count, tok_rows):
    half_rows = tok_rows // 2
    within = jnp.arange(tok_rows, dtype=jnp.int32)
    span_id = jnp.where(within < half_rows, block_rank, 2 * ctx_count - 1 - block_rank)
    return span_id * half_rows + within % half_rows


def attend_head(query, keys_in, values_in, causal, scale_root):
    scores = (
        jnp.einsum("tgd,sd->gts", query, keys_in, preferred_element_type=jnp.float32) / scale_root
    )
    expo = jnp.where(causal[None], jnp.exp(scores), 0.0)
    totals = jnp.sum(expo, axis=-1, keepdims=True)
    probs = (expo / totals).astype(jnp.bfloat16)
    attended = jnp.einsum("gts,sd->tgd", probs, values_in, preferred_element_type=jnp.float32)
    return (attended, jnp.log(totals[..., 0]))


def attend_back(query, keys_in, values_in, causal, log_total, grad_attended, scale_root):
    scores = (
        jnp.einsum("tgd,sd->gts", query, keys_in, preferred_element_type=jnp.float32) / scale_root
    )
    probs = jnp.where(causal[None], jnp.exp(scores - log_total[..., None]), 0.0)
    low_probs = probs.astype(jnp.bfloat16)
    grad_values = jnp.einsum(
        "gts,tgd->sd", low_probs, grad_attended, preferred_element_type=jnp.float32
    )
    grad_probs = jnp.einsum(
        "tgd,sd->gts", grad_attended, values_in, preferred_element_type=jnp.float32
    )
    delta_rows = jnp.sum(grad_probs * probs, axis=-1, keepdims=True)
    grad_scores = (probs * (grad_probs - delta_rows)).astype(jnp.bfloat16)
    grad_query = (
        jnp.einsum("gts,sd->tgd", grad_scores, keys_in, preferred_element_type=jnp.float32)
        / scale_root
    )
    grad_keys = (
        jnp.einsum("gts,tgd->sd", grad_scores, query, preferred_element_type=jnp.float32)
        / scale_root
    )
    return (grad_query, grad_keys, grad_values)


def swiglu(paired):
    half_width = paired.shape[-1] // 2
    return jax.nn.silu(paired[..., :half_width]) * paired[..., half_width:]


def gating(selected):
    expo = jnp.exp(selected)
    return expo / jnp.sum(expo, axis=1, keepdims=True)


def body_routed(
    tokens,
    qkv_weight,
    out_weight,
    router_weight,
    attn_gain,
    moe_gain,
    query_gain,
    key_gain,
    expert_gate_up,
    expert_down,
    routes,
    cotangent,
):
    rows_dev, width = tokens.shape
    head_dim = query_gain.shape[0]
    top_k = routes.shape[1]
    ctx_count = lax.axis_size("ctx")
    ctx_rank = lax.axis_index("ctx")
    qkv_all, out_all, router_all, attn_all, moe_all = (
        lax.all_gather(qkv_weight, "fsdp", axis=0, tiled=True),
        lax.all_gather(out_weight, "fsdp", axis=0, tiled=True),
        lax.all_gather(router_weight, "fsdp", axis=0, tiled=True),
        lax.all_gather(attn_gain, "fsdp", axis=0, tiled=True),
        lax.all_gather(moe_gain, "fsdp", axis=0, tiled=True),
    )
    experts_all = router_all.shape[1]
    heads = out_all.shape[0] // head_dim
    kv_heads = (qkv_all.shape[1] // head_dim - heads) // 2
    group_size = heads // kv_heads
    capacity = 2 * rows_dev * top_k // experts_all
    width_q = heads * head_dim
    width_k = kv_heads * head_dim
    scale_root = math.sqrt(head_dim)
    inputs = tokens.astype(jnp.float32)
    normed_in = rms_scale(inputs, attn_all.astype(jnp.float32))
    low_in = normed_in.astype(jnp.bfloat16)
    projected = jnp.dot(low_in, qkv_all, preferred_element_type=jnp.float32)
    query_raw = projected[:, :width_q].reshape(rows_dev, heads, head_dim)
    key_raw = projected[:, width_q : width_q + width_k].reshape(rows_dev, kv_heads, head_dim)
    value_low = (
        projected[:, width_q + width_k :].astype(jnp.bfloat16).reshape(rows_dev, kv_heads, head_dim)
    )
    positions = device_positions(ctx_rank, ctx_count, rows_dev)
    cosine, sine = angles(positions, head_dim)
    query_gain_f = query_gain.astype(jnp.float32)
    key_gain_f = key_gain.astype(jnp.float32)

    def query_rope(values_in, gain):
        return rotate(rms_scale(values_in, gain), cosine, sine)

    query_low = query_rope(query_raw, query_gain_f).astype(jnp.bfloat16)
    key_low = query_rope(key_raw, key_gain_f).astype(jnp.bfloat16)
    keys_all, values_all = (
        lax.all_gather(key_low, "ctx", axis=0, tiled=True),
        lax.all_gather(value_low, "ctx", axis=0, tiled=True),
    )
    key_pos = jnp.concatenate(
        [device_positions(other, ctx_count, rows_dev) for other in range(ctx_count)]
    )
    causal = key_pos[None, :] <= positions[:, None]
    query_heads = query_low.reshape(rows_dev, kv_heads, group_size, head_dim).transpose(1, 0, 2, 3)
    key_heads = keys_all.transpose(1, 0, 2)
    value_heads = values_all.transpose(1, 0, 2)
    attended, log_total = lax.map(
        lambda member: attend_head(member[0], member[1], member[2], causal, scale_root),
        (query_heads, key_heads, value_heads),
    )
    attended_low = attended.transpose(1, 0, 2, 3).reshape(rows_dev, width_q).astype(jnp.bfloat16)
    mixed = inputs + jnp.dot(attended_low, out_all, preferred_element_type=jnp.float32)
    normed_mid = rms_scale(mixed, moe_all.astype(jnp.float32))
    low_mid = normed_mid.astype(jnp.bfloat16)
    logits = jnp.dot(low_mid, router_all, preferred_element_type=jnp.float32)
    selected = jnp.take_along_axis(logits, routes, axis=1)
    gates, gate_back = jax.vjp(gating, selected)
    flat_routes = routes.reshape(-1)
    expert_ids = jnp.arange(experts_all, dtype=jnp.int32)
    hit_table = (flat_routes[:, None] == expert_ids[None, :]).astype(jnp.int32)
    slot_index = jnp.sum(jnp.cumsum(hit_table, axis=0) * hit_table, axis=1) - 1
    target = flat_routes * capacity + slot_index
    pair_count = rows_dev * top_k
    source_pair = (
        jnp.full((experts_all * capacity,), pair_count, jnp.int32)
        .at[target]
        .set(jnp.arange(pair_count, dtype=jnp.int32))
    )
    padded = jnp.concatenate([low_mid, jnp.zeros((1, width), jnp.bfloat16)], axis=0)
    outgoing = padded[source_pair // top_k].reshape(experts_all, capacity, width)
    received = lax.all_to_all(outgoing, ("fsdp", "ctx"), split_axis=0, concat_axis=1, tiled=True)
    gate_and_up = jnp.einsum(
        "esd,edf->esf", received, expert_gate_up, preferred_element_type=jnp.float32
    )
    hidden_val, swiglu_back = jax.vjp(swiglu, gate_and_up)
    hidden_low = hidden_val.astype(jnp.bfloat16)
    result_low = jnp.einsum(
        "esf,efd->esd", hidden_low, expert_down, preferred_element_type=jnp.float32
    ).astype(jnp.bfloat16)
    returned = lax.all_to_all(
        result_low, ("fsdp", "ctx"), split_axis=1, concat_axis=0, tiled=True
    ).reshape(experts_all * capacity, width)
    picked = returned[target].reshape(rows_dev, top_k, width).astype(jnp.float32)
    output = (mixed + jnp.sum(gates[:, :, None] * picked, axis=1)).astype(jnp.bfloat16)
    qkv_back, out_back, router_back, attn_back_g, moe_back_g = (
        qkv_all,
        out_all,
        router_all,
        attn_all,
        moe_all,
    )
    grad_final = cotangent.astype(jnp.float32)
    grad_gates = jnp.sum(grad_final[:, None, :] * picked, axis=2)
    grad_result = (
        (gates[:, :, None] * grad_final[:, None, :]).astype(jnp.bfloat16).reshape(pair_count, width)
    )
    grad_padded = jnp.concatenate([grad_result, jnp.zeros((1, width), jnp.bfloat16)], axis=0)
    grad_outgoing = grad_padded[source_pair].reshape(experts_all, capacity, width)
    grad_received = lax.all_to_all(
        grad_outgoing, ("fsdp", "ctx"), split_axis=0, concat_axis=1, tiled=True
    )
    grad_down = jnp.einsum(
        "esf,esd->efd", hidden_low, grad_received, preferred_element_type=jnp.float32
    )
    grad_hidden = jnp.einsum(
        "esd,efd->esf", grad_received, expert_down, preferred_element_type=jnp.float32
    )
    grad_paired = swiglu_back(grad_hidden)[0].astype(jnp.bfloat16)
    grad_gate_up = jnp.einsum(
        "esd,esf->edf", received, grad_paired, preferred_element_type=jnp.float32
    )
    grad_rows = jnp.einsum(
        "esf,edf->esd", grad_paired, expert_gate_up, preferred_element_type=jnp.float32
    ).astype(jnp.bfloat16)
    grad_returned = lax.all_to_all(
        grad_rows, ("fsdp", "ctx"), split_axis=1, concat_axis=0, tiled=True
    ).reshape(experts_all * capacity, width)
    grad_mid = jnp.sum(
        grad_returned[target].reshape(rows_dev, top_k, width).astype(jnp.float32), axis=1
    )
    grad_selected = gate_back(grad_gates)[0]
    route_table = (routes[:, :, None] == expert_ids[None, None, :]).astype(jnp.float32)
    grad_logits = jnp.sum(route_table * grad_selected[:, :, None], axis=1).astype(jnp.bfloat16)
    grad_router = jnp.dot(low_mid.T, grad_logits, preferred_element_type=jnp.float32)
    grad_mid = grad_mid + jnp.dot(grad_logits, router_back.T, preferred_element_type=jnp.float32)
    unused_mid, mid_back = jax.vjp(rms_scale, mixed, moe_back_g.astype(jnp.float32))
    grad_mixed_part, grad_moe_gain = mid_back(grad_mid)
    grad_mixed = grad_final + grad_mixed_part
    grad_branch = grad_mixed.astype(jnp.bfloat16)
    grad_out = jnp.dot(attended_low.T, grad_branch, preferred_element_type=jnp.float32)
    grad_attended = jnp.dot(grad_branch, out_back.T, preferred_element_type=jnp.float32).astype(
        jnp.bfloat16
    )
    grad_heads = grad_attended.reshape(rows_dev, kv_heads, group_size, head_dim).transpose(
        1, 0, 2, 3
    )
    grad_query_h, grad_key_h, grad_value_h = lax.map(
        lambda member: attend_back(
            member[0], member[1], member[2], causal, member[3], member[4], scale_root
        ),
        (query_heads, key_heads, value_heads, log_total, grad_heads),
    )
    grad_keys, grad_values = (
        lax.psum_scatter(
            grad_key_h.transpose(1, 0, 2).astype(jnp.bfloat16),
            "ctx",
            scatter_dimension=0,
            tiled=True,
        ).astype(jnp.float32),
        lax.psum_scatter(
            grad_value_h.transpose(1, 0, 2).astype(jnp.bfloat16),
            "ctx",
            scatter_dimension=0,
            tiled=True,
        ).astype(jnp.float32),
    )
    grad_query_rot = (
        grad_query_h.transpose(1, 0, 2, 3).reshape(rows_dev, heads, head_dim).astype(jnp.bfloat16)
    )
    grad_query_rot = lax.optimization_barrier(grad_query_rot).astype(jnp.float32)
    grad_key_rot = lax.optimization_barrier(grad_keys.astype(jnp.bfloat16)).astype(jnp.float32)
    unused_query, query_back = jax.vjp(query_rope, query_raw, query_gain_f)
    grad_query_raw, grad_query_gain = query_back(grad_query_rot)
    unused_key, key_back = jax.vjp(query_rope, key_raw, key_gain_f)
    grad_key_raw, grad_key_gain = key_back(grad_key_rot)
    grad_projected = jnp.concatenate(
        [
            grad_query_raw.reshape(rows_dev, width_q).astype(jnp.bfloat16),
            grad_key_raw.reshape(rows_dev, width_k).astype(jnp.bfloat16),
            grad_values.reshape(rows_dev, width_k).astype(jnp.bfloat16),
        ],
        axis=1,
    )
    grad_qkv = jnp.dot(low_in.T, grad_projected, preferred_element_type=jnp.float32)
    grad_normed = jnp.dot(grad_projected, qkv_back.T, preferred_element_type=jnp.float32)
    unused_in, in_back = jax.vjp(rms_scale, inputs, attn_back_g.astype(jnp.float32))
    grad_in_part, grad_attn_gain = in_back(grad_normed)
    grad_tokens = grad_mixed + grad_in_part
    gradients = (grad_qkv, grad_out, grad_router, grad_attn_gain, grad_moe_gain)
    pieces = (
        lax.psum_scatter(gradients[0], "fsdp", scatter_dimension=0, tiled=True),
        lax.psum_scatter(gradients[1], "fsdp", scatter_dimension=0, tiled=True),
        lax.psum_scatter(gradients[2], "fsdp", scatter_dimension=0, tiled=True),
        lax.psum_scatter(gradients[3], "fsdp", scatter_dimension=0, tiled=True),
        lax.psum_scatter(gradients[4], "fsdp", scatter_dimension=0, tiled=True),
    )
    reduced = (
        lax.psum(pieces[0].astype(jnp.bfloat16), "ctx").astype(jnp.float32),
        lax.psum(pieces[1].astype(jnp.bfloat16), "ctx").astype(jnp.float32),
        lax.psum(pieces[2].astype(jnp.bfloat16), "ctx").astype(jnp.float32),
        lax.psum(pieces[3].astype(jnp.bfloat16), "ctx").astype(jnp.float32),
        lax.psum(pieces[4].astype(jnp.bfloat16), "ctx").astype(jnp.float32),
    )
    gain_sums = lax.psum((grad_query_gain, grad_key_gain), ("fsdp", "ctx"))
    return (
        output,
        grad_tokens,
        reduced[0],
        reduced[1],
        reduced[2],
        reduced[3],
        reduced[4],
        gain_sums[0],
        gain_sums[1],
        grad_gate_up,
        grad_down,
    )


low = jnp.bfloat16
full = jnp.float32
plain = (((1,), (0,)), ((), ()))
rhs_turned = (((1,), (1,)), ((), ()))
lhs_turned = (((0,), (0,)), ((), ()))
vmem_bytes = 58 << 20


def mul(left, right, dims=plain):
    return lax.dot_general(left, right, dims, preferred_element_type=full)


def core_pairs(fsdp):
    return [(i, i ^ 1) for i in range(fsdp)]


def side_pairs(fsdp):
    return [(i, i ^ 2) for i in range(fsdp)]


def swap_core(values):
    return lax.ppermute(values, "fsdp", core_pairs(lax.axis_size("fsdp")))


def swap_side(values):
    return lax.ppermute(values, "fsdp", side_pairs(lax.axis_size("fsdp")))


def swap_ctx(values):
    return lax.ppermute(values, "ctx", [(0, 1), (1, 0)])


def add_low(one, two):
    return (one.astype(full) + two.astype(full)).astype(low)


def hold(values, first):
    return lax.optimization_barrier((values, first))


def take(values, index):
    return lax.dynamic_index_in_dim(values, index, 0, keepdims=False)


def line_shift(values, step):
    fsdp = lax.axis_size("fsdp")
    return lax.ppermute(values, "fsdp", [(i, (i + 4 * step) % fsdp) for i in range(fsdp)])


def line_total(own, arrived):
    total = own.astype(full)
    for item in arrived.values():
        total = total + item.astype(full)
    return total


def line_first(entries, place):
    fsdp = lax.axis_size("fsdp")
    even = place % 2 == 0
    one, two = jnp.where(even, entries[3], entries[1]), jnp.where(even, entries[1], entries[3])
    return [lax.ppermute(item, "fsdp", [(i, i ^ 4) for i in range(fsdp)]) for item in (one, two)]


def line_second(entries, two):
    return lax.ppermute(
        add_low(entries[2], two), "fsdp", [(i, i ^ 8) for i in range(lax.axis_size("fsdp"))]
    )


def joined(places, own, got):
    from_ctx, from_side, one_side, two_ctx = got
    entries = {}
    for at, p in enumerate(places):
        one = add_low(add_low(own[0][at], from_ctx[at]), one_side[at])
        two = add_low(add_low(own[1][at], from_side[at]), two_ctx[at])
        entries[p] = jnp.concatenate([one, two], axis=-1)
    return entries


def over_core(keep, send):
    return keep, swap_core(send)


def pick_sum(parts, start, stop, column):
    keep, other = parts
    half = keep.shape[-1] // 2
    cut = (slice(start, stop), slice(None), slice(column * half, (column + 1) * half))
    return add_low(keep[cut], other[cut])


def sum_partners(values, fsdp, steps):
    for step in steps:
        values = values + lax.ppermute(values, "fsdp", [(i, i ^ step) for i in range(fsdp)])
    return values


def halve_owned(values, fsdp, spot, steps):
    for step in steps:
        bit = (spot // step) % 2
        values = values.reshape(2, values.shape[0] // 2, *values.shape[1:])
        other = lax.ppermute(take(values, 1 - bit), "fsdp", [(i, i ^ step) for i in range(fsdp)])
        values = take(values, bit) + other
    return values


def turn(values):
    return pltpu.roll(values, values.shape[-1] // 2, 1)


def norm_rope(raw, gain, cosine, sine):
    scale = lax.rsqrt(jnp.mean(raw * raw, axis=-1, keepdims=True) + eps_norm)
    scaled = raw * scale * gain
    return scaled * cosine + turn(scaled) * sine


def norm_rope_back(raw, gain, cosine, sine, grad):
    scale = lax.rsqrt(jnp.mean(raw * raw, axis=-1, keepdims=True) + eps_norm)
    unit = raw * scale
    grad_scaled = grad * cosine - turn(grad) * sine
    grad_gain = jnp.sum(grad_scaled * unit, axis=0, keepdims=True)
    grad_unit = grad_scaled * gain
    grad_raw = scale * (grad_unit - unit * jnp.mean(grad_unit * unit, axis=-1, keepdims=True))
    return grad_raw, grad_gain


def tiles_of(rows):
    step = rows // 2
    return [(start, start + step) for start in range(0, rows, step)]


def allowed(start, stop):
    shape = (stop - start, stop)
    return lax.broadcasted_iota(jnp.int32, shape, 1) <= (
        lax.broadcasted_iota(jnp.int32, shape, 0) + start
    )


def attend_kernel(q_ref, k_ref, v_ref, cos_ref, sin_ref, qg_ref, kg_ref, o_ref, qr_ref, kr_ref, vl_ref):
    head_dim = k_ref.shape[1]
    rows = k_ref.shape[0]
    cosine, sine = cos_ref[...], sin_ref[...]
    keys = norm_rope(k_ref[...], kg_ref[...], cosine, sine).astype(low)
    values = v_ref[...].astype(low)
    kr_ref[...] = keys
    vl_ref[...] = values
    for head in range(q_ref.shape[1] // head_dim):
        cols = slice(head * head_dim, (head + 1) * head_dim)
        query = norm_rope(q_ref[:, cols], qg_ref[...], cosine, sine).astype(low)
        qr_ref[:, cols] = query
        for start, stop in tiles_of(rows):
            scores = mul(query[start:stop], keys[:stop], rhs_turned) * (1.0 / math.sqrt(head_dim))
            expo = jnp.where(allowed(start, stop), jnp.exp(scores), 0.0)
            probs = (expo / jnp.sum(expo, axis=-1, keepdims=True)).astype(low)
            o_ref[start:stop, cols] = mul(probs, values[:stop]).astype(low)


def attend_grad_kernel(
    q_ref, k_ref, qr_ref, kr_ref, vl_ref, go_ref, cos_ref, sin_ref, qg_ref, kg_ref,
    dq_ref, dk_ref, dv_ref, dqg_ref, dkg_ref, dk_sum, dv_sum, dq_sum,
):
    head_dim = k_ref.shape[1]
    rows = k_ref.shape[0]
    root = 1.0 / math.sqrt(head_dim)
    cosine, sine = cos_ref[...], sin_ref[...]
    keys, values = kr_ref[...], vl_ref[...]
    gain_sum = jnp.zeros((1, head_dim), full)
    dk_sum[...] = jnp.zeros_like(dk_sum)
    dv_sum[...] = jnp.zeros_like(dv_sum)
    for head in range(q_ref.shape[1] // head_dim):
        cols = slice(head * head_dim, (head + 1) * head_dim)
        for start, stop in tiles_of(rows):
            query = qr_ref[start:stop, cols]
            grad = go_ref[start:stop, cols]
            scores = mul(query, keys[:stop], rhs_turned) * root
            expo = jnp.where(allowed(start, stop), jnp.exp(scores), 0.0)
            probs = expo / jnp.sum(expo, axis=-1, keepdims=True)
            grad_probs = mul(grad, values[:stop], rhs_turned)
            delta = jnp.sum(grad_probs * probs, axis=-1, keepdims=True)
            grad_scores = (probs * (grad_probs - delta)).astype(low)
            dv_sum[:stop] += mul(probs.astype(low), grad, lhs_turned)
            dk_sum[:stop] += mul(grad_scores, query, lhs_turned)
            dq_sum[start:stop] = mul(grad_scores, keys[:stop])
        grad_query = (dq_sum[...] * root).astype(low).astype(full)
        grad_raw, grad_gain = norm_rope_back(q_ref[:, cols], qg_ref[...], cosine, sine, grad_query)
        dq_ref[:, cols] = grad_raw.astype(low)
        gain_sum = gain_sum + grad_gain
    dqg_ref[0] = gain_sum
    grad_key = (dk_sum[...] * root).astype(low).astype(full)
    grad_raw, grad_gain = norm_rope_back(k_ref[...], kg_ref[...], cosine, sine, grad_key)
    dk_ref[...] = grad_raw.astype(low)
    dkg_ref[0] = grad_gain
    dv_ref[...] = dv_sum[...].astype(low)


def attention_specs(rows, head_dim, kv_heads, group):
    wide, narrow = group * head_dim, head_dim
    heads_end = kv_heads * group
    return dict(
        q=pl.BlockSpec((rows, wide), lambda i: (0, i)),
        k=pl.BlockSpec((rows, narrow), lambda i: (0, heads_end + i)),
        v=pl.BlockSpec((rows, narrow), lambda i: (0, heads_end + kv_heads + i)),
        own=pl.BlockSpec((rows, narrow), lambda i: (0, i)),
        table=pl.BlockSpec((rows, head_dim), lambda i: (0, 0)),
        gain=pl.BlockSpec((1, head_dim), lambda i: (0, 0)),
        gain_out=pl.BlockSpec((1, 1, head_dim), lambda i: (i, 0, 0)),
    )


def attend(projected, cosine, sine, query_gain, key_gain, kv_heads, group):
    rows, head_dim = cosine.shape
    s = attention_specs(rows, head_dim, kv_heads, group)
    shape = jax.ShapeDtypeStruct
    work = rows * rows * head_dim * kv_heads * group
    return pl.pallas_call(
        attend_kernel,
        grid=(kv_heads,),
        in_specs=[s["q"], s["k"], s["v"], s["table"], s["table"], s["gain"], s["gain"]],
        out_specs=[s["q"], s["q"], s["own"], s["own"]],
        out_shape=[
            shape((rows, kv_heads * group * head_dim), low),
            shape((rows, kv_heads * group * head_dim), low),
            shape((rows, kv_heads * head_dim), low),
            shape((rows, kv_heads * head_dim), low),
        ],
        compiler_params=pltpu.CompilerParams(vmem_limit_bytes=48 << 20),
        cost_estimate=pl.CostEstimate(
            flops=4 * work, bytes_accessed=projected.size * 6, transcendentals=work // head_dim
        ),
        name="attend",
    )(projected, projected, projected, cosine, sine, query_gain, key_gain)


def attend_grad(projected, roped_q, roped_k, values_low, grad, cosine, sine, query_gain, key_gain, kv_heads, group):
    rows, head_dim = cosine.shape
    s = attention_specs(rows, head_dim, kv_heads, group)
    shape = jax.ShapeDtypeStruct
    work = rows * rows * head_dim * kv_heads * group
    return pl.pallas_call(
        attend_grad_kernel,
        grid=(kv_heads,),
        in_specs=[
            s["q"], s["k"], s["q"], s["own"], s["own"], s["q"],
            s["table"], s["table"], s["gain"], s["gain"],
        ],
        out_specs=[s["q"], s["own"], s["own"], s["gain_out"], s["gain_out"]],
        out_shape=[
            shape((rows, kv_heads * group * head_dim), low),
            shape((rows, kv_heads * head_dim), low),
            shape((rows, kv_heads * head_dim), low),
            shape((kv_heads, 1, head_dim), full),
            shape((kv_heads, 1, head_dim), full),
        ],
        scratch_shapes=[pltpu.VMEM((rows, head_dim), full)] * 3,
        compiler_params=pltpu.CompilerParams(vmem_limit_bytes=48 << 20),
        cost_estimate=pl.CostEstimate(
            flops=10 * work, bytes_accessed=projected.size * 10, transcendentals=work // head_dim
        ),
        name="attend_grad",
    )(projected, projected, roped_q, roped_k, values_low, grad, cosine, sine, query_gain, key_gain)


def placed(gate, slots):
    block = gate.shape[1]
    shape = (block, block)
    earlier = (
        lax.broadcasted_iota(jnp.int32, shape, 0) < lax.broadcasted_iota(jnp.int32, shape, 1)
    ).astype(low)
    hit = jnp.where(gate >= 0.0, 1.0, 0.0)
    count = mul(jnp.broadcast_to(hit, (8, block)).astype(low), earlier)[:1].astype(jnp.int32)
    place = (lax.broadcasted_iota(jnp.int32, (slots, block), 0) == count) & (hit > 0.5)
    weight = jnp.sum(jnp.where(place, gate, 0.0), axis=1, keepdims=True)
    return place, place.astype(full).astype(low), weight


def expert_kernel(core_ref, order, m_ref, g_ref, far_ref, w_ref, gu_ref, dn_ref, *refs):
    keep_back, send_back, gate_back, rows_ref, dy_ref, z_ref, pair_ref = refs[-7:]
    core = core_ref[0]
    far = order[4 * pl.program_id(0) + 2] == 1
    width = m_ref.shape[4]
    hidden = dn_ref.shape[0]
    slots = z_ref.shape[0] // 2
    places, picks, weights, rows, grads = [], [], [], [], []
    for part in range(2):
        at = lax.rem(core + part, 2)
        place, pick, weight = placed(w_ref[0, at, 0], slots)
        places.append(place)
        picks.append(pick)
        weights.append(weight)
        rows.append(mul(pick, m_ref[0, at, 0]).astype(low))
        near_rows = g_ref[0, at, :, :width]
        far_rows = jnp.concatenate([far_ref[0, at], g_ref[0, at, :, width:]], axis=1)
        grads.append(mul(pick, jnp.where(far, far_rows, near_rows)).astype(low))
    row, grad, weight = (jnp.concatenate(items, axis=0) for items in (rows, grads, weights))
    rows_ref[...] = row
    paired = mul(row, gu_ref[...])
    gate_in, up = paired[:, :hidden], paired[:, hidden:]
    sig = jax.nn.sigmoid(gate_in)
    act = gate_in * sig
    z = (act * up).astype(low)
    z_ref[...] = z
    dy_ref[...] = (weight * grad.astype(full)).astype(low)
    unweighted = mul(grad, dn_ref[...], rhs_turned)
    grad_gate = jnp.sum(unweighted * z.astype(full), axis=1, keepdims=True)
    dz = weight * unweighted
    grad_in = dz * up * (sig * (1.0 + gate_in * (1.0 - sig)))
    pair = jnp.concatenate([grad_in, dz * act], axis=1).astype(low)
    pair_ref[...] = pair
    back = mul(pair, gu_ref[...], rhs_turned).astype(low)
    for part, out in enumerate((keep_back, send_back)):
        mine = slice(part * slots, (part + 1) * slots)
        out[0] = mul(picks[part], back[mine], lhs_turned).astype(low)
        gate_back[0, lax.rem(core + part, 2), 0] = jnp.sum(
            jnp.where(places[part], grad_gate[mine], 0.0), axis=0, keepdims=True
        )


def run_expert(core, order, first, total_steps, m_all, g_all, g_far, gates_all, gate_up, down, slots, kept):
    places, _, _, block, width = m_all.shape
    paired = gate_up.shape[1]
    steps = order.shape[0] // 4
    part_rows = steps * 2 * slots
    hidden = paired // 2
    shape = jax.ShapeDtypeStruct

    def gates_at(i, core, order):
        return (order[4 * i], 0, order[4 * i + 1], 0, 0)

    def token_at(i, core, order):
        return (order[4 * i], 0, order[4 * i + 2], 0, 0)

    def near_at(i, core, order):
        return (order[4 * i], 0, 0, 0)

    def far_at(i, core, order):
        return (order[4 * i + 3], 0, 0, 0)

    def fixed(i, core, order):
        return (0, 0)

    def flat(i, core, order):
        return (first + i, 0)

    def stacked(i, core, order):
        return (i, 0, 0)

    small = pl.BlockSpec((1, 2, 1, 1, block), gates_at)
    one_block = pl.BlockSpec((1, block, width), stacked)
    widths = (width, width, hidden, paired)
    grid_spec = pltpu.PrefetchScalarGridSpec(
        num_scalar_prefetch=2,
        grid=(steps,),
        in_specs=[
            pl.BlockSpec((1, 2, 1, block, width), token_at),
            pl.BlockSpec((1, 2, block, g_all.shape[3]), near_at),
            pl.BlockSpec((1, 2, block, g_far.shape[3]), far_at),
            small,
            pl.BlockSpec(gate_up.shape, fixed, pipeline_mode=pl.Buffered(1)),
            pl.BlockSpec(down.shape, fixed, pipeline_mode=pl.Buffered(1)),
        ]
        + [pl.BlockSpec(memory_space=pl.ANY)] * (0 if kept is None else 5),
        out_specs=[one_block] * 2 + [small] + [pl.BlockSpec((2 * slots, n), flat) for n in widths],
    )
    return pl.pallas_call(
        expert_kernel,
        grid_spec=grid_spec,
        out_shape=[shape((steps, block, width), low)] * 2
        + [shape((places, 2, 2, 1, block), full)]
        + [shape((total_steps * 2 * slots, n), low) for n in widths],
        input_output_aliases={} if kept is None else {8 + i: 2 + i for i in range(5)},
        compiler_params=pltpu.CompilerParams(vmem_limit_bytes=vmem_bytes),
        cost_estimate=pl.CostEstimate(
            flops=part_rows * width * (4 * paired + 2 * hidden + 6 * block),
            bytes_accessed=steps * block * width * 12 + part_rows * (width * 4 + paired * 3),
            transcendentals=part_rows * hidden,
        ),
        name="experts",
    )(core, order, m_all, g_all, g_far, gates_all, gate_up, down, *(() if kept is None else kept))


def result_kernel(core_ref, order, z_ref, w_ref, dn_ref, keep_out, send_out):
    core = core_ref[0]
    slots = z_ref.shape[0] // 2
    y = mul(z_ref[...], dn_ref[...]).astype(low).astype(full)
    for part, out in enumerate((keep_out, send_out)):
        _, pick, weight = placed(w_ref[0, lax.rem(core + part, 2), 0], slots)
        scaled = (weight * y[part * slots : (part + 1) * slots]).astype(low)
        out[0] = mul(pick, scaled, lhs_turned).astype(low)


def run_result(core, order, first, hidden, gates_all, down, slots):
    block, width, inner = gates_all.shape[4], down.shape[1], down.shape[0]
    steps = order.shape[0] // 4
    one_block = pl.BlockSpec((1, block, width), lambda i, core, order: (i, 0, 0))
    return pl.pallas_call(
        result_kernel,
        grid_spec=pltpu.PrefetchScalarGridSpec(
            num_scalar_prefetch=2,
            grid=(steps,),
            in_specs=[
                pl.BlockSpec((2 * slots, inner), lambda i, core, order: (first + i, 0)),
                pl.BlockSpec(
                    (1, 2, 1, 1, block), lambda i, core, order: (order[4 * i], 0, order[4 * i + 1], 0, 0)
                ),
                pl.BlockSpec(down.shape, lambda i, core, order: (0, 0), pipeline_mode=pl.Buffered(1)),
            ],
            out_specs=[one_block] * 2,
        ),
        out_shape=[jax.ShapeDtypeStruct((steps, block, width), low)] * 2,
        compiler_params=pltpu.CompilerParams(vmem_limit_bytes=vmem_bytes),
        cost_estimate=pl.CostEstimate(
            flops=steps * 2 * slots * width * (2 * inner + 2 * block),
            bytes_accessed=steps * (4 * block * width + 4 * slots * inner) + 2 * inner * width,
            transcendentals=0,
        ),
        name="results",
    )(core, order, hidden, gates_all, down)


def own_heads_kernel(rank, qkv_ref, out_ref, o_ref, *, head_dim, heads):
    first = rank[0] == 0
    for head in range(heads):
        pair = [qkv_ref[:, (2 * head + i) * head_dim : (2 * head + i + 1) * head_dim] for i in range(2)]
        o_ref[:, head * head_dim : (head + 1) * head_dim] = jnp.where(first, pair[0], pair[1])
    kv = qkv_ref.shape[1] - 2 * heads * head_dim
    o_ref[:, heads * head_dim : heads * head_dim + kv] = qkv_ref[:, 2 * heads * head_dim :]
    o_ref[:, heads * head_dim + kv :] = jnp.where(first, out_ref[:head_dim], out_ref[head_dim:])


def own_heads(rank, qkv_weight, out_weight, head_dim, heads):
    kv = qkv_weight.shape[1] - 2 * heads * head_dim
    return pl.pallas_call(
        functools.partial(own_heads_kernel, head_dim=head_dim, heads=heads),
        grid_spec=pltpu.PrefetchScalarGridSpec(
            num_scalar_prefetch=1,
            grid=(1,),
            in_specs=[
                pl.BlockSpec(qkv_weight.shape, lambda i, rank: (0, 0)),
                pl.BlockSpec(out_weight.shape, lambda i, rank: (0, 0)),
            ],
            out_specs=pl.BlockSpec(
                (qkv_weight.shape[0], heads * head_dim + kv + out_weight.shape[1]), lambda i, rank: (0, 0)
            ),
        ),
        out_shape=jax.ShapeDtypeStruct(
            (qkv_weight.shape[0], heads * head_dim + kv + out_weight.shape[1]), qkv_weight.dtype
        ),
        name="own_heads",
    )(rank, qkv_weight, out_weight)


def all_heads_kernel(rank, mine_ref, other_ref, o_ref, *, head_dim, heads):
    first = rank[0] == 0
    for head in range(heads):
        cols = slice(head * head_dim, (head + 1) * head_dim)
        mine, other = mine_ref[:, cols].astype(full), other_ref[:, cols].astype(full)
        o_ref[:, 2 * head * head_dim : (2 * head + 1) * head_dim] = jnp.where(first, mine, other)
        o_ref[:, (2 * head + 1) * head_dim : (2 * head + 2) * head_dim] = jnp.where(first, other, mine)
    o_ref[:, 2 * heads * head_dim :] = mine_ref[:, heads * head_dim :].astype(full) + other_ref[
        :, heads * head_dim :
    ].astype(full)


def all_heads(rank, mine, other, head_dim, heads):
    rows, width = mine.shape
    return pl.pallas_call(
        functools.partial(all_heads_kernel, head_dim=head_dim, heads=heads),
        grid_spec=pltpu.PrefetchScalarGridSpec(
            num_scalar_prefetch=1,
            grid=(1,),
            in_specs=[pl.BlockSpec((rows, width), lambda i, rank: (0, 0))] * 2,
            out_specs=pl.BlockSpec((rows, width + heads * head_dim), lambda i, rank: (0, 0)),
        ),
        out_shape=jax.ShapeDtypeStruct((rows, width + heads * head_dim), full),
        name="all_heads",
    )(rank, mine, other)


def rms_back(values, gain, grad):
    scale = lax.rsqrt(jnp.mean(values * values, axis=-1, keepdims=True) + eps_norm)
    unit = values * scale
    grad_gain = jnp.sum(grad * unit, axis=0)
    grad_unit = grad * gain
    back = scale * (grad_unit - unit * jnp.mean(grad_unit * unit, axis=-1, keepdims=True))
    return back, grad_gain


def in_order(first, second):
    half = first.shape[0] // 2
    return jnp.concatenate([first[:half], second, first[half:]], axis=0)


def of_block(values, rank):
    quarter = values.shape[0] // 4
    outer = jnp.concatenate([values[:quarter], values[3 * quarter :]], axis=0)
    return jnp.where(rank == 0, outer, values[quarter : 3 * quarter])


def body_gathered(
    tokens, qkv_weight, out_weight, router_weight, attn_gain, moe_gain, query_gain, key_gain,
    expert_gate_up, expert_down, routes, cotangent,
):
    rows_dev, width = tokens.shape
    head_dim = query_gain.shape[0]
    top_k = routes.shape[1]
    fsdp = lax.axis_size("fsdp")
    spot = lax.axis_index("fsdp")
    rank = lax.axis_index("ctx")
    place, side, core = spot // 4, (spot // 2) % 2, spot % 2
    shard = qkv_weight.shape[0]
    heads = out_weight.shape[0] * fsdp // head_dim
    kv_heads = (qkv_weight.shape[1] // head_dim - heads) // 2
    group = heads // kv_heads // 2
    my_heads = heads // 2
    width_q, width_k = my_heads * head_dim, kv_heads * head_dim
    experts_all = router_weight.shape[1]
    capacity = 2 * rows_dev * top_k // experts_all
    both = ("fsdp", "ctx")

    def sequence(values):
        other = swap_ctx(values)
        first = jnp.where(rank == 0, values, other)
        second = jnp.where(rank == 0, other, values)
        return in_order(first, second)

    rank_at = rank[None].astype(jnp.int32)
    weights_local = own_heads(rank_at, qkv_weight, out_weight, head_dim, my_heads)
    small_local = jnp.concatenate([router_weight, attn_gain[:, None], moe_gain[:, None]], axis=1)
    small_all = lax.all_gather(small_local, "fsdp", axis=0, tiled=True)
    weights_all = lax.all_gather(weights_local, "fsdp", axis=0, tiled=True)
    qkv_all = weights_all[:, : width_q + 2 * width_k]
    out_all = weights_all[:, width_q + 2 * width_k :]
    router_all = small_all[:, :experts_all]
    attn_all = small_all[:, experts_all].astype(full)
    moe_all = small_all[:, experts_all + 1].astype(full)
    late_cols = width * 7 // 16
    g_all = lax.all_gather(
        jnp.concatenate([cotangent, swap_ctx(cotangent[:, late_cols:])], axis=1), "fsdp", axis=0, tiled=True
    ).reshape(fsdp // 2, 2, rows_dev, 2 * width - late_cols)

    sequence_in = sequence(tokens).astype(full)
    low_in = rms_scale(sequence_in, attn_all).astype(low)
    projected = mul(low_in, qkv_all)
    cosine, sine = (t[:, 0] for t in angles(jnp.arange(2 * rows_dev, dtype=jnp.int32), head_dim))
    sine = jnp.concatenate([-sine[:, : head_dim // 2], sine[:, head_dim // 2 :]], axis=1)
    gain_q, gain_k = query_gain.astype(full)[None], key_gain.astype(full)[None]
    attended, roped_q, roped_k, values_low = attend(
        projected, cosine, sine, gain_q, gain_k, kv_heads, group
    )
    branch = mul(attended, out_all)
    inputs = tokens.astype(full)
    mixed = (
        inputs
        + of_block(branch, rank)
        + swap_ctx(of_block(branch, 1 - rank).astype(low)).astype(full)
    )
    low_mid = rms_scale(mixed, moe_all).astype(low)
    m_all = lax.all_gather(jnp.concatenate([low_mid, swap_ctx(low_mid)]), "fsdp", axis=0, tiled=True)

    logits = mul(low_mid, router_all)
    named = routes[:, :, None] == jnp.arange(experts_all, dtype=jnp.int32)[None, None, :]
    selected = jnp.sum(jnp.where(named, logits[:, None, :], 0.0), axis=2)
    gates = gating(selected)
    chosen = jnp.any(named, axis=1)
    gates_wide = jnp.sum(jnp.where(named, gates[:, :, None], 0.0), axis=1)
    gates_sent = jnp.where(chosen, gates_wide, -1.0).T
    gates_all = lax.all_to_all(gates_sent, both, split_axis=0, concat_axis=0, tiled=True)

    g_all, gates_all = hold(g_all, gates_all)
    g_far = swap_ctx(g_all[..., :late_cols])

    lines = fsdp // 4
    places = list(range(1, lines)) + [0]
    cut = lines // 2
    parts = [places[:cut], places[cut:]]
    m_all = m_all.reshape(fsdp // 2, 2, 2, rows_dev, width)
    gates_all = gates_all.reshape(fsdp // 2, 2, 2, 1, rows_dev)
    state = dict(kept=None, first=0, core=core[None].astype(jnp.int32))

    def order_of(steps):
        spots = [((place - p) % lines) * 2 + (side + d) % 2 for d, _, p in steps]
        far = [i for i, step in enumerate(steps) if step[1] == 1] or [0]
        return jnp.stack(
            [
                jnp.asarray(item, jnp.int32)
                for i, step in enumerate(steps)
                for item in (
                    spots[i],
                    (rank + step[1]) % 2,
                    step[1],
                    spots[min(far, key=lambda j, i=i: abs(j - i))],
                )
            ]
        )

    def call(steps, raw=False):
        keep_back, send_back, *kept = run_expert(
            state["core"],
            order_of(steps),
            state["first"],
            4 * lines,
            m_all,
            g_all,
            g_far,
            gates_all,
            expert_gate_up[0],
            expert_down[0],
            capacity,
            state["kept"],
        )
        state["kept"] = kept
        state["first"] += len(steps)
        return (keep_back, send_back) if raw else over_core(keep_back, send_back)

    def wait(first):
        state["core"], first = hold(state["core"], first)
        return first

    steps_far, steps_own = ([(d, d, p) for p in places] for d in (1, 0))
    steps_mixed = [[(1, 0, p) for p in part] + [(0, 1, p) for p in part] for part in parts]
    back = call(steps_far)
    far_one, far_two = wait([pick_sum(back, 0, lines, column) for column in range(2)])
    far_one, far_two = swap_ctx(far_one), swap_side(far_two)

    def mixed_sums(back, at=0):
        return [
            pick_sum(back, start, start + cut, column) for start in (at, at + cut) for column in range(2)
        ]

    def rounds(sums, part):
        side_one, side_two, ctx_one, ctx_two = sums
        span = slice(part * cut, (part + 1) * cut)
        return [
            swap_ctx(ctx_one),
            swap_side(side_two),
            swap_side(add_low(side_one, far_one[span])),
            swap_ctx(add_low(ctx_two, far_two[span])),
        ]

    keep, send = call(steps_mixed[0], raw=True)
    send, (far_one, far_two) = hold(send, (far_one, far_two))
    back = over_core(keep, send)
    back_own = call(steps_own)
    sums = wait(mixed_sums(back))
    back_own = [pick_sum(back_own, 0, lines, column) for column in range(2)]
    got = rounds(sums, 0)
    keep, send = call(steps_mixed[1], raw=True)
    send, got = hold(send, got)
    back = over_core(keep, send)
    entries = joined(parts[0], [item[:cut] for item in back_own], got)
    arrived = {p: line_shift(entries[p], lines - p) for p in parts[0]}
    gate_back, rows, grad_rows, hidden, grad_pair = state["kept"]
    hidden, sums = hold(hidden, mixed_sums(back))
    got = rounds(sums, 1)
    grad_gates = lax.all_to_all(
        gate_back.reshape(fsdp * 2, rows_dev), both, split_axis=0, concat_axis=0, tiled=True
    ).T
    def results(first, steps, hidden):
        return run_result(
            state["core"], order_of(steps), first, hidden, gates_all, expert_down[0], capacity
        )

    out_far = results(0, steps_far, hidden)
    out_rest = results(lines, steps_mixed[0] + steps_own + steps_mixed[1], hidden)
    got, out_far, out_rest, arrived, grad_gates = lax.optimization_barrier(
        (got, out_far, out_rest, arrived, grad_gates)
    )
    entries.update(joined(parts[1], [item[cut:] for item in back_own], got))
    out_far = over_core(*out_far)
    out_far = [pick_sum(out_far, 0, lines, 0), swap_side(pick_sum(out_far, 0, lines, 1))]
    out_rest = over_core(*out_rest)
    for p in parts[1][:-1]:
        arrived[p] = line_shift(entries[p], lines - p)
    grad_mid = line_total(entries[0], arrived)

    grad_wide = jnp.where(chosen, grad_gates, 0.0)
    grad_logits = (
        gates_wide * (grad_wide - jnp.sum(gates_wide * grad_wide, axis=1, keepdims=True))
    ).astype(low)
    grad_router = mul(low_mid, grad_logits, lhs_turned)
    grad_mid = grad_mid + mul(grad_logits, router_all, rhs_turned)
    grad_mixed_part, grad_moe_gain = rms_back(mixed, moe_all, grad_mid)
    grad_mixed = cotangent.astype(full) + grad_mixed_part

    low_mixed, (out_far[0], out_rest) = hold(grad_mixed.astype(low), (out_far[0], out_rest))
    grad_branch = sequence(low_mixed)
    out_sums = [
        jnp.concatenate([one, two])
        for one, two in zip(mixed_sums(out_rest), mixed_sums(out_rest, 2 * cut + lines))
    ]
    out_own = [pick_sum(out_rest, 2 * cut, 2 * cut + lines, column) for column in range(2)]
    (out_far[0], out_sums, out_own), grad_branch = hold((out_far[0], out_sums, out_own), grad_branch)
    side_one, side_two, ctx_one, ctx_two = out_sums
    out_far[0] = swap_ctx(out_far[0])
    grad_attended = mul(grad_branch, out_all, rhs_turned).astype(low)
    grad_out_part = mul(attended, grad_branch, lhs_turned).astype(low)
    grad_q, grad_k, grad_v, gain_q_part, gain_k_part = attend_grad(
        projected, roped_q, roped_k, values_low, grad_attended, cosine, sine, gain_q, gain_k, kv_heads, group
    )
    grad_projected = jnp.concatenate([grad_q, grad_k, grad_v], axis=1)
    grad_projected, out_far = hold(grad_projected, out_far)
    got = [
        swap_ctx(ctx_one),
        swap_side(side_two),
        swap_side(add_low(side_one, out_far[0])),
        swap_ctx(add_low(ctx_two, out_far[1])),
    ]
    grad_qkv_part = mul(low_in, grad_projected, lhs_turned).astype(low)
    grad_normed_part = mul(grad_projected, qkv_all, rhs_turned)
    early = jnp.concatenate([grad_router.T, grad_moe_gain[None]], axis=0)
    early = early.reshape(experts_all + 1, fsdp, shard).swapaxes(0, 1)
    early = halve_owned(early, fsdp, spot, (8, 4))
    grad_gate_up = mul(rows, grad_pair, lhs_turned)[None]
    got, early = hold(got, early)
    entries = joined(places, out_own, got)
    one, two = line_first(entries, place)
    grad_normed = of_block(grad_normed_part, rank) + swap_ctx(
        of_block(grad_normed_part, 1 - rank).astype(low)
    ).astype(full)
    grad_in_part, grad_attn_gain = rms_back(inputs, attn_all, grad_normed)
    grad_tokens = grad_mixed + grad_in_part

    out_mine = lax.psum_scatter(grad_out_part, "fsdp", scatter_dimension=0, tiled=True).astype(full)
    out_other = swap_ctx(out_mine.astype(low)).astype(full)
    grad_out = jnp.where(
        rank == 0,
        jnp.concatenate([out_mine, out_other], axis=0),
        jnp.concatenate([out_other, out_mine], axis=0),
    )
    qkv_mine = lax.psum_scatter(grad_qkv_part, "fsdp", scatter_dimension=0, tiled=True)
    grad_qkv = all_heads(rank_at, qkv_mine, swap_ctx(qkv_mine), head_dim, my_heads)
    early = halve_owned(early, fsdp, spot, (2, 1))[0]
    early = early + swap_ctx(early)
    late = jnp.concatenate(
        [
            grad_attn_gain.reshape(-1, head_dim),
            jnp.sum(gain_q_part, axis=0),
            jnp.sum(gain_k_part, axis=0),
        ],
        axis=0,
    )
    grad_down = mul(hidden, grad_rows, lhs_turned)[None]
    late, (one, two, grad_gate_up, grad_down) = hold(late, (one, two, grad_gate_up, grad_down))
    far = line_second(entries, two)
    late = swap_ctx(late) + late
    late, far = hold(sum_partners(late, fsdp, (1, 2)), far)
    output = (mixed + entries[0].astype(full) + one.astype(full) + far.astype(full)).astype(low)
    late = sum_partners(late, fsdp, (4, 8))
    gain_rows = width // head_dim
    return (
        output,
        grad_tokens,
        grad_qkv,
        grad_out,
        early[:experts_all].T,
        lax.dynamic_slice_in_dim(late[:gain_rows].reshape(-1), spot * shard, shard, 0),
        early[experts_all],
        late[gain_rows],
        late[gain_rows + 1],
        grad_gate_up,
        grad_down,
    )


gathered_bytes = 1 << 26


def choose_body(*args):
    tokens, gate_up = args[0], args[8]
    fsdp, ctx = lax.axis_size("fsdp"), lax.axis_size("ctx")
    fits = tokens.size * tokens.dtype.itemsize * fsdp * ctx <= gathered_bytes
    if fits and ctx == 2 and fsdp == 16 and gate_up.shape[0] == 1:
        return body_gathered(*args)
    return body_routed(*args)


def solution(mesh):
    in_specs = (
        P(("fsdp", "ctx"), None),
        P("fsdp", None),
        P("fsdp", None),
        P("fsdp", None),
        P("fsdp"),
        P("fsdp"),
        P(),
        P(),
        P(("fsdp", "ctx"), None, None),
        P(("fsdp", "ctx"), None, None),
        P(("fsdp", "ctx"), None),
        P(("fsdp", "ctx"), None),
    )
    out_specs = (
        P(("fsdp", "ctx"), None),
        P(("fsdp", "ctx"), None),
        P("fsdp", None),
        P("fsdp", None),
        P("fsdp", None),
        P("fsdp"),
        P("fsdp"),
        P(),
        P(),
        P(("fsdp", "ctx"), None, None),
        P(("fsdp", "ctx"), None, None),
    )
    return jax.shard_map(choose_body, mesh=mesh, in_specs=in_specs, out_specs=out_specs, check_vma=False)
```

```python
import functools
import math

import jax
import jax.numpy as jnp
from jax import lax
from jax.experimental import pallas as pl
from jax.experimental.pallas import tpu as pltpu
from jax.sharding import PartitionSpec as P

eps_norm = 1e-06
theta_base = 1000000.0


def rms_scale(values, gain):
    return values * lax.rsqrt(jnp.mean(values * values, axis=-1, keepdims=True) + eps_norm) * gain


def rotate(values, cosine, sine):
    half_width = values.shape[-1] // 2
    turned = jnp.concatenate([-values[..., half_width:], values[..., :half_width]], axis=-1)
    return values * cosine + turned * sine


def angles(positions, width):
    freqs = theta_base ** (-(jnp.arange(width // 2, dtype=jnp.float32) * 2.0) / width)
    phase = positions.astype(jnp.float32)[:, None] * freqs[None, :]
    phase = jnp.concatenate([phase, phase], axis=-1)
    return (jnp.cos(phase)[:, None, :], jnp.sin(phase)[:, None, :])


def device_positions(block_rank, ctx_count, tok_rows):
    half_rows = tok_rows // 2
    within = jnp.arange(tok_rows, dtype=jnp.int32)
    span_id = jnp.where(within < half_rows, block_rank, 2 * ctx_count - 1 - block_rank)
    return span_id * half_rows + within % half_rows


def attend_head(query, keys_in, values_in, causal, scale_root):
    scores = (
        jnp.einsum("tgd,sd->gts", query, keys_in, preferred_element_type=jnp.float32) / scale_root
    )
    expo = jnp.where(causal[None], jnp.exp(scores), 0.0)
    totals = jnp.sum(expo, axis=-1, keepdims=True)
    probs = (expo / totals).astype(jnp.bfloat16)
    attended = jnp.einsum("gts,sd->tgd", probs, values_in, preferred_element_type=jnp.float32)
    return (attended, jnp.log(totals[..., 0]))


def attend_back(query, keys_in, values_in, causal, log_total, grad_attended, scale_root):
    scores = (
        jnp.einsum("tgd,sd->gts", query, keys_in, preferred_element_type=jnp.float32) / scale_root
    )
    probs = jnp.where(causal[None], jnp.exp(scores - log_total[..., None]), 0.0)
    low_probs = probs.astype(jnp.bfloat16)
    grad_values = jnp.einsum(
        "gts,tgd->sd", low_probs, grad_attended, preferred_element_type=jnp.float32
    )
    grad_probs = jnp.einsum(
        "tgd,sd->gts", grad_attended, values_in, preferred_element_type=jnp.float32
    )
    delta_rows = jnp.sum(grad_probs * probs, axis=-1, keepdims=True)
    grad_scores = (probs * (grad_probs - delta_rows)).astype(jnp.bfloat16)
    grad_query = (
        jnp.einsum("gts,sd->tgd", grad_scores, keys_in, preferred_element_type=jnp.float32)
        / scale_root
    )
    grad_keys = (
        jnp.einsum("gts,tgd->sd", grad_scores, query, preferred_element_type=jnp.float32)
        / scale_root
    )
    return (grad_query, grad_keys, grad_values)


def swiglu(paired):
    half_width = paired.shape[-1] // 2
    return jax.nn.silu(paired[..., :half_width]) * paired[..., half_width:]


def gating(selected):
    expo = jnp.exp(selected)
    return expo / jnp.sum(expo, axis=1, keepdims=True)


def body_routed(
    tokens,
    qkv_weight,
    out_weight,
    router_weight,
    attn_gain,
    moe_gain,
    query_gain,
    key_gain,
    expert_gate_up,
    expert_down,
    routes,
    cotangent,
):
    rows_dev, width = tokens.shape
    head_dim = query_gain.shape[0]
    top_k = routes.shape[1]
    ctx_count = lax.axis_size("ctx")
    ctx_rank = lax.axis_index("ctx")
    qkv_all, out_all, router_all, attn_all, moe_all = (
        lax.all_gather(qkv_weight, "fsdp", axis=0, tiled=True),
        lax.all_gather(out_weight, "fsdp", axis=0, tiled=True),
        lax.all_gather(router_weight, "fsdp", axis=0, tiled=True),
        lax.all_gather(attn_gain, "fsdp", axis=0, tiled=True),
        lax.all_gather(moe_gain, "fsdp", axis=0, tiled=True),
    )
    experts_all = router_all.shape[1]
    heads = out_all.shape[0] // head_dim
    kv_heads = (qkv_all.shape[1] // head_dim - heads) // 2
    group_size = heads // kv_heads
    capacity = 2 * rows_dev * top_k // experts_all
    width_q = heads * head_dim
    width_k = kv_heads * head_dim
    scale_root = math.sqrt(head_dim)
    inputs = tokens.astype(jnp.float32)
    normed_in = rms_scale(inputs, attn_all.astype(jnp.float32))
    low_in = normed_in.astype(jnp.bfloat16)
    projected = jnp.dot(low_in, qkv_all, preferred_element_type=jnp.float32)
    query_raw = projected[:, :width_q].reshape(rows_dev, heads, head_dim)
    key_raw = projected[:, width_q : width_q + width_k].reshape(rows_dev, kv_heads, head_dim)
    value_low = (
        projected[:, width_q + width_k :].astype(jnp.bfloat16).reshape(rows_dev, kv_heads, head_dim)
    )
    positions = device_positions(ctx_rank, ctx_count, rows_dev)
    cosine, sine = angles(positions, head_dim)
    query_gain_f = query_gain.astype(jnp.float32)
    key_gain_f = key_gain.astype(jnp.float32)

    def query_rope(values_in, gain):
        return rotate(rms_scale(values_in, gain), cosine, sine)

    query_low = query_rope(query_raw, query_gain_f).astype(jnp.bfloat16)
    key_low = query_rope(key_raw, key_gain_f).astype(jnp.bfloat16)
    keys_all, values_all = (
        lax.all_gather(key_low, "ctx", axis=0, tiled=True),
        lax.all_gather(value_low, "ctx", axis=0, tiled=True),
    )
    key_pos = jnp.concatenate(
        [device_positions(other, ctx_count, rows_dev) for other in range(ctx_count)]
    )
    causal = key_pos[None, :] <= positions[:, None]
    query_heads = query_low.reshape(rows_dev, kv_heads, group_size, head_dim).transpose(1, 0, 2, 3)
    key_heads = keys_all.transpose(1, 0, 2)
    value_heads = values_all.transpose(1, 0, 2)
    attended, log_total = lax.map(
        lambda member: attend_head(member[0], member[1], member[2], causal, scale_root),
        (query_heads, key_heads, value_heads),
    )
    attended_low = attended.transpose(1, 0, 2, 3).reshape(rows_dev, width_q).astype(jnp.bfloat16)
    mixed = inputs + jnp.dot(attended_low, out_all, preferred_element_type=jnp.float32)
    normed_mid = rms_scale(mixed, moe_all.astype(jnp.float32))
    low_mid = normed_mid.astype(jnp.bfloat16)
    logits = jnp.dot(low_mid, router_all, preferred_element_type=jnp.float32)
    selected = jnp.take_along_axis(logits, routes, axis=1)
    gates, gate_back = jax.vjp(gating, selected)
    flat_routes = routes.reshape(-1)
    expert_ids = jnp.arange(experts_all, dtype=jnp.int32)
    hit_table = (flat_routes[:, None] == expert_ids[None, :]).astype(jnp.int32)
    slot_index = jnp.sum(jnp.cumsum(hit_table, axis=0) * hit_table, axis=1) - 1
    target = flat_routes * capacity + slot_index
    pair_count = rows_dev * top_k
    source_pair = (
        jnp.full((experts_all * capacity,), pair_count, jnp.int32)
        .at[target]
        .set(jnp.arange(pair_count, dtype=jnp.int32))
    )
    padded = jnp.concatenate([low_mid, jnp.zeros((1, width), jnp.bfloat16)], axis=0)
    outgoing = padded[source_pair // top_k].reshape(experts_all, capacity, width)
    received = lax.all_to_all(outgoing, ("fsdp", "ctx"), split_axis=0, concat_axis=1, tiled=True)
    gate_and_up = jnp.einsum(
        "esd,edf->esf", received, expert_gate_up, preferred_element_type=jnp.float32
    )
    hidden_val, swiglu_back = jax.vjp(swiglu, gate_and_up)
    hidden_low = hidden_val.astype(jnp.bfloat16)
    result_low = jnp.einsum(
        "esf,efd->esd", hidden_low, expert_down, preferred_element_type=jnp.float32
    ).astype(jnp.bfloat16)
    returned = lax.all_to_all(
        result_low, ("fsdp", "ctx"), split_axis=1, concat_axis=0, tiled=True
    ).reshape(experts_all * capacity, width)
    picked = returned[target].reshape(rows_dev, top_k, width).astype(jnp.float32)
    output = (mixed + jnp.sum(gates[:, :, None] * picked, axis=1)).astype(jnp.bfloat16)
    qkv_back, out_back, router_back, attn_back_g, moe_back_g = (
        qkv_all,
        out_all,
        router_all,
        attn_all,
        moe_all,
    )
    grad_final = cotangent.astype(jnp.float32)
    grad_gates = jnp.sum(grad_final[:, None, :] * picked, axis=2)
    grad_result = (
        (gates[:, :, None] * grad_final[:, None, :]).astype(jnp.bfloat16).reshape(pair_count, width)
    )
    grad_padded = jnp.concatenate([grad_result, jnp.zeros((1, width), jnp.bfloat16)], axis=0)
    grad_outgoing = grad_padded[source_pair].reshape(experts_all, capacity, width)
    grad_received = lax.all_to_all(
        grad_outgoing, ("fsdp", "ctx"), split_axis=0, concat_axis=1, tiled=True
    )
    grad_down = jnp.einsum(
        "esf,esd->efd", hidden_low, grad_received, preferred_element_type=jnp.float32
    )
    grad_hidden = jnp.einsum(
        "esd,efd->esf", grad_received, expert_down, preferred_element_type=jnp.float32
    )
    grad_paired = swiglu_back(grad_hidden)[0].astype(jnp.bfloat16)
    grad_gate_up = jnp.einsum(
        "esd,esf->edf", received, grad_paired, preferred_element_type=jnp.float32
    )
    grad_rows = jnp.einsum(
        "esf,edf->esd", grad_paired, expert_gate_up, preferred_element_type=jnp.float32
    ).astype(jnp.bfloat16)
    grad_returned = lax.all_to_all(
        grad_rows, ("fsdp", "ctx"), split_axis=1, concat_axis=0, tiled=True
    ).reshape(experts_all * capacity, width)
    grad_mid = jnp.sum(
        grad_returned[target].reshape(rows_dev, top_k, width).astype(jnp.float32), axis=1
    )
    grad_selected = gate_back(grad_gates)[0]
    route_table = (routes[:, :, None] == expert_ids[None, None, :]).astype(jnp.float32)
    grad_logits = jnp.sum(route_table * grad_selected[:, :, None], axis=1).astype(jnp.bfloat16)
    grad_router = jnp.dot(low_mid.T, grad_logits, preferred_element_type=jnp.float32)
    grad_mid = grad_mid + jnp.dot(grad_logits, router_back.T, preferred_element_type=jnp.float32)
    unused_mid, mid_back = jax.vjp(rms_scale, mixed, moe_back_g.astype(jnp.float32))
    grad_mixed_part, grad_moe_gain = mid_back(grad_mid)
    grad_mixed = grad_final + grad_mixed_part
    grad_branch = grad_mixed.astype(jnp.bfloat16)
    grad_out = jnp.dot(attended_low.T, grad_branch, preferred_element_type=jnp.float32)
    grad_attended = jnp.dot(grad_branch, out_back.T, preferred_element_type=jnp.float32).astype(
        jnp.bfloat16
    )
    grad_heads = grad_attended.reshape(rows_dev, kv_heads, group_size, head_dim).transpose(
        1, 0, 2, 3
    )
    grad_query_h, grad_key_h, grad_value_h = lax.map(
        lambda member: attend_back(
            member[0], member[1], member[2], causal, member[3], member[4], scale_root
        ),
        (query_heads, key_heads, value_heads, log_total, grad_heads),
    )
    grad_keys, grad_values = (
        lax.psum_scatter(
            grad_key_h.transpose(1, 0, 2).astype(jnp.bfloat16),
            "ctx",
            scatter_dimension=0,
            tiled=True,
        ).astype(jnp.float32),
        lax.psum_scatter(
            grad_value_h.transpose(1, 0, 2).astype(jnp.bfloat16),
            "ctx",
            scatter_dimension=0,
            tiled=True,
        ).astype(jnp.float32),
    )
    grad_query_rot = (
        grad_query_h.transpose(1, 0, 2, 3).reshape(rows_dev, heads, head_dim).astype(jnp.bfloat16)
    )
    grad_query_rot = lax.optimization_barrier(grad_query_rot).astype(jnp.float32)
    grad_key_rot = lax.optimization_barrier(grad_keys.astype(jnp.bfloat16)).astype(jnp.float32)
    unused_query, query_back = jax.vjp(query_rope, query_raw, query_gain_f)
    grad_query_raw, grad_query_gain = query_back(grad_query_rot)
    unused_key, key_back = jax.vjp(query_rope, key_raw, key_gain_f)
    grad_key_raw, grad_key_gain = key_back(grad_key_rot)
    grad_projected = jnp.concatenate(
        [
            grad_query_raw.reshape(rows_dev, width_q).astype(jnp.bfloat16),
            grad_key_raw.reshape(rows_dev, width_k).astype(jnp.bfloat16),
            grad_values.reshape(rows_dev, width_k).astype(jnp.bfloat16),
        ],
        axis=1,
    )
    grad_qkv = jnp.dot(low_in.T, grad_projected, preferred_element_type=jnp.float32)
    grad_normed = jnp.dot(grad_projected, qkv_back.T, preferred_element_type=jnp.float32)
    unused_in, in_back = jax.vjp(rms_scale, inputs, attn_back_g.astype(jnp.float32))
    grad_in_part, grad_attn_gain = in_back(grad_normed)
    grad_tokens = grad_mixed + grad_in_part
    gradients = (grad_qkv, grad_out, grad_router, grad_attn_gain, grad_moe_gain)
    pieces = (
        lax.psum_scatter(gradients[0], "fsdp", scatter_dimension=0, tiled=True),
        lax.psum_scatter(gradients[1], "fsdp", scatter_dimension=0, tiled=True),
        lax.psum_scatter(gradients[2], "fsdp", scatter_dimension=0, tiled=True),
        lax.psum_scatter(gradients[3], "fsdp", scatter_dimension=0, tiled=True),
        lax.psum_scatter(gradients[4], "fsdp", scatter_dimension=0, tiled=True),
    )
    reduced = (
        lax.psum(pieces[0].astype(jnp.bfloat16), "ctx").astype(jnp.float32),
        lax.psum(pieces[1].astype(jnp.bfloat16), "ctx").astype(jnp.float32),
        lax.psum(pieces[2].astype(jnp.bfloat16), "ctx").astype(jnp.float32),
        lax.psum(pieces[3].astype(jnp.bfloat16), "ctx").astype(jnp.float32),
        lax.psum(pieces[4].astype(jnp.bfloat16), "ctx").astype(jnp.float32),
    )
    gain_sums = lax.psum((grad_query_gain, grad_key_gain), ("fsdp", "ctx"))
    return (
        output,
        grad_tokens,
        reduced[0],
        reduced[1],
        reduced[2],
        reduced[3],
        reduced[4],
        gain_sums[0],
        gain_sums[1],
        grad_gate_up,
        grad_down,
    )


low = jnp.bfloat16
full = jnp.float32
plain = (((1,), (0,)), ((), ()))
rhs_turned = (((1,), (1,)), ((), ()))
lhs_turned = (((0,), (0,)), ((), ()))
vmem_bytes = 58 << 20


def mul(left, right, dims=plain):
    return lax.dot_general(left, right, dims, preferred_element_type=full)


def core_pairs(fsdp):
    return [(i, i ^ 1) for i in range(fsdp)]


def side_pairs(fsdp):
    return [(i, i ^ 2) for i in range(fsdp)]


def swap_core(values):
    return lax.ppermute(values, "fsdp", core_pairs(lax.axis_size("fsdp")))


def swap_side(values):
    return lax.ppermute(values, "fsdp", side_pairs(lax.axis_size("fsdp")))


def swap_ctx(values):
    return lax.ppermute(values, "ctx", [(0, 1), (1, 0)])


def add_low(one, two):
    return (one.astype(full) + two.astype(full)).astype(low)


def hold(values, first):
    return lax.optimization_barrier((values, first))


def take(values, index):
    return lax.dynamic_index_in_dim(values, index, 0, keepdims=False)


def line_shift(values, step):
    fsdp = lax.axis_size("fsdp")
    return lax.ppermute(values, "fsdp", [(i, (i + 4 * step) % fsdp) for i in range(fsdp)])


def line_total(own, arrived):
    total = own.astype(full)
    for item in arrived.values():
        total = total + item.astype(full)
    return total


def line_first(entries, place):
    fsdp = lax.axis_size("fsdp")
    even = place % 2 == 0
    one, two = jnp.where(even, entries[3], entries[1]), jnp.where(even, entries[1], entries[3])
    return [lax.ppermute(item, "fsdp", [(i, i ^ 4) for i in range(fsdp)]) for item in (one, two)]


def line_second(entries, two):
    return lax.ppermute(
        add_low(entries[2], two), "fsdp", [(i, i ^ 8) for i in range(lax.axis_size("fsdp"))]
    )


def joined(places, own, got):
    from_ctx, from_side, one_side, two_ctx = got
    entries = {}
    for at, p in enumerate(places):
        one = add_low(add_low(own[0][at], from_ctx[at]), one_side[at])
        two = add_low(add_low(own[1][at], from_side[at]), two_ctx[at])
        entries[p] = jnp.concatenate([one, two], axis=-1)
    return entries


def over_core(keep, send):
    return keep, swap_core(send)


def pick_sum(parts, start, stop, column):
    keep, other = parts
    half = keep.shape[-1] // 2
    cut = (slice(start, stop), slice(None), slice(column * half, (column + 1) * half))
    return add_low(keep[cut], other[cut])


def sum_partners(values, fsdp, steps):
    for step in steps:
        values = values + lax.ppermute(values, "fsdp", [(i, i ^ step) for i in range(fsdp)])
    return values


def sum_owned(values, fsdp, spot):
    items, shard = values.shape[0], values.shape[1] // fsdp
    values = values.reshape(items, fsdp, shard).swapaxes(0, 1)
    step = fsdp // 2
    while step:
        bit = (spot // step) % 2
        values = values.reshape(2, step, items, shard)
        other = lax.ppermute(take(values, 1 - bit), "fsdp", [(i, i ^ step) for i in range(fsdp)])
        values = take(values, bit) + other
        step //= 2
    values = values[0]
    return values + swap_ctx(values)


def turn(values):
    return pltpu.roll(values, values.shape[-1] // 2, 1)


def norm_rope(raw, gain, cosine, sine):
    scale = lax.rsqrt(jnp.mean(raw * raw, axis=-1, keepdims=True) + eps_norm)
    scaled = raw * scale * gain
    return scaled * cosine + turn(scaled) * sine


def norm_rope_back(raw, gain, cosine, sine, grad):
    scale = lax.rsqrt(jnp.mean(raw * raw, axis=-1, keepdims=True) + eps_norm)
    unit = raw * scale
    grad_scaled = grad * cosine - turn(grad) * sine
    grad_gain = jnp.sum(grad_scaled * unit, axis=0, keepdims=True)
    grad_unit = grad_scaled * gain
    grad_raw = scale * (grad_unit - unit * jnp.mean(grad_unit * unit, axis=-1, keepdims=True))
    return grad_raw, grad_gain


def tiles_of(rows):
    step = rows // 2
    return [(start, start + step) for start in range(0, rows, step)]


def allowed(start, stop):
    shape = (stop - start, stop)
    return lax.broadcasted_iota(jnp.int32, shape, 1) <= (
        lax.broadcasted_iota(jnp.int32, shape, 0) + start
    )


def attend_kernel(q_ref, k_ref, v_ref, cos_ref, sin_ref, qg_ref, kg_ref, o_ref, qr_ref, kr_ref, vl_ref):
    head_dim = k_ref.shape[1]
    rows = k_ref.shape[0]
    cosine, sine = cos_ref[...], sin_ref[...]
    keys = norm_rope(k_ref[...], kg_ref[...], cosine, sine).astype(low)
    values = v_ref[...].astype(low)
    kr_ref[...] = keys
    vl_ref[...] = values
    for head in range(q_ref.shape[1] // head_dim):
        cols = slice(head * head_dim, (head + 1) * head_dim)
        query = norm_rope(q_ref[:, cols], qg_ref[...], cosine, sine).astype(low)
        qr_ref[:, cols] = query
        for start, stop in tiles_of(rows):
            scores = mul(query[start:stop], keys[:stop], rhs_turned) * (1.0 / math.sqrt(head_dim))
            expo = jnp.where(allowed(start, stop), jnp.exp(scores), 0.0)
            probs = (expo / jnp.sum(expo, axis=-1, keepdims=True)).astype(low)
            o_ref[start:stop, cols] = mul(probs, values[:stop]).astype(low)


def attend_grad_kernel(
    q_ref, k_ref, qr_ref, kr_ref, vl_ref, go_ref, cos_ref, sin_ref, qg_ref, kg_ref,
    dq_ref, dk_ref, dv_ref, dqg_ref, dkg_ref, dk_sum, dv_sum, dq_sum,
):
    head_dim = k_ref.shape[1]
    rows = k_ref.shape[0]
    root = 1.0 / math.sqrt(head_dim)
    cosine, sine = cos_ref[...], sin_ref[...]
    keys, values = kr_ref[...], vl_ref[...]
    gain_sum = jnp.zeros((1, head_dim), full)
    dk_sum[...] = jnp.zeros_like(dk_sum)
    dv_sum[...] = jnp.zeros_like(dv_sum)
    for head in range(q_ref.shape[1] // head_dim):
        cols = slice(head * head_dim, (head + 1) * head_dim)
        for start, stop in tiles_of(rows):
            query = qr_ref[start:stop, cols]
            grad = go_ref[start:stop, cols]
            scores = mul(query, keys[:stop], rhs_turned) * root
            expo = jnp.where(allowed(start, stop), jnp.exp(scores), 0.0)
            probs = expo / jnp.sum(expo, axis=-1, keepdims=True)
            grad_probs = mul(grad, values[:stop], rhs_turned)
            delta = jnp.sum(grad_probs * probs, axis=-1, keepdims=True)
            grad_scores = (probs * (grad_probs - delta)).astype(low)
            dv_sum[:stop] += mul(probs.astype(low), grad, lhs_turned)
            dk_sum[:stop] += mul(grad_scores, query, lhs_turned)
            dq_sum[start:stop] = mul(grad_scores, keys[:stop])
        grad_query = (dq_sum[...] * root).astype(low).astype(full)
        grad_raw, grad_gain = norm_rope_back(q_ref[:, cols], qg_ref[...], cosine, sine, grad_query)
        dq_ref[:, cols] = grad_raw.astype(low)
        gain_sum = gain_sum + grad_gain
    dqg_ref[0] = gain_sum
    grad_key = (dk_sum[...] * root).astype(low).astype(full)
    grad_raw, grad_gain = norm_rope_back(k_ref[...], kg_ref[...], cosine, sine, grad_key)
    dk_ref[...] = grad_raw.astype(low)
    dkg_ref[0] = grad_gain
    dv_ref[...] = dv_sum[...].astype(low)


def attention_specs(rows, head_dim, kv_heads, group):
    wide, narrow = group * head_dim, head_dim
    heads_end = kv_heads * group
    return dict(
        q=pl.BlockSpec((rows, wide), lambda i: (0, i)),
        k=pl.BlockSpec((rows, narrow), lambda i: (0, heads_end + i)),
        v=pl.BlockSpec((rows, narrow), lambda i: (0, heads_end + kv_heads + i)),
        own=pl.BlockSpec((rows, narrow), lambda i: (0, i)),
        table=pl.BlockSpec((rows, head_dim), lambda i: (0, 0)),
        gain=pl.BlockSpec((1, head_dim), lambda i: (0, 0)),
        gain_out=pl.BlockSpec((1, 1, head_dim), lambda i: (i, 0, 0)),
    )


def attend(projected, cosine, sine, query_gain, key_gain, kv_heads, group):
    rows, head_dim = cosine.shape
    s = attention_specs(rows, head_dim, kv_heads, group)
    shape = jax.ShapeDtypeStruct
    work = rows * rows * head_dim * kv_heads * group
    return pl.pallas_call(
        attend_kernel,
        grid=(kv_heads,),
        in_specs=[s["q"], s["k"], s["v"], s["table"], s["table"], s["gain"], s["gain"]],
        out_specs=[s["q"], s["q"], s["own"], s["own"]],
        out_shape=[
            shape((rows, kv_heads * group * head_dim), low),
            shape((rows, kv_heads * group * head_dim), low),
            shape((rows, kv_heads * head_dim), low),
            shape((rows, kv_heads * head_dim), low),
        ],
        compiler_params=pltpu.CompilerParams(vmem_limit_bytes=48 << 20),
        cost_estimate=pl.CostEstimate(
            flops=4 * work, bytes_accessed=projected.size * 6, transcendentals=work // head_dim
        ),
        name="attend",
    )(projected, projected, projected, cosine, sine, query_gain, key_gain)


def attend_grad(projected, roped_q, roped_k, values_low, grad, cosine, sine, query_gain, key_gain, kv_heads, group):
    rows, head_dim = cosine.shape
    s = attention_specs(rows, head_dim, kv_heads, group)
    shape = jax.ShapeDtypeStruct
    work = rows * rows * head_dim * kv_heads * group
    return pl.pallas_call(
        attend_grad_kernel,
        grid=(kv_heads,),
        in_specs=[
            s["q"], s["k"], s["q"], s["own"], s["own"], s["q"],
            s["table"], s["table"], s["gain"], s["gain"],
        ],
        out_specs=[s["q"], s["own"], s["own"], s["gain_out"], s["gain_out"]],
        out_shape=[
            shape((rows, kv_heads * group * head_dim), low),
            shape((rows, kv_heads * head_dim), low),
            shape((rows, kv_heads * head_dim), low),
            shape((kv_heads, 1, head_dim), full),
            shape((kv_heads, 1, head_dim), full),
        ],
        scratch_shapes=[pltpu.VMEM((rows, head_dim), full)] * 3,
        compiler_params=pltpu.CompilerParams(vmem_limit_bytes=48 << 20),
        cost_estimate=pl.CostEstimate(
            flops=10 * work, bytes_accessed=projected.size * 10, transcendentals=work // head_dim
        ),
        name="attend_grad",
    )(projected, projected, roped_q, roped_k, values_low, grad, cosine, sine, query_gain, key_gain)


def placed(gate, slots):
    block = gate.shape[1]
    shape = (block, block)
    earlier = (
        lax.broadcasted_iota(jnp.int32, shape, 0) < lax.broadcasted_iota(jnp.int32, shape, 1)
    ).astype(low)
    hit = jnp.where(gate >= 0.0, 1.0, 0.0)
    count = mul(jnp.broadcast_to(hit, (8, block)).astype(low), earlier)[:1].astype(jnp.int32)
    place = (lax.broadcasted_iota(jnp.int32, (slots, block), 0) == count) & (hit > 0.5)
    weight = jnp.sum(jnp.where(place, gate, 0.0), axis=1, keepdims=True)
    return place, place.astype(full).astype(low), weight


def expert_kernel(core_ref, order, m_ref, g_ref, far_ref, w_ref, gu_ref, dn_ref, *refs):
    keep_back, send_back, gate_back, rows_ref, dy_ref, z_ref, pair_ref = refs[-7:]
    core = core_ref[0]
    far = order[4 * pl.program_id(0) + 2] == 1
    width = m_ref.shape[4]
    hidden = dn_ref.shape[0]
    slots = z_ref.shape[0] // 2
    places, picks, weights, rows, grads = [], [], [], [], []
    for part in range(2):
        at = lax.rem(core + part, 2)
        place, pick, weight = placed(w_ref[0, at, 0], slots)
        places.append(place)
        picks.append(pick)
        weights.append(weight)
        rows.append(mul(pick, m_ref[0, at, 0]).astype(low))
        near_rows = g_ref[0, at, :, :width]
        far_rows = jnp.concatenate([far_ref[0, at], g_ref[0, at, :, width:]], axis=1)
        grads.append(mul(pick, jnp.where(far, far_rows, near_rows)).astype(low))
    row, grad, weight = (jnp.concatenate(items, axis=0) for items in (rows, grads, weights))
    rows_ref[...] = row
    paired = mul(row, gu_ref[...])
    gate_in, up = paired[:, :hidden], paired[:, hidden:]
    sig = jax.nn.sigmoid(gate_in)
    act = gate_in * sig
    z = (act * up).astype(low)
    z_ref[...] = z
    dy_ref[...] = (weight * grad.astype(full)).astype(low)
    unweighted = mul(grad, dn_ref[...], rhs_turned)
    grad_gate = jnp.sum(unweighted * z.astype(full), axis=1, keepdims=True)
    dz = weight * unweighted
    grad_in = dz * up * (sig * (1.0 + gate_in * (1.0 - sig)))
    pair = jnp.concatenate([grad_in, dz * act], axis=1).astype(low)
    pair_ref[...] = pair
    back = mul(pair, gu_ref[...], rhs_turned).astype(low)
    for part, out in enumerate((keep_back, send_back)):
        mine = slice(part * slots, (part + 1) * slots)
        out[0] = mul(picks[part], back[mine], lhs_turned).astype(low)
        gate_back[0, lax.rem(core + part, 2), 0] = jnp.sum(
            jnp.where(places[part], grad_gate[mine], 0.0), axis=0, keepdims=True
        )


def run_expert(core, order, first, total_steps, m_all, g_all, g_far, gates_all, gate_up, down, slots, kept):
    places, _, _, block, width = m_all.shape
    paired = gate_up.shape[1]
    steps = order.shape[0] // 4
    part_rows = steps * 2 * slots
    hidden = paired // 2
    shape = jax.ShapeDtypeStruct

    def gates_at(i, core, order):
        return (order[4 * i], 0, order[4 * i + 1], 0, 0)

    def token_at(i, core, order):
        return (order[4 * i], 0, order[4 * i + 2], 0, 0)

    def near_at(i, core, order):
        return (order[4 * i], 0, 0, 0)

    def far_at(i, core, order):
        return (order[4 * i + 3], 0, 0, 0)

    def fixed(i, core, order):
        return (0, 0)

    def flat(i, core, order):
        return (first + i, 0)

    def stacked(i, core, order):
        return (i, 0, 0)

    small = pl.BlockSpec((1, 2, 1, 1, block), gates_at)
    one_block = pl.BlockSpec((1, block, width), stacked)
    widths = (width, width, hidden, paired)
    grid_spec = pltpu.PrefetchScalarGridSpec(
        num_scalar_prefetch=2,
        grid=(steps,),
        in_specs=[
            pl.BlockSpec((1, 2, 1, block, width), token_at),
            pl.BlockSpec((1, 2, block, g_all.shape[3]), near_at),
            pl.BlockSpec((1, 2, block, g_far.shape[3]), far_at),
            small,
            pl.BlockSpec(gate_up.shape, fixed, pipeline_mode=pl.Buffered(1)),
            pl.BlockSpec(down.shape, fixed, pipeline_mode=pl.Buffered(1)),
        ]
        + [pl.BlockSpec(memory_space=pl.ANY)] * (0 if kept is None else 5),
        out_specs=[one_block] * 2 + [small] + [pl.BlockSpec((2 * slots, n), flat) for n in widths],
    )
    return pl.pallas_call(
        expert_kernel,
        grid_spec=grid_spec,
        out_shape=[shape((steps, block, width), low)] * 2
        + [shape((places, 2, 2, 1, block), full)]
        + [shape((total_steps * 2 * slots, n), low) for n in widths],
        input_output_aliases={} if kept is None else {8 + i: 2 + i for i in range(5)},
        compiler_params=pltpu.CompilerParams(vmem_limit_bytes=vmem_bytes),
        cost_estimate=pl.CostEstimate(
            flops=part_rows * width * (4 * paired + 2 * hidden + 6 * block),
            bytes_accessed=steps * block * width * 12 + part_rows * (width * 4 + paired * 3),
            transcendentals=part_rows * hidden,
        ),
        name="experts",
    )(core, order, m_all, g_all, g_far, gates_all, gate_up, down, *(() if kept is None else kept))


def result_kernel(core_ref, order, z_ref, w_ref, dn_ref, keep_out, send_out):
    core = core_ref[0]
    slots = z_ref.shape[0] // 2
    y = mul(z_ref[...], dn_ref[...]).astype(low).astype(full)
    for part, out in enumerate((keep_out, send_out)):
        _, pick, weight = placed(w_ref[0, lax.rem(core + part, 2), 0], slots)
        scaled = (weight * y[part * slots : (part + 1) * slots]).astype(low)
        out[0] = mul(pick, scaled, lhs_turned).astype(low)


def run_result(core, order, first, hidden, gates_all, down, slots):
    block, width, inner = gates_all.shape[4], down.shape[1], down.shape[0]
    steps = order.shape[0] // 4
    one_block = pl.BlockSpec((1, block, width), lambda i, core, order: (i, 0, 0))
    return pl.pallas_call(
        result_kernel,
        grid_spec=pltpu.PrefetchScalarGridSpec(
            num_scalar_prefetch=2,
            grid=(steps,),
            in_specs=[
                pl.BlockSpec((2 * slots, inner), lambda i, core, order: (first + i, 0)),
                pl.BlockSpec(
                    (1, 2, 1, 1, block), lambda i, core, order: (order[4 * i], 0, order[4 * i + 1], 0, 0)
                ),
                pl.BlockSpec(down.shape, lambda i, core, order: (0, 0), pipeline_mode=pl.Buffered(1)),
            ],
            out_specs=[one_block] * 2,
        ),
        out_shape=[jax.ShapeDtypeStruct((steps, block, width), low)] * 2,
        compiler_params=pltpu.CompilerParams(vmem_limit_bytes=vmem_bytes),
        cost_estimate=pl.CostEstimate(
            flops=steps * 2 * slots * width * (2 * inner + 2 * block),
            bytes_accessed=steps * (4 * block * width + 4 * slots * inner) + 2 * inner * width,
            transcendentals=0,
        ),
        name="results",
    )(core, order, hidden, gates_all, down)


def own_heads_kernel(rank, qkv_ref, out_ref, o_ref, *, head_dim, heads):
    first = rank[0] == 0
    for head in range(heads):
        pair = [qkv_ref[:, (2 * head + i) * head_dim : (2 * head + i + 1) * head_dim] for i in range(2)]
        o_ref[:, head * head_dim : (head + 1) * head_dim] = jnp.where(first, pair[0], pair[1])
    kv = qkv_ref.shape[1] - 2 * heads * head_dim
    o_ref[:, heads * head_dim : heads * head_dim + kv] = qkv_ref[:, 2 * heads * head_dim :]
    o_ref[:, heads * head_dim + kv :] = jnp.where(first, out_ref[:head_dim], out_ref[head_dim:])


def own_heads(rank, qkv_weight, out_weight, head_dim, heads):
    kv = qkv_weight.shape[1] - 2 * heads * head_dim
    return pl.pallas_call(
        functools.partial(own_heads_kernel, head_dim=head_dim, heads=heads),
        grid_spec=pltpu.PrefetchScalarGridSpec(
            num_scalar_prefetch=1,
            grid=(1,),
            in_specs=[
                pl.BlockSpec(qkv_weight.shape, lambda i, rank: (0, 0)),
                pl.BlockSpec(out_weight.shape, lambda i, rank: (0, 0)),
            ],
            out_specs=pl.BlockSpec(
                (qkv_weight.shape[0], heads * head_dim + kv + out_weight.shape[1]), lambda i, rank: (0, 0)
            ),
        ),
        out_shape=jax.ShapeDtypeStruct(
            (qkv_weight.shape[0], heads * head_dim + kv + out_weight.shape[1]), qkv_weight.dtype
        ),
        name="own_heads",
    )(rank, qkv_weight, out_weight)


def all_heads_kernel(rank, mine_ref, other_ref, o_ref, *, head_dim, heads):
    first = rank[0] == 0
    for head in range(heads):
        cols = slice(head * head_dim, (head + 1) * head_dim)
        mine, other = mine_ref[:, cols].astype(full), other_ref[:, cols].astype(full)
        o_ref[:, 2 * head * head_dim : (2 * head + 1) * head_dim] = jnp.where(first, mine, other)
        o_ref[:, (2 * head + 1) * head_dim : (2 * head + 2) * head_dim] = jnp.where(first, other, mine)
    o_ref[:, 2 * heads * head_dim :] = mine_ref[:, heads * head_dim :].astype(full) + other_ref[
        :, heads * head_dim :
    ].astype(full)


def all_heads(rank, mine, other, head_dim, heads):
    rows, width = mine.shape
    return pl.pallas_call(
        functools.partial(all_heads_kernel, head_dim=head_dim, heads=heads),
        grid_spec=pltpu.PrefetchScalarGridSpec(
            num_scalar_prefetch=1,
            grid=(1,),
            in_specs=[pl.BlockSpec((rows, width), lambda i, rank: (0, 0))] * 2,
            out_specs=pl.BlockSpec((rows, width + heads * head_dim), lambda i, rank: (0, 0)),
        ),
        out_shape=jax.ShapeDtypeStruct((rows, width + heads * head_dim), full),
        name="all_heads",
    )(rank, mine, other)


def rms_back(values, gain, grad):
    scale = lax.rsqrt(jnp.mean(values * values, axis=-1, keepdims=True) + eps_norm)
    unit = values * scale
    grad_gain = jnp.sum(grad * unit, axis=0)
    grad_unit = grad * gain
    back = scale * (grad_unit - unit * jnp.mean(grad_unit * unit, axis=-1, keepdims=True))
    return back, grad_gain


def in_order(first, second):
    half = first.shape[0] // 2
    return jnp.concatenate([first[:half], second, first[half:]], axis=0)


def of_block(values, rank):
    quarter = values.shape[0] // 4
    outer = jnp.concatenate([values[:quarter], values[3 * quarter :]], axis=0)
    return jnp.where(rank == 0, outer, values[quarter : 3 * quarter])


def body_gathered(
    tokens, qkv_weight, out_weight, router_weight, attn_gain, moe_gain, query_gain, key_gain,
    expert_gate_up, expert_down, routes, cotangent,
):
    rows_dev, width = tokens.shape
    head_dim = query_gain.shape[0]
    top_k = routes.shape[1]
    fsdp = lax.axis_size("fsdp")
    spot = lax.axis_index("fsdp")
    rank = lax.axis_index("ctx")
    place, side, core = spot // 4, (spot // 2) % 2, spot % 2
    shard = qkv_weight.shape[0]
    heads = out_weight.shape[0] * fsdp // head_dim
    kv_heads = (qkv_weight.shape[1] // head_dim - heads) // 2
    group = heads // kv_heads // 2
    my_heads = heads // 2
    width_q, width_k = my_heads * head_dim, kv_heads * head_dim
    experts_all = router_weight.shape[1]
    capacity = 2 * rows_dev * top_k // experts_all
    both = ("fsdp", "ctx")

    def sequence(values):
        other = swap_ctx(values)
        first = jnp.where(rank == 0, values, other)
        second = jnp.where(rank == 0, other, values)
        return in_order(first, second)

    rank_at = rank[None].astype(jnp.int32)
    weights_local = own_heads(rank_at, qkv_weight, out_weight, head_dim, my_heads)
    small_local = jnp.concatenate([router_weight, attn_gain[:, None], moe_gain[:, None]], axis=1)
    small_all = lax.all_gather(small_local, "fsdp", axis=0, tiled=True)
    weights_all = lax.all_gather(weights_local, "fsdp", axis=0, tiled=True)
    qkv_all = weights_all[:, : width_q + 2 * width_k]
    out_all = weights_all[:, width_q + 2 * width_k :]
    router_all = small_all[:, :experts_all]
    attn_all = small_all[:, experts_all].astype(full)
    moe_all = small_all[:, experts_all + 1].astype(full)
    late_cols = width * 7 // 16
    g_all = lax.all_gather(
        jnp.concatenate([cotangent, swap_ctx(cotangent[:, late_cols:])], axis=1), "fsdp", axis=0, tiled=True
    ).reshape(fsdp // 2, 2, rows_dev, 2 * width - late_cols)

    sequence_in = sequence(tokens).astype(full)
    low_in = rms_scale(sequence_in, attn_all).astype(low)
    projected = mul(low_in, qkv_all)
    cosine, sine = (t[:, 0] for t in angles(jnp.arange(2 * rows_dev, dtype=jnp.int32), head_dim))
    sine = jnp.concatenate([-sine[:, : head_dim // 2], sine[:, head_dim // 2 :]], axis=1)
    gain_q, gain_k = query_gain.astype(full)[None], key_gain.astype(full)[None]
    attended, roped_q, roped_k, values_low = attend(
        projected, cosine, sine, gain_q, gain_k, kv_heads, group
    )
    branch = mul(attended, out_all)
    inputs = tokens.astype(full)
    mixed = (
        inputs
        + of_block(branch, rank)
        + swap_ctx(of_block(branch, 1 - rank).astype(low)).astype(full)
    )
    low_mid = rms_scale(mixed, moe_all).astype(low)
    m_all = lax.all_gather(jnp.concatenate([low_mid, swap_ctx(low_mid)]), "fsdp", axis=0, tiled=True)

    logits = mul(low_mid, router_all)
    named = routes[:, :, None] == jnp.arange(experts_all, dtype=jnp.int32)[None, None, :]
    selected = jnp.sum(jnp.where(named, logits[:, None, :], 0.0), axis=2)
    gates = gating(selected)
    chosen = jnp.any(named, axis=1)
    gates_wide = jnp.sum(jnp.where(named, gates[:, :, None], 0.0), axis=1)
    gates_sent = jnp.where(chosen, gates_wide, -1.0).T
    gates_all = lax.all_to_all(gates_sent, both, split_axis=0, concat_axis=0, tiled=True)

    g_all, gates_all = hold(g_all, gates_all)
    g_far = swap_ctx(g_all[..., :late_cols])

    lines = fsdp // 4
    places = list(range(1, lines)) + [0]
    cut = lines // 2
    parts = [places[:cut], places[cut:]]
    m_all = m_all.reshape(fsdp // 2, 2, 2, rows_dev, width)
    gates_all = gates_all.reshape(fsdp // 2, 2, 2, 1, rows_dev)
    state = dict(kept=None, first=0, core=core[None].astype(jnp.int32))

    def order_of(steps):
        spots = [((place - p) % lines) * 2 + (side + d) % 2 for d, _, p in steps]
        far = [i for i, step in enumerate(steps) if step[1] == 1] or [0]
        return jnp.stack(
            [
                jnp.asarray(item, jnp.int32)
                for i, step in enumerate(steps)
                for item in (
                    spots[i],
                    (rank + step[1]) % 2,
                    step[1],
                    spots[min(far, key=lambda j, i=i: abs(j - i))],
                )
            ]
        )

    def call(steps, raw=False):
        keep_back, send_back, *kept = run_expert(
            state["core"],
            order_of(steps),
            state["first"],
            4 * lines,
            m_all,
            g_all,
            g_far,
            gates_all,
            expert_gate_up[0],
            expert_down[0],
            capacity,
            state["kept"],
        )
        state["kept"] = kept
        state["first"] += len(steps)
        return (keep_back, send_back) if raw else over_core(keep_back, send_back)

    def wait(first):
        state["core"], first = hold(state["core"], first)
        return first

    steps_far, steps_own = ([(d, d, p) for p in places] for d in (1, 0))
    steps_mixed = [[(1, 0, p) for p in part] + [(0, 1, p) for p in part] for part in parts]
    back = call(steps_far)
    far_one, far_two = wait([pick_sum(back, 0, lines, column) for column in range(2)])
    far_one, far_two = swap_ctx(far_one), swap_side(far_two)

    def mixed_sums(back, at=0):
        return [
            pick_sum(back, start, start + cut, column) for start in (at, at + cut) for column in range(2)
        ]

    def rounds(sums, part):
        side_one, side_two, ctx_one, ctx_two = sums
        span = slice(part * cut, (part + 1) * cut)
        return [
            swap_ctx(ctx_one),
            swap_side(side_two),
            swap_side(add_low(side_one, far_one[span])),
            swap_ctx(add_low(ctx_two, far_two[span])),
        ]

    keep, send = call(steps_mixed[0], raw=True)
    send, (far_one, far_two) = hold(send, (far_one, far_two))
    back = over_core(keep, send)
    back_own = call(steps_own)
    sums = wait(mixed_sums(back))
    back_own = [pick_sum(back_own, 0, lines, column) for column in range(2)]
    got = rounds(sums, 0)
    keep, send = call(steps_mixed[1], raw=True)
    send, got = hold(send, got)
    back = over_core(keep, send)
    entries = joined(parts[0], [item[:cut] for item in back_own], got)
    arrived = {p: line_shift(entries[p], lines - p) for p in parts[0]}
    gate_back, rows, grad_rows, hidden, grad_pair = state["kept"]
    hidden, sums = hold(hidden, mixed_sums(back))
    got = rounds(sums, 1)
    grad_gates = lax.all_to_all(
        gate_back.reshape(fsdp * 2, rows_dev), both, split_axis=0, concat_axis=0, tiled=True
    ).T
    def results(first, steps, hidden):
        return run_result(
            state["core"], order_of(steps), first, hidden, gates_all, expert_down[0], capacity
        )

    out_far = results(0, steps_far, hidden)
    out_rest = results(lines, steps_mixed[0] + steps_own + steps_mixed[1], hidden)
    got, out_far, out_rest, arrived, grad_gates = lax.optimization_barrier(
        (got, out_far, out_rest, arrived, grad_gates)
    )
    entries.update(joined(parts[1], [item[cut:] for item in back_own], got))
    out_far = over_core(*out_far)
    out_far = [pick_sum(out_far, 0, lines, 0), swap_side(pick_sum(out_far, 0, lines, 1))]
    out_rest = over_core(*out_rest)
    for p in parts[1][:-1]:
        arrived[p] = line_shift(entries[p], lines - p)
    grad_mid = line_total(entries[0], arrived)

    grad_wide = jnp.where(chosen, grad_gates, 0.0)
    grad_logits = (
        gates_wide * (grad_wide - jnp.sum(gates_wide * grad_wide, axis=1, keepdims=True))
    ).astype(low)
    grad_router = mul(low_mid, grad_logits, lhs_turned)
    grad_mid = grad_mid + mul(grad_logits, router_all, rhs_turned)
    grad_mixed_part, grad_moe_gain = rms_back(mixed, moe_all, grad_mid)
    grad_mixed = cotangent.astype(full) + grad_mixed_part

    low_mixed, (out_far[0], out_rest) = hold(grad_mixed.astype(low), (out_far[0], out_rest))
    grad_branch = sequence(low_mixed)
    out_sums = [
        jnp.concatenate([one, two])
        for one, two in zip(mixed_sums(out_rest), mixed_sums(out_rest, 2 * cut + lines))
    ]
    out_own = [pick_sum(out_rest, 2 * cut, 2 * cut + lines, column) for column in range(2)]
    (out_far[0], out_sums, out_own), grad_branch = hold((out_far[0], out_sums, out_own), grad_branch)
    side_one, side_two, ctx_one, ctx_two = out_sums
    out_far[0] = swap_ctx(out_far[0])
    grad_attended = mul(grad_branch, out_all, rhs_turned).astype(low)
    grad_attended, out_far = hold(grad_attended, out_far)
    got = [
        swap_ctx(ctx_one),
        swap_side(side_two),
        swap_side(add_low(side_one, out_far[0])),
        swap_ctx(add_low(ctx_two, out_far[1])),
    ]
    grad_out_part = mul(attended, grad_branch, lhs_turned).astype(low)
    grad_q, grad_k, grad_v, gain_q_part, gain_k_part = attend_grad(
        projected, roped_q, roped_k, values_low, grad_attended, cosine, sine, gain_q, gain_k, kv_heads, group
    )
    grad_projected = jnp.concatenate([grad_q, grad_k, grad_v], axis=1)
    grad_projected, (got[0], got[1]) = hold(grad_projected, (got[0], got[1]))
    grad_qkv_part = mul(low_in, grad_projected, lhs_turned).astype(low)
    grad_projected, got = hold(grad_projected, got)
    entries = joined(places, out_own, got)
    grad_normed_part = mul(grad_projected, qkv_all, rhs_turned)
    (rows, grad_pair, hidden, grad_rows), entries = hold((rows, grad_pair, hidden, grad_rows), entries)
    one, two = line_first(entries, place)
    grad_gate_up = mul(rows, grad_pair, lhs_turned)[None]
    grad_down = mul(hidden, grad_rows, lhs_turned)[None]
    grad_normed = of_block(grad_normed_part, rank) + swap_ctx(
        of_block(grad_normed_part, 1 - rank).astype(low)
    ).astype(full)
    grad_in_part, grad_attn_gain = rms_back(inputs, attn_all, grad_normed)
    grad_tokens = grad_mixed + grad_in_part

    out_mine = lax.psum_scatter(grad_out_part, "fsdp", scatter_dimension=0, tiled=True).astype(full)
    out_other = swap_ctx(out_mine.astype(low)).astype(full)
    grad_out = jnp.where(
        rank == 0,
        jnp.concatenate([out_mine, out_other], axis=0),
        jnp.concatenate([out_other, out_mine], axis=0),
    )
    qkv_mine = lax.psum_scatter(grad_qkv_part, "fsdp", scatter_dimension=0, tiled=True)
    grad_qkv = all_heads(rank_at, qkv_mine, swap_ctx(qkv_mine), head_dim, my_heads)
    early, got = hold(jnp.concatenate([grad_router.T, grad_moe_gain[None]], axis=0), got)
    early = sum_owned(early, fsdp, spot)
    late = jnp.concatenate(
        [
            grad_attn_gain.reshape(-1, head_dim),
            jnp.sum(gain_q_part, axis=0),
            jnp.sum(gain_k_part, axis=0),
        ],
        axis=0,
    )
    late, (one, two, grad_gate_up, grad_down) = hold(late, (one, two, grad_gate_up, grad_down))
    far = line_second(entries, two)
    late = late + swap_ctx(late)
    late, far = hold(sum_partners(late, fsdp, (1, 2)), far)
    output = (mixed + entries[0].astype(full) + one.astype(full) + far.astype(full)).astype(low)
    late = sum_partners(late, fsdp, (4, 8))
    gain_rows = width // head_dim
    return (
        output,
        grad_tokens,
        grad_qkv,
        grad_out,
        early[:experts_all].T,
        lax.dynamic_slice_in_dim(late[:gain_rows].reshape(-1), spot * shard, shard, 0),
        early[experts_all],
        late[gain_rows],
        late[gain_rows + 1],
        grad_gate_up,
        grad_down,
    )


gathered_bytes = 1 << 26


def choose_body(*args):
    tokens, gate_up = args[0], args[8]
    fsdp, ctx = lax.axis_size("fsdp"), lax.axis_size("ctx")
    fits = tokens.size * tokens.dtype.itemsize * fsdp * ctx <= gathered_bytes
    if fits and ctx == 2 and fsdp == 16 and gate_up.shape[0] == 1:
        return body_gathered(*args)
    return body_routed(*args)


def solution(mesh):
    in_specs = (
        P(("fsdp", "ctx"), None),
        P("fsdp", None),
        P("fsdp", None),
        P("fsdp", None),
        P("fsdp"),
        P("fsdp"),
        P(),
        P(),
        P(("fsdp", "ctx"), None, None),
        P(("fsdp", "ctx"), None, None),
        P(("fsdp", "ctx"), None),
        P(("fsdp", "ctx"), None),
    )
    out_specs = (
        P(("fsdp", "ctx"), None),
        P(("fsdp", "ctx"), None),
        P("fsdp", None),
        P("fsdp", None),
        P("fsdp", None),
        P("fsdp"),
        P("fsdp"),
        P(),
        P(),
        P(("fsdp", "ctx"), None, None),
        P(("fsdp", "ctx"), None, None),
    )
    return jax.shard_map(choose_body, mesh=mesh, in_specs=in_specs, out_specs=out_specs, check_vma=False)
```

```python
import functools
import math

import jax
import jax.numpy as jnp
from jax import lax
from jax.experimental import pallas as pl
from jax.experimental.pallas import tpu as pltpu
from jax.sharding import PartitionSpec as P

eps_norm = 1e-06
theta_base = 1000000.0


def rms_scale(values, gain):
    return values * lax.rsqrt(jnp.mean(values * values, axis=-1, keepdims=True) + eps_norm) * gain


def rotate(values, cosine, sine):
    half_width = values.shape[-1] // 2
    turned = jnp.concatenate([-values[..., half_width:], values[..., :half_width]], axis=-1)
    return values * cosine + turned * sine


def angles(positions, width):
    freqs = theta_base ** (-(jnp.arange(width // 2, dtype=jnp.float32) * 2.0) / width)
    phase = positions.astype(jnp.float32)[:, None] * freqs[None, :]
    phase = jnp.concatenate([phase, phase], axis=-1)
    return (jnp.cos(phase)[:, None, :], jnp.sin(phase)[:, None, :])


def device_positions(block_rank, ctx_count, tok_rows):
    half_rows = tok_rows // 2
    within = jnp.arange(tok_rows, dtype=jnp.int32)
    span_id = jnp.where(within < half_rows, block_rank, 2 * ctx_count - 1 - block_rank)
    return span_id * half_rows + within % half_rows


def attend_head(query, keys_in, values_in, causal, scale_root):
    scores = (
        jnp.einsum("tgd,sd->gts", query, keys_in, preferred_element_type=jnp.float32) / scale_root
    )
    expo = jnp.where(causal[None], jnp.exp(scores), 0.0)
    totals = jnp.sum(expo, axis=-1, keepdims=True)
    probs = (expo / totals).astype(jnp.bfloat16)
    attended = jnp.einsum("gts,sd->tgd", probs, values_in, preferred_element_type=jnp.float32)
    return (attended, jnp.log(totals[..., 0]))


def attend_back(query, keys_in, values_in, causal, log_total, grad_attended, scale_root):
    scores = (
        jnp.einsum("tgd,sd->gts", query, keys_in, preferred_element_type=jnp.float32) / scale_root
    )
    probs = jnp.where(causal[None], jnp.exp(scores - log_total[..., None]), 0.0)
    low_probs = probs.astype(jnp.bfloat16)
    grad_values = jnp.einsum(
        "gts,tgd->sd", low_probs, grad_attended, preferred_element_type=jnp.float32
    )
    grad_probs = jnp.einsum(
        "tgd,sd->gts", grad_attended, values_in, preferred_element_type=jnp.float32
    )
    delta_rows = jnp.sum(grad_probs * probs, axis=-1, keepdims=True)
    grad_scores = (probs * (grad_probs - delta_rows)).astype(jnp.bfloat16)
    grad_query = (
        jnp.einsum("gts,sd->tgd", grad_scores, keys_in, preferred_element_type=jnp.float32)
        / scale_root
    )
    grad_keys = (
        jnp.einsum("gts,tgd->sd", grad_scores, query, preferred_element_type=jnp.float32)
        / scale_root
    )
    return (grad_query, grad_keys, grad_values)


def swiglu(paired):
    half_width = paired.shape[-1] // 2
    return jax.nn.silu(paired[..., :half_width]) * paired[..., half_width:]


def gating(selected):
    expo = jnp.exp(selected)
    return expo / jnp.sum(expo, axis=1, keepdims=True)


def body_routed(
    tokens,
    qkv_weight,
    out_weight,
    router_weight,
    attn_gain,
    moe_gain,
    query_gain,
    key_gain,
    expert_gate_up,
    expert_down,
    routes,
    cotangent,
):
    rows_dev, width = tokens.shape
    head_dim = query_gain.shape[0]
    top_k = routes.shape[1]
    ctx_count = lax.axis_size("ctx")
    ctx_rank = lax.axis_index("ctx")
    qkv_all, out_all, router_all, attn_all, moe_all = (
        lax.all_gather(qkv_weight, "fsdp", axis=0, tiled=True),
        lax.all_gather(out_weight, "fsdp", axis=0, tiled=True),
        lax.all_gather(router_weight, "fsdp", axis=0, tiled=True),
        lax.all_gather(attn_gain, "fsdp", axis=0, tiled=True),
        lax.all_gather(moe_gain, "fsdp", axis=0, tiled=True),
    )
    experts_all = router_all.shape[1]
    heads = out_all.shape[0] // head_dim
    kv_heads = (qkv_all.shape[1] // head_dim - heads) // 2
    group_size = heads // kv_heads
    capacity = 2 * rows_dev * top_k // experts_all
    width_q = heads * head_dim
    width_k = kv_heads * head_dim
    scale_root = math.sqrt(head_dim)
    inputs = tokens.astype(jnp.float32)
    normed_in = rms_scale(inputs, attn_all.astype(jnp.float32))
    low_in = normed_in.astype(jnp.bfloat16)
    projected = jnp.dot(low_in, qkv_all, preferred_element_type=jnp.float32)
    query_raw = projected[:, :width_q].reshape(rows_dev, heads, head_dim)
    key_raw = projected[:, width_q : width_q + width_k].reshape(rows_dev, kv_heads, head_dim)
    value_low = (
        projected[:, width_q + width_k :].astype(jnp.bfloat16).reshape(rows_dev, kv_heads, head_dim)
    )
    positions = device_positions(ctx_rank, ctx_count, rows_dev)
    cosine, sine = angles(positions, head_dim)
    query_gain_f = query_gain.astype(jnp.float32)
    key_gain_f = key_gain.astype(jnp.float32)

    def query_rope(values_in, gain):
        return rotate(rms_scale(values_in, gain), cosine, sine)

    query_low = query_rope(query_raw, query_gain_f).astype(jnp.bfloat16)
    key_low = query_rope(key_raw, key_gain_f).astype(jnp.bfloat16)
    keys_all, values_all = (
        lax.all_gather(key_low, "ctx", axis=0, tiled=True),
        lax.all_gather(value_low, "ctx", axis=0, tiled=True),
    )
    key_pos = jnp.concatenate(
        [device_positions(other, ctx_count, rows_dev) for other in range(ctx_count)]
    )
    causal = key_pos[None, :] <= positions[:, None]
    query_heads = query_low.reshape(rows_dev, kv_heads, group_size, head_dim).transpose(1, 0, 2, 3)
    key_heads = keys_all.transpose(1, 0, 2)
    value_heads = values_all.transpose(1, 0, 2)
    attended, log_total = lax.map(
        lambda member: attend_head(member[0], member[1], member[2], causal, scale_root),
        (query_heads, key_heads, value_heads),
    )
    attended_low = attended.transpose(1, 0, 2, 3).reshape(rows_dev, width_q).astype(jnp.bfloat16)
    mixed = inputs + jnp.dot(attended_low, out_all, preferred_element_type=jnp.float32)
    normed_mid = rms_scale(mixed, moe_all.astype(jnp.float32))
    low_mid = normed_mid.astype(jnp.bfloat16)
    logits = jnp.dot(low_mid, router_all, preferred_element_type=jnp.float32)
    selected = jnp.take_along_axis(logits, routes, axis=1)
    gates, gate_back = jax.vjp(gating, selected)
    flat_routes = routes.reshape(-1)
    expert_ids = jnp.arange(experts_all, dtype=jnp.int32)
    hit_table = (flat_routes[:, None] == expert_ids[None, :]).astype(jnp.int32)
    slot_index = jnp.sum(jnp.cumsum(hit_table, axis=0) * hit_table, axis=1) - 1
    target = flat_routes * capacity + slot_index
    pair_count = rows_dev * top_k
    source_pair = (
        jnp.full((experts_all * capacity,), pair_count, jnp.int32)
        .at[target]
        .set(jnp.arange(pair_count, dtype=jnp.int32))
    )
    padded = jnp.concatenate([low_mid, jnp.zeros((1, width), jnp.bfloat16)], axis=0)
    outgoing = padded[source_pair // top_k].reshape(experts_all, capacity, width)
    received = lax.all_to_all(outgoing, ("fsdp", "ctx"), split_axis=0, concat_axis=1, tiled=True)
    gate_and_up = jnp.einsum(
        "esd,edf->esf", received, expert_gate_up, preferred_element_type=jnp.float32
    )
    hidden_val, swiglu_back = jax.vjp(swiglu, gate_and_up)
    hidden_low = hidden_val.astype(jnp.bfloat16)
    result_low = jnp.einsum(
        "esf,efd->esd", hidden_low, expert_down, preferred_element_type=jnp.float32
    ).astype(jnp.bfloat16)
    returned = lax.all_to_all(
        result_low, ("fsdp", "ctx"), split_axis=1, concat_axis=0, tiled=True
    ).reshape(experts_all * capacity, width)
    picked = returned[target].reshape(rows_dev, top_k, width).astype(jnp.float32)
    output = (mixed + jnp.sum(gates[:, :, None] * picked, axis=1)).astype(jnp.bfloat16)
    qkv_back, out_back, router_back, attn_back_g, moe_back_g = (
        qkv_all,
        out_all,
        router_all,
        attn_all,
        moe_all,
    )
    grad_final = cotangent.astype(jnp.float32)
    grad_gates = jnp.sum(grad_final[:, None, :] * picked, axis=2)
    grad_result = (
        (gates[:, :, None] * grad_final[:, None, :]).astype(jnp.bfloat16).reshape(pair_count, width)
    )
    grad_padded = jnp.concatenate([grad_result, jnp.zeros((1, width), jnp.bfloat16)], axis=0)
    grad_outgoing = grad_padded[source_pair].reshape(experts_all, capacity, width)
    grad_received = lax.all_to_all(
        grad_outgoing, ("fsdp", "ctx"), split_axis=0, concat_axis=1, tiled=True
    )
    grad_down = jnp.einsum(
        "esf,esd->efd", hidden_low, grad_received, preferred_element_type=jnp.float32
    )
    grad_hidden = jnp.einsum(
        "esd,efd->esf", grad_received, expert_down, preferred_element_type=jnp.float32
    )
    grad_paired = swiglu_back(grad_hidden)[0].astype(jnp.bfloat16)
    grad_gate_up = jnp.einsum(
        "esd,esf->edf", received, grad_paired, preferred_element_type=jnp.float32
    )
    grad_rows = jnp.einsum(
        "esf,edf->esd", grad_paired, expert_gate_up, preferred_element_type=jnp.float32
    ).astype(jnp.bfloat16)
    grad_returned = lax.all_to_all(
        grad_rows, ("fsdp", "ctx"), split_axis=1, concat_axis=0, tiled=True
    ).reshape(experts_all * capacity, width)
    grad_mid = jnp.sum(
        grad_returned[target].reshape(rows_dev, top_k, width).astype(jnp.float32), axis=1
    )
    grad_selected = gate_back(grad_gates)[0]
    route_table = (routes[:, :, None] == expert_ids[None, None, :]).astype(jnp.float32)
    grad_logits = jnp.sum(route_table * grad_selected[:, :, None], axis=1).astype(jnp.bfloat16)
    grad_router = jnp.dot(low_mid.T, grad_logits, preferred_element_type=jnp.float32)
    grad_mid = grad_mid + jnp.dot(grad_logits, router_back.T, preferred_element_type=jnp.float32)
    unused_mid, mid_back = jax.vjp(rms_scale, mixed, moe_back_g.astype(jnp.float32))
    grad_mixed_part, grad_moe_gain = mid_back(grad_mid)
    grad_mixed = grad_final + grad_mixed_part
    grad_branch = grad_mixed.astype(jnp.bfloat16)
    grad_out = jnp.dot(attended_low.T, grad_branch, preferred_element_type=jnp.float32)
    grad_attended = jnp.dot(grad_branch, out_back.T, preferred_element_type=jnp.float32).astype(
        jnp.bfloat16
    )
    grad_heads = grad_attended.reshape(rows_dev, kv_heads, group_size, head_dim).transpose(
        1, 0, 2, 3
    )
    grad_query_h, grad_key_h, grad_value_h = lax.map(
        lambda member: attend_back(
            member[0], member[1], member[2], causal, member[3], member[4], scale_root
        ),
        (query_heads, key_heads, value_heads, log_total, grad_heads),
    )
    grad_keys, grad_values = (
        lax.psum_scatter(
            grad_key_h.transpose(1, 0, 2).astype(jnp.bfloat16),
            "ctx",
            scatter_dimension=0,
            tiled=True,
        ).astype(jnp.float32),
        lax.psum_scatter(
            grad_value_h.transpose(1, 0, 2).astype(jnp.bfloat16),
            "ctx",
            scatter_dimension=0,
            tiled=True,
        ).astype(jnp.float32),
    )
    grad_query_rot = (
        grad_query_h.transpose(1, 0, 2, 3).reshape(rows_dev, heads, head_dim).astype(jnp.bfloat16)
    )
    grad_query_rot = lax.optimization_barrier(grad_query_rot).astype(jnp.float32)
    grad_key_rot = lax.optimization_barrier(grad_keys.astype(jnp.bfloat16)).astype(jnp.float32)
    unused_query, query_back = jax.vjp(query_rope, query_raw, query_gain_f)
    grad_query_raw, grad_query_gain = query_back(grad_query_rot)
    unused_key, key_back = jax.vjp(query_rope, key_raw, key_gain_f)
    grad_key_raw, grad_key_gain = key_back(grad_key_rot)
    grad_projected = jnp.concatenate(
        [
            grad_query_raw.reshape(rows_dev, width_q).astype(jnp.bfloat16),
            grad_key_raw.reshape(rows_dev, width_k).astype(jnp.bfloat16),
            grad_values.reshape(rows_dev, width_k).astype(jnp.bfloat16),
        ],
        axis=1,
    )
    grad_qkv = jnp.dot(low_in.T, grad_projected, preferred_element_type=jnp.float32)
    grad_normed = jnp.dot(grad_projected, qkv_back.T, preferred_element_type=jnp.float32)
    unused_in, in_back = jax.vjp(rms_scale, inputs, attn_back_g.astype(jnp.float32))
    grad_in_part, grad_attn_gain = in_back(grad_normed)
    grad_tokens = grad_mixed + grad_in_part
    gradients = (grad_qkv, grad_out, grad_router, grad_attn_gain, grad_moe_gain)
    pieces = (
        lax.psum_scatter(gradients[0], "fsdp", scatter_dimension=0, tiled=True),
        lax.psum_scatter(gradients[1], "fsdp", scatter_dimension=0, tiled=True),
        lax.psum_scatter(gradients[2], "fsdp", scatter_dimension=0, tiled=True),
        lax.psum_scatter(gradients[3], "fsdp", scatter_dimension=0, tiled=True),
        lax.psum_scatter(gradients[4], "fsdp", scatter_dimension=0, tiled=True),
    )
    reduced = (
        lax.psum(pieces[0].astype(jnp.bfloat16), "ctx").astype(jnp.float32),
        lax.psum(pieces[1].astype(jnp.bfloat16), "ctx").astype(jnp.float32),
        lax.psum(pieces[2].astype(jnp.bfloat16), "ctx").astype(jnp.float32),
        lax.psum(pieces[3].astype(jnp.bfloat16), "ctx").astype(jnp.float32),
        lax.psum(pieces[4].astype(jnp.bfloat16), "ctx").astype(jnp.float32),
    )
    gain_sums = lax.psum((grad_query_gain, grad_key_gain), ("fsdp", "ctx"))
    return (
        output,
        grad_tokens,
        reduced[0],
        reduced[1],
        reduced[2],
        reduced[3],
        reduced[4],
        gain_sums[0],
        gain_sums[1],
        grad_gate_up,
        grad_down,
    )


low = jnp.bfloat16
full = jnp.float32
plain = (((1,), (0,)), ((), ()))
rhs_turned = (((1,), (1,)), ((), ()))
lhs_turned = (((0,), (0,)), ((), ()))
vmem_bytes = 58 << 20


def mul(left, right, dims=plain):
    return lax.dot_general(left, right, dims, preferred_element_type=full)


def core_pairs(fsdp):
    return [(i, i ^ 1) for i in range(fsdp)]


def side_pairs(fsdp):
    return [(i, i ^ 2) for i in range(fsdp)]


def swap_core(values):
    return lax.ppermute(values, "fsdp", core_pairs(lax.axis_size("fsdp")))


def swap_side(values):
    return lax.ppermute(values, "fsdp", side_pairs(lax.axis_size("fsdp")))


def swap_ctx(values):
    return lax.ppermute(values, "ctx", [(0, 1), (1, 0)])


def add_low(one, two):
    return (one.astype(full) + two.astype(full)).astype(low)


def hold(values, first):
    return lax.optimization_barrier((values, first))


def take(values, index):
    return lax.dynamic_index_in_dim(values, index, 0, keepdims=False)


def line_shift(values, step):
    fsdp = lax.axis_size("fsdp")
    return lax.ppermute(values, "fsdp", [(i, (i + 4 * step) % fsdp) for i in range(fsdp)])


def line_total(own, arrived):
    total = own.astype(full)
    for item in arrived.values():
        total = total + item.astype(full)
    return total


def line_first(entries, place):
    fsdp = lax.axis_size("fsdp")
    even = place % 2 == 0
    one, two = jnp.where(even, entries[3], entries[1]), jnp.where(even, entries[1], entries[3])
    return [lax.ppermute(item, "fsdp", [(i, i ^ 4) for i in range(fsdp)]) for item in (one, two)]


def line_second(entries, two):
    return lax.ppermute(
        add_low(entries[2], two), "fsdp", [(i, i ^ 8) for i in range(lax.axis_size("fsdp"))]
    )


def joined(places, own, got):
    from_ctx, from_side, one_side, two_ctx = got
    entries = {}
    for at, p in enumerate(places):
        one = add_low(add_low(own[0][at], from_ctx[at]), one_side[at])
        two = add_low(add_low(own[1][at], from_side[at]), two_ctx[at])
        entries[p] = jnp.concatenate([one, two], axis=-1)
    return entries


def over_core(keep, send):
    return keep, swap_core(send)


def pick_sum(parts, start, stop, column):
    keep, other = parts
    half = keep.shape[-1] // 2
    cut = (slice(start, stop), slice(None), slice(column * half, (column + 1) * half))
    return add_low(keep[cut], other[cut])


def sum_partners(values, fsdp, steps):
    for step in steps:
        values = values + lax.ppermute(values, "fsdp", [(i, i ^ step) for i in range(fsdp)])
    return values


def turn(values):
    return pltpu.roll(values, values.shape[-1] // 2, 1)


def norm_rope(raw, gain, cosine, sine):
    scale = lax.rsqrt(jnp.mean(raw * raw, axis=-1, keepdims=True) + eps_norm)
    scaled = raw * scale * gain
    return scaled * cosine + turn(scaled) * sine


def norm_rope_back(raw, gain, cosine, sine, grad):
    scale = lax.rsqrt(jnp.mean(raw * raw, axis=-1, keepdims=True) + eps_norm)
    unit = raw * scale
    grad_scaled = grad * cosine - turn(grad) * sine
    grad_gain = jnp.sum(grad_scaled * unit, axis=0, keepdims=True)
    grad_unit = grad_scaled * gain
    grad_raw = scale * (grad_unit - unit * jnp.mean(grad_unit * unit, axis=-1, keepdims=True))
    return grad_raw, grad_gain


def tiles_of(rows):
    step = rows // 2
    return [(start, start + step) for start in range(0, rows, step)]


def allowed(start, stop):
    shape = (stop - start, stop)
    return lax.broadcasted_iota(jnp.int32, shape, 1) <= (
        lax.broadcasted_iota(jnp.int32, shape, 0) + start
    )


def attend_kernel(q_ref, k_ref, v_ref, cos_ref, sin_ref, qg_ref, kg_ref, o_ref, qr_ref, kr_ref, vl_ref):
    head_dim = k_ref.shape[1]
    rows = k_ref.shape[0]
    cosine, sine = cos_ref[...], sin_ref[...]
    keys = norm_rope(k_ref[...], kg_ref[...], cosine, sine).astype(low)
    values = v_ref[...].astype(low)
    kr_ref[...] = keys
    vl_ref[...] = values
    for head in range(q_ref.shape[1] // head_dim):
        cols = slice(head * head_dim, (head + 1) * head_dim)
        query = norm_rope(q_ref[:, cols], qg_ref[...], cosine, sine).astype(low)
        qr_ref[:, cols] = query
        for start, stop in tiles_of(rows):
            scores = mul(query[start:stop], keys[:stop], rhs_turned) * (1.0 / math.sqrt(head_dim))
            expo = jnp.where(allowed(start, stop), jnp.exp(scores), 0.0)
            probs = (expo / jnp.sum(expo, axis=-1, keepdims=True)).astype(low)
            o_ref[start:stop, cols] = mul(probs, values[:stop]).astype(low)


def attend_grad_kernel(
    q_ref, k_ref, qr_ref, kr_ref, vl_ref, go_ref, cos_ref, sin_ref, qg_ref, kg_ref,
    dq_ref, dk_ref, dv_ref, dqg_ref, dkg_ref, dk_sum, dv_sum, dq_sum,
):
    head_dim = k_ref.shape[1]
    rows = k_ref.shape[0]
    root = 1.0 / math.sqrt(head_dim)
    cosine, sine = cos_ref[...], sin_ref[...]
    keys, values = kr_ref[...], vl_ref[...]
    gain_sum = jnp.zeros((1, head_dim), full)
    dk_sum[...] = jnp.zeros_like(dk_sum)
    dv_sum[...] = jnp.zeros_like(dv_sum)
    for head in range(q_ref.shape[1] // head_dim):
        cols = slice(head * head_dim, (head + 1) * head_dim)
        for start, stop in tiles_of(rows):
            query = qr_ref[start:stop, cols]
            grad = go_ref[start:stop, cols]
            scores = mul(query, keys[:stop], rhs_turned) * root
            expo = jnp.where(allowed(start, stop), jnp.exp(scores), 0.0)
            probs = expo / jnp.sum(expo, axis=-1, keepdims=True)
            grad_probs = mul(grad, values[:stop], rhs_turned)
            delta = jnp.sum(grad_probs * probs, axis=-1, keepdims=True)
            grad_scores = (probs * (grad_probs - delta)).astype(low)
            dv_sum[:stop] += mul(probs.astype(low), grad, lhs_turned)
            dk_sum[:stop] += mul(grad_scores, query, lhs_turned)
            dq_sum[start:stop] = mul(grad_scores, keys[:stop])
        grad_query = (dq_sum[...] * root).astype(low).astype(full)
        grad_raw, grad_gain = norm_rope_back(q_ref[:, cols], qg_ref[...], cosine, sine, grad_query)
        dq_ref[:, cols] = grad_raw.astype(low)
        gain_sum = gain_sum + grad_gain
    dqg_ref[0] = gain_sum
    grad_key = (dk_sum[...] * root).astype(low).astype(full)
    grad_raw, grad_gain = norm_rope_back(k_ref[...], kg_ref[...], cosine, sine, grad_key)
    dk_ref[...] = grad_raw.astype(low)
    dkg_ref[0] = grad_gain
    dv_ref[...] = dv_sum[...].astype(low)


def attention_specs(rows, head_dim, kv_heads, group):
    wide, narrow = group * head_dim, head_dim
    heads_end = kv_heads * group
    return dict(
        q=pl.BlockSpec((rows, wide), lambda i: (0, i)),
        k=pl.BlockSpec((rows, narrow), lambda i: (0, heads_end + i)),
        v=pl.BlockSpec((rows, narrow), lambda i: (0, heads_end + kv_heads + i)),
        own=pl.BlockSpec((rows, narrow), lambda i: (0, i)),
        table=pl.BlockSpec((rows, head_dim), lambda i: (0, 0)),
        gain=pl.BlockSpec((1, head_dim), lambda i: (0, 0)),
        gain_out=pl.BlockSpec((1, 1, head_dim), lambda i: (i, 0, 0)),
    )


def attend(projected, cosine, sine, query_gain, key_gain, kv_heads, group):
    rows, head_dim = cosine.shape
    s = attention_specs(rows, head_dim, kv_heads, group)
    shape = jax.ShapeDtypeStruct
    work = rows * rows * head_dim * kv_heads * group
    return pl.pallas_call(
        attend_kernel,
        grid=(kv_heads,),
        in_specs=[s["q"], s["k"], s["v"], s["table"], s["table"], s["gain"], s["gain"]],
        out_specs=[s["q"], s["q"], s["own"], s["own"]],
        out_shape=[
            shape((rows, kv_heads * group * head_dim), low),
            shape((rows, kv_heads * group * head_dim), low),
            shape((rows, kv_heads * head_dim), low),
            shape((rows, kv_heads * head_dim), low),
        ],
        compiler_params=pltpu.CompilerParams(vmem_limit_bytes=48 << 20),
        cost_estimate=pl.CostEstimate(
            flops=4 * work, bytes_accessed=projected.size * 6, transcendentals=work // head_dim
        ),
        name="attend",
    )(projected, projected, projected, cosine, sine, query_gain, key_gain)


def attend_grad(projected, roped_q, roped_k, values_low, grad, cosine, sine, query_gain, key_gain, kv_heads, group):
    rows, head_dim = cosine.shape
    s = attention_specs(rows, head_dim, kv_heads, group)
    shape = jax.ShapeDtypeStruct
    work = rows * rows * head_dim * kv_heads * group
    return pl.pallas_call(
        attend_grad_kernel,
        grid=(kv_heads,),
        in_specs=[
            s["q"], s["k"], s["q"], s["own"], s["own"], s["q"],
            s["table"], s["table"], s["gain"], s["gain"],
        ],
        out_specs=[s["q"], s["own"], s["own"], s["gain_out"], s["gain_out"]],
        out_shape=[
            shape((rows, kv_heads * group * head_dim), low),
            shape((rows, kv_heads * head_dim), low),
            shape((rows, kv_heads * head_dim), low),
            shape((kv_heads, 1, head_dim), full),
            shape((kv_heads, 1, head_dim), full),
        ],
        scratch_shapes=[pltpu.VMEM((rows, head_dim), full)] * 3,
        compiler_params=pltpu.CompilerParams(vmem_limit_bytes=48 << 20),
        cost_estimate=pl.CostEstimate(
            flops=10 * work, bytes_accessed=projected.size * 10, transcendentals=work // head_dim
        ),
        name="attend_grad",
    )(projected, projected, roped_q, roped_k, values_low, grad, cosine, sine, query_gain, key_gain)


def placed(gate, slots):
    block = gate.shape[1]
    shape = (block, block)
    earlier = (
        lax.broadcasted_iota(jnp.int32, shape, 0) < lax.broadcasted_iota(jnp.int32, shape, 1)
    ).astype(low)
    hit = jnp.where(gate >= 0.0, 1.0, 0.0)
    count = mul(jnp.broadcast_to(hit, (8, block)).astype(low), earlier)[:1].astype(jnp.int32)
    place = (lax.broadcasted_iota(jnp.int32, (slots, block), 0) == count) & (hit > 0.5)
    weight = jnp.sum(jnp.where(place, gate, 0.0), axis=1, keepdims=True)
    return place, place.astype(full).astype(low), weight


def expert_kernel(core_ref, order, m_ref, g_ref, far_ref, w_ref, gu_ref, dn_ref, *refs):
    keep_back, send_back, gate_back, rows_ref, dy_ref, z_ref, pair_ref = refs[-7:]
    core = core_ref[0]
    far = order[4 * pl.program_id(0) + 2] == 1
    width = m_ref.shape[4]
    hidden = dn_ref.shape[0]
    slots = z_ref.shape[0] // 2
    places, picks, weights, rows, grads = [], [], [], [], []
    for part in range(2):
        at = lax.rem(core + part, 2)
        place, pick, weight = placed(w_ref[0, at, 0], slots)
        places.append(place)
        picks.append(pick)
        weights.append(weight)
        rows.append(mul(pick, m_ref[0, at, 0]).astype(low))
        near_rows = g_ref[0, at, :, :width]
        far_rows = jnp.concatenate([far_ref[0, at], g_ref[0, at, :, width:]], axis=1)
        grads.append(mul(pick, jnp.where(far, far_rows, near_rows)).astype(low))
    row, grad, weight = (jnp.concatenate(items, axis=0) for items in (rows, grads, weights))
    rows_ref[...] = row
    paired = mul(row, gu_ref[...])
    gate_in, up = paired[:, :hidden], paired[:, hidden:]
    sig = jax.nn.sigmoid(gate_in)
    act = gate_in * sig
    z = (act * up).astype(low)
    z_ref[...] = z
    dy_ref[...] = (weight * grad.astype(full)).astype(low)
    unweighted = mul(grad, dn_ref[...], rhs_turned)
    grad_gate = jnp.sum(unweighted * z.astype(full), axis=1, keepdims=True)
    dz = weight * unweighted
    grad_in = dz * up * (sig * (1.0 + gate_in * (1.0 - sig)))
    pair = jnp.concatenate([grad_in, dz * act], axis=1).astype(low)
    pair_ref[...] = pair
    back = mul(pair, gu_ref[...], rhs_turned).astype(low)
    for part, out in enumerate((keep_back, send_back)):
        mine = slice(part * slots, (part + 1) * slots)
        out[0] = mul(picks[part], back[mine], lhs_turned).astype(low)
        gate_back[0, lax.rem(core + part, 2), 0] = jnp.sum(
            jnp.where(places[part], grad_gate[mine], 0.0), axis=0, keepdims=True
        )


def run_expert(core, order, first, total_steps, m_all, g_all, g_far, gates_all, gate_up, down, slots, kept):
    places, _, _, block, width = m_all.shape
    paired = gate_up.shape[1]
    steps = order.shape[0] // 4
    part_rows = steps * 2 * slots
    hidden = paired // 2
    shape = jax.ShapeDtypeStruct

    def gates_at(i, core, order):
        return (order[4 * i], 0, order[4 * i + 1], 0, 0)

    def token_at(i, core, order):
        return (order[4 * i], 0, order[4 * i + 2], 0, 0)

    def near_at(i, core, order):
        return (order[4 * i], 0, 0, 0)

    def far_at(i, core, order):
        return (order[4 * i + 3], 0, 0, 0)

    def fixed(i, core, order):
        return (0, 0)

    def flat(i, core, order):
        return (first + i, 0)

    def stacked(i, core, order):
        return (i, 0, 0)

    small = pl.BlockSpec((1, 2, 1, 1, block), gates_at)
    one_block = pl.BlockSpec((1, block, width), stacked)
    widths = (width, width, hidden, paired)
    grid_spec = pltpu.PrefetchScalarGridSpec(
        num_scalar_prefetch=2,
        grid=(steps,),
        in_specs=[
            pl.BlockSpec((1, 2, 1, block, width), token_at),
            pl.BlockSpec((1, 2, block, g_all.shape[3]), near_at),
            pl.BlockSpec((1, 2, block, g_far.shape[3]), far_at),
            small,
            pl.BlockSpec(gate_up.shape, fixed, pipeline_mode=pl.Buffered(1)),
            pl.BlockSpec(down.shape, fixed, pipeline_mode=pl.Buffered(1)),
        ]
        + [pl.BlockSpec(memory_space=pl.ANY)] * (0 if kept is None else 5),
        out_specs=[one_block] * 2 + [small] + [pl.BlockSpec((2 * slots, n), flat) for n in widths],
    )
    return pl.pallas_call(
        expert_kernel,
        grid_spec=grid_spec,
        out_shape=[shape((steps, block, width), low)] * 2
        + [shape((places, 2, 2, 1, block), full)]
        + [shape((total_steps * 2 * slots, n), low) for n in widths],
        input_output_aliases={} if kept is None else {8 + i: 2 + i for i in range(5)},
        compiler_params=pltpu.CompilerParams(vmem_limit_bytes=vmem_bytes),
        cost_estimate=pl.CostEstimate(
            flops=part_rows * width * (4 * paired + 2 * hidden + 6 * block),
            bytes_accessed=steps * block * width * 12 + part_rows * (width * 4 + paired * 3),
            transcendentals=part_rows * hidden,
        ),
        name="experts",
    )(core, order, m_all, g_all, g_far, gates_all, gate_up, down, *(() if kept is None else kept))


def result_kernel(core_ref, order, z_ref, w_ref, dn_ref, keep_out, send_out):
    core = core_ref[0]
    slots = z_ref.shape[0] // 2
    y = mul(z_ref[...], dn_ref[...]).astype(low).astype(full)
    for part, out in enumerate((keep_out, send_out)):
        _, pick, weight = placed(w_ref[0, lax.rem(core + part, 2), 0], slots)
        scaled = (weight * y[part * slots : (part + 1) * slots]).astype(low)
        out[0] = mul(pick, scaled, lhs_turned).astype(low)


def run_result(core, order, first, hidden, gates_all, down, slots):
    block, width, inner = gates_all.shape[4], down.shape[1], down.shape[0]
    steps = order.shape[0] // 4
    one_block = pl.BlockSpec((1, block, width), lambda i, core, order: (i, 0, 0))
    return pl.pallas_call(
        result_kernel,
        grid_spec=pltpu.PrefetchScalarGridSpec(
            num_scalar_prefetch=2,
            grid=(steps,),
            in_specs=[
                pl.BlockSpec((2 * slots, inner), lambda i, core, order: (first + i, 0)),
                pl.BlockSpec(
                    (1, 2, 1, 1, block), lambda i, core, order: (order[4 * i], 0, order[4 * i + 1], 0, 0)
                ),
                pl.BlockSpec(down.shape, lambda i, core, order: (0, 0), pipeline_mode=pl.Buffered(1)),
            ],
            out_specs=[one_block] * 2,
        ),
        out_shape=[jax.ShapeDtypeStruct((steps, block, width), low)] * 2,
        compiler_params=pltpu.CompilerParams(vmem_limit_bytes=vmem_bytes),
        cost_estimate=pl.CostEstimate(
            flops=steps * 2 * slots * width * (2 * inner + 2 * block),
            bytes_accessed=steps * (4 * block * width + 4 * slots * inner) + 2 * inner * width,
            transcendentals=0,
        ),
        name="results",
    )(core, order, hidden, gates_all, down)


def own_heads_kernel(rank, qkv_ref, out_ref, o_ref, *, head_dim, heads):
    first = rank[0] == 0
    for head in range(heads):
        pair = [qkv_ref[:, (2 * head + i) * head_dim : (2 * head + i + 1) * head_dim] for i in range(2)]
        o_ref[:, head * head_dim : (head + 1) * head_dim] = jnp.where(first, pair[0], pair[1])
    kv = qkv_ref.shape[1] - 2 * heads * head_dim
    o_ref[:, heads * head_dim : heads * head_dim + kv] = qkv_ref[:, 2 * heads * head_dim :]
    o_ref[:, heads * head_dim + kv :] = jnp.where(first, out_ref[:head_dim], out_ref[head_dim:])


def own_heads(rank, qkv_weight, out_weight, head_dim, heads):
    kv = qkv_weight.shape[1] - 2 * heads * head_dim
    return pl.pallas_call(
        functools.partial(own_heads_kernel, head_dim=head_dim, heads=heads),
        grid_spec=pltpu.PrefetchScalarGridSpec(
            num_scalar_prefetch=1,
            grid=(1,),
            in_specs=[
                pl.BlockSpec(qkv_weight.shape, lambda i, rank: (0, 0)),
                pl.BlockSpec(out_weight.shape, lambda i, rank: (0, 0)),
            ],
            out_specs=pl.BlockSpec(
                (qkv_weight.shape[0], heads * head_dim + kv + out_weight.shape[1]), lambda i, rank: (0, 0)
            ),
        ),
        out_shape=jax.ShapeDtypeStruct(
            (qkv_weight.shape[0], heads * head_dim + kv + out_weight.shape[1]), qkv_weight.dtype
        ),
        name="own_heads",
    )(rank, qkv_weight, out_weight)


def all_heads_kernel(rank, mine_ref, other_ref, o_ref, *, head_dim, heads):
    first = rank[0] == 0
    for head in range(heads):
        cols = slice(head * head_dim, (head + 1) * head_dim)
        mine, other = mine_ref[:, cols].astype(full), other_ref[:, cols].astype(full)
        o_ref[:, 2 * head * head_dim : (2 * head + 1) * head_dim] = jnp.where(first, mine, other)
        o_ref[:, (2 * head + 1) * head_dim : (2 * head + 2) * head_dim] = jnp.where(first, other, mine)
    o_ref[:, 2 * heads * head_dim :] = mine_ref[:, heads * head_dim :].astype(full) + other_ref[
        :, heads * head_dim :
    ].astype(full)


def all_heads(rank, mine, other, head_dim, heads):
    rows, width = mine.shape
    return pl.pallas_call(
        functools.partial(all_heads_kernel, head_dim=head_dim, heads=heads),
        grid_spec=pltpu.PrefetchScalarGridSpec(
            num_scalar_prefetch=1,
            grid=(1,),
            in_specs=[pl.BlockSpec((rows, width), lambda i, rank: (0, 0))] * 2,
            out_specs=pl.BlockSpec((rows, width + heads * head_dim), lambda i, rank: (0, 0)),
        ),
        out_shape=jax.ShapeDtypeStruct((rows, width + heads * head_dim), full),
        name="all_heads",
    )(rank, mine, other)


def rms_back(values, gain, grad):
    scale = lax.rsqrt(jnp.mean(values * values, axis=-1, keepdims=True) + eps_norm)
    unit = values * scale
    grad_gain = jnp.sum(grad * unit, axis=0)
    grad_unit = grad * gain
    back = scale * (grad_unit - unit * jnp.mean(grad_unit * unit, axis=-1, keepdims=True))
    return back, grad_gain


def in_order(first, second):
    half = first.shape[0] // 2
    return jnp.concatenate([first[:half], second, first[half:]], axis=0)


def of_block(values, rank):
    quarter = values.shape[0] // 4
    outer = jnp.concatenate([values[:quarter], values[3 * quarter :]], axis=0)
    return jnp.where(rank == 0, outer, values[quarter : 3 * quarter])


def body_gathered(
    tokens, qkv_weight, out_weight, router_weight, attn_gain, moe_gain, query_gain, key_gain,
    expert_gate_up, expert_down, routes, cotangent,
):
    rows_dev, width = tokens.shape
    head_dim = query_gain.shape[0]
    top_k = routes.shape[1]
    fsdp = lax.axis_size("fsdp")
    spot = lax.axis_index("fsdp")
    rank = lax.axis_index("ctx")
    place, side, core = spot // 4, (spot // 2) % 2, spot % 2
    shard = qkv_weight.shape[0]
    heads = out_weight.shape[0] * fsdp // head_dim
    kv_heads = (qkv_weight.shape[1] // head_dim - heads) // 2
    group = heads // kv_heads // 2
    my_heads = heads // 2
    width_q, width_k = my_heads * head_dim, kv_heads * head_dim
    experts_all = router_weight.shape[1]
    capacity = 2 * rows_dev * top_k // experts_all
    both = ("fsdp", "ctx")

    def sequence(values):
        other = swap_ctx(values)
        first = jnp.where(rank == 0, values, other)
        second = jnp.where(rank == 0, other, values)
        return in_order(first, second)

    rank_at = rank[None].astype(jnp.int32)
    weights_local = own_heads(rank_at, qkv_weight, out_weight, head_dim, my_heads)
    small_local = jnp.concatenate([router_weight, attn_gain[:, None], moe_gain[:, None]], axis=1)
    small_all = lax.all_gather(small_local, "fsdp", axis=0, tiled=True)
    weights_all = lax.all_gather(weights_local, "fsdp", axis=0, tiled=True)
    qkv_all = weights_all[:, : width_q + 2 * width_k]
    out_all = weights_all[:, width_q + 2 * width_k :]
    router_all = small_all[:, :experts_all]
    attn_all = small_all[:, experts_all].astype(full)
    moe_all = small_all[:, experts_all + 1].astype(full)
    late_cols = width * 7 // 16
    g_all = lax.all_gather(
        jnp.concatenate([cotangent, swap_ctx(cotangent[:, late_cols:])], axis=1), "fsdp", axis=0, tiled=True
    ).reshape(fsdp // 2, 2, rows_dev, 2 * width - late_cols)

    sequence_in = sequence(tokens).astype(full)
    low_in = rms_scale(sequence_in, attn_all).astype(low)
    projected = mul(low_in, qkv_all)
    cosine, sine = (t[:, 0] for t in angles(jnp.arange(2 * rows_dev, dtype=jnp.int32), head_dim))
    sine = jnp.concatenate([-sine[:, : head_dim // 2], sine[:, head_dim // 2 :]], axis=1)
    gain_q, gain_k = query_gain.astype(full)[None], key_gain.astype(full)[None]
    attended, roped_q, roped_k, values_low = attend(
        projected, cosine, sine, gain_q, gain_k, kv_heads, group
    )
    branch = mul(attended, out_all)
    inputs = tokens.astype(full)
    mixed = (
        inputs
        + of_block(branch, rank)
        + swap_ctx(of_block(branch, 1 - rank).astype(low)).astype(full)
    )
    low_mid = rms_scale(mixed, moe_all).astype(low)
    m_all = lax.all_gather(jnp.concatenate([low_mid, swap_ctx(low_mid)]), "fsdp", axis=0, tiled=True)

    logits = mul(low_mid, router_all)
    named = routes[:, :, None] == jnp.arange(experts_all, dtype=jnp.int32)[None, None, :]
    selected = jnp.sum(jnp.where(named, logits[:, None, :], 0.0), axis=2)
    gates = gating(selected)
    chosen = jnp.any(named, axis=1)
    gates_wide = jnp.sum(jnp.where(named, gates[:, :, None], 0.0), axis=1)
    gates_sent = jnp.where(chosen, gates_wide, -1.0).T
    gates_all = lax.all_to_all(gates_sent, both, split_axis=0, concat_axis=0, tiled=True)

    g_all, gates_all = hold(g_all, gates_all)
    g_far = swap_ctx(g_all[..., :late_cols])

    lines = fsdp // 4
    places = list(range(1, lines)) + [0]
    cut = lines // 2
    parts = [places[:cut], places[cut:]]
    m_all = m_all.reshape(fsdp // 2, 2, 2, rows_dev, width)
    gates_all = gates_all.reshape(fsdp // 2, 2, 2, 1, rows_dev)
    state = dict(kept=None, first=0, core=core[None].astype(jnp.int32))

    def order_of(steps):
        spots = [((place - p) % lines) * 2 + (side + d) % 2 for d, _, p in steps]
        far = [i for i, step in enumerate(steps) if step[1] == 1] or [0]
        return jnp.stack(
            [
                jnp.asarray(item, jnp.int32)
                for i, step in enumerate(steps)
                for item in (
                    spots[i],
                    (rank + step[1]) % 2,
                    step[1],
                    spots[min(far, key=lambda j, i=i: abs(j - i))],
                )
            ]
        )

    def call(steps, raw=False):
        keep_back, send_back, *kept = run_expert(
            state["core"],
            order_of(steps),
            state["first"],
            4 * lines,
            m_all,
            g_all,
            g_far,
            gates_all,
            expert_gate_up[0],
            expert_down[0],
            capacity,
            state["kept"],
        )
        state["kept"] = kept
        state["first"] += len(steps)
        return (keep_back, send_back) if raw else over_core(keep_back, send_back)

    def wait(first):
        state["core"], first = hold(state["core"], first)
        return first

    steps_far, steps_own = ([(d, d, p) for p in places] for d in (1, 0))
    steps_mixed = [[(1, 0, p) for p in part] + [(0, 1, p) for p in part] for part in parts]
    back = call(steps_far)
    far_one, far_two = wait([pick_sum(back, 0, lines, column) for column in range(2)])
    far_one, far_two = swap_ctx(far_one), swap_side(far_two)

    def mixed_sums(back, at=0):
        return [
            pick_sum(back, start, start + cut, column) for start in (at, at + cut) for column in range(2)
        ]

    def rounds(sums, part):
        side_one, side_two, ctx_one, ctx_two = sums
        span = slice(part * cut, (part + 1) * cut)
        return [
            swap_ctx(ctx_one),
            swap_side(side_two),
            swap_side(add_low(side_one, far_one[span])),
            swap_ctx(add_low(ctx_two, far_two[span])),
        ]

    keep, send = call(steps_mixed[0], raw=True)
    send, (far_one, far_two) = hold(send, (far_one, far_two))
    back = over_core(keep, send)
    back_own = call(steps_own)
    sums = wait(mixed_sums(back))
    back_own = [pick_sum(back_own, 0, lines, column) for column in range(2)]
    got = rounds(sums, 0)
    keep, send = call(steps_mixed[1], raw=True)
    send, got = hold(send, got)
    back = over_core(keep, send)
    entries = joined(parts[0], [item[:cut] for item in back_own], got)
    arrived = {p: line_shift(entries[p], lines - p) for p in parts[0]}
    gate_back, rows, grad_rows, hidden, grad_pair = state["kept"]
    hidden, sums = hold(hidden, mixed_sums(back))
    got = rounds(sums, 1)
    grad_gates = lax.all_to_all(
        gate_back.reshape(fsdp * 2, rows_dev), both, split_axis=0, concat_axis=0, tiled=True
    ).T
    def results(first, steps, hidden):
        return run_result(
            state["core"], order_of(steps), first, hidden, gates_all, expert_down[0], capacity
        )

    out_far = results(0, steps_far, hidden)
    out_rest = results(lines, steps_mixed[0] + steps_own + steps_mixed[1], hidden)
    got, out_far, out_rest, arrived, grad_gates = lax.optimization_barrier(
        (got, out_far, out_rest, arrived, grad_gates)
    )
    entries.update(joined(parts[1], [item[cut:] for item in back_own], got))
    out_far = over_core(*out_far)
    out_far = [pick_sum(out_far, 0, lines, 0), swap_side(pick_sum(out_far, 0, lines, 1))]
    out_rest = over_core(*out_rest)
    for p in parts[1][:-1]:
        arrived[p] = line_shift(entries[p], lines - p)
    grad_mid = line_total(entries[0], arrived)

    grad_wide = jnp.where(chosen, grad_gates, 0.0)
    grad_logits = (
        gates_wide * (grad_wide - jnp.sum(gates_wide * grad_wide, axis=1, keepdims=True))
    ).astype(low)
    grad_router = mul(low_mid, grad_logits, lhs_turned)
    grad_mid = grad_mid + mul(grad_logits, router_all, rhs_turned)
    grad_mixed_part, grad_moe_gain = rms_back(mixed, moe_all, grad_mid)
    grad_mixed = cotangent.astype(full) + grad_mixed_part

    low_mixed, (out_far[0], out_rest) = hold(grad_mixed.astype(low), (out_far[0], out_rest))
    grad_branch = sequence(low_mixed)
    out_sums = [
        jnp.concatenate([one, two])
        for one, two in zip(mixed_sums(out_rest), mixed_sums(out_rest, 2 * cut + lines))
    ]
    out_own = [pick_sum(out_rest, 2 * cut, 2 * cut + lines, column) for column in range(2)]
    (out_far[0], out_sums, out_own), grad_branch = hold((out_far[0], out_sums, out_own), grad_branch)
    side_one, side_two, ctx_one, ctx_two = out_sums
    out_far[0] = swap_ctx(out_far[0])
    grad_attended = mul(grad_branch, out_all, rhs_turned).astype(low)
    (rows, grad_pair), grad_attended = hold((rows, grad_pair), grad_attended)
    grad_gate_up = mul(rows, grad_pair, lhs_turned)[None]
    grad_attended, (out_far, grad_gate_up) = hold(grad_attended, (out_far, grad_gate_up))
    got = [
        swap_ctx(ctx_one),
        swap_side(side_two),
        swap_side(add_low(side_one, out_far[0])),
        swap_ctx(add_low(ctx_two, out_far[1])),
    ]
    grad_out_part = mul(attended, grad_branch, lhs_turned).astype(low)
    grad_q, grad_k, grad_v, gain_q_part, gain_k_part = attend_grad(
        projected, roped_q, roped_k, values_low, grad_attended, cosine, sine, gain_q, gain_k, kv_heads, group
    )
    grad_projected = jnp.concatenate([grad_q, grad_k, grad_v], axis=1)
    (hidden, grad_rows), grad_projected = hold((hidden, grad_rows), grad_projected)
    grad_down = mul(hidden, grad_rows, lhs_turned)[None]
    grad_projected, (got[0], got[1], grad_down) = hold(grad_projected, (got[0], got[1], grad_down))
    grad_qkv_part = mul(low_in, grad_projected, lhs_turned).astype(low)
    entries = joined(places, out_own, got)
    grad_projected, entries = hold(grad_projected, entries)
    one, two = line_first(entries, place)
    grad_normed_part = mul(grad_projected, qkv_all, rhs_turned)
    grad_normed = of_block(grad_normed_part, rank) + swap_ctx(
        of_block(grad_normed_part, 1 - rank).astype(low)
    ).astype(full)
    grad_in_part, grad_attn_gain = rms_back(inputs, attn_all, grad_normed)
    grad_tokens = grad_mixed + grad_in_part

    small_part = jnp.concatenate([grad_router, grad_moe_gain[:, None]], axis=1).astype(low)
    small_cols = -(-small_part.shape[1] // head_dim) * head_dim
    small_part = jnp.pad(small_part, ((0, 0), (0, small_cols - small_part.shape[1])))
    out_mine = lax.psum_scatter(
        jnp.concatenate([grad_out_part, small_part], axis=1), "fsdp", scatter_dimension=0, tiled=True
    )
    out_other = swap_ctx(out_mine).astype(full)
    out_mine = out_mine.astype(full)
    early = (out_mine + out_other)[:, width:]
    out_mine, out_other = out_mine[:, :width], out_other[:, :width]
    grad_out = jnp.where(
        rank == 0,
        jnp.concatenate([out_mine, out_other], axis=0),
        jnp.concatenate([out_other, out_mine], axis=0),
    )
    qkv_mine = lax.psum_scatter(grad_qkv_part, "fsdp", scatter_dimension=0, tiled=True)
    grad_qkv = all_heads(rank_at, qkv_mine, swap_ctx(qkv_mine), head_dim, my_heads)
    late = jnp.concatenate(
        [
            grad_attn_gain.reshape(-1, head_dim),
            jnp.sum(gain_q_part, axis=0),
            jnp.sum(gain_k_part, axis=0),
        ],
        axis=0,
    )
    late, (one, two) = hold(late, (one, two))
    far = line_second(entries, two)
    late = late + swap_ctx(late)
    late, far = hold(sum_partners(late, fsdp, (1, 2)), far)
    output = (mixed + entries[0].astype(full) + one.astype(full) + far.astype(full)).astype(low)
    late = sum_partners(late, fsdp, (4, 8))
    gain_rows = width // head_dim
    return (
        output,
        grad_tokens,
        grad_qkv,
        grad_out,
        early[:, :experts_all],
        lax.dynamic_slice_in_dim(late[:gain_rows].reshape(-1), spot * shard, shard, 0),
        early[:, experts_all],
        late[gain_rows],
        late[gain_rows + 1],
        grad_gate_up,
        grad_down,
    )


gathered_bytes = 1 << 26


def choose_body(*args):
    tokens, gate_up = args[0], args[8]
    fsdp, ctx = lax.axis_size("fsdp"), lax.axis_size("ctx")
    fits = tokens.size * tokens.dtype.itemsize * fsdp * ctx <= gathered_bytes
    if fits and ctx == 2 and fsdp == 16 and gate_up.shape[0] == 1:
        return body_gathered(*args)
    return body_routed(*args)


def solution(mesh):
    in_specs = (
        P(("fsdp", "ctx"), None),
        P("fsdp", None),
        P("fsdp", None),
        P("fsdp", None),
        P("fsdp"),
        P("fsdp"),
        P(),
        P(),
        P(("fsdp", "ctx"), None, None),
        P(("fsdp", "ctx"), None, None),
        P(("fsdp", "ctx"), None),
        P(("fsdp", "ctx"), None),
    )
    out_specs = (
        P(("fsdp", "ctx"), None),
        P(("fsdp", "ctx"), None),
        P("fsdp", None),
        P("fsdp", None),
        P("fsdp", None),
        P("fsdp"),
        P("fsdp"),
        P(),
        P(),
        P(("fsdp", "ctx"), None, None),
        P(("fsdp", "ctx"), None, None),
    )
    return jax.shard_map(choose_body, mesh=mesh, in_specs=in_specs, out_specs=out_specs, check_vma=False)
```

```python
import functools
import math

import jax
import jax.numpy as jnp
from jax import lax
from jax.experimental import pallas as pl
from jax.experimental.pallas import tpu as pltpu
from jax.sharding import PartitionSpec as P

eps_norm = 1e-06
theta_base = 1000000.0


def rms_scale(values, gain):
    return values * lax.rsqrt(jnp.mean(values * values, axis=-1, keepdims=True) + eps_norm) * gain


def rotate(values, cosine, sine):
    half_width = values.shape[-1] // 2
    turned = jnp.concatenate([-values[..., half_width:], values[..., :half_width]], axis=-1)
    return values * cosine + turned * sine


def angles(positions, width):
    freqs = theta_base ** (-(jnp.arange(width // 2, dtype=jnp.float32) * 2.0) / width)
    phase = positions.astype(jnp.float32)[:, None] * freqs[None, :]
    phase = jnp.concatenate([phase, phase], axis=-1)
    return (jnp.cos(phase)[:, None, :], jnp.sin(phase)[:, None, :])


def device_positions(block_rank, ctx_count, tok_rows):
    half_rows = tok_rows // 2
    within = jnp.arange(tok_rows, dtype=jnp.int32)
    span_id = jnp.where(within < half_rows, block_rank, 2 * ctx_count - 1 - block_rank)
    return span_id * half_rows + within % half_rows


def attend_head(query, keys_in, values_in, causal, scale_root):
    scores = (
        jnp.einsum("tgd,sd->gts", query, keys_in, preferred_element_type=jnp.float32) / scale_root
    )
    expo = jnp.where(causal[None], jnp.exp(scores), 0.0)
    totals = jnp.sum(expo, axis=-1, keepdims=True)
    probs = (expo / totals).astype(jnp.bfloat16)
    attended = jnp.einsum("gts,sd->tgd", probs, values_in, preferred_element_type=jnp.float32)
    return (attended, jnp.log(totals[..., 0]))


def attend_back(query, keys_in, values_in, causal, log_total, grad_attended, scale_root):
    scores = (
        jnp.einsum("tgd,sd->gts", query, keys_in, preferred_element_type=jnp.float32) / scale_root
    )
    probs = jnp.where(causal[None], jnp.exp(scores - log_total[..., None]), 0.0)
    low_probs = probs.astype(jnp.bfloat16)
    grad_values = jnp.einsum(
        "gts,tgd->sd", low_probs, grad_attended, preferred_element_type=jnp.float32
    )
    grad_probs = jnp.einsum(
        "tgd,sd->gts", grad_attended, values_in, preferred_element_type=jnp.float32
    )
    delta_rows = jnp.sum(grad_probs * probs, axis=-1, keepdims=True)
    grad_scores = (probs * (grad_probs - delta_rows)).astype(jnp.bfloat16)
    grad_query = (
        jnp.einsum("gts,sd->tgd", grad_scores, keys_in, preferred_element_type=jnp.float32)
        / scale_root
    )
    grad_keys = (
        jnp.einsum("gts,tgd->sd", grad_scores, query, preferred_element_type=jnp.float32)
        / scale_root
    )
    return (grad_query, grad_keys, grad_values)


def swiglu(paired):
    half_width = paired.shape[-1] // 2
    return jax.nn.silu(paired[..., :half_width]) * paired[..., half_width:]


def gating(selected):
    expo = jnp.exp(selected)
    return expo / jnp.sum(expo, axis=1, keepdims=True)


def body_routed(
    tokens,
    qkv_weight,
    out_weight,
    router_weight,
    attn_gain,
    moe_gain,
    query_gain,
    key_gain,
    expert_gate_up,
    expert_down,
    routes,
    cotangent,
):
    rows_dev, width = tokens.shape
    head_dim = query_gain.shape[0]
    top_k = routes.shape[1]
    ctx_count = lax.axis_size("ctx")
    ctx_rank = lax.axis_index("ctx")
    qkv_all, out_all, router_all, attn_all, moe_all = (
        lax.all_gather(qkv_weight, "fsdp", axis=0, tiled=True),
        lax.all_gather(out_weight, "fsdp", axis=0, tiled=True),
        lax.all_gather(router_weight, "fsdp", axis=0, tiled=True),
        lax.all_gather(attn_gain, "fsdp", axis=0, tiled=True),
        lax.all_gather(moe_gain, "fsdp", axis=0, tiled=True),
    )
    experts_all = router_all.shape[1]
    heads = out_all.shape[0] // head_dim
    kv_heads = (qkv_all.shape[1] // head_dim - heads) // 2
    group_size = heads // kv_heads
    capacity = 2 * rows_dev * top_k // experts_all
    width_q = heads * head_dim
    width_k = kv_heads * head_dim
    scale_root = math.sqrt(head_dim)
    inputs = tokens.astype(jnp.float32)
    normed_in = rms_scale(inputs, attn_all.astype(jnp.float32))
    low_in = normed_in.astype(jnp.bfloat16)
    projected = jnp.dot(low_in, qkv_all, preferred_element_type=jnp.float32)
    query_raw = projected[:, :width_q].reshape(rows_dev, heads, head_dim)
    key_raw = projected[:, width_q : width_q + width_k].reshape(rows_dev, kv_heads, head_dim)
    value_low = (
        projected[:, width_q + width_k :].astype(jnp.bfloat16).reshape(rows_dev, kv_heads, head_dim)
    )
    positions = device_positions(ctx_rank, ctx_count, rows_dev)
    cosine, sine = angles(positions, head_dim)
    query_gain_f = query_gain.astype(jnp.float32)
    key_gain_f = key_gain.astype(jnp.float32)

    def query_rope(values_in, gain):
        return rotate(rms_scale(values_in, gain), cosine, sine)

    query_low = query_rope(query_raw, query_gain_f).astype(jnp.bfloat16)
    key_low = query_rope(key_raw, key_gain_f).astype(jnp.bfloat16)
    keys_all, values_all = (
        lax.all_gather(key_low, "ctx", axis=0, tiled=True),
        lax.all_gather(value_low, "ctx", axis=0, tiled=True),
    )
    key_pos = jnp.concatenate(
        [device_positions(other, ctx_count, rows_dev) for other in range(ctx_count)]
    )
    causal = key_pos[None, :] <= positions[:, None]
    query_heads = query_low.reshape(rows_dev, kv_heads, group_size, head_dim).transpose(1, 0, 2, 3)
    key_heads = keys_all.transpose(1, 0, 2)
    value_heads = values_all.transpose(1, 0, 2)
    attended, log_total = lax.map(
        lambda member: attend_head(member[0], member[1], member[2], causal, scale_root),
        (query_heads, key_heads, value_heads),
    )
    attended_low = attended.transpose(1, 0, 2, 3).reshape(rows_dev, width_q).astype(jnp.bfloat16)
    mixed = inputs + jnp.dot(attended_low, out_all, preferred_element_type=jnp.float32)
    normed_mid = rms_scale(mixed, moe_all.astype(jnp.float32))
    low_mid = normed_mid.astype(jnp.bfloat16)
    logits = jnp.dot(low_mid, router_all, preferred_element_type=jnp.float32)
    selected = jnp.take_along_axis(logits, routes, axis=1)
    gates, gate_back = jax.vjp(gating, selected)
    flat_routes = routes.reshape(-1)
    expert_ids = jnp.arange(experts_all, dtype=jnp.int32)
    hit_table = (flat_routes[:, None] == expert_ids[None, :]).astype(jnp.int32)
    slot_index = jnp.sum(jnp.cumsum(hit_table, axis=0) * hit_table, axis=1) - 1
    target = flat_routes * capacity + slot_index
    pair_count = rows_dev * top_k
    source_pair = (
        jnp.full((experts_all * capacity,), pair_count, jnp.int32)
        .at[target]
        .set(jnp.arange(pair_count, dtype=jnp.int32))
    )
    padded = jnp.concatenate([low_mid, jnp.zeros((1, width), jnp.bfloat16)], axis=0)
    outgoing = padded[source_pair // top_k].reshape(experts_all, capacity, width)
    received = lax.all_to_all(outgoing, ("fsdp", "ctx"), split_axis=0, concat_axis=1, tiled=True)
    gate_and_up = jnp.einsum(
        "esd,edf->esf", received, expert_gate_up, preferred_element_type=jnp.float32
    )
    hidden_val, swiglu_back = jax.vjp(swiglu, gate_and_up)
    hidden_low = hidden_val.astype(jnp.bfloat16)
    result_low = jnp.einsum(
        "esf,efd->esd", hidden_low, expert_down, preferred_element_type=jnp.float32
    ).astype(jnp.bfloat16)
    returned = lax.all_to_all(
        result_low, ("fsdp", "ctx"), split_axis=1, concat_axis=0, tiled=True
    ).reshape(experts_all * capacity, width)
    picked = returned[target].reshape(rows_dev, top_k, width).astype(jnp.float32)
    output = (mixed + jnp.sum(gates[:, :, None] * picked, axis=1)).astype(jnp.bfloat16)
    qkv_back, out_back, router_back, attn_back_g, moe_back_g = (
        qkv_all,
        out_all,
        router_all,
        attn_all,
        moe_all,
    )
    grad_final = cotangent.astype(jnp.float32)
    grad_gates = jnp.sum(grad_final[:, None, :] * picked, axis=2)
    grad_result = (
        (gates[:, :, None] * grad_final[:, None, :]).astype(jnp.bfloat16).reshape(pair_count, width)
    )
    grad_padded = jnp.concatenate([grad_result, jnp.zeros((1, width), jnp.bfloat16)], axis=0)
    grad_outgoing = grad_padded[source_pair].reshape(experts_all, capacity, width)
    grad_received = lax.all_to_all(
        grad_outgoing, ("fsdp", "ctx"), split_axis=0, concat_axis=1, tiled=True
    )
    grad_down = jnp.einsum(
        "esf,esd->efd", hidden_low, grad_received, preferred_element_type=jnp.float32
    )
    grad_hidden = jnp.einsum(
        "esd,efd->esf", grad_received, expert_down, preferred_element_type=jnp.float32
    )
    grad_paired = swiglu_back(grad_hidden)[0].astype(jnp.bfloat16)
    grad_gate_up = jnp.einsum(
        "esd,esf->edf", received, grad_paired, preferred_element_type=jnp.float32
    )
    grad_rows = jnp.einsum(
        "esf,edf->esd", grad_paired, expert_gate_up, preferred_element_type=jnp.float32
    ).astype(jnp.bfloat16)
    grad_returned = lax.all_to_all(
        grad_rows, ("fsdp", "ctx"), split_axis=1, concat_axis=0, tiled=True
    ).reshape(experts_all * capacity, width)
    grad_mid = jnp.sum(
        grad_returned[target].reshape(rows_dev, top_k, width).astype(jnp.float32), axis=1
    )
    grad_selected = gate_back(grad_gates)[0]
    route_table = (routes[:, :, None] == expert_ids[None, None, :]).astype(jnp.float32)
    grad_logits = jnp.sum(route_table * grad_selected[:, :, None], axis=1).astype(jnp.bfloat16)
    grad_router = jnp.dot(low_mid.T, grad_logits, preferred_element_type=jnp.float32)
    grad_mid = grad_mid + jnp.dot(grad_logits, router_back.T, preferred_element_type=jnp.float32)
    unused_mid, mid_back = jax.vjp(rms_scale, mixed, moe_back_g.astype(jnp.float32))
    grad_mixed_part, grad_moe_gain = mid_back(grad_mid)
    grad_mixed = grad_final + grad_mixed_part
    grad_branch = grad_mixed.astype(jnp.bfloat16)
    grad_out = jnp.dot(attended_low.T, grad_branch, preferred_element_type=jnp.float32)
    grad_attended = jnp.dot(grad_branch, out_back.T, preferred_element_type=jnp.float32).astype(
        jnp.bfloat16
    )
    grad_heads = grad_attended.reshape(rows_dev, kv_heads, group_size, head_dim).transpose(
        1, 0, 2, 3
    )
    grad_query_h, grad_key_h, grad_value_h = lax.map(
        lambda member: attend_back(
            member[0], member[1], member[2], causal, member[3], member[4], scale_root
        ),
        (query_heads, key_heads, value_heads, log_total, grad_heads),
    )
    grad_keys, grad_values = (
        lax.psum_scatter(
            grad_key_h.transpose(1, 0, 2).astype(jnp.bfloat16),
            "ctx",
            scatter_dimension=0,
            tiled=True,
        ).astype(jnp.float32),
        lax.psum_scatter(
            grad_value_h.transpose(1, 0, 2).astype(jnp.bfloat16),
            "ctx",
            scatter_dimension=0,
            tiled=True,
        ).astype(jnp.float32),
    )
    grad_query_rot = (
        grad_query_h.transpose(1, 0, 2, 3).reshape(rows_dev, heads, head_dim).astype(jnp.bfloat16)
    )
    grad_query_rot = lax.optimization_barrier(grad_query_rot).astype(jnp.float32)
    grad_key_rot = lax.optimization_barrier(grad_keys.astype(jnp.bfloat16)).astype(jnp.float32)
    unused_query, query_back = jax.vjp(query_rope, query_raw, query_gain_f)
    grad_query_raw, grad_query_gain = query_back(grad_query_rot)
    unused_key, key_back = jax.vjp(query_rope, key_raw, key_gain_f)
    grad_key_raw, grad_key_gain = key_back(grad_key_rot)
    grad_projected = jnp.concatenate(
        [
            grad_query_raw.reshape(rows_dev, width_q).astype(jnp.bfloat16),
            grad_key_raw.reshape(rows_dev, width_k).astype(jnp.bfloat16),
            grad_values.reshape(rows_dev, width_k).astype(jnp.bfloat16),
        ],
        axis=1,
    )
    grad_qkv = jnp.dot(low_in.T, grad_projected, preferred_element_type=jnp.float32)
    grad_normed = jnp.dot(grad_projected, qkv_back.T, preferred_element_type=jnp.float32)
    unused_in, in_back = jax.vjp(rms_scale, inputs, attn_back_g.astype(jnp.float32))
    grad_in_part, grad_attn_gain = in_back(grad_normed)
    grad_tokens = grad_mixed + grad_in_part
    gradients = (grad_qkv, grad_out, grad_router, grad_attn_gain, grad_moe_gain)
    pieces = (
        lax.psum_scatter(gradients[0], "fsdp", scatter_dimension=0, tiled=True),
        lax.psum_scatter(gradients[1], "fsdp", scatter_dimension=0, tiled=True),
        lax.psum_scatter(gradients[2], "fsdp", scatter_dimension=0, tiled=True),
        lax.psum_scatter(gradients[3], "fsdp", scatter_dimension=0, tiled=True),
        lax.psum_scatter(gradients[4], "fsdp", scatter_dimension=0, tiled=True),
    )
    reduced = (
        lax.psum(pieces[0].astype(jnp.bfloat16), "ctx").astype(jnp.float32),
        lax.psum(pieces[1].astype(jnp.bfloat16), "ctx").astype(jnp.float32),
        lax.psum(pieces[2].astype(jnp.bfloat16), "ctx").astype(jnp.float32),
        lax.psum(pieces[3].astype(jnp.bfloat16), "ctx").astype(jnp.float32),
        lax.psum(pieces[4].astype(jnp.bfloat16), "ctx").astype(jnp.float32),
    )
    gain_sums = lax.psum((grad_query_gain, grad_key_gain), ("fsdp", "ctx"))
    return (
        output,
        grad_tokens,
        reduced[0],
        reduced[1],
        reduced[2],
        reduced[3],
        reduced[4],
        gain_sums[0],
        gain_sums[1],
        grad_gate_up,
        grad_down,
    )


low = jnp.bfloat16
full = jnp.float32
plain = (((1,), (0,)), ((), ()))
rhs_turned = (((1,), (1,)), ((), ()))
lhs_turned = (((0,), (0,)), ((), ()))
vmem_bytes = 58 << 20


def mul(left, right, dims=plain):
    return lax.dot_general(left, right, dims, preferred_element_type=full)


def core_pairs(fsdp):
    return [(i, i ^ 1) for i in range(fsdp)]


def side_pairs(fsdp):
    return [(i, i ^ 2) for i in range(fsdp)]


def swap_core(values):
    return lax.ppermute(values, "fsdp", core_pairs(lax.axis_size("fsdp")))


def swap_side(values):
    return lax.ppermute(values, "fsdp", side_pairs(lax.axis_size("fsdp")))


def swap_ctx(values):
    return lax.ppermute(values, "ctx", [(0, 1), (1, 0)])


def add_low(one, two):
    return (one.astype(full) + two.astype(full)).astype(low)


def hold(values, first):
    return lax.optimization_barrier((values, first))


def take(values, index):
    return lax.dynamic_index_in_dim(values, index, 0, keepdims=False)


def line_shift(values, step):
    fsdp = lax.axis_size("fsdp")
    return lax.ppermute(values, "fsdp", [(i, (i + 4 * step) % fsdp) for i in range(fsdp)])


def line_total(own, arrived):
    total = own.astype(full)
    for item in arrived.values():
        total = total + item.astype(full)
    return total


def line_first(entries, place):
    fsdp = lax.axis_size("fsdp")
    even = place % 2 == 0
    one, two = jnp.where(even, entries[3], entries[1]), jnp.where(even, entries[1], entries[3])
    return [lax.ppermute(item, "fsdp", [(i, i ^ 4) for i in range(fsdp)]) for item in (one, two)]


def line_second(entries, two):
    return lax.ppermute(
        add_low(entries[2], two), "fsdp", [(i, i ^ 8) for i in range(lax.axis_size("fsdp"))]
    )


def joined(places, own, got):
    from_ctx, from_side, one_side, two_ctx = got
    entries = {}
    for at, p in enumerate(places):
        one = add_low(add_low(own[0][at], from_ctx[at]), one_side[at])
        two = add_low(add_low(own[1][at], from_side[at]), two_ctx[at])
        entries[p] = jnp.concatenate([one, two], axis=-1)
    return entries


def over_core(keep, send):
    return keep, swap_core(send)


def pick_sum(parts, start, stop, column):
    keep, other = parts
    half = keep.shape[-1] // 2
    cut = (slice(start, stop), slice(None), slice(column * half, (column + 1) * half))
    return add_low(keep[cut], other[cut])


def sum_partners(values, fsdp, steps):
    for step in steps:
        values = values + lax.ppermute(values, "fsdp", [(i, i ^ step) for i in range(fsdp)])
    return values


def turn(values):
    return pltpu.roll(values, values.shape[-1] // 2, 1)


def norm_rope(raw, gain, cosine, sine):
    scale = lax.rsqrt(jnp.mean(raw * raw, axis=-1, keepdims=True) + eps_norm)
    scaled = raw * scale * gain
    return scaled * cosine + turn(scaled) * sine


def norm_rope_back(raw, gain, cosine, sine, grad):
    scale = lax.rsqrt(jnp.mean(raw * raw, axis=-1, keepdims=True) + eps_norm)
    unit = raw * scale
    grad_scaled = grad * cosine - turn(grad) * sine
    grad_gain = jnp.sum(grad_scaled * unit, axis=0, keepdims=True)
    grad_unit = grad_scaled * gain
    grad_raw = scale * (grad_unit - unit * jnp.mean(grad_unit * unit, axis=-1, keepdims=True))
    return grad_raw, grad_gain


def tiles_of(rows):
    step = rows // 2
    return [(start, start + step) for start in range(0, rows, step)]


def allowed(start, stop):
    shape = (stop - start, stop)
    return lax.broadcasted_iota(jnp.int32, shape, 1) <= (
        lax.broadcasted_iota(jnp.int32, shape, 0) + start
    )


def attend_kernel(q_ref, k_ref, v_ref, cos_ref, sin_ref, qg_ref, kg_ref, o_ref, qr_ref, kr_ref, vl_ref):
    head_dim = k_ref.shape[1]
    rows = k_ref.shape[0]
    cosine, sine = cos_ref[...], sin_ref[...]
    keys = norm_rope(k_ref[...], kg_ref[...], cosine, sine).astype(low)
    values = v_ref[...].astype(low)
    kr_ref[...] = keys
    vl_ref[...] = values
    for head in range(q_ref.shape[1] // head_dim):
        cols = slice(head * head_dim, (head + 1) * head_dim)
        query = norm_rope(q_ref[:, cols], qg_ref[...], cosine, sine).astype(low)
        qr_ref[:, cols] = query
        for start, stop in tiles_of(rows):
            scores = mul(query[start:stop], keys[:stop], rhs_turned) * (1.0 / math.sqrt(head_dim))
            expo = jnp.where(allowed(start, stop), jnp.exp(scores), 0.0)
            probs = (expo / jnp.sum(expo, axis=-1, keepdims=True)).astype(low)
            o_ref[start:stop, cols] = mul(probs, values[:stop]).astype(low)


def attend_grad_kernel(
    q_ref, k_ref, qr_ref, kr_ref, vl_ref, go_ref, cos_ref, sin_ref, qg_ref, kg_ref,
    dq_ref, dk_ref, dv_ref, dqg_ref, dkg_ref, dk_sum, dv_sum, dq_sum,
):
    head_dim = k_ref.shape[1]
    rows = k_ref.shape[0]
    root = 1.0 / math.sqrt(head_dim)
    cosine, sine = cos_ref[...], sin_ref[...]
    keys, values = kr_ref[...], vl_ref[...]
    gain_sum = jnp.zeros((1, head_dim), full)
    dk_sum[...] = jnp.zeros_like(dk_sum)
    dv_sum[...] = jnp.zeros_like(dv_sum)
    for head in range(q_ref.shape[1] // head_dim):
        cols = slice(head * head_dim, (head + 1) * head_dim)
        for start, stop in tiles_of(rows):
            query = qr_ref[start:stop, cols]
            grad = go_ref[start:stop, cols]
            scores = mul(query, keys[:stop], rhs_turned) * root
            expo = jnp.where(allowed(start, stop), jnp.exp(scores), 0.0)
            probs = expo / jnp.sum(expo, axis=-1, keepdims=True)
            grad_probs = mul(grad, values[:stop], rhs_turned)
            delta = jnp.sum(grad_probs * probs, axis=-1, keepdims=True)
            grad_scores = (probs * (grad_probs - delta)).astype(low)
            dv_sum[:stop] += mul(probs.astype(low), grad, lhs_turned)
            dk_sum[:stop] += mul(grad_scores, query, lhs_turned)
            dq_sum[start:stop] = mul(grad_scores, keys[:stop])
        grad_query = (dq_sum[...] * root).astype(low).astype(full)
        grad_raw, grad_gain = norm_rope_back(q_ref[:, cols], qg_ref[...], cosine, sine, grad_query)
        dq_ref[:, cols] = grad_raw.astype(low)
        gain_sum = gain_sum + grad_gain
    dqg_ref[0] = gain_sum
    grad_key = (dk_sum[...] * root).astype(low).astype(full)
    grad_raw, grad_gain = norm_rope_back(k_ref[...], kg_ref[...], cosine, sine, grad_key)
    dk_ref[...] = grad_raw.astype(low)
    dkg_ref[0] = grad_gain
    dv_ref[...] = dv_sum[...].astype(low)


def attention_specs(rows, head_dim, kv_heads, group):
    wide, narrow = group * head_dim, head_dim
    heads_end = kv_heads * group
    return dict(
        q=pl.BlockSpec((rows, wide), lambda i: (0, i)),
        k=pl.BlockSpec((rows, narrow), lambda i: (0, heads_end + i)),
        v=pl.BlockSpec((rows, narrow), lambda i: (0, heads_end + kv_heads + i)),
        own=pl.BlockSpec((rows, narrow), lambda i: (0, i)),
        table=pl.BlockSpec((rows, head_dim), lambda i: (0, 0)),
        gain=pl.BlockSpec((1, head_dim), lambda i: (0, 0)),
        gain_out=pl.BlockSpec((1, 1, head_dim), lambda i: (i, 0, 0)),
    )


def attend(projected, cosine, sine, query_gain, key_gain, kv_heads, group):
    rows, head_dim = cosine.shape
    s = attention_specs(rows, head_dim, kv_heads, group)
    shape = jax.ShapeDtypeStruct
    work = rows * rows * head_dim * kv_heads * group
    return pl.pallas_call(
        attend_kernel,
        grid=(kv_heads,),
        in_specs=[s["q"], s["k"], s["v"], s["table"], s["table"], s["gain"], s["gain"]],
        out_specs=[s["q"], s["q"], s["own"], s["own"]],
        out_shape=[
            shape((rows, kv_heads * group * head_dim), low),
            shape((rows, kv_heads * group * head_dim), low),
            shape((rows, kv_heads * head_dim), low),
            shape((rows, kv_heads * head_dim), low),
        ],
        compiler_params=pltpu.CompilerParams(vmem_limit_bytes=48 << 20),
        cost_estimate=pl.CostEstimate(
            flops=4 * work, bytes_accessed=projected.size * 6, transcendentals=work // head_dim
        ),
        name="attend",
    )(projected, projected, projected, cosine, sine, query_gain, key_gain)


def attend_grad(projected, roped_q, roped_k, values_low, grad, cosine, sine, query_gain, key_gain, kv_heads, group):
    rows, head_dim = cosine.shape
    s = attention_specs(rows, head_dim, kv_heads, group)
    shape = jax.ShapeDtypeStruct
    work = rows * rows * head_dim * kv_heads * group
    return pl.pallas_call(
        attend_grad_kernel,
        grid=(kv_heads,),
        in_specs=[
            s["q"], s["k"], s["q"], s["own"], s["own"], s["q"],
            s["table"], s["table"], s["gain"], s["gain"],
        ],
        out_specs=[s["q"], s["own"], s["own"], s["gain_out"], s["gain_out"]],
        out_shape=[
            shape((rows, kv_heads * group * head_dim), low),
            shape((rows, kv_heads * head_dim), low),
            shape((rows, kv_heads * head_dim), low),
            shape((kv_heads, 1, head_dim), full),
            shape((kv_heads, 1, head_dim), full),
        ],
        scratch_shapes=[pltpu.VMEM((rows, head_dim), full)] * 3,
        compiler_params=pltpu.CompilerParams(vmem_limit_bytes=48 << 20),
        cost_estimate=pl.CostEstimate(
            flops=10 * work, bytes_accessed=projected.size * 10, transcendentals=work // head_dim
        ),
        name="attend_grad",
    )(projected, projected, roped_q, roped_k, values_low, grad, cosine, sine, query_gain, key_gain)


def placed(gate, slots):
    block = gate.shape[1]
    shape = (block, block)
    earlier = (
        lax.broadcasted_iota(jnp.int32, shape, 0) < lax.broadcasted_iota(jnp.int32, shape, 1)
    ).astype(low)
    hit = jnp.where(gate >= 0.0, 1.0, 0.0)
    count = mul(jnp.broadcast_to(hit, (8, block)).astype(low), earlier)[:1].astype(jnp.int32)
    place = (lax.broadcasted_iota(jnp.int32, (slots, block), 0) == count) & (hit > 0.5)
    weight = jnp.sum(jnp.where(place, gate, 0.0), axis=1, keepdims=True)
    return place, place.astype(full).astype(low), weight


def expert_kernel(core_ref, order, m_ref, g_ref, far_ref, w_ref, gu_ref, dn_ref, *refs):
    keep_back, send_back, gate_back, rows_ref, dy_ref, z_ref, pair_ref = refs[-7:]
    core = core_ref[0]
    far = order[4 * pl.program_id(0) + 2] == 1
    width = m_ref.shape[4]
    hidden = dn_ref.shape[0]
    slots = z_ref.shape[0] // 2
    places, picks, weights, rows, grads = [], [], [], [], []
    for part in range(2):
        at = lax.rem(core + part, 2)
        place, pick, weight = placed(w_ref[0, at, 0], slots)
        places.append(place)
        picks.append(pick)
        weights.append(weight)
        rows.append(mul(pick, m_ref[0, at, 0]).astype(low))
        near_rows = g_ref[0, at, :, :width]
        far_rows = jnp.concatenate([far_ref[0, at], g_ref[0, at, :, width:]], axis=1)
        grads.append(mul(pick, jnp.where(far, far_rows, near_rows)).astype(low))
    row, grad, weight = (jnp.concatenate(items, axis=0) for items in (rows, grads, weights))
    rows_ref[...] = row
    paired = mul(row, gu_ref[...])
    gate_in, up = paired[:, :hidden], paired[:, hidden:]
    sig = jax.nn.sigmoid(gate_in)
    act = gate_in * sig
    z = (act * up).astype(low)
    z_ref[...] = z
    dy_ref[...] = (weight * grad.astype(full)).astype(low)
    unweighted = mul(grad, dn_ref[...], rhs_turned)
    grad_gate = jnp.sum(unweighted * z.astype(full), axis=1, keepdims=True)
    dz = weight * unweighted
    grad_in = dz * up * (sig * (1.0 + gate_in * (1.0 - sig)))
    pair = jnp.concatenate([grad_in, dz * act], axis=1).astype(low)
    pair_ref[...] = pair
    back = mul(pair, gu_ref[...], rhs_turned).astype(low)
    for part, out in enumerate((keep_back, send_back)):
        mine = slice(part * slots, (part + 1) * slots)
        out[0] = mul(picks[part], back[mine], lhs_turned).astype(low)
        gate_back[0, lax.rem(core + part, 2), 0] = jnp.sum(
            jnp.where(places[part], grad_gate[mine], 0.0), axis=0, keepdims=True
        )


def run_expert(core, order, first, total_steps, m_all, g_all, g_far, gates_all, gate_up, down, slots, kept):
    places, _, _, block, width = m_all.shape
    paired = gate_up.shape[1]
    steps = order.shape[0] // 4
    part_rows = steps * 2 * slots
    hidden = paired // 2
    shape = jax.ShapeDtypeStruct

    def gates_at(i, core, order):
        return (order[4 * i], 0, order[4 * i + 1], 0, 0)

    def token_at(i, core, order):
        return (order[4 * i], 0, order[4 * i + 2], 0, 0)

    def near_at(i, core, order):
        return (order[4 * i], 0, 0, 0)

    def far_at(i, core, order):
        return (order[4 * i + 3], 0, 0, 0)

    def fixed(i, core, order):
        return (0, 0)

    def flat(i, core, order):
        return (first + i, 0)

    def stacked(i, core, order):
        return (i, 0, 0)

    small = pl.BlockSpec((1, 2, 1, 1, block), gates_at)
    one_block = pl.BlockSpec((1, block, width), stacked)
    widths = (width, width, hidden, paired)
    grid_spec = pltpu.PrefetchScalarGridSpec(
        num_scalar_prefetch=2,
        grid=(steps,),
        in_specs=[
            pl.BlockSpec((1, 2, 1, block, width), token_at),
            pl.BlockSpec((1, 2, block, g_all.shape[3]), near_at),
            pl.BlockSpec((1, 2, block, g_far.shape[3]), far_at),
            small,
            pl.BlockSpec(gate_up.shape, fixed, pipeline_mode=pl.Buffered(1)),
            pl.BlockSpec(down.shape, fixed, pipeline_mode=pl.Buffered(1)),
        ]
        + [pl.BlockSpec(memory_space=pl.ANY)] * (0 if kept is None else 5),
        out_specs=[one_block] * 2 + [small] + [pl.BlockSpec((2 * slots, n), flat) for n in widths],
    )
    return pl.pallas_call(
        expert_kernel,
        grid_spec=grid_spec,
        out_shape=[shape((steps, block, width), low)] * 2
        + [shape((places, 2, 2, 1, block), full)]
        + [shape((total_steps * 2 * slots, n), low) for n in widths],
        input_output_aliases={} if kept is None else {8 + i: 2 + i for i in range(5)},
        compiler_params=pltpu.CompilerParams(vmem_limit_bytes=vmem_bytes),
        cost_estimate=pl.CostEstimate(
            flops=part_rows * width * (4 * paired + 2 * hidden + 6 * block),
            bytes_accessed=steps * block * width * 12 + part_rows * (width * 4 + paired * 3),
            transcendentals=part_rows * hidden,
        ),
        name="experts",
    )(core, order, m_all, g_all, g_far, gates_all, gate_up, down, *(() if kept is None else kept))


def result_kernel(core_ref, order, z_ref, w_ref, dn_ref, keep_out, send_out):
    core = core_ref[0]
    slots = z_ref.shape[0] // 2
    y = mul(z_ref[...], dn_ref[...]).astype(low).astype(full)
    for part, out in enumerate((keep_out, send_out)):
        _, pick, weight = placed(w_ref[0, lax.rem(core + part, 2), 0], slots)
        scaled = (weight * y[part * slots : (part + 1) * slots]).astype(low)
        out[0] = mul(pick, scaled, lhs_turned).astype(low)


def run_result(core, order, first, hidden, gates_all, down, slots):
    block, width, inner = gates_all.shape[4], down.shape[1], down.shape[0]
    steps = order.shape[0] // 4
    one_block = pl.BlockSpec((1, block, width), lambda i, core, order: (i, 0, 0))
    return pl.pallas_call(
        result_kernel,
        grid_spec=pltpu.PrefetchScalarGridSpec(
            num_scalar_prefetch=2,
            grid=(steps,),
            in_specs=[
                pl.BlockSpec((2 * slots, inner), lambda i, core, order: (first + i, 0)),
                pl.BlockSpec(
                    (1, 2, 1, 1, block), lambda i, core, order: (order[4 * i], 0, order[4 * i + 1], 0, 0)
                ),
                pl.BlockSpec(down.shape, lambda i, core, order: (0, 0), pipeline_mode=pl.Buffered(1)),
            ],
            out_specs=[one_block] * 2,
        ),
        out_shape=[jax.ShapeDtypeStruct((steps, block, width), low)] * 2,
        compiler_params=pltpu.CompilerParams(vmem_limit_bytes=vmem_bytes),
        cost_estimate=pl.CostEstimate(
            flops=steps * 2 * slots * width * (2 * inner + 2 * block),
            bytes_accessed=steps * (4 * block * width + 4 * slots * inner) + 2 * inner * width,
            transcendentals=0,
        ),
        name="results",
    )(core, order, hidden, gates_all, down)


def own_heads_kernel(rank, qkv_ref, out_ref, o_ref, *, head_dim, heads):
    first = rank[0] == 0
    for head in range(heads):
        pair = [qkv_ref[:, (2 * head + i) * head_dim : (2 * head + i + 1) * head_dim] for i in range(2)]
        o_ref[:, head * head_dim : (head + 1) * head_dim] = jnp.where(first, pair[0], pair[1])
    kv = qkv_ref.shape[1] - 2 * heads * head_dim
    o_ref[:, heads * head_dim : heads * head_dim + kv] = qkv_ref[:, 2 * heads * head_dim :]
    o_ref[:, heads * head_dim + kv :] = jnp.where(first, out_ref[:head_dim], out_ref[head_dim:])


def own_heads(rank, qkv_weight, out_weight, head_dim, heads):
    kv = qkv_weight.shape[1] - 2 * heads * head_dim
    return pl.pallas_call(
        functools.partial(own_heads_kernel, head_dim=head_dim, heads=heads),
        grid_spec=pltpu.PrefetchScalarGridSpec(
            num_scalar_prefetch=1,
            grid=(1,),
            in_specs=[
                pl.BlockSpec(qkv_weight.shape, lambda i, rank: (0, 0)),
                pl.BlockSpec(out_weight.shape, lambda i, rank: (0, 0)),
            ],
            out_specs=pl.BlockSpec(
                (qkv_weight.shape[0], heads * head_dim + kv + out_weight.shape[1]), lambda i, rank: (0, 0)
            ),
        ),
        out_shape=jax.ShapeDtypeStruct(
            (qkv_weight.shape[0], heads * head_dim + kv + out_weight.shape[1]), qkv_weight.dtype
        ),
        name="own_heads",
    )(rank, qkv_weight, out_weight)


def all_heads_kernel(rank, mine_ref, other_ref, o_ref, *, head_dim, heads):
    first = rank[0] == 0
    for head in range(heads):
        cols = slice(head * head_dim, (head + 1) * head_dim)
        mine, other = mine_ref[:, cols].astype(full), other_ref[:, cols].astype(full)
        o_ref[:, 2 * head * head_dim : (2 * head + 1) * head_dim] = jnp.where(first, mine, other)
        o_ref[:, (2 * head + 1) * head_dim : (2 * head + 2) * head_dim] = jnp.where(first, other, mine)
    o_ref[:, 2 * heads * head_dim :] = mine_ref[:, heads * head_dim :].astype(full) + other_ref[
        :, heads * head_dim :
    ].astype(full)


def all_heads(rank, mine, other, head_dim, heads):
    rows, width = mine.shape
    return pl.pallas_call(
        functools.partial(all_heads_kernel, head_dim=head_dim, heads=heads),
        grid_spec=pltpu.PrefetchScalarGridSpec(
            num_scalar_prefetch=1,
            grid=(1,),
            in_specs=[pl.BlockSpec((rows, width), lambda i, rank: (0, 0))] * 2,
            out_specs=pl.BlockSpec((rows, width + heads * head_dim), lambda i, rank: (0, 0)),
        ),
        out_shape=jax.ShapeDtypeStruct((rows, width + heads * head_dim), full),
        name="all_heads",
    )(rank, mine, other)


def rms_back(values, gain, grad):
    scale = lax.rsqrt(jnp.mean(values * values, axis=-1, keepdims=True) + eps_norm)
    unit = values * scale
    grad_gain = jnp.sum(grad * unit, axis=0)
    grad_unit = grad * gain
    back = scale * (grad_unit - unit * jnp.mean(grad_unit * unit, axis=-1, keepdims=True))
    return back, grad_gain


def in_order(first, second):
    half = first.shape[0] // 2
    return jnp.concatenate([first[:half], second, first[half:]], axis=0)


def of_block(values, rank):
    quarter = values.shape[0] // 4
    outer = jnp.concatenate([values[:quarter], values[3 * quarter :]], axis=0)
    return jnp.where(rank == 0, outer, values[quarter : 3 * quarter])


def body_gathered(
    tokens, qkv_weight, out_weight, router_weight, attn_gain, moe_gain, query_gain, key_gain,
    expert_gate_up, expert_down, routes, cotangent,
):
    rows_dev, width = tokens.shape
    head_dim = query_gain.shape[0]
    top_k = routes.shape[1]
    fsdp = lax.axis_size("fsdp")
    spot = lax.axis_index("fsdp")
    rank = lax.axis_index("ctx")
    place, side, core = spot // 4, (spot // 2) % 2, spot % 2
    shard = qkv_weight.shape[0]
    heads = out_weight.shape[0] * fsdp // head_dim
    kv_heads = (qkv_weight.shape[1] // head_dim - heads) // 2
    group = heads // kv_heads // 2
    my_heads = heads // 2
    width_q, width_k = my_heads * head_dim, kv_heads * head_dim
    experts_all = router_weight.shape[1]
    capacity = 2 * rows_dev * top_k // experts_all
    both = ("fsdp", "ctx")

    def sequence(values):
        other = swap_ctx(values)
        first = jnp.where(rank == 0, values, other)
        second = jnp.where(rank == 0, other, values)
        return in_order(first, second)

    rank_at = rank[None].astype(jnp.int32)
    weights_local = own_heads(rank_at, qkv_weight, out_weight, head_dim, my_heads)
    small_local = jnp.concatenate([router_weight, attn_gain[:, None], moe_gain[:, None]], axis=1)
    small_all = lax.all_gather(small_local, "fsdp", axis=0, tiled=True)
    weights_all = lax.all_gather(weights_local, "fsdp", axis=0, tiled=True)
    qkv_all = weights_all[:, : width_q + 2 * width_k]
    out_all = weights_all[:, width_q + 2 * width_k :]
    router_all = small_all[:, :experts_all]
    attn_all = small_all[:, experts_all].astype(full)
    moe_all = small_all[:, experts_all + 1].astype(full)
    late_cols = width * 7 // 16
    g_all = lax.all_gather(
        jnp.concatenate([cotangent, swap_ctx(cotangent[:, late_cols:])], axis=1), "fsdp", axis=0, tiled=True
    ).reshape(fsdp // 2, 2, rows_dev, 2 * width - late_cols)

    sequence_in = sequence(tokens).astype(full)
    low_in = rms_scale(sequence_in, attn_all).astype(low)
    projected = mul(low_in, qkv_all)
    cosine, sine = (t[:, 0] for t in angles(jnp.arange(2 * rows_dev, dtype=jnp.int32), head_dim))
    sine = jnp.concatenate([-sine[:, : head_dim // 2], sine[:, head_dim // 2 :]], axis=1)
    gain_q, gain_k = query_gain.astype(full)[None], key_gain.astype(full)[None]
    attended, roped_q, roped_k, values_low = attend(
        projected, cosine, sine, gain_q, gain_k, kv_heads, group
    )
    branch = mul(attended, out_all)
    inputs = tokens.astype(full)
    mixed = (
        inputs
        + of_block(branch, rank)
        + swap_ctx(of_block(branch, 1 - rank).astype(low)).astype(full)
    )
    low_mid = rms_scale(mixed, moe_all).astype(low)
    m_all = lax.all_gather(jnp.concatenate([low_mid, swap_ctx(low_mid)]), "fsdp", axis=0, tiled=True)

    logits = mul(low_mid, router_all)
    named = routes[:, :, None] == jnp.arange(experts_all, dtype=jnp.int32)[None, None, :]
    selected = jnp.sum(jnp.where(named, logits[:, None, :], 0.0), axis=2)
    gates = gating(selected)
    chosen = jnp.any(named, axis=1)
    gates_wide = jnp.sum(jnp.where(named, gates[:, :, None], 0.0), axis=1)
    gates_sent = jnp.where(chosen, gates_wide, -1.0).T
    gates_all = lax.all_to_all(gates_sent, both, split_axis=0, concat_axis=0, tiled=True)

    g_all, gates_all = hold(g_all, gates_all)
    g_far = swap_ctx(g_all[..., :late_cols])

    lines = fsdp // 4
    places = list(range(1, lines)) + [0]
    cut = lines // 2
    parts = [places[:cut], places[cut:]]
    m_all = m_all.reshape(fsdp // 2, 2, 2, rows_dev, width)
    gates_all = gates_all.reshape(fsdp // 2, 2, 2, 1, rows_dev)
    state = dict(kept=None, first=0, core=core[None].astype(jnp.int32))

    def order_of(steps):
        spots = [((place - p) % lines) * 2 + (side + d) % 2 for d, _, p in steps]
        far = [i for i, step in enumerate(steps) if step[1] == 1] or [0]
        return jnp.stack(
            [
                jnp.asarray(item, jnp.int32)
                for i, step in enumerate(steps)
                for item in (
                    spots[i],
                    (rank + step[1]) % 2,
                    step[1],
                    spots[min(far, key=lambda j, i=i: abs(j - i))],
                )
            ]
        )

    def call(steps, raw=False):
        keep_back, send_back, *kept = run_expert(
            state["core"],
            order_of(steps),
            state["first"],
            4 * lines,
            m_all,
            g_all,
            g_far,
            gates_all,
            expert_gate_up[0],
            expert_down[0],
            capacity,
            state["kept"],
        )
        state["kept"] = kept
        state["first"] += len(steps)
        return (keep_back, send_back) if raw else over_core(keep_back, send_back)

    def wait(first):
        state["core"], first = hold(state["core"], first)
        return first

    steps_far, steps_own = ([(d, d, p) for p in places] for d in (1, 0))
    steps_mixed = [[(1, 0, p) for p in part] + [(0, 1, p) for p in part] for part in parts]
    back = call(steps_far)
    far_one, far_two = wait([pick_sum(back, 0, lines, column) for column in range(2)])
    far_one, far_two = swap_ctx(far_one), swap_side(far_two)

    def mixed_sums(back, at=0):
        return [
            pick_sum(back, start, start + cut, column) for start in (at, at + cut) for column in range(2)
        ]

    def rounds(sums, part):
        side_one, side_two, ctx_one, ctx_two = sums
        span = slice(part * cut, (part + 1) * cut)
        to_ctx = swap_ctx(jnp.stack([ctx_one, add_low(ctx_two, far_two[span])]))
        to_side = swap_side(jnp.stack([side_two, add_low(side_one, far_one[span])]))
        return [to_ctx[0], to_side[0], to_side[1], to_ctx[1]]

    keep, send = call(steps_mixed[0], raw=True)
    send, (far_one, far_two) = hold(send, (far_one, far_two))
    back = over_core(keep, send)
    back_own = call(steps_own)
    sums = wait(mixed_sums(back))
    back_own = [pick_sum(back_own, 0, lines, column) for column in range(2)]
    got = rounds(sums, 0)
    keep, send = call(steps_mixed[1], raw=True)
    send, got = hold(send, got)
    back = over_core(keep, send)
    entries = joined(parts[0], [item[:cut] for item in back_own], got)
    arrived = {p: line_shift(entries[p], lines - p) for p in parts[0]}
    gate_back, rows, grad_rows, hidden, grad_pair = state["kept"]
    hidden, sums = hold(hidden, mixed_sums(back))
    got = rounds(sums, 1)
    grad_gates = lax.all_to_all(
        gate_back.reshape(fsdp * 2, rows_dev), both, split_axis=0, concat_axis=0, tiled=True
    ).T
    def results(first, steps, hidden):
        return run_result(
            state["core"], order_of(steps), first, hidden, gates_all, expert_down[0], capacity
        )

    out_far = results(0, steps_far, hidden)
    out_rest = results(lines, steps_mixed[0] + steps_own + steps_mixed[1], hidden)
    got, out_far, out_rest, arrived, grad_gates = lax.optimization_barrier(
        (got, out_far, out_rest, arrived, grad_gates)
    )
    entries.update(joined(parts[1], [item[cut:] for item in back_own], got))
    out_far = over_core(*out_far)
    out_far = [pick_sum(out_far, 0, lines, column) for column in range(2)]
    out_rest, out_far = hold(out_rest, out_far)
    out_far[1] = swap_side(out_far[1])
    out_rest = over_core(*out_rest)
    for p in parts[1][:-1]:
        arrived[p] = line_shift(entries[p], lines - p)
    grad_mid = line_total(entries[0], arrived)

    grad_wide = jnp.where(chosen, grad_gates, 0.0)
    grad_logits = (
        gates_wide * (grad_wide - jnp.sum(gates_wide * grad_wide, axis=1, keepdims=True))
    ).astype(low)
    grad_router = mul(low_mid, grad_logits, lhs_turned)
    grad_mid = grad_mid + mul(grad_logits, router_all, rhs_turned)
    grad_mixed_part, grad_moe_gain = rms_back(mixed, moe_all, grad_mid)
    grad_mixed = cotangent.astype(full) + grad_mixed_part

    low_mixed, (out_far[0], out_rest) = hold(grad_mixed.astype(low), (out_far[0], out_rest))
    grad_branch = sequence(low_mixed)
    out_sums = [
        jnp.concatenate([one, two])
        for one, two in zip(mixed_sums(out_rest), mixed_sums(out_rest, 2 * cut + lines))
    ]
    out_own = [pick_sum(out_rest, 2 * cut, 2 * cut + lines, column) for column in range(2)]
    (out_far, out_sums, out_own), grad_branch = hold((out_far, out_sums, out_own), grad_branch)
    side_one, side_two, ctx_one, ctx_two = out_sums
    out_far[0], from_side = swap_ctx(out_far[0]), swap_side(side_two)
    two_ctx = add_low(ctx_two, out_far[1])
    grad_attended = mul(grad_branch, out_all, rhs_turned).astype(low)
    (rows, grad_pair), grad_attended = hold((rows, grad_pair), grad_attended)
    grad_gate_up = mul(rows, grad_pair, lhs_turned)[None]
    grad_attended, (out_far[0], from_side, grad_gate_up) = hold(
        grad_attended, (out_far[0], from_side, grad_gate_up)
    )
    got = [
        swap_ctx(ctx_one),
        from_side,
        swap_side(add_low(side_one, out_far[0])),
        swap_ctx(two_ctx),
    ]
    grad_out_part = mul(attended, grad_branch, lhs_turned).astype(low)
    grad_q, grad_k, grad_v, gain_q_part, gain_k_part = attend_grad(
        projected, roped_q, roped_k, values_low, grad_attended, cosine, sine, gain_q, gain_k, kv_heads, group
    )
    grad_projected = jnp.concatenate([grad_q, grad_k, grad_v], axis=1)
    (hidden, grad_rows), grad_projected = hold((hidden, grad_rows), grad_projected)
    grad_down = mul(hidden, grad_rows, lhs_turned)[None]
    grad_projected, (got[2], got[3], grad_down) = hold(grad_projected, (got[2], got[3], grad_down))
    grad_qkv_part = mul(low_in, grad_projected, lhs_turned).astype(low)
    entries = joined(places, out_own, got)
    grad_projected, entries = hold(grad_projected, entries)
    one, two = line_first(entries, place)
    grad_normed_part = mul(grad_projected, qkv_all, rhs_turned)
    grad_normed = of_block(grad_normed_part, rank) + swap_ctx(
        of_block(grad_normed_part, 1 - rank).astype(low)
    ).astype(full)
    grad_in_part, grad_attn_gain = rms_back(inputs, attn_all, grad_normed)
    grad_tokens = grad_mixed + grad_in_part

    small_part = jnp.concatenate([grad_router, grad_moe_gain[:, None]], axis=1).astype(low)
    small_cols = -(-small_part.shape[1] // head_dim) * head_dim
    small_part = jnp.pad(small_part, ((0, 0), (0, small_cols - small_part.shape[1])))
    out_mine = lax.psum_scatter(
        jnp.concatenate([grad_out_part, small_part], axis=1), "fsdp", scatter_dimension=0, tiled=True
    )
    out_other = swap_ctx(out_mine).astype(full)
    out_mine = out_mine.astype(full)
    early = (out_mine + out_other)[:, width:]
    out_mine, out_other = out_mine[:, :width], out_other[:, :width]
    grad_out = jnp.where(
        rank == 0,
        jnp.concatenate([out_mine, out_other], axis=0),
        jnp.concatenate([out_other, out_mine], axis=0),
    )
    qkv_mine = lax.psum_scatter(grad_qkv_part, "fsdp", scatter_dimension=0, tiled=True)
    grad_qkv = all_heads(rank_at, qkv_mine, swap_ctx(qkv_mine), head_dim, my_heads)
    late = jnp.concatenate(
        [
            grad_attn_gain.reshape(-1, head_dim),
            jnp.sum(gain_q_part, axis=0),
            jnp.sum(gain_k_part, axis=0),
        ],
        axis=0,
    )
    late, (one, two) = hold(late, (one, two))
    far = line_second(entries, two)
    late = late + swap_ctx(late)
    late, far = hold(sum_partners(late, fsdp, (1, 2)), far)
    output = (mixed + entries[0].astype(full) + one.astype(full) + far.astype(full)).astype(low)
    late = sum_partners(late, fsdp, (4, 8))
    gain_rows = width // head_dim
    return (
        output,
        grad_tokens,
        grad_qkv,
        grad_out,
        early[:, :experts_all],
        lax.dynamic_slice_in_dim(late[:gain_rows].reshape(-1), spot * shard, shard, 0),
        early[:, experts_all],
        late[gain_rows],
        late[gain_rows + 1],
        grad_gate_up,
        grad_down,
    )


gathered_bytes = 1 << 26


def choose_body(*args):
    tokens, gate_up = args[0], args[8]
    fsdp, ctx = lax.axis_size("fsdp"), lax.axis_size("ctx")
    fits = tokens.size * tokens.dtype.itemsize * fsdp * ctx <= gathered_bytes
    if fits and ctx == 2 and fsdp == 16 and gate_up.shape[0] == 1:
        return body_gathered(*args)
    return body_routed(*args)


def solution(mesh):
    in_specs = (
        P(("fsdp", "ctx"), None),
        P("fsdp", None),
        P("fsdp", None),
        P("fsdp", None),
        P("fsdp"),
        P("fsdp"),
        P(),
        P(),
        P(("fsdp", "ctx"), None, None),
        P(("fsdp", "ctx"), None, None),
        P(("fsdp", "ctx"), None),
        P(("fsdp", "ctx"), None),
    )
    out_specs = (
        P(("fsdp", "ctx"), None),
        P(("fsdp", "ctx"), None),
        P("fsdp", None),
        P("fsdp", None),
        P("fsdp", None),
        P("fsdp"),
        P("fsdp"),
        P(),
        P(),
        P(("fsdp", "ctx"), None, None),
        P(("fsdp", "ctx"), None, None),
    )
    return jax.shard_map(choose_body, mesh=mesh, in_specs=in_specs, out_specs=out_specs, check_vma=False)
```

```python
import functools
import math

import jax
import jax.numpy as jnp
from jax import lax
from jax.experimental import pallas as pl
from jax.experimental.pallas import tpu as pltpu
from jax.sharding import PartitionSpec as P

eps_norm = 1e-06
theta_base = 1000000.0


def rms_scale(values, gain):
    return values * lax.rsqrt(jnp.mean(values * values, axis=-1, keepdims=True) + eps_norm) * gain


def rotate(values, cosine, sine):
    half_width = values.shape[-1] // 2
    turned = jnp.concatenate([-values[..., half_width:], values[..., :half_width]], axis=-1)
    return values * cosine + turned * sine


def angles(positions, width):
    freqs = theta_base ** (-(jnp.arange(width // 2, dtype=jnp.float32) * 2.0) / width)
    phase = positions.astype(jnp.float32)[:, None] * freqs[None, :]
    phase = jnp.concatenate([phase, phase], axis=-1)
    return (jnp.cos(phase)[:, None, :], jnp.sin(phase)[:, None, :])


def device_positions(block_rank, ctx_count, tok_rows):
    half_rows = tok_rows // 2
    within = jnp.arange(tok_rows, dtype=jnp.int32)
    span_id = jnp.where(within < half_rows, block_rank, 2 * ctx_count - 1 - block_rank)
    return span_id * half_rows + within % half_rows


def attend_head(query, keys_in, values_in, causal, scale_root):
    scores = (
        jnp.einsum("tgd,sd->gts", query, keys_in, preferred_element_type=jnp.float32) / scale_root
    )
    expo = jnp.where(causal[None], jnp.exp(scores), 0.0)
    totals = jnp.sum(expo, axis=-1, keepdims=True)
    probs = (expo / totals).astype(jnp.bfloat16)
    attended = jnp.einsum("gts,sd->tgd", probs, values_in, preferred_element_type=jnp.float32)
    return (attended, jnp.log(totals[..., 0]))


def attend_back(query, keys_in, values_in, causal, log_total, grad_attended, scale_root):
    scores = (
        jnp.einsum("tgd,sd->gts", query, keys_in, preferred_element_type=jnp.float32) / scale_root
    )
    probs = jnp.where(causal[None], jnp.exp(scores - log_total[..., None]), 0.0)
    low_probs = probs.astype(jnp.bfloat16)
    grad_values = jnp.einsum(
        "gts,tgd->sd", low_probs, grad_attended, preferred_element_type=jnp.float32
    )
    grad_probs = jnp.einsum(
        "tgd,sd->gts", grad_attended, values_in, preferred_element_type=jnp.float32
    )
    delta_rows = jnp.sum(grad_probs * probs, axis=-1, keepdims=True)
    grad_scores = (probs * (grad_probs - delta_rows)).astype(jnp.bfloat16)
    grad_query = (
        jnp.einsum("gts,sd->tgd", grad_scores, keys_in, preferred_element_type=jnp.float32)
        / scale_root
    )
    grad_keys = (
        jnp.einsum("gts,tgd->sd", grad_scores, query, preferred_element_type=jnp.float32)
        / scale_root
    )
    return (grad_query, grad_keys, grad_values)


def swiglu(paired):
    half_width = paired.shape[-1] // 2
    return jax.nn.silu(paired[..., :half_width]) * paired[..., half_width:]


def gating(selected):
    expo = jnp.exp(selected)
    return expo / jnp.sum(expo, axis=1, keepdims=True)


def body_routed(
    tokens,
    qkv_weight,
    out_weight,
    router_weight,
    attn_gain,
    moe_gain,
    query_gain,
    key_gain,
    expert_gate_up,
    expert_down,
    routes,
    cotangent,
):
    rows_dev, width = tokens.shape
    head_dim = query_gain.shape[0]
    top_k = routes.shape[1]
    ctx_count = lax.axis_size("ctx")
    ctx_rank = lax.axis_index("ctx")
    qkv_all, out_all, router_all, attn_all, moe_all = (
        lax.all_gather(qkv_weight, "fsdp", axis=0, tiled=True),
        lax.all_gather(out_weight, "fsdp", axis=0, tiled=True),
        lax.all_gather(router_weight, "fsdp", axis=0, tiled=True),
        lax.all_gather(attn_gain, "fsdp", axis=0, tiled=True),
        lax.all_gather(moe_gain, "fsdp", axis=0, tiled=True),
    )
    experts_all = router_all.shape[1]
    heads = out_all.shape[0] // head_dim
    kv_heads = (qkv_all.shape[1] // head_dim - heads) // 2
    group_size = heads // kv_heads
    capacity = 2 * rows_dev * top_k // experts_all
    width_q = heads * head_dim
    width_k = kv_heads * head_dim
    scale_root = math.sqrt(head_dim)
    inputs = tokens.astype(jnp.float32)
    normed_in = rms_scale(inputs, attn_all.astype(jnp.float32))
    low_in = normed_in.astype(jnp.bfloat16)
    projected = jnp.dot(low_in, qkv_all, preferred_element_type=jnp.float32)
    query_raw = projected[:, :width_q].reshape(rows_dev, heads, head_dim)
    key_raw = projected[:, width_q : width_q + width_k].reshape(rows_dev, kv_heads, head_dim)
    value_low = (
        projected[:, width_q + width_k :].astype(jnp.bfloat16).reshape(rows_dev, kv_heads, head_dim)
    )
    positions = device_positions(ctx_rank, ctx_count, rows_dev)
    cosine, sine = angles(positions, head_dim)
    query_gain_f = query_gain.astype(jnp.float32)
    key_gain_f = key_gain.astype(jnp.float32)

    def query_rope(values_in, gain):
        return rotate(rms_scale(values_in, gain), cosine, sine)

    query_low = query_rope(query_raw, query_gain_f).astype(jnp.bfloat16)
    key_low = query_rope(key_raw, key_gain_f).astype(jnp.bfloat16)
    keys_all, values_all = (
        lax.all_gather(key_low, "ctx", axis=0, tiled=True),
        lax.all_gather(value_low, "ctx", axis=0, tiled=True),
    )
    key_pos = jnp.concatenate(
        [device_positions(other, ctx_count, rows_dev) for other in range(ctx_count)]
    )
    causal = key_pos[None, :] <= positions[:, None]
    query_heads = query_low.reshape(rows_dev, kv_heads, group_size, head_dim).transpose(1, 0, 2, 3)
    key_heads = keys_all.transpose(1, 0, 2)
    value_heads = values_all.transpose(1, 0, 2)
    attended, log_total = lax.map(
        lambda member: attend_head(member[0], member[1], member[2], causal, scale_root),
        (query_heads, key_heads, value_heads),
    )
    attended_low = attended.transpose(1, 0, 2, 3).reshape(rows_dev, width_q).astype(jnp.bfloat16)
    mixed = inputs + jnp.dot(attended_low, out_all, preferred_element_type=jnp.float32)
    normed_mid = rms_scale(mixed, moe_all.astype(jnp.float32))
    low_mid = normed_mid.astype(jnp.bfloat16)
    logits = jnp.dot(low_mid, router_all, preferred_element_type=jnp.float32)
    selected = jnp.take_along_axis(logits, routes, axis=1)
    gates, gate_back = jax.vjp(gating, selected)
    flat_routes = routes.reshape(-1)
    expert_ids = jnp.arange(experts_all, dtype=jnp.int32)
    hit_table = (flat_routes[:, None] == expert_ids[None, :]).astype(jnp.int32)
    slot_index = jnp.sum(jnp.cumsum(hit_table, axis=0) * hit_table, axis=1) - 1
    target = flat_routes * capacity + slot_index
    pair_count = rows_dev * top_k
    source_pair = (
        jnp.full((experts_all * capacity,), pair_count, jnp.int32)
        .at[target]
        .set(jnp.arange(pair_count, dtype=jnp.int32))
    )
    padded = jnp.concatenate([low_mid, jnp.zeros((1, width), jnp.bfloat16)], axis=0)
    outgoing = padded[source_pair // top_k].reshape(experts_all, capacity, width)
    received = lax.all_to_all(outgoing, ("fsdp", "ctx"), split_axis=0, concat_axis=1, tiled=True)
    gate_and_up = jnp.einsum(
        "esd,edf->esf", received, expert_gate_up, preferred_element_type=jnp.float32
    )
    hidden_val, swiglu_back = jax.vjp(swiglu, gate_and_up)
    hidden_low = hidden_val.astype(jnp.bfloat16)
    result_low = jnp.einsum(
        "esf,efd->esd", hidden_low, expert_down, preferred_element_type=jnp.float32
    ).astype(jnp.bfloat16)
    returned = lax.all_to_all(
        result_low, ("fsdp", "ctx"), split_axis=1, concat_axis=0, tiled=True
    ).reshape(experts_all * capacity, width)
    picked = returned[target].reshape(rows_dev, top_k, width).astype(jnp.float32)
    output = (mixed + jnp.sum(gates[:, :, None] * picked, axis=1)).astype(jnp.bfloat16)
    qkv_back, out_back, router_back, attn_back_g, moe_back_g = (
        qkv_all,
        out_all,
        router_all,
        attn_all,
        moe_all,
    )
    grad_final = cotangent.astype(jnp.float32)
    grad_gates = jnp.sum(grad_final[:, None, :] * picked, axis=2)
    grad_result = (
        (gates[:, :, None] * grad_final[:, None, :]).astype(jnp.bfloat16).reshape(pair_count, width)
    )
    grad_padded = jnp.concatenate([grad_result, jnp.zeros((1, width), jnp.bfloat16)], axis=0)
    grad_outgoing = grad_padded[source_pair].reshape(experts_all, capacity, width)
    grad_received = lax.all_to_all(
        grad_outgoing, ("fsdp", "ctx"), split_axis=0, concat_axis=1, tiled=True
    )
    grad_down = jnp.einsum(
        "esf,esd->efd", hidden_low, grad_received, preferred_element_type=jnp.float32
    )
    grad_hidden = jnp.einsum(
        "esd,efd->esf", grad_received, expert_down, preferred_element_type=jnp.float32
    )
    grad_paired = swiglu_back(grad_hidden)[0].astype(jnp.bfloat16)
    grad_gate_up = jnp.einsum(
        "esd,esf->edf", received, grad_paired, preferred_element_type=jnp.float32
    )
    grad_rows = jnp.einsum(
        "esf,edf->esd", grad_paired, expert_gate_up, preferred_element_type=jnp.float32
    ).astype(jnp.bfloat16)
    grad_returned = lax.all_to_all(
        grad_rows, ("fsdp", "ctx"), split_axis=1, concat_axis=0, tiled=True
    ).reshape(experts_all * capacity, width)
    grad_mid = jnp.sum(
        grad_returned[target].reshape(rows_dev, top_k, width).astype(jnp.float32), axis=1
    )
    grad_selected = gate_back(grad_gates)[0]
    route_table = (routes[:, :, None] == expert_ids[None, None, :]).astype(jnp.float32)
    grad_logits = jnp.sum(route_table * grad_selected[:, :, None], axis=1).astype(jnp.bfloat16)
    grad_router = jnp.dot(low_mid.T, grad_logits, preferred_element_type=jnp.float32)
    grad_mid = grad_mid + jnp.dot(grad_logits, router_back.T, preferred_element_type=jnp.float32)
    unused_mid, mid_back = jax.vjp(rms_scale, mixed, moe_back_g.astype(jnp.float32))
    grad_mixed_part, grad_moe_gain = mid_back(grad_mid)
    grad_mixed = grad_final + grad_mixed_part
    grad_branch = grad_mixed.astype(jnp.bfloat16)
    grad_out = jnp.dot(attended_low.T, grad_branch, preferred_element_type=jnp.float32)
    grad_attended = jnp.dot(grad_branch, out_back.T, preferred_element_type=jnp.float32).astype(
        jnp.bfloat16
    )
    grad_heads = grad_attended.reshape(rows_dev, kv_heads, group_size, head_dim).transpose(
        1, 0, 2, 3
    )
    grad_query_h, grad_key_h, grad_value_h = lax.map(
        lambda member: attend_back(
            member[0], member[1], member[2], causal, member[3], member[4], scale_root
        ),
        (query_heads, key_heads, value_heads, log_total, grad_heads),
    )
    grad_keys, grad_values = (
        lax.psum_scatter(
            grad_key_h.transpose(1, 0, 2).astype(jnp.bfloat16),
            "ctx",
            scatter_dimension=0,
            tiled=True,
        ).astype(jnp.float32),
        lax.psum_scatter(
            grad_value_h.transpose(1, 0, 2).astype(jnp.bfloat16),
            "ctx",
            scatter_dimension=0,
            tiled=True,
        ).astype(jnp.float32),
    )
    grad_query_rot = (
        grad_query_h.transpose(1, 0, 2, 3).reshape(rows_dev, heads, head_dim).astype(jnp.bfloat16)
    )
    grad_query_rot = lax.optimization_barrier(grad_query_rot).astype(jnp.float32)
    grad_key_rot = lax.optimization_barrier(grad_keys.astype(jnp.bfloat16)).astype(jnp.float32)
    unused_query, query_back = jax.vjp(query_rope, query_raw, query_gain_f)
    grad_query_raw, grad_query_gain = query_back(grad_query_rot)
    unused_key, key_back = jax.vjp(query_rope, key_raw, key_gain_f)
    grad_key_raw, grad_key_gain = key_back(grad_key_rot)
    grad_projected = jnp.concatenate(
        [
            grad_query_raw.reshape(rows_dev, width_q).astype(jnp.bfloat16),
            grad_key_raw.reshape(rows_dev, width_k).astype(jnp.bfloat16),
            grad_values.reshape(rows_dev, width_k).astype(jnp.bfloat16),
        ],
        axis=1,
    )
    grad_qkv = jnp.dot(low_in.T, grad_projected, preferred_element_type=jnp.float32)
    grad_normed = jnp.dot(grad_projected, qkv_back.T, preferred_element_type=jnp.float32)
    unused_in, in_back = jax.vjp(rms_scale, inputs, attn_back_g.astype(jnp.float32))
    grad_in_part, grad_attn_gain = in_back(grad_normed)
    grad_tokens = grad_mixed + grad_in_part
    gradients = (grad_qkv, grad_out, grad_router, grad_attn_gain, grad_moe_gain)
    pieces = (
        lax.psum_scatter(gradients[0], "fsdp", scatter_dimension=0, tiled=True),
        lax.psum_scatter(gradients[1], "fsdp", scatter_dimension=0, tiled=True),
        lax.psum_scatter(gradients[2], "fsdp", scatter_dimension=0, tiled=True),
        lax.psum_scatter(gradients[3], "fsdp", scatter_dimension=0, tiled=True),
        lax.psum_scatter(gradients[4], "fsdp", scatter_dimension=0, tiled=True),
    )
    reduced = (
        lax.psum(pieces[0].astype(jnp.bfloat16), "ctx").astype(jnp.float32),
        lax.psum(pieces[1].astype(jnp.bfloat16), "ctx").astype(jnp.float32),
        lax.psum(pieces[2].astype(jnp.bfloat16), "ctx").astype(jnp.float32),
        lax.psum(pieces[3].astype(jnp.bfloat16), "ctx").astype(jnp.float32),
        lax.psum(pieces[4].astype(jnp.bfloat16), "ctx").astype(jnp.float32),
    )
    gain_sums = lax.psum((grad_query_gain, grad_key_gain), ("fsdp", "ctx"))
    return (
        output,
        grad_tokens,
        reduced[0],
        reduced[1],
        reduced[2],
        reduced[3],
        reduced[4],
        gain_sums[0],
        gain_sums[1],
        grad_gate_up,
        grad_down,
    )


low = jnp.bfloat16
full = jnp.float32
plain = (((1,), (0,)), ((), ()))
rhs_turned = (((1,), (1,)), ((), ()))
lhs_turned = (((0,), (0,)), ((), ()))
vmem_bytes = 58 << 20


def mul(left, right, dims=plain):
    return lax.dot_general(left, right, dims, preferred_element_type=full)


def core_pairs(fsdp):
    return [(i, i ^ 1) for i in range(fsdp)]


def side_pairs(fsdp):
    return [(i, i ^ 2) for i in range(fsdp)]


def swap_core(values):
    return lax.ppermute(values, "fsdp", core_pairs(lax.axis_size("fsdp")))


def swap_side(values):
    return lax.ppermute(values, "fsdp", side_pairs(lax.axis_size("fsdp")))


def swap_ctx(values):
    return lax.ppermute(values, "ctx", [(0, 1), (1, 0)])


def add_low(one, two):
    return (one.astype(full) + two.astype(full)).astype(low)


def hold(values, first):
    return lax.optimization_barrier((values, first))


def take(values, index):
    return lax.dynamic_index_in_dim(values, index, 0, keepdims=False)


def line_shift(values, step):
    fsdp = lax.axis_size("fsdp")
    return lax.ppermute(values, "fsdp", [(i, (i + 4 * step) % fsdp) for i in range(fsdp)])


def line_total(own, arrived):
    total = own.astype(full)
    for item in arrived.values():
        total = total + item.astype(full)
    return total


def line_first(entries, place):
    fsdp = lax.axis_size("fsdp")
    even = place % 2 == 0
    one, two = jnp.where(even, entries[3], entries[1]), jnp.where(even, entries[1], entries[3])
    return [lax.ppermute(item, "fsdp", [(i, i ^ 4) for i in range(fsdp)]) for item in (one, two)]


def line_second(entries, two):
    return lax.ppermute(
        add_low(entries[2], two), "fsdp", [(i, i ^ 8) for i in range(lax.axis_size("fsdp"))]
    )


def joined(places, own, got):
    from_ctx, from_side, one_side, two_ctx = got
    entries = {}
    for at, p in enumerate(places):
        one = add_low(add_low(own[0][at], from_ctx[at]), one_side[at])
        two = add_low(add_low(own[1][at], from_side[at]), two_ctx[at])
        entries[p] = jnp.concatenate([one, two], axis=-1)
    return entries


def over_core(keep, send):
    return keep, swap_core(send)


def pick_sum(parts, start, stop, column):
    keep, other = parts
    half = keep.shape[-1] // 2
    cut = (slice(start, stop), slice(None), slice(column * half, (column + 1) * half))
    return add_low(keep[cut], other[cut])


def sum_partners(values, fsdp, steps):
    for step in steps:
        values = values + lax.ppermute(values, "fsdp", [(i, i ^ step) for i in range(fsdp)])
    return values


def halve_line(values, fsdp, place):
    for step, bit in ((2, place // 2), (1, place % 2)):
        values = values.reshape(2, step, *values.shape[1:])
        other = lax.ppermute(take(values, 1 - bit), "fsdp", [(i, i ^ (4 * step)) for i in range(fsdp)])
        values = take(values, bit) + other
    return values[0]


def turn(values):
    return pltpu.roll(values, values.shape[-1] // 2, 1)


def norm_rope(raw, gain, cosine, sine):
    scale = lax.rsqrt(jnp.mean(raw * raw, axis=-1, keepdims=True) + eps_norm)
    scaled = raw * scale * gain
    return scaled * cosine + turn(scaled) * sine


def norm_rope_back(raw, gain, cosine, sine, grad):
    scale = lax.rsqrt(jnp.mean(raw * raw, axis=-1, keepdims=True) + eps_norm)
    unit = raw * scale
    grad_scaled = grad * cosine - turn(grad) * sine
    grad_gain = jnp.sum(grad_scaled * unit, axis=0, keepdims=True)
    grad_unit = grad_scaled * gain
    grad_raw = scale * (grad_unit - unit * jnp.mean(grad_unit * unit, axis=-1, keepdims=True))
    return grad_raw, grad_gain


def tiles_of(rows):
    step = rows // 2
    return [(start, start + step) for start in range(0, rows, step)]


def allowed(start, stop):
    shape = (stop - start, stop)
    return lax.broadcasted_iota(jnp.int32, shape, 1) <= (
        lax.broadcasted_iota(jnp.int32, shape, 0) + start
    )


def attend_kernel(q_ref, k_ref, v_ref, cos_ref, sin_ref, qg_ref, kg_ref, o_ref, qr_ref, kr_ref, vl_ref):
    head_dim = k_ref.shape[1]
    rows = k_ref.shape[0]
    cosine, sine = cos_ref[...], sin_ref[...]
    keys = norm_rope(k_ref[...], kg_ref[...], cosine, sine).astype(low)
    values = v_ref[...].astype(low)
    kr_ref[...] = keys
    vl_ref[...] = values
    for head in range(q_ref.shape[1] // head_dim):
        cols = slice(head * head_dim, (head + 1) * head_dim)
        query = norm_rope(q_ref[:, cols], qg_ref[...], cosine, sine).astype(low)
        qr_ref[:, cols] = query
        for start, stop in tiles_of(rows):
            scores = mul(query[start:stop], keys[:stop], rhs_turned) * (1.0 / math.sqrt(head_dim))
            expo = jnp.where(allowed(start, stop), jnp.exp(scores), 0.0)
            probs = (expo / jnp.sum(expo, axis=-1, keepdims=True)).astype(low)
            o_ref[start:stop, cols] = mul(probs, values[:stop]).astype(low)


def attend_grad_kernel(
    q_ref, k_ref, qr_ref, kr_ref, vl_ref, go_ref, cos_ref, sin_ref, qg_ref, kg_ref,
    dq_ref, dk_ref, dv_ref, dqg_ref, dkg_ref, dk_sum, dv_sum, dq_sum,
):
    head_dim = k_ref.shape[1]
    rows = k_ref.shape[0]
    root = 1.0 / math.sqrt(head_dim)
    cosine, sine = cos_ref[...], sin_ref[...]
    keys, values = kr_ref[...], vl_ref[...]
    gain_sum = jnp.zeros((1, head_dim), full)
    dk_sum[...] = jnp.zeros_like(dk_sum)
    dv_sum[...] = jnp.zeros_like(dv_sum)
    for head in range(q_ref.shape[1] // head_dim):
        cols = slice(head * head_dim, (head + 1) * head_dim)
        for start, stop in tiles_of(rows):
            query = qr_ref[start:stop, cols]
            grad = go_ref[start:stop, cols]
            scores = mul(query, keys[:stop], rhs_turned) * root
            expo = jnp.where(allowed(start, stop), jnp.exp(scores), 0.0)
            probs = expo / jnp.sum(expo, axis=-1, keepdims=True)
            grad_probs = mul(grad, values[:stop], rhs_turned)
            delta = jnp.sum(grad_probs * probs, axis=-1, keepdims=True)
            grad_scores = (probs * (grad_probs - delta)).astype(low)
            dv_sum[:stop] += mul(probs.astype(low), grad, lhs_turned)
            dk_sum[:stop] += mul(grad_scores, query, lhs_turned)
            dq_sum[start:stop] = mul(grad_scores, keys[:stop])
        grad_query = (dq_sum[...] * root).astype(low).astype(full)
        grad_raw, grad_gain = norm_rope_back(q_ref[:, cols], qg_ref[...], cosine, sine, grad_query)
        dq_ref[:, cols] = grad_raw.astype(low)
        gain_sum = gain_sum + grad_gain
    dqg_ref[0] = gain_sum
    grad_key = (dk_sum[...] * root).astype(low).astype(full)
    grad_raw, grad_gain = norm_rope_back(k_ref[...], kg_ref[...], cosine, sine, grad_key)
    dk_ref[...] = grad_raw.astype(low)
    dkg_ref[0] = grad_gain
    dv_ref[...] = dv_sum[...].astype(low)


def attention_specs(rows, head_dim, kv_heads, group):
    wide, narrow = group * head_dim, head_dim
    heads_end = kv_heads * group
    return dict(
        q=pl.BlockSpec((rows, wide), lambda i: (0, i)),
        k=pl.BlockSpec((rows, narrow), lambda i: (0, heads_end + i)),
        v=pl.BlockSpec((rows, narrow), lambda i: (0, heads_end + kv_heads + i)),
        own=pl.BlockSpec((rows, narrow), lambda i: (0, i)),
        table=pl.BlockSpec((rows, head_dim), lambda i: (0, 0)),
        gain=pl.BlockSpec((1, head_dim), lambda i: (0, 0)),
        gain_out=pl.BlockSpec((1, 1, head_dim), lambda i: (i, 0, 0)),
    )


def attend(projected, cosine, sine, query_gain, key_gain, kv_heads, group):
    rows, head_dim = cosine.shape
    s = attention_specs(rows, head_dim, kv_heads, group)
    shape = jax.ShapeDtypeStruct
    work = rows * rows * head_dim * kv_heads * group
    return pl.pallas_call(
        attend_kernel,
        grid=(kv_heads,),
        in_specs=[s["q"], s["k"], s["v"], s["table"], s["table"], s["gain"], s["gain"]],
        out_specs=[s["q"], s["q"], s["own"], s["own"]],
        out_shape=[
            shape((rows, kv_heads * group * head_dim), low),
            shape((rows, kv_heads * group * head_dim), low),
            shape((rows, kv_heads * head_dim), low),
            shape((rows, kv_heads * head_dim), low),
        ],
        compiler_params=pltpu.CompilerParams(vmem_limit_bytes=48 << 20),
        cost_estimate=pl.CostEstimate(
            flops=4 * work, bytes_accessed=projected.size * 6, transcendentals=work // head_dim
        ),
        name="attend",
    )(projected, projected, projected, cosine, sine, query_gain, key_gain)


def attend_grad(projected, roped_q, roped_k, values_low, grad, cosine, sine, query_gain, key_gain, kv_heads, group):
    rows, head_dim = cosine.shape
    s = attention_specs(rows, head_dim, kv_heads, group)
    shape = jax.ShapeDtypeStruct
    work = rows * rows * head_dim * kv_heads * group
    return pl.pallas_call(
        attend_grad_kernel,
        grid=(kv_heads,),
        in_specs=[
            s["q"], s["k"], s["q"], s["own"], s["own"], s["q"],
            s["table"], s["table"], s["gain"], s["gain"],
        ],
        out_specs=[s["q"], s["own"], s["own"], s["gain_out"], s["gain_out"]],
        out_shape=[
            shape((rows, kv_heads * group * head_dim), low),
            shape((rows, kv_heads * head_dim), low),
            shape((rows, kv_heads * head_dim), low),
            shape((kv_heads, 1, head_dim), full),
            shape((kv_heads, 1, head_dim), full),
        ],
        scratch_shapes=[pltpu.VMEM((rows, head_dim), full)] * 3,
        compiler_params=pltpu.CompilerParams(vmem_limit_bytes=48 << 20),
        cost_estimate=pl.CostEstimate(
            flops=10 * work, bytes_accessed=projected.size * 10, transcendentals=work // head_dim
        ),
        name="attend_grad",
    )(projected, projected, roped_q, roped_k, values_low, grad, cosine, sine, query_gain, key_gain)


def placed(gate, slots):
    block = gate.shape[1]
    shape = (block, block)
    earlier = (
        lax.broadcasted_iota(jnp.int32, shape, 0) < lax.broadcasted_iota(jnp.int32, shape, 1)
    ).astype(low)
    hit = jnp.where(gate >= 0.0, 1.0, 0.0)
    count = mul(jnp.broadcast_to(hit, (8, block)).astype(low), earlier)[:1].astype(jnp.int32)
    place = (lax.broadcasted_iota(jnp.int32, (slots, block), 0) == count) & (hit > 0.5)
    weight = jnp.sum(jnp.where(place, gate, 0.0), axis=1, keepdims=True)
    return place, place.astype(full).astype(low), weight


def expert_kernel(core_ref, order, m_ref, g_ref, far_ref, w_ref, gu_ref, dn_ref, *refs):
    keep_back, send_back, gate_back, rows_ref, dy_ref, z_ref, pair_ref = refs[-7:]
    core = core_ref[0]
    far = order[4 * pl.program_id(0) + 2] == 1
    width = m_ref.shape[4]
    hidden = dn_ref.shape[0]
    slots = z_ref.shape[0] // 2
    places, picks, weights, rows, grads = [], [], [], [], []
    for part in range(2):
        at = lax.rem(core + part, 2)
        place, pick, weight = placed(w_ref[0, at, 0], slots)
        places.append(place)
        picks.append(pick)
        weights.append(weight)
        rows.append(mul(pick, m_ref[0, at, 0]).astype(low))
        near_rows = g_ref[0, at, :, :width]
        far_rows = jnp.concatenate([far_ref[0, at], g_ref[0, at, :, width:]], axis=1)
        grads.append(mul(pick, jnp.where(far, far_rows, near_rows)).astype(low))
    row, grad, weight = (jnp.concatenate(items, axis=0) for items in (rows, grads, weights))
    rows_ref[...] = row
    paired = mul(row, gu_ref[...])
    gate_in, up = paired[:, :hidden], paired[:, hidden:]
    sig = jax.nn.sigmoid(gate_in)
    act = gate_in * sig
    z = (act * up).astype(low)
    z_ref[...] = z
    dy_ref[...] = (weight * grad.astype(full)).astype(low)
    unweighted = mul(grad, dn_ref[...], rhs_turned)
    grad_gate = jnp.sum(unweighted * z.astype(full), axis=1, keepdims=True)
    dz = weight * unweighted
    grad_in = dz * up * (sig * (1.0 + gate_in * (1.0 - sig)))
    pair = jnp.concatenate([grad_in, dz * act], axis=1).astype(low)
    pair_ref[...] = pair
    back = mul(pair, gu_ref[...], rhs_turned).astype(low)
    for part, out in enumerate((keep_back, send_back)):
        mine = slice(part * slots, (part + 1) * slots)
        out[0] = mul(picks[part], back[mine], lhs_turned).astype(low)
        gate_back[0, lax.rem(core + part, 2), 0] = jnp.sum(
            jnp.where(places[part], grad_gate[mine], 0.0), axis=0, keepdims=True
        )


def run_expert(core, order, first, total_steps, m_all, g_all, g_far, gates_all, gate_up, down, slots, kept):
    places, _, _, block, width = m_all.shape
    paired = gate_up.shape[1]
    steps = order.shape[0] // 4
    part_rows = steps * 2 * slots
    hidden = paired // 2
    shape = jax.ShapeDtypeStruct

    def gates_at(i, core, order):
        return (order[4 * i], 0, order[4 * i + 1], 0, 0)

    def token_at(i, core, order):
        return (order[4 * i], 0, order[4 * i + 2], 0, 0)

    def near_at(i, core, order):
        return (order[4 * i], 0, 0, 0)

    def far_at(i, core, order):
        return (order[4 * i + 3], 0, 0, 0)

    def fixed(i, core, order):
        return (0, 0)

    def flat(i, core, order):
        return (first + i, 0)

    def stacked(i, core, order):
        return (i, 0, 0)

    small = pl.BlockSpec((1, 2, 1, 1, block), gates_at)
    one_block = pl.BlockSpec((1, block, width), stacked)
    widths = (width, width, hidden, paired)
    grid_spec = pltpu.PrefetchScalarGridSpec(
        num_scalar_prefetch=2,
        grid=(steps,),
        in_specs=[
            pl.BlockSpec((1, 2, 1, block, width), token_at),
            pl.BlockSpec((1, 2, block, g_all.shape[3]), near_at),
            pl.BlockSpec((1, 2, block, g_far.shape[3]), far_at),
            small,
            pl.BlockSpec(gate_up.shape, fixed, pipeline_mode=pl.Buffered(1)),
            pl.BlockSpec(down.shape, fixed, pipeline_mode=pl.Buffered(1)),
        ]
        + [pl.BlockSpec(memory_space=pl.ANY)] * (0 if kept is None else 5),
        out_specs=[one_block] * 2 + [small] + [pl.BlockSpec((2 * slots, n), flat) for n in widths],
    )
    return pl.pallas_call(
        expert_kernel,
        grid_spec=grid_spec,
        out_shape=[shape((steps, block, width), low)] * 2
        + [shape((places, 2, 2, 1, block), full)]
        + [shape((total_steps * 2 * slots, n), low) for n in widths],
        input_output_aliases={} if kept is None else {8 + i: 2 + i for i in range(5)},
        compiler_params=pltpu.CompilerParams(vmem_limit_bytes=vmem_bytes),
        cost_estimate=pl.CostEstimate(
            flops=part_rows * width * (4 * paired + 2 * hidden + 6 * block),
            bytes_accessed=steps * block * width * 12 + part_rows * (width * 4 + paired * 3),
            transcendentals=part_rows * hidden,
        ),
        name="experts",
    )(core, order, m_all, g_all, g_far, gates_all, gate_up, down, *(() if kept is None else kept))


def result_kernel(core_ref, order, z_ref, w_ref, dn_ref, keep_out, send_out):
    core = core_ref[0]
    slots = z_ref.shape[0] // 2
    y = mul(z_ref[...], dn_ref[...]).astype(low).astype(full)
    for part, out in enumerate((keep_out, send_out)):
        _, pick, weight = placed(w_ref[0, lax.rem(core + part, 2), 0], slots)
        scaled = (weight * y[part * slots : (part + 1) * slots]).astype(low)
        out[0] = mul(pick, scaled, lhs_turned).astype(low)


def run_result(core, order, first, hidden, gates_all, down, slots):
    block, width, inner = gates_all.shape[4], down.shape[1], down.shape[0]
    steps = order.shape[0] // 4
    one_block = pl.BlockSpec((1, block, width), lambda i, core, order: (i, 0, 0))
    return pl.pallas_call(
        result_kernel,
        grid_spec=pltpu.PrefetchScalarGridSpec(
            num_scalar_prefetch=2,
            grid=(steps,),
            in_specs=[
                pl.BlockSpec((2 * slots, inner), lambda i, core, order: (first + i, 0)),
                pl.BlockSpec(
                    (1, 2, 1, 1, block), lambda i, core, order: (order[4 * i], 0, order[4 * i + 1], 0, 0)
                ),
                pl.BlockSpec(down.shape, lambda i, core, order: (0, 0), pipeline_mode=pl.Buffered(1)),
            ],
            out_specs=[one_block] * 2,
        ),
        out_shape=[jax.ShapeDtypeStruct((steps, block, width), low)] * 2,
        compiler_params=pltpu.CompilerParams(vmem_limit_bytes=vmem_bytes),
        cost_estimate=pl.CostEstimate(
            flops=steps * 2 * slots * width * (2 * inner + 2 * block),
            bytes_accessed=steps * (4 * block * width + 4 * slots * inner) + 2 * inner * width,
            transcendentals=0,
        ),
        name="results",
    )(core, order, hidden, gates_all, down)


def own_heads_kernel(rank, qkv_ref, out_ref, o_ref, *, head_dim, heads):
    first = rank[0] == 0
    for head in range(heads):
        pair = [qkv_ref[:, (2 * head + i) * head_dim : (2 * head + i + 1) * head_dim] for i in range(2)]
        o_ref[:, head * head_dim : (head + 1) * head_dim] = jnp.where(first, pair[0], pair[1])
    kv = qkv_ref.shape[1] - 2 * heads * head_dim
    o_ref[:, heads * head_dim : heads * head_dim + kv] = qkv_ref[:, 2 * heads * head_dim :]
    o_ref[:, heads * head_dim + kv :] = jnp.where(first, out_ref[:head_dim], out_ref[head_dim:])


def own_heads(rank, qkv_weight, out_weight, head_dim, heads):
    kv = qkv_weight.shape[1] - 2 * heads * head_dim
    return pl.pallas_call(
        functools.partial(own_heads_kernel, head_dim=head_dim, heads=heads),
        grid_spec=pltpu.PrefetchScalarGridSpec(
            num_scalar_prefetch=1,
            grid=(1,),
            in_specs=[
                pl.BlockSpec(qkv_weight.shape, lambda i, rank: (0, 0)),
                pl.BlockSpec(out_weight.shape, lambda i, rank: (0, 0)),
            ],
            out_specs=pl.BlockSpec(
                (qkv_weight.shape[0], heads * head_dim + kv + out_weight.shape[1]), lambda i, rank: (0, 0)
            ),
        ),
        out_shape=jax.ShapeDtypeStruct(
            (qkv_weight.shape[0], heads * head_dim + kv + out_weight.shape[1]), qkv_weight.dtype
        ),
        name="own_heads",
    )(rank, qkv_weight, out_weight)


def all_heads_kernel(rank, mine_ref, other_ref, o_ref, *, head_dim, heads):
    first = rank[0] == 0
    for head in range(heads):
        cols = slice(head * head_dim, (head + 1) * head_dim)
        mine, other = mine_ref[:, cols].astype(full), other_ref[:, cols].astype(full)
        o_ref[:, 2 * head * head_dim : (2 * head + 1) * head_dim] = jnp.where(first, mine, other)
        o_ref[:, (2 * head + 1) * head_dim : (2 * head + 2) * head_dim] = jnp.where(first, other, mine)
    o_ref[:, 2 * heads * head_dim :] = mine_ref[:, heads * head_dim :].astype(full) + other_ref[
        :, heads * head_dim :
    ].astype(full)


def all_heads(rank, mine, other, head_dim, heads):
    rows, width = mine.shape
    return pl.pallas_call(
        functools.partial(all_heads_kernel, head_dim=head_dim, heads=heads),
        grid_spec=pltpu.PrefetchScalarGridSpec(
            num_scalar_prefetch=1,
            grid=(1,),
            in_specs=[pl.BlockSpec((rows, width), lambda i, rank: (0, 0))] * 2,
            out_specs=pl.BlockSpec((rows, width + heads * head_dim), lambda i, rank: (0, 0)),
        ),
        out_shape=jax.ShapeDtypeStruct((rows, width + heads * head_dim), full),
        name="all_heads",
    )(rank, mine, other)


def rms_back(values, gain, grad):
    scale = lax.rsqrt(jnp.mean(values * values, axis=-1, keepdims=True) + eps_norm)
    unit = values * scale
    grad_gain = jnp.sum(grad * unit, axis=0)
    grad_unit = grad * gain
    back = scale * (grad_unit - unit * jnp.mean(grad_unit * unit, axis=-1, keepdims=True))
    return back, grad_gain


def in_order(first, second):
    half = first.shape[0] // 2
    return jnp.concatenate([first[:half], second, first[half:]], axis=0)


def of_block(values, rank):
    quarter = values.shape[0] // 4
    outer = jnp.concatenate([values[:quarter], values[3 * quarter :]], axis=0)
    return jnp.where(rank == 0, outer, values[quarter : 3 * quarter])


def body_gathered(
    tokens, qkv_weight, out_weight, router_weight, attn_gain, moe_gain, query_gain, key_gain,
    expert_gate_up, expert_down, routes, cotangent,
):
    rows_dev, width = tokens.shape
    head_dim = query_gain.shape[0]
    top_k = routes.shape[1]
    fsdp = lax.axis_size("fsdp")
    spot = lax.axis_index("fsdp")
    rank = lax.axis_index("ctx")
    place, side, core = spot // 4, (spot // 2) % 2, spot % 2
    shard = qkv_weight.shape[0]
    heads = out_weight.shape[0] * fsdp // head_dim
    kv_heads = (qkv_weight.shape[1] // head_dim - heads) // 2
    group = heads // kv_heads // 2
    my_heads = heads // 2
    width_q, width_k = my_heads * head_dim, kv_heads * head_dim
    experts_all = router_weight.shape[1]
    capacity = 2 * rows_dev * top_k // experts_all
    both = ("fsdp", "ctx")

    def sequence(values):
        other = swap_ctx(values)
        first = jnp.where(rank == 0, values, other)
        second = jnp.where(rank == 0, other, values)
        return in_order(first, second)

    rank_at = rank[None].astype(jnp.int32)
    weights_local = own_heads(rank_at, qkv_weight, out_weight, head_dim, my_heads)
    small_local = jnp.concatenate([router_weight, attn_gain[:, None], moe_gain[:, None]], axis=1)
    small_all = lax.all_gather(small_local, "fsdp", axis=0, tiled=True)
    weights_all = lax.all_gather(weights_local, "fsdp", axis=0, tiled=True)
    qkv_all = weights_all[:, : width_q + 2 * width_k]
    out_all = weights_all[:, width_q + 2 * width_k :]
    router_all = small_all[:, :experts_all]
    attn_all = small_all[:, experts_all].astype(full)
    moe_all = small_all[:, experts_all + 1].astype(full)
    late_cols = width * 7 // 16
    g_all = lax.all_gather(
        jnp.concatenate([cotangent, swap_ctx(cotangent[:, late_cols:])], axis=1), "fsdp", axis=0, tiled=True
    ).reshape(fsdp // 2, 2, rows_dev, 2 * width - late_cols)

    sequence_in = sequence(tokens).astype(full)
    low_in = rms_scale(sequence_in, attn_all).astype(low)
    projected = mul(low_in, qkv_all)
    cosine, sine = (t[:, 0] for t in angles(jnp.arange(2 * rows_dev, dtype=jnp.int32), head_dim))
    sine = jnp.concatenate([-sine[:, : head_dim // 2], sine[:, head_dim // 2 :]], axis=1)
    gain_q, gain_k = query_gain.astype(full)[None], key_gain.astype(full)[None]
    attended, roped_q, roped_k, values_low = attend(
        projected, cosine, sine, gain_q, gain_k, kv_heads, group
    )
    branch = mul(attended, out_all)
    inputs = tokens.astype(full)
    mixed = (
        inputs
        + of_block(branch, rank)
        + swap_ctx(of_block(branch, 1 - rank).astype(low)).astype(full)
    )
    low_mid = rms_scale(mixed, moe_all).astype(low)
    m_all = lax.all_gather(jnp.concatenate([low_mid, swap_ctx(low_mid)]), "fsdp", axis=0, tiled=True)

    logits = mul(low_mid, router_all)
    named = routes[:, :, None] == jnp.arange(experts_all, dtype=jnp.int32)[None, None, :]
    selected = jnp.sum(jnp.where(named, logits[:, None, :], 0.0), axis=2)
    gates = gating(selected)
    chosen = jnp.any(named, axis=1)
    gates_wide = jnp.sum(jnp.where(named, gates[:, :, None], 0.0), axis=1)
    gates_sent = jnp.where(chosen, gates_wide, -1.0).T
    gates_all = lax.all_to_all(gates_sent, both, split_axis=0, concat_axis=0, tiled=True)

    g_all, gates_all = hold(g_all, gates_all)
    g_far = swap_ctx(g_all[..., :late_cols])

    lines = fsdp // 4
    places = list(range(1, lines)) + [0]
    cut = lines // 2
    parts = [places[:cut], places[cut:]]
    m_all = m_all.reshape(fsdp // 2, 2, 2, rows_dev, width)
    gates_all = gates_all.reshape(fsdp // 2, 2, 2, 1, rows_dev)
    state = dict(kept=None, first=0, core=core[None].astype(jnp.int32))

    def order_of(steps):
        spots = [((place - p) % lines) * 2 + (side + d) % 2 for d, _, p in steps]
        far = [i for i, step in enumerate(steps) if step[1] == 1] or [0]
        return jnp.stack(
            [
                jnp.asarray(item, jnp.int32)
                for i, step in enumerate(steps)
                for item in (
                    spots[i],
                    (rank + step[1]) % 2,
                    step[1],
                    spots[min(far, key=lambda j, i=i: abs(j - i))],
                )
            ]
        )

    def call(steps, raw=False):
        keep_back, send_back, *kept = run_expert(
            state["core"],
            order_of(steps),
            state["first"],
            4 * lines,
            m_all,
            g_all,
            g_far,
            gates_all,
            expert_gate_up[0],
            expert_down[0],
            capacity,
            state["kept"],
        )
        state["kept"] = kept
        state["first"] += len(steps)
        return (keep_back, send_back) if raw else over_core(keep_back, send_back)

    def wait(first):
        state["core"], first = hold(state["core"], first)
        return first

    steps_far, steps_own = ([(d, d, p) for p in places] for d in (1, 0))
    steps_mixed = [[(1, 0, p) for p in part] + [(0, 1, p) for p in part] for part in parts]
    back = call(steps_far)
    far_one, far_two = wait([pick_sum(back, 0, lines, column) for column in range(2)])
    far_one, far_two = swap_ctx(far_one), swap_side(far_two)

    def mixed_sums(back, at=0):
        return [
            pick_sum(back, start, start + cut, column) for start in (at, at + cut) for column in range(2)
        ]

    def rounds(sums, part):
        side_one, side_two, ctx_one, ctx_two = sums
        span = slice(part * cut, (part + 1) * cut)
        if part == 1:
            to_ctx = swap_ctx(jnp.stack([ctx_one, add_low(ctx_two, far_two[span])]))
            to_side = swap_side(jnp.stack([side_two, add_low(side_one, far_one[span])]))
            return [to_ctx[0], to_side[0], to_side[1], to_ctx[1]]
        return [
            swap_ctx(ctx_one),
            swap_side(side_two),
            swap_side(add_low(side_one, far_one[span])),
            swap_ctx(add_low(ctx_two, far_two[span])),
        ]

    keep, send = call(steps_mixed[0], raw=True)
    send, (far_one, far_two) = hold(send, (far_one, far_two))
    back = over_core(keep, send)
    back_own = call(steps_own)
    sums = wait(mixed_sums(back))
    back_own = [pick_sum(back_own, 0, lines, column) for column in range(2)]
    got = rounds(sums, 0)
    keep, send = call(steps_mixed[1], raw=True)
    send, got = hold(send, got)
    back = over_core(keep, send)
    entries = joined(parts[0], [item[:cut] for item in back_own], got)
    arrived = {p: line_shift(entries[p], lines - p) for p in parts[0]}
    gate_back, rows, grad_rows, hidden, grad_pair = state["kept"]
    hidden, sums = hold(hidden, mixed_sums(back))
    got = rounds(sums, 1)
    grad_gates = lax.all_to_all(
        gate_back.reshape(fsdp * 2, rows_dev), both, split_axis=0, concat_axis=0, tiled=True
    ).T
    def results(first, steps, hidden):
        return run_result(
            state["core"], order_of(steps), first, hidden, gates_all, expert_down[0], capacity
        )

    out_far = results(0, steps_far, hidden)
    out_rest = results(lines, steps_mixed[0] + steps_own + steps_mixed[1], hidden)
    got, out_far, out_rest, arrived, grad_gates = lax.optimization_barrier(
        (got, out_far, out_rest, arrived, grad_gates)
    )
    entries.update(joined(parts[1], [item[cut:] for item in back_own], got))
    out_far = over_core(*out_far)
    out_far = [pick_sum(out_far, 0, lines, 0), swap_side(pick_sum(out_far, 0, lines, 1))]
    out_rest = over_core(*out_rest)
    for p in parts[1][:-1]:
        arrived[p] = line_shift(entries[p], lines - p)
    grad_mid = line_total(entries[0], arrived)

    grad_wide = jnp.where(chosen, grad_gates, 0.0)
    grad_logits = (
        gates_wide * (grad_wide - jnp.sum(gates_wide * grad_wide, axis=1, keepdims=True))
    ).astype(low)
    grad_router = mul(low_mid, grad_logits, lhs_turned)
    grad_mid = grad_mid + mul(grad_logits, router_all, rhs_turned)
    grad_mixed_part, grad_moe_gain = rms_back(mixed, moe_all, grad_mid)
    grad_mixed = cotangent.astype(full) + grad_mixed_part

    low_mixed, (out_far[0], out_rest) = hold(grad_mixed.astype(low), (out_far[0], out_rest))
    grad_branch = sequence(low_mixed)
    out_sums = [
        jnp.concatenate([one, two])
        for one, two in zip(mixed_sums(out_rest), mixed_sums(out_rest, 2 * cut + lines))
    ]
    out_own = [pick_sum(out_rest, 2 * cut, 2 * cut + lines, column) for column in range(2)]
    (out_far[0], out_sums, out_own), grad_branch = hold((out_far[0], out_sums, out_own), grad_branch)
    side_one, side_two, ctx_one, ctx_two = out_sums
    out_far[0] = swap_ctx(out_far[0])
    grad_attended = mul(grad_branch, out_all, rhs_turned).astype(low)
    grad_attended, out_far = hold(grad_attended, out_far)
    got = [
        swap_ctx(ctx_one),
        swap_side(side_two),
        swap_side(add_low(side_one, out_far[0])),
        swap_ctx(add_low(ctx_two, out_far[1])),
    ]
    grad_out_part = mul(attended, grad_branch, lhs_turned).astype(low)
    grad_q, grad_k, grad_v, gain_q_part, gain_k_part = attend_grad(
        projected, roped_q, roped_k, values_low, grad_attended, cosine, sine, gain_q, gain_k, kv_heads, group
    )
    grad_projected = jnp.concatenate([grad_q, grad_k, grad_v], axis=1)
    grad_projected, (got[0], got[1]) = hold(grad_projected, (got[0], got[1]))
    grad_qkv_part = mul(low_in, grad_projected, lhs_turned).astype(low)
    grad_projected, got = hold(grad_projected, got)
    entries = joined(places, out_own, got)
    (rows, grad_pair, hidden, grad_rows, grad_projected), entries = hold(
        (rows, grad_pair, hidden, grad_rows, grad_projected), entries
    )
    one, two = line_first(entries, place)
    grad_normed_part = mul(grad_projected, qkv_all, rhs_turned)
    grad_gate_up = mul(rows, grad_pair, lhs_turned)[None]
    grad_down = mul(hidden, grad_rows, lhs_turned)[None]
    grad_normed = of_block(grad_normed_part, rank) + swap_ctx(
        of_block(grad_normed_part, 1 - rank).astype(low)
    ).astype(full)
    grad_in_part, grad_attn_gain = rms_back(inputs, attn_all, grad_normed)
    grad_tokens = grad_mixed + grad_in_part

    out_mine = lax.psum_scatter(grad_out_part, "fsdp", scatter_dimension=0, tiled=True).astype(full)
    out_other = swap_ctx(out_mine.astype(low)).astype(full)
    grad_out = jnp.where(
        rank == 0,
        jnp.concatenate([out_mine, out_other], axis=0),
        jnp.concatenate([out_other, out_mine], axis=0),
    )
    qkv_mine = lax.psum_scatter(grad_qkv_part, "fsdp", scatter_dimension=0, tiled=True)
    grad_qkv = all_heads(rank_at, qkv_mine, swap_ctx(qkv_mine), head_dim, my_heads)
    late = jnp.concatenate(
        [
            grad_attn_gain.reshape(-1, head_dim),
            jnp.sum(gain_q_part, axis=0),
            jnp.sum(gain_k_part, axis=0),
        ],
        axis=0,
    )
    late, (one, two, grad_gate_up, grad_down) = hold(late, (one, two, grad_gate_up, grad_down))
    far = line_second(entries, two)
    late = late + swap_ctx(late)
    early = jnp.concatenate([grad_router.T, grad_moe_gain[None]], axis=0)
    early, late = hold(early, late)
    early = early.reshape(-1, lines, 2, 2, shard).transpose(3, 2, 1, 0, 4)
    early = take(early, core) + swap_core(take(early, 1 - core))
    early = take(early, side) + swap_side(take(early, 1 - side))
    early = early + swap_ctx(early)
    (late, early), far = hold((sum_partners(late, fsdp, (1, 2)), early), far)
    early = halve_line(early, fsdp, place)
    output = (mixed + entries[0].astype(full) + one.astype(full) + far.astype(full)).astype(low)
    late = sum_partners(late, fsdp, (4, 8))
    gain_rows = width // head_dim
    return (
        output,
        grad_tokens,
        grad_qkv,
        grad_out,
        early[:experts_all].T,
        lax.dynamic_slice_in_dim(late[:gain_rows].reshape(-1), spot * shard, shard, 0),
        early[experts_all],
        late[gain_rows],
        late[gain_rows + 1],
        grad_gate_up,
        grad_down,
    )


gathered_bytes = 1 << 26


def choose_body(*args):
    tokens, gate_up = args[0], args[8]
    fsdp, ctx = lax.axis_size("fsdp"), lax.axis_size("ctx")
    fits = tokens.size * tokens.dtype.itemsize * fsdp * ctx <= gathered_bytes
    if fits and ctx == 2 and fsdp == 16 and gate_up.shape[0] == 1:
        return body_gathered(*args)
    return body_routed(*args)


def solution(mesh):
    in_specs = (
        P(("fsdp", "ctx"), None),
        P("fsdp", None),
        P("fsdp", None),
        P("fsdp", None),
        P("fsdp"),
        P("fsdp"),
        P(),
        P(),
        P(("fsdp", "ctx"), None, None),
        P(("fsdp", "ctx"), None, None),
        P(("fsdp", "ctx"), None),
        P(("fsdp", "ctx"), None),
    )
    out_specs = (
        P(("fsdp", "ctx"), None),
        P(("fsdp", "ctx"), None),
        P("fsdp", None),
        P("fsdp", None),
        P("fsdp", None),
        P("fsdp"),
        P("fsdp"),
        P(),
        P(),
        P(("fsdp", "ctx"), None, None),
        P(("fsdp", "ctx"), None, None),
    )
    return jax.shard_map(choose_body, mesh=mesh, in_specs=in_specs, out_specs=out_specs, check_vma=False)
```

```python
import functools
import math

import jax
import jax.numpy as jnp
from jax import lax
from jax.experimental import pallas as pl
from jax.experimental.pallas import tpu as pltpu
from jax.sharding import PartitionSpec as P

eps_norm = 1e-06
theta_base = 1000000.0


def rms_scale(values, gain):
    return values * lax.rsqrt(jnp.mean(values * values, axis=-1, keepdims=True) + eps_norm) * gain


def rotate(values, cosine, sine):
    half_width = values.shape[-1] // 2
    turned = jnp.concatenate([-values[..., half_width:], values[..., :half_width]], axis=-1)
    return values * cosine + turned * sine


def angles(positions, width):
    freqs = theta_base ** (-(jnp.arange(width // 2, dtype=jnp.float32) * 2.0) / width)
    phase = positions.astype(jnp.float32)[:, None] * freqs[None, :]
    phase = jnp.concatenate([phase, phase], axis=-1)
    return (jnp.cos(phase)[:, None, :], jnp.sin(phase)[:, None, :])


def device_positions(block_rank, ctx_count, tok_rows):
    half_rows = tok_rows // 2
    within = jnp.arange(tok_rows, dtype=jnp.int32)
    span_id = jnp.where(within < half_rows, block_rank, 2 * ctx_count - 1 - block_rank)
    return span_id * half_rows + within % half_rows


def attend_head(query, keys_in, values_in, causal, scale_root):
    scores = (
        jnp.einsum("tgd,sd->gts", query, keys_in, preferred_element_type=jnp.float32) / scale_root
    )
    expo = jnp.where(causal[None], jnp.exp(scores), 0.0)
    totals = jnp.sum(expo, axis=-1, keepdims=True)
    probs = (expo / totals).astype(jnp.bfloat16)
    attended = jnp.einsum("gts,sd->tgd", probs, values_in, preferred_element_type=jnp.float32)
    return (attended, jnp.log(totals[..., 0]))


def attend_back(query, keys_in, values_in, causal, log_total, grad_attended, scale_root):
    scores = (
        jnp.einsum("tgd,sd->gts", query, keys_in, preferred_element_type=jnp.float32) / scale_root
    )
    probs = jnp.where(causal[None], jnp.exp(scores - log_total[..., None]), 0.0)
    low_probs = probs.astype(jnp.bfloat16)
    grad_values = jnp.einsum(
        "gts,tgd->sd", low_probs, grad_attended, preferred_element_type=jnp.float32
    )
    grad_probs = jnp.einsum(
        "tgd,sd->gts", grad_attended, values_in, preferred_element_type=jnp.float32
    )
    delta_rows = jnp.sum(grad_probs * probs, axis=-1, keepdims=True)
    grad_scores = (probs * (grad_probs - delta_rows)).astype(jnp.bfloat16)
    grad_query = (
        jnp.einsum("gts,sd->tgd", grad_scores, keys_in, preferred_element_type=jnp.float32)
        / scale_root
    )
    grad_keys = (
        jnp.einsum("gts,tgd->sd", grad_scores, query, preferred_element_type=jnp.float32)
        / scale_root
    )
    return (grad_query, grad_keys, grad_values)


def swiglu(paired):
    half_width = paired.shape[-1] // 2
    return jax.nn.silu(paired[..., :half_width]) * paired[..., half_width:]


def gating(selected):
    expo = jnp.exp(selected)
    return expo / jnp.sum(expo, axis=1, keepdims=True)


def body_routed(
    tokens,
    qkv_weight,
    out_weight,
    router_weight,
    attn_gain,
    moe_gain,
    query_gain,
    key_gain,
    expert_gate_up,
    expert_down,
    routes,
    cotangent,
):
    rows_dev, width = tokens.shape
    head_dim = query_gain.shape[0]
    top_k = routes.shape[1]
    ctx_count = lax.axis_size("ctx")
    ctx_rank = lax.axis_index("ctx")
    qkv_all, out_all, router_all, attn_all, moe_all = (
        lax.all_gather(qkv_weight, "fsdp", axis=0, tiled=True),
        lax.all_gather(out_weight, "fsdp", axis=0, tiled=True),
        lax.all_gather(router_weight, "fsdp", axis=0, tiled=True),
        lax.all_gather(attn_gain, "fsdp", axis=0, tiled=True),
        lax.all_gather(moe_gain, "fsdp", axis=0, tiled=True),
    )
    experts_all = router_all.shape[1]
    heads = out_all.shape[0] // head_dim
    kv_heads = (qkv_all.shape[1] // head_dim - heads) // 2
    group_size = heads // kv_heads
    capacity = 2 * rows_dev * top_k // experts_all
    width_q = heads * head_dim
    width_k = kv_heads * head_dim
    scale_root = math.sqrt(head_dim)
    inputs = tokens.astype(jnp.float32)
    normed_in = rms_scale(inputs, attn_all.astype(jnp.float32))
    low_in = normed_in.astype(jnp.bfloat16)
    projected = jnp.dot(low_in, qkv_all, preferred_element_type=jnp.float32)
    query_raw = projected[:, :width_q].reshape(rows_dev, heads, head_dim)
    key_raw = projected[:, width_q : width_q + width_k].reshape(rows_dev, kv_heads, head_dim)
    value_low = (
        projected[:, width_q + width_k :].astype(jnp.bfloat16).reshape(rows_dev, kv_heads, head_dim)
    )
    positions = device_positions(ctx_rank, ctx_count, rows_dev)
    cosine, sine = angles(positions, head_dim)
    query_gain_f = query_gain.astype(jnp.float32)
    key_gain_f = key_gain.astype(jnp.float32)

    def query_rope(values_in, gain):
        return rotate(rms_scale(values_in, gain), cosine, sine)

    query_low = query_rope(query_raw, query_gain_f).astype(jnp.bfloat16)
    key_low = query_rope(key_raw, key_gain_f).astype(jnp.bfloat16)
    keys_all, values_all = (
        lax.all_gather(key_low, "ctx", axis=0, tiled=True),
        lax.all_gather(value_low, "ctx", axis=0, tiled=True),
    )
    key_pos = jnp.concatenate(
        [device_positions(other, ctx_count, rows_dev) for other in range(ctx_count)]
    )
    causal = key_pos[None, :] <= positions[:, None]
    query_heads = query_low.reshape(rows_dev, kv_heads, group_size, head_dim).transpose(1, 0, 2, 3)
    key_heads = keys_all.transpose(1, 0, 2)
    value_heads = values_all.transpose(1, 0, 2)
    attended, log_total = lax.map(
        lambda member: attend_head(member[0], member[1], member[2], causal, scale_root),
        (query_heads, key_heads, value_heads),
    )
    attended_low = attended.transpose(1, 0, 2, 3).reshape(rows_dev, width_q).astype(jnp.bfloat16)
    mixed = inputs + jnp.dot(attended_low, out_all, preferred_element_type=jnp.float32)
    normed_mid = rms_scale(mixed, moe_all.astype(jnp.float32))
    low_mid = normed_mid.astype(jnp.bfloat16)
    logits = jnp.dot(low_mid, router_all, preferred_element_type=jnp.float32)
    selected = jnp.take_along_axis(logits, routes, axis=1)
    gates, gate_back = jax.vjp(gating, selected)
    flat_routes = routes.reshape(-1)
    expert_ids = jnp.arange(experts_all, dtype=jnp.int32)
    hit_table = (flat_routes[:, None] == expert_ids[None, :]).astype(jnp.int32)
    slot_index = jnp.sum(jnp.cumsum(hit_table, axis=0) * hit_table, axis=1) - 1
    target = flat_routes * capacity + slot_index
    pair_count = rows_dev * top_k
    source_pair = (
        jnp.full((experts_all * capacity,), pair_count, jnp.int32)
        .at[target]
        .set(jnp.arange(pair_count, dtype=jnp.int32))
    )
    padded = jnp.concatenate([low_mid, jnp.zeros((1, width), jnp.bfloat16)], axis=0)
    outgoing = padded[source_pair // top_k].reshape(experts_all, capacity, width)
    received = lax.all_to_all(outgoing, ("fsdp", "ctx"), split_axis=0, concat_axis=1, tiled=True)
    gate_and_up = jnp.einsum(
        "esd,edf->esf", received, expert_gate_up, preferred_element_type=jnp.float32
    )
    hidden_val, swiglu_back = jax.vjp(swiglu, gate_and_up)
    hidden_low = hidden_val.astype(jnp.bfloat16)
    result_low = jnp.einsum(
        "esf,efd->esd", hidden_low, expert_down, preferred_element_type=jnp.float32
    ).astype(jnp.bfloat16)
    returned = lax.all_to_all(
        result_low, ("fsdp", "ctx"), split_axis=1, concat_axis=0, tiled=True
    ).reshape(experts_all * capacity, width)
    picked = returned[target].reshape(rows_dev, top_k, width).astype(jnp.float32)
    output = (mixed + jnp.sum(gates[:, :, None] * picked, axis=1)).astype(jnp.bfloat16)
    qkv_back, out_back, router_back, attn_back_g, moe_back_g = (
        qkv_all,
        out_all,
        router_all,
        attn_all,
        moe_all,
    )
    grad_final = cotangent.astype(jnp.float32)
    grad_gates = jnp.sum(grad_final[:, None, :] * picked, axis=2)
    grad_result = (
        (gates[:, :, None] * grad_final[:, None, :]).astype(jnp.bfloat16).reshape(pair_count, width)
    )
    grad_padded = jnp.concatenate([grad_result, jnp.zeros((1, width), jnp.bfloat16)], axis=0)
    grad_outgoing = grad_padded[source_pair].reshape(experts_all, capacity, width)
    grad_received = lax.all_to_all(
        grad_outgoing, ("fsdp", "ctx"), split_axis=0, concat_axis=1, tiled=True
    )
    grad_down = jnp.einsum(
        "esf,esd->efd", hidden_low, grad_received, preferred_element_type=jnp.float32
    )
    grad_hidden = jnp.einsum(
        "esd,efd->esf", grad_received, expert_down, preferred_element_type=jnp.float32
    )
    grad_paired = swiglu_back(grad_hidden)[0].astype(jnp.bfloat16)
    grad_gate_up = jnp.einsum(
        "esd,esf->edf", received, grad_paired, preferred_element_type=jnp.float32
    )
    grad_rows = jnp.einsum(
        "esf,edf->esd", grad_paired, expert_gate_up, preferred_element_type=jnp.float32
    ).astype(jnp.bfloat16)
    grad_returned = lax.all_to_all(
        grad_rows, ("fsdp", "ctx"), split_axis=1, concat_axis=0, tiled=True
    ).reshape(experts_all * capacity, width)
    grad_mid = jnp.sum(
        grad_returned[target].reshape(rows_dev, top_k, width).astype(jnp.float32), axis=1
    )
    grad_selected = gate_back(grad_gates)[0]
    route_table = (routes[:, :, None] == expert_ids[None, None, :]).astype(jnp.float32)
    grad_logits = jnp.sum(route_table * grad_selected[:, :, None], axis=1).astype(jnp.bfloat16)
    grad_router = jnp.dot(low_mid.T, grad_logits, preferred_element_type=jnp.float32)
    grad_mid = grad_mid + jnp.dot(grad_logits, router_back.T, preferred_element_type=jnp.float32)
    unused_mid, mid_back = jax.vjp(rms_scale, mixed, moe_back_g.astype(jnp.float32))
    grad_mixed_part, grad_moe_gain = mid_back(grad_mid)
    grad_mixed = grad_final + grad_mixed_part
    grad_branch = grad_mixed.astype(jnp.bfloat16)
    grad_out = jnp.dot(attended_low.T, grad_branch, preferred_element_type=jnp.float32)
    grad_attended = jnp.dot(grad_branch, out_back.T, preferred_element_type=jnp.float32).astype(
        jnp.bfloat16
    )
    grad_heads = grad_attended.reshape(rows_dev, kv_heads, group_size, head_dim).transpose(
        1, 0, 2, 3
    )
    grad_query_h, grad_key_h, grad_value_h = lax.map(
        lambda member: attend_back(
            member[0], member[1], member[2], causal, member[3], member[4], scale_root
        ),
        (query_heads, key_heads, value_heads, log_total, grad_heads),
    )
    grad_keys, grad_values = (
        lax.psum_scatter(
            grad_key_h.transpose(1, 0, 2).astype(jnp.bfloat16),
            "ctx",
            scatter_dimension=0,
            tiled=True,
        ).astype(jnp.float32),
        lax.psum_scatter(
            grad_value_h.transpose(1, 0, 2).astype(jnp.bfloat16),
            "ctx",
            scatter_dimension=0,
            tiled=True,
        ).astype(jnp.float32),
    )
    grad_query_rot = (
        grad_query_h.transpose(1, 0, 2, 3).reshape(rows_dev, heads, head_dim).astype(jnp.bfloat16)
    )
    grad_query_rot = lax.optimization_barrier(grad_query_rot).astype(jnp.float32)
    grad_key_rot = lax.optimization_barrier(grad_keys.astype(jnp.bfloat16)).astype(jnp.float32)
    unused_query, query_back = jax.vjp(query_rope, query_raw, query_gain_f)
    grad_query_raw, grad_query_gain = query_back(grad_query_rot)
    unused_key, key_back = jax.vjp(query_rope, key_raw, key_gain_f)
    grad_key_raw, grad_key_gain = key_back(grad_key_rot)
    grad_projected = jnp.concatenate(
        [
            grad_query_raw.reshape(rows_dev, width_q).astype(jnp.bfloat16),
            grad_key_raw.reshape(rows_dev, width_k).astype(jnp.bfloat16),
            grad_values.reshape(rows_dev, width_k).astype(jnp.bfloat16),
        ],
        axis=1,
    )
    grad_qkv = jnp.dot(low_in.T, grad_projected, preferred_element_type=jnp.float32)
    grad_normed = jnp.dot(grad_projected, qkv_back.T, preferred_element_type=jnp.float32)
    unused_in, in_back = jax.vjp(rms_scale, inputs, attn_back_g.astype(jnp.float32))
    grad_in_part, grad_attn_gain = in_back(grad_normed)
    grad_tokens = grad_mixed + grad_in_part
    gradients = (grad_qkv, grad_out, grad_router, grad_attn_gain, grad_moe_gain)
    pieces = (
        lax.psum_scatter(gradients[0], "fsdp", scatter_dimension=0, tiled=True),
        lax.psum_scatter(gradients[1], "fsdp", scatter_dimension=0, tiled=True),
        lax.psum_scatter(gradients[2], "fsdp", scatter_dimension=0, tiled=True),
        lax.psum_scatter(gradients[3], "fsdp", scatter_dimension=0, tiled=True),
        lax.psum_scatter(gradients[4], "fsdp", scatter_dimension=0, tiled=True),
    )
    reduced = (
        lax.psum(pieces[0].astype(jnp.bfloat16), "ctx").astype(jnp.float32),
        lax.psum(pieces[1].astype(jnp.bfloat16), "ctx").astype(jnp.float32),
        lax.psum(pieces[2].astype(jnp.bfloat16), "ctx").astype(jnp.float32),
        lax.psum(pieces[3].astype(jnp.bfloat16), "ctx").astype(jnp.float32),
        lax.psum(pieces[4].astype(jnp.bfloat16), "ctx").astype(jnp.float32),
    )
    gain_sums = lax.psum((grad_query_gain, grad_key_gain), ("fsdp", "ctx"))
    return (
        output,
        grad_tokens,
        reduced[0],
        reduced[1],
        reduced[2],
        reduced[3],
        reduced[4],
        gain_sums[0],
        gain_sums[1],
        grad_gate_up,
        grad_down,
    )


low = jnp.bfloat16
full = jnp.float32
plain = (((1,), (0,)), ((), ()))
rhs_turned = (((1,), (1,)), ((), ()))
lhs_turned = (((0,), (0,)), ((), ()))
vmem_bytes = 58 << 20


def mul(left, right, dims=plain):
    return lax.dot_general(left, right, dims, preferred_element_type=full)


def core_pairs(fsdp):
    return [(i, i ^ 1) for i in range(fsdp)]


def side_pairs(fsdp):
    return [(i, i ^ 2) for i in range(fsdp)]


def swap_core(values):
    return lax.ppermute(values, "fsdp", core_pairs(lax.axis_size("fsdp")))


def swap_side(values):
    return lax.ppermute(values, "fsdp", side_pairs(lax.axis_size("fsdp")))


def swap_ctx(values):
    return lax.ppermute(values, "ctx", [(0, 1), (1, 0)])


def add_low(one, two):
    return (one.astype(full) + two.astype(full)).astype(low)


def hold(values, first):
    return lax.optimization_barrier((values, first))


def take(values, index):
    return lax.dynamic_index_in_dim(values, index, 0, keepdims=False)


def line_shift(values, step):
    fsdp = lax.axis_size("fsdp")
    return lax.ppermute(values, "fsdp", [(i, (i + 4 * step) % fsdp) for i in range(fsdp)])


def line_total(own, arrived):
    total = own.astype(full)
    for item in arrived.values():
        total = total + item.astype(full)
    return total


def line_halving(entries, place):
    fsdp = lax.axis_size("fsdp")
    even = place % 2 == 0
    one, two = jnp.where(even, entries[3], entries[1]), jnp.where(even, entries[1], entries[3])
    one, two = (lax.ppermute(item, "fsdp", [(i, i ^ 4) for i in range(fsdp)]) for item in (one, two))
    far = lax.ppermute(add_low(entries[2], two), "fsdp", [(i, i ^ 8) for i in range(fsdp)])
    return entries[0].astype(full) + one.astype(full) + far.astype(full)


def joined(places, own, got):
    from_ctx, from_side, one_side, two_ctx = got
    entries = {}
    for at, p in enumerate(places):
        one = add_low(add_low(own[0][at], from_ctx[at]), one_side[at])
        two = add_low(add_low(own[1][at], from_side[at]), two_ctx[at])
        entries[p] = jnp.concatenate([one, two], axis=-1)
    return entries


def over_core(keep, send):
    return keep, swap_core(send)


def pick_sum(parts, start, stop, column):
    keep, other = parts
    half = keep.shape[-1] // 2
    cut = (slice(start, stop), slice(None), slice(column * half, (column + 1) * half))
    return add_low(keep[cut], other[cut])


def sum_all(values, fsdp):
    values = values + lax.ppermute(values, "fsdp", core_pairs(fsdp))
    values = values + swap_ctx(values)
    step = 2
    while step < fsdp:
        values = values + lax.ppermute(values, "fsdp", [(i, i ^ step) for i in range(fsdp)])
        step *= 2
    return values


def sum_owned(values, fsdp, spot):
    items, shard = values.shape[0], values.shape[1] // fsdp
    values = values.reshape(items, fsdp, shard).swapaxes(0, 1)
    step = fsdp // 2
    while step:
        bit = (spot // step) % 2
        values = values.reshape(2, step, items, shard)
        other = lax.ppermute(take(values, 1 - bit), "fsdp", [(i, i ^ step) for i in range(fsdp)])
        values = take(values, bit) + other
        step //= 2
    values = values[0]
    return values + swap_ctx(values)


def turn(values):
    return pltpu.roll(values, values.shape[-1] // 2, 1)


def norm_rope(raw, gain, cosine, sine):
    scale = lax.rsqrt(jnp.mean(raw * raw, axis=-1, keepdims=True) + eps_norm)
    scaled = raw * scale * gain
    return scaled * cosine + turn(scaled) * sine


def norm_rope_back(raw, gain, cosine, sine, grad):
    scale = lax.rsqrt(jnp.mean(raw * raw, axis=-1, keepdims=True) + eps_norm)
    unit = raw * scale
    grad_scaled = grad * cosine - turn(grad) * sine
    grad_gain = jnp.sum(grad_scaled * unit, axis=0, keepdims=True)
    grad_unit = grad_scaled * gain
    grad_raw = scale * (grad_unit - unit * jnp.mean(grad_unit * unit, axis=-1, keepdims=True))
    return grad_raw, grad_gain


def tiles_of(rows):
    step = rows // 2
    return [(start, start + step) for start in range(0, rows, step)]


def allowed(start, stop):
    shape = (stop - start, stop)
    return lax.broadcasted_iota(jnp.int32, shape, 1) <= (
        lax.broadcasted_iota(jnp.int32, shape, 0) + start
    )


def attend_kernel(q_ref, k_ref, v_ref, cos_ref, sin_ref, qg_ref, kg_ref, o_ref, qr_ref, kr_ref, vl_ref):
    head_dim = k_ref.shape[1]
    rows = k_ref.shape[0]
    cosine, sine = cos_ref[...], sin_ref[...]
    keys = norm_rope(k_ref[...], kg_ref[...], cosine, sine).astype(low)
    values = v_ref[...].astype(low)
    kr_ref[...] = keys
    vl_ref[...] = values
    for head in range(q_ref.shape[1] // head_dim):
        cols = slice(head * head_dim, (head + 1) * head_dim)
        query = norm_rope(q_ref[:, cols], qg_ref[...], cosine, sine).astype(low)
        qr_ref[:, cols] = query
        for start, stop in tiles_of(rows):
            scores = mul(query[start:stop], keys[:stop], rhs_turned) * (1.0 / math.sqrt(head_dim))
            expo = jnp.where(allowed(start, stop), jnp.exp(scores), 0.0)
            probs = (expo / jnp.sum(expo, axis=-1, keepdims=True)).astype(low)
            o_ref[start:stop, cols] = mul(probs, values[:stop]).astype(low)


def attend_grad_kernel(
    q_ref, k_ref, qr_ref, kr_ref, vl_ref, go_ref, cos_ref, sin_ref, qg_ref, kg_ref,
    dq_ref, dk_ref, dv_ref, dqg_ref, dkg_ref, dk_sum, dv_sum, dq_sum,
):
    head_dim = k_ref.shape[1]
    rows = k_ref.shape[0]
    root = 1.0 / math.sqrt(head_dim)
    cosine, sine = cos_ref[...], sin_ref[...]
    keys, values = kr_ref[...], vl_ref[...]
    gain_sum = jnp.zeros((1, head_dim), full)
    dk_sum[...] = jnp.zeros_like(dk_sum)
    dv_sum[...] = jnp.zeros_like(dv_sum)
    for head in range(q_ref.shape[1] // head_dim):
        cols = slice(head * head_dim, (head + 1) * head_dim)
        for start, stop in tiles_of(rows):
            query = qr_ref[start:stop, cols]
            grad = go_ref[start:stop, cols]
            scores = mul(query, keys[:stop], rhs_turned) * root
            expo = jnp.where(allowed(start, stop), jnp.exp(scores), 0.0)
            probs = expo / jnp.sum(expo, axis=-1, keepdims=True)
            grad_probs = mul(grad, values[:stop], rhs_turned)
            delta = jnp.sum(grad_probs * probs, axis=-1, keepdims=True)
            grad_scores = (probs * (grad_probs - delta)).astype(low)
            dv_sum[:stop] += mul(probs.astype(low), grad, lhs_turned)
            dk_sum[:stop] += mul(grad_scores, query, lhs_turned)
            dq_sum[start:stop] = mul(grad_scores, keys[:stop])
        grad_query = (dq_sum[...] * root).astype(low).astype(full)
        grad_raw, grad_gain = norm_rope_back(q_ref[:, cols], qg_ref[...], cosine, sine, grad_query)
        dq_ref[:, cols] = grad_raw.astype(low)
        gain_sum = gain_sum + grad_gain
    dqg_ref[0] = gain_sum
    grad_key = (dk_sum[...] * root).astype(low).astype(full)
    grad_raw, grad_gain = norm_rope_back(k_ref[...], kg_ref[...], cosine, sine, grad_key)
    dk_ref[...] = grad_raw.astype(low)
    dkg_ref[0] = grad_gain
    dv_ref[...] = dv_sum[...].astype(low)


def attention_specs(rows, head_dim, kv_heads, group):
    wide, narrow = group * head_dim, head_dim
    heads_end = kv_heads * group
    return dict(
        q=pl.BlockSpec((rows, wide), lambda i: (0, i)),
        k=pl.BlockSpec((rows, narrow), lambda i: (0, heads_end + i)),
        v=pl.BlockSpec((rows, narrow), lambda i: (0, heads_end + kv_heads + i)),
        own=pl.BlockSpec((rows, narrow), lambda i: (0, i)),
        table=pl.BlockSpec((rows, head_dim), lambda i: (0, 0)),
        gain=pl.BlockSpec((1, head_dim), lambda i: (0, 0)),
        gain_out=pl.BlockSpec((1, 1, head_dim), lambda i: (i, 0, 0)),
    )


def attend(projected, cosine, sine, query_gain, key_gain, kv_heads, group):
    rows, head_dim = cosine.shape
    s = attention_specs(rows, head_dim, kv_heads, group)
    shape = jax.ShapeDtypeStruct
    work = rows * rows * head_dim * kv_heads * group
    return pl.pallas_call(
        attend_kernel,
        grid=(kv_heads,),
        in_specs=[s["q"], s["k"], s["v"], s["table"], s["table"], s["gain"], s["gain"]],
        out_specs=[s["q"], s["q"], s["own"], s["own"]],
        out_shape=[
            shape((rows, kv_heads * group * head_dim), low),
            shape((rows, kv_heads * group * head_dim), low),
            shape((rows, kv_heads * head_dim), low),
            shape((rows, kv_heads * head_dim), low),
        ],
        compiler_params=pltpu.CompilerParams(vmem_limit_bytes=48 << 20),
        cost_estimate=pl.CostEstimate(
            flops=4 * work, bytes_accessed=projected.size * 6, transcendentals=work // head_dim
        ),
        name="attend",
    )(projected, projected, projected, cosine, sine, query_gain, key_gain)


def attend_grad(projected, roped_q, roped_k, values_low, grad, cosine, sine, query_gain, key_gain, kv_heads, group):
    rows, head_dim = cosine.shape
    s = attention_specs(rows, head_dim, kv_heads, group)
    shape = jax.ShapeDtypeStruct
    work = rows * rows * head_dim * kv_heads * group
    return pl.pallas_call(
        attend_grad_kernel,
        grid=(kv_heads,),
        in_specs=[
            s["q"], s["k"], s["q"], s["own"], s["own"], s["q"],
            s["table"], s["table"], s["gain"], s["gain"],
        ],
        out_specs=[s["q"], s["own"], s["own"], s["gain_out"], s["gain_out"]],
        out_shape=[
            shape((rows, kv_heads * group * head_dim), low),
            shape((rows, kv_heads * head_dim), low),
            shape((rows, kv_heads * head_dim), low),
            shape((kv_heads, 1, head_dim), full),
            shape((kv_heads, 1, head_dim), full),
        ],
        scratch_shapes=[pltpu.VMEM((rows, head_dim), full)] * 3,
        compiler_params=pltpu.CompilerParams(vmem_limit_bytes=48 << 20),
        cost_estimate=pl.CostEstimate(
            flops=10 * work, bytes_accessed=projected.size * 10, transcendentals=work // head_dim
        ),
        name="attend_grad",
    )(projected, projected, roped_q, roped_k, values_low, grad, cosine, sine, query_gain, key_gain)


def placed(gate, slots):
    block = gate.shape[1]
    shape = (block, block)
    earlier = (
        lax.broadcasted_iota(jnp.int32, shape, 0) < lax.broadcasted_iota(jnp.int32, shape, 1)
    ).astype(low)
    hit = jnp.where(gate >= 0.0, 1.0, 0.0)
    count = mul(jnp.broadcast_to(hit, (8, block)).astype(low), earlier)[:1].astype(jnp.int32)
    place = (lax.broadcasted_iota(jnp.int32, (slots, block), 0) == count) & (hit > 0.5)
    weight = jnp.sum(jnp.where(place, gate, 0.0), axis=1, keepdims=True)
    return place, place.astype(full).astype(low), weight


def expert_kernel(core_ref, order, m_ref, g_ref, far_ref, w_ref, gu_ref, dn_ref, *refs):
    keep_back, send_back, gate_back, rows_ref, dy_ref, z_ref, pair_ref = refs[-7:]
    core = core_ref[0]
    far = order[4 * pl.program_id(0) + 2] == 1
    width = m_ref.shape[4]
    hidden = dn_ref.shape[0]
    slots = z_ref.shape[0] // 2
    places, picks, weights, rows, grads = [], [], [], [], []
    for part in range(2):
        at = lax.rem(core + part, 2)
        place, pick, weight = placed(w_ref[0, at, 0], slots)
        places.append(place)
        picks.append(pick)
        weights.append(weight)
        rows.append(mul(pick, m_ref[0, at, 0]).astype(low))
        near_rows = g_ref[0, at, :, :width]
        far_rows = jnp.concatenate([far_ref[0, at], g_ref[0, at, :, width:]], axis=1)
        grads.append(mul(pick, jnp.where(far, far_rows, near_rows)).astype(low))
    row, grad, weight = (jnp.concatenate(items, axis=0) for items in (rows, grads, weights))
    rows_ref[...] = row
    paired = mul(row, gu_ref[...])
    gate_in, up = paired[:, :hidden], paired[:, hidden:]
    sig = jax.nn.sigmoid(gate_in)
    act = gate_in * sig
    z = (act * up).astype(low)
    z_ref[...] = z
    dy_ref[...] = (weight * grad.astype(full)).astype(low)
    unweighted = mul(grad, dn_ref[...], rhs_turned)
    grad_gate = jnp.sum(unweighted * z.astype(full), axis=1, keepdims=True)
    dz = weight * unweighted
    grad_in = dz * up * (sig * (1.0 + gate_in * (1.0 - sig)))
    pair = jnp.concatenate([grad_in, dz * act], axis=1).astype(low)
    pair_ref[...] = pair
    back = mul(pair, gu_ref[...], rhs_turned).astype(low)
    for part, out in enumerate((keep_back, send_back)):
        mine = slice(part * slots, (part + 1) * slots)
        out[0] = mul(picks[part], back[mine], lhs_turned).astype(low)
        gate_back[0, lax.rem(core + part, 2), 0] = jnp.sum(
            jnp.where(places[part], grad_gate[mine], 0.0), axis=0, keepdims=True
        )


def run_expert(core, order, first, total_steps, m_all, g_all, g_far, gates_all, gate_up, down, slots, kept):
    places, _, _, block, width = m_all.shape
    paired = gate_up.shape[1]
    steps = order.shape[0] // 4
    part_rows = steps * 2 * slots
    hidden = paired // 2
    shape = jax.ShapeDtypeStruct

    def gates_at(i, core, order):
        return (order[4 * i], 0, order[4 * i + 1], 0, 0)

    def token_at(i, core, order):
        return (order[4 * i], 0, order[4 * i + 2], 0, 0)

    def near_at(i, core, order):
        return (order[4 * i], 0, 0, 0)

    def far_at(i, core, order):
        return (order[4 * i + 3], 0, 0, 0)

    def fixed(i, core, order):
        return (0, 0)

    def flat(i, core, order):
        return (first + i, 0)

    def stacked(i, core, order):
        return (i, 0, 0)

    small = pl.BlockSpec((1, 2, 1, 1, block), gates_at)
    one_block = pl.BlockSpec((1, block, width), stacked)
    widths = (width, width, hidden, paired)
    grid_spec = pltpu.PrefetchScalarGridSpec(
        num_scalar_prefetch=2,
        grid=(steps,),
        in_specs=[
            pl.BlockSpec((1, 2, 1, block, width), token_at),
            pl.BlockSpec((1, 2, block, g_all.shape[3]), near_at),
            pl.BlockSpec((1, 2, block, g_far.shape[3]), far_at),
            small,
            pl.BlockSpec(gate_up.shape, fixed, pipeline_mode=pl.Buffered(1)),
            pl.BlockSpec(down.shape, fixed, pipeline_mode=pl.Buffered(1)),
        ]
        + [pl.BlockSpec(memory_space=pl.ANY)] * (0 if kept is None else 5),
        out_specs=[one_block] * 2 + [small] + [pl.BlockSpec((2 * slots, n), flat) for n in widths],
    )
    return pl.pallas_call(
        expert_kernel,
        grid_spec=grid_spec,
        out_shape=[shape((steps, block, width), low)] * 2
        + [shape((places, 2, 2, 1, block), full)]
        + [shape((total_steps * 2 * slots, n), low) for n in widths],
        input_output_aliases={} if kept is None else {8 + i: 2 + i for i in range(5)},
        compiler_params=pltpu.CompilerParams(vmem_limit_bytes=vmem_bytes),
        cost_estimate=pl.CostEstimate(
            flops=part_rows * width * (4 * paired + 2 * hidden + 6 * block),
            bytes_accessed=steps * block * width * 12 + part_rows * (width * 4 + paired * 3),
            transcendentals=part_rows * hidden,
        ),
        name="experts",
    )(core, order, m_all, g_all, g_far, gates_all, gate_up, down, *(() if kept is None else kept))


def result_kernel(core_ref, order, z_ref, w_ref, dn_ref, keep_out, send_out):
    core = core_ref[0]
    slots = z_ref.shape[0] // 2
    y = mul(z_ref[...], dn_ref[...]).astype(low).astype(full)
    for part, out in enumerate((keep_out, send_out)):
        _, pick, weight = placed(w_ref[0, lax.rem(core + part, 2), 0], slots)
        scaled = (weight * y[part * slots : (part + 1) * slots]).astype(low)
        out[0] = mul(pick, scaled, lhs_turned).astype(low)


def run_result(core, order, first, hidden, gates_all, down, slots):
    block, width, inner = gates_all.shape[4], down.shape[1], down.shape[0]
    steps = order.shape[0] // 4
    one_block = pl.BlockSpec((1, block, width), lambda i, core, order: (i, 0, 0))
    return pl.pallas_call(
        result_kernel,
        grid_spec=pltpu.PrefetchScalarGridSpec(
            num_scalar_prefetch=2,
            grid=(steps,),
            in_specs=[
                pl.BlockSpec((2 * slots, inner), lambda i, core, order: (first + i, 0)),
                pl.BlockSpec(
                    (1, 2, 1, 1, block), lambda i, core, order: (order[4 * i], 0, order[4 * i + 1], 0, 0)
                ),
                pl.BlockSpec(down.shape, lambda i, core, order: (0, 0), pipeline_mode=pl.Buffered(1)),
            ],
            out_specs=[one_block] * 2,
        ),
        out_shape=[jax.ShapeDtypeStruct((steps, block, width), low)] * 2,
        compiler_params=pltpu.CompilerParams(vmem_limit_bytes=vmem_bytes),
        cost_estimate=pl.CostEstimate(
            flops=steps * 2 * slots * width * (2 * inner + 2 * block),
            bytes_accessed=steps * (4 * block * width + 4 * slots * inner) + 2 * inner * width,
            transcendentals=0,
        ),
        name="results",
    )(core, order, hidden, gates_all, down)


def own_heads_kernel(rank, qkv_ref, out_ref, o_ref, *, head_dim, heads):
    first = rank[0] == 0
    for head in range(heads):
        pair = [qkv_ref[:, (2 * head + i) * head_dim : (2 * head + i + 1) * head_dim] for i in range(2)]
        o_ref[:, head * head_dim : (head + 1) * head_dim] = jnp.where(first, pair[0], pair[1])
    kv = qkv_ref.shape[1] - 2 * heads * head_dim
    o_ref[:, heads * head_dim : heads * head_dim + kv] = qkv_ref[:, 2 * heads * head_dim :]
    o_ref[:, heads * head_dim + kv :] = jnp.where(first, out_ref[:head_dim], out_ref[head_dim:])


def own_heads(rank, qkv_weight, out_weight, head_dim, heads):
    kv = qkv_weight.shape[1] - 2 * heads * head_dim
    return pl.pallas_call(
        functools.partial(own_heads_kernel, head_dim=head_dim, heads=heads),
        grid_spec=pltpu.PrefetchScalarGridSpec(
            num_scalar_prefetch=1,
            grid=(1,),
            in_specs=[
                pl.BlockSpec(qkv_weight.shape, lambda i, rank: (0, 0)),
                pl.BlockSpec(out_weight.shape, lambda i, rank: (0, 0)),
            ],
            out_specs=pl.BlockSpec(
                (qkv_weight.shape[0], heads * head_dim + kv + out_weight.shape[1]), lambda i, rank: (0, 0)
            ),
        ),
        out_shape=jax.ShapeDtypeStruct(
            (qkv_weight.shape[0], heads * head_dim + kv + out_weight.shape[1]), qkv_weight.dtype
        ),
        name="own_heads",
    )(rank, qkv_weight, out_weight)


def all_heads_kernel(rank, mine_ref, other_ref, o_ref, *, head_dim, heads):
    first = rank[0] == 0
    for head in range(heads):
        cols = slice(head * head_dim, (head + 1) * head_dim)
        mine, other = mine_ref[:, cols].astype(full), other_ref[:, cols].astype(full)
        o_ref[:, 2 * head * head_dim : (2 * head + 1) * head_dim] = jnp.where(first, mine, other)
        o_ref[:, (2 * head + 1) * head_dim : (2 * head + 2) * head_dim] = jnp.where(first, other, mine)
    o_ref[:, 2 * heads * head_dim :] = mine_ref[:, heads * head_dim :].astype(full) + other_ref[
        :, heads * head_dim :
    ].astype(full)


def all_heads(rank, mine, other, head_dim, heads):
    rows, width = mine.shape
    return pl.pallas_call(
        functools.partial(all_heads_kernel, head_dim=head_dim, heads=heads),
        grid_spec=pltpu.PrefetchScalarGridSpec(
            num_scalar_prefetch=1,
            grid=(1,),
            in_specs=[pl.BlockSpec((rows, width), lambda i, rank: (0, 0))] * 2,
            out_specs=pl.BlockSpec((rows, width + heads * head_dim), lambda i, rank: (0, 0)),
        ),
        out_shape=jax.ShapeDtypeStruct((rows, width + heads * head_dim), full),
        name="all_heads",
    )(rank, mine, other)


def rms_back(values, gain, grad):
    scale = lax.rsqrt(jnp.mean(values * values, axis=-1, keepdims=True) + eps_norm)
    unit = values * scale
    grad_gain = jnp.sum(grad * unit, axis=0)
    grad_unit = grad * gain
    back = scale * (grad_unit - unit * jnp.mean(grad_unit * unit, axis=-1, keepdims=True))
    return back, grad_gain


def in_order(first, second):
    half = first.shape[0] // 2
    return jnp.concatenate([first[:half], second, first[half:]], axis=0)


def of_block(values, rank):
    quarter = values.shape[0] // 4
    outer = jnp.concatenate([values[:quarter], values[3 * quarter :]], axis=0)
    return jnp.where(rank == 0, outer, values[quarter : 3 * quarter])


def body_gathered(
    tokens, qkv_weight, out_weight, router_weight, attn_gain, moe_gain, query_gain, key_gain,
    expert_gate_up, expert_down, routes, cotangent,
):
    rows_dev, width = tokens.shape
    head_dim = query_gain.shape[0]
    top_k = routes.shape[1]
    fsdp = lax.axis_size("fsdp")
    spot = lax.axis_index("fsdp")
    rank = lax.axis_index("ctx")
    place, side, core = spot // 4, (spot // 2) % 2, spot % 2
    shard = qkv_weight.shape[0]
    heads = out_weight.shape[0] * fsdp // head_dim
    kv_heads = (qkv_weight.shape[1] // head_dim - heads) // 2
    group = heads // kv_heads // 2
    my_heads = heads // 2
    width_q, width_k = my_heads * head_dim, kv_heads * head_dim
    experts_all = router_weight.shape[1]
    capacity = 2 * rows_dev * top_k // experts_all
    both = ("fsdp", "ctx")

    def sequence(values):
        other = swap_ctx(values)
        first = jnp.where(rank == 0, values, other)
        second = jnp.where(rank == 0, other, values)
        return in_order(first, second)

    rank_at = rank[None].astype(jnp.int32)
    weights_local = own_heads(rank_at, qkv_weight, out_weight, head_dim, my_heads)
    small_local = jnp.concatenate([router_weight, attn_gain[:, None], moe_gain[:, None]], axis=1)
    small_all = lax.all_gather(small_local, "fsdp", axis=0, tiled=True)
    weights_all = lax.all_gather(weights_local, "fsdp", axis=0, tiled=True)
    qkv_all = weights_all[:, : width_q + 2 * width_k]
    out_all = weights_all[:, width_q + 2 * width_k :]
    router_all = small_all[:, :experts_all]
    attn_all = small_all[:, experts_all].astype(full)
    moe_all = small_all[:, experts_all + 1].astype(full)
    late_cols = width * 7 // 16
    g_all = lax.all_gather(
        jnp.concatenate([cotangent, swap_ctx(cotangent[:, late_cols:])], axis=1), "fsdp", axis=0, tiled=True
    ).reshape(fsdp // 2, 2, rows_dev, 2 * width - late_cols)

    sequence_in = sequence(tokens).astype(full)
    low_in = rms_scale(sequence_in, attn_all).astype(low)
    projected = mul(low_in, qkv_all)
    cosine, sine = (t[:, 0] for t in angles(jnp.arange(2 * rows_dev, dtype=jnp.int32), head_dim))
    sine = jnp.concatenate([-sine[:, : head_dim // 2], sine[:, head_dim // 2 :]], axis=1)
    gain_q, gain_k = query_gain.astype(full)[None], key_gain.astype(full)[None]
    attended, roped_q, roped_k, values_low = attend(
        projected, cosine, sine, gain_q, gain_k, kv_heads, group
    )
    branch = mul(attended, out_all)
    inputs = tokens.astype(full)
    mixed = (
        inputs
        + of_block(branch, rank)
        + swap_ctx(of_block(branch, 1 - rank).astype(low)).astype(full)
    )
    low_mid = rms_scale(mixed, moe_all).astype(low)
    m_all = lax.all_gather(jnp.concatenate([low_mid, swap_ctx(low_mid)]), "fsdp", axis=0, tiled=True)

    logits = mul(low_mid, router_all)
    named = routes[:, :, None] == jnp.arange(experts_all, dtype=jnp.int32)[None, None, :]
    selected = jnp.sum(jnp.where(named, logits[:, None, :], 0.0), axis=2)
    gates = gating(selected)
    chosen = jnp.any(named, axis=1)
    gates_wide = jnp.sum(jnp.where(named, gates[:, :, None], 0.0), axis=1)
    gates_sent = jnp.where(chosen, gates_wide, -1.0).T
    gates_all = lax.all_to_all(gates_sent, both, split_axis=0, concat_axis=0, tiled=True)

    g_all, gates_all = hold(g_all, gates_all)
    g_far = swap_ctx(g_all[..., :late_cols])

    lines = fsdp // 4
    places = list(range(1, lines)) + [0]
    cut = lines // 2
    parts = [places[:cut], places[cut:]]
    m_all = m_all.reshape(fsdp // 2, 2, 2, rows_dev, width)
    gates_all = gates_all.reshape(fsdp // 2, 2, 2, 1, rows_dev)
    state = dict(kept=None, first=0, core=core[None].astype(jnp.int32))

    def order_of(steps):
        spots = [((place - p) % lines) * 2 + (side + d) % 2 for d, _, p in steps]
        far = [i for i, step in enumerate(steps) if step[1] == 1] or [0]
        return jnp.stack(
            [
                jnp.asarray(item, jnp.int32)
                for i, step in enumerate(steps)
                for item in (
                    spots[i],
                    (rank + step[1]) % 2,
                    step[1],
                    spots[min(far, key=lambda j, i=i: abs(j - i))],
                )
            ]
        )

    def call(steps, raw=False):
        keep_back, send_back, *kept = run_expert(
            state["core"],
            order_of(steps),
            state["first"],
            4 * lines,
            m_all,
            g_all,
            g_far,
            gates_all,
            expert_gate_up[0],
            expert_down[0],
            capacity,
            state["kept"],
        )
        state["kept"] = kept
        state["first"] += len(steps)
        return (keep_back, send_back) if raw else over_core(keep_back, send_back)

    def wait(first):
        state["core"], first = hold(state["core"], first)
        return first

    steps_far, steps_own = ([(d, d, p) for p in places] for d in (1, 0))
    steps_mixed = [[(1, 0, p) for p in part] + [(0, 1, p) for p in part] for part in parts]
    back = call(steps_far)
    far_one, far_two = wait([pick_sum(back, 0, lines, column) for column in range(2)])
    far_one, far_two = swap_ctx(far_one), swap_side(far_two)

    def mixed_sums(back, at=0):
        return [
            pick_sum(back, start, start + cut, column) for start in (at, at + cut) for column in range(2)
        ]

    def rounds(sums, part):
        side_one, side_two, ctx_one, ctx_two = sums
        span = slice(part * cut, (part + 1) * cut)
        return [
            swap_ctx(ctx_one),
            swap_side(side_two),
            swap_side(add_low(side_one, far_one[span])),
            swap_ctx(add_low(ctx_two, far_two[span])),
        ]

    keep, send = call(steps_mixed[0], raw=True)
    send, (far_one, far_two) = hold(send, (far_one, far_two))
    back = over_core(keep, send)
    back_own = call(steps_own)
    sums = wait(mixed_sums(back))
    back_own = [pick_sum(back_own, 0, lines, column) for column in range(2)]
    got = rounds(sums, 0)
    keep, send = call(steps_mixed[1], raw=True)
    send, got = hold(send, got)
    back = over_core(keep, send)
    entries = joined(parts[0], [item[:cut] for item in back_own], got)
    arrived = {p: line_shift(entries[p], lines - p) for p in parts[0]}
    gate_back, rows, grad_rows, hidden, grad_pair = state["kept"]
    hidden, sums = hold(hidden, mixed_sums(back))
    got = rounds(sums, 1)
    grad_gates = lax.all_to_all(
        gate_back.reshape(fsdp * 2, rows_dev), both, split_axis=0, concat_axis=0, tiled=True
    ).T
    def results(first, steps, hidden):
        return run_result(
            state["core"], order_of(steps), first, hidden, gates_all, expert_down[0], capacity
        )

    out_far = results(0, steps_far, hidden)
    out_rest = results(lines, steps_mixed[0] + steps_own + steps_mixed[1], hidden)
    got, out_far, out_rest, arrived, grad_gates = lax.optimization_barrier(
        (got, out_far, out_rest, arrived, grad_gates)
    )
    entries.update(joined(parts[1], [item[cut:] for item in back_own], got))
    out_far = over_core(*out_far)
    out_far = [pick_sum(out_far, 0, lines, 0), swap_side(pick_sum(out_far, 0, lines, 1))]
    out_rest = over_core(*out_rest)
    for p in parts[1][:-1]:
        arrived[p] = line_shift(entries[p], lines - p)
    grad_mid = line_total(entries[0], arrived)

    grad_wide = jnp.where(chosen, grad_gates, 0.0)
    grad_logits = (
        gates_wide * (grad_wide - jnp.sum(gates_wide * grad_wide, axis=1, keepdims=True))
    ).astype(low)
    grad_router = mul(low_mid, grad_logits, lhs_turned)
    grad_mid = grad_mid + mul(grad_logits, router_all, rhs_turned)
    grad_mixed_part, grad_moe_gain = rms_back(mixed, moe_all, grad_mid)
    grad_mixed = cotangent.astype(full) + grad_mixed_part

    low_mixed, (out_far[0], out_rest) = hold(grad_mixed.astype(low), (out_far[0], out_rest))
    grad_branch = sequence(low_mixed)
    out_sums = [
        jnp.concatenate([one, two])
        for one, two in zip(mixed_sums(out_rest), mixed_sums(out_rest, 2 * cut + lines))
    ]
    out_own = [pick_sum(out_rest, 2 * cut, 2 * cut + lines, column) for column in range(2)]
    (out_far[0], out_sums, out_own), grad_branch = hold((out_far[0], out_sums, out_own), grad_branch)
    side_one, side_two, ctx_one, ctx_two = out_sums
    out_far[0] = swap_ctx(out_far[0])
    grad_attended = mul(grad_branch, out_all, rhs_turned).astype(low)
    (rows, grad_pair), grad_attended = hold((rows, grad_pair), grad_attended)
    grad_gate_up = mul(rows, grad_pair, lhs_turned)[None]
    grad_attended, (out_far, grad_gate_up) = hold(grad_attended, (out_far, grad_gate_up))
    got = [
        swap_ctx(ctx_one),
        swap_side(side_two),
        swap_side(add_low(side_one, out_far[0])),
        swap_ctx(add_low(ctx_two, out_far[1])),
    ]
    grad_out_part = mul(attended, grad_branch, lhs_turned).astype(low)
    grad_q, grad_k, grad_v, gain_q_part, gain_k_part = attend_grad(
        projected, roped_q, roped_k, values_low, grad_attended, cosine, sine, gain_q, gain_k, kv_heads, group
    )
    grad_projected = jnp.concatenate([grad_q, grad_k, grad_v], axis=1)
    (hidden, grad_rows), grad_projected = hold((hidden, grad_rows), grad_projected)
    grad_down = mul(hidden, grad_rows, lhs_turned)[None]
    grad_projected, (got[0], got[1], grad_down) = hold(grad_projected, (got[0], got[1], grad_down))
    grad_qkv_part = mul(low_in, grad_projected, lhs_turned).astype(low)
    entries = joined(places, out_own, got)
    if lines == 4:
        output = (mixed + line_halving(entries, place)).astype(low)
    else:
        output = (
            mixed + line_total(entries[0], {p: line_shift(entries[p], lines - p) for p in places[:-1]})
        ).astype(low)
    grad_normed_part = mul(grad_projected, qkv_all, rhs_turned)
    grad_normed = of_block(grad_normed_part, rank) + swap_ctx(
        of_block(grad_normed_part, 1 - rank).astype(low)
    ).astype(full)
    grad_in_part, grad_attn_gain = rms_back(inputs, attn_all, grad_normed)
    grad_tokens = grad_mixed + grad_in_part

    out_mine = lax.psum_scatter(grad_out_part, "fsdp", scatter_dimension=0, tiled=True).astype(full)
    out_other = swap_ctx(out_mine.astype(low)).astype(full)
    grad_out = jnp.where(
        rank == 0,
        jnp.concatenate([out_mine, out_other], axis=0),
        jnp.concatenate([out_other, out_mine], axis=0),
    )
    qkv_mine = lax.psum_scatter(grad_qkv_part, "fsdp", scatter_dimension=0, tiled=True)
    grad_qkv = all_heads(rank_at, qkv_mine, swap_ctx(qkv_mine), head_dim, my_heads)
    early, got = hold(jnp.concatenate([grad_router.T, grad_moe_gain[None]], axis=0), got)
    early = sum_owned(early, fsdp, spot)
    late = sum_all(
        jnp.concatenate(
            [
                grad_attn_gain.reshape(-1, head_dim),
                jnp.sum(gain_q_part, axis=0),
                jnp.sum(gain_k_part, axis=0),
            ],
            axis=0,
        ),
        fsdp,
    )
    gain_rows = width // head_dim
    return (
        output,
        grad_tokens,
        grad_qkv,
        grad_out,
        early[:experts_all].T,
        lax.dynamic_slice_in_dim(late[:gain_rows].reshape(-1), spot * shard, shard, 0),
        early[experts_all],
        late[gain_rows],
        late[gain_rows + 1],
        grad_gate_up,
        grad_down,
    )


gathered_bytes = 1 << 26


def choose_body(*args):
    tokens, gate_up = args[0], args[8]
    fsdp, ctx = lax.axis_size("fsdp"), lax.axis_size("ctx")
    fits = tokens.size * tokens.dtype.itemsize * fsdp * ctx <= gathered_bytes
    if fits and fsdp % 4 == 0 and ctx == 2 and fsdp >= 8 and fsdp & (fsdp - 1) == 0 and gate_up.shape[0] == 1:
        return body_gathered(*args)
    return body_routed(*args)


def solution(mesh):
    in_specs = (
        P(("fsdp", "ctx"), None),
        P("fsdp", None),
        P("fsdp", None),
        P("fsdp", None),
        P("fsdp"),
        P("fsdp"),
        P(),
        P(),
        P(("fsdp", "ctx"), None, None),
        P(("fsdp", "ctx"), None, None),
        P(("fsdp", "ctx"), None),
        P(("fsdp", "ctx"), None),
    )
    out_specs = (
        P(("fsdp", "ctx"), None),
        P(("fsdp", "ctx"), None),
        P("fsdp", None),
        P("fsdp", None),
        P("fsdp", None),
        P("fsdp"),
        P("fsdp"),
        P(),
        P(),
        P(("fsdp", "ctx"), None, None),
        P(("fsdp", "ctx"), None, None),
    )
    return jax.shard_map(choose_body, mesh=mesh, in_specs=in_specs, out_specs=out_specs, check_vma=False)
```
